32 devices in a mesh: dp: 2 (over x), row: 4 (over y, core), col: 4 (over z).
Axes of the slice: x: 2, y: 2, z: 4, core: 2. Of those that a mesh axis runs over, the one named last changes fastest.
Arguments:
- tokens: bfloat16 [768, 39200], P('row', ('dp', 'col')), may hold values from -6 to 6
- grad_out: bfloat16 [768, 39200], P('row', ('dp', 'col')), may hold values from -6 to 6
- adapter_index: int32 [8, 1], replicated, may hold values from 0 to 7
- norm1_gain: bfloat16 [768], P('row'), may hold values from 0.099609375 to 1.8984375
- norm2_gain: bfloat16 [768], P('row'), may hold values from 0.099609375 to 1.8984375
- qkv_weight: bfloat16 [768, 2304], P('row', 'col'), may hold values from -0.21875 to 0.21875
- proj_weight: bfloat16 [768, 768], P('col', 'row'), may hold values from -0.875 to 0.875
- fc1_weight: bfloat16 [768, 3072], P('row', 'col'), may hold values from -0.21875 to 0.21875
- fc2_weight: bfloat16 [768, 3072], P('row', 'col'), may hold values from -0.109375 to 0.109375
- rel_h: bfloat16 [27, 64], replicated, may hold values from -0.59765625 to 0.59765625
- rel_w: bfloat16 [27, 64], replicated, may hold values from -0.59765625 to 0.59765625
- qkv_down: bfloat16 [8, 768, 16], P(None, 'row'), may hold values from -0.21875 to 0.21875
- qkv_up: bfloat16 [8, 16, 2304], P(None, None, 'col'), may hold values from -0.75 to 0.75
- proj_down: bfloat16 [8, 768, 16], P(None, 'col'), may hold values from -0.21875 to 0.21875
- proj_up: bfloat16 [8, 16, 768], P(None, None, 'row'), may hold values from -0.75 to 0.75
- fc1_down: bfloat16 [8, 768, 16], P(None, 'row'), may hold values from -0.21875 to 0.21875
- fc1_up: bfloat16 [8, 16, 3072], P(None, None, 'col'), may hold values from -0.75 to 0.75
- fc2_down: bfloat16 [8, 3072, 16], P(None, 'col'), may hold values from -0.109375 to 0.109375
- fc2_up: bfloat16 [8, 16, 768], P(None, None, 'row'), may hold values from -0.75 to 0.75
Outputs:
- out: bfloat16 [768, 39200], P('row', ('dp', 'col'))
- tokens_grad: float32 [768, 39200], P('row', ('dp', 'col'))
- qkv_down_grad: float32 [8, 768, 16], P(None, 'row')
- qkv_up_grad: float32 [8, 16, 2304], P(None, None, 'col')
- proj_down_grad: float32 [8, 768, 16], P(None, 'col')
- proj_up_grad: float32 [8, 16, 768], P(None, None, 'row')
- fc1_down_grad: float32 [8, 768, 16], P(None, 'row')
- fc1_up_grad: float32 [8, 16, 3072], P(None, None, 'col')
- fc2_down_grad: float32 [8, 3072, 16], P(None, 'col')
- fc2_up_grad: float32 [8, 16, 768], P(None, None, 'row')
The draws below stay inside these ranges and needn't reach their ends.
Inputs may be any that keep to these rules, and one draw needn't show every extreme that they name: `adapter_index`: every one of the 8 adapters is chosen by at least one image.
All inputs are finite; a program needn't handle non-finite values.
Results may differ from the reference program's by a relative error of at most 0.015.
Values may be sent and summed in bfloat16 or wider, within the bound.
No kernel may reach another device: no remote copies, remote signals or barrier semaphores. Data moves between devices by JAX's collectives and lax.ppermute only.
A program may use at most 448 MiB of HBM per device.

```python
import jax
import jax.numpy as jnp
from jax import lax

D = 768
HEADS = 12
HD = 64
FF = 3072
WIN = 14
SIDE = 64
RANK = 16
ADAPT = 8
NWIN_SIDE = 5
IMG_TOK = 4900
IMAGES = 8
TOKENS = 39200


def levels(key, dims, shards, least, high):
    loudness, own = 1.0, jax.random.fold_in(key, 6)
    for dim, shards_of in shards:
        heights = jnp.exp(jax.random.uniform(jax.random.fold_in(own, dim), (shards_of,), jnp.float32, least / len(shards), high / len(shards)))
        loudness = loudness * jnp.repeat(heights, dims[dim] // shards_of).reshape([-1 if axis == dim else 1 for axis in range(len(dims))])
    return loudness


def picks_of(stream_key, rows, number_of, top, lift):
    ranking = jax.random.permutation(jax.random.fold_in(stream_key, 1), number_of)
    boost = ranking
    for power in range(3):
        boost = boost * boost // number_of
    boost = boost * lift // number_of
    chance = jax.random.randint(jax.random.fold_in(stream_key, 2), (rows, number_of), 0, 4096) + boost
    fixed_rows = jax.random.permutation(jax.random.fold_in(stream_key, 3), rows)[jnp.arange(number_of) % rows]
    chance = jnp.where(jnp.arange(rows)[:, None] == fixed_rows[None, :], 1 << 14, chance)
    priority = chance * number_of + jnp.arange(number_of)
    return lax.top_k(priority.astype(jnp.int32), top)[1].astype(jnp.int32)


def normal_values(rng, extent, scale, bound, split=(), kind=jnp.bfloat16):
    array = scale * jax.random.normal(rng, extent, jnp.float32)
    if split:
        array = array * levels(rng, extent, split, -0.22, 0.18)
    return jnp.clip(array, -bound, bound).astype(kind)


def setup_inputs(seed: int = 0) -> dict:
    key_of = jax.random.split(jax.random.key(seed), 20)
    return {
        "tokens": normal_values(key_of[0], (D, TOKENS), 1.0, 6.0, ((0, 4), (1, 8))),
        "grad_out": normal_values(key_of[1], (D, TOKENS), 1.0, 6.0, ((0, 4), (1, 8))),
        "adapter_index": picks_of(key_of[2], IMAGES, ADAPT, 1, 0),
        "norm1_gain": jnp.clip(1.0 + 0.18 * jax.random.normal(key_of[3], (D,), jnp.float32), 0.099609375, 1.8984375).astype(jnp.bfloat16),
        "norm2_gain": jnp.clip(1.0 + 0.18 * jax.random.normal(key_of[4], (D,), jnp.float32), 0.099609375, 1.8984375).astype(jnp.bfloat16),
        "qkv_weight": normal_values(key_of[5], (D, 3 * D), D ** -0.5, 0.21875, ((0, 4), (1, 4))),
        "proj_weight": normal_values(key_of[6], (D, D), (D // 16) ** -0.5, 0.875, ((0, 4), (1, 4))),
        "fc1_weight": normal_values(key_of[7], (D, FF), D ** -0.5, 0.21875, ((0, 4), (1, 4))),
        "fc2_weight": normal_values(key_of[8], (D, FF), FF ** -0.5, 0.109375, ((0, 4), (1, 4))),
        "rel_h": normal_values(key_of[9], (2 * WIN - 1, HD), 0.1, 0.59765625),
        "rel_w": normal_values(key_of[10], (2 * WIN - 1, HD), 0.1, 0.59765625),
        "qkv_down": normal_values(key_of[11], (ADAPT, D, RANK), D ** -0.5, 0.21875, ((1, 4),)),
        "qkv_up": normal_values(key_of[12], (ADAPT, RANK, 3 * D), (4 * RANK) ** -0.5, 0.75, ((2, 4),)),
        "proj_down": normal_values(key_of[13], (ADAPT, D, RANK), D ** -0.5, 0.21875, ((1, 4),)),
        "proj_up": normal_values(key_of[14], (ADAPT, RANK, D), (4 * RANK) ** -0.5, 0.75, ((2, 4),)),
        "fc1_down": normal_values(key_of[15], (ADAPT, D, RANK), D ** -0.5, 0.21875, ((1, 4),)),
        "fc1_up": normal_values(key_of[16], (ADAPT, RANK, FF), (4 * RANK) ** -0.5, 0.75, ((2, 4),)),
        "fc2_down": normal_values(key_of[17], (ADAPT, FF, RANK), FF ** -0.5, 0.109375, ((1, 4),)),
        "fc2_up": normal_values(key_of[18], (ADAPT, RANK, D), (4 * RANK) ** -0.5, 0.75, ((2, 4),)),
    }


@jax.custom_vjp
def low(v):
    return lax.optimization_barrier(v.astype(jnp.bfloat16)).astype(jnp.float32)

@jax.custom_vjp
def low_back(v):
    return v

def low_keep(v):
    return (low(v), None)

def low_pass(kept, grad):
    return (grad,)

def back_keep(v):
    return (v, None)

def back_low(kept, grad):
    return (low(grad),)
low.defvjp(low_keep, low_pass)
low_back.defvjp(back_keep, back_low)
PRECISE = lax.Precision.HIGHEST
EPSILON = 1e-06

def valid_rows():
    position = jnp.arange(IMG_TOK, dtype=jnp.int32)
    window = position // (WIN * WIN)
    inside = position % (WIN * WIN)
    image_row = window // NWIN_SIDE * WIN + inside // WIN
    image_col = window % NWIN_SIDE * WIN + inside % WIN
    return ((image_row < SIDE) & (image_col < SIDE)).astype(jnp.float32)

def rel_table(rel_param):
    offsets = jnp.arange(WIN, dtype=jnp.int32)[:, None] - jnp.arange(WIN, dtype=jnp.int32)[None, :] + WIN - 1
    one_hot = (offsets[:, :, None] == jnp.arange(2 * WIN - 1, dtype=jnp.int32)[None, None, :]).astype(jnp.float32)
    return jnp.einsum('akn,nc->akc', one_hot, rel_param, precision=PRECISE)

def layer_norm(values, gain_vec):
    center = lax.optimization_barrier(jnp.mean(values, axis=-1, keepdims=True))
    shifted = values - center
    variance = lax.optimization_barrier(jnp.mean(shifted * shifted, axis=-1, keepdims=True))
    return shifted * lax.rsqrt(variance + EPSILON) * gain_vec

def adapted(inputs, weight, down_mat, up_mat):
    product = jnp.dot(inputs, weight, precision=PRECISE)
    reduced = jnp.dot(inputs, down_mat, precision=PRECISE)
    return product + jnp.dot(reduced, up_mat, precision=PRECISE)

def score_matrix(query_f, key_f, table_rows, table_cols):
    windows = query_f.shape[0]
    dot_scores = jnp.einsum('nqhc,nkhc->nhqk', query_f, key_f, precision=PRECISE) * HD ** (-0.5)
    spatial = query_f.reshape(windows, WIN, WIN, HEADS, HD)
    rel_rows = jnp.einsum('nabhc,akc->nhabk', spatial, table_rows, precision=PRECISE)
    rel_cols = jnp.einsum('nabhc,bkc->nhabk', spatial, table_cols, precision=PRECISE)
    shaped = dot_scores.reshape(windows, HEADS, WIN, WIN, WIN, WIN)
    shaped = shaped + rel_rows[:, :, :, :, :, None] + rel_cols[:, :, :, :, None, :]
    return shaped.reshape(windows, HEADS, WIN * WIN, WIN * WIN)

def image_layer(image_rows, image_pick, frozen, adapters):
    gain_one, gain_two, w_qkv, w_proj, w_up, w_down, table_rows, table_cols = frozen

    def select(adapter):
        return jnp.einsum('a,ade->de', image_pick, adapter, precision=PRECISE)
    picked = [select(adapter) for adapter in adapters]
    validity = valid_rows()[:, None]
    windows = NWIN_SIDE * NWIN_SIDE
    hidden_one = low(layer_norm(image_rows, gain_one) * validity)
    qkv = low(low_back(adapted(hidden_one, w_qkv, picked[0], picked[1])))
    arranged = qkv.reshape(windows, WIN * WIN, HEADS, 3, HD)
    query_f = arranged[:, :, :, 0]
    key_f = arranged[:, :, :, 1]
    value_f = arranged[:, :, :, 2]
    scores = low_back(score_matrix(query_f, key_f, table_rows, table_cols))
    maxima = lax.optimization_barrier(jnp.max(scores, axis=3, keepdims=True))
    exponent = jnp.exp(scores - maxima)
    attn_prob = low(exponent / lax.optimization_barrier(jnp.sum(exponent, axis=3, keepdims=True)))
    attended = jnp.einsum('nhqk,nkhc->nqhc', attn_prob, value_f, precision=PRECISE).reshape(IMG_TOK, D)
    attended = low(low_back(attended))
    branch = low_back(adapted(attended, w_proj, picked[2], picked[3]))
    middle = image_rows + branch
    hidden_two = low(layer_norm(middle, gain_two))
    pre_act = low_back(adapted(hidden_two, w_up, picked[4], picked[5]))
    activated = low(jax.nn.gelu(pre_act, approximate=False))
    mlp_out = low_back(adapted(activated, w_down, picked[6], picked[7]))
    return (middle + mlp_out) * validity

def reference(tokens, grad_out, adapter_index, norm1_gain, norm2_gain, qkv_weight, proj_weight, fc1_weight, fc2_weight, rel_h, rel_w, qkv_down, qkv_up, proj_down, proj_up, fc1_down, fc1_up, fc2_down, fc2_up):
    frozen = (norm1_gain.astype(jnp.float32), norm2_gain.astype(jnp.float32), qkv_weight.astype(jnp.float32), proj_weight.astype(jnp.float32), fc1_weight.astype(jnp.float32), fc2_weight.astype(jnp.float32).T, rel_table(rel_h.astype(jnp.float32)), rel_table(rel_w.astype(jnp.float32)))
    adapters = (qkv_down.astype(jnp.float32), qkv_up.astype(jnp.float32), proj_down.astype(jnp.float32), proj_up.astype(jnp.float32), fc1_down.astype(jnp.float32), fc1_up.astype(jnp.float32), fc2_down.astype(jnp.float32), fc2_up.astype(jnp.float32))
    image_picks = (adapter_index[:, 0][:, None] == jnp.arange(ADAPT, dtype=jnp.int32)[None, :]).astype(jnp.float32)
    checked_layer = jax.checkpoint(image_layer)

    def forward(flat_tokens, adapt_set):
        images = flat_tokens.reshape(IMAGES, IMG_TOK, D)

        def per_image(scan_carry, scan_item):
            return (scan_carry, checked_layer(scan_item[0], scan_item[1], frozen, adapt_set))
        scan_carry, stacked = lax.scan(per_image, jnp.zeros((), jnp.float32), (images, image_picks))
        return stacked.reshape(IMAGES * IMG_TOK, D)
    result, pullback = jax.vjp(forward, tokens.astype(jnp.float32).T, adapters)
    grad_tokens, grad_adapt = pullback(grad_out.astype(jnp.float32).T)
    return (result.astype(jnp.bfloat16).T, grad_tokens.T, grad_adapt[0], grad_adapt[1], grad_adapt[2], grad_adapt[3], grad_adapt[4], grad_adapt[5], grad_adapt[6], grad_adapt[7])
```

```python
import jax
import jax.numpy as jnp
import numpy as np
from jax import lax
from jax.experimental import pallas as pl
from jax.experimental.pallas import tpu as pltpu
from jax.sharding import PartitionSpec as P

D = 768
HD = 64
WIN = 14
SLOTS = WIN * WIN
SIDE = 64
ADAPT = 8
NWIN = 5
IMG_TOK = NWIN * NWIN * SLOTS
RANK = 16
EDGE = SIDE - (NWIN - 1) * WIN
QUART = D // 4
FULLR = 208
KEYS = 208
EDGER = EDGE * WIN
CORNR = EDGE * EDGE
ROWS = 4 * FULLR + 2 * EDGER + CORNR
HALF = ROWS // 2
EPSILON = 1e-06
BF = jnp.bfloat16
F32 = jnp.float32
VMEM_LIMIT = 60 * 1024 * 1024

FULL, RIGHT, BOTTOM, CORNER = 0, 1, 2, 3
NQ = (FULLR, EDGER, EDGER, CORNR)
OFFS = (0, 4 * FULLR, 4 * FULLR + EDGER, 4 * FULLR + 2 * EDGER)


def slot_order(kind):
    rows = EDGE if kind in (BOTTOM, CORNER) else WIN
    cols = EDGE if kind in (RIGHT, CORNER) else WIN
    kept = [a * WIN + b for a in range(rows) for b in range(cols)]
    rest = [s for s in range(SLOTS) if s not in set(kept)]
    return kept, kept + rest


def build_tables():
    shift = np.zeros((4, FULLR, 128), np.int32)
    keys = np.zeros((4, KEYS, 128), np.float32)
    for kind in range(4):
        kept, order = slot_order(kind)
        for i, s in enumerate(kept):
            for base in (0, 64):
                shift[kind, i, base : base + 32] = WIN - 1 - s // WIN
                shift[kind, i, base + 32 : base + 64] = WIN - 1 - s % WIN
        for i, s in enumerate(order):
            for base in (0, 64):
                keys[kind, i, base + s // WIN] = 1.0
                keys[kind, i, base + 32 + s % WIN] = 1.0
    return shift, keys.astype(jnp.bfloat16)


SHIFT_NP, KEYS_NP = build_tables()


def nn(a, b):
    return jnp.dot(a, b, preferred_element_type=F32)


def nt(a, b):
    return lax.dot_general(a, b, (((1,), (1,)), ((), ())), preferred_element_type=F32)


def tn(a, b):
    return lax.dot_general(a, b, (((0,), (0,)), ((), ())), preferred_element_type=F32)


def vm():
    return pl.BlockSpec(memory_space=pltpu.VMEM)


def sm():
    return pl.BlockSpec(memory_space=pltpu.SMEM)


def params(**kw):
    return pltpu.CompilerParams(vmem_limit_bytes=VMEM_LIMIT, **kw)


def place_window(kind, count, shift, width):
    row = lax.broadcasted_iota(jnp.int32, (count, width), 0)
    lane = lax.broadcasted_iota(jnp.int32, (count, width), 1)
    if kind in (RIGHT, CORNER):
        src = (row // EDGE) * WIN + row % EDGE
    else:
        src = jnp.where(row < SLOTS, row, -100000)
    return (lane == src + shift).astype(F32).astype(BF)


def window_list(dest):
    items = [(FULL, FULLR * j, NWIN * dest + j) for j in range(4)]
    items.append((RIGHT, OFFS[1], NWIN * dest + 4))
    items.append((BOTTOM, OFFS[2], NWIN * 4 + dest))
    if dest == 3:
        items.append((CORNER, OFFS[3], NWIN * NWIN - 1))
    return items


def span_of(window):
    start = SLOTS * window
    low = start // 128 * 128
    high = min(-(-(start + SLOTS) // 128) * 128, IMG_TOK)
    return low, high, start - low


def pack_kernel(where_ref, x_ref, out_ref, rows_ref):
    mine = where_ref[0]
    for dest in range(4):
        if dest != 3:
            rows_ref[OFFS[3] :, :] = jnp.zeros((CORNR, QUART), BF)
        for kind, offset, window in window_list(dest):
            low, high, moved = span_of(window)
            pick = place_window(kind, NQ[kind], moved, high - low)
            rows_ref[offset : offset + NQ[kind], :] = nt(pick, x_ref[:, low:high]).astype(BF)
        slot = jnp.bitwise_xor(mine, dest)
        out_ref[slot, :, :QUART] = rows_ref[:HALF, :]
        out_ref[slot, :, QUART:] = rows_ref[HALF:, :]


def pack(where, x):
    return pl.pallas_call(
        pack_kernel,
        out_shape=jax.ShapeDtypeStruct((4, HALF, 2 * QUART), BF),
        in_specs=[sm(), vm()],
        out_specs=vm(),
        scratch_shapes=[pltpu.VMEM((ROWS, QUART), BF)],
        compiler_params=params(),
        name="pack",
    )(where, x)


def unpack_kernel(where_ref, y0, y1, y2, y3, out_ref, acc_ref, rows_ref):
    mine = where_ref[0]
    acc_ref[...] = jnp.zeros_like(acc_ref)
    for slot, y in enumerate((y0, y1, y2, y3)):
        rows_ref[slot, :HALF, :] = y[:, :QUART]
        rows_ref[slot, HALF:, :] = y[:, QUART:]
    for source in range(4):
        slot = jnp.bitwise_xor(mine, source)
        for kind, offset, window in window_list(source):
            low, high, moved = span_of(window)
            pick = place_window(kind, NQ[kind], moved, high - low)
            acc_ref[:, low:high] += tn(rows_ref[slot, offset : offset + NQ[kind], :], pick)
    out_ref[...] = acc_ref[:, :IMG_TOK].astype(out_ref.dtype)


def unpack(where, pieces, dtype):
    return pl.pallas_call(
        unpack_kernel,
        out_shape=jax.ShapeDtypeStruct((QUART, IMG_TOK), dtype),
        in_specs=[sm()] + [vm()] * 4,
        out_specs=vm(),
        scratch_shapes=[
            pltpu.VMEM((QUART, -(-IMG_TOK // 128) * 128), F32),
            pltpu.VMEM((4, ROWS, QUART), BF),
        ],
        compiler_params=params(),
        name="unpack",
    )(where, *pieces)


def join_pieces(pieces, dst_ref):
    for slot, piece in enumerate(pieces):
        dst_ref[:HALF, QUART * slot : QUART * (slot + 1)] = piece[:, :QUART]
        dst_ref[HALF:, QUART * slot : QUART * (slot + 1)] = piece[:, QUART:]


def split_pieces(src_ref, out_ref):
    for slot in range(4):
        out_ref[slot, :, :QUART] = src_ref[:HALF, QUART * slot : QUART * (slot + 1)]
        out_ref[slot, :, QUART:] = src_ref[HALF:, QUART * slot : QUART * (slot + 1)]


def apack_kernel(
    pick_ref, qkv_w, proj_w, qkv_up, proj_dn, fc1_up, fc2_dn, qkv_dn, fc1_dn, proj_up, fc2_up,
    send_ref, own_ref, row_ref,
):
    step = pl.program_id(0)
    heads = qkv_w.shape[1] // (3 * HD)

    @pl.when(step == 0)
    def _():
        for h in range(heads):
            for t in range(3):
                own_ref[:, QUART * t + HD * h : QUART * t + HD * (h + 1)] = qkv_w[
                    :, HD * (3 * h + t) : HD * (3 * h + t + 1)
                ]
        own_ref[:, 3 * QUART :] = proj_w[...]
        for i, ref in enumerate((qkv_dn, fc1_dn, proj_up, fc2_up)):
            row_ref[:, QUART * i : QUART * (i + 1)] = ref[0]

    half = pick_ref[4]
    send_ref[0, : QUART // 2, :] = own_ref[pl.ds(half * (QUART // 2), QUART // 2), :]
    base = QUART // 2
    for h in range(heads):
        for t in range(3):
            send_ref[0, base : base + RANK, QUART * t + HD * h : QUART * t + HD * (h + 1)] = qkv_up[
                0, :, HD * (3 * h + t) : HD * (3 * h + t + 1)
            ]
    send_ref[0, base : base + RANK, 3 * QUART :] = proj_dn[0]
    send_ref[0, base + RANK : base + 2 * RANK, :] = fc1_up[0]
    send_ref[0, base + 2 * RANK : base + 3 * RANK, :] = fc2_dn[0]


def apack(pick, qkv_w, proj_w, qkv_up, proj_dn, fc1_up, fc2_dn, qkv_dn, fc1_dn, proj_up, fc2_up):
    whole = lambda shape: pl.BlockSpec(shape, lambda j, p: (0, 0))
    each = lambda n: pl.BlockSpec((1, RANK, n), lambda j, p: (p[j], 0, 0))
    mine = lambda n: pl.BlockSpec((1, RANK, n), lambda j, p: (p[0], 0, 0))
    return pl.pallas_call(
        apack_kernel,
        out_shape=(
            jax.ShapeDtypeStruct((4, QUART // 2 + 3 * RANK, D), BF),
            jax.ShapeDtypeStruct((QUART, D), BF),
            jax.ShapeDtypeStruct((RANK, D), BF),
        ),
        grid_spec=pltpu.PrefetchScalarGridSpec(
            num_scalar_prefetch=1,
            grid=(4,),
            in_specs=[
                whole(qkv_w.shape), whole(proj_w.shape),
                each(qkv_up.shape[2]), each(proj_dn.shape[2]), each(fc1_up.shape[2]), each(fc2_dn.shape[2]),
                mine(QUART), mine(QUART), mine(QUART), mine(QUART),
            ],
            out_specs=(
                pl.BlockSpec((1, QUART // 2 + 3 * RANK, D), lambda j, p: (j, 0, 0)),
                whole((QUART, D)),
                whole((RANK, D)),
            ),
        ),
        compiler_params=params(),
        name="adapter_pack",
    )(pick, qkv_w, proj_w, qkv_up, proj_dn, fc1_up, fc2_dn, qkv_dn, fc1_dn, proj_up, fc2_up)


def block_rows(part, base, j, half):
    if j == 0:
        return [(0, base, QUART)]
    hh = QUART // 2
    return [
        (half * hh, base + QUART + hh * (j - 1), hh),
        ((1 - half) * hh, base + QUART + 3 * hh + hh * (j - 1), hh),
    ]


def prep1_kernel(
    where_ref, g0, gy, gc, a0, a1, a2, a3,
    wqkv_ref, wproj_ref, dqkv, uqkv, dproj, uproj, d1, u1, d2, u2,
):
    half = where_ref[1]
    tall = g0.shape[0]
    parts = ((g0, 0), (gc, 0), (gy, 0), (gc, tall))
    cb = QUART // 2
    for j, a in enumerate((a0, a1, a2, a3)):
        for t in range(3):
            uqkv[:, D * t + QUART * j : D * t + QUART * (j + 1)] = a[
                cb : cb + RANK, QUART * t : QUART * (t + 1)
            ]
        dproj[:, QUART * j : QUART * (j + 1)] = a[cb : cb + RANK, 3 * QUART :]
        u1[:, D * j : D * (j + 1)] = a[cb + RANK : cb + 2 * RANK, :]
        d2[:, D * j : D * (j + 1)] = a[cb + 2 * RANK : cb + 3 * RANK, :]
    for k, (ref, base) in enumerate(parts):
        rows = slice(base + tall - RANK, base + tall)
        for i, dst in enumerate((dqkv, d1, uproj, u2)):
            dst[:, QUART * k : QUART * (k + 1)] = ref[rows, QUART * i : QUART * (i + 1)]
    for k, (ref, base) in enumerate(parts):
        for j in range(4):
            for dst, src, count in block_rows(ref, base, j, half):
                if j == 0:
                    rows = pl.ds(QUART * k, count)
                    prow = pl.ds(QUART * j, count)
                else:
                    rows = pl.ds(pl.multiple_of(QUART * k + dst, 32), count)
                    prow = pl.ds(pl.multiple_of(QUART * j + dst, 32), count)
                for t in range(3):
                    wqkv_ref[rows, D * t + QUART * j : D * t + QUART * (j + 1)] = ref[
                        src : src + count, QUART * t : QUART * (t + 1)
                    ]
                wproj_ref[prow, QUART * k : QUART * (k + 1)] = ref[src : src + count, 3 * QUART :]
    for k in range(4):
        rows = slice(QUART * k, QUART * (k + 1))
        for t in range(3):
            cols = slice(D * t, D * (t + 1))
            low = tn(dqkv[:, rows], uqkv[:, cols])
            wqkv_ref[rows, cols] = (wqkv_ref[rows, cols].astype(F32) + low).astype(BF)
        low = tn(dproj[:, rows], uproj[...])
        wproj_ref[rows, :] = (wproj_ref[rows, :].astype(F32) + low).astype(BF)


def prep1(where, g0, gy, gc, pieces):
    s = lambda *shape: jax.ShapeDtypeStruct(shape, BF)
    return pl.pallas_call(
        prep1_kernel,
        out_shape=(
            s(D, 3 * D), s(D, D), s(RANK, D), s(RANK, 3 * D), s(RANK, D), s(RANK, D),
            s(RANK, D), s(RANK, 4 * D), s(RANK, 4 * D), s(RANK, D),
        ),
        in_specs=[sm()] + [vm()] * 7,
        out_specs=[vm()] * 10,
        compiler_params=params(),
        name="attention_weights",
    )(where, g0, gy, gc, *pieces)


def prep2_kernel(where_ref, g0, gy, gc, d1, u1, d2, u2, w1_ref, w2_ref):
    half = where_ref[1]
    tall = g0.shape[0]
    parts = ((g0, 0), (gc, 0), (gy, 0), (gc, tall))
    for k, (ref, base) in enumerate(parts):
        for j in range(4):
            cols = slice(D * j, D * (j + 1))
            for dst, src, count in block_rows(ref, base, j, half):
                rows = pl.ds(QUART * k, count) if j == 0 else pl.ds(pl.multiple_of(QUART * k + dst, 32), count)
                w1_ref[rows, cols] = ref[src : src + count, :D]
                w2_ref[rows, cols] = ref[src : src + count, D:]
    for k in range(4):
        rows = slice(QUART * k, QUART * (k + 1))
        for j in range(4):
            cols = slice(D * j, D * (j + 1))
            low = tn(d1[:, rows], u1[:, cols])
            w1_ref[rows, cols] = (w1_ref[rows, cols].astype(F32) + low).astype(BF)
            low = tn(u2[:, rows], d2[:, cols])
            w2_ref[rows, cols] = (w2_ref[rows, cols].astype(F32) + low).astype(BF)


def prep2(where, g0, gy, gc, d1, u1, d2, u2):
    s = lambda *shape: jax.ShapeDtypeStruct(shape, BF)
    return pl.pallas_call(
        prep2_kernel,
        out_shape=(s(D, 4 * D), s(D, 4 * D)),
        in_specs=[sm()] + [vm()] * 7,
        out_specs=[vm()] * 2,
        compiler_params=params(),
        name="mlp_weights",
    )(where, g0, gy, gc, d1, u1, d2, u2)


def normalize(values):
    center = jnp.sum(values, axis=1, keepdims=True) / D
    shifted = values - center
    inv_std = lax.rsqrt(jnp.sum(shifted * shifted, axis=1, keepdims=True) / D + EPSILON)
    return shifted * inv_std, inv_std


def norm_back(grad, normed, inv_std):
    first = jnp.sum(grad, axis=1, keepdims=True) / D
    second = jnp.sum(grad * normed, axis=1, keepdims=True) / D
    return inv_std * (grad - first - normed * second)


def barrel(values, amount, left):
    for bit in (1, 2, 4, 8):
        moved = pltpu.roll(values, (128 - bit) if left else bit, 1)
        values = jnp.where((amount & bit) != 0, moved, values)
    return values


def low_half(count):
    return lax.broadcasted_iota(jnp.int32, (count, 128), 1) < HD


def pad_rows(tile):
    if tile.shape[0] == KEYS:
        return tile
    return jnp.concatenate([tile, jnp.zeros((KEYS - tile.shape[0], tile.shape[1]), tile.dtype)], axis=0)


def attend_window(kind, row0, qkv_ref, att_ref, probs_ref, rel_ref, shift_ref, keys_ref):
    count = NQ[kind]
    rows = pl.ds(row0, count)
    low_q, low_k = low_half(count), low_half(KEYS)
    amount = shift_ref[kind, :count, :]
    onehot = keys_ref[kind]
    dead = jnp.where(lax.broadcasted_iota(jnp.int32, (1, KEYS), 1) < SLOTS, 0.0, -1e30)
    for pair in range(D // 128):
        cols = slice(128 * pair, 128 * (pair + 1))
        q_tile = qkv_ref[rows, cols]
        k_tile = pad_rows(qkv_ref[rows, D + 128 * pair : D + 128 * (pair + 1)] * BF(HD**-0.5))
        v_tile = pad_rows(qkv_ref[rows, 2 * D + 128 * pair : 2 * D + 128 * (pair + 1)])
        rel = barrel(nn(q_tile, rel_ref[...]), amount, True).astype(BF)
        halves = []
        for odd in range(2):
            if odd:
                q_aug = jnp.where(low_q, rel, q_tile)
                k_aug = jnp.where(low_k, onehot, k_tile)
            else:
                q_aug = jnp.where(low_q, q_tile, rel)
                k_aug = jnp.where(low_k, k_tile, onehot)
            scores = nt(q_aug, k_aug) + dead
            exponent = jnp.exp(scores - jnp.max(scores, axis=1, keepdims=True))
            total = jnp.sum(exponent, axis=1, keepdims=True)
            probs = (exponent * (1.0 / total)).astype(BF)
            probs_ref[2 * pair + odd, rows, :] = probs
            halves.append(nn(probs, v_tile))
        att_ref[rows, cols] = jnp.where(low_q, halves[0], halves[1]).astype(BF)


def attention_kernel(
    x0, x1, x2, x3, gain_ref, wqkv_ref, wproj_ref, rel_ref, shift_ref, keys_ref,
    x_ref, qkv_ref, att_ref, probs_ref, middle_ref, hid_ref,
):
    join_pieces((x0, x1, x2, x3), x_ref)
    gain = gain_ref[...]

    def norm_step(i, carry):
        rows = pl.ds(pl.multiple_of(i * 112, 16), 112)
        normed, _ = normalize(x_ref[rows, :].astype(F32))
        hid_ref[rows, :] = (normed * gain).astype(BF)
        return carry

    lax.fori_loop(0, ROWS // 112, norm_step, 0)
    for t in range(3):
        cols = slice(D * t, D * (t + 1))
        qkv_ref[:, cols] = nn(hid_ref[...], wqkv_ref[:, cols]).astype(BF)

    def full_step(w, carry):
        attend_window(
            FULL, pl.multiple_of(w * FULLR, 16), qkv_ref, att_ref, probs_ref, rel_ref, shift_ref, keys_ref
        )
        return carry

    lax.fori_loop(0, 4, full_step, 0)
    for kind in (RIGHT, BOTTOM, CORNER):
        attend_window(kind, OFFS[kind], qkv_ref, att_ref, probs_ref, rel_ref, shift_ref, keys_ref)
    middle_ref[...] = x_ref[...].astype(F32) + nn(att_ref[...], wproj_ref[...])


def attention(pieces, gain, wqkv, wproj, rel, shift, keys):
    s = lambda *shape, dtype=BF: jax.ShapeDtypeStruct(shape, dtype)
    return pl.pallas_call(
        attention_kernel,
        out_shape=(
            s(ROWS, D), s(ROWS, 3 * D), s(ROWS, D), s(D // HD, ROWS, KEYS), s(ROWS, D, dtype=F32), s(ROWS, D),
        ),
        in_specs=[vm()] * 10,
        out_specs=[vm()] * 6,
        compiler_params=params(),
        name="attention_forward",
    )(*pieces, gain, wqkv, wproj, rel, shift, keys)


CHUNK = 512


def mlp_kernel(
    where_ref, middle_ref, g0, g1, g2, g3, gain_ref, w1_ref, w2_ref, d1, u1, d2, u2,
    out_ref, gmid_ref, down1, up1, down2, up2,
    gm_ref, out_rows, h2_ref, acc_mlp, acc_gh, gu1, ad2,
):
    join_pieces((g0, g1, g2, g3), gm_ref)
    gain = gain_ref[...]
    down1[...] = jnp.zeros_like(down1)
    up1[...] = jnp.zeros_like(up1)
    down2[...] = jnp.zeros_like(down2)
    up2[...] = jnp.zeros_like(up2)

    def tile_step(t, carry):
        rows = pl.ds(pl.multiple_of(t * HALF, 16), HALF)
        normed, _ = normalize(middle_ref[rows, :])
        h2 = (normed * gain).astype(BF)
        h2_ref[...] = h2
        gm = gm_ref[rows, :]
        ad1 = nt(d1[...], h2).astype(BF)
        gu2 = nt(u2[...], gm).astype(BF)
        acc_mlp[...] = jnp.zeros_like(acc_mlp)
        acc_gh[...] = jnp.zeros_like(acc_gh)
        gu1[...] = jnp.zeros_like(gu1)
        ad2[...] = jnp.zeros_like(ad2)

        def chunk_step(c, inner_carry):
            cols = pl.ds(pl.multiple_of(c * CHUNK, CHUNK), CHUNK)
            w1 = w1_ref[:, cols]
            w2 = w2_ref[:, cols]
            inner = nn(h2_ref[...], w1)
            gact = nn(gm_ref[rows, :], w2)
            half = 0.5 * (1.0 + lax.erf(inner * 2**-0.5))
            act = (inner * half).astype(BF)
            slope = half + inner * (jnp.exp(-0.5 * inner * inner) * (2 * np.pi) ** -0.5)
            ginner = (gact * slope).astype(BF)
            acc_mlp[...] += nt(act, w2)
            acc_gh[...] += nt(ginner, w1)
            up1[:, cols] += nn(ad1, ginner)
            gu1[...] += nt(u1[:, cols], ginner)
            ad2[...] += nt(d2[:, cols], act)
            down2[:, cols] += nn(gu2, act)
            return inner_carry

        lax.fori_loop(0, 4 * D // CHUNK, chunk_step, 0)
        down1[...] += nn(gu1[...].astype(BF), h2_ref[...])
        up2[...] += nn(ad2[...].astype(BF), gm_ref[rows, :])
        middle = middle_ref[rows, :]
        out_rows[rows, :] = (middle + acc_mlp[...]).astype(BF)
        normed, inv_std = normalize(middle)
        gmid_ref[rows, :] = gm_ref[rows, :].astype(F32) + norm_back(acc_gh[...] * gain, normed, inv_std)
        return carry

    lax.fori_loop(0, 2, tile_step, 0)
    split_pieces(out_rows, out_ref)


def mlp(where, middle, pieces, gain, w1, w2, d1, u1, d2, u2):
    s = lambda *shape, dtype=F32: jax.ShapeDtypeStruct(shape, dtype)
    return pl.pallas_call(
        mlp_kernel,
        out_shape=(
            s(4, HALF, 2 * QUART, dtype=BF), s(ROWS, D),
            s(RANK, D), s(RANK, 4 * D), s(RANK, 4 * D), s(RANK, D),
        ),
        in_specs=[sm()] + [vm()] * 12,
        out_specs=[vm()] * 6,
        scratch_shapes=[
            pltpu.VMEM((ROWS, D), BF), pltpu.VMEM((ROWS, D), BF), pltpu.VMEM((HALF, D), BF),
            pltpu.VMEM((HALF, D), F32), pltpu.VMEM((HALF, D), F32),
            pltpu.VMEM((RANK, HALF), F32), pltpu.VMEM((RANK, HALF), F32),
        ],
        compiler_params=params(),
        name="mlp_forward_backward",
    )(where, middle, *pieces, gain, w1, w2, d1, u1, d2, u2)


def attend_back_window(
    kind, row0, qkv_ref, probs_ref, gatt_ref, gqkv_ref, rel_ref, shift_ref, keys_ref
):
    count = NQ[kind]
    rows = pl.ds(row0, count)
    low_q, low_k = low_half(count), low_half(KEYS)
    amount = shift_ref[kind, :count, :]
    onehot = keys_ref[kind]
    for pair in range(D // 128):
        cols = slice(128 * pair, 128 * (pair + 1))
        kcols = slice(D + 128 * pair, D + 128 * (pair + 1))
        vcols = slice(2 * D + 128 * pair, 2 * D + 128 * (pair + 1))
        q_tile = qkv_ref[rows, cols]
        k_tile = pad_rows(qkv_ref[rows, kcols] * BF(HD**-0.5))
        v_tile = pad_rows(qkv_ref[rows, vcols])
        go_tile = gatt_ref[rows, cols]
        q_t = q_tile.T
        go_t = go_tile.T
        gq, gk, gv = [], [], []
        for odd in range(2):
            go_half = jnp.where(low_q, 0, go_tile) if odd else jnp.where(low_q, go_tile, 0)
            k_aug = jnp.where(low_k, onehot, k_tile) if odd else jnp.where(low_k, k_tile, onehot)
            probs = probs_ref[2 * pair + odd, rows, :]
            gp = nt(go_half.astype(BF), v_tile)
            exact = probs.astype(F32)
            weighted = exact * gp
            gs = (weighted - exact * jnp.sum(weighted, axis=1, keepdims=True)).astype(BF)
            side = slice(HD * odd, HD * (odd + 1))
            gv.append(nn(go_t[side, :], probs))
            gk.append(nn(q_t[side, :], gs))
            gq.append(nn(gs, k_aug))
        sums = barrel(jnp.where(low_q, gq[1], gq[0]), amount, False).astype(BF)
        gqkv_ref[rows, cols] = (jnp.where(low_q, gq[0], gq[1]) + nt(sums, rel_ref[...])).astype(BF)
        gk_tile = (jnp.concatenate(gk, axis=0) * HD**-0.5).astype(BF).T
        gv_tile = jnp.concatenate(gv, axis=0).astype(BF).T
        gqkv_ref[rows, kcols] = gk_tile[:count, :]
        gqkv_ref[rows, vcols] = gv_tile[:count, :]


def attention_back_kernel(
    where_ref, gmid_ref, x_ref, hid_ref, qkv_ref, att_ref, probs_ref, gain_ref, wqkv_ref, wproj_ref,
    rel_ref, shift_ref, keys_ref, dqkv, uqkv, dproj, uproj,
    out_ref, down_q, up_q, down_p, up_p,
    gb_ref, gatt_ref, gqkv_ref, gh_ref, out_rows,
):
    gb_ref[...] = gmid_ref[...].astype(BF)
    gatt_ref[...] = nt(gb_ref[...], wproj_ref[...]).astype(BF)
    up_p[...] = nn(nt(dproj[...], att_ref[...]).astype(BF), gb_ref[...])
    down_p[...] = nn(nt(uproj[...], gb_ref[...]).astype(BF), att_ref[...])

    def full_step(w, carry):
        attend_back_window(
            FULL, pl.multiple_of(w * FULLR, 16), qkv_ref, probs_ref, gatt_ref, gqkv_ref, rel_ref, shift_ref, keys_ref
        )
        return carry

    lax.fori_loop(0, 4, full_step, 0)
    for kind in (RIGHT, BOTTOM, CORNER):
        attend_back_window(
            kind, OFFS[kind], qkv_ref, probs_ref, gatt_ref, gqkv_ref, rel_ref, shift_ref, keys_ref
        )
    up_q[...] = nn(nt(dqkv[...], hid_ref[...]).astype(BF), gqkv_ref[...])
    down_q[...] = nn(nt(uqkv[...], gqkv_ref[...]).astype(BF), hid_ref[...])
    gh_ref[...] = nt(gqkv_ref[...], wqkv_ref[...])
    gain = gain_ref[...]

    def norm_step(i, carry):
        rows = pl.ds(pl.multiple_of(i * 112, 16), 112)
        normed, inv_std = normalize(x_ref[rows, :].astype(F32))
        back = norm_back(gh_ref[rows, :] * gain, normed, inv_std)
        out_rows[rows, :] = (gmid_ref[rows, :] + back).astype(BF)
        return carry

    lax.fori_loop(0, ROWS // 112, norm_step, 0)
    split_pieces(out_rows, out_ref)


def attention_back(where, gmid, x, hid, qkv, att, probs, gain, wqkv, wproj, rel, shift, keys, dqkv, uqkv, dproj, uproj):
    s = lambda *shape, dtype=F32: jax.ShapeDtypeStruct(shape, dtype)
    return pl.pallas_call(
        attention_back_kernel,
        out_shape=(
            s(4, HALF, 2 * QUART, dtype=BF), s(RANK, D), s(RANK, 3 * D), s(RANK, D), s(RANK, D),
        ),
        in_specs=[sm()] + [vm()] * 16,
        out_specs=[vm()] * 5,
        scratch_shapes=[
            pltpu.VMEM((ROWS, D), BF), pltpu.VMEM((ROWS, D), BF), pltpu.VMEM((ROWS, 3 * D), BF),
            pltpu.VMEM((ROWS, D), F32), pltpu.VMEM((ROWS, D), BF),
        ],
        compiler_params=params(),
        name="attention_backward",
    )(where, gmid, x, hid, qkv, att, probs, gain, wqkv, wproj, rel, shift, keys, dqkv, uqkv, dproj, uproj)


def grad_pack_kernel(where_ref, down_q, up_q, down_p, up_p, down1, up1, down2, up2, out_ref, buf_ref):
    mine = where_ref[0]
    for k in range(4):
        for i, ref in enumerate((down_q, down1, up_p, up2)):
            buf_ref[k, :RANK, QUART * i : QUART * (i + 1)] = ref[:, QUART * k : QUART * (k + 1)]
    for dest in range(4):
        k = jnp.bitwise_xor(mine, dest)
        ranks = slice(RANK // 4 * dest, RANK // 4 * (dest + 1))
        for j in range(4):
            base = RANK + 12 * j
            for t in range(3):
                buf_ref[k, base : base + 4, QUART * t : QUART * (t + 1)] = up_q[
                    ranks, D * t + QUART * j : D * t + QUART * (j + 1)
                ]
            buf_ref[k, base : base + 4, 3 * QUART :] = down_p[ranks, QUART * j : QUART * (j + 1)]
            buf_ref[k, base + 4 : base + 8, :] = up1[ranks, D * j : D * (j + 1)]
            buf_ref[k, base + 8 : base + 12, :] = down2[ranks, D * j : D * (j + 1)]
    out_ref[...] = buf_ref[...].astype(BF)


def grad_pack(where, *grads):
    return pl.pallas_call(
        grad_pack_kernel,
        out_shape=jax.ShapeDtypeStruct((4, 4 * RANK, D), BF),
        in_specs=[sm()] + [vm()] * 8,
        out_specs=vm(),
        scratch_shapes=[pltpu.VMEM((4, 4 * RANK, D), F32)],
        compiler_params=params(),
        name="adapter_grad_pack",
    )(where, *grads)


def grad_sum_kernel(g0, g1, g2, g3, out_ref, buf_ref):
    total = g0[...].astype(F32) + g1[...].astype(F32) + g2[...].astype(F32) + g3[...].astype(F32)
    buf_ref[...] = jnp.zeros_like(buf_ref)
    for j in range(4):
        buf_ref[:RANK, :] = total[:RANK, :]
        buf_ref[RANK : RANK + 12, :] = total[RANK + 12 * j : RANK + 12 * (j + 1), :]
        out_ref[j] = buf_ref[...].astype(BF)


def grad_sum(pieces):
    return pl.pallas_call(
        grad_sum_kernel,
        out_shape=jax.ShapeDtypeStruct((4, 2 * RANK, D), BF),
        in_specs=[vm()] * 4,
        out_specs=vm(),
        scratch_shapes=[pltpu.VMEM((2 * RANK, D), F32)],
        compiler_params=params(),
        name="adapter_grad_sum",
    )(*pieces)


def grad_adapters_kernel(index_ref, x_ref, qkv_dn, fc1_dn, proj_up, fc2_up, rest_ref, acc_ref):
    acc_ref[...] = jnp.zeros_like(acc_ref)

    def add(i, carry):
        acc_ref[index_ref[i]] += x_ref[i].astype(F32)
        return carry

    lax.fori_loop(0, x_ref.shape[0], add, 0)
    for i, ref in enumerate((qkv_dn, fc1_dn, proj_up, fc2_up)):
        ref[...] = acc_ref[:, :RANK, QUART * i : QUART * (i + 1)]
    rest_ref[...] = acc_ref[:, RANK:, :].astype(BF)


def grad_adapters(index, x):
    s = lambda n, dtype=F32: jax.ShapeDtypeStruct((ADAPT, RANK, n), dtype)
    return pl.pallas_call(
        grad_adapters_kernel,
        out_shape=(s(QUART), s(QUART), s(QUART), s(QUART), s(D, BF)),
        in_specs=[sm(), vm()],
        out_specs=[vm()] * 5,
        scratch_shapes=[pltpu.VMEM((ADAPT, 2 * RANK, D), F32)],
        compiler_params=params(),
        name="adapter_grad_by_adapter",
    )(index, x)


def grad_join_kernel(where_ref, r0, r1, r2, r3, qkv_up, proj_dn, fc1_up, fc2_dn, buf_ref):
    mine = where_ref[0]
    heads = qkv_up.shape[2] // (3 * HD)
    for k, ref in enumerate((r0, r1, r2, r3)):
        buf_ref[jnp.bitwise_xor(mine, k)] = ref[...].astype(F32)
    for source in range(4):
        ranks = slice(RANK // 4 * source, RANK // 4 * (source + 1))
        for h in range(heads):
            for t in range(3):
                qkv_up[:, ranks, HD * (3 * h + t) : HD * (3 * h + t + 1)] = buf_ref[
                    source, :, 0:4, QUART * t + HD * h : QUART * t + HD * (h + 1)
                ]
        proj_dn[:, ranks, :] = buf_ref[source, :, 0:4, 3 * QUART :]
        fc1_up[:, ranks, :] = buf_ref[source, :, 4:8, :]
        fc2_dn[:, ranks, :] = buf_ref[source, :, 8:12, :]


def grad_join(where, pieces):
    s = lambda n: jax.ShapeDtypeStruct((ADAPT, RANK, n), F32)
    return pl.pallas_call(
        grad_join_kernel,
        out_shape=(s(3 * QUART), s(QUART), s(D), s(D)),
        in_specs=[sm()] + [vm()] * 4,
        out_specs=[vm()] * 4,
        scratch_shapes=[pltpu.VMEM((4, ADAPT, RANK, D), F32)],
        compiler_params=params(),
        name="adapter_grad_join",
    )(where, *pieces)


def flip(values, axis, distance):
    size = lax.axis_size(axis)
    return lax.ppermute(values, axis, [(i, i ^ distance) for i in range(size)])


def exchange(slots, axis):
    return [slots[0]] + [flip(slots[k], axis, k) for k in range(1, 4)]


def gather_blocks(own, halves_own, extra_rows):
    mine = [flip(halves_own[j], "col", j) for j in range(1, 4)]
    a = jnp.concatenate([m[: QUART // 2] for m in mine], axis=0)
    b = flip(a, "dp", 1)
    parts = [own, a, b] + extra_rows
    g = jnp.concatenate(parts, axis=0)
    gy = flip(g, "row", 2)
    gc = flip(jnp.concatenate([g, gy], axis=0), "row", 1)
    return g, gy, gc, mine


def rel_matrix(rel_h, rel_w):
    pad = jnp.zeros((32 - (2 * WIN - 1), HD), BF)
    block = jnp.concatenate([rel_h[::-1], pad, rel_w[::-1], pad], axis=0).T
    zero = jnp.zeros((HD, HD), BF)
    return jnp.concatenate(
        [jnp.concatenate([zero, block], axis=1), jnp.concatenate([block, zero], axis=1)], axis=0
    )


def body(
    tokens, grad_out, adapter_index, norm1_gain, norm2_gain, qkv_weight, proj_weight, fc1_weight, fc2_weight,
    rel_h, rel_w, qkv_down, qkv_up, proj_down, proj_up, fc1_down, fc1_up, fc2_down, fc2_up,
):
    members = lax.axis_size("col")
    batches = lax.axis_size("dp")
    row_index, col_index, dp_index = lax.axis_index("row"), lax.axis_index("col"), lax.axis_index("dp")
    half = dp_index % 2
    where = jnp.stack([row_index, half]).astype(jnp.int32)
    slot_images = (
        jnp.bitwise_xor(dp_index, jnp.arange(batches, dtype=jnp.int32))[:, None] * members
        + jnp.bitwise_xor(col_index, jnp.arange(members, dtype=jnp.int32))[None, :]
    ).reshape(-1)
    slot_adapters = jnp.sum(
        jnp.where(
            slot_images[:, None] == jnp.arange(adapter_index.shape[0], dtype=jnp.int32)[None, :],
            adapter_index[:, 0][None, :],
            0,
        ),
        axis=1,
    )
    pick = jnp.concatenate([slot_adapters[:4], half[None]]).astype(jnp.int32)
    swap = lambda m: jnp.swapaxes(m, 1, 2)

    token_slots = pack(where, tokens)
    x_pieces = exchange(token_slots, "row")

    send, own, row_adapters = apack(
        pick, qkv_weight, proj_weight, qkv_up, swap(proj_down), fc1_up, swap(fc2_down),
        swap(qkv_down), swap(fc1_down), proj_up, fc2_up,
    )
    g, gy, gc, arrived = gather_blocks(own, send, [row_adapters])
    own2 = jnp.concatenate([fc1_weight, fc2_weight], axis=1)
    half2 = lax.dynamic_slice_in_dim(own2, half * (QUART // 2), QUART // 2, 0)
    g2, g2y, g2c, _ = gather_blocks(own2, [half2] * 4, [])
    grad_slots = pack(where, grad_out)
    g_pieces = exchange(grad_slots, "row")

    gains = jnp.stack([norm1_gain, norm2_gain])
    gain_slots = [gains] + [flip(gains, "row", k) for k in range(1, 4)]
    gain_all = jnp.concatenate(gain_slots, axis=1).astype(F32)
    gain1, gain2 = gain_all[0:1], gain_all[1:2]
    rel = rel_matrix(rel_h, rel_w)
    shift, keys = jnp.asarray(SHIFT_NP), jnp.asarray(KEYS_NP)

    wqkv, wproj, dqkv, uqkv, dproj, uproj, d1, u1, d2, u2 = prep1(where, g, gy, gc, [send[0]] + arrived)
    x, qkv, att, probs, middle, hid = attention(x_pieces, gain1, wqkv, wproj, rel, shift, keys)
    w1, w2 = prep2(where, g2, g2y, g2c, d1, u1, d2, u2)
    out_slots, gmid, down1, up1, down2, up2 = mlp(where, middle, g_pieces, gain2, w1, w2, d1, u1, d2, u2)
    result = unpack(where, exchange(out_slots, "row"), BF)
    back_slots, down_q, up_q, down_p, up_p = attention_back(
        where, gmid, x, hid, qkv, att, probs, gain1, wqkv, wproj, rel, shift, keys, dqkv, uqkv, dproj, uproj
    )
    grad_tokens = unpack(where, exchange(back_slots, "row"), F32)

    packed = grad_pack(where, down_q, up_q, down_p, up_p, down1, up1, down2, up2)
    summed = grad_sum(exchange(packed, "row"))
    images = jnp.stack(exchange(summed, "col"))
    step = 1
    while step < batches:
        images = jnp.concatenate([images, flip(images, "dp", step)], axis=0)
        step *= 2
    qkv_dn, fc1_dn, proj_upg, fc2_upg, rest = grad_adapters(slot_adapters.astype(jnp.int32), images)
    rests = [rest] + [flip(rest, "row", k) for k in range(1, 4)]
    qkv_upg, proj_dn, fc1_upg, fc2_dn = grad_join(where, rests)
    return (
        result, grad_tokens,
        swap(qkv_dn), qkv_upg, swap(proj_dn), proj_upg, swap(fc1_dn), fc1_upg, swap(fc2_dn), fc2_upg,
    )


def solution(mesh):
    return jax.shard_map(
        body,
        mesh=mesh,
        in_specs=(
            P("row", ("dp", "col")), P("row", ("dp", "col")), P(), P("row"), P("row"),
            P("row", "col"), P("col", "row"), P("row", "col"), P("row", "col"), P(), P(),
            P(None, "row", None), P(None, None, "col"), P(None, "col", None), P(None, None, "row"),
            P(None, "row", None), P(None, None, "col"), P(None, "col", None), P(None, None, "row"),
        ),
        out_specs=(
            P("row", ("dp", "col")), P("row", ("dp", "col")),
            P(None, "row", None), P(None, None, "col"), P(None, "col", None), P(None, None, "row"),
            P(None, "row", None), P(None, None, "col"), P(None, "col", None), P(None, None, "row"),
        ),
        check_vma=False,
    )
```

```python
import functools

import jax
import jax.numpy as jnp
import numpy as np
from jax import lax
from jax.experimental import pallas as pl
from jax.experimental.pallas import tpu as pltpu
from jax.sharding import PartitionSpec as P

D = 768
HD = 64
WIN = 14
SLOTS = WIN * WIN
SIDE = 64
ADAPT = 8
NWIN = 5
IMG_TOK = NWIN * NWIN * SLOTS
RANK = 16
EDGE = SIDE - (NWIN - 1) * WIN
QUART = D // 4
FULLR = 208
KEYS = 208
EDGER = EDGE * WIN
CORNR = EDGE * EDGE
ROWS = 4 * FULLR + 2 * EDGER + CORNR
HALF = ROWS // 2
HBLK = QUART // 2
EPSILON = 1e-06
BF = jnp.bfloat16
F32 = jnp.float32
VMEM_LIMIT = 60 * 1024 * 1024

FULL, RIGHT, BOTTOM, CORNER = 0, 1, 2, 3
NQ = (FULLR, EDGER, EDGER, CORNR)
OFFS = (0, 4 * FULLR, 4 * FULLR + EDGER, 4 * FULLR + 2 * EDGER)


def slot_order(kind):
    rows = EDGE if kind in (BOTTOM, CORNER) else WIN
    cols = EDGE if kind in (RIGHT, CORNER) else WIN
    kept = [a * WIN + b for a in range(rows) for b in range(cols)]
    rest = [s for s in range(SLOTS) if s not in set(kept)]
    return kept, kept + rest


def build_tables():
    shift = np.zeros((4, FULLR, 128), np.int32)
    keys = np.zeros((4, KEYS, 128), np.float32)
    for kind in range(4):
        kept, order = slot_order(kind)
        for i, s in enumerate(kept):
            for base in (0, 64):
                shift[kind, i, base : base + 32] = WIN - 1 - s // WIN
                shift[kind, i, base + 32 : base + 64] = WIN - 1 - s % WIN
        spare = order[0] if kind == FULL else order[-1]
        for i, s in enumerate(order + [spare] * (KEYS - SLOTS)):
            for base in (0, 64):
                keys[kind, i, base + s // WIN] = 1.0
                keys[kind, i, base + 32 + s % WIN] = 1.0
    return shift, keys.astype(jnp.bfloat16)


SHIFT_NP, KEYS_NP = build_tables()


def nn(a, b):
    return jnp.dot(a, b, preferred_element_type=F32)


def nt(a, b):
    return lax.dot_general(a, b, (((1,), (1,)), ((), ())), preferred_element_type=F32)


def tn(a, b):
    return lax.dot_general(a, b, (((0,), (0,)), ((), ())), preferred_element_type=F32)


def vm():
    return pl.BlockSpec(memory_space=pltpu.VMEM)


def sm():
    return pl.BlockSpec(memory_space=pltpu.SMEM)


def params(**kw):
    return pltpu.CompilerParams(vmem_limit_bytes=VMEM_LIMIT, **kw)


def cost(us):
    return pl.CostEstimate(flops=int(us * 9e8), transcendentals=0, bytes_accessed=0)


def place_window(kind, count, shift, width, spare=-100000):
    row = lax.broadcasted_iota(jnp.int32, (count, width), 0)
    lane = lax.broadcasted_iota(jnp.int32, (count, width), 1)
    if kind in (RIGHT, CORNER):
        src = (row // EDGE) * WIN + row % EDGE
    else:
        src = jnp.where(row < SLOTS, row, spare)
    return (lane == src + shift).astype(F32).astype(BF)


def window_list(dest):
    items = [(FULL, FULLR * j, NWIN * dest + j) for j in range(4)]
    items.append((RIGHT, OFFS[1], NWIN * dest + 4))
    items.append((BOTTOM, OFFS[2], NWIN * 4 + dest))
    if dest == 3:
        items.append((CORNER, OFFS[3], NWIN * NWIN - 1))
    return items


def span_of(window):
    start = SLOTS * window
    low = start // 128 * 128
    high = min(-(-(start + SLOTS) // 128) * 128, IMG_TOK)
    return low, high, start - low


def pack_kernel(where_ref, x_ref, out_ref, rows_ref, *, spare):
    mine = where_ref[0]
    for dest in range(4):
        if dest != 3:
            rows_ref[OFFS[3] :, :] = jnp.zeros((CORNR, QUART), BF)
        for kind, offset, window in window_list(dest):
            low, high, moved = span_of(window)
            pick = place_window(kind, NQ[kind], moved, high - low, spare)
            rows_ref[offset : offset + NQ[kind], :] = nt(pick, x_ref[:, low:high]).astype(BF)
        slot = jnp.bitwise_xor(mine, dest)
        out_ref[slot, :, :QUART] = rows_ref[:HALF, :]
        out_ref[slot, :, QUART:] = rows_ref[HALF:, :]


def pack(where, x, spare=-100000):
    return pl.pallas_call(
        functools.partial(pack_kernel, spare=spare),
        out_shape=jax.ShapeDtypeStruct((4, HALF, 2 * QUART), BF),
        in_specs=[sm(), vm()],
        out_specs=vm(),
        scratch_shapes=[pltpu.VMEM((ROWS, QUART), BF)],
        compiler_params=params(),
        cost_estimate=cost(4),
        name="pack",
    )(where, x)


def unpack_kernel(where_ref, y0, y1, y2, y3, out_ref, acc_ref, rows_ref):
    mine = where_ref[0]
    acc_ref[...] = jnp.zeros_like(acc_ref)
    for slot, y in enumerate((y0, y1, y2, y3)):
        rows_ref[slot, :HALF, :] = y[:, :QUART]
        rows_ref[slot, HALF:, :] = y[:, QUART:]
    for source in range(4):
        slot = jnp.bitwise_xor(mine, source)
        for kind, offset, window in window_list(source):
            low, high, moved = span_of(window)
            pick = place_window(kind, NQ[kind], moved, high - low)
            acc_ref[:, low:high] += tn(rows_ref[slot, offset : offset + NQ[kind], :], pick)
    out_ref[...] = acc_ref[:, :IMG_TOK].astype(out_ref.dtype)


def unpack(where, pieces, dtype):
    return pl.pallas_call(
        unpack_kernel,
        out_shape=jax.ShapeDtypeStruct((QUART, IMG_TOK), dtype),
        in_specs=[sm()] + [vm()] * 4,
        out_specs=vm(),
        scratch_shapes=[
            pltpu.VMEM((QUART, -(-IMG_TOK // 128) * 128), F32),
            pltpu.VMEM((4, ROWS, QUART), BF),
        ],
        compiler_params=params(),
        cost_estimate=cost(4),
        name="unpack",
    )(where, *pieces)


def join_pieces(pieces, dst_ref):
    for slot, piece in enumerate(pieces):
        dst_ref[:HALF, QUART * slot : QUART * (slot + 1)] = piece[:, :QUART]
        dst_ref[HALF:, QUART * slot : QUART * (slot + 1)] = piece[:, QUART:]


def split_pieces(src_ref, out_ref):
    for slot in range(4):
        out_ref[slot, :, :QUART] = src_ref[:HALF, QUART * slot : QUART * (slot + 1)]
        out_ref[slot, :, QUART:] = src_ref[HALF:, QUART * slot : QUART * (slot + 1)]


def weight_pack_kernel(where_ref, qkv_w, proj_w, alpha_ref, beta_ref, alpha_half, beta_half):
    heads = qkv_w.shape[1] // (3 * HD)
    for h in range(heads):
        for t in range(3):
            ref, base = (alpha_ref, QUART * t) if t < 2 else (beta_ref, 0)
            ref[:, base + HD * h : base + HD * (h + 1)] = qkv_w[:, HD * (3 * h + t) : HD * (3 * h + t + 1)]
    beta_ref[:, QUART:] = proj_w[...]
    rows = pl.ds(pl.multiple_of(where_ref[1] * HBLK, 32), HBLK)
    alpha_half[...] = alpha_ref[rows, :]
    beta_half[...] = beta_ref[rows, :]


def weight_pack(where, qkv_w, proj_w):
    s = lambda *shape: jax.ShapeDtypeStruct(shape, BF)
    return pl.pallas_call(
        weight_pack_kernel,
        out_shape=(s(QUART, 2 * QUART), s(QUART, 2 * QUART), s(HBLK, 2 * QUART), s(HBLK, 2 * QUART)),
        in_specs=[sm(), vm(), vm()],
        out_specs=[vm()] * 4,
        compiler_params=params(),
        cost_estimate=cost(2),
        name="weight_pack",
    )(where, qkv_w, proj_w)


def adapter_pack_kernel(
    pick_ref, qkv_up, proj_dn, fc1_up, fc2_dn, qkv_dn, fc1_dn, proj_up, fc2_up, send_ref, row_ref,
):
    heads = qkv_up.shape[2] // (3 * HD)
    for j in range(4):
        a = pick_ref[j]
        for h in range(heads):
            for t in range(3):
                send_ref[j, :RANK, QUART * t + HD * h : QUART * t + HD * (h + 1)] = qkv_up[
                    a, :, HD * (3 * h + t) : HD * (3 * h + t + 1)
                ]
        send_ref[j, :RANK, 3 * QUART :] = proj_dn[a]
        send_ref[j, RANK : 2 * RANK, :] = fc1_up[a]
        send_ref[j, 2 * RANK :, :] = fc2_dn[a]
    for i, ref in enumerate((qkv_dn, fc1_dn, proj_up, fc2_up)):
        row_ref[:, QUART * i : QUART * (i + 1)] = ref[pick_ref[0]]


def adapter_pack(pick, *mats):
    s = lambda *shape: jax.ShapeDtypeStruct(shape, BF)
    return pl.pallas_call(
        adapter_pack_kernel,
        out_shape=(s(4, 3 * RANK, D), s(RANK, D)),
        in_specs=[sm()] + [vm()] * 8,
        out_specs=[vm()] * 2,
        compiler_params=params(),
        cost_estimate=cost(2),
        name="adapter_pack",
    )(pick, *mats)


def alpha_block(k, j):
    part = k
    if j == 0:
        return [(part, 0, QUART, None)]
    return [
        (part, QUART + HBLK * (j - 1), HBLK, 0),
        (part, QUART + 3 * HBLK + HBLK * (j - 1), HBLK, 1),
    ]


def beta_block(k, j):
    core, cross = k % 2, k // 2
    base = 3 * core
    if j == 0 and not cross:
        return [(base, 0, QUART, None)]
    row = 0 if j == 0 else HBLK + QUART * (j - 1) + HBLK * cross
    return [(base + 1, row, HBLK, 0), (base + 2, row, HBLK, 1)]


def block_dst(start, flag, half):
    if flag is None:
        return start
    offset = half if flag == 0 else 1 - half
    return pl.multiple_of(start + offset * HBLK, 32)


def prep1_kernel(
    where_ref, p0, p1, p2, p3, q0, q1, q2, q3, q4, q5, r0, r1, r2, r3, a0, a1, a2, a3,
    wqkv_ref, wproj_ref, dqkv, uqkv, dproj, uproj, d1, u1, d2, u2,
):
    half = where_ref[1]
    for j, a in enumerate((a0, a1, a2, a3)):
        for t in range(3):
            uqkv[:, D * t + QUART * j : D * t + QUART * (j + 1)] = a[:RANK, QUART * t : QUART * (t + 1)]
        dproj[:, QUART * j : QUART * (j + 1)] = a[:RANK, 3 * QUART :]
        u1[:, D * j : D * (j + 1)] = a[RANK : 2 * RANK, :]
        d2[:, D * j : D * (j + 1)] = a[2 * RANK :, :]
    for k, ref in enumerate((r0, r1, r2, r3)):
        for i, dst in enumerate((dqkv, d1, uproj, u2)):
            dst[:, QUART * k : QUART * (k + 1)] = ref[:, QUART * i : QUART * (i + 1)]
    alpha, beta = (p0, p1, p2, p3), (q0, q1, q2, q3, q4, q5)
    for k in range(4):
        for j in range(4):
            for part, row, count, flag in alpha_block(k, j):
                rows = pl.ds(block_dst(QUART * k, flag, half), count)
                for t in range(2):
                    wqkv_ref[rows, D * t + QUART * j : D * t + QUART * (j + 1)] = alpha[part][
                        row : row + count, QUART * t : QUART * (t + 1)
                    ]
            for part, row, count, flag in beta_block(k, j):
                rows = pl.ds(block_dst(QUART * k, flag, half), count)
                wqkv_ref[rows, 2 * D + QUART * j : 2 * D + QUART * (j + 1)] = beta[part][
                    row : row + count, :QUART
                ]
                rows = pl.ds(block_dst(QUART * j, flag, half), count)
                wproj_ref[rows, QUART * k : QUART * (k + 1)] = beta[part][row : row + count, QUART:]
    for k in range(4):
        rows = slice(QUART * k, QUART * (k + 1))
        for t in range(3):
            cols = slice(D * t, D * (t + 1))
            low = tn(dqkv[:, rows], uqkv[:, cols])
            wqkv_ref[rows, cols] = (wqkv_ref[rows, cols].astype(F32) + low).astype(BF)
        low = tn(dproj[:, rows], uproj[...])
        wproj_ref[rows, :] = (wproj_ref[rows, :].astype(F32) + low).astype(BF)


def prep1(where, alpha, beta, rows, cols):
    s = lambda *shape: jax.ShapeDtypeStruct(shape, BF)
    return pl.pallas_call(
        prep1_kernel,
        out_shape=(
            s(D, 3 * D), s(D, D), s(RANK, D), s(RANK, 3 * D), s(RANK, D), s(RANK, D),
            s(RANK, D), s(RANK, 4 * D), s(RANK, 4 * D), s(RANK, D),
        ),
        in_specs=[sm()] + [vm()] * 18,
        out_specs=[vm()] * 10,
        compiler_params=params(),
        cost_estimate=cost(7),
        name="attention_weights",
    )(where, *alpha, *beta, *rows, *cols)


def normalize(values):
    center = jnp.sum(values, axis=1, keepdims=True) / D
    shifted = values - center
    inv_std = lax.rsqrt(jnp.sum(shifted * shifted, axis=1, keepdims=True) / D + EPSILON)
    return shifted * inv_std, inv_std


def norm_back(grad, normed, inv_std):
    first = jnp.sum(grad, axis=1, keepdims=True) / D
    second = jnp.sum(grad * normed, axis=1, keepdims=True) / D
    return inv_std * (grad - first - normed * second)


def barrel(values, amount, left):
    for bit in (1, 2, 4, 8):
        moved = pltpu.roll(values, (128 - bit) if left else bit, 1)
        values = jnp.where((amount & bit) != 0, moved, values)
    return values


def low_half(count):
    return lax.broadcasted_iota(jnp.int32, (count, 128), 1) < HD


def pad_rows(tile):
    if tile.shape[0] == KEYS:
        return tile
    return jnp.concatenate([tile, jnp.zeros((KEYS - tile.shape[0], tile.shape[1]), tile.dtype)], axis=0)


def live_rows():
    return lax.broadcasted_iota(jnp.int32, (KEYS, 128), 0) < SLOTS


UNROLL = 6
UNROLL_BACK = 6


def pair_columns(pair):
    return tuple(pl.ds(pl.multiple_of(D * t + 128 * pair, 128), 128) for t in range(3))


def attend_window(kind, row0, qkv_ref, att_ref, exp_ref, inv_ref, rel_ref, shift_ref, keys_ref):
    count = NQ[kind]
    rows = pl.ds(row0, count)
    low_q, low_k = low_half(count), low_half(KEYS)
    live = live_rows()
    ones = jnp.where(live, 1.0, 0.0).astype(BF)
    amount = shift_ref[kind, :count, :]
    onehot = keys_ref[kind]

    def one_pair(pair, carry):
        cols, kcols, vcols = pair_columns(pair)
        q_tile = qkv_ref[rows, cols]
        k_tile = pad_rows(qkv_ref[rows, kcols] * BF(HD**-0.5))
        v_tile = pad_rows(qkv_ref[rows, vcols])
        if kind == FULL:
            v_tile = jnp.where(live, v_tile, 0).astype(BF)
        rel = barrel(nn(q_tile, rel_ref[...]), amount, True).astype(BF)
        both = []
        for odd in range(2):
            if odd:
                q_aug, k_aug = jnp.where(low_q, rel, q_tile), jnp.where(low_k, onehot, k_tile)
                v_aug = jnp.where(low_k, ones, v_tile)
            else:
                q_aug, k_aug = jnp.where(low_q, q_tile, rel), jnp.where(low_k, k_tile, onehot)
                v_aug = jnp.where(low_k, v_tile, ones)
            scores = nt(q_aug, k_aug)
            exponent = jnp.exp(scores - jnp.max(scores, axis=1, keepdims=True)).astype(BF)
            exp_ref[2 * pair + odd, rows, :] = exponent
            both.append(nn(exponent, v_aug))
        inverse = 1.0 / pltpu.roll(jnp.where(low_q, both[1], both[0]), HD, 1)
        inv_ref[rows, cols] = inverse
        att_ref[rows, cols] = (jnp.where(low_q, both[0], both[1]) * inverse).astype(BF)
        return carry

    lax.fori_loop(0, D // 128, one_pair, 0, unroll=UNROLL)


PARTS = ((FULL, FULL), (FULL, FULL), (RIGHT, BOTTOM, CORNER))
PART_ROWS = tuple(sum(NQ[kind] for kind in part) for part in PARTS)
PART_OFFS = (0, PART_ROWS[0], PART_ROWS[0] + PART_ROWS[1])


def qkv_kernel(x0, x1, x2, x3, gain_ref, wqkv_ref, x_ref, hid_ref, qkv_a, qkv_b, qkv_c):
    join_pieces((x0, x1, x2, x3), x_ref)
    gain = gain_ref[...]

    def norm_step(i, carry):
        rows = pl.ds(pl.multiple_of(i * 112, 16), 112)
        normed, _ = normalize(x_ref[rows, :].astype(F32))
        hid_ref[rows, :] = (normed * gain).astype(BF)
        return carry

    lax.fori_loop(0, ROWS // 112, norm_step, 0)
    for ref, offset, count in zip((qkv_a, qkv_b, qkv_c), PART_OFFS, PART_ROWS):
        hid = hid_ref[offset : offset + count, :]
        for t in range(3):
            cols = slice(D * t, D * (t + 1))
            ref[:, cols] = nn(hid, wqkv_ref[:, cols]).astype(BF)
    for w in range(4):
        hid_ref[FULLR * w + SLOTS : FULLR * (w + 1), :] = jnp.zeros((FULLR - SLOTS, D), BF)


def qkv_rows(pieces, gain, wqkv):
    s = lambda *shape: jax.ShapeDtypeStruct(shape, BF)
    return pl.pallas_call(
        qkv_kernel,
        out_shape=(s(ROWS, D), s(ROWS, D)) + tuple(s(n, 3 * D) for n in PART_ROWS),
        in_specs=[vm()] * 6,
        out_specs=[vm()] * 5,
        compiler_params=params(),
        cost_estimate=cost(12),
        name="norm_and_qkv",
    )(*pieces, gain, wqkv)


def attention_kernel(qkv_ref, rel_ref, shift_ref, keys_ref, att_ref, exp_ref, inv_ref, *, kinds):
    refs = (qkv_ref, att_ref, exp_ref, inv_ref, rel_ref, shift_ref, keys_ref)
    if kinds[0] == FULL:

        def step(w, carry):
            attend_window(FULL, pl.multiple_of(w * FULLR, 16), *refs)
            return carry

        lax.fori_loop(0, len(kinds), step, 0)
    else:
        row = 0
        for kind in kinds:
            attend_window(kind, row, *refs)
            row += NQ[kind]


def attention(part, qkv, rel, shift, keys):
    rows = PART_ROWS[part]
    s = lambda *shape, dtype=BF: jax.ShapeDtypeStruct(shape, dtype)
    return pl.pallas_call(
        functools.partial(attention_kernel, kinds=PARTS[part]),
        out_shape=(s(rows, D), s(D // HD, rows, KEYS), s(rows, D, dtype=F32)),
        in_specs=[vm()] * 4,
        out_specs=[vm()] * 3,
        compiler_params=params(),
        cost_estimate=cost(10),
        name="attention_forward",
    )(qkv, rel, shift, keys)


def project_kernel(x_ref, att_a, att_b, att_c, wproj_ref, middle_ref):
    for ref, offset, count in zip((att_a, att_b, att_c), PART_OFFS, PART_ROWS):
        rows = slice(offset, offset + count)
        middle_ref[rows, :] = x_ref[rows, :].astype(F32) + nn(ref[...], wproj_ref[...])


def project(x, atts, wproj):
    return pl.pallas_call(
        project_kernel,
        out_shape=jax.ShapeDtypeStruct((ROWS, D), F32),
        in_specs=[vm()] * 5,
        out_specs=vm(),
        compiler_params=params(),
        cost_estimate=cost(5),
        name="projection",
    )(x, *atts, wproj)


CHUNK = 512


def mlp_kernel(
    where_ref, middle_ref, g0, g1, g2, g3, gain_ref,
    p0, p1, p2, p3, q0, q1, q2, q3, q4, q5, d1, u1, d2, u2,
    out_ref, gmid_ref, down1, up1, down2, up2,
    gm_ref, out_rows, h2_ref, acc_mlp, acc_gh, gu1, ad2, w1_ref, w2_ref, sem,
):
    half = where_ref[1]
    copies = []

    def fetch(src, dst):
        copies.append(pltpu.make_async_copy(src, dst, sem.at[len(copies)]))
        copies[-1].start()

    alpha, beta = (p0, p1, p2, p3), (q0, q1, q2, q3, q4, q5)
    for k in range(4):
        for j in range(4):
            for part, row, count, flag in alpha_block(k, j):
                rows = pl.ds(block_dst(QUART * k, flag, half), count)
                fetch(alpha[part].at[row : row + count, :], w1_ref.at[rows, D * j : D * (j + 1)])
            for part, row, count, flag in beta_block(k, j):
                rows = pl.ds(block_dst(QUART * k, flag, half), count)
                fetch(beta[part].at[row : row + count, :], w2_ref.at[rows, D * j : D * (j + 1)])
    join_pieces((g0, g1, g2, g3), gm_ref)
    for copy in copies:
        copy.wait()
    for k in range(4):
        rows = slice(QUART * k, QUART * (k + 1))
        for j in range(4):
            cols = slice(D * j, D * (j + 1))
            low = tn(d1[:, rows], u1[:, cols])
            w1_ref[rows, cols] = (w1_ref[rows, cols].astype(F32) + low).astype(BF)
            low = tn(u2[:, rows], d2[:, cols])
            w2_ref[rows, cols] = (w2_ref[rows, cols].astype(F32) + low).astype(BF)
    gain = gain_ref[...]
    down1[...] = jnp.zeros_like(down1)
    up1[...] = jnp.zeros_like(up1)
    down2[...] = jnp.zeros_like(down2)
    up2[...] = jnp.zeros_like(up2)

    def tile_step(t, carry):
        rows = pl.ds(pl.multiple_of(t * HALF, 16), HALF)
        normed, _ = normalize(middle_ref[rows, :])
        h2 = (normed * gain).astype(BF)
        h2_ref[...] = h2
        gm = gm_ref[rows, :]
        ad1 = nt(d1[...], h2).astype(BF)
        gu2 = nt(u2[...], gm).astype(BF)
        acc_mlp[...] = jnp.zeros_like(acc_mlp)
        acc_gh[...] = jnp.zeros_like(acc_gh)
        gu1[...] = jnp.zeros_like(gu1)
        ad2[...] = jnp.zeros_like(ad2)

        def chunk_step(c, inner_carry):
            cols = pl.ds(pl.multiple_of(c * CHUNK, CHUNK), CHUNK)
            w1 = w1_ref[:, cols]
            w2 = w2_ref[:, cols]
            inner = nn(h2_ref[...], w1)
            gact = nn(gm_ref[rows, :], w2)
            half = 0.5 * (1.0 + lax.erf(inner * 2**-0.5))
            act = (inner * half).astype(BF)
            slope = half + inner * (jnp.exp(-0.5 * inner * inner) * (2 * np.pi) ** -0.5)
            ginner = (gact * slope).astype(BF)
            acc_mlp[...] += nt(act, w2)
            acc_gh[...] += nt(ginner, w1)
            up1[:, cols] += nn(ad1, ginner)
            gu1[...] += nt(u1[:, cols], ginner)
            ad2[...] += nt(d2[:, cols], act)
            down2[:, cols] += nn(gu2, act)
            return inner_carry

        lax.fori_loop(0, 4 * D // CHUNK, chunk_step, 0)
        down1[...] += nn(gu1[...].astype(BF), h2_ref[...])
        up2[...] += nn(ad2[...].astype(BF), gm_ref[rows, :])
        middle = middle_ref[rows, :]
        out_rows[rows, :] = (middle + acc_mlp[...]).astype(BF)
        normed, inv_std = normalize(middle)
        gmid_ref[rows, :] = gm_ref[rows, :].astype(F32) + norm_back(acc_gh[...] * gain, normed, inv_std)
        return carry

    lax.fori_loop(0, 2, tile_step, 0)
    split_pieces(out_rows, out_ref)


def mlp(where, middle, pieces, gain, alpha, beta, d1, u1, d2, u2):
    s = lambda *shape, dtype=F32: jax.ShapeDtypeStruct(shape, dtype)
    return pl.pallas_call(
        mlp_kernel,
        out_shape=(
            s(4, HALF, 2 * QUART, dtype=BF), s(ROWS, D),
            s(RANK, D), s(RANK, 4 * D), s(RANK, 4 * D), s(RANK, D),
        ),
        in_specs=[sm()] + [vm()] * 6 + [pl.BlockSpec(memory_space=pl.ANY)] * 10 + [vm()] * 4,
        out_specs=[vm()] * 6,
        scratch_shapes=[
            pltpu.VMEM((ROWS, D), BF), pltpu.VMEM((ROWS, D), BF), pltpu.VMEM((HALF, D), BF),
            pltpu.VMEM((HALF, D), F32), pltpu.VMEM((HALF, D), F32),
            pltpu.VMEM((RANK, HALF), F32), pltpu.VMEM((RANK, HALF), F32),
            pltpu.VMEM((D, 4 * D), BF), pltpu.VMEM((D, 4 * D), BF),
            pltpu.SemaphoreType.DMA((4 * 4 * 4,)),
        ],
        compiler_params=params(),
        cost_estimate=cost(48),
        name="mlp_forward_backward",
    )(where, middle, *pieces, gain, *alpha, *beta, d1, u1, d2, u2)


def attend_back_window(
    kind, row0, qkv_ref, att_ref, exp_ref, inv_ref, gatt_ref, gqkv_ref, rel_ref, shift_ref, keys_ref
):
    count = NQ[kind]
    rows = pl.ds(row0, count)
    low_q, low_k = low_half(count), low_half(KEYS)
    live = live_rows()
    lane_k = lax.broadcasted_iota(jnp.int32, (KEYS, 128), 1) % HD
    lane_q = lax.broadcasted_iota(jnp.int32, (count, 128), 1) % HD
    ones = jnp.where(live & (lane_k < 2), 1.0, 0.0).astype(BF)
    across = jnp.where(
        low_half(128) != (lax.broadcasted_iota(jnp.int32, (128, 128), 0) < HD), -1.0, 0.0
    ).astype(BF)
    amount = shift_ref[kind, :count, :]
    onehot = keys_ref[kind]

    def one_pair(pair, carry):
        cols, kcols, vcols = pair_columns(pair)
        q_tile = qkv_ref[rows, cols]
        k_tile = pad_rows(qkv_ref[rows, kcols] * BF(HD**-0.5))
        v_tile = pad_rows(qkv_ref[rows, vcols])
        if kind == FULL:
            v_tile = jnp.where(live, v_tile, 0).astype(BF)
        go_tile = (gatt_ref[rows, cols].astype(F32) * inv_ref[rows, cols]).astype(BF)
        delta = nn((go_tile.astype(F32) * att_ref[rows, cols].astype(F32)).astype(BF), across)
        high = delta.astype(BF)
        rest = (delta - high.astype(F32)).astype(BF)
        delta = jnp.where(lane_q == 0, high, jnp.where(lane_q == 1, rest, 0)).astype(BF)
        q_t = q_tile.T
        go_t = go_tile.T
        gq, gk, gv = [], [], []
        for odd in range(2):
            if odd:
                go_aug, v_aug = jnp.where(low_q, delta, go_tile), jnp.where(low_k, ones, v_tile)
                k_aug = jnp.where(low_k, onehot, k_tile)
            else:
                go_aug, v_aug = jnp.where(low_q, go_tile, delta), jnp.where(low_k, v_tile, ones)
                k_aug = jnp.where(low_k, k_tile, onehot)
            exponent = exp_ref[2 * pair + odd, rows, :]
            gs = (exponent.astype(F32) * nt(go_aug, v_aug)).astype(BF)
            side = slice(HD * odd, HD * (odd + 1))
            gv.append(nn(go_t[side, :], exponent))
            gk.append(nn(q_t[side, :], gs))
            gq.append(nn(gs, k_aug))
        sums = barrel(jnp.where(low_q, gq[1], gq[0]), amount, False).astype(BF)
        gqkv_ref[rows, cols] = (jnp.where(low_q, gq[0], gq[1]) + nt(sums, rel_ref[...])).astype(BF)
        gk_tile = (jnp.concatenate(gk, axis=0) * HD**-0.5).astype(BF).T
        gv_tile = jnp.concatenate(gv, axis=0).astype(BF).T
        gqkv_ref[rows, kcols] = gk_tile[:count, :]
        gqkv_ref[rows, vcols] = gv_tile[:count, :]
        return carry

    lax.fori_loop(0, D // 128, one_pair, 0, unroll=UNROLL_BACK)


def attention_back_kernel(
    gmid_ref, hid_ref, qkv_a, qkv_b, qkv_c, att_a, att_b, att_c, exp_a, exp_b, exp_c, inv_a, inv_b, inv_c,
    wproj_ref, rel_ref, shift_ref, keys_ref, dqkv, uqkv, dproj, uproj,
    gqkv_ref, down_q, up_q, down_p, up_p, gb_ref, gatt_ref, att_ref,
):
    gb_ref[...] = gmid_ref[...].astype(BF)
    gatt_ref[...] = nt(gb_ref[...], wproj_ref[...]).astype(BF)
    for ref, offset, count in zip((att_a, att_b, att_c), PART_OFFS, PART_ROWS):
        att_ref[offset : offset + count, :] = ref[...]
    up_p[...] = nn(nt(dproj[...], att_ref[...]).astype(BF), gb_ref[...])
    down_p[...] = nn(nt(uproj[...], gb_ref[...]).astype(BF), att_ref[...])
    tables = (rel_ref, shift_ref, keys_ref)
    for part, parts in enumerate(
        ((qkv_a, att_a, exp_a, inv_a), (qkv_b, att_b, exp_b, inv_b), (qkv_c, att_c, exp_c, inv_c))
    ):
        span = pl.ds(PART_OFFS[part], PART_ROWS[part])
        refs = parts + (gatt_ref.at[span, :], gqkv_ref.at[span, :]) + tables
        if PARTS[part][0] == FULL:

            def step(w, carry, refs=refs):
                attend_back_window(FULL, pl.multiple_of(w * FULLR, 16), *refs)
                return carry

            lax.fori_loop(0, len(PARTS[part]), step, 0)
        else:
            row = 0
            for kind in PARTS[part]:
                attend_back_window(kind, row, *refs)
                row += NQ[kind]
    up_q[...] = nn(nt(dqkv[...], hid_ref[...]).astype(BF), gqkv_ref[...])
    down_q[...] = nn(nt(uqkv[...], gqkv_ref[...]).astype(BF), hid_ref[...])


def attention_back(gmid, hid, qkvs, atts, exps, invs, wproj, rel, shift, keys, dqkv, uqkv, dproj, uproj):
    s = lambda *shape, dtype=F32: jax.ShapeDtypeStruct(shape, dtype)
    return pl.pallas_call(
        attention_back_kernel,
        out_shape=(s(ROWS, 3 * D, dtype=BF), s(RANK, D), s(RANK, 3 * D), s(RANK, D), s(RANK, D)),
        in_specs=[vm()] * 22,
        out_specs=[vm()] * 5,
        scratch_shapes=[pltpu.VMEM((ROWS, D), BF)] * 3,
        compiler_params=params(),
        cost_estimate=cost(45),
        name="attention_backward",
    )(gmid, hid, *qkvs, *atts, *exps, *invs, wproj, rel, shift, keys, dqkv, uqkv, dproj, uproj)


def token_grad_kernel(gmid_ref, x_ref, gqkv_ref, gain_ref, wqkv_ref, out_ref, gh_ref, out_rows):
    gh_ref[...] = nt(gqkv_ref[...], wqkv_ref[...])
    gain = gain_ref[...]

    def norm_step(i, carry):
        rows = pl.ds(pl.multiple_of(i * 112, 16), 112)
        normed, inv_std = normalize(x_ref[rows, :].astype(F32))
        back = norm_back(gh_ref[rows, :] * gain, normed, inv_std)
        out_rows[rows, :] = (gmid_ref[rows, :] + back).astype(BF)
        return carry

    lax.fori_loop(0, ROWS // 112, norm_step, 0)
    split_pieces(out_rows, out_ref)


def token_grad(gmid, x, gqkv, gain, wqkv):
    return pl.pallas_call(
        token_grad_kernel,
        out_shape=jax.ShapeDtypeStruct((4, HALF, 2 * QUART), BF),
        in_specs=[vm()] * 5,
        out_specs=vm(),
        scratch_shapes=[pltpu.VMEM((ROWS, D), F32), pltpu.VMEM((ROWS, D), BF)],
        compiler_params=params(),
        cost_estimate=cost(14),
        name="token_gradient",
    )(gmid, x, gqkv, gain, wqkv)


def grad_pack_kernel(where_ref, down_q, up_q, down_p, up_p, down1, up1, down2, up2, out_ref, buf_ref):
    mine = where_ref[0]
    for k in range(4):
        for i, ref in enumerate((down_q, down1, up_p, up2)):
            buf_ref[k, :RANK, QUART * i : QUART * (i + 1)] = ref[:, QUART * k : QUART * (k + 1)]
    for dest in range(4):
        k = jnp.bitwise_xor(mine, dest)
        ranks = slice(RANK // 4 * dest, RANK // 4 * (dest + 1))
        for j in range(4):
            base = RANK + 12 * j
            for t in range(3):
                buf_ref[k, base : base + 4, QUART * t : QUART * (t + 1)] = up_q[
                    ranks, D * t + QUART * j : D * t + QUART * (j + 1)
                ]
            buf_ref[k, base : base + 4, 3 * QUART :] = down_p[ranks, QUART * j : QUART * (j + 1)]
            buf_ref[k, base + 4 : base + 8, :] = up1[ranks, D * j : D * (j + 1)]
            buf_ref[k, base + 8 : base + 12, :] = down2[ranks, D * j : D * (j + 1)]
    out_ref[...] = buf_ref[...].astype(BF)


def grad_pack(where, *grads):
    return pl.pallas_call(
        grad_pack_kernel,
        out_shape=jax.ShapeDtypeStruct((4, 4 * RANK, D), BF),
        in_specs=[sm()] + [vm()] * 8,
        out_specs=vm(),
        scratch_shapes=[pltpu.VMEM((4, 4 * RANK, D), F32)],
        compiler_params=params(),
        cost_estimate=cost(2),
        name="adapter_grad_pack",
    )(where, *grads)


def grad_sum_kernel(g0, g1, g2, g3, out_ref, buf_ref):
    total = g0[...].astype(F32) + g1[...].astype(F32) + g2[...].astype(F32) + g3[...].astype(F32)
    buf_ref[...] = jnp.zeros_like(buf_ref)
    for j in range(4):
        buf_ref[:RANK, :] = total[:RANK, :]
        buf_ref[RANK : RANK + 12, :] = total[RANK + 12 * j : RANK + 12 * (j + 1), :]
        out_ref[j] = buf_ref[...].astype(BF)


def grad_sum(pieces):
    return pl.pallas_call(
        grad_sum_kernel,
        out_shape=jax.ShapeDtypeStruct((4, 2 * RANK, D), BF),
        in_specs=[vm()] * 4,
        out_specs=vm(),
        scratch_shapes=[pltpu.VMEM((2 * RANK, D), F32)],
        compiler_params=params(),
        cost_estimate=cost(2),
        name="adapter_grad_sum",
    )(*pieces)


def grad_adapters_kernel(index_ref, x_ref, qkv_dn, fc1_dn, proj_up, fc2_up, rest_ref, acc_ref):
    acc_ref[...] = jnp.zeros_like(acc_ref)

    def add(i, carry):
        acc_ref[index_ref[i]] += x_ref[i].astype(F32)
        return carry

    lax.fori_loop(0, x_ref.shape[0], add, 0)
    for i, ref in enumerate((qkv_dn, fc1_dn, proj_up, fc2_up)):
        ref[...] = acc_ref[:, :RANK, QUART * i : QUART * (i + 1)]
    rest_ref[...] = acc_ref[:, RANK:, :].astype(BF)


def grad_adapters(index, x):
    s = lambda n, dtype=F32: jax.ShapeDtypeStruct((ADAPT, RANK, n), dtype)
    return pl.pallas_call(
        grad_adapters_kernel,
        out_shape=(s(QUART), s(QUART), s(QUART), s(QUART), s(D, BF)),
        in_specs=[sm(), vm()],
        out_specs=[vm()] * 5,
        scratch_shapes=[pltpu.VMEM((ADAPT, 2 * RANK, D), F32)],
        compiler_params=params(),
        cost_estimate=cost(2),
        name="adapter_grad_by_adapter",
    )(index, x)


def grad_join_kernel(where_ref, r0, r1, r2, r3, qkv_up, proj_dn, fc1_up, fc2_dn, buf_ref):
    mine = where_ref[0]
    heads = qkv_up.shape[2] // (3 * HD)
    for k, ref in enumerate((r0, r1, r2, r3)):
        buf_ref[jnp.bitwise_xor(mine, k)] = ref[...].astype(F32)
    for source in range(4):
        ranks = slice(RANK // 4 * source, RANK // 4 * (source + 1))
        for h in range(heads):
            for t in range(3):
                qkv_up[:, ranks, HD * (3 * h + t) : HD * (3 * h + t + 1)] = buf_ref[
                    source, :, 0:4, QUART * t + HD * h : QUART * t + HD * (h + 1)
                ]
        proj_dn[:, ranks, :] = buf_ref[source, :, 0:4, 3 * QUART :]
        fc1_up[:, ranks, :] = buf_ref[source, :, 4:8, :]
        fc2_dn[:, ranks, :] = buf_ref[source, :, 8:12, :]


def grad_join(where, pieces):
    s = lambda n: jax.ShapeDtypeStruct((ADAPT, RANK, n), F32)
    return pl.pallas_call(
        grad_join_kernel,
        out_shape=(s(3 * QUART), s(QUART), s(D), s(D)),
        in_specs=[sm()] + [vm()] * 4,
        out_specs=[vm()] * 4,
        scratch_shapes=[pltpu.VMEM((4, ADAPT, RANK, D), F32)],
        compiler_params=params(),
        cost_estimate=cost(2),
        name="adapter_grad_join",
    )(where, *pieces)


def flip(values, axis, distance):
    size = lax.axis_size(axis)
    return lax.ppermute(values, axis, [(i, i ^ distance) for i in range(size)])


def exchange(slots, axis):
    return [slots[0]] + [flip(slots[k], axis, k) for k in range(1, 4)]


def after(values, *deps):
    return lax.optimization_barrier((tuple(values), deps))[0]


def col_halves(half):
    return jnp.concatenate([flip(half, "col", j) for j in range(1, 4)], axis=0)


def col_pairs(half, other_row):
    two = jnp.concatenate([half, other_row], axis=0)
    return jnp.concatenate([other_row] + [flip(two, "col", j) for j in range(1, 4)], axis=0)


def rel_matrix(rel_h, rel_w):
    pad = jnp.zeros((32 - (2 * WIN - 1), HD), BF)
    block = jnp.concatenate([rel_h[::-1], pad, rel_w[::-1], pad], axis=0).T
    zero = jnp.zeros((HD, HD), BF)
    return jnp.concatenate(
        [jnp.concatenate([zero, block], axis=1), jnp.concatenate([block, zero], axis=1)], axis=0
    )


def body(
    tokens, grad_out, adapter_index, norm1_gain, norm2_gain, qkv_weight, proj_weight, fc1_weight, fc2_weight,
    rel_h, rel_w, qkv_down, qkv_up, proj_down, proj_up, fc1_down, fc1_up, fc2_down, fc2_up,
):
    members = lax.axis_size("col")
    batches = lax.axis_size("dp")
    row_index, col_index, dp_index = lax.axis_index("row"), lax.axis_index("col"), lax.axis_index("dp")
    half = dp_index % 2
    where = jnp.stack([row_index, half]).astype(jnp.int32)
    slot_images = (
        jnp.bitwise_xor(dp_index, jnp.arange(batches, dtype=jnp.int32))[:, None] * members
        + jnp.bitwise_xor(col_index, jnp.arange(members, dtype=jnp.int32))[None, :]
    ).reshape(-1)
    slot_adapters = jnp.sum(
        jnp.where(
            slot_images[:, None] == jnp.arange(adapter_index.shape[0], dtype=jnp.int32)[None, :],
            adapter_index[:, 0][None, :],
            0,
        ),
        axis=1,
    )
    pick = jnp.concatenate([slot_adapters[:4], half[None]]).astype(jnp.int32)
    swap = lambda m: jnp.swapaxes(m, 1, 2)

    rel = rel_matrix(rel_h, rel_w)
    shift, keys = jnp.asarray(SHIFT_NP), jnp.asarray(KEYS_NP)

    alpha_own, beta_own, alpha_half, beta_half = weight_pack(where, qkv_weight, proj_weight)
    b0 = flip(beta_half, "row", 2)
    alpha_near = col_halves(alpha_half)
    token_slots = pack(where, tokens, 0)
    x_pieces = exchange(token_slots, "row")
    beta_near = col_pairs(beta_half, b0)
    alpha_far = flip(alpha_near, "dp", 1)
    g = jnp.concatenate([alpha_own, alpha_near, alpha_far], axis=0)
    g, _ = after((g, x_pieces[1]), x_pieces[2])
    gy = flip(g, "row", 2)
    beta_far = flip(beta_near, "dp", 1)
    beta1 = [beta_own, beta_near, beta_far] + [flip(m, "row", 1) for m in (beta_own, beta_near, beta_far)]

    gains = jnp.stack([norm1_gain, norm2_gain]).astype(F32)
    send, row_adapters = adapter_pack(
        pick, qkv_up, swap(proj_down), fc1_up, swap(fc2_down), swap(qkv_down), swap(fc1_down), proj_up, fc2_up,
    )
    gains, send, row_adapters = after((gains, send, row_adapters), beta_near)
    col_adapters = exchange(send, "col")
    gain_all = jnp.concatenate(exchange([gains] * 4, "row"), axis=1)
    gain1, gain2 = gain_all[0:1], gain_all[1:2]
    row_adapters = exchange([row_adapters] * 4, "row")

    fc1_half = lax.dynamic_slice_in_dim(fc1_weight, half * HBLK, HBLK, 0)
    fc2_half = lax.dynamic_slice_in_dim(fc2_weight, half * HBLK, HBLK, 0)
    c0 = flip(fc2_half, "row", 2)
    fc1_half, fc2_half, c0 = after((fc1_half, fc2_half, c0), col_adapters[1], col_adapters[2], col_adapters[3])
    fc1_near = col_halves(fc1_half)
    fc2_near = col_pairs(fc2_half, c0)
    fc1_far = flip(fc1_near, "dp", 1)
    h = jnp.concatenate([fc1_weight, fc1_near, fc1_far], axis=0)

    grad_slots = pack(where, grad_out)
    alpha1 = [g, flip(g, "row", 1), gy, flip(gy, "row", 1)]
    wqkv, wproj, dqkv, uqkv, dproj, uproj, d1, u1, d2, u2 = prep1(where, alpha1, beta1, row_adapters, col_adapters)
    x, hid, *qkvs = qkv_rows(x_pieces, gain1, wqkv)
    qkv0, h = after((qkvs[0], h), gy)
    hy = flip(h, "row", 2)
    part0 = attention(0, qkv0, rel, shift, keys)
    qkv1, fc2_near = after((qkvs[1], fc2_near), part0[0])
    fc2_far = flip(fc2_near, "dp", 1)
    part1 = attention(1, qkv1, rel, shift, keys)
    qkv2, hy, grad_slots = after((qkvs[2], hy, grad_slots), part1[0])
    g_pieces = exchange(grad_slots, "row")
    alpha2 = [h, flip(h, "row", 1), hy, flip(hy, "row", 1)]
    part2 = attention(2, qkv2, rel, shift, keys)
    atts, exps, invs = zip(part0, part1, part2)
    middle = project(x, atts, wproj)
    beta2 = [fc2_weight, fc2_near, fc2_far] + [flip(m, "row", 1) for m in (fc2_weight, fc2_near, fc2_far)]

    out_slots, gmid, down1, up1, down2, up2 = mlp(where, middle, g_pieces, gain2, alpha2, beta2, d1, u1, d2, u2)
    out_pieces = exchange(out_slots, "row")
    gqkv, down_q, up_q, down_p, up_p = attention_back(
        gmid, hid, qkvs, atts, exps, invs, wproj, rel, shift, keys, dqkv, uqkv, dproj, uproj
    )
    gqkv, down_q, up_q, down_p, up_p = after((gqkv, down_q, up_q, down_p, up_p), *out_pieces)
    packed = grad_pack(where, down_q, up_q, down_p, up_p, down1, up1, down2, up2)
    row_sums = exchange(packed, "row")
    back_slots = token_grad(gmid, x, gqkv, gain1, wqkv)
    back_slots, *row_sums = after((back_slots, *row_sums))
    back_pieces = exchange(back_slots, "row")
    summed = grad_sum(row_sums)
    images = jnp.stack(exchange(summed, "col"))
    step = 1
    while step < batches:
        images = jnp.concatenate([images, flip(images, "dp", step)], axis=0)
        step *= 2
    qkv_dn, fc1_dn, proj_upg, fc2_upg, rest = grad_adapters(slot_adapters.astype(jnp.int32), images)
    rests = [rest] + [flip(rest, "row", k) for k in range(1, 4)]
    qkv_upg, proj_dn, fc1_upg, fc2_dn = grad_join(where, rests)
    result = unpack(where, out_pieces, BF)
    grad_tokens = unpack(where, back_pieces, F32)
    return (
        result, grad_tokens,
        swap(qkv_dn), qkv_upg, swap(proj_dn), proj_upg, swap(fc1_dn), fc1_upg, swap(fc2_dn), fc2_upg,
    )


def solution(mesh):
    return jax.shard_map(
        body,
        mesh=mesh,
        in_specs=(
            P("row", ("dp", "col")), P("row", ("dp", "col")), P(), P("row"), P("row"),
            P("row", "col"), P("col", "row"), P("row", "col"), P("row", "col"), P(), P(),
            P(None, "row", None), P(None, None, "col"), P(None, "col", None), P(None, None, "row"),
            P(None, "row", None), P(None, None, "col"), P(None, "col", None), P(None, None, "row"),
        ),
        out_specs=(
            P("row", ("dp", "col")), P("row", ("dp", "col")),
            P(None, "row", None), P(None, None, "col"), P(None, "col", None), P(None, None, "row"),
            P(None, "row", None), P(None, None, "col"), P(None, "col", None), P(None, None, "row"),
        ),
        check_vma=False,
    )
```

```python
import functools

import jax
import jax.numpy as jnp
import numpy as np
from jax import lax
from jax.experimental import pallas as pl
from jax.experimental.pallas import tpu as pltpu
from jax.sharding import PartitionSpec as P

D = 768
HD = 64
WIN = 14
SLOTS = WIN * WIN
SIDE = 64
ADAPT = 8
NWIN = 5
IMG_TOK = NWIN * NWIN * SLOTS
RANK = 16
EDGE = SIDE - (NWIN - 1) * WIN
QUART = D // 4
FULLR = 208
KEYS = 208
EDGER = EDGE * WIN
CORNR = EDGE * EDGE
ROWS = 4 * FULLR + 2 * EDGER + CORNR
HALF = ROWS // 2
HBLK = QUART // 2
EPSILON = 1e-06
BF = jnp.bfloat16
F32 = jnp.float32
VMEM_LIMIT = 60 * 1024 * 1024

FULL, RIGHT, BOTTOM, CORNER = 0, 1, 2, 3
NQ = (FULLR, EDGER, EDGER, CORNR)
OFFS = (0, 4 * FULLR, 4 * FULLR + EDGER, 4 * FULLR + 2 * EDGER)


def slot_order(kind):
    rows = EDGE if kind in (BOTTOM, CORNER) else WIN
    cols = EDGE if kind in (RIGHT, CORNER) else WIN
    kept = [a * WIN + b for a in range(rows) for b in range(cols)]
    rest = [s for s in range(SLOTS) if s not in set(kept)]
    return kept, kept + rest


def build_tables():
    shift = np.zeros((4, FULLR, 128), np.int32)
    keys = np.zeros((4, KEYS, 128), np.float32)
    for kind in range(4):
        kept, order = slot_order(kind)
        for i, s in enumerate(kept):
            for base in (0, 64):
                shift[kind, i, base : base + 32] = WIN - 1 - s // WIN
                shift[kind, i, base + 32 : base + 64] = WIN - 1 - s % WIN
        spare = order[0] if kind == FULL else order[-1]
        for i, s in enumerate(order + [spare] * (KEYS - SLOTS)):
            for base in (0, 64):
                keys[kind, i, base + s // WIN] = 1.0
                keys[kind, i, base + 32 + s % WIN] = 1.0
    return shift, keys.astype(jnp.bfloat16)


SHIFT_NP, KEYS_NP = build_tables()


def nn(a, b):
    return jnp.dot(a, b, preferred_element_type=F32)


def nt(a, b):
    return lax.dot_general(a, b, (((1,), (1,)), ((), ())), preferred_element_type=F32)


def tn(a, b):
    return lax.dot_general(a, b, (((0,), (0,)), ((), ())), preferred_element_type=F32)


def vm():
    return pl.BlockSpec(memory_space=pltpu.VMEM)


def sm():
    return pl.BlockSpec(memory_space=pltpu.SMEM)


def params(**kw):
    return pltpu.CompilerParams(vmem_limit_bytes=VMEM_LIMIT, **kw)


def cost(us):
    return pl.CostEstimate(flops=int(us * 9e8), transcendentals=0, bytes_accessed=0)


def place_window(kind, count, moved, width, spare=-100000):
    row = lax.broadcasted_iota(jnp.int32, (count, width), 0)
    lane = lax.broadcasted_iota(jnp.int32, (count, width), 1)
    if kind in (RIGHT, CORNER):
        src = (row // EDGE) * WIN + row % EDGE
    else:
        src = jnp.where(row < SLOTS, row, spare)
    return (lane == src + moved).astype(F32).astype(BF)


SPAN = 384
LAST = SLOTS * (NWIN * NWIN - 1)
LAST_LOW = LAST // 128 * 128


def window_span(window):
    start = window * SLOTS
    low = start // 128 * 128
    return pl.ds(pl.multiple_of(low, 128), SPAN), start - low


def each_window(dest, visit):
    def full(j, carry):
        visit(FULL, pl.multiple_of(FULLR * j, 16), NWIN * dest + j)
        return carry

    lax.fori_loop(0, 4, full, 0)
    visit(RIGHT, OFFS[1], NWIN * dest + 4)
    visit(BOTTOM, OFFS[2], NWIN * 4 + dest)


def pack_rows(mine, x_ref, rows_ref, spare):
    def one(dest, carry):
        slot = jnp.bitwise_xor(mine, dest)

        def visit(kind, offset, window):
            span, moved = window_span(window)
            pick = place_window(kind, NQ[kind], moved, SPAN, spare)
            rows_ref[slot, pl.ds(offset, NQ[kind]), :] = nt(pick, x_ref[:, span]).astype(BF)

        each_window(dest, visit)
        rows_ref[slot, OFFS[3] :, :] = jnp.zeros((CORNR, QUART), BF)
        return carry

    lax.fori_loop(0, 4, one, 0)
    pick = place_window(CORNER, CORNR, LAST - LAST_LOW, IMG_TOK - LAST_LOW)
    rows_ref[jnp.bitwise_xor(mine, 3), OFFS[3] :, :] = nt(pick, x_ref[:, LAST_LOW:]).astype(BF)


def pack_kernel(where_ref, x_ref, o0, o1, o2, o3, rows_ref):
    pack_rows(where_ref[0], x_ref, rows_ref, -100000)
    for slot, out in enumerate((o0, o1, o2, o3)):
        out[:, :QUART] = rows_ref[slot, :HALF, :]
        out[:, QUART:] = rows_ref[slot, HALF:, :]


PIECE = jax.ShapeDtypeStruct((HALF, 2 * QUART), BF)


def pack(where, x):
    return pl.pallas_call(
        pack_kernel,
        out_shape=(PIECE,) * 4,
        in_specs=[sm(), vm()],
        out_specs=[vm()] * 4,
        scratch_shapes=[pltpu.VMEM((4, ROWS, QUART), BF)],
        compiler_params=params(),
        cost_estimate=cost(4),
        name="pack",
    )(where, x)


def front_kernel(
    where_ref, x_ref, qkv_w, proj_w, o0, o1, o2, o3, alpha_ref, beta_ref, alpha_half, beta_half, rows_ref,
):
    heads = qkv_w.shape[1] // (3 * HD)
    for h in range(heads):
        for t in range(3):
            ref, base = (alpha_ref, QUART * t) if t < 2 else (beta_ref, 0)
            ref[:, base + HD * h : base + HD * (h + 1)] = qkv_w[:, HD * (3 * h + t) : HD * (3 * h + t + 1)]
    beta_ref[:, QUART:] = proj_w[...]
    rows = pl.ds(pl.multiple_of(where_ref[1] * HBLK, 32), HBLK)
    alpha_half[...] = alpha_ref[rows, :]
    beta_half[...] = beta_ref[rows, :]
    pack_rows(where_ref[0], x_ref, rows_ref, 0)
    for slot, out in enumerate((o0, o1, o2, o3)):
        out[:, :QUART] = rows_ref[slot, :HALF, :]
        out[:, QUART:] = rows_ref[slot, HALF:, :]


def front(where, x, qkv_w, proj_w):
    s = lambda *shape: jax.ShapeDtypeStruct(shape, BF)
    return pl.pallas_call(
        front_kernel,
        out_shape=(PIECE,) * 4
        + (s(QUART, 2 * QUART), s(QUART, 2 * QUART), s(HBLK, 2 * QUART), s(HBLK, 2 * QUART)),
        in_specs=[sm(), vm(), vm(), vm()],
        out_specs=[vm()] * 8,
        scratch_shapes=[pltpu.VMEM((4, ROWS, QUART), BF)],
        compiler_params=params(),
        cost_estimate=cost(5),
        name="token_and_weight_pack",
    )(where, x, qkv_w, proj_w)


def unpack_kernel(where_ref, *refs, bounds):
    pieces, (out_ref, acc_ref, rows_ref) = refs[:-3], refs[-3:]
    mine = where_ref[0]
    acc_ref[...] = jnp.zeros_like(acc_ref)
    index = 0
    for low, high in bounds:
        half = (high - low) // 2
        for slot in range(4):
            piece = pieces[index]
            rows_ref[slot, low : low + half, :] = piece[:, :QUART]
            rows_ref[slot, low + half : high, :] = piece[:, QUART:]
            index += 1

    def one(source, carry):
        slot = jnp.bitwise_xor(mine, source)

        def visit(kind, offset, window):
            span, moved = window_span(window)
            pick = place_window(kind, NQ[kind], moved, SPAN)
            acc_ref[:, span] += tn(rows_ref[slot, pl.ds(offset, NQ[kind]), :], pick)

        each_window(source, visit)
        return carry

    lax.fori_loop(0, 4, one, 0)
    pick = place_window(CORNER, CORNR, LAST - LAST_LOW, IMG_TOK - LAST_LOW)
    acc_ref[:, LAST_LOW:IMG_TOK] += tn(rows_ref[jnp.bitwise_xor(mine, 3), OFFS[3] :, :], pick)
    out_ref[...] = acc_ref[:, :IMG_TOK].astype(out_ref.dtype)


def unpack(where, pieces, dtype, bounds=((0, ROWS),)):
    return pl.pallas_call(
        functools.partial(unpack_kernel, bounds=bounds),
        out_shape=jax.ShapeDtypeStruct((QUART, IMG_TOK), dtype),
        in_specs=[sm()] + [vm()] * len(pieces),
        out_specs=vm(),
        scratch_shapes=[
            pltpu.VMEM((QUART, -(-IMG_TOK // 128) * 128), F32),
            pltpu.VMEM((4, ROWS, QUART), BF),
        ],
        compiler_params=params(),
        cost_estimate=cost(4),
        name="unpack",
    )(where, *pieces)


def join_pieces(pieces, dst_ref):
    for slot, piece in enumerate(pieces):
        dst_ref[:HALF, QUART * slot : QUART * (slot + 1)] = piece[:, :QUART]
        dst_ref[HALF:, QUART * slot : QUART * (slot + 1)] = piece[:, QUART:]


def split_pieces(src_ref, outs):
    half = src_ref.shape[0] // 2
    for slot, out in enumerate(outs):
        out[:, :QUART] = src_ref[:half, QUART * slot : QUART * (slot + 1)]
        out[:, QUART:] = src_ref[half:, QUART * slot : QUART * (slot + 1)]


def adapter_pack_kernel(
    pick_ref, qkv_up, proj_dn, fc1_up, fc2_dn, qkv_dn, fc1_dn, proj_up, fc2_up, gain1, gain2,
    s0, s1, s2, s3, row_ref,
):
    heads = qkv_up.shape[2] // (3 * HD)
    for j, send_ref in enumerate((s0, s1, s2, s3)):
        a = pick_ref[j]
        for h in range(heads):
            for t in range(3):
                send_ref[:RANK, QUART * t + HD * h : QUART * t + HD * (h + 1)] = qkv_up[
                    a, :, HD * (3 * h + t) : HD * (3 * h + t + 1)
                ]
        send_ref[:RANK, 3 * QUART :] = proj_dn[a]
        send_ref[RANK : 2 * RANK, :] = fc1_up[a]
        send_ref[2 * RANK :, :] = fc2_dn[a]
    for i, ref in enumerate((qkv_dn, fc1_dn, proj_up, fc2_up)):
        row_ref[:RANK, QUART * i : QUART * (i + 1)] = ref[pick_ref[0]]
    for i, ref in enumerate((gain1, gain2)):
        row_ref[RANK:, QUART * i : QUART * (i + 1)] = jnp.broadcast_to(ref[...], (RANK, QUART))
    row_ref[RANK:, 2 * QUART :] = jnp.zeros((RANK, 2 * QUART), BF)


def adapter_pack(pick, *mats):
    s = lambda *shape: jax.ShapeDtypeStruct(shape, BF)
    return pl.pallas_call(
        adapter_pack_kernel,
        out_shape=(s(3 * RANK, D),) * 4 + (s(2 * RANK, D),),
        in_specs=[sm()] + [vm()] * 10,
        out_specs=[vm()] * 5,
        compiler_params=params(),
        cost_estimate=cost(2),
        name="adapter_pack",
    )(pick, *mats)


def alpha_block(k, j):
    part = k
    if j == 0:
        return [(part, 0, QUART, None)]
    return [
        (part, QUART + HBLK * (j - 1), HBLK, 0),
        (part, QUART + 3 * HBLK + HBLK * (j - 1), HBLK, 1),
    ]


def beta_block(k, j):
    core, cross = k % 2, k // 2
    base = 3 * core
    if j == 0 and not cross:
        return [(base, 0, QUART, None)]
    row = 0 if j == 0 else HBLK + QUART * (j - 1) + HBLK * cross
    return [(base + 1, row, HBLK, 0), (base + 2, row, HBLK, 1)]


def block_dst(start, flag, half):
    if flag is None:
        return start
    offset = half if flag == 0 else 1 - half
    return pl.multiple_of(start + offset * HBLK, 32)


def prep1_kernel(
    where_ref, p0, p1, p2, p3, q0, q1, q2, q3, q4, q5, r0, r1, r2, r3, a0, a1, a2, a3,
    wqkv_ref, wproj_ref, dqkv, uqkv, dproj, uproj, d1, u1, d2, u2, gain1, gain2,
):
    half = where_ref[1]
    for j, a in enumerate((a0, a1, a2, a3)):
        for t in range(3):
            uqkv[:, D * t + QUART * j : D * t + QUART * (j + 1)] = a[:RANK, QUART * t : QUART * (t + 1)]
        dproj[:, QUART * j : QUART * (j + 1)] = a[:RANK, 3 * QUART :]
        u1[:, D * j : D * (j + 1)] = a[RANK : 2 * RANK, :]
        d2[:, D * j : D * (j + 1)] = a[2 * RANK :, :]
    for k, ref in enumerate((r0, r1, r2, r3)):
        for i, dst in enumerate((dqkv, d1, uproj, u2)):
            dst[:, QUART * k : QUART * (k + 1)] = ref[:RANK, QUART * i : QUART * (i + 1)]
        for i, dst in enumerate((gain1, gain2)):
            dst[:, QUART * k : QUART * (k + 1)] = ref[RANK : RANK + 1, QUART * i : QUART * (i + 1)].astype(F32)
    alpha, beta = (p0, p1, p2, p3), (q0, q1, q2, q3, q4, q5)
    for k in range(4):
        for j in range(4):
            for part, row, count, flag in alpha_block(k, j):
                rows = pl.ds(block_dst(QUART * k, flag, half), count)
                for t in range(2):
                    wqkv_ref[rows, D * t + QUART * j : D * t + QUART * (j + 1)] = alpha[part][
                        row : row + count, QUART * t : QUART * (t + 1)
                    ]
            for part, row, count, flag in beta_block(k, j):
                rows = pl.ds(block_dst(QUART * k, flag, half), count)
                wqkv_ref[rows, 2 * D + QUART * j : 2 * D + QUART * (j + 1)] = beta[part][
                    row : row + count, :QUART
                ]
                rows = pl.ds(block_dst(QUART * j, flag, half), count)
                wproj_ref[rows, QUART * k : QUART * (k + 1)] = beta[part][row : row + count, QUART:]
    for k in range(4):
        rows = slice(QUART * k, QUART * (k + 1))
        for t in range(3):
            cols = slice(D * t, D * (t + 1))
            low = tn(dqkv[:, rows], uqkv[:, cols])
            wqkv_ref[rows, cols] = (wqkv_ref[rows, cols].astype(F32) + low).astype(BF)
        low = tn(dproj[:, rows], uproj[...])
        wproj_ref[rows, :] = (wproj_ref[rows, :].astype(F32) + low).astype(BF)


def prep1(where, alpha, beta, rows, cols):
    s = lambda *shape: jax.ShapeDtypeStruct(shape, BF)
    return pl.pallas_call(
        prep1_kernel,
        out_shape=(
            s(D, 3 * D), s(D, D), s(RANK, D), s(RANK, 3 * D), s(RANK, D), s(RANK, D),
            s(RANK, D), s(RANK, 4 * D), s(RANK, 4 * D), s(RANK, D),
            jax.ShapeDtypeStruct((1, D), F32), jax.ShapeDtypeStruct((1, D), F32),
        ),
        in_specs=[sm()] + [vm()] * 18,
        out_specs=[vm()] * 12,
        compiler_params=params(),
        cost_estimate=cost(7),
        name="attention_weights",
    )(where, *alpha, *beta, *rows, *cols)


def normalize(values):
    center = jnp.sum(values, axis=1, keepdims=True) / D
    shifted = values - center
    inv_std = lax.rsqrt(jnp.sum(shifted * shifted, axis=1, keepdims=True) / D + EPSILON)
    return shifted * inv_std, inv_std


def norm_back(grad, normed, inv_std):
    first = jnp.sum(grad, axis=1, keepdims=True) / D
    second = jnp.sum(grad * normed, axis=1, keepdims=True) / D
    return inv_std * (grad - first - normed * second)


def barrel(values, amount, left):
    for bit in (1, 2, 4, 8):
        moved = pltpu.roll(values, (128 - bit) if left else bit, 1)
        values = jnp.where((amount & bit) != 0, moved, values)
    return values


def low_half(count):
    return lax.broadcasted_iota(jnp.int32, (count, 128), 1) < HD


def pad_rows(tile):
    if tile.shape[0] == KEYS:
        return tile
    return jnp.concatenate([tile, jnp.zeros((KEYS - tile.shape[0], tile.shape[1]), tile.dtype)], axis=0)


def live_rows():
    return lax.broadcasted_iota(jnp.int32, (KEYS, 128), 0) < SLOTS


GROUP = 6
GROUP_BACK = 6


def pair_columns(pair):
    return tuple(slice(D * t + 128 * pair, D * t + 128 * (pair + 1)) for t in range(3))


def attend_window(kind, row0, qkv_ref, att_ref, exp_ref, inv_ref, rel_ref, shift_ref, keys_ref):
    count = NQ[kind]
    rows = pl.ds(row0, count)
    low_q, low_k = low_half(count), low_half(KEYS)
    live = live_rows()
    ones = jnp.where(live, 1.0, 0.0).astype(BF)
    amount = shift_ref[kind, :count, :]
    onehot = keys_ref[kind]
    rel_mat = rel_ref[...]
    for first in range(0, D // 128, GROUP):
        pairs = range(first, first + GROUP)
        heads = [(pair, odd) for pair in pairs for odd in range(2)]
        q_tile = {p: qkv_ref[rows, pair_columns(p)[0]] for p in pairs}
        rel = {p: nn(q_tile[p], rel_mat) for p in pairs}
        rel = {p: barrel(rel[p], amount, True).astype(BF) for p in pairs}
        k_tile = {p: pad_rows(qkv_ref[rows, pair_columns(p)[1]] * BF(HD**-0.5)) for p in pairs}
        scores = {}
        for p, odd in heads:
            if odd:
                q_aug, k_aug = jnp.where(low_q, rel[p], q_tile[p]), jnp.where(low_k, onehot, k_tile[p])
            else:
                q_aug, k_aug = jnp.where(low_q, q_tile[p], rel[p]), jnp.where(low_k, k_tile[p], onehot)
            scores[p, odd] = nt(q_aug, k_aug)
        top = {h: jnp.max(scores[h], axis=1, keepdims=True) for h in heads}
        exponent = {h: jnp.exp(scores[h] - top[h]).astype(BF) for h in heads}
        both = {}
        for p, odd in heads:
            exp_ref[2 * p + odd, rows, :] = exponent[p, odd]
            v_tile = pad_rows(qkv_ref[rows, pair_columns(p)[2]])
            if kind == FULL:
                v_tile = jnp.where(live, v_tile, 0).astype(BF)
            v_aug = jnp.where(low_k, ones, v_tile) if odd else jnp.where(low_k, v_tile, ones)
            both[p, odd] = nn(exponent[p, odd], v_aug)
        for p in pairs:
            cols = pair_columns(p)[0]
            inverse = 1.0 / pltpu.roll(jnp.where(low_q, both[p, 1], both[p, 0]), HD, 1)
            inv_ref[rows, cols] = inverse
            att_ref[rows, cols] = (jnp.where(low_q, both[p, 0], both[p, 1]) * inverse).astype(BF)


PARTS = ((FULL, FULL), (FULL, FULL), (RIGHT, BOTTOM, CORNER))
PART_ROWS = tuple(sum(NQ[kind] for kind in part) for part in PARTS)
PART_OFFS = (0, PART_ROWS[0], PART_ROWS[0] + PART_ROWS[1])


TAIL = ((0, 576), (576, ROWS))


def qkv_kernel(x0, x1, x2, x3, gain_ref, wqkv_ref, x_ref, hid_ref, qkv_a, qkv_b, qkv_c):
    join_pieces((x0, x1, x2, x3), x_ref)
    gain = gain_ref[...]

    def norm_step(i, carry):
        rows = pl.ds(pl.multiple_of(i * 112, 16), 112)
        normed, _ = normalize(x_ref[rows, :].astype(F32))
        hid_ref[rows, :] = (normed * gain).astype(BF)
        return carry

    lax.fori_loop(0, ROWS // 112, norm_step, 0)
    for ref, offset, count in zip((qkv_a, qkv_b, qkv_c), PART_OFFS, PART_ROWS):
        hid = hid_ref[offset : offset + count, :]
        for t in range(3):
            cols = slice(D * t, D * (t + 1))
            ref[:, cols] = nn(hid, wqkv_ref[:, cols]).astype(BF)
    for w in range(4):
        hid_ref[FULLR * w + SLOTS : FULLR * (w + 1), :] = jnp.zeros((FULLR - SLOTS, D), BF)


def qkv_rows(pieces, gain, wqkv):
    s = lambda *shape: jax.ShapeDtypeStruct(shape, BF)
    return pl.pallas_call(
        qkv_kernel,
        out_shape=(s(ROWS, D), s(ROWS, D)) + tuple(s(n, 3 * D) for n in PART_ROWS),
        in_specs=[vm()] * 6,
        out_specs=[vm()] * 5,
        compiler_params=params(),
        cost_estimate=cost(12),
        name="norm_and_qkv",
    )(*pieces, gain, wqkv)


def attention_kernel(qkv_ref, rel_ref, shift_ref, keys_ref, att_ref, exp_ref, inv_ref, *, kinds):
    refs = (qkv_ref, att_ref, exp_ref, inv_ref, rel_ref, shift_ref, keys_ref)
    if kinds[0] == FULL:

        def step(w, carry):
            attend_window(FULL, pl.multiple_of(w * FULLR, 16), *refs)
            return carry

        lax.fori_loop(0, len(kinds), step, 0)
    else:
        row = 0
        for kind in kinds:
            attend_window(kind, row, *refs)
            row += NQ[kind]


def attention(part, qkv, rel, shift, keys):
    rows = PART_ROWS[part]
    s = lambda *shape, dtype=BF: jax.ShapeDtypeStruct(shape, dtype)
    return pl.pallas_call(
        functools.partial(attention_kernel, kinds=PARTS[part]),
        out_shape=(s(rows, D), s(D // HD, rows, KEYS), s(rows, D, dtype=F32)),
        in_specs=[vm()] * 4,
        out_specs=[vm()] * 3,
        compiler_params=params(),
        cost_estimate=cost(10),
        name="attention_forward",
    )(qkv, rel, shift, keys)


def project_kernel(x_ref, att_a, att_b, att_c, wproj_ref, middle_ref):
    for ref, offset, count in zip((att_a, att_b, att_c), PART_OFFS, PART_ROWS):
        rows = slice(offset, offset + count)
        middle_ref[rows, :] = x_ref[rows, :].astype(F32) + nn(ref[...], wproj_ref[...])


def project(x, atts, wproj):
    return pl.pallas_call(
        project_kernel,
        out_shape=jax.ShapeDtypeStruct((ROWS, D), F32),
        in_specs=[vm()] * 5,
        out_specs=vm(),
        compiler_params=params(),
        cost_estimate=cost(5),
        name="projection",
    )(x, *atts, wproj)


CHUNK = 512
LOCK = 2


def mlp_kernel(
    where_ref, middle_ref, g0, g1, g2, g3, gain_ref,
    p0, p1, p2, p3, q0, q1, q2, q3, q4, q5, d1, u1, d2, u2,
    o0, o1, o2, o3, gmid_ref, down1, up1, down2, up2,
    gm_ref, out_rows, h2_ref, acc_mlp, acc_gh, gu1, ad2, w1_ref, w2_ref, sem,
):
    half = where_ref[1]
    copies = []

    def fetch(src, dst):
        copies.append(pltpu.make_async_copy(src, dst, sem.at[len(copies)]))
        copies[-1].start()

    alpha, beta = (p0, p1, p2, p3), (q0, q1, q2, q3, q4, q5)
    for k in range(4):
        for j in range(4):
            for part, row, count, flag in alpha_block(k, j):
                rows = pl.ds(block_dst(QUART * k, flag, half), count)
                fetch(alpha[part].at[row : row + count, :], w1_ref.at[rows, D * j : D * (j + 1)])
            for part, row, count, flag in beta_block(k, j):
                rows = pl.ds(block_dst(QUART * k, flag, half), count)
                fetch(beta[part].at[row : row + count, :], w2_ref.at[rows, D * j : D * (j + 1)])
    join_pieces((g0, g1, g2, g3), gm_ref)
    for copy in copies:
        copy.wait()
    for k in range(4):
        rows = slice(QUART * k, QUART * (k + 1))
        for j in range(4):
            cols = slice(D * j, D * (j + 1))
            low = tn(d1[:, rows], u1[:, cols])
            w1_ref[rows, cols] = (w1_ref[rows, cols].astype(F32) + low).astype(BF)
            low = tn(u2[:, rows], d2[:, cols])
            w2_ref[rows, cols] = (w2_ref[rows, cols].astype(F32) + low).astype(BF)
    gain = gain_ref[...]
    down1[...] = jnp.zeros_like(down1)
    up1[...] = jnp.zeros_like(up1)
    down2[...] = jnp.zeros_like(down2)
    up2[...] = jnp.zeros_like(up2)

    def tile_step(t, carry):
        rows = pl.ds(pl.multiple_of(t * HALF, 16), HALF)
        normed, _ = normalize(middle_ref[rows, :])
        h2 = (normed * gain).astype(BF)
        h2_ref[...] = h2
        gm = gm_ref[rows, :]
        ad1 = nt(d1[...], h2).astype(BF)
        gu2 = nt(u2[...], gm).astype(BF)
        acc_mlp[...] = jnp.zeros_like(acc_mlp)
        acc_gh[...] = jnp.zeros_like(acc_gh)
        gu1[...] = jnp.zeros_like(gu1)
        ad2[...] = jnp.zeros_like(ad2)

        def chunk_step(c, inner_carry):
            spans = [
                pl.ds(pl.multiple_of((c * LOCK + i) * CHUNK, CHUNK), CHUNK) for i in range(LOCK)
            ]
            h2 = h2_ref[...]
            gm = gm_ref[rows, :]
            inner = [nn(h2, w1_ref[:, span]) for span in spans]
            gact = [nn(gm, w2_ref[:, span]) for span in spans]
            act, ginner = [], []
            for i in range(LOCK):
                half = 0.5 * (1.0 + lax.erf(inner[i] * 2**-0.5))
                act.append((inner[i] * half).astype(BF))
                slope = half + inner[i] * (jnp.exp(-0.5 * inner[i] * inner[i]) * (2 * np.pi) ** -0.5)
                ginner.append((gact[i] * slope).astype(BF))
            for i, span in enumerate(spans):
                acc_mlp[...] += nt(act[i], w2_ref[:, span])
                acc_gh[...] += nt(ginner[i], w1_ref[:, span])
                up1[:, span] += nn(ad1, ginner[i])
                gu1[...] += nt(u1[:, span], ginner[i])
                ad2[...] += nt(d2[:, span], act[i])
                down2[:, span] += nn(gu2, act[i])
            return inner_carry

        lax.fori_loop(0, 4 * D // (CHUNK * LOCK), chunk_step, 0)
        down1[...] += nn(gu1[...].astype(BF), h2_ref[...])
        up2[...] += nn(ad2[...].astype(BF), gm_ref[rows, :])
        middle = middle_ref[rows, :]
        out_rows[rows, :] = (middle + acc_mlp[...]).astype(BF)
        normed, inv_std = normalize(middle)
        gmid_ref[rows, :] = gm_ref[rows, :].astype(F32) + norm_back(acc_gh[...] * gain, normed, inv_std)
        return carry

    lax.fori_loop(0, 2, tile_step, 0)
    split_pieces(out_rows, (o0, o1, o2, o3))


def mlp(where, middle, pieces, gain, alpha, beta, d1, u1, d2, u2):
    s = lambda *shape, dtype=F32: jax.ShapeDtypeStruct(shape, dtype)
    return pl.pallas_call(
        mlp_kernel,
        out_shape=(PIECE,) * 4
        + (s(ROWS, D), s(RANK, D), s(RANK, 4 * D), s(RANK, 4 * D), s(RANK, D)),
        in_specs=[sm()] + [vm()] * 6 + [pl.BlockSpec(memory_space=pl.ANY)] * 10 + [vm()] * 4,
        out_specs=[vm()] * 9,
        scratch_shapes=[
            pltpu.VMEM((ROWS, D), BF), pltpu.VMEM((ROWS, D), BF), pltpu.VMEM((HALF, D), BF),
            pltpu.VMEM((HALF, D), F32), pltpu.VMEM((HALF, D), F32),
            pltpu.VMEM((RANK, HALF), F32), pltpu.VMEM((RANK, HALF), F32),
            pltpu.VMEM((D, 4 * D), BF), pltpu.VMEM((D, 4 * D), BF),
            pltpu.SemaphoreType.DMA((4 * 4 * 4,)),
        ],
        compiler_params=params(),
        cost_estimate=cost(48),
        name="mlp_forward_backward",
    )(where, middle, *pieces, gain, *alpha, *beta, d1, u1, d2, u2)


def attend_back_window(
    kind, row0, qkv_ref, att_ref, exp_ref, inv_ref, gatt_ref, gqkv_ref, rel_ref, shift_ref, keys_ref
):
    count = NQ[kind]
    rows = pl.ds(row0, count)
    low_q, low_k = low_half(count), low_half(KEYS)
    live = live_rows()
    lane_k = lax.broadcasted_iota(jnp.int32, (KEYS, 128), 1) % HD
    lane_q = lax.broadcasted_iota(jnp.int32, (count, 128), 1) % HD
    ones = jnp.where(live & (lane_k < 2), 1.0, 0.0).astype(BF)
    across = jnp.where(
        low_half(128) != (lax.broadcasted_iota(jnp.int32, (128, 128), 0) < HD), -1.0, 0.0
    ).astype(BF)
    amount = shift_ref[kind, :count, :]
    onehot = keys_ref[kind]
    rel_mat = rel_ref[...]
    for first in range(0, D // 128, GROUP_BACK):
        pairs = range(first, first + GROUP_BACK)
        heads = [(pair, odd) for pair in pairs for odd in range(2)]
        go_tile = {
            p: (gatt_ref[rows, pair_columns(p)[0]].astype(F32) * inv_ref[rows, pair_columns(p)[0]]).astype(BF)
            for p in pairs
        }
        delta = {
            p: nn((go_tile[p].astype(F32) * att_ref[rows, pair_columns(p)[0]].astype(F32)).astype(BF), across)
            for p in pairs
        }
        go_t = {p: go_tile[p].T for p in pairs}
        gv = {}
        for p, odd in heads:
            gv[p, odd] = nn(go_t[p][HD * odd : HD * (odd + 1), :], exp_ref[2 * p + odd, rows, :])
        gscore = {}
        for p in pairs:
            high = delta[p].astype(BF)
            rest = (delta[p] - high.astype(F32)).astype(BF)
            low_delta = jnp.where(lane_q == 0, high, jnp.where(lane_q == 1, rest, 0)).astype(BF)
            v_tile = pad_rows(qkv_ref[rows, pair_columns(p)[2]])
            if kind == FULL:
                v_tile = jnp.where(live, v_tile, 0).astype(BF)
            gscore[p, 0] = nt(jnp.where(low_q, go_tile[p], low_delta), jnp.where(low_k, v_tile, ones))
            gscore[p, 1] = nt(jnp.where(low_q, low_delta, go_tile[p]), jnp.where(low_k, ones, v_tile))
        q_t = {p: qkv_ref[rows, pair_columns(p)[0]].T for p in pairs}
        gs = {(p, odd): (exp_ref[2 * p + odd, rows, :].astype(F32) * gscore[p, odd]).astype(BF) for p, odd in heads}
        gk = {(p, odd): nn(q_t[p][HD * odd : HD * (odd + 1), :], gs[p, odd]) for p, odd in heads}
        gq = {}
        for p in pairs:
            k_tile = pad_rows(qkv_ref[rows, pair_columns(p)[1]] * BF(HD**-0.5))
            gq[p, 0] = nn(gs[p, 0], jnp.where(low_k, k_tile, onehot))
            gq[p, 1] = nn(gs[p, 1], jnp.where(low_k, onehot, k_tile))
        sums = {p: barrel(jnp.where(low_q, gq[p, 1], gq[p, 0]), amount, False).astype(BF) for p in pairs}
        for p in pairs:
            cols, kcols, vcols = pair_columns(p)
            gv_tile = jnp.concatenate([gv[p, 0], gv[p, 1]], axis=0).astype(BF).T
            gqkv_ref[rows, vcols] = gv_tile[:count, :]
            gk_tile = (jnp.concatenate([gk[p, 0], gk[p, 1]], axis=0) * HD**-0.5).astype(BF).T
            gqkv_ref[rows, kcols] = gk_tile[:count, :]
            gqkv_ref[rows, cols] = (jnp.where(low_q, gq[p, 0], gq[p, 1]) + nt(sums[p], rel_mat)).astype(BF)


def attention_back_kernel(
    gmid_ref, hid_ref, qkv_a, qkv_b, qkv_c, att_a, att_b, att_c, exp_a, exp_b, exp_c, inv_a, inv_b, inv_c,
    wproj_ref, rel_ref, shift_ref, keys_ref, dqkv, uqkv, dproj, uproj,
    gqkv_ref, down_q, up_q, down_p, up_p, gb_ref, gatt_ref, att_ref,
):
    gb_ref[...] = gmid_ref[...].astype(BF)
    gatt_ref[...] = nt(gb_ref[...], wproj_ref[...]).astype(BF)
    for ref, offset, count in zip((att_a, att_b, att_c), PART_OFFS, PART_ROWS):
        att_ref[offset : offset + count, :] = ref[...]
    up_p[...] = nn(nt(dproj[...], att_ref[...]).astype(BF), gb_ref[...])
    down_p[...] = nn(nt(uproj[...], gb_ref[...]).astype(BF), att_ref[...])
    tables = (rel_ref, shift_ref, keys_ref)
    for part, parts in enumerate(
        ((qkv_a, att_a, exp_a, inv_a), (qkv_b, att_b, exp_b, inv_b), (qkv_c, att_c, exp_c, inv_c))
    ):
        span = pl.ds(PART_OFFS[part], PART_ROWS[part])
        refs = parts + (gatt_ref.at[span, :], gqkv_ref.at[span, :]) + tables
        if PARTS[part][0] == FULL:

            def step(w, carry, refs=refs):
                attend_back_window(FULL, pl.multiple_of(w * FULLR, 16), *refs)
                return carry

            lax.fori_loop(0, len(PARTS[part]), step, 0)
        else:
            row = 0
            for kind in PARTS[part]:
                attend_back_window(kind, row, *refs)
                row += NQ[kind]
    up_q[...] = nn(nt(dqkv[...], hid_ref[...]).astype(BF), gqkv_ref[...])
    down_q[...] = nn(nt(uqkv[...], gqkv_ref[...]).astype(BF), hid_ref[...])


def attention_back(gmid, hid, qkvs, atts, exps, invs, wproj, rel, shift, keys, dqkv, uqkv, dproj, uproj):
    s = lambda *shape, dtype=F32: jax.ShapeDtypeStruct(shape, dtype)
    return pl.pallas_call(
        attention_back_kernel,
        out_shape=(s(ROWS, 3 * D, dtype=BF), s(RANK, D), s(RANK, 3 * D), s(RANK, D), s(RANK, D)),
        in_specs=[vm()] * 22,
        out_specs=[vm()] * 5,
        scratch_shapes=[pltpu.VMEM((ROWS, D), BF)] * 3,
        compiler_params=params(),
        cost_estimate=cost(45),
        name="attention_backward",
    )(gmid, hid, *qkvs, *atts, *exps, *invs, wproj, rel, shift, keys, dqkv, uqkv, dproj, uproj)


def token_grad_kernel(gmid_hbm, x_hbm, gqkv_hbm, gain_ref, wqkv_ref, o0, o1, o2, o3,
                      gmid_ref, x_ref, gqkv_ref, gh_ref, out_rows, sem, *, low, high):
    span = pl.ds(low, high - low)
    copies = [
        pltpu.make_async_copy(src.at[span, :], dst, sem.at[i])
        for i, (src, dst) in enumerate(((gqkv_hbm, gqkv_ref), (x_hbm, x_ref), (gmid_hbm, gmid_ref)))
    ]
    for copy in copies:
        copy.start()
    copies[0].wait()
    gh_ref[...] = nt(gqkv_ref[...], wqkv_ref[...])
    copies[1].wait()
    copies[2].wait()
    gain = gain_ref[...]

    def norm_step(i, carry):
        rows = pl.ds(pl.multiple_of(i * TAIL_STEP, 16), TAIL_STEP)
        normed, inv_std = normalize(x_ref[rows, :].astype(F32))
        back = norm_back(gh_ref[rows, :] * gain, normed, inv_std)
        out_rows[rows, :] = (gmid_ref[rows, :] + back).astype(BF)
        return carry

    lax.fori_loop(0, (high - low) // TAIL_STEP, norm_step, 0)
    split_pieces(out_rows, (o0, o1, o2, o3))


TAIL_STEP = 32


def token_grad(gmid, x, gqkv, gain, wqkv, low, high):
    count = high - low
    hbm = pl.BlockSpec(memory_space=pl.ANY)
    return pl.pallas_call(
        functools.partial(token_grad_kernel, low=low, high=high),
        out_shape=(jax.ShapeDtypeStruct((count // 2, 2 * QUART), BF),) * 4,
        in_specs=[hbm, hbm, hbm, vm(), vm()],
        out_specs=[vm()] * 4,
        scratch_shapes=[
            pltpu.VMEM((count, D), F32), pltpu.VMEM((count, D), BF), pltpu.VMEM((count, 3 * D), BF),
            pltpu.VMEM((count, D), F32), pltpu.VMEM((count, D), BF), pltpu.SemaphoreType.DMA((3,)),
        ],
        compiler_params=params(),
        cost_estimate=cost(8),
        name="token_gradient",
    )(gmid, x, gqkv, gain, wqkv)


def grad_pack_kernel(where_ref, down_q, up_q, down_p, up_p, down1, up1, down2, up2, o0, o1, o2, o3, buf_ref):
    mine = where_ref[0]
    for k in range(4):
        for i, ref in enumerate((down_q, down1, up_p, up2)):
            buf_ref[k, :RANK, QUART * i : QUART * (i + 1)] = ref[:, QUART * k : QUART * (k + 1)]
    for dest in range(4):
        k = jnp.bitwise_xor(mine, dest)
        ranks = slice(RANK // 4 * dest, RANK // 4 * (dest + 1))
        for j in range(4):
            base = RANK + 12 * j
            for t in range(3):
                buf_ref[k, base : base + 4, QUART * t : QUART * (t + 1)] = up_q[
                    ranks, D * t + QUART * j : D * t + QUART * (j + 1)
                ]
            buf_ref[k, base : base + 4, 3 * QUART :] = down_p[ranks, QUART * j : QUART * (j + 1)]
            buf_ref[k, base + 4 : base + 8, :] = up1[ranks, D * j : D * (j + 1)]
            buf_ref[k, base + 8 : base + 12, :] = down2[ranks, D * j : D * (j + 1)]
    for k, out in enumerate((o0, o1, o2, o3)):
        out[...] = buf_ref[k].astype(BF)


def grad_pack(where, *grads):
    return pl.pallas_call(
        grad_pack_kernel,
        out_shape=(jax.ShapeDtypeStruct((4 * RANK, D), BF),) * 4,
        in_specs=[sm()] + [vm()] * 8,
        out_specs=[vm()] * 4,
        scratch_shapes=[pltpu.VMEM((4, 4 * RANK, D), F32)],
        compiler_params=params(),
        cost_estimate=cost(2),
        name="adapter_grad_pack",
    )(where, *grads)


def grad_sum_kernel(g0, g1, g2, g3, o0, o1, o2, o3, buf_ref):
    total = g0[...].astype(F32) + g1[...].astype(F32) + g2[...].astype(F32) + g3[...].astype(F32)
    buf_ref[...] = jnp.zeros_like(buf_ref)
    buf_ref[:RANK, :] = total[:RANK, :]
    for j, out in enumerate((o0, o1, o2, o3)):
        buf_ref[RANK : RANK + 12, :] = total[RANK + 12 * j : RANK + 12 * (j + 1), :]
        out[...] = buf_ref[...].astype(BF)


def grad_sum(pieces):
    return pl.pallas_call(
        grad_sum_kernel,
        out_shape=(jax.ShapeDtypeStruct((2 * RANK, D), BF),) * 4,
        in_specs=[vm()] * 4,
        out_specs=[vm()] * 4,
        scratch_shapes=[pltpu.VMEM((2 * RANK, D), F32)],
        compiler_params=params(),
        cost_estimate=cost(2),
        name="adapter_grad_sum",
    )(*pieces)


def grad_adapters_kernel(index_ref, x_ref, qkv_dn, fc1_dn, proj_up, fc2_up, rest_ref, acc_ref):
    acc_ref[...] = jnp.zeros_like(acc_ref)

    def add(i, carry):
        acc_ref[index_ref[i]] += x_ref[i].astype(F32)
        return carry

    lax.fori_loop(0, x_ref.shape[0], add, 0)
    for i, ref in enumerate((qkv_dn, fc1_dn, proj_up, fc2_up)):
        ref[...] = acc_ref[:, :RANK, QUART * i : QUART * (i + 1)]
    rest_ref[...] = acc_ref[:, RANK:, :].astype(BF)


def grad_adapters(index, x):
    s = lambda n, dtype=F32: jax.ShapeDtypeStruct((ADAPT, RANK, n), dtype)
    return pl.pallas_call(
        grad_adapters_kernel,
        out_shape=(s(QUART), s(QUART), s(QUART), s(QUART), s(D, BF)),
        in_specs=[sm(), vm()],
        out_specs=[vm()] * 5,
        scratch_shapes=[pltpu.VMEM((ADAPT, 2 * RANK, D), F32)],
        compiler_params=params(),
        cost_estimate=cost(2),
        name="adapter_grad_by_adapter",
    )(index, x)


def grad_join_kernel(where_ref, r0, r1, r2, r3, qkv_up, proj_dn, fc1_up, fc2_dn, buf_ref):
    mine = where_ref[0]
    heads = qkv_up.shape[2] // (3 * HD)
    for k, ref in enumerate((r0, r1, r2, r3)):
        buf_ref[jnp.bitwise_xor(mine, k)] = ref[...].astype(F32)
    for source in range(4):
        ranks = slice(RANK // 4 * source, RANK // 4 * (source + 1))
        for h in range(heads):
            for t in range(3):
                qkv_up[:, ranks, HD * (3 * h + t) : HD * (3 * h + t + 1)] = buf_ref[
                    source, :, 0:4, QUART * t + HD * h : QUART * t + HD * (h + 1)
                ]
        proj_dn[:, ranks, :] = buf_ref[source, :, 0:4, 3 * QUART :]
        fc1_up[:, ranks, :] = buf_ref[source, :, 4:8, :]
        fc2_dn[:, ranks, :] = buf_ref[source, :, 8:12, :]


def grad_join(where, pieces):
    s = lambda n: jax.ShapeDtypeStruct((ADAPT, RANK, n), F32)
    return pl.pallas_call(
        grad_join_kernel,
        out_shape=(s(3 * QUART), s(QUART), s(D), s(D)),
        in_specs=[sm()] + [vm()] * 4,
        out_specs=[vm()] * 4,
        scratch_shapes=[pltpu.VMEM((4, ADAPT, RANK, D), F32)],
        compiler_params=params(),
        cost_estimate=cost(2),
        name="adapter_grad_join",
    )(where, *pieces)


def flip(values, axis, distance):
    size = lax.axis_size(axis)
    return lax.ppermute(values, axis, [(i, i ^ distance) for i in range(size)])


def exchange(slots, axis):
    return [slots[0]] + [flip(slots[k], axis, k) for k in range(1, 4)]


def after(values, *deps):
    return lax.optimization_barrier((tuple(values), deps))[0]


def col_halves(half):
    return jnp.concatenate([flip(half, "col", j) for j in range(1, 4)], axis=0)


def col_pairs(half, other_row):
    two = jnp.concatenate([half, other_row], axis=0)
    return jnp.concatenate([other_row] + [flip(two, "col", j) for j in range(1, 4)], axis=0)


def rel_matrix(rel_h, rel_w):
    pad = jnp.zeros((32 - (2 * WIN - 1), HD), BF)
    block = jnp.concatenate([rel_h[::-1], pad, rel_w[::-1], pad], axis=0).T
    zero = jnp.zeros((HD, HD), BF)
    return jnp.concatenate(
        [jnp.concatenate([zero, block], axis=1), jnp.concatenate([block, zero], axis=1)], axis=0
    )


def body(
    tokens, grad_out, adapter_index, norm1_gain, norm2_gain, qkv_weight, proj_weight, fc1_weight, fc2_weight,
    rel_h, rel_w, qkv_down, qkv_up, proj_down, proj_up, fc1_down, fc1_up, fc2_down, fc2_up,
):
    members = lax.axis_size("col")
    batches = lax.axis_size("dp")
    row_index, col_index, dp_index = lax.axis_index("row"), lax.axis_index("col"), lax.axis_index("dp")
    half = dp_index % 2
    where = jnp.stack([row_index, half]).astype(jnp.int32)
    slot_images = (
        jnp.bitwise_xor(dp_index, jnp.arange(batches, dtype=jnp.int32))[:, None] * members
        + jnp.bitwise_xor(col_index, jnp.arange(members, dtype=jnp.int32))[None, :]
    ).reshape(-1)
    slot_adapters = jnp.sum(
        jnp.where(
            slot_images[:, None] == jnp.arange(adapter_index.shape[0], dtype=jnp.int32)[None, :],
            adapter_index[:, 0][None, :],
            0,
        ),
        axis=1,
    )
    pick = jnp.concatenate([slot_adapters[:4], half[None]]).astype(jnp.int32)
    swap = lambda m: jnp.swapaxes(m, 1, 2)

    rel = rel_matrix(rel_h, rel_w)
    shift, keys = jnp.asarray(SHIFT_NP), jnp.asarray(KEYS_NP)

    *token_slots, alpha_own, beta_own, alpha_half, beta_half = front(where, tokens, qkv_weight, proj_weight)
    b0 = flip(beta_half, "row", 2)
    alpha_near = col_halves(alpha_half)
    x_pieces = exchange(token_slots, "row")
    beta_near = col_pairs(beta_half, b0)
    alpha_far = flip(alpha_near, "dp", 1)
    g = jnp.concatenate([alpha_own, alpha_near, alpha_far], axis=0)
    g, *x_pieces = after((g, *x_pieces))
    gy = flip(g, "row", 2)
    beta_far = flip(beta_near, "dp", 1)

    *send, row_adapters = adapter_pack(
        pick, qkv_up, swap(proj_down), fc1_up, swap(fc2_down), swap(qkv_down), swap(fc1_down), proj_up, fc2_up,
        norm1_gain.reshape(1, -1), norm2_gain.reshape(1, -1),
    )
    *send, row_adapters = after((*send, row_adapters), alpha_near)
    col_adapters = exchange(send, "col")
    row_adapters = exchange([row_adapters] * 4, "row")

    fc1_half = lax.dynamic_slice_in_dim(fc1_weight, half * HBLK, HBLK, 0)
    fc2_half = lax.dynamic_slice_in_dim(fc2_weight, half * HBLK, HBLK, 0)
    fc1_half, fc2_half = after((fc1_half, fc2_half), *col_adapters)
    fc1_near = [flip(fc1_half, "col", j) for j in range(1, 4)]
    c0 = flip(fc2_half, "row", 2)
    grad_slots = pack(where, grad_out)

    alpha1 = [g, flip(g, "row", 1), gy, flip(gy, "row", 1)]
    beta1 = [beta_own, beta_near, beta_far] + [flip(m, "row", 1) for m in (beta_own, beta_near, beta_far)]
    wqkv, wproj, dqkv, uqkv, dproj, uproj, d1, u1, d2, u2, gain1, gain2 = prep1(
        where, alpha1, beta1, row_adapters, col_adapters
    )
    *grad_slots, wqkv = after((*grad_slots, wqkv), c0)
    g_pieces = exchange(grad_slots, "row")
    fc2_two = after((jnp.concatenate([fc2_half, c0], axis=0),), wqkv)[0]
    fc2_near = [flip(fc2_two, "col", j) for j in range(1, 4)]
    fc1_near = after(tuple(fc1_near), wqkv)
    fc1_near = jnp.concatenate(fc1_near, axis=0)
    fc1_far = flip(fc1_near, "dp", 1)
    x, hid, *qkvs = qkv_rows(x_pieces, gain1, wqkv)
    *qkvs, fc1_far = after((*qkvs, fc1_far))
    h = jnp.concatenate([fc1_weight, fc1_near, fc1_far], axis=0)
    hy = flip(h, "row", 2)
    part0 = attention(0, qkvs[0], rel, shift, keys)
    qkv1, *fc2_near = after((qkvs[1], *fc2_near), part0[0])
    fc2_near = jnp.concatenate([c0] + fc2_near, axis=0)
    fc2_far = flip(fc2_near, "dp", 1)
    part1 = attention(1, qkv1, rel, shift, keys)
    qkv2, hy = after((qkvs[2], hy), part1[0])
    alpha2 = [h, flip(h, "row", 1), hy, flip(hy, "row", 1)]
    part2 = attention(2, qkv2, rel, shift, keys)
    atts, exps, invs = zip(part0, part1, part2)
    middle = project(x, atts, wproj)
    middle, fc2_far, *g_pieces = after((middle, fc2_far, *g_pieces))
    beta2 = [fc2_weight, fc2_near, fc2_far] + [flip(m, "row", 1) for m in (fc2_weight, fc2_near, fc2_far)]

    *out_slots, gmid, down1, up1, down2, up2 = mlp(where, middle, g_pieces, gain2, alpha2, beta2, d1, u1, d2, u2)
    out_pieces = exchange(out_slots, "row")
    gqkv, down_q, up_q, down_p, up_p = attention_back(
        gmid, hid, qkvs, atts, exps, invs, wproj, rel, shift, keys, dqkv, uqkv, dproj, uproj
    )
    gqkv, down_q, up_q, down_p, up_p = after((gqkv, down_q, up_q, down_p, up_p), *out_pieces)
    packed = grad_pack(where, down_q, up_q, down_p, up_p, down1, up1, down2, up2)
    *packed, gqkv = after((*packed, gqkv))
    row_sums = exchange(packed, "row")
    back0 = token_grad(gmid, x, gqkv, gain1, wqkv, *TAIL[0])
    *row_sums, gqkv = after((*row_sums, gqkv), back0[0])
    back_pieces = exchange(back0, "row")
    back1 = token_grad(gmid, x, gqkv, gain1, wqkv, *TAIL[1])
    *row_sums, = after(tuple(row_sums), back1[0])
    back_pieces += exchange(back1, "row")
    summed = grad_sum(row_sums)
    images = jnp.stack(exchange(summed, "col"))
    step = 1
    while step < batches:
        images = jnp.concatenate([images, flip(images, "dp", step)], axis=0)
        step *= 2
    qkv_dn, fc1_dn, proj_upg, fc2_upg, rest = grad_adapters(slot_adapters.astype(jnp.int32), images)
    rests = [rest] + [flip(rest, "row", k) for k in range(1, 4)]
    qkv_upg, proj_dn, fc1_upg, fc2_dn = grad_join(where, rests)
    result = unpack(where, out_pieces, BF)
    grad_tokens = unpack(where, back_pieces, F32, TAIL)
    return (
        result, grad_tokens,
        swap(qkv_dn), qkv_upg, swap(proj_dn), proj_upg, swap(fc1_dn), fc1_upg, swap(fc2_dn), fc2_upg,
    )


def solution(mesh):
    return jax.shard_map(
        body,
        mesh=mesh,
        in_specs=(
            P("row", ("dp", "col")), P("row", ("dp", "col")), P(), P("row"), P("row"),
            P("row", "col"), P("col", "row"), P("row", "col"), P("row", "col"), P(), P(),
            P(None, "row", None), P(None, None, "col"), P(None, "col", None), P(None, None, "row"),
            P(None, "row", None), P(None, None, "col"), P(None, "col", None), P(None, None, "row"),
        ),
        out_specs=(
            P("row", ("dp", "col")), P("row", ("dp", "col")),
            P(None, "row", None), P(None, None, "col"), P(None, "col", None), P(None, None, "row"),
            P(None, "row", None), P(None, None, "col"), P(None, "col", None), P(None, None, "row"),
        ),
        check_vma=False,
    )
```

```python
import functools

import jax
import jax.numpy as jnp
import numpy as np
from jax import lax
from jax.experimental import pallas as pl
from jax.experimental.pallas import tpu as pltpu
from jax.sharding import PartitionSpec as P

D = 768
HD = 64
WIN = 14
SLOTS = WIN * WIN
SIDE = 64
ADAPT = 8
NWIN = 5
IMG_TOK = NWIN * NWIN * SLOTS
RANK = 16
EDGE = SIDE - (NWIN - 1) * WIN
QUART = D // 4
FULLR = 208
KEYS = 208
EDGER = EDGE * WIN
CORNR = EDGE * EDGE
ROWS = 4 * FULLR + 2 * EDGER + CORNR
HALF = ROWS // 2
HBLK = QUART // 2
EPSILON = 1e-06
BF = jnp.bfloat16
F32 = jnp.float32
VMEM_LIMIT = 60 * 1024 * 1024

FULL, RIGHT, BOTTOM, CORNER = 0, 1, 2, 3
NQ = (FULLR, EDGER, EDGER, CORNR)
OFFS = (0, 4 * FULLR, 4 * FULLR + EDGER, 4 * FULLR + 2 * EDGER)


def slot_order(kind):
    rows = EDGE if kind in (BOTTOM, CORNER) else WIN
    cols = EDGE if kind in (RIGHT, CORNER) else WIN
    kept = [a * WIN + b for a in range(rows) for b in range(cols)]
    rest = [s for s in range(SLOTS) if s not in set(kept)]
    return kept, kept + rest


def build_tables():
    shift = np.zeros((4, FULLR, 128), np.int32)
    keys = np.zeros((4, KEYS, 128), np.float32)
    for kind in range(4):
        kept, order = slot_order(kind)
        for i, s in enumerate(kept):
            for base in (0, 64):
                shift[kind, i, base : base + 32] = WIN - 1 - s // WIN
                shift[kind, i, base + 32 : base + 64] = WIN - 1 - s % WIN
        spare = order[0] if kind == FULL else order[-1]
        for i, s in enumerate(order + [spare] * (KEYS - SLOTS)):
            for base in (0, 64):
                keys[kind, i, base + s // WIN] = 1.0
                keys[kind, i, base + 32 + s % WIN] = 1.0
    return shift, keys.astype(jnp.bfloat16)


SHIFT_NP, KEYS_NP = build_tables()


def nn(a, b):
    return jnp.dot(a, b, preferred_element_type=F32)


def nt(a, b):
    return lax.dot_general(a, b, (((1,), (1,)), ((), ())), preferred_element_type=F32)


def tn(a, b):
    return lax.dot_general(a, b, (((0,), (0,)), ((), ())), preferred_element_type=F32)


def vm():
    return pl.BlockSpec(memory_space=pltpu.VMEM)


def sm():
    return pl.BlockSpec(memory_space=pltpu.SMEM)


def params(**kw):
    return pltpu.CompilerParams(vmem_limit_bytes=VMEM_LIMIT, **kw)


def cost(us):
    return pl.CostEstimate(flops=int(us * 9e8), transcendentals=0, bytes_accessed=0)


def place_window(kind, count, moved, width, spare=-100000):
    row = lax.broadcasted_iota(jnp.int32, (count, width), 0)
    lane = lax.broadcasted_iota(jnp.int32, (count, width), 1)
    if kind in (RIGHT, CORNER):
        src = (row // EDGE) * WIN + row % EDGE
    else:
        src = jnp.where(row < SLOTS, row, spare)
    return (lane == src + moved).astype(F32).astype(BF)


def window_list(dest):
    items = [(FULL, FULLR * j, NWIN * dest + j) for j in range(4)]
    items.append((RIGHT, OFFS[1], NWIN * dest + 4))
    items.append((BOTTOM, OFFS[2], NWIN * 4 + dest))
    if dest == 3:
        items.append((CORNER, OFFS[3], NWIN * NWIN - 1))
    return items


def window_span(window):
    start = window * SLOTS
    low = start // 128 * 128
    high = min(-(-(start + SLOTS) // 128) * 128, IMG_TOK)
    return low, high, start - low


def pack_rows(mine, x_ref, rows_ref, spare):
    for dest in range(4):
        slot = jnp.bitwise_xor(mine, dest)
        if dest != 3:
            rows_ref[slot, OFFS[3] :, :] = jnp.zeros((CORNR, QUART), BF)
        for kind, offset, window in window_list(dest):
            low, high, moved = window_span(window)
            pick = place_window(kind, NQ[kind], moved, high - low, spare)
            rows_ref[slot, offset : offset + NQ[kind], :] = nt(pick, x_ref[:, low:high]).astype(BF)


def pack_kernel(where_ref, x_ref, o0, o1, o2, o3, rows_ref):
    pack_rows(where_ref[0], x_ref, rows_ref, -100000)
    for slot, out in enumerate((o0, o1, o2, o3)):
        out[:, :QUART] = rows_ref[slot, :HALF, :]
        out[:, QUART:] = rows_ref[slot, HALF:, :]


PIECE = jax.ShapeDtypeStruct((HALF, 2 * QUART), BF)


def pack(where, x):
    return pl.pallas_call(
        pack_kernel,
        out_shape=(PIECE,) * 4,
        in_specs=[sm(), vm()],
        out_specs=[vm()] * 4,
        scratch_shapes=[pltpu.VMEM((4, ROWS, QUART), BF)],
        compiler_params=params(),
        cost_estimate=cost(4),
        name="pack",
    )(where, x)


def front_kernel(
    where_ref, x_ref, qkv_w, proj_w, o0, o1, o2, o3, alpha_ref, beta_ref, alpha_half, beta_half, rows_ref,
):
    heads = qkv_w.shape[1] // (3 * HD)
    for h in range(heads):
        for t in range(3):
            ref, base = (alpha_ref, QUART * t) if t < 2 else (beta_ref, 0)
            ref[:, base + HD * h : base + HD * (h + 1)] = qkv_w[:, HD * (3 * h + t) : HD * (3 * h + t + 1)]
    beta_ref[:, QUART:] = proj_w[...]
    rows = pl.ds(pl.multiple_of(where_ref[1] * HBLK, 32), HBLK)
    alpha_half[...] = alpha_ref[rows, :]
    beta_half[...] = beta_ref[rows, :]
    pack_rows(where_ref[0], x_ref, rows_ref, 0)
    for slot, out in enumerate((o0, o1, o2, o3)):
        out[:, :QUART] = rows_ref[slot, :HALF, :]
        out[:, QUART:] = rows_ref[slot, HALF:, :]


def front(where, x, qkv_w, proj_w):
    s = lambda *shape: jax.ShapeDtypeStruct(shape, BF)
    return pl.pallas_call(
        front_kernel,
        out_shape=(PIECE,) * 4
        + (s(QUART, 2 * QUART), s(QUART, 2 * QUART), s(HBLK, 2 * QUART), s(HBLK, 2 * QUART)),
        in_specs=[sm(), vm(), vm(), vm()],
        out_specs=[vm()] * 8,
        scratch_shapes=[pltpu.VMEM((4, ROWS, QUART), BF)],
        compiler_params=params(),
        cost_estimate=cost(5),
        name="token_and_weight_pack",
    )(where, x, qkv_w, proj_w)


def unpack_kernel(where_ref, *refs, bounds):
    pieces, (out_ref, acc_ref, rows_ref) = refs[:-3], refs[-3:]
    mine = where_ref[0]
    acc_ref[...] = jnp.zeros_like(acc_ref)
    index = 0
    for low, high in bounds:
        half = (high - low) // 2
        for slot in range(4):
            piece = pieces[index]
            rows_ref[slot, low : low + half, :] = piece[:, :QUART]
            rows_ref[slot, low + half : high, :] = piece[:, QUART:]
            index += 1

    for source in range(4):
        slot = jnp.bitwise_xor(mine, source)
        for kind, offset, window in window_list(source):
            low, high, moved = window_span(window)
            pick = place_window(kind, NQ[kind], moved, high - low)
            acc_ref[:, low:high] += tn(rows_ref[slot, offset : offset + NQ[kind], :], pick)
    out_ref[...] = acc_ref[:, :IMG_TOK].astype(out_ref.dtype)


def unpack(where, pieces, dtype, bounds=((0, ROWS),)):
    return pl.pallas_call(
        functools.partial(unpack_kernel, bounds=bounds),
        out_shape=jax.ShapeDtypeStruct((QUART, IMG_TOK), dtype),
        in_specs=[sm()] + [vm()] * len(pieces),
        out_specs=vm(),
        scratch_shapes=[
            pltpu.VMEM((QUART, -(-IMG_TOK // 128) * 128), F32),
            pltpu.VMEM((4, ROWS, QUART), BF),
        ],
        compiler_params=params(),
        cost_estimate=cost(4),
        name="unpack",
    )(where, *pieces)


def join_pieces(pieces, dst_ref):
    for slot, piece in enumerate(pieces):
        dst_ref[:HALF, QUART * slot : QUART * (slot + 1)] = piece[:, :QUART]
        dst_ref[HALF:, QUART * slot : QUART * (slot + 1)] = piece[:, QUART:]


def split_pieces(src_ref, outs):
    half = src_ref.shape[0] // 2
    for slot, out in enumerate(outs):
        out[:, :QUART] = src_ref[:half, QUART * slot : QUART * (slot + 1)]
        out[:, QUART:] = src_ref[half:, QUART * slot : QUART * (slot + 1)]


def adapter_pack_kernel(
    pick_ref, qkv_up, proj_dn, fc1_up, fc2_dn, qkv_dn, fc1_dn, proj_up, fc2_up, gain1, gain2,
    s0, s1, s2, s3, row_ref,
):
    heads = qkv_up.shape[2] // (3 * HD)
    for j, send_ref in enumerate((s0, s1, s2, s3)):
        a = pick_ref[j]
        for h in range(heads):
            for t in range(3):
                send_ref[:RANK, QUART * t + HD * h : QUART * t + HD * (h + 1)] = qkv_up[
                    a, :, HD * (3 * h + t) : HD * (3 * h + t + 1)
                ]
        send_ref[:RANK, 3 * QUART :] = proj_dn[a]
        send_ref[RANK : 2 * RANK, :] = fc1_up[a]
        send_ref[2 * RANK :, :] = fc2_dn[a]
    for i, ref in enumerate((qkv_dn, fc1_dn, proj_up, fc2_up)):
        row_ref[:RANK, QUART * i : QUART * (i + 1)] = ref[pick_ref[0]]
    for i, ref in enumerate((gain1, gain2)):
        row_ref[RANK:, QUART * i : QUART * (i + 1)] = jnp.broadcast_to(ref[...], (RANK, QUART))
    row_ref[RANK:, 2 * QUART :] = jnp.zeros((RANK, 2 * QUART), BF)


def adapter_pack(pick, *mats):
    s = lambda *shape: jax.ShapeDtypeStruct(shape, BF)
    return pl.pallas_call(
        adapter_pack_kernel,
        out_shape=(s(3 * RANK, D),) * 4 + (s(2 * RANK, D),),
        in_specs=[sm()] + [vm()] * 10,
        out_specs=[vm()] * 5,
        compiler_params=params(),
        cost_estimate=cost(2),
        name="adapter_pack",
    )(pick, *mats)


def alpha_block(k, j):
    part = k
    if j == 0:
        return [(part, 0, QUART, None)]
    return [
        (part, QUART + HBLK * (j - 1), HBLK, 0),
        (part, QUART + 3 * HBLK + HBLK * (j - 1), HBLK, 1),
    ]


def beta_block(k, j):
    core, cross = k % 2, k // 2
    base = 3 * core
    if j == 0 and not cross:
        return [(base, 0, QUART, None)]
    row = 0 if j == 0 else HBLK + QUART * (j - 1) + HBLK * cross
    return [(base + 1, row, HBLK, 0), (base + 2, row, HBLK, 1)]


def block_dst(start, flag, half):
    if flag is None:
        return start
    offset = half if flag == 0 else 1 - half
    return pl.multiple_of(start + offset * HBLK, 32)


def prep1_kernel(
    where_ref, p0, p1, p2, p3, q0, q1, q2, q3, q4, q5, r0, r1, r2, r3, a0, a1, a2, a3,
    wqkv_ref, wproj_ref, dqkv, uqkv, dproj, uproj, d1, u1, d2, u2, gain1, gain2,
):
    half = where_ref[1]
    for j, a in enumerate((a0, a1, a2, a3)):
        for t in range(3):
            uqkv[:, D * t + QUART * j : D * t + QUART * (j + 1)] = a[:RANK, QUART * t : QUART * (t + 1)]
        dproj[:, QUART * j : QUART * (j + 1)] = a[:RANK, 3 * QUART :]
        u1[:, D * j : D * (j + 1)] = a[RANK : 2 * RANK, :]
        d2[:, D * j : D * (j + 1)] = a[2 * RANK :, :]
    for k, ref in enumerate((r0, r1, r2, r3)):
        for i, dst in enumerate((dqkv, d1, uproj, u2)):
            dst[:, QUART * k : QUART * (k + 1)] = ref[:RANK, QUART * i : QUART * (i + 1)]
        for i, dst in enumerate((gain1, gain2)):
            dst[:, QUART * k : QUART * (k + 1)] = ref[RANK : RANK + 1, QUART * i : QUART * (i + 1)].astype(F32)
    alpha, beta = (p0, p1, p2, p3), (q0, q1, q2, q3, q4, q5)
    for k in range(4):
        for j in range(4):
            for part, row, count, flag in alpha_block(k, j):
                rows = pl.ds(block_dst(QUART * k, flag, half), count)
                for t in range(2):
                    wqkv_ref[rows, D * t + QUART * j : D * t + QUART * (j + 1)] = alpha[part][
                        row : row + count, QUART * t : QUART * (t + 1)
                    ]
            for part, row, count, flag in beta_block(k, j):
                rows = pl.ds(block_dst(QUART * k, flag, half), count)
                wqkv_ref[rows, 2 * D + QUART * j : 2 * D + QUART * (j + 1)] = beta[part][
                    row : row + count, :QUART
                ]
                rows = pl.ds(block_dst(QUART * j, flag, half), count)
                wproj_ref[rows, QUART * k : QUART * (k + 1)] = beta[part][row : row + count, QUART:]
    for k in range(4):
        rows = slice(QUART * k, QUART * (k + 1))
        for t in range(3):
            cols = slice(D * t, D * (t + 1))
            low = tn(dqkv[:, rows], uqkv[:, cols])
            wqkv_ref[rows, cols] = (wqkv_ref[rows, cols].astype(F32) + low).astype(BF)
        low = tn(dproj[:, rows], uproj[...])
        wproj_ref[rows, :] = (wproj_ref[rows, :].astype(F32) + low).astype(BF)


def prep1(where, alpha, beta, rows, cols):
    s = lambda *shape: jax.ShapeDtypeStruct(shape, BF)
    return pl.pallas_call(
        prep1_kernel,
        out_shape=(
            s(D, 3 * D), s(D, D), s(RANK, D), s(RANK, 3 * D), s(RANK, D), s(RANK, D),
            s(RANK, D), s(RANK, 4 * D), s(RANK, 4 * D), s(RANK, D),
            jax.ShapeDtypeStruct((1, D), F32), jax.ShapeDtypeStruct((1, D), F32),
        ),
        in_specs=[sm()] + [vm()] * 18,
        out_specs=[vm()] * 12,
        compiler_params=params(),
        cost_estimate=cost(7),
        name="attention_weights",
    )(where, *alpha, *beta, *rows, *cols)


def normalize(values):
    center = jnp.sum(values, axis=1, keepdims=True) / D
    shifted = values - center
    inv_std = lax.rsqrt(jnp.sum(shifted * shifted, axis=1, keepdims=True) / D + EPSILON)
    return shifted * inv_std, inv_std


def norm_back(grad, normed, inv_std):
    first = jnp.sum(grad, axis=1, keepdims=True) / D
    second = jnp.sum(grad * normed, axis=1, keepdims=True) / D
    return inv_std * (grad - first - normed * second)


def barrel(values, amount, left):
    for bit in (1, 2, 4, 8):
        moved = pltpu.roll(values, (128 - bit) if left else bit, 1)
        values = jnp.where((amount & bit) != 0, moved, values)
    return values


def low_half(count):
    return lax.broadcasted_iota(jnp.int32, (count, 128), 1) < HD


def pad_rows(tile):
    if tile.shape[0] == KEYS:
        return tile
    return jnp.concatenate([tile, jnp.zeros((KEYS - tile.shape[0], tile.shape[1]), tile.dtype)], axis=0)


def live_rows():
    return lax.broadcasted_iota(jnp.int32, (KEYS, 128), 0) < SLOTS


GROUP = 6
GROUP_BACK = 6


def pair_columns(pair):
    return tuple(slice(D * t + 128 * pair, D * t + 128 * (pair + 1)) for t in range(3))


def attend_window(kind, row0, qkv_ref, att_ref, exp_ref, inv_ref, rel_ref, shift_ref, keys_ref):
    count = NQ[kind]
    rows = pl.ds(row0, count)
    low_q, low_k = low_half(count), low_half(KEYS)
    live = live_rows()
    ones = jnp.where(live, 1.0, 0.0).astype(BF)
    amount = shift_ref[kind, :count, :]
    onehot = keys_ref[kind]
    rel_mat = rel_ref[...]
    for first in range(0, D // 128, GROUP):
        pairs = range(first, first + GROUP)
        heads = [(pair, odd) for pair in pairs for odd in range(2)]
        q_tile = {p: qkv_ref[rows, pair_columns(p)[0]] for p in pairs}
        rel = {p: nn(q_tile[p], rel_mat) for p in pairs}
        rel = {p: barrel(rel[p], amount, True).astype(BF) for p in pairs}
        k_tile = {p: pad_rows(qkv_ref[rows, pair_columns(p)[1]] * BF(HD**-0.5)) for p in pairs}
        scores = {}
        for p, odd in heads:
            if odd:
                q_aug, k_aug = jnp.where(low_q, rel[p], q_tile[p]), jnp.where(low_k, onehot, k_tile[p])
            else:
                q_aug, k_aug = jnp.where(low_q, q_tile[p], rel[p]), jnp.where(low_k, k_tile[p], onehot)
            scores[p, odd] = nt(q_aug, k_aug)
        top = {h: jnp.max(scores[h], axis=1, keepdims=True) for h in heads}
        exponent = {h: jnp.exp(scores[h] - top[h]).astype(BF) for h in heads}
        both = {}
        for p, odd in heads:
            exp_ref[2 * p + odd, rows, :] = exponent[p, odd]
            v_tile = pad_rows(qkv_ref[rows, pair_columns(p)[2]])
            if kind == FULL:
                v_tile = jnp.where(live, v_tile, 0).astype(BF)
            v_aug = jnp.where(low_k, ones, v_tile) if odd else jnp.where(low_k, v_tile, ones)
            both[p, odd] = nn(exponent[p, odd], v_aug)
        for p in pairs:
            cols = pair_columns(p)[0]
            inverse = 1.0 / pltpu.roll(jnp.where(low_q, both[p, 1], both[p, 0]), HD, 1)
            inv_ref[rows, cols] = inverse
            att_ref[rows, cols] = (jnp.where(low_q, both[p, 0], both[p, 1]) * inverse).astype(BF)


PARTS = ((FULL, FULL), (FULL, FULL), (RIGHT, BOTTOM, CORNER))
PART_ROWS = tuple(sum(NQ[kind] for kind in part) for part in PARTS)
PART_OFFS = (0, PART_ROWS[0], PART_ROWS[0] + PART_ROWS[1])


TAIL = ((0, 576), (576, ROWS))


def qkv_kernel(x0, x1, x2, x3, gain_ref, wqkv_ref, x_ref, hid_ref, qkv_a, qkv_b, qkv_c):
    join_pieces((x0, x1, x2, x3), x_ref)
    gain = gain_ref[...]

    def norm_step(i, carry):
        rows = pl.ds(pl.multiple_of(i * 112, 16), 112)
        normed, _ = normalize(x_ref[rows, :].astype(F32))
        hid_ref[rows, :] = (normed * gain).astype(BF)
        return carry

    lax.fori_loop(0, ROWS // 112, norm_step, 0)
    for ref, offset, count in zip((qkv_a, qkv_b, qkv_c), PART_OFFS, PART_ROWS):
        hid = hid_ref[offset : offset + count, :]
        for t in range(3):
            cols = slice(D * t, D * (t + 1))
            ref[:, cols] = nn(hid, wqkv_ref[:, cols]).astype(BF)
    for w in range(4):
        hid_ref[FULLR * w + SLOTS : FULLR * (w + 1), :] = jnp.zeros((FULLR - SLOTS, D), BF)


def qkv_rows(pieces, gain, wqkv):
    s = lambda *shape: jax.ShapeDtypeStruct(shape, BF)
    return pl.pallas_call(
        qkv_kernel,
        out_shape=(s(ROWS, D), s(ROWS, D)) + tuple(s(n, 3 * D) for n in PART_ROWS),
        in_specs=[vm()] * 6,
        out_specs=[vm()] * 5,
        compiler_params=params(),
        cost_estimate=cost(12),
        name="norm_and_qkv",
    )(*pieces, gain, wqkv)


def attention_kernel(qkv_ref, rel_ref, shift_ref, keys_ref, att_ref, exp_ref, inv_ref, *, kinds):
    refs = (qkv_ref, att_ref, exp_ref, inv_ref, rel_ref, shift_ref, keys_ref)
    if kinds[0] == FULL:

        def step(w, carry):
            attend_window(FULL, pl.multiple_of(w * FULLR, 16), *refs)
            return carry

        lax.fori_loop(0, len(kinds), step, 0)
    else:
        row = 0
        for kind in kinds:
            attend_window(kind, row, *refs)
            row += NQ[kind]


def attention(part, qkv, rel, shift, keys):
    rows = PART_ROWS[part]
    s = lambda *shape, dtype=BF: jax.ShapeDtypeStruct(shape, dtype)
    return pl.pallas_call(
        functools.partial(attention_kernel, kinds=PARTS[part]),
        out_shape=(s(rows, D), s(D // HD, rows, KEYS), s(rows, D, dtype=F32)),
        in_specs=[vm()] * 4,
        out_specs=[vm()] * 3,
        compiler_params=params(),
        cost_estimate=cost(10),
        name="attention_forward",
    )(qkv, rel, shift, keys)


def project_kernel(x_ref, att_a, att_b, att_c, wproj_ref, middle_ref):
    for ref, offset, count in zip((att_a, att_b, att_c), PART_OFFS, PART_ROWS):
        rows = slice(offset, offset + count)
        middle_ref[rows, :] = x_ref[rows, :].astype(F32) + nn(ref[...], wproj_ref[...])


def project(x, atts, wproj):
    return pl.pallas_call(
        project_kernel,
        out_shape=jax.ShapeDtypeStruct((ROWS, D), F32),
        in_specs=[vm()] * 5,
        out_specs=vm(),
        compiler_params=params(),
        cost_estimate=cost(5),
        name="projection",
    )(x, *atts, wproj)


CHUNK = 512
LOCK = 2


def mlp_kernel(
    where_ref, middle_ref, g0, g1, g2, g3, gain_ref,
    p0, p1, p2, p3, q0, q1, q2, q3, q4, q5, s0, s1, s2, s3, s4, s5, d1, u1, d2, u2,
    o0, o1, o2, o3, gmid_ref, down1, up1, down2, up2,
    gm_ref, out_rows, h2_ref, acc_mlp, acc_gh, gu1, ad2, w1_ref, w2_ref, sem,
):
    half = where_ref[1]
    copies = []

    def fetch(src, dst):
        copies.append(pltpu.make_async_copy(src, dst, sem.at[len(copies)]))
        copies[-1].start()

    alpha = (p0, p1, p2, p3)
    betas = ((q0, q1, q2, q3, q4, q5), (s0, s1, s2, s3, s4, s5))
    for k in range(4):
        for j in range(4):
            for part, row, count, flag in alpha_block(k, j):
                rows = pl.ds(block_dst(QUART * k, flag, half), count)
                fetch(alpha[part].at[row : row + count, :], w1_ref.at[rows, D * j : D * (j + 1)])
            for part, row, count, flag in beta_block(k, j):
                rows = pl.ds(block_dst(QUART * k, flag, half), count)
                for i, beta in enumerate(betas):
                    cols = slice(D * j + D // 2 * i, D * j + D // 2 * (i + 1))
                    fetch(beta[part].at[row : row + count, :], w2_ref.at[rows, cols])
    join_pieces((g0, g1, g2, g3), gm_ref)
    for copy in copies:
        copy.wait()
    for k in range(4):
        rows = slice(QUART * k, QUART * (k + 1))
        for j in range(4):
            cols = slice(D * j, D * (j + 1))
            low = tn(d1[:, rows], u1[:, cols])
            w1_ref[rows, cols] = (w1_ref[rows, cols].astype(F32) + low).astype(BF)
            low = tn(u2[:, rows], d2[:, cols])
            w2_ref[rows, cols] = (w2_ref[rows, cols].astype(F32) + low).astype(BF)
    gain = gain_ref[...]
    down1[...] = jnp.zeros_like(down1)
    up1[...] = jnp.zeros_like(up1)
    down2[...] = jnp.zeros_like(down2)
    up2[...] = jnp.zeros_like(up2)

    def tile_step(t, carry):
        rows = pl.ds(pl.multiple_of(t * HALF, 16), HALF)
        normed, _ = normalize(middle_ref[rows, :])
        h2 = (normed * gain).astype(BF)
        h2_ref[...] = h2
        gm = gm_ref[rows, :]
        ad1 = nt(d1[...], h2).astype(BF)
        gu2 = nt(u2[...], gm).astype(BF)
        acc_mlp[...] = jnp.zeros_like(acc_mlp)
        acc_gh[...] = jnp.zeros_like(acc_gh)
        gu1[...] = jnp.zeros_like(gu1)
        ad2[...] = jnp.zeros_like(ad2)

        def chunk_step(c, inner_carry):
            spans = [
                pl.ds(pl.multiple_of((c * LOCK + i) * CHUNK, CHUNK), CHUNK) for i in range(LOCK)
            ]
            h2 = h2_ref[...]
            gm = gm_ref[rows, :]
            inner = [nn(h2, w1_ref[:, span]) for span in spans]
            gact = [nn(gm, w2_ref[:, span]) for span in spans]
            act, ginner = [], []
            for i in range(LOCK):
                half = 0.5 * (1.0 + lax.erf(inner[i] * 2**-0.5))
                act.append((inner[i] * half).astype(BF))
                slope = half + inner[i] * (jnp.exp(-0.5 * inner[i] * inner[i]) * (2 * np.pi) ** -0.5)
                ginner.append((gact[i] * slope).astype(BF))
            for i, span in enumerate(spans):
                acc_mlp[...] += nt(act[i], w2_ref[:, span])
                acc_gh[...] += nt(ginner[i], w1_ref[:, span])
                up1[:, span] += nn(ad1, ginner[i])
                gu1[...] += nt(u1[:, span], ginner[i])
                ad2[...] += nt(d2[:, span], act[i])
                down2[:, span] += nn(gu2, act[i])
            return inner_carry

        lax.fori_loop(0, 4 * D // (CHUNK * LOCK), chunk_step, 0)
        down1[...] += nn(gu1[...].astype(BF), h2_ref[...])
        up2[...] += nn(ad2[...].astype(BF), gm_ref[rows, :])
        middle = middle_ref[rows, :]
        out_rows[rows, :] = (middle + acc_mlp[...]).astype(BF)
        normed, inv_std = normalize(middle)
        gmid_ref[rows, :] = gm_ref[rows, :].astype(F32) + norm_back(acc_gh[...] * gain, normed, inv_std)
        return carry

    lax.fori_loop(0, 2, tile_step, 0)
    split_pieces(out_rows, (o0, o1, o2, o3))


def mlp(where, middle, pieces, gain, alpha, betas, d1, u1, d2, u2):
    s = lambda *shape, dtype=F32: jax.ShapeDtypeStruct(shape, dtype)
    return pl.pallas_call(
        mlp_kernel,
        out_shape=(PIECE,) * 4
        + (s(ROWS, D), s(RANK, D), s(RANK, 4 * D), s(RANK, 4 * D), s(RANK, D)),
        in_specs=[sm()] + [vm()] * 6 + [pl.BlockSpec(memory_space=pl.ANY)] * 16 + [vm()] * 4,
        out_specs=[vm()] * 9,
        scratch_shapes=[
            pltpu.VMEM((ROWS, D), BF), pltpu.VMEM((ROWS, D), BF), pltpu.VMEM((HALF, D), BF),
            pltpu.VMEM((HALF, D), F32), pltpu.VMEM((HALF, D), F32),
            pltpu.VMEM((RANK, HALF), F32), pltpu.VMEM((RANK, HALF), F32),
            pltpu.VMEM((D, 4 * D), BF), pltpu.VMEM((D, 4 * D), BF),
            pltpu.SemaphoreType.DMA((4 * 4 * 6,)),
        ],
        compiler_params=params(),
        cost_estimate=cost(48),
        name="mlp_forward_backward",
    )(where, middle, *pieces, gain, *alpha, *betas[0], *betas[1], d1, u1, d2, u2)


def attend_back_window(
    kind, row0, qkv_ref, att_ref, exp_ref, inv_ref, gatt_ref, gqkv_ref, rel_ref, shift_ref, keys_ref
):
    count = NQ[kind]
    rows = pl.ds(row0, count)
    low_q, low_k = low_half(count), low_half(KEYS)
    live = live_rows()
    lane_k = lax.broadcasted_iota(jnp.int32, (KEYS, 128), 1) % HD
    lane_q = lax.broadcasted_iota(jnp.int32, (count, 128), 1) % HD
    ones = jnp.where(live & (lane_k < 2), 1.0, 0.0).astype(BF)
    across = jnp.where(
        low_half(128) != (lax.broadcasted_iota(jnp.int32, (128, 128), 0) < HD), -1.0, 0.0
    ).astype(BF)
    amount = shift_ref[kind, :count, :]
    onehot = keys_ref[kind]
    rel_mat = rel_ref[...]
    for first in range(0, D // 128, GROUP_BACK):
        pairs = range(first, first + GROUP_BACK)
        heads = [(pair, odd) for pair in pairs for odd in range(2)]
        go_tile = {
            p: (gatt_ref[rows, pair_columns(p)[0]].astype(F32) * inv_ref[rows, pair_columns(p)[0]]).astype(BF)
            for p in pairs
        }
        delta = {
            p: nn((go_tile[p].astype(F32) * att_ref[rows, pair_columns(p)[0]].astype(F32)).astype(BF), across)
            for p in pairs
        }
        go_t = {p: go_tile[p].T for p in pairs}
        gv = {}
        for p, odd in heads:
            gv[p, odd] = nn(go_t[p][HD * odd : HD * (odd + 1), :], exp_ref[2 * p + odd, rows, :])
        gscore = {}
        for p in pairs:
            high = delta[p].astype(BF)
            rest = (delta[p] - high.astype(F32)).astype(BF)
            low_delta = jnp.where(lane_q == 0, high, jnp.where(lane_q == 1, rest, 0)).astype(BF)
            v_tile = pad_rows(qkv_ref[rows, pair_columns(p)[2]])
            if kind == FULL:
                v_tile = jnp.where(live, v_tile, 0).astype(BF)
            gscore[p, 0] = nt(jnp.where(low_q, go_tile[p], low_delta), jnp.where(low_k, v_tile, ones))
            gscore[p, 1] = nt(jnp.where(low_q, low_delta, go_tile[p]), jnp.where(low_k, ones, v_tile))
        q_t = {p: qkv_ref[rows, pair_columns(p)[0]].T for p in pairs}
        gs = {(p, odd): (exp_ref[2 * p + odd, rows, :].astype(F32) * gscore[p, odd]).astype(BF) for p, odd in heads}
        gk = {(p, odd): nn(q_t[p][HD * odd : HD * (odd + 1), :], gs[p, odd]) for p, odd in heads}
        gq = {}
        for p in pairs:
            k_tile = pad_rows(qkv_ref[rows, pair_columns(p)[1]] * BF(HD**-0.5))
            gq[p, 0] = nn(gs[p, 0], jnp.where(low_k, k_tile, onehot))
            gq[p, 1] = nn(gs[p, 1], jnp.where(low_k, onehot, k_tile))
        sums = {p: barrel(jnp.where(low_q, gq[p, 1], gq[p, 0]), amount, False).astype(BF) for p in pairs}
        for p in pairs:
            cols, kcols, vcols = pair_columns(p)
            gv_tile = jnp.concatenate([gv[p, 0], gv[p, 1]], axis=0).astype(BF).T
            gqkv_ref[rows, vcols] = gv_tile[:count, :]
            gk_tile = (jnp.concatenate([gk[p, 0], gk[p, 1]], axis=0) * HD**-0.5).astype(BF).T
            gqkv_ref[rows, kcols] = gk_tile[:count, :]
            gqkv_ref[rows, cols] = (jnp.where(low_q, gq[p, 0], gq[p, 1]) + nt(sums[p], rel_mat)).astype(BF)


def attention_back_kernel(
    gmid_ref, hid_ref, qkv_a, qkv_b, qkv_c, att_a, att_b, att_c, exp_a, exp_b, exp_c, inv_a, inv_b, inv_c,
    wproj_ref, rel_ref, shift_ref, keys_ref, dqkv, uqkv, dproj, uproj,
    gqkv_ref, down_q, up_q, down_p, up_p, gb_ref, gatt_ref, att_ref,
):
    gb_ref[...] = gmid_ref[...].astype(BF)
    gatt_ref[...] = nt(gb_ref[...], wproj_ref[...]).astype(BF)
    for ref, offset, count in zip((att_a, att_b, att_c), PART_OFFS, PART_ROWS):
        att_ref[offset : offset + count, :] = ref[...]
    up_p[...] = nn(nt(dproj[...], att_ref[...]).astype(BF), gb_ref[...])
    down_p[...] = nn(nt(uproj[...], gb_ref[...]).astype(BF), att_ref[...])
    tables = (rel_ref, shift_ref, keys_ref)
    for part, parts in enumerate(
        ((qkv_a, att_a, exp_a, inv_a), (qkv_b, att_b, exp_b, inv_b), (qkv_c, att_c, exp_c, inv_c))
    ):
        span = pl.ds(PART_OFFS[part], PART_ROWS[part])
        refs = parts + (gatt_ref.at[span, :], gqkv_ref.at[span, :]) + tables
        if PARTS[part][0] == FULL:

            def step(w, carry, refs=refs):
                attend_back_window(FULL, pl.multiple_of(w * FULLR, 16), *refs)
                return carry

            lax.fori_loop(0, len(PARTS[part]), step, 0)
        else:
            row = 0
            for kind in PARTS[part]:
                attend_back_window(kind, row, *refs)
                row += NQ[kind]
    up_q[...] = nn(nt(dqkv[...], hid_ref[...]).astype(BF), gqkv_ref[...])
    down_q[...] = nn(nt(uqkv[...], gqkv_ref[...]).astype(BF), hid_ref[...])


def attention_back(gmid, hid, qkvs, atts, exps, invs, wproj, rel, shift, keys, dqkv, uqkv, dproj, uproj):
    s = lambda *shape, dtype=F32: jax.ShapeDtypeStruct(shape, dtype)
    return pl.pallas_call(
        attention_back_kernel,
        out_shape=(s(ROWS, 3 * D, dtype=BF), s(RANK, D), s(RANK, 3 * D), s(RANK, D), s(RANK, D)),
        in_specs=[vm()] * 22,
        out_specs=[vm()] * 5,
        scratch_shapes=[pltpu.VMEM((ROWS, D), BF)] * 3,
        compiler_params=params(),
        cost_estimate=cost(45),
        name="attention_backward",
    )(gmid, hid, *qkvs, *atts, *exps, *invs, wproj, rel, shift, keys, dqkv, uqkv, dproj, uproj)


def token_grad_kernel(gmid_hbm, x_hbm, gqkv_hbm, gain_ref, wqkv_ref, o0, o1, o2, o3,
                      gmid_ref, x_ref, gqkv_ref, gh_ref, out_rows, sem, *, low, high):
    span = pl.ds(low, high - low)
    copies = [
        pltpu.make_async_copy(src.at[span, :], dst, sem.at[i])
        for i, (src, dst) in enumerate(((gqkv_hbm, gqkv_ref), (x_hbm, x_ref), (gmid_hbm, gmid_ref)))
    ]
    for copy in copies:
        copy.start()
    copies[0].wait()
    gh_ref[...] = nt(gqkv_ref[...], wqkv_ref[...])
    copies[1].wait()
    copies[2].wait()
    gain = gain_ref[...]
    step = (high - low) // 2

    def norm_step(i, carry):
        rows = pl.ds(pl.multiple_of(i * step, 16), step)
        normed, inv_std = normalize(x_ref[rows, :].astype(F32))
        back = norm_back(gh_ref[rows, :] * gain, normed, inv_std)
        out_rows[rows, :] = (gmid_ref[rows, :] + back).astype(BF)
        return carry

    lax.fori_loop(0, 2, norm_step, 0)
    split_pieces(out_rows, (o0, o1, o2, o3))


def token_grad(gmid, x, gqkv, gain, wqkv, low, high):
    count = high - low
    hbm = pl.BlockSpec(memory_space=pl.ANY)
    return pl.pallas_call(
        functools.partial(token_grad_kernel, low=low, high=high),
        out_shape=(jax.ShapeDtypeStruct((count // 2, 2 * QUART), BF),) * 4,
        in_specs=[hbm, hbm, hbm, vm(), vm()],
        out_specs=[vm()] * 4,
        scratch_shapes=[
            pltpu.VMEM((count, D), F32), pltpu.VMEM((count, D), BF), pltpu.VMEM((count, 3 * D), BF),
            pltpu.VMEM((count, D), F32), pltpu.VMEM((count, D), BF), pltpu.SemaphoreType.DMA((3,)),
        ],
        compiler_params=params(),
        cost_estimate=cost(8),
        name="token_gradient",
    )(gmid, x, gqkv, gain, wqkv)


def grad_pack_kernel(where_ref, down_q, up_q, down_p, up_p, down1, up1, down2, up2, o0, o1, o2, o3, buf_ref):
    mine = where_ref[0]
    for k in range(4):
        for i, ref in enumerate((down_q, down1, up_p, up2)):
            buf_ref[k, :RANK, QUART * i : QUART * (i + 1)] = ref[:, QUART * k : QUART * (k + 1)]
    for dest in range(4):
        k = jnp.bitwise_xor(mine, dest)
        ranks = slice(RANK // 4 * dest, RANK // 4 * (dest + 1))
        for j in range(4):
            base = RANK + 12 * j
            for t in range(3):
                buf_ref[k, base : base + 4, QUART * t : QUART * (t + 1)] = up_q[
                    ranks, D * t + QUART * j : D * t + QUART * (j + 1)
                ]
            buf_ref[k, base : base + 4, 3 * QUART :] = down_p[ranks, QUART * j : QUART * (j + 1)]
            buf_ref[k, base + 4 : base + 8, :] = up1[ranks, D * j : D * (j + 1)]
            buf_ref[k, base + 8 : base + 12, :] = down2[ranks, D * j : D * (j + 1)]
    for k, out in enumerate((o0, o1, o2, o3)):
        out[...] = buf_ref[k].astype(BF)


def grad_pack(where, *grads):
    return pl.pallas_call(
        grad_pack_kernel,
        out_shape=(jax.ShapeDtypeStruct((4 * RANK, D), BF),) * 4,
        in_specs=[sm()] + [vm()] * 8,
        out_specs=[vm()] * 4,
        scratch_shapes=[pltpu.VMEM((4, 4 * RANK, D), F32)],
        compiler_params=params(),
        cost_estimate=cost(2),
        name="adapter_grad_pack",
    )(where, *grads)


def grad_sum_kernel(g0, g1, g2, g3, o0, o1, o2, o3, buf_ref):
    total = g0[...].astype(F32) + g1[...].astype(F32) + g2[...].astype(F32) + g3[...].astype(F32)
    buf_ref[...] = jnp.zeros_like(buf_ref)
    buf_ref[:RANK, :] = total[:RANK, :]
    for j, out in enumerate((o0, o1, o2, o3)):
        buf_ref[RANK : RANK + 12, :] = total[RANK + 12 * j : RANK + 12 * (j + 1), :]
        out[...] = buf_ref[...].astype(BF)


def grad_sum(pieces):
    return pl.pallas_call(
        grad_sum_kernel,
        out_shape=(jax.ShapeDtypeStruct((2 * RANK, D), BF),) * 4,
        in_specs=[vm()] * 4,
        out_specs=[vm()] * 4,
        scratch_shapes=[pltpu.VMEM((2 * RANK, D), F32)],
        compiler_params=params(),
        cost_estimate=cost(2),
        name="adapter_grad_sum",
    )(*pieces)


def grad_adapters_kernel(index_ref, x_ref, qkv_dn, fc1_dn, proj_up, fc2_up, rest_ref, acc_ref):
    acc_ref[...] = jnp.zeros_like(acc_ref)

    def add(i, carry):
        acc_ref[index_ref[i]] += x_ref[i].astype(F32)
        return carry

    lax.fori_loop(0, x_ref.shape[0], add, 0)
    for i, ref in enumerate((qkv_dn, fc1_dn, proj_up, fc2_up)):
        ref[...] = acc_ref[:, :RANK, QUART * i : QUART * (i + 1)]
    rest_ref[...] = acc_ref[:, RANK:, :].astype(BF)


def grad_adapters(index, x):
    s = lambda n, dtype=F32: jax.ShapeDtypeStruct((ADAPT, RANK, n), dtype)
    return pl.pallas_call(
        grad_adapters_kernel,
        out_shape=(s(QUART), s(QUART), s(QUART), s(QUART), s(D, BF)),
        in_specs=[sm(), vm()],
        out_specs=[vm()] * 5,
        scratch_shapes=[pltpu.VMEM((ADAPT, 2 * RANK, D), F32)],
        compiler_params=params(),
        cost_estimate=cost(2),
        name="adapter_grad_by_adapter",
    )(index, x)


def grad_join_kernel(where_ref, r0, r1, r2, r3, qkv_up, proj_dn, fc1_up, fc2_dn, buf_ref):
    mine = where_ref[0]
    heads = qkv_up.shape[2] // (3 * HD)
    for k, ref in enumerate((r0, r1, r2, r3)):
        buf_ref[jnp.bitwise_xor(mine, k)] = ref[...].astype(F32)
    for source in range(4):
        ranks = slice(RANK // 4 * source, RANK // 4 * (source + 1))
        for h in range(heads):
            for t in range(3):
                qkv_up[:, ranks, HD * (3 * h + t) : HD * (3 * h + t + 1)] = buf_ref[
                    source, :, 0:4, QUART * t + HD * h : QUART * t + HD * (h + 1)
                ]
        proj_dn[:, ranks, :] = buf_ref[source, :, 0:4, 3 * QUART :]
        fc1_up[:, ranks, :] = buf_ref[source, :, 4:8, :]
        fc2_dn[:, ranks, :] = buf_ref[source, :, 8:12, :]


def grad_join(where, pieces):
    s = lambda n: jax.ShapeDtypeStruct((ADAPT, RANK, n), F32)
    return pl.pallas_call(
        grad_join_kernel,
        out_shape=(s(3 * QUART), s(QUART), s(D), s(D)),
        in_specs=[sm()] + [vm()] * 4,
        out_specs=[vm()] * 4,
        scratch_shapes=[pltpu.VMEM((4, ADAPT, RANK, D), F32)],
        compiler_params=params(),
        cost_estimate=cost(2),
        name="adapter_grad_join",
    )(where, *pieces)


def flip(values, axis, distance):
    size = lax.axis_size(axis)
    return lax.ppermute(values, axis, [(i, i ^ distance) for i in range(size)])


def exchange(slots, axis):
    return [slots[0]] + [flip(slots[k], axis, k) for k in range(1, 4)]


def after(values, *deps):
    return lax.optimization_barrier((tuple(values), deps))[0]


def col_halves(half):
    return jnp.concatenate([flip(half, "col", j) for j in range(1, 4)], axis=0)


def col_pairs(half, other_row):
    two = jnp.concatenate([half, other_row], axis=0)
    return jnp.concatenate([other_row] + [flip(two, "col", j) for j in range(1, 4)], axis=0)


def rel_matrix(rel_h, rel_w):
    pad = jnp.zeros((32 - (2 * WIN - 1), HD), BF)
    block = jnp.concatenate([rel_h[::-1], pad, rel_w[::-1], pad], axis=0).T
    zero = jnp.zeros((HD, HD), BF)
    return jnp.concatenate(
        [jnp.concatenate([zero, block], axis=1), jnp.concatenate([block, zero], axis=1)], axis=0
    )


def body(
    tokens, grad_out, adapter_index, norm1_gain, norm2_gain, qkv_weight, proj_weight, fc1_weight, fc2_weight,
    rel_h, rel_w, qkv_down, qkv_up, proj_down, proj_up, fc1_down, fc1_up, fc2_down, fc2_up,
):
    members = lax.axis_size("col")
    batches = lax.axis_size("dp")
    row_index, col_index, dp_index = lax.axis_index("row"), lax.axis_index("col"), lax.axis_index("dp")
    half = dp_index % 2
    where = jnp.stack([row_index, half]).astype(jnp.int32)
    slot_images = (
        jnp.bitwise_xor(dp_index, jnp.arange(batches, dtype=jnp.int32))[:, None] * members
        + jnp.bitwise_xor(col_index, jnp.arange(members, dtype=jnp.int32))[None, :]
    ).reshape(-1)
    slot_adapters = jnp.sum(
        jnp.where(
            slot_images[:, None] == jnp.arange(adapter_index.shape[0], dtype=jnp.int32)[None, :],
            adapter_index[:, 0][None, :],
            0,
        ),
        axis=1,
    )
    pick = jnp.concatenate([slot_adapters[:4], half[None]]).astype(jnp.int32)
    swap = lambda m: jnp.swapaxes(m, 1, 2)

    rel = rel_matrix(rel_h, rel_w)
    shift, keys = jnp.asarray(SHIFT_NP), jnp.asarray(KEYS_NP)

    *token_slots, alpha_own, beta_own, alpha_half, beta_half = front(where, tokens, qkv_weight, proj_weight)
    b0 = flip(beta_half, "row", 2)
    alpha_near = col_halves(alpha_half)
    x_pieces = exchange(token_slots, "row")
    beta_near = col_pairs(beta_half, b0)
    alpha_far = flip(alpha_near, "dp", 1)
    g = jnp.concatenate([alpha_own, alpha_near, alpha_far], axis=0)
    g, *x_pieces = after((g, *x_pieces), beta_near)
    gy = flip(g, "row", 2)
    beta_far = flip(beta_near, "dp", 1)

    *send, row_adapters = adapter_pack(
        pick, qkv_up, swap(proj_down), fc1_up, swap(fc2_down), swap(qkv_down), swap(fc1_down), proj_up, fc2_up,
        norm1_gain.reshape(1, -1), norm2_gain.reshape(1, -1),
    )
    *send, row_adapters = after((*send, row_adapters), alpha_near)
    col_adapters = exchange(send, "col")
    row_adapters = exchange([row_adapters] * 4, "row")

    cut = lambda m: lax.dynamic_slice_in_dim(m, half * HBLK, HBLK, 0)
    fc2_cols = [fc2_weight[:, : D // 2], fc2_weight[:, D // 2 :]]
    fc1_half, fc2_half = after((cut(fc1_weight), cut(fc2_weight)), beta_near)
    c0 = flip(fc2_half, "row", 2)
    fc1_near = [flip(fc1_half, "col", j) for j in range(1, 4)]
    grad_slots = pack(where, grad_out)

    alpha1 = [g, flip(g, "row", 1), gy, flip(gy, "row", 1)]
    beta1 = [beta_own, beta_near, beta_far] + [flip(m, "row", 1) for m in (beta_own, beta_near, beta_far)]
    grad_slots = after(tuple(grad_slots), gy)
    g_pieces = exchange(grad_slots, "row")
    *alpha1, c0 = after((*alpha1, c0))
    two = jnp.concatenate([fc2_half, c0], axis=0)
    fc2_near = [[flip(two[:, D // 2 * i : D // 2 * (i + 1)], "col", j) for j in range(1, 4)] for i in range(2)]
    wqkv, wproj, dqkv, uqkv, dproj, uproj, d1, u1, d2, u2, gain1, gain2 = prep1(
        where, alpha1, beta1, row_adapters, col_adapters
    )
    wqkv, *fc1_near = after((wqkv, *fc1_near))
    fc1_near = jnp.concatenate(fc1_near, axis=0)
    fc1_far = flip(fc1_near, "dp", 1)
    x, hid, *qkvs = qkv_rows(x_pieces, gain1, wqkv)
    *qkvs, fc1_far, n1, n2, n3 = after((*qkvs, fc1_far, *fc2_near[0]), *g_pieces)
    h = jnp.concatenate([fc1_weight, fc1_near, fc1_far], axis=0)
    hy = flip(h, "row", 2)
    fc2_near0 = jnp.concatenate([c0[:, : D // 2], n1, n2, n3], axis=0)
    fc2_far0 = flip(fc2_near0, "dp", 1)
    part0 = attention(0, qkvs[0], rel, shift, keys)
    qkv1, n1, n2, n3 = after((qkvs[1], *fc2_near[1]), part0[0])
    fc2_near1 = jnp.concatenate([c0[:, D // 2 :], n1, n2, n3], axis=0)
    fc2_near1, fc2_far0 = after((fc2_near1, fc2_far0))
    fc2_far1 = flip(fc2_near1, "dp", 1)
    part1 = attention(1, qkv1, rel, shift, keys)
    qkv2, _ = after((qkvs[2], fc2_far0), part1[0])
    part2 = attention(2, qkv2, rel, shift, keys)
    atts, exps, invs = zip(part0, part1, part2)
    atts = list(atts)
    atts[2], hy = after((atts[2], hy))
    alpha2 = [h, flip(h, "row", 1), hy, flip(hy, "row", 1)]
    middle = project(x, atts, wproj)
    middle, fc2_far1 = after((middle, fc2_far1))
    betas = [
        [own, near, far] + [flip(m, "row", 1) for m in (own, near, far)]
        for own, near, far in zip(fc2_cols, (fc2_near0, fc2_near1), (fc2_far0, fc2_far1))
    ]

    *out_slots, gmid, down1, up1, down2, up2 = mlp(where, middle, g_pieces, gain2, alpha2, betas, d1, u1, d2, u2)
    out_pieces = exchange(out_slots, "row")
    gqkv, down_q, up_q, down_p, up_p = attention_back(
        gmid, hid, qkvs, atts, exps, invs, wproj, rel, shift, keys, dqkv, uqkv, dproj, uproj
    )
    gqkv, down_q, up_q, down_p, up_p = after((gqkv, down_q, up_q, down_p, up_p), *out_pieces)
    packed = grad_pack(where, down_q, up_q, down_p, up_p, down1, up1, down2, up2)
    *packed, gqkv = after((*packed, gqkv))
    row_sums = exchange(packed, "row")
    back0 = token_grad(gmid, x, gqkv, gain1, wqkv, *TAIL[0])
    *row_sums, gqkv = after((*row_sums, gqkv), back0[0])
    back_pieces = exchange(back0, "row")
    back1 = token_grad(gmid, x, gqkv, gain1, wqkv, *TAIL[1])
    *row_sums, = after(tuple(row_sums), back1[0])
    back_pieces += exchange(back1, "row")
    summed = grad_sum(row_sums)
    images = jnp.stack(exchange(summed, "col"))
    step = 1
    while step < batches:
        images = jnp.concatenate([images, flip(images, "dp", step)], axis=0)
        step *= 2
    qkv_dn, fc1_dn, proj_upg, fc2_upg, rest = grad_adapters(slot_adapters.astype(jnp.int32), images)
    rests = [rest] + [flip(rest, "row", k) for k in range(1, 4)]
    qkv_upg, proj_dn, fc1_upg, fc2_dn = grad_join(where, rests)
    *out_pieces, = after(tuple(out_pieces), summed[0])
    result = unpack(where, out_pieces, BF)
    grad_tokens = unpack(where, back_pieces, F32, TAIL)
    return (
        result, grad_tokens,
        swap(qkv_dn), qkv_upg, swap(proj_dn), proj_upg, swap(fc1_dn), fc1_upg, swap(fc2_dn), fc2_upg,
    )


def solution(mesh):
    return jax.shard_map(
        body,
        mesh=mesh,
        in_specs=(
            P("row", ("dp", "col")), P("row", ("dp", "col")), P(), P("row"), P("row"),
            P("row", "col"), P("col", "row"), P("row", "col"), P("row", "col"), P(), P(),
            P(None, "row", None), P(None, None, "col"), P(None, "col", None), P(None, None, "row"),
            P(None, "row", None), P(None, None, "col"), P(None, "col", None), P(None, None, "row"),
        ),
        out_specs=(
            P("row", ("dp", "col")), P("row", ("dp", "col")),
            P(None, "row", None), P(None, None, "col"), P(None, "col", None), P(None, None, "row"),
            P(None, "row", None), P(None, None, "col"), P(None, "col", None), P(None, None, "row"),
        ),
        check_vma=False,
    )
```

```python
import functools

import jax
import jax.numpy as jnp
import numpy as np
from jax import lax
from jax.experimental import pallas as pl
from jax.experimental.pallas import tpu as pltpu
from jax.sharding import PartitionSpec as P

D = 768
HD = 64
WIN = 14
SLOTS = WIN * WIN
SIDE = 64
ADAPT = 8
NWIN = 5
IMG_TOK = NWIN * NWIN * SLOTS
RANK = 16
EDGE = SIDE - (NWIN - 1) * WIN
QUART = D // 4
FULLR = 208
KEYS = 208
EDGER = EDGE * WIN
CORNR = EDGE * EDGE
ROWS = 4 * FULLR + 2 * EDGER + CORNR
HALF = ROWS // 2
HBLK = QUART // 2
EPSILON = 1e-06
BF = jnp.bfloat16
F32 = jnp.float32
VMEM_LIMIT = 60 * 1024 * 1024

FULL, RIGHT, BOTTOM, CORNER = 0, 1, 2, 3
NQ = (FULLR, EDGER, EDGER, CORNR)
OFFS = (0, 4 * FULLR, 4 * FULLR + EDGER, 4 * FULLR + 2 * EDGER)


def slot_order(kind):
    rows = EDGE if kind in (BOTTOM, CORNER) else WIN
    cols = EDGE if kind in (RIGHT, CORNER) else WIN
    kept = [a * WIN + b for a in range(rows) for b in range(cols)]
    rest = [s for s in range(SLOTS) if s not in set(kept)]
    return kept, kept + rest


def build_tables():
    shift = np.zeros((4, FULLR, 128), np.int32)
    keys = np.zeros((4, KEYS, 128), np.float32)
    for kind in range(4):
        kept, order = slot_order(kind)
        for i, s in enumerate(kept):
            for base in (0, 64):
                shift[kind, i, base : base + 32] = WIN - 1 - s // WIN
                shift[kind, i, base + 32 : base + 64] = WIN - 1 - s % WIN
        spare = order[0] if kind == FULL else order[-1]
        for i, s in enumerate(order + [spare] * (KEYS - SLOTS)):
            for base in (0, 64):
                keys[kind, i, base + s // WIN] = 1.0
                keys[kind, i, base + 32 + s % WIN] = 1.0
    return shift, keys.astype(jnp.bfloat16)


SHIFT_NP, KEYS_NP = build_tables()


def nn(a, b):
    return jnp.dot(a, b, preferred_element_type=F32)


def nt(a, b):
    return lax.dot_general(a, b, (((1,), (1,)), ((), ())), preferred_element_type=F32)


def tn(a, b):
    return lax.dot_general(a, b, (((0,), (0,)), ((), ())), preferred_element_type=F32)


def vm():
    return pl.BlockSpec(memory_space=pltpu.VMEM)


def sm():
    return pl.BlockSpec(memory_space=pltpu.SMEM)


def params(**kw):
    return pltpu.CompilerParams(vmem_limit_bytes=VMEM_LIMIT, **kw)


def cost(us):
    return pl.CostEstimate(flops=int(us * 3e8), transcendentals=0, bytes_accessed=0)


def place_window(kind, count, moved, width, spare=-100000):
    row = lax.broadcasted_iota(jnp.int32, (count, width), 0)
    lane = lax.broadcasted_iota(jnp.int32, (count, width), 1)
    if kind in (RIGHT, CORNER):
        src = (row // EDGE) * WIN + row % EDGE
    else:
        src = jnp.where(row < SLOTS, row, spare)
    return (lane == src + moved).astype(F32).astype(BF)


def window_list(dest):
    items = [(FULL, FULLR * j, NWIN * dest + j) for j in range(4)]
    items.append((RIGHT, OFFS[1], NWIN * dest + 4))
    items.append((BOTTOM, OFFS[2], NWIN * 4 + dest))
    if dest == 3:
        items.append((CORNER, OFFS[3], NWIN * NWIN - 1))
    return items


def window_span(window):
    start = window * SLOTS
    low = start // 128 * 128
    high = min(-(-(start + SLOTS) // 128) * 128, IMG_TOK)
    return low, high, start - low


def pack_rows(mine, x_ref, rows_ref, spare):
    for dest in range(4):
        slot = jnp.bitwise_xor(mine, dest)
        if dest != 3:
            rows_ref[slot, OFFS[3] :, :] = jnp.zeros((CORNR, QUART), BF)
        for kind, offset, window in window_list(dest):
            low, high, moved = window_span(window)
            pick = place_window(kind, NQ[kind], moved, high - low, spare)
            rows_ref[slot, offset : offset + NQ[kind], :] = nt(pick, x_ref[:, low:high]).astype(BF)


def fold(rows_ref, outs):
    half = rows_ref.shape[1] // 2
    for slot, (out, base) in enumerate(((outs[0], 0), (outs[1], 0), (outs[2], 0), (outs[2], half))):
        out[base : base + half, :QUART] = rows_ref[slot, :half, :]
        out[base : base + half, QUART:] = rows_ref[slot, half:, :]


def pack_kernel(where_ref, x_ref, o0, o1, o2, rows_ref):
    pack_rows(where_ref[0], x_ref, rows_ref, -100000)
    fold(rows_ref, (o0, o1, o2))


def pieces_of(rows):
    piece = lambda n: jax.ShapeDtypeStruct((n, 2 * QUART), BF)
    return (piece(rows // 2), piece(rows // 2), piece(rows))


def pack(where, x):
    return pl.pallas_call(
        pack_kernel,
        out_shape=pieces_of(ROWS),
        in_specs=[sm(), vm()],
        out_specs=[vm()] * 3,
        scratch_shapes=[pltpu.VMEM((4, ROWS, QUART), BF)],
        compiler_params=params(),
        cost_estimate=cost(4),
        name="pack",
    )(where, x)


def front_kernel(
    where_ref, x_ref, qkv_w, proj_w, o0, o1, o2, alpha_ref, beta_ref, alpha_half, beta_half, rows_ref,
):
    heads = qkv_w.shape[1] // (3 * HD)
    for h in range(heads):
        for t in range(3):
            ref, base = (alpha_ref, QUART * t) if t < 2 else (beta_ref, 0)
            ref[:, base + HD * h : base + HD * (h + 1)] = qkv_w[:, HD * (3 * h + t) : HD * (3 * h + t + 1)]
    beta_ref[:, QUART:] = proj_w[...]
    rows = pl.ds(pl.multiple_of(where_ref[1] * HBLK, 32), HBLK)
    alpha_half[...] = alpha_ref[rows, :]
    beta_half[...] = beta_ref[rows, :]
    pack_rows(where_ref[0], x_ref, rows_ref, 0)
    fold(rows_ref, (o0, o1, o2))


def front(where, x, qkv_w, proj_w):
    s = lambda *shape: jax.ShapeDtypeStruct(shape, BF)
    return pl.pallas_call(
        front_kernel,
        out_shape=pieces_of(ROWS)
        + (s(QUART, 2 * QUART), s(QUART, 2 * QUART), s(HBLK, 2 * QUART), s(HBLK, 2 * QUART)),
        in_specs=[sm(), vm(), vm(), vm()],
        out_specs=[vm()] * 7,
        scratch_shapes=[pltpu.VMEM((4, ROWS, QUART), BF)],
        compiler_params=params(),
        cost_estimate=cost(5),
        name="token_and_weight_pack",
    )(where, x, qkv_w, proj_w)


def unpack_kernel(where_ref, *refs, bounds):
    pieces, (out_ref, acc_ref, rows_ref) = refs[:-3], refs[-3:]
    mine = where_ref[0]
    acc_ref[...] = jnp.zeros_like(acc_ref)
    index = 0
    for low, high in bounds:
        half = (high - low) // 2
        for slot in range(4):
            piece = pieces[index]
            rows = slice(half, 2 * half) if slot == 3 else slice(0, half)
            rows_ref[slot, low : low + half, :] = piece[rows, :QUART]
            rows_ref[slot, low + half : high, :] = piece[rows, QUART:]
            index += 1

    for source in range(4):
        slot = jnp.bitwise_xor(mine, source)
        for kind, offset, window in window_list(source):
            low, high, moved = window_span(window)
            pick = place_window(kind, NQ[kind], moved, high - low)
            acc_ref[:, low:high] += tn(rows_ref[slot, offset : offset + NQ[kind], :], pick)
    out_ref[...] = acc_ref[:, :IMG_TOK].astype(out_ref.dtype)


def unpack(where, pieces, dtype, bounds=((0, ROWS),)):
    return pl.pallas_call(
        functools.partial(unpack_kernel, bounds=bounds),
        out_shape=jax.ShapeDtypeStruct((QUART, IMG_TOK), dtype),
        in_specs=[sm()] + [vm()] * len(pieces),
        out_specs=vm(),
        scratch_shapes=[
            pltpu.VMEM((QUART, -(-IMG_TOK // 128) * 128), F32),
            pltpu.VMEM((4, ROWS, QUART), BF),
        ],
        compiler_params=params(),
        cost_estimate=cost(4),
        name="unpack",
    )(where, *pieces)


def join_pieces(pieces, dst_ref):
    for slot, piece in enumerate(pieces):
        rows = slice(HALF, ROWS) if slot == 3 else slice(0, HALF)
        dst_ref[:HALF, QUART * slot : QUART * (slot + 1)] = piece[rows, :QUART]
        dst_ref[HALF:, QUART * slot : QUART * (slot + 1)] = piece[rows, QUART:]


def split_pieces(src_ref, outs):
    half = src_ref.shape[0] // 2
    for slot, (out, base) in enumerate(((outs[0], 0), (outs[1], 0), (outs[2], 0), (outs[2], half))):
        out[base : base + half, :QUART] = src_ref[:half, QUART * slot : QUART * (slot + 1)]
        out[base : base + half, QUART:] = src_ref[half:, QUART * slot : QUART * (slot + 1)]


def adapter_pack_kernel(
    pick_ref, qkv_up, proj_dn, fc1_up, fc2_dn, qkv_dn, fc1_dn, proj_up, fc2_up, gain1, gain2,
    s0, s1, s2, s3, row_ref,
):
    heads = qkv_up.shape[2] // (3 * HD)
    half = 2 * QUART
    for j, send_ref in enumerate((s0, s1, s2, s3)):
        a = pick_ref[j]
        for h in range(heads):
            for t in range(3):
                row, base = (0, QUART * t) if t < 2 else (RANK, 0)
                send_ref[row : row + RANK, base + HD * h : base + HD * (h + 1)] = qkv_up[
                    a, :, HD * (3 * h + t) : HD * (3 * h + t + 1)
                ]
        send_ref[RANK : 2 * RANK, QUART:] = proj_dn[a]
        for i, ref in enumerate((fc1_up, fc2_dn)):
            for part in range(2):
                row = RANK * (2 + 2 * i + part)
                send_ref[row : row + RANK, :] = ref[a, :, half * part : half * (part + 1)]
    for i, ref in enumerate((qkv_dn, fc1_dn, proj_up, fc2_up)):
        row, base = RANK * (i // 2), QUART * (i % 2)
        row_ref[row : row + RANK, base : base + QUART] = ref[pick_ref[0]]
    for i, ref in enumerate((gain1, gain2)):
        row_ref[2 * RANK :, QUART * i : QUART * (i + 1)] = jnp.broadcast_to(ref[...], (RANK, QUART))


def adapter_pack(pick, *mats):
    s = lambda *shape: jax.ShapeDtypeStruct(shape, BF)
    return pl.pallas_call(
        adapter_pack_kernel,
        out_shape=(s(6 * RANK, 2 * QUART),) * 4 + (s(3 * RANK, 2 * QUART),),
        in_specs=[sm()] + [vm()] * 10,
        out_specs=[vm()] * 5,
        compiler_params=params(),
        cost_estimate=cost(2),
        name="adapter_pack",
    )(pick, *mats)


def alpha_block(k, j):
    part = k
    if j == 0:
        return [(part, 0, QUART, None)]
    return [
        (part, QUART + HBLK * (j - 1), HBLK, 0),
        (part, QUART + 3 * HBLK + HBLK * (j - 1), HBLK, 1),
    ]


def beta_block(k, j):
    core, cross = k % 2, k // 2
    base = 3 * core
    if j == 0 and not cross:
        return [(base, 0, QUART, None)]
    row = 0 if j == 0 else HBLK + QUART * (j - 1) + HBLK * cross
    return [(base + 1, row, HBLK, 0), (base + 2, row, HBLK, 1)]


def block_dst(start, flag, half):
    if flag is None:
        return start
    offset = half if flag == 0 else 1 - half
    return pl.multiple_of(start + offset * HBLK, 32)


def prep1_kernel(
    where_ref, p0, p1, p2, p3, q0, q1, q2, q3, q4, q5, a0, a1, a2, a3,
    wqkv_ref, wproj_ref, dqkv, uqkv, dproj, uproj, d1, u1, d2, u2, gain1, gain2,
):
    half = where_ref[1]
    for j, a in enumerate((a0, a1, a2, a3)):
        base = a.shape[0] - 6 * RANK
        part = lambda i: slice(base + RANK * i, base + RANK * (i + 1))
        for t in range(3):
            uqkv[:, D * t + QUART * j : D * t + QUART * (j + 1)] = a[
                part(t // 2), QUART * (t % 2) : QUART * (t % 2 + 1)
            ]
        dproj[:, QUART * j : QUART * (j + 1)] = a[part(1), QUART:]
        for i in range(2):
            u1[:, D * j + D // 2 * i : D * j + D // 2 * (i + 1)] = a[part(2 + i), :]
            d2[:, D * j + D // 2 * i : D * j + D // 2 * (i + 1)] = a[part(4 + i), :]
    for k, ref in enumerate((p0, p1, p2, p3)):
        for i, dst in enumerate((dqkv, d1, uproj, u2)):
            rows = slice(D + RANK * (i // 2), D + RANK * (i // 2 + 1))
            dst[:, QUART * k : QUART * (k + 1)] = ref[rows, QUART * (i % 2) : QUART * (i % 2 + 1)]
        for i, dst in enumerate((gain1, gain2)):
            row = D + 2 * RANK
            dst[:, QUART * k : QUART * (k + 1)] = ref[row : row + 1, QUART * i : QUART * (i + 1)].astype(F32)
    alpha, beta = (p0, p1, p2, p3), (q0, q1, q2, q3, q4, q5)
    for k in range(4):
        for j in range(4):
            for part, row, count, flag in alpha_block(k, j):
                rows = pl.ds(block_dst(QUART * k, flag, half), count)
                for t in range(2):
                    wqkv_ref[rows, D * t + QUART * j : D * t + QUART * (j + 1)] = alpha[part][
                        row : row + count, QUART * t : QUART * (t + 1)
                    ]
            for part, row, count, flag in beta_block(k, j):
                rows = pl.ds(block_dst(QUART * k, flag, half), count)
                wqkv_ref[rows, 2 * D + QUART * j : 2 * D + QUART * (j + 1)] = beta[part][
                    row : row + count, :QUART
                ]
                rows = pl.ds(block_dst(QUART * j, flag, half), count)
                wproj_ref[rows, QUART * k : QUART * (k + 1)] = beta[part][row : row + count, QUART:]
    for k in range(4):
        rows = slice(QUART * k, QUART * (k + 1))
        for t in range(3):
            cols = slice(D * t, D * (t + 1))
            low = tn(dqkv[:, rows], uqkv[:, cols])
            wqkv_ref[rows, cols] = (wqkv_ref[rows, cols].astype(F32) + low).astype(BF)
        low = tn(dproj[:, rows], uproj[...])
        wproj_ref[rows, :] = (wproj_ref[rows, :].astype(F32) + low).astype(BF)


def prep1(where, alpha, beta, cols):
    s = lambda *shape: jax.ShapeDtypeStruct(shape, BF)
    return pl.pallas_call(
        prep1_kernel,
        out_shape=(
            s(D, 3 * D), s(D, D), s(RANK, D), s(RANK, 3 * D), s(RANK, D), s(RANK, D),
            s(RANK, D), s(RANK, 4 * D), s(RANK, 4 * D), s(RANK, D),
            jax.ShapeDtypeStruct((1, D), F32), jax.ShapeDtypeStruct((1, D), F32),
        ),
        in_specs=[sm()] + [vm()] * 14,
        out_specs=[vm()] * 12,
        compiler_params=params(),
        cost_estimate=cost(7),
        name="attention_weights",
    )(where, *alpha, *beta, *cols)


def normalize(values):
    center = jnp.sum(values, axis=1, keepdims=True) / D
    shifted = values - center
    inv_std = lax.rsqrt(jnp.sum(shifted * shifted, axis=1, keepdims=True) / D + EPSILON)
    return shifted * inv_std, inv_std


def norm_back(grad, normed, inv_std):
    first = jnp.sum(grad, axis=1, keepdims=True) / D
    second = jnp.sum(grad * normed, axis=1, keepdims=True) / D
    return inv_std * (grad - first - normed * second)


def barrel(values, amount, left):
    for bit in (1, 2, 4, 8):
        moved = pltpu.roll(values, (128 - bit) if left else bit, 1)
        values = jnp.where((amount & bit) != 0, moved, values)
    return values


def low_half(count):
    return lax.broadcasted_iota(jnp.int32, (count, 128), 1) < HD


def pad_rows(tile):
    if tile.shape[0] == KEYS:
        return tile
    return jnp.concatenate([tile, jnp.zeros((KEYS - tile.shape[0], tile.shape[1]), tile.dtype)], axis=0)


def live_rows():
    return lax.broadcasted_iota(jnp.int32, (KEYS, 128), 0) < SLOTS


GROUP = 6
GROUP_BACK = 6


def pair_columns(pair):
    return tuple(slice(D * t + 128 * pair, D * t + 128 * (pair + 1)) for t in range(3))


def attend_window(kind, row0, qkv_ref, att_ref, exp_ref, inv_ref, rel_ref, shift_ref, keys_ref):
    count = NQ[kind]
    rows = pl.ds(row0, count)
    low_q, low_k = low_half(count), low_half(KEYS)
    live = live_rows()
    ones = jnp.where(live, 1.0, 0.0).astype(BF)
    amount = shift_ref[kind, :count, :]
    onehot = keys_ref[kind]
    rel_mat = rel_ref[...]
    for first in range(0, D // 128, GROUP):
        pairs = range(first, first + GROUP)
        heads = [(pair, odd) for pair in pairs for odd in range(2)]
        q_tile = {p: qkv_ref[rows, pair_columns(p)[0]] for p in pairs}
        rel = {p: nn(q_tile[p], rel_mat) for p in pairs}
        rel = {p: barrel(rel[p], amount, True).astype(BF) for p in pairs}
        k_tile = {p: pad_rows(qkv_ref[rows, pair_columns(p)[1]] * BF(HD**-0.5)) for p in pairs}
        scores = {}
        for p, odd in heads:
            if odd:
                q_aug, k_aug = jnp.where(low_q, rel[p], q_tile[p]), jnp.where(low_k, onehot, k_tile[p])
            else:
                q_aug, k_aug = jnp.where(low_q, q_tile[p], rel[p]), jnp.where(low_k, k_tile[p], onehot)
            scores[p, odd] = nt(q_aug, k_aug)
        top = {h: jnp.max(scores[h], axis=1, keepdims=True) for h in heads}
        exponent = {h: jnp.exp(scores[h] - top[h]).astype(BF) for h in heads}
        both = {}
        for p, odd in heads:
            exp_ref[2 * p + odd, rows, :] = exponent[p, odd]
            v_tile = pad_rows(qkv_ref[rows, pair_columns(p)[2]])
            if kind == FULL:
                v_tile = jnp.where(live, v_tile, 0).astype(BF)
            v_aug = jnp.where(low_k, ones, v_tile) if odd else jnp.where(low_k, v_tile, ones)
            both[p, odd] = nn(exponent[p, odd], v_aug)
        for p in pairs:
            cols = pair_columns(p)[0]
            inverse = 1.0 / pltpu.roll(jnp.where(low_q, both[p, 1], both[p, 0]), HD, 1)
            inv_ref[rows, cols] = inverse
            att_ref[rows, cols] = (jnp.where(low_q, both[p, 0], both[p, 1]) * inverse).astype(BF)


PARTS = ((FULL, FULL), (FULL, FULL), (RIGHT, BOTTOM, CORNER))
PART_ROWS = tuple(sum(NQ[kind] for kind in part) for part in PARTS)
PART_OFFS = (0, PART_ROWS[0], PART_ROWS[0] + PART_ROWS[1])


TAIL = ((0, 576), (576, ROWS))


def qkv_kernel(x0, x1, x2, x3, gain_ref, wqkv_ref, x_ref, hid_ref, qkv_a, qkv_b, qkv_c):
    join_pieces((x0, x1, x2, x3), x_ref)
    gain = gain_ref[...]

    def norm_step(i, carry):
        rows = pl.ds(pl.multiple_of(i * 112, 16), 112)
        normed, _ = normalize(x_ref[rows, :].astype(F32))
        hid_ref[rows, :] = (normed * gain).astype(BF)
        return carry

    lax.fori_loop(0, ROWS // 112, norm_step, 0)
    for ref, offset, count in zip((qkv_a, qkv_b, qkv_c), PART_OFFS, PART_ROWS):
        hid = hid_ref[offset : offset + count, :]
        for t in range(3):
            cols = slice(D * t, D * (t + 1))
            ref[:, cols] = nn(hid, wqkv_ref[:, cols]).astype(BF)
    for w in range(4):
        hid_ref[FULLR * w + SLOTS : FULLR * (w + 1), :] = jnp.zeros((FULLR - SLOTS, D), BF)


def qkv_rows(pieces, gain, wqkv):
    s = lambda *shape: jax.ShapeDtypeStruct(shape, BF)
    return pl.pallas_call(
        qkv_kernel,
        out_shape=(s(ROWS, D), s(ROWS, D)) + tuple(s(n, 3 * D) for n in PART_ROWS),
        in_specs=[vm()] * 6,
        out_specs=[vm()] * 5,
        compiler_params=params(),
        cost_estimate=cost(12),
        name="norm_and_qkv",
    )(*pieces, gain, wqkv)


def attention_kernel(qkv_ref, rel_ref, shift_ref, keys_ref, att_ref, exp_ref, inv_ref, *, kinds):
    refs = (qkv_ref, att_ref, exp_ref, inv_ref, rel_ref, shift_ref, keys_ref)
    if kinds[0] == FULL:

        def step(w, carry):
            attend_window(FULL, pl.multiple_of(w * FULLR, 16), *refs)
            return carry

        lax.fori_loop(0, len(kinds), step, 0)
    else:
        row = 0
        for kind in kinds:
            attend_window(kind, row, *refs)
            row += NQ[kind]


def attention(part, qkv, rel, shift, keys):
    rows = PART_ROWS[part]
    s = lambda *shape, dtype=BF: jax.ShapeDtypeStruct(shape, dtype)
    return pl.pallas_call(
        functools.partial(attention_kernel, kinds=PARTS[part]),
        out_shape=(s(rows, D), s(D // HD, rows, KEYS), s(rows, D, dtype=F32)),
        in_specs=[vm()] * 4,
        out_specs=[vm()] * 3,
        compiler_params=params(),
        cost_estimate=cost(10),
        name="attention_forward",
    )(qkv, rel, shift, keys)


def project_kernel(x_ref, att_a, att_b, att_c, wproj_ref, middle_ref):
    for ref, offset, count in zip((att_a, att_b, att_c), PART_OFFS, PART_ROWS):
        rows = slice(offset, offset + count)
        middle_ref[rows, :] = x_ref[rows, :].astype(F32) + nn(ref[...], wproj_ref[...])


def project(x, atts, wproj):
    return pl.pallas_call(
        project_kernel,
        out_shape=jax.ShapeDtypeStruct((ROWS, D), F32),
        in_specs=[vm()] * 5,
        out_specs=vm(),
        compiler_params=params(),
        cost_estimate=cost(5),
        name="projection",
    )(x, *atts, wproj)


CHUNK = 512
LOCK = 2


def mlp_kernel(
    where_ref, middle_ref, g0, g1, g2, g3, gain_ref,
    p0, p1, p2, p3, q0, q1, q2, q3, q4, q5, s0, s1, s2, s3, s4, s5, d1, u1, d2, u2,
    o0, o1, o2, gmid_ref, down1, up1, down2, up2,
    gm_ref, out_rows, h2_ref, acc_mlp, acc_gh, gu1, ad2, w1_ref, w2_ref, sem,
):
    half = where_ref[1]
    copies = []

    def fetch(src, dst):
        copies.append(pltpu.make_async_copy(src, dst, sem.at[len(copies)]))
        copies[-1].start()

    alpha = (p0, p1, p2, p3)
    betas = ((q0, q1, q2, q3, q4, q5), (s0, s1, s2, s3, s4, s5))
    for k in range(4):
        for j in range(4):
            for part, row, count, flag in alpha_block(k, j):
                rows = pl.ds(block_dst(QUART * k, flag, half), count)
                fetch(alpha[part].at[row : row + count, :], w1_ref.at[rows, D * j : D * (j + 1)])
            for part, row, count, flag in beta_block(k, j):
                rows = pl.ds(block_dst(QUART * k, flag, half), count)
                for i, beta in enumerate(betas):
                    cols = slice(D * j + D // 2 * i, D * j + D // 2 * (i + 1))
                    fetch(beta[part].at[row : row + count, :], w2_ref.at[rows, cols])
    join_pieces((g0, g1, g2, g3), gm_ref)
    for copy in copies:
        copy.wait()
    for k in range(4):
        rows = slice(QUART * k, QUART * (k + 1))
        for j in range(4):
            cols = slice(D * j, D * (j + 1))
            low = tn(d1[:, rows], u1[:, cols])
            w1_ref[rows, cols] = (w1_ref[rows, cols].astype(F32) + low).astype(BF)
            low = tn(u2[:, rows], d2[:, cols])
            w2_ref[rows, cols] = (w2_ref[rows, cols].astype(F32) + low).astype(BF)
    gain = gain_ref[...]
    down1[...] = jnp.zeros_like(down1)
    up1[...] = jnp.zeros_like(up1)
    down2[...] = jnp.zeros_like(down2)
    up2[...] = jnp.zeros_like(up2)

    def tile_step(t, carry):
        rows = pl.ds(pl.multiple_of(t * HALF, 16), HALF)
        normed, _ = normalize(middle_ref[rows, :])
        h2 = (normed * gain).astype(BF)
        h2_ref[...] = h2
        gm = gm_ref[rows, :]
        ad1 = nt(d1[...], h2).astype(BF)
        gu2 = nt(u2[...], gm).astype(BF)
        acc_mlp[...] = jnp.zeros_like(acc_mlp)
        acc_gh[...] = jnp.zeros_like(acc_gh)
        gu1[...] = jnp.zeros_like(gu1)
        ad2[...] = jnp.zeros_like(ad2)

        def chunk_step(c, inner_carry):
            spans = [
                pl.ds(pl.multiple_of((c * LOCK + i) * CHUNK, CHUNK), CHUNK) for i in range(LOCK)
            ]
            h2 = h2_ref[...]
            gm = gm_ref[rows, :]
            inner = [nn(h2, w1_ref[:, span]) for span in spans]
            gact = [nn(gm, w2_ref[:, span]) for span in spans]
            act, ginner = [], []
            for i in range(LOCK):
                half = 0.5 * (1.0 + lax.erf(inner[i] * 2**-0.5))
                act.append((inner[i] * half).astype(BF))
                slope = half + inner[i] * (jnp.exp(-0.5 * inner[i] * inner[i]) * (2 * np.pi) ** -0.5)
                ginner.append((gact[i] * slope).astype(BF))
            for i, span in enumerate(spans):
                acc_mlp[...] += nt(act[i], w2_ref[:, span])
                acc_gh[...] += nt(ginner[i], w1_ref[:, span])
                up1[:, span] += nn(ad1, ginner[i])
                gu1[...] += nt(u1[:, span], ginner[i])
                ad2[...] += nt(d2[:, span], act[i])
                down2[:, span] += nn(gu2, act[i])
            return inner_carry

        lax.fori_loop(0, 4 * D // (CHUNK * LOCK), chunk_step, 0)
        down1[...] += nn(gu1[...].astype(BF), h2_ref[...])
        up2[...] += nn(ad2[...].astype(BF), gm_ref[rows, :])
        middle = middle_ref[rows, :]
        out_rows[rows, :] = (middle + acc_mlp[...]).astype(BF)
        normed, inv_std = normalize(middle)
        gmid_ref[rows, :] = gm_ref[rows, :].astype(F32) + norm_back(acc_gh[...] * gain, normed, inv_std)
        return carry

    lax.fori_loop(0, 2, tile_step, 0)
    split_pieces(out_rows, (o0, o1, o2))


def mlp(where, middle, pieces, gain, alpha, betas, d1, u1, d2, u2):
    s = lambda *shape, dtype=F32: jax.ShapeDtypeStruct(shape, dtype)
    return pl.pallas_call(
        mlp_kernel,
        out_shape=pieces_of(ROWS)
        + (s(ROWS, D), s(RANK, D), s(RANK, 4 * D), s(RANK, 4 * D), s(RANK, D)),
        in_specs=[sm()] + [vm()] * 6 + [pl.BlockSpec(memory_space=pl.ANY)] * 16 + [vm()] * 4,
        out_specs=[vm()] * 8,
        scratch_shapes=[
            pltpu.VMEM((ROWS, D), BF), pltpu.VMEM((ROWS, D), BF), pltpu.VMEM((HALF, D), BF),
            pltpu.VMEM((HALF, D), F32), pltpu.VMEM((HALF, D), F32),
            pltpu.VMEM((RANK, HALF), F32), pltpu.VMEM((RANK, HALF), F32),
            pltpu.VMEM((D, 4 * D), BF), pltpu.VMEM((D, 4 * D), BF),
            pltpu.SemaphoreType.DMA((4 * 4 * 6,)),
        ],
        compiler_params=params(),
        cost_estimate=cost(48),
        name="mlp_forward_backward",
    )(where, middle, *pieces, gain, *alpha, *betas[0], *betas[1], d1, u1, d2, u2)


def attend_back_window(
    kind, row0, qkv_ref, att_ref, exp_ref, inv_ref, gatt_ref, gqkv_ref, rel_ref, shift_ref, keys_ref
):
    count = NQ[kind]
    rows = pl.ds(row0, count)
    low_q, low_k = low_half(count), low_half(KEYS)
    live = live_rows()
    lane_k = lax.broadcasted_iota(jnp.int32, (KEYS, 128), 1) % HD
    lane_q = lax.broadcasted_iota(jnp.int32, (count, 128), 1) % HD
    ones = jnp.where(live & (lane_k < 2), 1.0, 0.0).astype(BF)
    across = jnp.where(
        low_half(128) != (lax.broadcasted_iota(jnp.int32, (128, 128), 0) < HD), -1.0, 0.0
    ).astype(BF)
    amount = shift_ref[kind, :count, :]
    onehot = keys_ref[kind]
    rel_mat = rel_ref[...]
    for first in range(0, D // 128, GROUP_BACK):
        pairs = range(first, first + GROUP_BACK)
        heads = [(pair, odd) for pair in pairs for odd in range(2)]
        go_tile = {
            p: (gatt_ref[rows, pair_columns(p)[0]].astype(F32) * inv_ref[rows, pair_columns(p)[0]]).astype(BF)
            for p in pairs
        }
        delta = {
            p: nn((go_tile[p].astype(F32) * att_ref[rows, pair_columns(p)[0]].astype(F32)).astype(BF), across)
            for p in pairs
        }
        go_t = {p: go_tile[p].T for p in pairs}
        gv = {}
        for p, odd in heads:
            gv[p, odd] = nn(go_t[p][HD * odd : HD * (odd + 1), :], exp_ref[2 * p + odd, rows, :])
        gscore = {}
        for p in pairs:
            high = delta[p].astype(BF)
            rest = (delta[p] - high.astype(F32)).astype(BF)
            low_delta = jnp.where(lane_q == 0, high, jnp.where(lane_q == 1, rest, 0)).astype(BF)
            v_tile = pad_rows(qkv_ref[rows, pair_columns(p)[2]])
            if kind == FULL:
                v_tile = jnp.where(live, v_tile, 0).astype(BF)
            gscore[p, 0] = nt(jnp.where(low_q, go_tile[p], low_delta), jnp.where(low_k, v_tile, ones))
            gscore[p, 1] = nt(jnp.where(low_q, low_delta, go_tile[p]), jnp.where(low_k, ones, v_tile))
        q_t = {p: qkv_ref[rows, pair_columns(p)[0]].T for p in pairs}
        gs = {(p, odd): (exp_ref[2 * p + odd, rows, :].astype(F32) * gscore[p, odd]).astype(BF) for p, odd in heads}
        gk = {(p, odd): nn(q_t[p][HD * odd : HD * (odd + 1), :], gs[p, odd]) for p, odd in heads}
        gq = {}
        for p in pairs:
            k_tile = pad_rows(qkv_ref[rows, pair_columns(p)[1]] * BF(HD**-0.5))
            gq[p, 0] = nn(gs[p, 0], jnp.where(low_k, k_tile, onehot))
            gq[p, 1] = nn(gs[p, 1], jnp.where(low_k, onehot, k_tile))
        sums = {p: barrel(jnp.where(low_q, gq[p, 1], gq[p, 0]), amount, False).astype(BF) for p in pairs}
        for p in pairs:
            cols, kcols, vcols = pair_columns(p)
            gv_tile = jnp.concatenate([gv[p, 0], gv[p, 1]], axis=0).astype(BF).T
            gqkv_ref[rows, vcols] = gv_tile[:count, :]
            gk_tile = (jnp.concatenate([gk[p, 0], gk[p, 1]], axis=0) * HD**-0.5).astype(BF).T
            gqkv_ref[rows, kcols] = gk_tile[:count, :]
            gqkv_ref[rows, cols] = (jnp.where(low_q, gq[p, 0], gq[p, 1]) + nt(sums[p], rel_mat)).astype(BF)


def attention_back_kernel(
    gmid_ref, hid_ref, qkv_a, qkv_b, qkv_c, att_a, att_b, att_c, exp_a, exp_b, exp_c, inv_a, inv_b, inv_c,
    wproj_ref, rel_ref, shift_ref, keys_ref, dqkv, uqkv, dproj, uproj,
    gqkv_ref, down_q, up_q, down_p, up_p, gb_ref, gatt_ref, att_ref,
):
    gb_ref[...] = gmid_ref[...].astype(BF)
    gatt_ref[...] = nt(gb_ref[...], wproj_ref[...]).astype(BF)
    for ref, offset, count in zip((att_a, att_b, att_c), PART_OFFS, PART_ROWS):
        att_ref[offset : offset + count, :] = ref[...]
    up_p[...] = nn(nt(dproj[...], att_ref[...]).astype(BF), gb_ref[...])
    down_p[...] = nn(nt(uproj[...], gb_ref[...]).astype(BF), att_ref[...])
    tables = (rel_ref, shift_ref, keys_ref)
    for part, parts in enumerate(
        ((qkv_a, att_a, exp_a, inv_a), (qkv_b, att_b, exp_b, inv_b), (qkv_c, att_c, exp_c, inv_c))
    ):
        span = pl.ds(PART_OFFS[part], PART_ROWS[part])
        refs = parts + (gatt_ref.at[span, :], gqkv_ref.at[span, :]) + tables
        if PARTS[part][0] == FULL:

            def step(w, carry, refs=refs):
                attend_back_window(FULL, pl.multiple_of(w * FULLR, 16), *refs)
                return carry

            lax.fori_loop(0, len(PARTS[part]), step, 0)
        else:
            row = 0
            for kind in PARTS[part]:
                attend_back_window(kind, row, *refs)
                row += NQ[kind]
    up_q[...] = nn(nt(dqkv[...], hid_ref[...]).astype(BF), gqkv_ref[...])
    down_q[...] = nn(nt(uqkv[...], gqkv_ref[...]).astype(BF), hid_ref[...])


def attention_back(gmid, hid, qkvs, atts, exps, invs, wproj, rel, shift, keys, dqkv, uqkv, dproj, uproj):
    s = lambda *shape, dtype=F32: jax.ShapeDtypeStruct(shape, dtype)
    return pl.pallas_call(
        attention_back_kernel,
        out_shape=(s(ROWS, 3 * D, dtype=BF), s(RANK, D), s(RANK, 3 * D), s(RANK, D), s(RANK, D)),
        in_specs=[vm()] * 22,
        out_specs=[vm()] * 5,
        scratch_shapes=[pltpu.VMEM((ROWS, D), BF)] * 3,
        compiler_params=params(),
        cost_estimate=cost(45),
        name="attention_backward",
    )(gmid, hid, *qkvs, *atts, *exps, *invs, wproj, rel, shift, keys, dqkv, uqkv, dproj, uproj)


def token_grad_kernel(gmid_hbm, x_hbm, gqkv_hbm, gain_ref, wqkv_ref, o0, o1, o2,
                      gmid_ref, x_ref, gqkv_ref, gh_ref, out_rows, sem, *, low, high):
    span = pl.ds(low, high - low)
    copies = [
        pltpu.make_async_copy(src.at[span, :], dst, sem.at[i])
        for i, (src, dst) in enumerate(((gqkv_hbm, gqkv_ref), (x_hbm, x_ref), (gmid_hbm, gmid_ref)))
    ]
    for copy in copies:
        copy.start()
    copies[0].wait()
    gh_ref[...] = nt(gqkv_ref[...], wqkv_ref[...])
    copies[1].wait()
    copies[2].wait()
    gain = gain_ref[...]
    step = (high - low) // 2

    def norm_step(i, carry):
        rows = pl.ds(pl.multiple_of(i * step, 16), step)
        normed, inv_std = normalize(x_ref[rows, :].astype(F32))
        back = norm_back(gh_ref[rows, :] * gain, normed, inv_std)
        out_rows[rows, :] = (gmid_ref[rows, :] + back).astype(BF)
        return carry

    lax.fori_loop(0, 2, norm_step, 0)
    split_pieces(out_rows, (o0, o1, o2))


def token_grad(gmid, x, gqkv, gain, wqkv, low, high):
    count = high - low
    hbm = pl.BlockSpec(memory_space=pl.ANY)
    return pl.pallas_call(
        functools.partial(token_grad_kernel, low=low, high=high),
        out_shape=pieces_of(count),
        in_specs=[hbm, hbm, hbm, vm(), vm()],
        out_specs=[vm()] * 3,
        scratch_shapes=[
            pltpu.VMEM((count, D), F32), pltpu.VMEM((count, D), BF), pltpu.VMEM((count, 3 * D), BF),
            pltpu.VMEM((count, D), F32), pltpu.VMEM((count, D), BF), pltpu.SemaphoreType.DMA((3,)),
        ],
        compiler_params=params(),
        cost_estimate=cost(8),
        name="token_gradient",
    )(gmid, x, gqkv, gain, wqkv)


def grad_pack_kernel(where_ref, down_q, up_q, down_p, up_p, down1, up1, down2, up2, o0, o1, o2, o3, buf_ref):
    mine = where_ref[0]
    for k in range(4):
        for i, ref in enumerate((down_q, down1, up_p, up2)):
            buf_ref[k, :RANK, QUART * i : QUART * (i + 1)] = ref[:, QUART * k : QUART * (k + 1)]
    for dest in range(4):
        k = jnp.bitwise_xor(mine, dest)
        ranks = slice(RANK // 4 * dest, RANK // 4 * (dest + 1))
        for j in range(4):
            base = RANK + 12 * j
            for t in range(3):
                buf_ref[k, base : base + 4, QUART * t : QUART * (t + 1)] = up_q[
                    ranks, D * t + QUART * j : D * t + QUART * (j + 1)
                ]
            buf_ref[k, base : base + 4, 3 * QUART :] = down_p[ranks, QUART * j : QUART * (j + 1)]
            buf_ref[k, base + 4 : base + 8, :] = up1[ranks, D * j : D * (j + 1)]
            buf_ref[k, base + 8 : base + 12, :] = down2[ranks, D * j : D * (j + 1)]
    for k, out in enumerate((o0, o1, o2, o3)):
        out[...] = buf_ref[k].astype(BF)


def grad_pack(where, *grads):
    return pl.pallas_call(
        grad_pack_kernel,
        out_shape=(jax.ShapeDtypeStruct((4 * RANK, D), BF),) * 4,
        in_specs=[sm()] + [vm()] * 8,
        out_specs=[vm()] * 4,
        scratch_shapes=[pltpu.VMEM((4, 4 * RANK, D), F32)],
        compiler_params=params(),
        cost_estimate=cost(2),
        name="adapter_grad_pack",
    )(where, *grads)


def grad_sum_kernel(g0, g1, g2, g3, o0, o1, o2, o3, buf_ref):
    total = g0[...].astype(F32) + g1[...].astype(F32) + g2[...].astype(F32) + g3[...].astype(F32)
    buf_ref[...] = jnp.zeros_like(buf_ref)
    buf_ref[:RANK, :] = total[:RANK, :]
    for j, out in enumerate((o0, o1, o2, o3)):
        buf_ref[RANK : RANK + 12, :] = total[RANK + 12 * j : RANK + 12 * (j + 1), :]
        out[...] = buf_ref[...].astype(BF)


def grad_sum(pieces):
    return pl.pallas_call(
        grad_sum_kernel,
        out_shape=(jax.ShapeDtypeStruct((2 * RANK, D), BF),) * 4,
        in_specs=[vm()] * 4,
        out_specs=[vm()] * 4,
        scratch_shapes=[pltpu.VMEM((2 * RANK, D), F32)],
        compiler_params=params(),
        cost_estimate=cost(2),
        name="adapter_grad_sum",
    )(*pieces)


def grad_adapters_kernel(index_ref, x_ref, qkv_dn, fc1_dn, proj_up, fc2_up, rest_ref, acc_ref):
    acc_ref[...] = jnp.zeros_like(acc_ref)

    def add(i, carry):
        acc_ref[index_ref[i]] += x_ref[i].astype(F32)
        return carry

    lax.fori_loop(0, x_ref.shape[0], add, 0)
    for i, ref in enumerate((qkv_dn, fc1_dn, proj_up, fc2_up)):
        ref[...] = acc_ref[:, :RANK, QUART * i : QUART * (i + 1)]
    rest_ref[...] = acc_ref[:, RANK:, :].astype(BF)


def grad_adapters(index, x):
    s = lambda n, dtype=F32: jax.ShapeDtypeStruct((ADAPT, RANK, n), dtype)
    return pl.pallas_call(
        grad_adapters_kernel,
        out_shape=(s(QUART), s(QUART), s(QUART), s(QUART), s(D, BF)),
        in_specs=[sm(), vm()],
        out_specs=[vm()] * 5,
        scratch_shapes=[pltpu.VMEM((ADAPT, 2 * RANK, D), F32)],
        compiler_params=params(),
        cost_estimate=cost(2),
        name="adapter_grad_by_adapter",
    )(index, x)


def grad_join_kernel(where_ref, r0, r1, r2, r3, qkv_up, proj_dn, fc1_up, fc2_dn, buf_ref):
    mine = where_ref[0]
    heads = qkv_up.shape[2] // (3 * HD)
    for k, ref in enumerate((r0, r1, r2, r3)):
        buf_ref[jnp.bitwise_xor(mine, k)] = ref[...].astype(F32)
    for source in range(4):
        ranks = slice(RANK // 4 * source, RANK // 4 * (source + 1))
        for h in range(heads):
            for t in range(3):
                qkv_up[:, ranks, HD * (3 * h + t) : HD * (3 * h + t + 1)] = buf_ref[
                    source, :, 0:4, QUART * t + HD * h : QUART * t + HD * (h + 1)
                ]
        proj_dn[:, ranks, :] = buf_ref[source, :, 0:4, 3 * QUART :]
        fc1_up[:, ranks, :] = buf_ref[source, :, 4:8, :]
        fc2_dn[:, ranks, :] = buf_ref[source, :, 8:12, :]


def grad_join(where, pieces):
    s = lambda n: jax.ShapeDtypeStruct((ADAPT, RANK, n), F32)
    return pl.pallas_call(
        grad_join_kernel,
        out_shape=(s(3 * QUART), s(QUART), s(D), s(D)),
        in_specs=[sm()] + [vm()] * 4,
        out_specs=[vm()] * 4,
        scratch_shapes=[pltpu.VMEM((4, ADAPT, RANK, D), F32)],
        compiler_params=params(),
        cost_estimate=cost(2),
        name="adapter_grad_join",
    )(where, *pieces)


def flip(values, axis, distance):
    size = lax.axis_size(axis)
    return lax.ppermute(values, axis, [(i, i ^ distance) for i in range(size)])


def send_rows(pieces):
    own, near, pair = pieces
    return [own, flip(near, "row", 1), flip(pair, "row", 2)]


def hand_on(pieces, *deps):
    own, near, crossed = pieces
    if deps:
        near, crossed = after((near, crossed), *deps)
    return [own, near, crossed, flip(crossed, "row", 1)]


def exchange(slots, axis):
    return [slots[0]] + [flip(slots[k], axis, k) for k in range(1, 4)]


def after(values, *deps):
    return lax.optimization_barrier((tuple(values), deps))[0]


def col_halves(half):
    return jnp.concatenate([flip(half, "col", j) for j in range(1, 4)], axis=0)


def col_pairs(half, other_row):
    two = jnp.concatenate([half, other_row], axis=0)
    return jnp.concatenate([other_row] + [flip(two, "col", j) for j in range(1, 4)], axis=0)


def rel_matrix(rel_h, rel_w):
    pad = jnp.zeros((32 - (2 * WIN - 1), HD), BF)
    block = jnp.concatenate([rel_h[::-1], pad, rel_w[::-1], pad], axis=0).T
    zero = jnp.zeros((HD, HD), BF)
    return jnp.concatenate(
        [jnp.concatenate([zero, block], axis=1), jnp.concatenate([block, zero], axis=1)], axis=0
    )


def body(
    tokens, grad_out, adapter_index, norm1_gain, norm2_gain, qkv_weight, proj_weight, fc1_weight, fc2_weight,
    rel_h, rel_w, qkv_down, qkv_up, proj_down, proj_up, fc1_down, fc1_up, fc2_down, fc2_up,
):
    members = lax.axis_size("col")
    batches = lax.axis_size("dp")
    row_index, col_index, dp_index = lax.axis_index("row"), lax.axis_index("col"), lax.axis_index("dp")
    half = dp_index % 2
    where = jnp.stack([row_index, half]).astype(jnp.int32)
    slot_images = (
        jnp.bitwise_xor(dp_index, jnp.arange(batches, dtype=jnp.int32))[:, None] * members
        + jnp.bitwise_xor(col_index, jnp.arange(members, dtype=jnp.int32))[None, :]
    ).reshape(-1)
    slot_adapters = jnp.sum(
        jnp.where(
            slot_images[:, None] == jnp.arange(adapter_index.shape[0], dtype=jnp.int32)[None, :],
            adapter_index[:, 0][None, :],
            0,
        ),
        axis=1,
    )
    pick = jnp.concatenate([slot_adapters[:4], half[None]]).astype(jnp.int32)
    swap = lambda m: jnp.swapaxes(m, 1, 2)

    rel = rel_matrix(rel_h, rel_w)
    shift, keys = jnp.asarray(SHIFT_NP), jnp.asarray(KEYS_NP)

    *token_slots, alpha_own, beta_own, alpha_half, beta_half = front(where, tokens, qkv_weight, proj_weight)
    b0 = flip(beta_half, "row", 2)
    alpha_near = col_halves(alpha_half)
    x_pieces = send_rows(token_slots)
    *send, row_adapters = adapter_pack(
        pick, qkv_up, swap(proj_down), fc1_up, swap(fc2_down), swap(qkv_down), swap(fc1_down), proj_up, fc2_up,
        norm1_gain.reshape(1, -1), norm2_gain.reshape(1, -1),
    )
    beta_sent = [jnp.concatenate([beta_half, b0, send[j]], axis=0) for j in range(1, 4)]
    beta_got = [flip(m, "col", j) for j, m in enumerate(beta_sent, 1)]
    beta_near = jnp.concatenate([b0] + [m[:QUART] for m in beta_got], axis=0)
    col_adapters = [send[0]] + beta_got
    alpha_far = flip(alpha_near, "dp", 1)
    g = jnp.concatenate([alpha_own, alpha_near, alpha_far, row_adapters], axis=0)
    beta_near, *x_pieces = after((beta_near, *x_pieces), alpha_far)
    beta_far = flip(beta_near, "dp", 1)
    g, _ = after((g, x_pieces[2]), beta_near)
    gy = flip(g, "row", 2)
    x_pieces = hand_on(x_pieces)

    cut = lambda m: lax.dynamic_slice_in_dim(m, half * HBLK, HBLK, 0)
    fc2_cols = [fc2_weight[:, : D // 2], fc2_weight[:, D // 2 :]]
    fc1_half, fc2_half = after((cut(fc1_weight), cut(fc2_weight)), beta_near)
    c0 = flip(fc2_half, "row", 2)
    fc1_near = [flip(fc1_half, "col", j) for j in range(1, 4)]
    grad_slots = pack(where, grad_out)

    alpha1 = [g, flip(g, "row", 1), gy, flip(gy, "row", 1)]
    beta1 = [beta_own, beta_near, beta_far] + [flip(m, "row", 1) for m in (beta_own, beta_near, beta_far)]
    grad_slots = after(tuple(grad_slots), gy)
    g_pieces = send_rows(grad_slots)
    *alpha1, c0 = after((*alpha1, c0))
    two = jnp.concatenate([fc2_half, c0], axis=0)
    fc2_near = [[flip(two[:, D // 2 * i : D // 2 * (i + 1)], "col", j) for j in range(1, 4)] for i in range(2)]
    wqkv, wproj, dqkv, uqkv, dproj, uproj, d1, u1, d2, u2, gain1, gain2 = prep1(
        where, alpha1, beta1, col_adapters
    )
    wqkv, *fc1_near = after((wqkv, *fc1_near))
    fc1_near = jnp.concatenate(fc1_near, axis=0)
    fc1_far = flip(fc1_near, "dp", 1)
    x, hid, *qkvs = qkv_rows(x_pieces, gain1, wqkv)
    *qkvs, fc1_far, n1, n2, n3 = after((*qkvs, fc1_far, *fc2_near[0]), *g_pieces)
    g_pieces = hand_on(g_pieces, fc1_far)
    h = jnp.concatenate([fc1_weight, fc1_near, fc1_far], axis=0)
    hy = flip(h, "row", 2)
    fc2_near0 = jnp.concatenate([c0[:, : D // 2], n1, n2, n3], axis=0)
    fc2_far0 = flip(fc2_near0, "dp", 1)
    part0 = attention(0, qkvs[0], rel, shift, keys)
    qkv1, n1, n2, n3 = after((qkvs[1], *fc2_near[1]), part0[0])
    fc2_near1 = jnp.concatenate([c0[:, D // 2 :], n1, n2, n3], axis=0)
    fc2_near1, fc2_far0 = after((fc2_near1, fc2_far0))
    fc2_far1 = flip(fc2_near1, "dp", 1)
    part1 = attention(1, qkv1, rel, shift, keys)
    qkv2, _ = after((qkvs[2], fc2_far0), part1[0])
    part2 = attention(2, qkv2, rel, shift, keys)
    atts, exps, invs = zip(part0, part1, part2)
    atts = list(atts)
    atts[2], hy = after((atts[2], hy))
    alpha2 = [h, flip(h, "row", 1), hy, flip(hy, "row", 1)]
    middle = project(x, atts, wproj)
    middle, fc2_far1 = after((middle, fc2_far1))
    betas = [
        [own, near, far] + [flip(m, "row", 1) for m in (own, near, far)]
        for own, near, far in zip(fc2_cols, (fc2_near0, fc2_near1), (fc2_far0, fc2_far1))
    ]

    *out_slots, gmid, down1, up1, down2, up2 = mlp(where, middle, g_pieces, gain2, alpha2, betas, d1, u1, d2, u2)
    out_pieces = send_rows(out_slots)
    gqkv, down_q, up_q, down_p, up_p = attention_back(
        gmid, hid, qkvs, atts, exps, invs, wproj, rel, shift, keys, dqkv, uqkv, dproj, uproj
    )
    out_pieces = hand_on(out_pieces, gqkv)
    gqkv, down_q, up_q, down_p, up_p = after((gqkv, down_q, up_q, down_p, up_p), *out_pieces[:3])
    packed = grad_pack(where, down_q, up_q, down_p, up_p, down1, up1, down2, up2)
    *packed, gqkv = after((*packed, gqkv))
    row_sums = exchange(packed, "row")
    back0 = token_grad(gmid, x, gqkv, gain1, wqkv, *TAIL[0])
    *row_sums, gqkv = after((*row_sums, gqkv), back0[0])
    back_pieces = send_rows(back0)
    summed = grad_sum(row_sums)
    *summed, gqkv = after((*summed, gqkv))
    images = exchange(summed, "col")
    back1 = token_grad(gmid, x, gqkv, gain1, wqkv, *TAIL[1])
    last_pieces = send_rows(back1)
    *images, near, crossed = after((*images, *back_pieces[1:]), back1[0])
    back_pieces = hand_on([back_pieces[0], near, crossed])
    images = jnp.stack(images)
    step = 1
    while step < batches:
        images = jnp.concatenate([images, flip(images, "dp", step)], axis=0)
        step *= 2
    result = unpack(where, out_pieces, BF)
    images, = after((images,), result)
    qkv_dn, fc1_dn, proj_upg, fc2_upg, rest = grad_adapters(slot_adapters.astype(jnp.int32), images)
    rests = [rest] + [flip(rest, "row", k) for k in range(1, 4)]
    grad_tokens = unpack(where, back_pieces + hand_on(last_pieces, rest), F32, TAIL)
    rests = after(tuple(rests), grad_tokens)
    qkv_upg, proj_dn, fc1_upg, fc2_dn = grad_join(where, rests)
    return (
        result, grad_tokens,
        swap(qkv_dn), qkv_upg, swap(proj_dn), proj_upg, swap(fc1_dn), fc1_upg, swap(fc2_dn), fc2_upg,
    )


def solution(mesh):
    return jax.shard_map(
        body,
        mesh=mesh,
        in_specs=(
            P("row", ("dp", "col")), P("row", ("dp", "col")), P(), P("row"), P("row"),
            P("row", "col"), P("col", "row"), P("row", "col"), P("row", "col"), P(), P(),
            P(None, "row", None), P(None, None, "col"), P(None, "col", None), P(None, None, "row"),
            P(None, "row", None), P(None, None, "col"), P(None, "col", None), P(None, None, "row"),
        ),
        out_specs=(
            P("row", ("dp", "col")), P("row", ("dp", "col")),
            P(None, "row", None), P(None, None, "col"), P(None, "col", None), P(None, None, "row"),
            P(None, "row", None), P(None, None, "col"), P(None, "col", None), P(None, None, "row"),
        ),
        check_vma=False,
    )
```

```python
import functools

import jax
import jax.numpy as jnp
import numpy as np
from jax import lax
from jax.experimental import pallas as pl
from jax.experimental.pallas import tpu as pltpu
from jax.sharding import PartitionSpec as P

D = 768
HD = 64
WIN = 14
SLOTS = WIN * WIN
SIDE = 64
ADAPT = 8
NWIN = 5
IMG_TOK = NWIN * NWIN * SLOTS
RANK = 16
EDGE = SIDE - (NWIN - 1) * WIN
QUART = D // 4
FULLR = 208
KEYS = 208
EDGER = EDGE * WIN
CORNR = EDGE * EDGE
ROWS = 4 * FULLR + 2 * EDGER + CORNR
HALF = ROWS // 2
HBLK = QUART // 2
EPSILON = 1e-06
BF = jnp.bfloat16
F32 = jnp.float32
VMEM_LIMIT = 60 * 1024 * 1024

FULL, RIGHT, BOTTOM, CORNER = 0, 1, 2, 3
NQ = (FULLR, EDGER, EDGER, CORNR)
OFFS = (0, 4 * FULLR, 4 * FULLR + EDGER, 4 * FULLR + 2 * EDGER)


def slot_order(kind):
    rows = EDGE if kind in (BOTTOM, CORNER) else WIN
    cols = EDGE if kind in (RIGHT, CORNER) else WIN
    kept = [a * WIN + b for a in range(rows) for b in range(cols)]
    rest = [s for s in range(SLOTS) if s not in set(kept)]
    return kept, kept + rest


def build_tables():
    shift = np.zeros((4, FULLR, 128), np.int32)
    keys = np.zeros((4, KEYS, 128), np.float32)
    for kind in range(4):
        kept, order = slot_order(kind)
        for i, s in enumerate(kept):
            for base in (0, 64):
                shift[kind, i, base : base + 32] = WIN - 1 - s // WIN
                shift[kind, i, base + 32 : base + 64] = WIN - 1 - s % WIN
        spare = order[0] if kind == FULL else order[-1]
        for i, s in enumerate(order + [spare] * (KEYS - SLOTS)):
            for base in (0, 64):
                keys[kind, i, base + s // WIN] = 1.0
                keys[kind, i, base + 32 + s % WIN] = 1.0
    return shift, keys.astype(jnp.bfloat16)


SHIFT_NP, KEYS_NP = build_tables()


def nn(a, b):
    return jnp.dot(a, b, preferred_element_type=F32)


def nt(a, b):
    return lax.dot_general(a, b, (((1,), (1,)), ((), ())), preferred_element_type=F32)


def tn(a, b):
    return lax.dot_general(a, b, (((0,), (0,)), ((), ())), preferred_element_type=F32)


def vm():
    return pl.BlockSpec(memory_space=pltpu.VMEM)


def sm():
    return pl.BlockSpec(memory_space=pltpu.SMEM)


def params(**kw):
    return pltpu.CompilerParams(vmem_limit_bytes=VMEM_LIMIT, **kw)


def cost(us):
    return pl.CostEstimate(flops=int(us * 3e8), transcendentals=0, bytes_accessed=0)


def place_window(kind, count, moved, width, spare=-100000):
    row = lax.broadcasted_iota(jnp.int32, (count, width), 0)
    lane = lax.broadcasted_iota(jnp.int32, (count, width), 1)
    if kind in (RIGHT, CORNER):
        src = (row // EDGE) * WIN + row % EDGE
    else:
        src = jnp.where(row < SLOTS, row, spare)
    return (lane == src + moved).astype(F32).astype(BF)


def window_list(dest):
    items = [(FULL, FULLR * j, NWIN * dest + j) for j in range(4)]
    items.append((RIGHT, OFFS[1], NWIN * dest + 4))
    items.append((BOTTOM, OFFS[2], NWIN * 4 + dest))
    if dest == 3:
        items.append((CORNER, OFFS[3], NWIN * NWIN - 1))
    return items


def window_span(window):
    start = window * SLOTS
    low = start // 128 * 128
    high = min(-(-(start + SLOTS) // 128) * 128, IMG_TOK)
    return low, high, start - low


def pack_rows(mine, x_ref, rows_ref, spare):
    for dest in range(4):
        slot = jnp.bitwise_xor(mine, dest)
        if dest != 3:
            rows_ref[slot, OFFS[3] :, :] = jnp.zeros((CORNR, QUART), BF)
        for kind, offset, window in window_list(dest):
            low, high, moved = window_span(window)
            pick = place_window(kind, NQ[kind], moved, high - low, spare)
            rows_ref[slot, offset : offset + NQ[kind], :] = nt(pick, x_ref[:, low:high]).astype(BF)


def fold(rows_ref, outs):
    half = rows_ref.shape[1] // 2
    for slot, (out, base) in enumerate(((outs[0], 0), (outs[1], 0), (outs[2], 0), (outs[2], half))):
        out[base : base + half, :QUART] = rows_ref[slot, :half, :]
        out[base : base + half, QUART:] = rows_ref[slot, half:, :]


def pack_kernel(where_ref, x_ref, o0, o1, o2, rows_ref):
    pack_rows(where_ref[0], x_ref, rows_ref, -100000)
    fold(rows_ref, (o0, o1, o2))


def pieces_of(rows):
    piece = lambda n: jax.ShapeDtypeStruct((n, 2 * QUART), BF)
    return (piece(rows // 2), piece(rows // 2), piece(rows))


def pack(where, x):
    return pl.pallas_call(
        pack_kernel,
        out_shape=pieces_of(ROWS),
        in_specs=[sm(), vm()],
        out_specs=[vm()] * 3,
        scratch_shapes=[pltpu.VMEM((4, ROWS, QUART), BF)],
        compiler_params=params(),
        cost_estimate=cost(4),
        name="pack",
    )(where, x)


def front_kernel(
    where_ref, x_ref, qkv_w, proj_w, o0, o1, o2, alpha_ref, beta_ref, alpha_half, beta_half, rows_ref,
):
    heads = qkv_w.shape[1] // (3 * HD)
    for h in range(heads):
        for t in range(3):
            ref, base = (alpha_ref, QUART * t) if t < 2 else (beta_ref, 0)
            ref[:, base + HD * h : base + HD * (h + 1)] = qkv_w[:, HD * (3 * h + t) : HD * (3 * h + t + 1)]
    beta_ref[:, QUART:] = proj_w[...]
    rows = pl.ds(pl.multiple_of(where_ref[1] * HBLK, 32), HBLK)
    alpha_half[...] = alpha_ref[rows, :]
    beta_half[...] = beta_ref[rows, :]
    pack_rows(where_ref[0], x_ref, rows_ref, 0)
    fold(rows_ref, (o0, o1, o2))


def front(where, x, qkv_w, proj_w):
    s = lambda *shape: jax.ShapeDtypeStruct(shape, BF)
    return pl.pallas_call(
        front_kernel,
        out_shape=pieces_of(ROWS)
        + (s(QUART, 2 * QUART), s(QUART, 2 * QUART), s(HBLK, 2 * QUART), s(HBLK, 2 * QUART)),
        in_specs=[sm(), vm(), vm(), vm()],
        out_specs=[vm()] * 7,
        scratch_shapes=[pltpu.VMEM((4, ROWS, QUART), BF)],
        compiler_params=params(),
        cost_estimate=cost(5),
        name="token_and_weight_pack",
    )(where, x, qkv_w, proj_w)


def unpack_kernel(where_ref, *refs, bounds):
    pieces, (out_ref, acc_ref, rows_ref) = refs[:-3], refs[-3:]
    mine = where_ref[0]
    acc_ref[...] = jnp.zeros_like(acc_ref)
    index = 0
    for low, high in bounds:
        half = (high - low) // 2
        for slot in range(4):
            piece = pieces[index]
            rows = slice(half, 2 * half) if slot == 3 else slice(0, half)
            rows_ref[slot, low : low + half, :] = piece[rows, :QUART]
            rows_ref[slot, low + half : high, :] = piece[rows, QUART:]
            index += 1

    for source in range(4):
        slot = jnp.bitwise_xor(mine, source)
        for kind, offset, window in window_list(source):
            low, high, moved = window_span(window)
            pick = place_window(kind, NQ[kind], moved, high - low)
            acc_ref[:, low:high] += tn(rows_ref[slot, offset : offset + NQ[kind], :], pick)
    out_ref[...] = acc_ref[:, :IMG_TOK].astype(out_ref.dtype)


def unpack(where, pieces, dtype, bounds=((0, ROWS),)):
    return pl.pallas_call(
        functools.partial(unpack_kernel, bounds=bounds),
        out_shape=jax.ShapeDtypeStruct((QUART, IMG_TOK), dtype),
        in_specs=[sm()] + [vm()] * len(pieces),
        out_specs=vm(),
        scratch_shapes=[
            pltpu.VMEM((QUART, -(-IMG_TOK // 128) * 128), F32),
            pltpu.VMEM((4, ROWS, QUART), BF),
        ],
        compiler_params=params(),
        cost_estimate=cost(4),
        name="unpack",
    )(where, *pieces)


def join_pieces(pieces, dst_ref):
    for slot, piece in enumerate(pieces):
        rows = slice(HALF, ROWS) if slot == 3 else slice(0, HALF)
        dst_ref[:HALF, QUART * slot : QUART * (slot + 1)] = piece[rows, :QUART]
        dst_ref[HALF:, QUART * slot : QUART * (slot + 1)] = piece[rows, QUART:]


def split_pieces(src_ref, outs):
    half = src_ref.shape[0] // 2
    for slot, (out, base) in enumerate(((outs[0], 0), (outs[1], 0), (outs[2], 0), (outs[2], half))):
        out[base : base + half, :QUART] = src_ref[:half, QUART * slot : QUART * (slot + 1)]
        out[base : base + half, QUART:] = src_ref[half:, QUART * slot : QUART * (slot + 1)]


def adapter_pack_kernel(
    pick_ref, qkv_up, proj_dn, fc1_up, fc2_dn, qkv_dn, fc1_dn, proj_up, fc2_up, gain1, gain2,
    s0, s1, s2, s3, row_ref,
):
    heads = qkv_up.shape[2] // (3 * HD)
    half = 2 * QUART
    for j, send_ref in enumerate((s0, s1, s2, s3)):
        a = pick_ref[j]
        for h in range(heads):
            for t in range(3):
                row, base = (0, QUART * t) if t < 2 else (RANK, 0)
                send_ref[row : row + RANK, base + HD * h : base + HD * (h + 1)] = qkv_up[
                    a, :, HD * (3 * h + t) : HD * (3 * h + t + 1)
                ]
        send_ref[RANK : 2 * RANK, QUART:] = proj_dn[a]
        for i, ref in enumerate((fc1_up, fc2_dn)):
            for part in range(2):
                row = RANK * (2 + 2 * i + part)
                send_ref[row : row + RANK, :] = ref[a, :, half * part : half * (part + 1)]
    for i, ref in enumerate((qkv_dn, fc1_dn, proj_up, fc2_up)):
        row, base = RANK * (i // 2), QUART * (i % 2)
        row_ref[row : row + RANK, base : base + QUART] = ref[pick_ref[0]]
    for i, ref in enumerate((gain1, gain2)):
        row_ref[2 * RANK :, QUART * i : QUART * (i + 1)] = jnp.broadcast_to(ref[...], (RANK, QUART))


def adapter_pack(pick, *mats):
    s = lambda *shape: jax.ShapeDtypeStruct(shape, BF)
    return pl.pallas_call(
        adapter_pack_kernel,
        out_shape=(s(6 * RANK, 2 * QUART),) * 4 + (s(3 * RANK, 2 * QUART),),
        in_specs=[sm()] + [vm()] * 10,
        out_specs=[vm()] * 5,
        compiler_params=params(),
        cost_estimate=cost(2),
        name="adapter_pack",
    )(pick, *mats)


def alpha_block(k, j):
    part = k
    if j == 0:
        return [(part, 0, QUART, None)]
    return [
        (part, QUART + HBLK * (j - 1), HBLK, 0),
        (part, QUART + 3 * HBLK + HBLK * (j - 1), HBLK, 1),
    ]


def beta_block(k, j):
    core, cross = k % 2, k // 2
    base = 3 * core
    if j == 0 and not cross:
        return [(base, 0, QUART, None)]
    row = 0 if j == 0 else HBLK + QUART * (j - 1) + HBLK * cross
    return [(base + 1, row, HBLK, 0), (base + 2, row, HBLK, 1)]


def block_dst(start, flag, half):
    if flag is None:
        return start
    offset = half if flag == 0 else 1 - half
    return pl.multiple_of(start + offset * HBLK, 32)


def prep1_kernel(
    where_ref, p0, p1, p2, p3, q0, q1, q2, q3, q4, q5, a0, a1, a2, a3,
    wqkv_ref, wproj_ref, dqkv, uqkv, dproj, uproj, d1, u1, d2, u2, gain1, gain2,
):
    half = where_ref[1]
    for j, a in enumerate((a0, a1, a2, a3)):
        base = a.shape[0] - 6 * RANK
        part = lambda i: slice(base + RANK * i, base + RANK * (i + 1))
        for t in range(3):
            uqkv[:, D * t + QUART * j : D * t + QUART * (j + 1)] = a[
                part(t // 2), QUART * (t % 2) : QUART * (t % 2 + 1)
            ]
        dproj[:, QUART * j : QUART * (j + 1)] = a[part(1), QUART:]
        for i in range(2):
            u1[:, D * j + D // 2 * i : D * j + D // 2 * (i + 1)] = a[part(2 + i), :]
            d2[:, D * j + D // 2 * i : D * j + D // 2 * (i + 1)] = a[part(4 + i), :]
    for k, ref in enumerate((p0, p1, p2, p3)):
        for i, dst in enumerate((dqkv, d1, uproj, u2)):
            rows = slice(D + RANK * (i // 2), D + RANK * (i // 2 + 1))
            dst[:, QUART * k : QUART * (k + 1)] = ref[rows, QUART * (i % 2) : QUART * (i % 2 + 1)]
        for i, dst in enumerate((gain1, gain2)):
            row = D + 2 * RANK
            dst[:, QUART * k : QUART * (k + 1)] = ref[row : row + 1, QUART * i : QUART * (i + 1)].astype(F32)
    alpha, beta = (p0, p1, p2, p3), (q0, q1, q2, q3, q4, q5)
    for k in range(4):
        for j in range(4):
            for part, row, count, flag in alpha_block(k, j):
                rows = pl.ds(block_dst(QUART * k, flag, half), count)
                for t in range(2):
                    wqkv_ref[rows, D * t + QUART * j : D * t + QUART * (j + 1)] = alpha[part][
                        row : row + count, QUART * t : QUART * (t + 1)
                    ]
            for part, row, count, flag in beta_block(k, j):
                rows = pl.ds(block_dst(QUART * k, flag, half), count)
                wqkv_ref[rows, 2 * D + QUART * j : 2 * D + QUART * (j + 1)] = beta[part][
                    row : row + count, :QUART
                ]
                rows = pl.ds(block_dst(QUART * j, flag, half), count)
                wproj_ref[rows, QUART * k : QUART * (k + 1)] = beta[part][row : row + count, QUART:]
    for k in range(4):
        rows = slice(QUART * k, QUART * (k + 1))
        for t in range(3):
            cols = slice(D * t, D * (t + 1))
            low = tn(dqkv[:, rows], uqkv[:, cols])
            wqkv_ref[rows, cols] = (wqkv_ref[rows, cols].astype(F32) + low).astype(BF)
        low = tn(dproj[:, rows], uproj[...])
        wproj_ref[rows, :] = (wproj_ref[rows, :].astype(F32) + low).astype(BF)


def prep1(where, alpha, beta, cols):
    s = lambda *shape: jax.ShapeDtypeStruct(shape, BF)
    return pl.pallas_call(
        prep1_kernel,
        out_shape=(
            s(D, 3 * D), s(D, D), s(RANK, D), s(RANK, 3 * D), s(RANK, D), s(RANK, D),
            s(RANK, D), s(RANK, 4 * D), s(RANK, 4 * D), s(RANK, D),
            jax.ShapeDtypeStruct((1, D), F32), jax.ShapeDtypeStruct((1, D), F32),
        ),
        in_specs=[sm()] + [vm()] * 14,
        out_specs=[vm()] * 12,
        compiler_params=params(),
        cost_estimate=cost(7),
        name="attention_weights",
    )(where, *alpha, *beta, *cols)


def normalize(values):
    center = jnp.sum(values, axis=1, keepdims=True) / D
    shifted = values - center
    inv_std = lax.rsqrt(jnp.sum(shifted * shifted, axis=1, keepdims=True) / D + EPSILON)
    return shifted * inv_std, inv_std


def norm_back(grad, normed, inv_std):
    first = jnp.sum(grad, axis=1, keepdims=True) / D
    second = jnp.sum(grad * normed, axis=1, keepdims=True) / D
    return inv_std * (grad - first - normed * second)


def barrel(values, amount, left):
    for bit in (1, 2, 4, 8):
        moved = pltpu.roll(values, (128 - bit) if left else bit, 1)
        values = jnp.where((amount & bit) != 0, moved, values)
    return values


def low_half(count):
    return lax.broadcasted_iota(jnp.int32, (count, 128), 1) < HD


def pad_rows(tile):
    if tile.shape[0] == KEYS:
        return tile
    return jnp.concatenate([tile, jnp.zeros((KEYS - tile.shape[0], tile.shape[1]), tile.dtype)], axis=0)


def live_rows():
    return lax.broadcasted_iota(jnp.int32, (KEYS, 128), 0) < SLOTS


GROUP = 6
GROUP_BACK = 6


def pair_columns(pair):
    return tuple(slice(D * t + 128 * pair, D * t + 128 * (pair + 1)) for t in range(3))


def attend_window(kind, row0, qkv_ref, att_ref, exp_ref, inv_ref, rel_ref, shift_ref, keys_ref):
    count = NQ[kind]
    rows = pl.ds(row0, count)
    low_q, low_k = low_half(count), low_half(KEYS)
    live = live_rows()
    ones = jnp.where(live, 1.0, 0.0).astype(BF)
    amount = shift_ref[kind, :count, :]
    onehot = keys_ref[kind]
    rel_mat = rel_ref[...]
    for first in range(0, D // 128, GROUP):
        pairs = range(first, first + GROUP)
        heads = [(pair, odd) for pair in pairs for odd in range(2)]
        q_tile = {p: qkv_ref[rows, pair_columns(p)[0]] for p in pairs}
        rel = {p: nn(q_tile[p], rel_mat) for p in pairs}
        rel = {p: barrel(rel[p], amount, True).astype(BF) for p in pairs}
        k_tile = {p: pad_rows(qkv_ref[rows, pair_columns(p)[1]] * BF(HD**-0.5)) for p in pairs}
        scores = {}
        for p, odd in heads:
            if odd:
                q_aug, k_aug = jnp.where(low_q, rel[p], q_tile[p]), jnp.where(low_k, onehot, k_tile[p])
            else:
                q_aug, k_aug = jnp.where(low_q, q_tile[p], rel[p]), jnp.where(low_k, k_tile[p], onehot)
            scores[p, odd] = nt(q_aug, k_aug)
        top = {h: jnp.max(scores[h], axis=1, keepdims=True) for h in heads}
        exponent = {h: jnp.exp(scores[h] - top[h]).astype(BF) for h in heads}
        both = {}
        for p, odd in heads:
            exp_ref[2 * p + odd, rows, :] = exponent[p, odd]
            v_tile = pad_rows(qkv_ref[rows, pair_columns(p)[2]])
            if kind == FULL:
                v_tile = jnp.where(live, v_tile, 0).astype(BF)
            v_aug = jnp.where(low_k, ones, v_tile) if odd else jnp.where(low_k, v_tile, ones)
            both[p, odd] = nn(exponent[p, odd], v_aug)
        for p in pairs:
            cols = pair_columns(p)[0]
            inverse = 1.0 / pltpu.roll(jnp.where(low_q, both[p, 1], both[p, 0]), HD, 1)
            inv_ref[rows, cols] = inverse
            att_ref[rows, cols] = (jnp.where(low_q, both[p, 0], both[p, 1]) * inverse).astype(BF)


PARTS = ((FULL, FULL), (FULL, FULL), (RIGHT, BOTTOM, CORNER))
PART_ROWS = tuple(sum(NQ[kind] for kind in part) for part in PARTS)
PART_OFFS = (0, PART_ROWS[0], PART_ROWS[0] + PART_ROWS[1])


TAIL = ((0, 576), (576, ROWS))


def qkv_kernel(
    x0, x1, x2, x3, gain_ref, w_hbm, x_hbm, hid_hbm, qkv_a, qkv_b, qkv_c,
    x_ref, hid_ref, rows_ref, w_ref, qkv_ref, sem, out_sem,
):
    loads = [
        pltpu.make_async_copy(w_hbm.at[:, D * t : D * (t + 1)], w_ref.at[t], sem.at[t]) for t in range(3)
    ]
    for load in loads:
        load.start()
    join_pieces((x0, x1, x2, x3), x_ref)
    kept = [
        pltpu.make_async_copy(src, dst, sem.at[3 + i])
        for i, (src, dst) in enumerate(((x_ref, x_hbm), (hid_ref, hid_hbm)))
    ]
    kept[0].start()
    gain = gain_ref[...]

    def norm_step(i, carry):
        rows = pl.ds(pl.multiple_of(i * 112, 16), 112)
        normed, _ = normalize(x_ref[rows, :].astype(F32))
        hidden = (normed * gain).astype(BF)
        rows_ref[rows, :] = hidden
        hid_ref[rows, :] = hidden
        return carry

    lax.fori_loop(0, ROWS // 112, norm_step, 0)
    for w in range(4):
        hid_ref[FULLR * w + SLOTS : FULLR * (w + 1), :] = jnp.zeros((FULLR - SLOTS, D), BF)
    kept[1].start()
    for load in loads:
        load.wait()

    def stores(t):
        cols = pl.ds(pl.multiple_of(D * t, 128), D)
        return [
            pltpu.make_async_copy(
                qkv_ref.at[t, pl.ds(offset, count), :], out.at[:, cols], out_sem.at[t, i]
            )
            for i, (out, offset, count) in enumerate(zip((qkv_a, qkv_b, qkv_c), PART_OFFS, PART_ROWS))
        ]

    def project_step(t, carry):
        qkv_ref[t] = nn(rows_ref[...], w_ref[t]).astype(BF)
        for store in stores(t):
            store.start()
        return carry

    lax.fori_loop(0, 3, project_step, 0)
    for t in range(3):
        for store in stores(t):
            store.wait()
    for store in kept:
        store.wait()


def qkv_rows(pieces, gain, wqkv):
    s = lambda *shape: jax.ShapeDtypeStruct(shape, BF)
    hbm = pl.BlockSpec(memory_space=pl.ANY)
    return pl.pallas_call(
        qkv_kernel,
        out_shape=(s(ROWS, D), s(ROWS, D)) + tuple(s(n, 3 * D) for n in PART_ROWS),
        in_specs=[vm()] * 5 + [hbm],
        out_specs=[hbm] * 5,
        scratch_shapes=[
            pltpu.VMEM((ROWS, D), BF), pltpu.VMEM((ROWS, D), BF), pltpu.VMEM((ROWS, D), BF),
            pltpu.VMEM((3, D, D), BF), pltpu.VMEM((3, ROWS, D), BF),
            pltpu.SemaphoreType.DMA((5,)), pltpu.SemaphoreType.DMA((3, 3)),
        ],
        compiler_params=params(),
        cost_estimate=cost(10),
        name="norm_and_qkv",
    )(*pieces, gain, wqkv)


def attention_kernel(qkv_ref, rel_ref, shift_ref, keys_ref, att_ref, exp_ref, inv_ref, *, kinds):
    refs = (qkv_ref, att_ref, exp_ref, inv_ref, rel_ref, shift_ref, keys_ref)
    if kinds[0] == FULL:

        def step(w, carry):
            attend_window(FULL, pl.multiple_of(w * FULLR, 16), *refs)
            return carry

        lax.fori_loop(0, len(kinds), step, 0)
    else:
        row = 0
        for kind in kinds:
            attend_window(kind, row, *refs)
            row += NQ[kind]


def attention(part, qkv, rel, shift, keys):
    rows = PART_ROWS[part]
    s = lambda *shape, dtype=BF: jax.ShapeDtypeStruct(shape, dtype)
    return pl.pallas_call(
        functools.partial(attention_kernel, kinds=PARTS[part]),
        out_shape=(s(rows, D), s(D // HD, rows, KEYS), s(rows, D, dtype=F32)),
        in_specs=[vm()] * 4,
        out_specs=[vm()] * 3,
        compiler_params=params(),
        cost_estimate=cost(10),
        name="attention_forward",
    )(qkv, rel, shift, keys)


def project_kernel(x_ref, att_a, att_b, att_c, wproj_ref, middle_ref):
    for ref, offset, count in zip((att_a, att_b, att_c), PART_OFFS, PART_ROWS):
        rows = slice(offset, offset + count)
        middle_ref[rows, :] = x_ref[rows, :].astype(F32) + nn(ref[...], wproj_ref[...])


def project(x, atts, wproj):
    return pl.pallas_call(
        project_kernel,
        out_shape=jax.ShapeDtypeStruct((ROWS, D), F32),
        in_specs=[vm()] * 5,
        out_specs=vm(),
        compiler_params=params(),
        cost_estimate=cost(5),
        name="projection",
    )(x, *atts, wproj)


CHUNK = 512
LOCK = 1


def mlp_kernel(
    where_ref, middle_ref, g0, g1, g2, g3, gain_ref,
    p0, p1, p2, p3, q0, q1, q2, q3, q4, q5, s0, s1, s2, s3, s4, s5, d1, u1, d2, u2,
    o0, o1, o2, gmid_ref, down1, up1, down2, up2,
    gm_ref, out_rows, h2_ref, acc_mlp, acc_gh, gu1, ad2, w1_ref, w2_ref, sem,
):
    half = where_ref[1]
    copies = []

    def fetch(src, dst):
        copies.append(pltpu.make_async_copy(src, dst, sem.at[len(copies)]))
        copies[-1].start()

    alpha = (p0, p1, p2, p3)
    betas = ((q0, q1, q2, q3, q4, q5), (s0, s1, s2, s3, s4, s5))
    for k in range(4):
        for j in range(4):
            for part, row, count, flag in alpha_block(k, j):
                rows = pl.ds(block_dst(QUART * k, flag, half), count)
                fetch(alpha[part].at[row : row + count, :], w1_ref.at[rows, D * j : D * (j + 1)])
            for part, row, count, flag in beta_block(k, j):
                rows = pl.ds(block_dst(QUART * k, flag, half), count)
                for i, beta in enumerate(betas):
                    cols = slice(D * j + D // 2 * i, D * j + D // 2 * (i + 1))
                    fetch(beta[part].at[row : row + count, :], w2_ref.at[rows, cols])
    join_pieces((g0, g1, g2, g3), gm_ref)
    for copy in copies:
        copy.wait()
    for k in range(4):
        rows = slice(QUART * k, QUART * (k + 1))
        for j in range(4):
            cols = slice(D * j, D * (j + 1))
            low = tn(d1[:, rows], u1[:, cols])
            w1_ref[rows, cols] = (w1_ref[rows, cols].astype(F32) + low).astype(BF)
            low = tn(u2[:, rows], d2[:, cols])
            w2_ref[rows, cols] = (w2_ref[rows, cols].astype(F32) + low).astype(BF)
    gain = gain_ref[...]
    down1[...] = jnp.zeros_like(down1)
    up1[...] = jnp.zeros_like(up1)
    down2[...] = jnp.zeros_like(down2)
    up2[...] = jnp.zeros_like(up2)

    def tile_step(t, carry):
        rows = pl.ds(pl.multiple_of(t * HALF, 16), HALF)
        normed, _ = normalize(middle_ref[rows, :])
        h2 = (normed * gain).astype(BF)
        h2_ref[...] = h2
        gm = gm_ref[rows, :]
        ad1 = nt(d1[...], h2).astype(BF)
        gu2 = nt(u2[...], gm).astype(BF)
        acc_mlp[...] = jnp.zeros_like(acc_mlp)
        acc_gh[...] = jnp.zeros_like(acc_gh)
        gu1[...] = jnp.zeros_like(gu1)
        ad2[...] = jnp.zeros_like(ad2)

        def chunk_step(c, inner_carry):
            spans = [
                pl.ds(pl.multiple_of((c * LOCK + i) * CHUNK, CHUNK), CHUNK) for i in range(LOCK)
            ]
            h2 = h2_ref[...]
            gm = gm_ref[rows, :]
            inner = [nn(h2, w1_ref[:, span]) for span in spans]
            gact = [nn(gm, w2_ref[:, span]) for span in spans]
            act, ginner = [], []
            for i in range(LOCK):
                half = 0.5 * (1.0 + lax.erf(inner[i] * 2**-0.5))
                act.append((inner[i] * half).astype(BF))
                slope = half + inner[i] * (jnp.exp(-0.5 * inner[i] * inner[i]) * (2 * np.pi) ** -0.5)
                ginner.append((gact[i] * slope).astype(BF))
            for i, span in enumerate(spans):
                acc_mlp[...] += nt(act[i], w2_ref[:, span])
                acc_gh[...] += nt(ginner[i], w1_ref[:, span])
                up1[:, span] += nn(ad1, ginner[i])
                gu1[...] += nt(u1[:, span], ginner[i])
                ad2[...] += nt(d2[:, span], act[i])
                down2[:, span] += nn(gu2, act[i])
            return inner_carry

        lax.fori_loop(0, 4 * D // (CHUNK * LOCK), chunk_step, 0)
        down1[...] += nn(gu1[...].astype(BF), h2_ref[...])
        up2[...] += nn(ad2[...].astype(BF), gm_ref[rows, :])
        middle = middle_ref[rows, :]
        out_rows[rows, :] = (middle + acc_mlp[...]).astype(BF)
        normed, inv_std = normalize(middle)
        gmid_ref[rows, :] = gm_ref[rows, :].astype(F32) + norm_back(acc_gh[...] * gain, normed, inv_std)
        return carry

    lax.fori_loop(0, 2, tile_step, 0)
    split_pieces(out_rows, (o0, o1, o2))


def mlp(where, middle, pieces, gain, alpha, betas, d1, u1, d2, u2):
    s = lambda *shape, dtype=F32: jax.ShapeDtypeStruct(shape, dtype)
    return pl.pallas_call(
        mlp_kernel,
        out_shape=pieces_of(ROWS)
        + (s(ROWS, D), s(RANK, D), s(RANK, 4 * D), s(RANK, 4 * D), s(RANK, D)),
        in_specs=[sm()] + [vm()] * 6 + [pl.BlockSpec(memory_space=pl.ANY)] * 16 + [vm()] * 4,
        out_specs=[vm()] * 8,
        scratch_shapes=[
            pltpu.VMEM((ROWS, D), BF), pltpu.VMEM((ROWS, D), BF), pltpu.VMEM((HALF, D), BF),
            pltpu.VMEM((HALF, D), F32), pltpu.VMEM((HALF, D), F32),
            pltpu.VMEM((RANK, HALF), F32), pltpu.VMEM((RANK, HALF), F32),
            pltpu.VMEM((D, 4 * D), BF), pltpu.VMEM((D, 4 * D), BF),
            pltpu.SemaphoreType.DMA((4 * 4 * 6,)),
        ],
        compiler_params=params(),
        cost_estimate=cost(48),
        name="mlp_forward_backward",
    )(where, middle, *pieces, gain, *alpha, *betas[0], *betas[1], d1, u1, d2, u2)


def attend_back_window(
    kind, row0, qkv_ref, att_ref, exp_ref, inv_ref, gatt_ref, gqkv_ref, rel_ref, shift_ref, keys_ref
):
    count = NQ[kind]
    rows = pl.ds(row0, count)
    low_q, low_k = low_half(count), low_half(KEYS)
    live = live_rows()
    lane_k = lax.broadcasted_iota(jnp.int32, (KEYS, 128), 1) % HD
    lane_q = lax.broadcasted_iota(jnp.int32, (count, 128), 1) % HD
    ones = jnp.where(live & (lane_k < 2), 1.0, 0.0).astype(BF)
    across = jnp.where(
        low_half(128) != (lax.broadcasted_iota(jnp.int32, (128, 128), 0) < HD), -1.0, 0.0
    ).astype(BF)
    amount = shift_ref[kind, :count, :]
    onehot = keys_ref[kind]
    rel_mat = rel_ref[...]
    for first in range(0, D // 128, GROUP_BACK):
        pairs = range(first, first + GROUP_BACK)
        heads = [(pair, odd) for pair in pairs for odd in range(2)]
        go_tile = {
            p: (gatt_ref[rows, pair_columns(p)[0]].astype(F32) * inv_ref[rows, pair_columns(p)[0]]).astype(BF)
            for p in pairs
        }
        delta = {
            p: nn((go_tile[p].astype(F32) * att_ref[rows, pair_columns(p)[0]].astype(F32)).astype(BF), across)
            for p in pairs
        }
        go_t = {p: go_tile[p].T for p in pairs}
        gv = {}
        for p, odd in heads:
            gv[p, odd] = nn(go_t[p][HD * odd : HD * (odd + 1), :], exp_ref[2 * p + odd, rows, :])
        gscore = {}
        for p in pairs:
            high = delta[p].astype(BF)
            rest = (delta[p] - high.astype(F32)).astype(BF)
            low_delta = jnp.where(lane_q == 0, high, jnp.where(lane_q == 1, rest, 0)).astype(BF)
            v_tile = pad_rows(qkv_ref[rows, pair_columns(p)[2]])
            if kind == FULL:
                v_tile = jnp.where(live, v_tile, 0).astype(BF)
            gscore[p, 0] = nt(jnp.where(low_q, go_tile[p], low_delta), jnp.where(low_k, v_tile, ones))
            gscore[p, 1] = nt(jnp.where(low_q, low_delta, go_tile[p]), jnp.where(low_k, ones, v_tile))
        q_t = {p: qkv_ref[rows, pair_columns(p)[0]].T for p in pairs}
        gs = {(p, odd): (exp_ref[2 * p + odd, rows, :].astype(F32) * gscore[p, odd]).astype(BF) for p, odd in heads}
        gk = {(p, odd): nn(q_t[p][HD * odd : HD * (odd + 1), :], gs[p, odd]) for p, odd in heads}
        gq = {}
        for p in pairs:
            k_tile = pad_rows(qkv_ref[rows, pair_columns(p)[1]] * BF(HD**-0.5))
            gq[p, 0] = nn(gs[p, 0], jnp.where(low_k, k_tile, onehot))
            gq[p, 1] = nn(gs[p, 1], jnp.where(low_k, onehot, k_tile))
        sums = {p: barrel(jnp.where(low_q, gq[p, 1], gq[p, 0]), amount, False).astype(BF) for p in pairs}
        for p in pairs:
            cols, kcols, vcols = pair_columns(p)
            gv_tile = jnp.concatenate([gv[p, 0], gv[p, 1]], axis=0).astype(BF).T
            gqkv_ref[rows, vcols] = gv_tile[:count, :]
            gk_tile = (jnp.concatenate([gk[p, 0], gk[p, 1]], axis=0) * HD**-0.5).astype(BF).T
            gqkv_ref[rows, kcols] = gk_tile[:count, :]
            gqkv_ref[rows, cols] = (jnp.where(low_q, gq[p, 0], gq[p, 1]) + nt(sums[p], rel_mat)).astype(BF)


def attention_back_kernel(
    gmid_hbm, hid_hbm, qkv_a, qkv_b, qkv_c, att_a, att_b, att_c, exp_a, exp_b, exp_c, inv_a, inv_b, inv_c,
    wproj_ref, rel_ref, shift_ref, keys_ref, dqkv, uqkv, dproj, uproj,
    gqkv_hbm, down_q, up_q, down_p, up_p,
    gmid_ref, hid_ref, qkv_ref, att_ref, exp_ref, inv_ref, gqkv_ref, gb_ref, gatt_ref, sem, out_sem,
):
    spans = [pl.ds(offset, count) for offset, count in zip(PART_OFFS, PART_ROWS)]
    pairs = [(gmid_hbm, gmid_ref)]
    for part, srcs in enumerate(
        ((qkv_a, inv_a, att_a, exp_a), (qkv_b, inv_b, att_b, exp_b), (qkv_c, inv_c, att_c, exp_c))
    ):
        rows = spans[part]
        for src, dst in zip(srcs, (qkv_ref, inv_ref, att_ref)):
            pairs.append((src, dst.at[rows, :]))
        pairs.append((srcs[3], exp_ref.at[:, rows, :]))
    pairs.append((hid_hbm, hid_ref))
    loads = [pltpu.make_async_copy(src, dst, sem.at[i]) for i, (src, dst) in enumerate(pairs)]
    for load in loads:
        load.start()

    def wait_part(part):
        for load in loads[1 + 4 * part : 5 + 4 * part]:
            load.wait()

    stores = [
        pltpu.make_async_copy(gqkv_ref.at[rows, :], gqkv_hbm.at[rows, :], out_sem.at[i])
        for i, rows in enumerate(spans)
    ]
    loads[0].wait()
    gb_ref[...] = gmid_ref[...].astype(BF)
    gatt_ref[...] = nt(gb_ref[...], wproj_ref[...]).astype(BF)
    refs = (qkv_ref, att_ref, exp_ref, inv_ref, gatt_ref, gqkv_ref, rel_ref, shift_ref, keys_ref)

    def step(w, carry):
        for part in range(2):

            @pl.when(w == 2 * part)
            def _():
                wait_part(part)

        attend_back_window(FULL, pl.multiple_of(w * FULLR, 16), *refs)
        return carry

    lax.fori_loop(0, 4, step, 0)
    stores[0].start()
    stores[1].start()
    wait_part(2)
    for kind in (RIGHT, BOTTOM, CORNER):
        attend_back_window(kind, OFFS[kind], *refs)
    stores[2].start()
    up_p[...] = nn(nt(dproj[...], att_ref[...]).astype(BF), gb_ref[...])
    down_p[...] = nn(nt(uproj[...], gb_ref[...]).astype(BF), att_ref[...])
    loads[-1].wait()
    up_q[...] = nn(nt(dqkv[...], hid_ref[...]).astype(BF), gqkv_ref[...])
    down_q[...] = nn(nt(uqkv[...], gqkv_ref[...]).astype(BF), hid_ref[...])
    for store in stores:
        store.wait()


def attention_back(gmid, hid, qkvs, atts, exps, invs, wproj, rel, shift, keys, dqkv, uqkv, dproj, uproj):
    s = lambda *shape, dtype=F32: jax.ShapeDtypeStruct(shape, dtype)
    hbm = pl.BlockSpec(memory_space=pl.ANY)
    return pl.pallas_call(
        attention_back_kernel,
        out_shape=(s(ROWS, 3 * D, dtype=BF), s(RANK, D), s(RANK, 3 * D), s(RANK, D), s(RANK, D)),
        in_specs=[hbm] * 14 + [vm()] * 8,
        out_specs=[hbm] + [vm()] * 4,
        scratch_shapes=[
            pltpu.VMEM((ROWS, D), F32), pltpu.VMEM((ROWS, D), BF), pltpu.VMEM((ROWS, 3 * D), BF),
            pltpu.VMEM((ROWS, D), BF), pltpu.VMEM((D // HD, ROWS, KEYS), BF), pltpu.VMEM((ROWS, D), F32),
            pltpu.VMEM((ROWS, 3 * D), BF), pltpu.VMEM((ROWS, D), BF), pltpu.VMEM((ROWS, D), BF),
            pltpu.SemaphoreType.DMA((14,)), pltpu.SemaphoreType.DMA((3,)),
        ],
        compiler_params=params(),
        cost_estimate=cost(28),
        name="attention_backward",
    )(gmid, hid, *qkvs, *atts, *exps, *invs, wproj, rel, shift, keys, dqkv, uqkv, dproj, uproj)


def token_grad_kernel(gmid_hbm, x_hbm, gqkv_hbm, gain_ref, wqkv_ref, o0, o1, o2,
                      gmid_ref, x_ref, gqkv_ref, gh_ref, out_rows, sem, *, low, high):
    span = pl.ds(low, high - low)
    copies = [
        pltpu.make_async_copy(src.at[span, :], dst, sem.at[i])
        for i, (src, dst) in enumerate(((gqkv_hbm, gqkv_ref), (x_hbm, x_ref), (gmid_hbm, gmid_ref)))
    ]
    for copy in copies:
        copy.start()
    copies[0].wait()
    gh_ref[...] = nt(gqkv_ref[...], wqkv_ref[...])
    copies[1].wait()
    copies[2].wait()
    gain = gain_ref[...]
    step = (high - low) // 2

    def norm_step(i, carry):
        rows = pl.ds(pl.multiple_of(i * step, 16), step)
        normed, inv_std = normalize(x_ref[rows, :].astype(F32))
        back = norm_back(gh_ref[rows, :] * gain, normed, inv_std)
        out_rows[rows, :] = (gmid_ref[rows, :] + back).astype(BF)
        return carry

    lax.fori_loop(0, 2, norm_step, 0)
    split_pieces(out_rows, (o0, o1, o2))


def token_grad(gmid, x, gqkv, gain, wqkv, low, high):
    count = high - low
    hbm = pl.BlockSpec(memory_space=pl.ANY)
    return pl.pallas_call(
        functools.partial(token_grad_kernel, low=low, high=high),
        out_shape=pieces_of(count),
        in_specs=[hbm, hbm, hbm, vm(), vm()],
        out_specs=[vm()] * 3,
        scratch_shapes=[
            pltpu.VMEM((count, D), F32), pltpu.VMEM((count, D), BF), pltpu.VMEM((count, 3 * D), BF),
            pltpu.VMEM((count, D), F32), pltpu.VMEM((count, D), BF), pltpu.SemaphoreType.DMA((3,)),
        ],
        compiler_params=params(),
        cost_estimate=cost(8),
        name="token_gradient",
    )(gmid, x, gqkv, gain, wqkv)


def grad_pack_kernel(where_ref, down_q, up_q, down_p, up_p, down1, up1, down2, up2, o0, o1, o2, o3, buf_ref):
    mine = where_ref[0]
    for k in range(4):
        for i, ref in enumerate((down_q, down1, up_p, up2)):
            buf_ref[k, :RANK, QUART * i : QUART * (i + 1)] = ref[:, QUART * k : QUART * (k + 1)]
    for dest in range(4):
        k = jnp.bitwise_xor(mine, dest)
        ranks = slice(RANK // 4 * dest, RANK // 4 * (dest + 1))
        for j in range(4):
            base = RANK + 12 * j
            for t in range(3):
                buf_ref[k, base : base + 4, QUART * t : QUART * (t + 1)] = up_q[
                    ranks, D * t + QUART * j : D * t + QUART * (j + 1)
                ]
            buf_ref[k, base : base + 4, 3 * QUART :] = down_p[ranks, QUART * j : QUART * (j + 1)]
            buf_ref[k, base + 4 : base + 8, :] = up1[ranks, D * j : D * (j + 1)]
            buf_ref[k, base + 8 : base + 12, :] = down2[ranks, D * j : D * (j + 1)]
    for k, out in enumerate((o0, o1, o2, o3)):
        out[...] = buf_ref[k].astype(BF)


def grad_pack(where, *grads):
    return pl.pallas_call(
        grad_pack_kernel,
        out_shape=(jax.ShapeDtypeStruct((4 * RANK, D), BF),) * 4,
        in_specs=[sm()] + [vm()] * 8,
        out_specs=[vm()] * 4,
        scratch_shapes=[pltpu.VMEM((4, 4 * RANK, D), F32)],
        compiler_params=params(),
        cost_estimate=cost(2),
        name="adapter_grad_pack",
    )(where, *grads)


def grad_sum_kernel(g0, g1, g2, g3, o0, o1, o2, o3, buf_ref):
    total = g0[...].astype(F32) + g1[...].astype(F32) + g2[...].astype(F32) + g3[...].astype(F32)
    buf_ref[...] = jnp.zeros_like(buf_ref)
    buf_ref[:RANK, :] = total[:RANK, :]
    for j, out in enumerate((o0, o1, o2, o3)):
        buf_ref[RANK : RANK + 12, :] = total[RANK + 12 * j : RANK + 12 * (j + 1), :]
        out[...] = buf_ref[...].astype(BF)


def grad_sum(pieces):
    return pl.pallas_call(
        grad_sum_kernel,
        out_shape=(jax.ShapeDtypeStruct((2 * RANK, D), BF),) * 4,
        in_specs=[vm()] * 4,
        out_specs=[vm()] * 4,
        scratch_shapes=[pltpu.VMEM((2 * RANK, D), F32)],
        compiler_params=params(),
        cost_estimate=cost(2),
        name="adapter_grad_sum",
    )(*pieces)


def grad_adapters_kernel(index_ref, x_ref, qkv_dn, fc1_dn, proj_up, fc2_up, rest_ref, acc_ref):
    acc_ref[...] = jnp.zeros_like(acc_ref)

    def add(i, carry):
        acc_ref[index_ref[i]] += x_ref[i].astype(F32)
        return carry

    lax.fori_loop(0, x_ref.shape[0], add, 0)
    for i, ref in enumerate((qkv_dn, fc1_dn, proj_up, fc2_up)):
        ref[...] = acc_ref[:, :RANK, QUART * i : QUART * (i + 1)]
    rest_ref[...] = acc_ref[:, RANK:, :].astype(BF)


def grad_adapters(index, x):
    s = lambda n, dtype=F32: jax.ShapeDtypeStruct((ADAPT, RANK, n), dtype)
    return pl.pallas_call(
        grad_adapters_kernel,
        out_shape=(s(QUART), s(QUART), s(QUART), s(QUART), s(D, BF)),
        in_specs=[sm(), vm()],
        out_specs=[vm()] * 5,
        scratch_shapes=[pltpu.VMEM((ADAPT, 2 * RANK, D), F32)],
        compiler_params=params(),
        cost_estimate=cost(2),
        name="adapter_grad_by_adapter",
    )(index, x)


def grad_join_kernel(where_ref, r0, r1, r2, r3, qkv_up, proj_dn, fc1_up, fc2_dn, buf_ref):
    mine = where_ref[0]
    heads = qkv_up.shape[2] // (3 * HD)
    for k, ref in enumerate((r0, r1, r2, r3)):
        buf_ref[jnp.bitwise_xor(mine, k)] = ref[...].astype(F32)
    for source in range(4):
        ranks = slice(RANK // 4 * source, RANK // 4 * (source + 1))
        for h in range(heads):
            for t in range(3):
                qkv_up[:, ranks, HD * (3 * h + t) : HD * (3 * h + t + 1)] = buf_ref[
                    source, :, 0:4, QUART * t + HD * h : QUART * t + HD * (h + 1)
                ]
        proj_dn[:, ranks, :] = buf_ref[source, :, 0:4, 3 * QUART :]
        fc1_up[:, ranks, :] = buf_ref[source, :, 4:8, :]
        fc2_dn[:, ranks, :] = buf_ref[source, :, 8:12, :]


def grad_join(where, pieces):
    s = lambda n: jax.ShapeDtypeStruct((ADAPT, RANK, n), F32)
    return pl.pallas_call(
        grad_join_kernel,
        out_shape=(s(3 * QUART), s(QUART), s(D), s(D)),
        in_specs=[sm()] + [vm()] * 4,
        out_specs=[vm()] * 4,
        scratch_shapes=[pltpu.VMEM((4, ADAPT, RANK, D), F32)],
        compiler_params=params(),
        cost_estimate=cost(2),
        name="adapter_grad_join",
    )(where, *pieces)


def flip(values, axis, distance):
    size = lax.axis_size(axis)
    return lax.ppermute(values, axis, [(i, i ^ distance) for i in range(size)])


def send_rows(pieces):
    own, near, pair = pieces
    return [own, flip(near, "row", 1), flip(pair, "row", 2)]


def hand_on(pieces, *deps):
    own, near, crossed = pieces
    if deps:
        near, crossed = after((near, crossed), *deps)
    return [own, near, crossed, flip(crossed, "row", 1)]


def exchange(slots, axis):
    return [slots[0]] + [flip(slots[k], axis, k) for k in range(1, 4)]


def after(values, *deps):
    return lax.optimization_barrier((tuple(values), deps))[0]


def col_halves(half):
    return jnp.concatenate([flip(half, "col", j) for j in range(1, 4)], axis=0)


def col_pairs(half, other_row):
    two = jnp.concatenate([half, other_row], axis=0)
    return jnp.concatenate([other_row] + [flip(two, "col", j) for j in range(1, 4)], axis=0)


def rel_matrix(rel_h, rel_w):
    pad = jnp.zeros((32 - (2 * WIN - 1), HD), BF)
    block = jnp.concatenate([rel_h[::-1], pad, rel_w[::-1], pad], axis=0).T
    zero = jnp.zeros((HD, HD), BF)
    return jnp.concatenate(
        [jnp.concatenate([zero, block], axis=1), jnp.concatenate([block, zero], axis=1)], axis=0
    )


def body(
    tokens, grad_out, adapter_index, norm1_gain, norm2_gain, qkv_weight, proj_weight, fc1_weight, fc2_weight,
    rel_h, rel_w, qkv_down, qkv_up, proj_down, proj_up, fc1_down, fc1_up, fc2_down, fc2_up,
):
    members = lax.axis_size("col")
    batches = lax.axis_size("dp")
    row_index, col_index, dp_index = lax.axis_index("row"), lax.axis_index("col"), lax.axis_index("dp")
    half = dp_index % 2
    where = jnp.stack([row_index, half]).astype(jnp.int32)
    slot_images = (
        jnp.bitwise_xor(dp_index, jnp.arange(batches, dtype=jnp.int32))[:, None] * members
        + jnp.bitwise_xor(col_index, jnp.arange(members, dtype=jnp.int32))[None, :]
    ).reshape(-1)
    slot_adapters = jnp.sum(
        jnp.where(
            slot_images[:, None] == jnp.arange(adapter_index.shape[0], dtype=jnp.int32)[None, :],
            adapter_index[:, 0][None, :],
            0,
        ),
        axis=1,
    )
    pick = jnp.concatenate([slot_adapters[:4], half[None]]).astype(jnp.int32)
    swap = lambda m: jnp.swapaxes(m, 1, 2)

    rel = rel_matrix(rel_h, rel_w)
    shift, keys = jnp.asarray(SHIFT_NP), jnp.asarray(KEYS_NP)

    *token_slots, alpha_own, beta_own, alpha_half, beta_half = front(where, tokens, qkv_weight, proj_weight)
    cut = lambda m: lax.dynamic_slice_in_dim(m, half * HBLK, HBLK, 0)
    b0 = flip(beta_half, "row", 2)
    alpha_near = col_halves(alpha_half)
    x_pieces = send_rows(token_slots)
    *send, row_adapters = adapter_pack(
        pick, qkv_up, swap(proj_down), fc1_up, swap(fc2_down), swap(qkv_down), swap(fc1_down), proj_up, fc2_up,
        norm1_gain.reshape(1, -1), norm2_gain.reshape(1, -1),
    )
    beta_sent = [jnp.concatenate([beta_half, b0, send[j]], axis=0) for j in range(1, 4)]
    beta_got = [flip(m, "col", j) for j, m in enumerate(beta_sent, 1)]
    alpha_far = flip(alpha_near, "dp", 1)
    fc2_half, = after((cut(fc2_weight),), b0)
    c0 = flip(fc2_half, "row", 2)
    g = jnp.concatenate([alpha_own, alpha_near, alpha_far, row_adapters], axis=0)
    g, *x_pieces = after((g, *x_pieces), c0)
    gy = flip(g, "row", 2)
    grad_slots = pack(where, grad_out)
    *beta_got, _ = after((*beta_got, grad_slots[0]))
    beta_near = jnp.concatenate([b0] + [m[:QUART] for m in beta_got], axis=0)
    col_adapters = [send[0]] + beta_got
    beta_far = flip(beta_near, "dp", 1)
    x_pieces = hand_on(x_pieces)

    fc2_cols = [fc2_weight[:, : D // 2], fc2_weight[:, D // 2 :]]
    fc1_half, = after((cut(fc1_weight),), beta_near)
    fc1_near = [flip(fc1_half, "col", j) for j in range(1, 4)]

    alpha1 = [g, flip(g, "row", 1), gy, flip(gy, "row", 1)]
    beta1 = [beta_own, beta_near, beta_far] + [flip(m, "row", 1) for m in (beta_own, beta_near, beta_far)]
    grad_slots = after(tuple(grad_slots), gy)
    g_pieces = send_rows(grad_slots)
    two = jnp.concatenate([fc2_half, c0], axis=0)
    fc2_near = [[flip(two[:, D // 2 * i : D // 2 * (i + 1)], "col", j) for j in range(1, 4)] for i in range(2)]
    wqkv, wproj, dqkv, uqkv, dproj, uproj, d1, u1, d2, u2, gain1, gain2 = prep1(
        where, alpha1, beta1, col_adapters
    )
    wqkv, *fc1_near = after((wqkv, *fc1_near))
    fc1_near = jnp.concatenate(fc1_near, axis=0)
    fc1_far = flip(fc1_near, "dp", 1)
    x, hid, *qkvs = qkv_rows(x_pieces, gain1, wqkv)
    *qkvs, fc1_far, n1, n2, n3 = after((*qkvs, fc1_far, *fc2_near[0]), *g_pieces)
    g_pieces = hand_on(g_pieces, fc1_far)
    h = jnp.concatenate([fc1_weight, fc1_near, fc1_far], axis=0)
    hy = flip(h, "row", 2)
    fc2_near0 = jnp.concatenate([c0[:, : D // 2], n1, n2, n3], axis=0)
    fc2_far0 = flip(fc2_near0, "dp", 1)
    part0 = attention(0, qkvs[0], rel, shift, keys)
    qkv1, n1, n2, n3 = after((qkvs[1], *fc2_near[1]), part0[0])
    fc2_near1 = jnp.concatenate([c0[:, D // 2 :], n1, n2, n3], axis=0)
    fc2_near1, fc2_far0 = after((fc2_near1, fc2_far0))
    fc2_far1 = flip(fc2_near1, "dp", 1)
    part1 = attention(1, qkv1, rel, shift, keys)
    qkv2, _ = after((qkvs[2], fc2_far0), part1[0])
    part2 = attention(2, qkv2, rel, shift, keys)
    atts, exps, invs = zip(part0, part1, part2)
    atts = list(atts)
    atts[2], hy = after((atts[2], hy))
    alpha2 = [h, flip(h, "row", 1), hy, flip(hy, "row", 1)]
    middle = project(x, atts, wproj)
    middle, fc2_far1 = after((middle, fc2_far1))
    betas = [
        [own, near, far] + [flip(m, "row", 1) for m in (own, near, far)]
        for own, near, far in zip(fc2_cols, (fc2_near0, fc2_near1), (fc2_far0, fc2_far1))
    ]

    *out_slots, gmid, down1, up1, down2, up2 = mlp(where, middle, g_pieces, gain2, alpha2, betas, d1, u1, d2, u2)
    out_pieces = send_rows(out_slots)
    gqkv, down_q, up_q, down_p, up_p = attention_back(
        gmid, hid, qkvs, atts, exps, invs, wproj, rel, shift, keys, dqkv, uqkv, dproj, uproj
    )
    out_pieces = hand_on(out_pieces, gqkv)
    gqkv, down_q, up_q, down_p, up_p = after((gqkv, down_q, up_q, down_p, up_p), *out_pieces[:3])
    packed = grad_pack(where, down_q, up_q, down_p, up_p, down1, up1, down2, up2)
    *packed, gqkv = after((*packed, gqkv))
    row_sums = exchange(packed, "row")
    back0 = token_grad(gmid, x, gqkv, gain1, wqkv, *TAIL[0])
    *row_sums, gqkv, b0, b1, b2 = after((*row_sums, gqkv, *back0))
    back_pieces = send_rows((b0, b1, b2))
    summed = grad_sum(row_sums)
    *summed, gqkv = after((*summed, gqkv))
    images = exchange(summed, "col")
    back1 = token_grad(gmid, x, gqkv, gain1, wqkv, *TAIL[1])
    last_pieces = send_rows(back1)
    *images, near, crossed = after((*images, *back_pieces[1:]), back1[0])
    back_pieces = hand_on([back_pieces[0], near, crossed])
    images = jnp.stack(images)
    images, *out_pieces = after((images, *out_pieces))
    step = 1
    while step < batches:
        images = jnp.concatenate([images, flip(images, "dp", step)], axis=0)
        step *= 2
    result = unpack(where, out_pieces, BF)
    images, = after((images,), result)
    qkv_dn, fc1_dn, proj_upg, fc2_upg, rest = grad_adapters(slot_adapters.astype(jnp.int32), images)
    rests = [rest] + [flip(rest, "row", k) for k in range(1, 4)]
    grad_tokens = unpack(where, back_pieces + hand_on(last_pieces, rest), F32, TAIL)
    rests = after(tuple(rests), grad_tokens)
    qkv_upg, proj_dn, fc1_upg, fc2_dn = grad_join(where, rests)
    return (
        result, grad_tokens,
        swap(qkv_dn), qkv_upg, swap(proj_dn), proj_upg, swap(fc1_dn), fc1_upg, swap(fc2_dn), fc2_upg,
    )


def solution(mesh):
    return jax.shard_map(
        body,
        mesh=mesh,
        in_specs=(
            P("row", ("dp", "col")), P("row", ("dp", "col")), P(), P("row"), P("row"),
            P("row", "col"), P("col", "row"), P("row", "col"), P("row", "col"), P(), P(),
            P(None, "row", None), P(None, None, "col"), P(None, "col", None), P(None, None, "row"),
            P(None, "row", None), P(None, None, "col"), P(None, "col", None), P(None, None, "row"),
        ),
        out_specs=(
            P("row", ("dp", "col")), P("row", ("dp", "col")),
            P(None, "row", None), P(None, None, "col"), P(None, "col", None), P(None, None, "row"),
            P(None, "row", None), P(None, None, "col"), P(None, "col", None), P(None, None, "row"),
        ),
        check_vma=False,
    )
```

```python
import functools

import jax
import jax.numpy as jnp
import numpy as np
from jax import lax
from jax.experimental import pallas as pl
from jax.experimental.pallas import tpu as pltpu
from jax.sharding import PartitionSpec as P

D = 768
HD = 64
WIN = 14
SLOTS = WIN * WIN
SIDE = 64
ADAPT = 8
NWIN = 5
IMG_TOK = NWIN * NWIN * SLOTS
RANK = 16
EDGE = SIDE - (NWIN - 1) * WIN
QUART = D // 4
FULLR = 208
KEYS = 208
EDGER = EDGE * WIN
CORNR = EDGE * EDGE
ROWS = 4 * FULLR + 2 * EDGER + CORNR
HALF = ROWS // 2
HBLK = QUART // 2
EPSILON = 1e-06
BF = jnp.bfloat16
F32 = jnp.float32

FULL, RIGHT, BOTTOM, CORNER = 0, 1, 2, 3
NQ = (FULLR, EDGER, EDGER, CORNR)
OFFS = (0, 4 * FULLR, 4 * FULLR + EDGER, 4 * FULLR + 2 * EDGER)


def slot_order(kind):
    rows = EDGE if kind in (BOTTOM, CORNER) else WIN
    cols = EDGE if kind in (RIGHT, CORNER) else WIN
    kept = [a * WIN + b for a in range(rows) for b in range(cols)]
    rest = [s for s in range(SLOTS) if s not in set(kept)]
    return kept, kept + rest


def build_tables():
    shift = np.zeros((4, FULLR, 128), np.int32)
    keys = np.zeros((4, KEYS, 128), np.float32)
    for kind in range(4):
        kept, order = slot_order(kind)
        for i, s in enumerate(kept):
            for base in (0, 64):
                shift[kind, i, base : base + 32] = WIN - 1 - s // WIN
                shift[kind, i, base + 32 : base + 64] = WIN - 1 - s % WIN
        spare = order[0] if kind == FULL else order[-1]
        for i, s in enumerate(order + [spare] * (KEYS - SLOTS)):
            for base in (0, 64):
                keys[kind, i, base + s // WIN] = 1.0
                keys[kind, i, base + 32 + s % WIN] = 1.0
    return shift, keys.astype(jnp.bfloat16)


SHIFT_NP, KEYS_NP = build_tables()


def nn(a, b):
    return jnp.dot(a, b, preferred_element_type=F32)


def nt(a, b):
    return lax.dot_general(a, b, (((1,), (1,)), ((), ())), preferred_element_type=F32)


def tn(a, b):
    return lax.dot_general(a, b, (((0,), (0,)), ((), ())), preferred_element_type=F32)


def vm():
    return pl.BlockSpec(memory_space=pltpu.VMEM)


def sm():
    return pl.BlockSpec(memory_space=pltpu.SMEM)


def params(mib=60):
    return pltpu.CompilerParams(vmem_limit_bytes=mib * 1024 * 1024)


def cost(us):
    return pl.CostEstimate(flops=int(us * 3e8), transcendentals=0, bytes_accessed=0)


def place_window(kind, count, moved, width, spare=-100000):
    row = lax.broadcasted_iota(jnp.int32, (count, width), 0)
    lane = lax.broadcasted_iota(jnp.int32, (count, width), 1)
    if kind in (RIGHT, CORNER):
        src = (row // EDGE) * WIN + row % EDGE
    else:
        src = jnp.where(row < SLOTS, row, spare)
    return (lane == src + moved).astype(F32).astype(BF)


def window_list(dest):
    items = [(FULL, FULLR * j, NWIN * dest + j) for j in range(4)]
    items.append((RIGHT, OFFS[1], NWIN * dest + 4))
    items.append((BOTTOM, OFFS[2], NWIN * 4 + dest))
    if dest == 3:
        items.append((CORNER, OFFS[3], NWIN * NWIN - 1))
    return items


def window_span(window):
    start = window * SLOTS
    low = start // 128 * 128
    high = min(-(-(start + SLOTS) // 128) * 128, IMG_TOK)
    return low, high, start - low


def pack_rows(mine, x_ref, rows_ref, spare):
    for dest in range(4):
        slot = jnp.bitwise_xor(mine, dest)
        if dest != 3:
            rows_ref[slot, OFFS[3] :, :] = jnp.zeros((CORNR, QUART), BF)
        for kind, offset, window in window_list(dest):
            low, high, moved = window_span(window)
            pick = place_window(kind, NQ[kind], moved, high - low, spare)
            rows_ref[slot, offset : offset + NQ[kind], :] = nt(pick, x_ref[:, low:high]).astype(BF)


def fold(rows_ref, outs):
    half = rows_ref.shape[1] // 2
    for slot, (out, base) in enumerate(((outs[0], 0), (outs[1], 0), (outs[2], 0), (outs[2], half))):
        out[base : base + half, :QUART] = rows_ref[slot, :half, :]
        out[base : base + half, QUART:] = rows_ref[slot, half:, :]


def pack_kernel(where_ref, x_ref, o0, o1, o2, rows_ref):
    pack_rows(where_ref[0], x_ref, rows_ref, -100000)
    fold(rows_ref, (o0, o1, o2))


def pieces_of(rows):
    piece = lambda n: jax.ShapeDtypeStruct((n, 2 * QUART), BF)
    return (piece(rows // 2), piece(rows // 2), piece(rows))


def pack(where, x):
    return pl.pallas_call(
        pack_kernel,
        out_shape=pieces_of(ROWS),
        in_specs=[sm(), vm()],
        out_specs=[vm()] * 3,
        scratch_shapes=[pltpu.VMEM((4, ROWS, QUART), BF)],
        compiler_params=params(16),
        cost_estimate=cost(4),
        name="pack",
    )(where, x)


def front_kernel(
    where_ref, x_ref, qkv_w, proj_w, o0, o1, o2, alpha_ref, beta_ref, alpha_half, beta_half, rows_ref,
):
    heads = qkv_w.shape[1] // (3 * HD)
    for h in range(heads):
        for t in range(3):
            ref, base = (alpha_ref, QUART * t) if t < 2 else (beta_ref, 0)
            ref[:, base + HD * h : base + HD * (h + 1)] = qkv_w[:, HD * (3 * h + t) : HD * (3 * h + t + 1)]
    beta_ref[:, QUART:] = proj_w[...]
    rows = pl.ds(pl.multiple_of(where_ref[1] * HBLK, 32), HBLK)
    alpha_half[...] = alpha_ref[rows, :]
    beta_half[...] = beta_ref[rows, :]
    pack_rows(where_ref[0], x_ref, rows_ref, 0)
    fold(rows_ref, (o0, o1, o2))


def front(where, x, qkv_w, proj_w):
    s = lambda *shape: jax.ShapeDtypeStruct(shape, BF)
    return pl.pallas_call(
        front_kernel,
        out_shape=pieces_of(ROWS)
        + (s(QUART, 2 * QUART), s(QUART, 2 * QUART), s(HBLK, 2 * QUART), s(HBLK, 2 * QUART)),
        in_specs=[sm(), vm(), vm(), vm()],
        out_specs=[vm()] * 7,
        scratch_shapes=[pltpu.VMEM((4, ROWS, QUART), BF)],
        compiler_params=params(16),
        cost_estimate=cost(5),
        name="token_and_weight_pack",
    )(where, x, qkv_w, proj_w)


def unpack_kernel(where_ref, *refs, bounds):
    pieces, (out_ref, acc_ref, rows_ref) = refs[:-3], refs[-3:]
    mine = where_ref[0]
    acc_ref[...] = jnp.zeros_like(acc_ref)
    index = 0
    for low, high in bounds:
        half = (high - low) // 2
        for slot in range(4):
            piece = pieces[index]
            rows = slice(half, 2 * half) if slot == 3 else slice(0, half)
            rows_ref[slot, low : low + half, :] = piece[rows, :QUART]
            rows_ref[slot, low + half : high, :] = piece[rows, QUART:]
            index += 1

    for source in range(4):
        slot = jnp.bitwise_xor(mine, source)
        for kind, offset, window in window_list(source):
            low, high, moved = window_span(window)
            pick = place_window(kind, NQ[kind], moved, high - low)
            acc_ref[:, low:high] += tn(rows_ref[slot, offset : offset + NQ[kind], :], pick)
    out_ref[...] = acc_ref[:, :IMG_TOK].astype(out_ref.dtype)


def unpack(where, pieces, dtype, bounds=((0, ROWS),)):
    return pl.pallas_call(
        functools.partial(unpack_kernel, bounds=bounds),
        out_shape=jax.ShapeDtypeStruct((QUART, IMG_TOK), dtype),
        in_specs=[sm()] + [vm()] * len(pieces),
        out_specs=vm(),
        scratch_shapes=[
            pltpu.VMEM((QUART, -(-IMG_TOK // 128) * 128), F32),
            pltpu.VMEM((4, ROWS, QUART), BF),
        ],
        compiler_params=params(24),
        cost_estimate=cost(4),
        name="unpack",
    )(where, *pieces)


def join_pieces(pieces, dst_ref):
    for slot, piece in enumerate(pieces):
        rows = slice(HALF, ROWS) if slot == 3 else slice(0, HALF)
        dst_ref[:HALF, QUART * slot : QUART * (slot + 1)] = piece[rows, :QUART]
        dst_ref[HALF:, QUART * slot : QUART * (slot + 1)] = piece[rows, QUART:]


def split_pieces(src_ref, outs):
    half = src_ref.shape[0] // 2
    for slot, (out, base) in enumerate(((outs[0], 0), (outs[1], 0), (outs[2], 0), (outs[2], half))):
        out[base : base + half, :QUART] = src_ref[:half, QUART * slot : QUART * (slot + 1)]
        out[base : base + half, QUART:] = src_ref[half:, QUART * slot : QUART * (slot + 1)]


def adapter_pack_kernel(
    pick_ref, qkv_up, proj_dn, fc1_up, fc2_dn, qkv_dn, fc1_dn, proj_up, fc2_up, gain1, gain2,
    s0, s1, s2, s3, row_ref,
):
    heads = qkv_up.shape[2] // (3 * HD)
    half = 2 * QUART
    for j, send_ref in enumerate((s0, s1, s2, s3)):
        a = pick_ref[j]
        for h in range(heads):
            for t in range(3):
                row, base = (0, QUART * t) if t < 2 else (RANK, 0)
                send_ref[row : row + RANK, base + HD * h : base + HD * (h + 1)] = qkv_up[
                    a, :, HD * (3 * h + t) : HD * (3 * h + t + 1)
                ]
        send_ref[RANK : 2 * RANK, QUART:] = proj_dn[a]
        for i, ref in enumerate((fc1_up, fc2_dn)):
            for part in range(2):
                row = RANK * (2 + 2 * i + part)
                send_ref[row : row + RANK, :] = ref[a, :, half * part : half * (part + 1)]
    for i, ref in enumerate((qkv_dn, fc1_dn, proj_up, fc2_up)):
        row, base = RANK * (i // 2), QUART * (i % 2)
        row_ref[row : row + RANK, base : base + QUART] = ref[pick_ref[0]]
    for i, ref in enumerate((gain1, gain2)):
        row_ref[2 * RANK :, QUART * i : QUART * (i + 1)] = jnp.broadcast_to(ref[...], (RANK, QUART))


def adapter_pack(pick, *mats):
    s = lambda *shape: jax.ShapeDtypeStruct(shape, BF)
    return pl.pallas_call(
        adapter_pack_kernel,
        out_shape=(s(6 * RANK, 2 * QUART),) * 4 + (s(3 * RANK, 2 * QUART),),
        in_specs=[sm()] + [vm()] * 10,
        out_specs=[vm()] * 5,
        compiler_params=params(8),
        cost_estimate=cost(2),
        name="adapter_pack",
    )(pick, *mats)


def alpha_block(k, j):
    part = k
    if j == 0:
        return [(part, 0, QUART, None)]
    return [
        (part, QUART + HBLK * (j - 1), HBLK, 0),
        (part, QUART + 3 * HBLK + HBLK * (j - 1), HBLK, 1),
    ]


def beta_block(k, j):
    core, cross = k % 2, k // 2
    base = 3 * core
    if j == 0 and not cross:
        return [(base, 0, QUART, None)]
    row = 0 if j == 0 else HBLK + QUART * (j - 1) + HBLK * cross
    return [(base + 1, row, HBLK, 0), (base + 2, row, HBLK, 1)]


def block_dst(start, flag, half):
    if flag is None:
        return start
    offset = half if flag == 0 else 1 - half
    return pl.multiple_of(start + offset * HBLK, 32)


def prep1_kernel(
    where_ref, p0, p1, p2, p3, q0, q1, q2, q3, q4, q5, a0, a1, a2, a3,
    wqkv_ref, wproj_ref, dqkv, uqkv, dproj, uproj, d1, u1, d2, u2, gain1, gain2, ups, downs,
):
    half = where_ref[1]
    for j, a in enumerate((a0, a1, a2, a3)):
        base = a.shape[0] - 6 * RANK
        part = lambda i: slice(base + RANK * i, base + RANK * (i + 1))
        for t in range(3):
            uqkv[:, D * t + QUART * j : D * t + QUART * (j + 1)] = a[
                part(t // 2), QUART * (t % 2) : QUART * (t % 2 + 1)
            ]
        dproj[:, QUART * j : QUART * (j + 1)] = a[part(1), QUART:]
        for i in range(2):
            u1[:, D * j + D // 2 * i : D * j + D // 2 * (i + 1)] = a[part(2 + i), :]
            d2[:, D * j + D // 2 * i : D * j + D // 2 * (i + 1)] = a[part(4 + i), :]
    for k, ref in enumerate((p0, p1, p2, p3)):
        for i, dst in enumerate((dqkv, d1, uproj, u2)):
            rows = slice(D + RANK * (i // 2), D + RANK * (i // 2 + 1))
            dst[:, QUART * k : QUART * (k + 1)] = ref[rows, QUART * (i % 2) : QUART * (i % 2 + 1)]
        for i, dst in enumerate((gain1, gain2)):
            row = D + 2 * RANK
            dst[:, QUART * k : QUART * (k + 1)] = ref[row : row + 1, QUART * i : QUART * (i + 1)].astype(F32)
    alpha, beta = (p0, p1, p2, p3), (q0, q1, q2, q3, q4, q5)
    for k in range(4):
        for j in range(4):
            for part, row, count, flag in alpha_block(k, j):
                rows = pl.ds(block_dst(QUART * k, flag, half), count)
                for t in range(2):
                    wqkv_ref[rows, D * t + QUART * j : D * t + QUART * (j + 1)] = alpha[part][
                        row : row + count, QUART * t : QUART * (t + 1)
                    ]
            for part, row, count, flag in beta_block(k, j):
                rows = pl.ds(block_dst(QUART * k, flag, half), count)
                wqkv_ref[rows, 2 * D + QUART * j : 2 * D + QUART * (j + 1)] = beta[part][
                    row : row + count, :QUART
                ]
                rows = pl.ds(block_dst(QUART * j, flag, half), count)
                wproj_ref[rows, QUART * k : QUART * (k + 1)] = beta[part][row : row + count, QUART:]
    for t in range(3):
        ups[t] = uqkv[:, D * t : D * (t + 1)]
    ups[3] = uproj[...]
    for k in range(4):
        downs[k] = dqkv[:, QUART * k : QUART * (k + 1)]
        downs[4 + k] = dproj[:, QUART * k : QUART * (k + 1)]

    def merge(t, carry):
        cols = pl.ds(pl.multiple_of(D * t, 128), D)
        for k in range(4):
            rows = slice(QUART * k, QUART * (k + 1))
            wqkv_ref[rows, cols] = (wqkv_ref[rows, cols].astype(F32) + tn(downs[k], ups[t])).astype(BF)
        return carry

    lax.fori_loop(0, 3, merge, 0)
    for k in range(4):
        rows = slice(QUART * k, QUART * (k + 1))
        wproj_ref[rows, :] = (wproj_ref[rows, :].astype(F32) + tn(downs[4 + k], ups[3])).astype(BF)


def prep1(where, alpha, beta, cols):
    s = lambda *shape: jax.ShapeDtypeStruct(shape, BF)
    return pl.pallas_call(
        prep1_kernel,
        out_shape=(
            s(D, 3 * D), s(D, D), s(RANK, D), s(RANK, 3 * D), s(RANK, D), s(RANK, D),
            s(RANK, D), s(RANK, 4 * D), s(RANK, 4 * D), s(RANK, D),
            jax.ShapeDtypeStruct((1, D), F32), jax.ShapeDtypeStruct((1, D), F32),
        ),
        in_specs=[sm()] + [vm()] * 14,
        out_specs=[vm()] * 12,
        scratch_shapes=[pltpu.VMEM((4, RANK, D), BF), pltpu.VMEM((8, RANK, QUART), BF)],
        compiler_params=params(24),
        cost_estimate=cost(7),
        name="attention_weights",
    )(where, *alpha, *beta, *cols)


def normalize(values):
    center = jnp.sum(values, axis=1, keepdims=True) / D
    shifted = values - center
    inv_std = lax.rsqrt(jnp.sum(shifted * shifted, axis=1, keepdims=True) / D + EPSILON)
    return shifted * inv_std, inv_std


def norm_back(grad, normed, inv_std):
    first = jnp.sum(grad, axis=1, keepdims=True) / D
    second = jnp.sum(grad * normed, axis=1, keepdims=True) / D
    return inv_std * (grad - first - normed * second)


def barrel(values, amount, left):
    for bit in (1, 2, 4, 8):
        moved = pltpu.roll(values, (128 - bit) if left else bit, 1)
        values = jnp.where((amount & bit) != 0, moved, values)
    return values


def low_half(count):
    return lax.broadcasted_iota(jnp.int32, (count, 128), 1) < HD


def pad_rows(tile):
    if tile.shape[0] == KEYS:
        return tile
    return jnp.concatenate([tile, jnp.zeros((KEYS - tile.shape[0], tile.shape[1]), tile.dtype)], axis=0)


def live_rows():
    return lax.broadcasted_iota(jnp.int32, (KEYS, 128), 0) < SLOTS


GROUP = 6
GROUP_BACK = 6


def pair_columns(pair):
    return tuple(slice(D * t + 128 * pair, D * t + 128 * (pair + 1)) for t in range(3))


def attend_window(kind, row0, qkv_ref, att_ref, exp_ref, inv_ref, rel_ref, shift_ref, keys_ref):
    count = NQ[kind]
    rows = pl.ds(row0, count)
    low_q, low_k = low_half(count), low_half(KEYS)
    live = live_rows()
    ones = jnp.where(live, 1.0, 0.0).astype(BF)
    amount = shift_ref[kind, :count, :]
    onehot = keys_ref[kind]
    rel_mat = rel_ref[...]
    for first in range(0, D // 128, GROUP):
        pairs = range(first, first + GROUP)
        heads = [(pair, odd) for pair in pairs for odd in range(2)]
        q_tile = {p: qkv_ref[rows, pair_columns(p)[0]] for p in pairs}
        rel = {p: nn(q_tile[p], rel_mat) for p in pairs}
        rel = {p: barrel(rel[p], amount, True).astype(BF) for p in pairs}
        k_tile = {p: pad_rows(qkv_ref[rows, pair_columns(p)[1]] * BF(HD**-0.5)) for p in pairs}
        scores = {}
        for p, odd in heads:
            if odd:
                q_aug, k_aug = jnp.where(low_q, rel[p], q_tile[p]), jnp.where(low_k, onehot, k_tile[p])
            else:
                q_aug, k_aug = jnp.where(low_q, q_tile[p], rel[p]), jnp.where(low_k, k_tile[p], onehot)
            scores[p, odd] = nt(q_aug, k_aug)
        top = {h: jnp.max(scores[h], axis=1, keepdims=True) for h in heads}
        exponent = {h: jnp.exp(scores[h] - top[h]).astype(BF) for h in heads}
        both = {}
        for p, odd in heads:
            exp_ref[2 * p + odd, rows, :] = exponent[p, odd]
            v_tile = pad_rows(qkv_ref[rows, pair_columns(p)[2]])
            if kind == FULL:
                v_tile = jnp.where(live, v_tile, 0).astype(BF)
            v_aug = jnp.where(low_k, ones, v_tile) if odd else jnp.where(low_k, v_tile, ones)
            both[p, odd] = nn(exponent[p, odd], v_aug)
        for p in pairs:
            cols = pair_columns(p)[0]
            inverse = 1.0 / pltpu.roll(jnp.where(low_q, both[p, 1], both[p, 0]), HD, 1)
            inv_ref[rows, cols] = inverse
            att_ref[rows, cols] = (jnp.where(low_q, both[p, 0], both[p, 1]) * inverse).astype(BF)


PARTS = ((FULL, FULL), (FULL, FULL), (RIGHT, BOTTOM, CORNER))
PART_ROWS = tuple(sum(NQ[kind] for kind in part) for part in PARTS)
PART_OFFS = (0, PART_ROWS[0], PART_ROWS[0] + PART_ROWS[1])


TAIL = ((0, 576), (576, ROWS))


def qkv_kernel(
    x0, x1, x2, x3, gain_ref, w_hbm, x_hbm, hid_hbm, qkv_a, qkv_b, qkv_c,
    x_ref, hid_ref, rows_ref, w_ref, qkv_ref, sem, out_sem,
):
    loads = [
        pltpu.make_async_copy(w_hbm.at[:, D * t : D * (t + 1)], w_ref.at[t], sem.at[t]) for t in range(3)
    ]
    for load in loads:
        load.start()
    join_pieces((x0, x1, x2, x3), x_ref)
    kept = [
        pltpu.make_async_copy(src, dst, sem.at[3 + i])
        for i, (src, dst) in enumerate(((x_ref, x_hbm), (hid_ref, hid_hbm)))
    ]
    kept[0].start()
    gain = gain_ref[...]

    def norm_step(i, carry):
        rows = pl.ds(pl.multiple_of(i * 112, 16), 112)
        normed, _ = normalize(x_ref[rows, :].astype(F32))
        hidden = (normed * gain).astype(BF)
        rows_ref[rows, :] = hidden
        hid_ref[rows, :] = hidden
        return carry

    lax.fori_loop(0, ROWS // 112, norm_step, 0)
    for w in range(4):
        hid_ref[FULLR * w + SLOTS : FULLR * (w + 1), :] = jnp.zeros((FULLR - SLOTS, D), BF)
    kept[1].start()
    for load in loads:
        load.wait()

    def stores(t):
        cols = pl.ds(pl.multiple_of(D * t, 128), D)
        return [
            pltpu.make_async_copy(
                qkv_ref.at[t, pl.ds(offset, count), :], out.at[:, cols], out_sem.at[t, i]
            )
            for i, (out, offset, count) in enumerate(zip((qkv_a, qkv_b, qkv_c), PART_OFFS, PART_ROWS))
        ]

    def project_step(t, carry):
        qkv_ref[t] = nn(rows_ref[...], w_ref[t]).astype(BF)
        for store in stores(t):
            store.start()
        return carry

    lax.fori_loop(0, 3, project_step, 0)
    for t in range(3):
        for store in stores(t):
            store.wait()
    for store in kept:
        store.wait()


def qkv_rows(pieces, gain, wqkv):
    s = lambda *shape: jax.ShapeDtypeStruct(shape, BF)
    hbm = pl.BlockSpec(memory_space=pl.ANY)
    return pl.pallas_call(
        qkv_kernel,
        out_shape=(s(ROWS, D), s(ROWS, D)) + tuple(s(n, 3 * D) for n in PART_ROWS),
        in_specs=[vm()] * 5 + [hbm],
        out_specs=[hbm] * 5,
        scratch_shapes=[
            pltpu.VMEM((ROWS, D), BF), pltpu.VMEM((ROWS, D), BF), pltpu.VMEM((ROWS, D), BF),
            pltpu.VMEM((3, D, D), BF), pltpu.VMEM((3, ROWS, D), BF),
            pltpu.SemaphoreType.DMA((5,)), pltpu.SemaphoreType.DMA((3, 3)),
        ],
        compiler_params=params(32),
        cost_estimate=cost(10),
        name="norm_and_qkv",
    )(*pieces, gain, wqkv)


def attention_kernel(qkv_ref, rel_ref, shift_ref, keys_ref, att_ref, exp_ref, inv_ref, *, kinds):
    refs = (qkv_ref, att_ref, exp_ref, inv_ref, rel_ref, shift_ref, keys_ref)
    if kinds[0] == FULL:

        def step(w, carry):
            attend_window(FULL, pl.multiple_of(w * FULLR, 16), *refs)
            return carry

        lax.fori_loop(0, len(kinds), step, 0)
    else:
        row = 0
        for kind in kinds:
            attend_window(kind, row, *refs)
            row += NQ[kind]


def attention(part, qkv, rel, shift, keys):
    rows = PART_ROWS[part]
    s = lambda *shape, dtype=BF: jax.ShapeDtypeStruct(shape, dtype)
    return pl.pallas_call(
        functools.partial(attention_kernel, kinds=PARTS[part]),
        out_shape=(s(rows, D), s(D // HD, rows, KEYS), s(rows, D, dtype=F32)),
        in_specs=[vm()] * 4,
        out_specs=[vm()] * 3,
        compiler_params=params(24),
        cost_estimate=cost(10),
        name="attention_forward",
    )(qkv, rel, shift, keys)


def project_kernel(x_ref, att_a, att_b, att_c, wproj_ref, middle_ref):
    for ref, offset, count in zip((att_a, att_b, att_c), PART_OFFS, PART_ROWS):
        rows = slice(offset, offset + count)
        middle_ref[rows, :] = x_ref[rows, :].astype(F32) + nn(ref[...], wproj_ref[...])


def project(x, atts, wproj):
    return pl.pallas_call(
        project_kernel,
        out_shape=jax.ShapeDtypeStruct((ROWS, D), F32),
        in_specs=[vm()] * 5,
        out_specs=vm(),
        compiler_params=params(20),
        cost_estimate=cost(5),
        name="projection",
    )(x, *atts, wproj)


CHUNK = 512
LOCK = 1


def mlp_kernel(
    where_ref, middle_ref, g0, g1, g2, g3, gain_ref,
    p0, p1, p2, p3, q0, q1, q2, q3, q4, q5, d1, u1, d2, u2,
    o0, o1, o2, gmid_ref, down1, up1, down2, up2,
    gm_ref, out_rows, h2_ref, acc_mlp, acc_gh, gu1, ad2, w1_ref, w2_ref, downs, sem,
):
    half = where_ref[1]
    copies = []

    def fetch(src, dst):
        copies.append(pltpu.make_async_copy(src, dst, sem.at[len(copies)]))
        copies[-1].start()

    alpha, beta = (p0, p1, p2, p3), (q0, q1, q2, q3, q4, q5)
    for k in range(4):
        for j in range(4):
            for part, row, count, flag in alpha_block(k, j):
                rows = pl.ds(block_dst(QUART * k, flag, half), count)
                fetch(alpha[part].at[row : row + count, :], w1_ref.at[rows, D * j : D * (j + 1)])
            for part, row, count, flag in beta_block(k, j):
                rows = pl.ds(block_dst(QUART * k, flag, half), count)
                fetch(beta[part].at[row : row + count, :], w2_ref.at[rows, D * j : D * (j + 1)])
    join_pieces((g0, g1, g2, g3), gm_ref)
    for k in range(4):
        downs[k] = d1[:, QUART * k : QUART * (k + 1)]
        downs[4 + k] = u2[:, QUART * k : QUART * (k + 1)]
    for copy in copies:
        copy.wait()

    def merge(j, carry):
        cols = pl.ds(pl.multiple_of(D * j, 128), D)
        for k in range(4):
            rows = slice(QUART * k, QUART * (k + 1))
            w1_ref[rows, cols] = (w1_ref[rows, cols].astype(F32) + tn(downs[k], u1[:, cols])).astype(BF)
            w2_ref[rows, cols] = (w2_ref[rows, cols].astype(F32) + tn(downs[4 + k], d2[:, cols])).astype(BF)
        return carry

    lax.fori_loop(0, 4, merge, 0)
    gain = gain_ref[...]
    down1[...] = jnp.zeros_like(down1)
    up1[...] = jnp.zeros_like(up1)
    down2[...] = jnp.zeros_like(down2)
    up2[...] = jnp.zeros_like(up2)

    def tile_step(t, carry):
        rows = pl.ds(pl.multiple_of(t * HALF, 16), HALF)
        normed, _ = normalize(middle_ref[rows, :])
        h2 = (normed * gain).astype(BF)
        h2_ref[...] = h2
        gm = gm_ref[rows, :]
        ad1 = nt(d1[...], h2).astype(BF)
        gu2 = nt(u2[...], gm).astype(BF)
        acc_mlp[...] = jnp.zeros_like(acc_mlp)
        acc_gh[...] = jnp.zeros_like(acc_gh)
        gu1[...] = jnp.zeros_like(gu1)
        ad2[...] = jnp.zeros_like(ad2)

        def chunk_step(c, inner_carry):
            spans = [
                pl.ds(pl.multiple_of((c * LOCK + i) * CHUNK, CHUNK), CHUNK) for i in range(LOCK)
            ]
            h2 = h2_ref[...]
            gm = gm_ref[rows, :]
            inner = [nn(h2, w1_ref[:, span]) for span in spans]
            gact = [nn(gm, w2_ref[:, span]) for span in spans]
            act, ginner = [], []
            for i in range(LOCK):
                half = 0.5 * (1.0 + lax.erf(inner[i] * 2**-0.5))
                act.append((inner[i] * half).astype(BF))
                slope = half + inner[i] * (jnp.exp(-0.5 * inner[i] * inner[i]) * (2 * np.pi) ** -0.5)
                ginner.append((gact[i] * slope).astype(BF))
            for i, span in enumerate(spans):
                acc_mlp[...] += nt(act[i], w2_ref[:, span])
                acc_gh[...] += nt(ginner[i], w1_ref[:, span])
                up1[:, span] += nn(ad1, ginner[i])
                gu1[...] += nt(u1[:, span], ginner[i])
                ad2[...] += nt(d2[:, span], act[i])
                down2[:, span] += nn(gu2, act[i])
            return inner_carry

        lax.fori_loop(0, 4 * D // (CHUNK * LOCK), chunk_step, 0)
        down1[...] += nn(gu1[...].astype(BF), h2_ref[...])
        up2[...] += nn(ad2[...].astype(BF), gm_ref[rows, :])
        middle = middle_ref[rows, :]
        out_rows[rows, :] = (middle + acc_mlp[...]).astype(BF)
        normed, inv_std = normalize(middle)
        gmid_ref[rows, :] = gm_ref[rows, :].astype(F32) + norm_back(acc_gh[...] * gain, normed, inv_std)
        return carry

    lax.fori_loop(0, 2, tile_step, 0)
    split_pieces(out_rows, (o0, o1, o2))


def mlp(where, middle, pieces, gain, alpha, beta, d1, u1, d2, u2):
    s = lambda *shape, dtype=F32: jax.ShapeDtypeStruct(shape, dtype)
    return pl.pallas_call(
        mlp_kernel,
        out_shape=pieces_of(ROWS)
        + (s(ROWS, D), s(RANK, D), s(RANK, 4 * D), s(RANK, 4 * D), s(RANK, D)),
        in_specs=[sm()] + [vm()] * 6 + [pl.BlockSpec(memory_space=pl.ANY)] * 10 + [vm()] * 4,
        out_specs=[vm()] * 8,
        scratch_shapes=[
            pltpu.VMEM((ROWS, D), BF), pltpu.VMEM((ROWS, D), BF), pltpu.VMEM((HALF, D), BF),
            pltpu.VMEM((HALF, D), F32), pltpu.VMEM((HALF, D), F32),
            pltpu.VMEM((RANK, HALF), F32), pltpu.VMEM((RANK, HALF), F32),
            pltpu.VMEM((D, 4 * D), BF), pltpu.VMEM((D, 4 * D), BF), pltpu.VMEM((8, RANK, QUART), BF),
            pltpu.SemaphoreType.DMA((4 * 4 * 4,)),
        ],
        compiler_params=params(48),
        cost_estimate=cost(48),
        name="mlp_forward_backward",
    )(where, middle, *pieces, gain, *alpha, *beta, d1, u1, d2, u2)


def attend_back_window(
    kind, row0, qkv_ref, att_ref, exp_ref, inv_ref, gatt_ref, gqkv_ref, rel_ref, shift_ref, keys_ref
):
    count = NQ[kind]
    rows = pl.ds(row0, count)
    low_q, low_k = low_half(count), low_half(KEYS)
    live = live_rows()
    lane_k = lax.broadcasted_iota(jnp.int32, (KEYS, 128), 1) % HD
    lane_q = lax.broadcasted_iota(jnp.int32, (count, 128), 1) % HD
    ones = jnp.where(live & (lane_k < 2), 1.0, 0.0).astype(BF)
    across = jnp.where(
        low_half(128) != (lax.broadcasted_iota(jnp.int32, (128, 128), 0) < HD), -1.0, 0.0
    ).astype(BF)
    amount = shift_ref[kind, :count, :]
    onehot = keys_ref[kind]
    rel_mat = rel_ref[...]
    for first in range(0, D // 128, GROUP_BACK):
        pairs = range(first, first + GROUP_BACK)
        heads = [(pair, odd) for pair in pairs for odd in range(2)]
        go_tile = {
            p: (gatt_ref[rows, pair_columns(p)[0]].astype(F32) * inv_ref[rows, pair_columns(p)[0]]).astype(BF)
            for p in pairs
        }
        delta = {
            p: nn((go_tile[p].astype(F32) * att_ref[rows, pair_columns(p)[0]].astype(F32)).astype(BF), across)
            for p in pairs
        }
        go_t = {p: go_tile[p].T for p in pairs}
        gv = {}
        for p, odd in heads:
            gv[p, odd] = nn(go_t[p][HD * odd : HD * (odd + 1), :], exp_ref[2 * p + odd, rows, :])
        gscore = {}
        for p in pairs:
            high = delta[p].astype(BF)
            rest = (delta[p] - high.astype(F32)).astype(BF)
            low_delta = jnp.where(lane_q == 0, high, jnp.where(lane_q == 1, rest, 0)).astype(BF)
            v_tile = pad_rows(qkv_ref[rows, pair_columns(p)[2]])
            if kind == FULL:
                v_tile = jnp.where(live, v_tile, 0).astype(BF)
            gscore[p, 0] = nt(jnp.where(low_q, go_tile[p], low_delta), jnp.where(low_k, v_tile, ones))
            gscore[p, 1] = nt(jnp.where(low_q, low_delta, go_tile[p]), jnp.where(low_k, ones, v_tile))
        q_t = {p: qkv_ref[rows, pair_columns(p)[0]].T for p in pairs}
        gs = {(p, odd): (exp_ref[2 * p + odd, rows, :].astype(F32) * gscore[p, odd]).astype(BF) for p, odd in heads}
        gk = {(p, odd): nn(q_t[p][HD * odd : HD * (odd + 1), :], gs[p, odd]) for p, odd in heads}
        gq = {}
        for p in pairs:
            k_tile = pad_rows(qkv_ref[rows, pair_columns(p)[1]] * BF(HD**-0.5))
            gq[p, 0] = nn(gs[p, 0], jnp.where(low_k, k_tile, onehot))
            gq[p, 1] = nn(gs[p, 1], jnp.where(low_k, onehot, k_tile))
        sums = {p: barrel(jnp.where(low_q, gq[p, 1], gq[p, 0]), amount, False).astype(BF) for p in pairs}
        for p in pairs:
            cols, kcols, vcols = pair_columns(p)
            gv_tile = jnp.concatenate([gv[p, 0], gv[p, 1]], axis=0).astype(BF).T
            gqkv_ref[rows, vcols] = gv_tile[:count, :]
            gk_tile = (jnp.concatenate([gk[p, 0], gk[p, 1]], axis=0) * HD**-0.5).astype(BF).T
            gqkv_ref[rows, kcols] = gk_tile[:count, :]
            gqkv_ref[rows, cols] = (jnp.where(low_q, gq[p, 0], gq[p, 1]) + nt(sums[p], rel_mat)).astype(BF)


def attention_back_kernel(
    gmid_hbm, hid_hbm, qkv_a, qkv_b, qkv_c, att_a, att_b, att_c, exp_a, exp_b, exp_c, inv_a, inv_b, inv_c,
    wproj_ref, rel_ref, shift_ref, keys_ref, dqkv, uqkv, dproj, uproj,
    gqkv_hbm, down_q, up_q, down_p, up_p,
    gmid_ref, hid_ref, qkv_ref, att_ref, exp_ref, inv_ref, gqkv_ref, gb_ref, gatt_ref, sem, out_sem,
):
    spans = [pl.ds(offset, count) for offset, count in zip(PART_OFFS, PART_ROWS)]
    pairs = [(gmid_hbm, gmid_ref)]
    for part, srcs in enumerate(
        ((qkv_a, inv_a, att_a, exp_a), (qkv_b, inv_b, att_b, exp_b), (qkv_c, inv_c, att_c, exp_c))
    ):
        rows = spans[part]
        for src, dst in zip(srcs, (qkv_ref, inv_ref, att_ref)):
            pairs.append((src, dst.at[rows, :]))
        pairs.append((srcs[3], exp_ref.at[:, rows, :]))
    pairs.append((hid_hbm, hid_ref))
    loads = [pltpu.make_async_copy(src, dst, sem.at[i]) for i, (src, dst) in enumerate(pairs)]
    for load in loads:
        load.start()

    def wait_part(part):
        for load in loads[1 + 4 * part : 5 + 4 * part]:
            load.wait()

    stores = [
        pltpu.make_async_copy(gqkv_ref.at[rows, :], gqkv_hbm.at[rows, :], out_sem.at[i])
        for i, rows in enumerate(spans)
    ]
    loads[0].wait()
    gb_ref[...] = gmid_ref[...].astype(BF)
    gatt_ref[...] = nt(gb_ref[...], wproj_ref[...]).astype(BF)
    refs = (qkv_ref, att_ref, exp_ref, inv_ref, gatt_ref, gqkv_ref, rel_ref, shift_ref, keys_ref)

    def step(w, carry):
        for part in range(2):

            @pl.when(w == 2 * part)
            def _():
                wait_part(part)

        attend_back_window(FULL, pl.multiple_of(w * FULLR, 16), *refs)
        return carry

    lax.fori_loop(0, 4, step, 0)
    stores[0].start()
    stores[1].start()
    wait_part(2)
    for kind in (RIGHT, BOTTOM, CORNER):
        attend_back_window(kind, OFFS[kind], *refs)
    stores[2].start()
    up_p[...] = nn(nt(dproj[...], att_ref[...]).astype(BF), gb_ref[...])
    down_p[...] = nn(nt(uproj[...], gb_ref[...]).astype(BF), att_ref[...])
    loads[-1].wait()
    up_q[...] = nn(nt(dqkv[...], hid_ref[...]).astype(BF), gqkv_ref[...])
    down_q[...] = nn(nt(uqkv[...], gqkv_ref[...]).astype(BF), hid_ref[...])
    for store in stores:
        store.wait()


def attention_back(gmid, hid, qkvs, atts, exps, invs, wproj, rel, shift, keys, dqkv, uqkv, dproj, uproj):
    s = lambda *shape, dtype=F32: jax.ShapeDtypeStruct(shape, dtype)
    hbm = pl.BlockSpec(memory_space=pl.ANY)
    return pl.pallas_call(
        attention_back_kernel,
        out_shape=(s(ROWS, 3 * D, dtype=BF), s(RANK, D), s(RANK, 3 * D), s(RANK, D), s(RANK, D)),
        in_specs=[hbm] * 14 + [vm()] * 8,
        out_specs=[hbm] + [vm()] * 4,
        scratch_shapes=[
            pltpu.VMEM((ROWS, D), F32), pltpu.VMEM((ROWS, D), BF), pltpu.VMEM((ROWS, 3 * D), BF),
            pltpu.VMEM((ROWS, D), BF), pltpu.VMEM((D // HD, ROWS, KEYS), BF), pltpu.VMEM((ROWS, D), F32),
            pltpu.VMEM((ROWS, 3 * D), BF), pltpu.VMEM((ROWS, D), BF), pltpu.VMEM((ROWS, D), BF),
            pltpu.SemaphoreType.DMA((14,)), pltpu.SemaphoreType.DMA((3,)),
        ],
        compiler_params=params(52),
        cost_estimate=cost(28),
        name="attention_backward",
    )(gmid, hid, *qkvs, *atts, *exps, *invs, wproj, rel, shift, keys, dqkv, uqkv, dproj, uproj)


def token_grad_kernel(gmid_hbm, x_hbm, gqkv_hbm, gain_ref, wqkv_ref, o0, o1, o2,
                      gmid_ref, x_ref, gqkv_ref, gh_ref, out_rows, sem, *, low, high):
    span = pl.ds(low, high - low)
    copies = [
        pltpu.make_async_copy(src.at[span, :], dst, sem.at[i])
        for i, (src, dst) in enumerate(((gqkv_hbm, gqkv_ref), (x_hbm, x_ref), (gmid_hbm, gmid_ref)))
    ]
    for copy in copies:
        copy.start()
    copies[0].wait()
    gh_ref[...] = nt(gqkv_ref[...], wqkv_ref[...])
    copies[1].wait()
    copies[2].wait()
    gain = gain_ref[...]
    step = (high - low) // 2

    def norm_step(i, carry):
        rows = pl.ds(pl.multiple_of(i * step, 16), step)
        normed, inv_std = normalize(x_ref[rows, :].astype(F32))
        back = norm_back(gh_ref[rows, :] * gain, normed, inv_std)
        out_rows[rows, :] = (gmid_ref[rows, :] + back).astype(BF)
        return carry

    lax.fori_loop(0, 2, norm_step, 0)
    split_pieces(out_rows, (o0, o1, o2))


def token_grad(gmid, x, gqkv, gain, wqkv, low, high):
    count = high - low
    hbm = pl.BlockSpec(memory_space=pl.ANY)
    return pl.pallas_call(
        functools.partial(token_grad_kernel, low=low, high=high),
        out_shape=pieces_of(count),
        in_specs=[hbm, hbm, hbm, vm(), vm()],
        out_specs=[vm()] * 3,
        scratch_shapes=[
            pltpu.VMEM((count, D), F32), pltpu.VMEM((count, D), BF), pltpu.VMEM((count, 3 * D), BF),
            pltpu.VMEM((count, D), F32), pltpu.VMEM((count, D), BF), pltpu.SemaphoreType.DMA((3,)),
        ],
        compiler_params=params(28),
        cost_estimate=cost(8),
        name="token_gradient",
    )(gmid, x, gqkv, gain, wqkv)


def grad_pack_kernel(where_ref, down_q, up_q, down_p, up_p, down1, up1, down2, up2, o0, o1, o2, o3, buf_ref):
    mine = where_ref[0]
    for k in range(4):
        for i, ref in enumerate((down_q, down1, up_p, up2)):
            buf_ref[k, :RANK, QUART * i : QUART * (i + 1)] = ref[:, QUART * k : QUART * (k + 1)]
    for dest in range(4):
        k = jnp.bitwise_xor(mine, dest)
        ranks = slice(RANK // 4 * dest, RANK // 4 * (dest + 1))
        for j in range(4):
            base = RANK + 12 * j
            for t in range(3):
                buf_ref[k, base : base + 4, QUART * t : QUART * (t + 1)] = up_q[
                    ranks, D * t + QUART * j : D * t + QUART * (j + 1)
                ]
            buf_ref[k, base : base + 4, 3 * QUART :] = down_p[ranks, QUART * j : QUART * (j + 1)]
            buf_ref[k, base + 4 : base + 8, :] = up1[ranks, D * j : D * (j + 1)]
            buf_ref[k, base + 8 : base + 12, :] = down2[ranks, D * j : D * (j + 1)]
    for k, out in enumerate((o0, o1, o2, o3)):
        out[...] = buf_ref[k].astype(BF)


def grad_pack(where, *grads):
    return pl.pallas_call(
        grad_pack_kernel,
        out_shape=(jax.ShapeDtypeStruct((4 * RANK, D), BF),) * 4,
        in_specs=[sm()] + [vm()] * 8,
        out_specs=[vm()] * 4,
        scratch_shapes=[pltpu.VMEM((4, 4 * RANK, D), F32)],
        compiler_params=params(8),
        cost_estimate=cost(2),
        name="adapter_grad_pack",
    )(where, *grads)


def grad_sum_kernel(g0, g1, g2, g3, o0, o1, o2, o3, buf_ref):
    total = g0[...].astype(F32) + g1[...].astype(F32) + g2[...].astype(F32) + g3[...].astype(F32)
    buf_ref[...] = jnp.zeros_like(buf_ref)
    buf_ref[:RANK, :] = total[:RANK, :]
    for j, out in enumerate((o0, o1, o2, o3)):
        buf_ref[RANK : RANK + 12, :] = total[RANK + 12 * j : RANK + 12 * (j + 1), :]
        out[...] = buf_ref[...].astype(BF)


def grad_sum(pieces):
    return pl.pallas_call(
        grad_sum_kernel,
        out_shape=(jax.ShapeDtypeStruct((2 * RANK, D), BF),) * 4,
        in_specs=[vm()] * 4,
        out_specs=[vm()] * 4,
        scratch_shapes=[pltpu.VMEM((2 * RANK, D), F32)],
        compiler_params=params(4),
        cost_estimate=cost(2),
        name="adapter_grad_sum",
    )(*pieces)


def grad_adapters_kernel(index_ref, x_ref, qkv_dn, fc1_dn, proj_up, fc2_up, rest_ref, acc_ref):
    acc_ref[...] = jnp.zeros_like(acc_ref)

    def add(i, carry):
        acc_ref[index_ref[i]] += x_ref[i].astype(F32)
        return carry

    lax.fori_loop(0, x_ref.shape[0], add, 0)
    for i, ref in enumerate((qkv_dn, fc1_dn, proj_up, fc2_up)):
        ref[...] = acc_ref[:, :RANK, QUART * i : QUART * (i + 1)]
    rest_ref[...] = acc_ref[:, RANK:, :].astype(BF)


def grad_adapters(index, x):
    s = lambda n, dtype=F32: jax.ShapeDtypeStruct((ADAPT, RANK, n), dtype)
    return pl.pallas_call(
        grad_adapters_kernel,
        out_shape=(s(QUART), s(QUART), s(QUART), s(QUART), s(D, BF)),
        in_specs=[sm(), vm()],
        out_specs=[vm()] * 5,
        scratch_shapes=[pltpu.VMEM((ADAPT, 2 * RANK, D), F32)],
        compiler_params=params(8),
        cost_estimate=cost(2),
        name="adapter_grad_by_adapter",
    )(index, x)


def grad_join_kernel(where_ref, r0, r1, r2, r3, qkv_up, proj_dn, fc1_up, fc2_dn, buf_ref):
    mine = where_ref[0]
    heads = qkv_up.shape[2] // (3 * HD)
    for k, ref in enumerate((r0, r1, r2, r3)):
        buf_ref[jnp.bitwise_xor(mine, k)] = ref[...].astype(F32)
    for source in range(4):
        ranks = slice(RANK // 4 * source, RANK // 4 * (source + 1))
        for h in range(heads):
            for t in range(3):
                qkv_up[:, ranks, HD * (3 * h + t) : HD * (3 * h + t + 1)] = buf_ref[
                    source, :, 0:4, QUART * t + HD * h : QUART * t + HD * (h + 1)
                ]
        proj_dn[:, ranks, :] = buf_ref[source, :, 0:4, 3 * QUART :]
        fc1_up[:, ranks, :] = buf_ref[source, :, 4:8, :]
        fc2_dn[:, ranks, :] = buf_ref[source, :, 8:12, :]


def grad_join(where, pieces):
    s = lambda n: jax.ShapeDtypeStruct((ADAPT, RANK, n), F32)
    return pl.pallas_call(
        grad_join_kernel,
        out_shape=(s(3 * QUART), s(QUART), s(D), s(D)),
        in_specs=[sm()] + [vm()] * 4,
        out_specs=[vm()] * 4,
        scratch_shapes=[pltpu.VMEM((4, ADAPT, RANK, D), F32)],
        compiler_params=params(12),
        cost_estimate=cost(2),
        name="adapter_grad_join",
    )(where, *pieces)


def flip(values, axis, distance):
    size = lax.axis_size(axis)
    return lax.ppermute(values, axis, [(i, i ^ distance) for i in range(size)])


def send_rows(pieces):
    own, near, pair = pieces
    return [own, flip(near, "row", 1), flip(pair, "row", 2)]


def hand_on(pieces, *deps):
    own, near, crossed = pieces
    if deps:
        near, crossed = after((near, crossed), *deps)
    return [own, near, crossed, flip(crossed, "row", 1)]


def exchange(slots, axis):
    return [slots[0]] + [flip(slots[k], axis, k) for k in range(1, 4)]


def after(values, *deps):
    return lax.optimization_barrier((tuple(values), deps))[0]


def col_halves(half):
    return jnp.concatenate([flip(half, "col", j) for j in range(1, 4)], axis=0)


def col_pairs(half, other_row):
    two = jnp.concatenate([half, other_row], axis=0)
    return jnp.concatenate([other_row] + [flip(two, "col", j) for j in range(1, 4)], axis=0)


def rel_matrix(rel_h, rel_w):
    pad = jnp.zeros((32 - (2 * WIN - 1), HD), BF)
    block = jnp.concatenate([rel_h[::-1], pad, rel_w[::-1], pad], axis=0).T
    zero = jnp.zeros((HD, HD), BF)
    return jnp.concatenate(
        [jnp.concatenate([zero, block], axis=1), jnp.concatenate([block, zero], axis=1)], axis=0
    )


def body(
    tokens, grad_out, adapter_index, norm1_gain, norm2_gain, qkv_weight, proj_weight, fc1_weight, fc2_weight,
    rel_h, rel_w, qkv_down, qkv_up, proj_down, proj_up, fc1_down, fc1_up, fc2_down, fc2_up,
):
    members = lax.axis_size("col")
    batches = lax.axis_size("dp")
    row_index, col_index, dp_index = lax.axis_index("row"), lax.axis_index("col"), lax.axis_index("dp")
    half = dp_index % 2
    where = jnp.stack([row_index, half]).astype(jnp.int32)
    slot_images = (
        jnp.bitwise_xor(dp_index, jnp.arange(batches, dtype=jnp.int32))[:, None] * members
        + jnp.bitwise_xor(col_index, jnp.arange(members, dtype=jnp.int32))[None, :]
    ).reshape(-1)
    slot_adapters = jnp.sum(
        jnp.where(
            slot_images[:, None] == jnp.arange(adapter_index.shape[0], dtype=jnp.int32)[None, :],
            adapter_index[:, 0][None, :],
            0,
        ),
        axis=1,
    )
    pick = jnp.concatenate([slot_adapters[:4], half[None]]).astype(jnp.int32)
    swap = lambda m: jnp.swapaxes(m, 1, 2)

    rel = rel_matrix(rel_h, rel_w)
    shift, keys = jnp.asarray(SHIFT_NP), jnp.asarray(KEYS_NP)

    *token_slots, alpha_own, beta_own, alpha_half, beta_half = front(where, tokens, qkv_weight, proj_weight)
    cut = lambda m: lax.dynamic_slice_in_dim(m, half * HBLK, HBLK, 0)
    b0 = flip(beta_half, "row", 2)
    alpha_near = col_halves(alpha_half)
    x_pieces = send_rows(token_slots)
    *send, row_adapters = adapter_pack(
        pick, qkv_up, swap(proj_down), fc1_up, swap(fc2_down), swap(qkv_down), swap(fc1_down), proj_up, fc2_up,
        norm1_gain.reshape(1, -1), norm2_gain.reshape(1, -1),
    )
    beta_sent = [jnp.concatenate([beta_half, b0, send[j]], axis=0) for j in range(1, 4)]
    beta_got = [flip(m, "col", j) for j, m in enumerate(beta_sent, 1)]
    alpha_far = flip(alpha_near, "dp", 1)
    g = jnp.concatenate([alpha_own, alpha_near, alpha_far, row_adapters], axis=0)
    g, *x_pieces = after((g, *x_pieces))
    gy = flip(g, "row", 2)
    grad_slots = pack(where, grad_out)
    *beta_got, _ = after((*beta_got, grad_slots[0]))
    beta_near = jnp.concatenate([b0] + [m[:QUART] for m in beta_got], axis=0)
    col_adapters = [send[0]] + beta_got
    beta_far = flip(beta_near, "dp", 1)
    x_pieces = hand_on(x_pieces)

    fc1_half, fc2_half = after((cut(fc1_weight), cut(fc2_weight)), beta_near)
    c0 = flip(fc2_half, "row", 2)
    fc1_near = [flip(fc1_half, "col", j) for j in range(1, 4)]

    alpha1 = [g, flip(g, "row", 1), gy, flip(gy, "row", 1)]
    beta1 = [beta_own, beta_near, beta_far] + [flip(m, "row", 1) for m in (beta_own, beta_near, beta_far)]
    grad_slots = after(tuple(grad_slots), gy)
    g_pieces = send_rows(grad_slots)
    two = jnp.concatenate([fc2_half, c0], axis=0)
    fc2_near = [flip(two, "col", j) for j in range(1, 4)]
    wqkv, wproj, dqkv, uqkv, dproj, uproj, d1, u1, d2, u2, gain1, gain2 = prep1(
        where, alpha1, beta1, col_adapters
    )
    wqkv, *fc1_near = after((wqkv, *fc1_near))
    fc1_near = jnp.concatenate(fc1_near, axis=0)
    fc1_far = flip(fc1_near, "dp", 1)
    x, hid, *qkvs = qkv_rows(x_pieces, gain1, wqkv)
    *qkvs, fc1_far = after((*qkvs, fc1_far), *g_pieces)
    g_pieces = hand_on(g_pieces, fc1_far)
    h = jnp.concatenate([fc1_weight, fc1_near, fc1_far], axis=0)
    hy = flip(h, "row", 2)
    part0 = attention(0, qkvs[0], rel, shift, keys)
    qkv1, *fc2_near = after((qkvs[1], *fc2_near), part0[0])
    fc2_near = jnp.concatenate([c0] + fc2_near, axis=0)
    fc2_far = flip(fc2_near, "dp", 1)
    part1 = attention(1, qkv1, rel, shift, keys)
    qkv2, _ = after((qkvs[2], part1[0]))
    part2 = attention(2, qkv2, rel, shift, keys)
    atts, exps, invs = zip(part0, part1, part2)
    atts = list(atts)
    atts[2], hy = after((atts[2], hy))
    alpha2 = [h, flip(h, "row", 1), hy, flip(hy, "row", 1)]
    middle = project(x, atts, wproj)
    middle, fc2_far = after((middle, fc2_far))
    beta2 = [fc2_weight, fc2_near, fc2_far] + [flip(m, "row", 1) for m in (fc2_weight, fc2_near, fc2_far)]

    *out_slots, gmid, down1, up1, down2, up2 = mlp(where, middle, g_pieces, gain2, alpha2, beta2, d1, u1, d2, u2)
    out_pieces = send_rows(out_slots)
    gqkv, down_q, up_q, down_p, up_p = attention_back(
        gmid, hid, qkvs, atts, exps, invs, wproj, rel, shift, keys, dqkv, uqkv, dproj, uproj
    )
    out_pieces = hand_on(out_pieces, gqkv)
    gqkv, down_q, up_q, down_p, up_p = after((gqkv, down_q, up_q, down_p, up_p), *out_pieces[:3])
    packed = grad_pack(where, down_q, up_q, down_p, up_p, down1, up1, down2, up2)
    *packed, gqkv = after((*packed, gqkv))
    row_sums = exchange(packed, "row")
    back0 = token_grad(gmid, x, gqkv, gain1, wqkv, *TAIL[0])
    *row_sums, gqkv, b0, b1, b2 = after((*row_sums, gqkv, *back0))
    back_pieces = send_rows((b0, b1, b2))
    summed = grad_sum(row_sums)
    *summed, gqkv = after((*summed, gqkv))
    images = exchange(summed, "col")
    back1 = token_grad(gmid, x, gqkv, gain1, wqkv, *TAIL[1])
    last_pieces = send_rows(back1)
    *images, near, crossed = after((*images, *back_pieces[1:]), back1[0])
    back_pieces = hand_on([back_pieces[0], near, crossed])
    images = jnp.stack(images)
    images, *out_pieces = after((images, *out_pieces))
    step = 1
    while step < batches:
        images = jnp.concatenate([images, flip(images, "dp", step)], axis=0)
        step *= 2
    result = unpack(where, out_pieces, BF)
    images, = after((images,), result)
    qkv_dn, fc1_dn, proj_upg, fc2_upg, rest = grad_adapters(slot_adapters.astype(jnp.int32), images)
    rests = [rest] + [flip(rest, "row", k) for k in range(1, 4)]
    grad_tokens = unpack(where, back_pieces + hand_on(last_pieces, rest), F32, TAIL)
    rests = after(tuple(rests), grad_tokens)
    qkv_upg, proj_dn, fc1_upg, fc2_dn = grad_join(where, rests)
    return (
        result, grad_tokens,
        swap(qkv_dn), qkv_upg, swap(proj_dn), proj_upg, swap(fc1_dn), fc1_upg, swap(fc2_dn), fc2_upg,
    )


def solution(mesh):
    return jax.shard_map(
        body,
        mesh=mesh,
        in_specs=(
            P("row", ("dp", "col")), P("row", ("dp", "col")), P(), P("row"), P("row"),
            P("row", "col"), P("col", "row"), P("row", "col"), P("row", "col"), P(), P(),
            P(None, "row", None), P(None, None, "col"), P(None, "col", None), P(None, None, "row"),
            P(None, "row", None), P(None, None, "col"), P(None, "col", None), P(None, None, "row"),
        ),
        out_specs=(
            P("row", ("dp", "col")), P("row", ("dp", "col")),
            P(None, "row", None), P(None, None, "col"), P(None, "col", None), P(None, None, "row"),
            P(None, "row", None), P(None, None, "col"), P(None, "col", None), P(None, None, "row"),
        ),
        check_vma=False,
    )
```

```python
import functools

import jax
import jax.numpy as jnp
import numpy as np
from jax import lax
from jax.experimental import pallas as pl
from jax.experimental.pallas import tpu as pltpu
from jax.sharding import PartitionSpec as P

D = 768
HD = 64
WIN = 14
SLOTS = WIN * WIN
SIDE = 64
ADAPT = 8
NWIN = 5
IMG_TOK = NWIN * NWIN * SLOTS
RANK = 16
EDGE = SIDE - (NWIN - 1) * WIN
QUART = D // 4
FULLR = 208
KEYS = 208
EDGER = EDGE * WIN
CORNR = EDGE * EDGE
ROWS = 4 * FULLR + 2 * EDGER + CORNR
HALF = ROWS // 2
HBLK = QUART // 2
EPSILON = 1e-06
BF = jnp.bfloat16
F32 = jnp.float32

FULL, RIGHT, BOTTOM, CORNER = 0, 1, 2, 3
NQ = (FULLR, EDGER, EDGER, CORNR)
OFFS = (0, 4 * FULLR, 4 * FULLR + EDGER, 4 * FULLR + 2 * EDGER)


def slot_order(kind):
    rows = EDGE if kind in (BOTTOM, CORNER) else WIN
    cols = EDGE if kind in (RIGHT, CORNER) else WIN
    kept = [a * WIN + b for a in range(rows) for b in range(cols)]
    rest = [s for s in range(SLOTS) if s not in set(kept)]
    return kept, kept + rest


def build_tables():
    shift = np.zeros((4, FULLR, 128), np.int32)
    keys = np.zeros((4, KEYS, 128), np.float32)
    for kind in range(4):
        kept, order = slot_order(kind)
        for i, s in enumerate(kept):
            for base in (0, 64):
                shift[kind, i, base : base + 32] = WIN - 1 - s // WIN
                shift[kind, i, base + 32 : base + 64] = WIN - 1 - s % WIN
        spare = order[0] if kind == FULL else order[-1]
        for i, s in enumerate(order + [spare] * (KEYS - SLOTS)):
            for base in (0, 64):
                keys[kind, i, base + s // WIN] = 1.0
                keys[kind, i, base + 32 + s % WIN] = 1.0
    return shift, keys.astype(jnp.bfloat16)


SHIFT_NP, KEYS_NP = build_tables()


def nn(a, b):
    return jnp.dot(a, b, preferred_element_type=F32)


def nt(a, b):
    return lax.dot_general(a, b, (((1,), (1,)), ((), ())), preferred_element_type=F32)


def tn(a, b):
    return lax.dot_general(a, b, (((0,), (0,)), ((), ())), preferred_element_type=F32)


def vm():
    return pl.BlockSpec(memory_space=pltpu.VMEM)


def sm():
    return pl.BlockSpec(memory_space=pltpu.SMEM)


def params(mib=60):
    return pltpu.CompilerParams(vmem_limit_bytes=mib * 1024 * 1024)


def cost(us):
    return pl.CostEstimate(flops=int(us * 1e6), transcendentals=0, bytes_accessed=0)


def place_window(kind, count, moved, width, spare=-100000):
    row = lax.broadcasted_iota(jnp.int32, (count, width), 0)
    lane = lax.broadcasted_iota(jnp.int32, (count, width), 1)
    if kind in (RIGHT, CORNER):
        src = (row // EDGE) * WIN + row % EDGE
    else:
        src = jnp.where(row < SLOTS, row, spare)
    return (lane == src + moved).astype(F32).astype(BF)


def window_list(dest):
    items = [(FULL, FULLR * j, NWIN * dest + j) for j in range(4)]
    items.append((RIGHT, OFFS[1], NWIN * dest + 4))
    items.append((BOTTOM, OFFS[2], NWIN * 4 + dest))
    if dest == 3:
        items.append((CORNER, OFFS[3], NWIN * NWIN - 1))
    return items


def window_span(window):
    start = window * SLOTS
    low = start // 128 * 128
    high = min(-(-(start + SLOTS) // 128) * 128, IMG_TOK)
    return low, high, start - low


def pack_rows(mine, x_ref, rows_ref, spare):
    for dest in range(4):
        slot = jnp.bitwise_xor(mine, dest)
        if dest != 3:
            rows_ref[slot, OFFS[3] :, :] = jnp.zeros((CORNR, QUART), BF)
        for kind, offset, window in window_list(dest):
            low, high, moved = window_span(window)
            pick = place_window(kind, NQ[kind], moved, high - low, spare)
            rows_ref[slot, offset : offset + NQ[kind], :] = nt(pick, x_ref[:, low:high]).astype(BF)


def fold(rows_ref, outs):
    half = rows_ref.shape[1] // 2
    for slot, (out, base) in enumerate(((outs[0], 0), (outs[1], 0), (outs[2], 0), (outs[2], half))):
        out[base : base + half, :QUART] = rows_ref[slot, :half, :]
        out[base : base + half, QUART:] = rows_ref[slot, half:, :]


def pack_kernel(where_ref, x_ref, o0, o1, o2, rows_ref):
    pack_rows(where_ref[0], x_ref, rows_ref, -100000)
    fold(rows_ref, (o0, o1, o2))


def pieces_of(rows):
    piece = lambda n: jax.ShapeDtypeStruct((n, 2 * QUART), BF)
    return (piece(rows // 2), piece(rows // 2), piece(rows))


def pack(where, x):
    return pl.pallas_call(
        pack_kernel,
        out_shape=pieces_of(ROWS),
        in_specs=[sm(), vm()],
        out_specs=[vm()] * 3,
        scratch_shapes=[pltpu.VMEM((4, ROWS, QUART), BF)],
        compiler_params=params(16),
        cost_estimate=cost(4),
        name="pack",
    )(where, x)


def front_kernel(
    where_ref, x_ref, qkv_w, proj_w, o0, o1, o2, alpha_ref, beta_ref, alpha_half, beta_half, rows_ref,
):
    heads = qkv_w.shape[1] // (3 * HD)
    for h in range(heads):
        for t in range(3):
            ref, base = (alpha_ref, QUART * t) if t < 2 else (beta_ref, 0)
            ref[:, base + HD * h : base + HD * (h + 1)] = qkv_w[:, HD * (3 * h + t) : HD * (3 * h + t + 1)]
    beta_ref[:, QUART:] = proj_w[...]
    rows = pl.ds(pl.multiple_of(where_ref[1] * HBLK, 32), HBLK)
    alpha_half[...] = alpha_ref[rows, :]
    beta_half[...] = beta_ref[rows, :]
    pack_rows(where_ref[0], x_ref, rows_ref, 0)
    fold(rows_ref, (o0, o1, o2))


def front(where, x, qkv_w, proj_w):
    s = lambda *shape: jax.ShapeDtypeStruct(shape, BF)
    return pl.pallas_call(
        front_kernel,
        out_shape=pieces_of(ROWS)
        + (s(QUART, 2 * QUART), s(QUART, 2 * QUART), s(HBLK, 2 * QUART), s(HBLK, 2 * QUART)),
        in_specs=[sm(), vm(), vm(), vm()],
        out_specs=[vm()] * 7,
        scratch_shapes=[pltpu.VMEM((4, ROWS, QUART), BF)],
        compiler_params=params(16),
        cost_estimate=cost(5),
        name="token_and_weight_pack",
    )(where, x, qkv_w, proj_w)


def unpack_kernel(where_ref, *refs, bounds):
    pieces, (out_ref, acc_ref, rows_ref) = refs[:-3], refs[-3:]
    mine = where_ref[0]
    acc_ref[...] = jnp.zeros_like(acc_ref)
    index = 0
    for low, high in bounds:
        half = (high - low) // 2
        for slot in range(4):
            piece = pieces[index]
            rows = slice(half, 2 * half) if slot == 3 else slice(0, half)
            rows_ref[slot, low : low + half, :] = piece[rows, :QUART]
            rows_ref[slot, low + half : high, :] = piece[rows, QUART:]
            index += 1

    for source in range(4):
        slot = jnp.bitwise_xor(mine, source)
        for kind, offset, window in window_list(source):
            low, high, moved = window_span(window)
            pick = place_window(kind, NQ[kind], moved, high - low)
            acc_ref[:, low:high] += tn(rows_ref[slot, offset : offset + NQ[kind], :], pick)
    out_ref[...] = acc_ref[:, :IMG_TOK].astype(out_ref.dtype)


def unpack(where, pieces, dtype, bounds=((0, ROWS),)):
    return pl.pallas_call(
        functools.partial(unpack_kernel, bounds=bounds),
        out_shape=jax.ShapeDtypeStruct((QUART, IMG_TOK), dtype),
        in_specs=[sm()] + [vm()] * len(pieces),
        out_specs=vm(),
        scratch_shapes=[
            pltpu.VMEM((QUART, -(-IMG_TOK // 128) * 128), F32),
            pltpu.VMEM((4, ROWS, QUART), BF),
        ],
        compiler_params=params(24),
        cost_estimate=cost(4),
        name="unpack",
    )(where, *pieces)


def join_pieces(pieces, dst_ref):
    for slot, piece in enumerate(pieces):
        rows = slice(HALF, ROWS) if slot == 3 else slice(0, HALF)
        dst_ref[:HALF, QUART * slot : QUART * (slot + 1)] = piece[rows, :QUART]
        dst_ref[HALF:, QUART * slot : QUART * (slot + 1)] = piece[rows, QUART:]


def split_pieces(src_ref, outs):
    half = src_ref.shape[0] // 2
    for slot, (out, base) in enumerate(((outs[0], 0), (outs[1], 0), (outs[2], 0), (outs[2], half))):
        out[base : base + half, :QUART] = src_ref[:half, QUART * slot : QUART * (slot + 1)]
        out[base : base + half, QUART:] = src_ref[half:, QUART * slot : QUART * (slot + 1)]


def adapter_pack_kernel(
    pick_ref, qkv_up, proj_dn, fc1_up, fc2_dn, qkv_dn, fc1_dn, proj_up, fc2_up, gain1, gain2,
    s0, s1, s2, s3, row_ref,
):
    heads = qkv_up.shape[2] // (3 * HD)
    half = 2 * QUART
    for j, send_ref in enumerate((s0, s1, s2, s3)):
        a = pick_ref[j]
        for h in range(heads):
            for t in range(3):
                row, base = (0, QUART * t) if t < 2 else (RANK, 0)
                send_ref[row : row + RANK, base + HD * h : base + HD * (h + 1)] = qkv_up[
                    a, :, HD * (3 * h + t) : HD * (3 * h + t + 1)
                ]
        send_ref[RANK : 2 * RANK, QUART:] = proj_dn[a]
        for i, ref in enumerate((fc1_up, fc2_dn)):
            for part in range(2):
                row = RANK * (2 + 2 * i + part)
                send_ref[row : row + RANK, :] = ref[a, :, half * part : half * (part + 1)]
    for i, ref in enumerate((qkv_dn, fc1_dn, proj_up, fc2_up)):
        row, base = RANK * (i // 2), QUART * (i % 2)
        row_ref[row : row + RANK, base : base + QUART] = ref[pick_ref[0]]
    for i, ref in enumerate((gain1, gain2)):
        row_ref[2 * RANK :, QUART * i : QUART * (i + 1)] = jnp.broadcast_to(ref[...], (RANK, QUART))


def adapter_pack(pick, *mats):
    s = lambda *shape: jax.ShapeDtypeStruct(shape, BF)
    return pl.pallas_call(
        adapter_pack_kernel,
        out_shape=(s(6 * RANK, 2 * QUART),) * 4 + (s(3 * RANK, 2 * QUART),),
        in_specs=[sm()] + [vm()] * 10,
        out_specs=[vm()] * 5,
        compiler_params=params(8),
        cost_estimate=cost(2),
        name="adapter_pack",
    )(pick, *mats)


def alpha_block(k, j):
    part = k
    if j == 0:
        return [(part, 0, QUART, None)]
    return [
        (part, QUART + HBLK * (j - 1), HBLK, 0),
        (part, QUART + 3 * HBLK + HBLK * (j - 1), HBLK, 1),
    ]


def beta_block(k, j):
    core, cross = k % 2, k // 2
    base = 3 * core
    if j == 0 and not cross:
        return [(base, 0, QUART, None)]
    row = 0 if j == 0 else HBLK + QUART * (j - 1) + HBLK * cross
    return [(base + 1, row, HBLK, 0), (base + 2, row, HBLK, 1)]


def block_dst(start, flag, half):
    if flag is None:
        return start
    offset = half if flag == 0 else 1 - half
    return pl.multiple_of(start + offset * HBLK, 32)


def prep1_kernel(
    where_ref, p0, p1, p2, p3, q0, q1, q2, q3, q4, q5, a0, a1, a2, a3,
    wqkv_ref, wproj_ref, dqkv, uqkv, dproj, uproj, d1, u1, d2, u2, gain1, gain2, ups, downs,
):
    half = where_ref[1]
    for j, a in enumerate((a0, a1, a2, a3)):
        base = a.shape[0] - 6 * RANK
        part = lambda i: slice(base + RANK * i, base + RANK * (i + 1))
        for t in range(3):
            uqkv[:, D * t + QUART * j : D * t + QUART * (j + 1)] = a[
                part(t // 2), QUART * (t % 2) : QUART * (t % 2 + 1)
            ]
        dproj[:, QUART * j : QUART * (j + 1)] = a[part(1), QUART:]
        for i in range(2):
            u1[:, D * j + D // 2 * i : D * j + D // 2 * (i + 1)] = a[part(2 + i), :]
            d2[:, D * j + D // 2 * i : D * j + D // 2 * (i + 1)] = a[part(4 + i), :]
    for k, ref in enumerate((p0, p1, p2, p3)):
        for i, dst in enumerate((dqkv, d1, uproj, u2)):
            rows = slice(D + RANK * (i // 2), D + RANK * (i // 2 + 1))
            dst[:, QUART * k : QUART * (k + 1)] = ref[rows, QUART * (i % 2) : QUART * (i % 2 + 1)]
        for i, dst in enumerate((gain1, gain2)):
            row = D + 2 * RANK
            dst[:, QUART * k : QUART * (k + 1)] = ref[row : row + 1, QUART * i : QUART * (i + 1)].astype(F32)
    alpha, beta = (p0, p1, p2, p3), (q0, q1, q2, q3, q4, q5)
    for k in range(4):
        for j in range(4):
            for part, row, count, flag in alpha_block(k, j):
                rows = pl.ds(block_dst(QUART * k, flag, half), count)
                for t in range(2):
                    wqkv_ref[rows, D * t + QUART * j : D * t + QUART * (j + 1)] = alpha[part][
                        row : row + count, QUART * t : QUART * (t + 1)
                    ]
            for part, row, count, flag in beta_block(k, j):
                rows = pl.ds(block_dst(QUART * k, flag, half), count)
                wqkv_ref[rows, 2 * D + QUART * j : 2 * D + QUART * (j + 1)] = beta[part][
                    row : row + count, :QUART
                ]
                rows = pl.ds(block_dst(QUART * j, flag, half), count)
                wproj_ref[rows, QUART * k : QUART * (k + 1)] = beta[part][row : row + count, QUART:]
    for t in range(3):
        ups[t] = uqkv[:, D * t : D * (t + 1)]
    ups[3] = uproj[...]
    for k in range(4):
        downs[k] = dqkv[:, QUART * k : QUART * (k + 1)]
        downs[4 + k] = dproj[:, QUART * k : QUART * (k + 1)]

    def merge(t, carry):
        cols = pl.ds(pl.multiple_of(D * t, 128), D)
        for k in range(4):
            rows = slice(QUART * k, QUART * (k + 1))
            wqkv_ref[rows, cols] = (wqkv_ref[rows, cols].astype(F32) + tn(downs[k], ups[t])).astype(BF)
        return carry

    lax.fori_loop(0, 3, merge, 0)
    for k in range(4):
        rows = slice(QUART * k, QUART * (k + 1))
        wproj_ref[rows, :] = (wproj_ref[rows, :].astype(F32) + tn(downs[4 + k], ups[3])).astype(BF)


def prep1(where, alpha, beta, cols):
    s = lambda *shape: jax.ShapeDtypeStruct(shape, BF)
    return pl.pallas_call(
        prep1_kernel,
        out_shape=(
            s(D, 3 * D), s(D, D), s(RANK, D), s(RANK, 3 * D), s(RANK, D), s(RANK, D),
            s(RANK, D), s(RANK, 4 * D), s(RANK, 4 * D), s(RANK, D),
            jax.ShapeDtypeStruct((1, D), F32), jax.ShapeDtypeStruct((1, D), F32),
        ),
        in_specs=[sm()] + [vm()] * 14,
        out_specs=[vm()] * 12,
        scratch_shapes=[pltpu.VMEM((4, RANK, D), BF), pltpu.VMEM((8, RANK, QUART), BF)],
        compiler_params=params(24),
        cost_estimate=cost(7),
        name="attention_weights",
    )(where, *alpha, *beta, *cols)


def normalize(values):
    center = jnp.sum(values, axis=1, keepdims=True) / D
    shifted = values - center
    inv_std = lax.rsqrt(jnp.sum(shifted * shifted, axis=1, keepdims=True) / D + EPSILON)
    return shifted * inv_std, inv_std


def norm_back(grad, normed, inv_std):
    first = jnp.sum(grad, axis=1, keepdims=True) / D
    second = jnp.sum(grad * normed, axis=1, keepdims=True) / D
    return inv_std * (grad - first - normed * second)


def barrel(values, amount, left):
    for bit in (1, 2, 4, 8):
        moved = pltpu.roll(values, (128 - bit) if left else bit, 1)
        values = jnp.where((amount & bit) != 0, moved, values)
    return values


def low_half(count):
    return lax.broadcasted_iota(jnp.int32, (count, 128), 1) < HD


def pad_rows(tile):
    if tile.shape[0] == KEYS:
        return tile
    return jnp.concatenate([tile, jnp.zeros((KEYS - tile.shape[0], tile.shape[1]), tile.dtype)], axis=0)


def live_rows():
    return lax.broadcasted_iota(jnp.int32, (KEYS, 128), 0) < SLOTS


GROUP = 6
GROUP_BACK = 6


def pair_columns(pair):
    return tuple(slice(D * t + 128 * pair, D * t + 128 * (pair + 1)) for t in range(3))


def attend_window(kind, row0, qkv_ref, att_ref, exp_ref, inv_ref, rel_ref, shift_ref, keys_ref):
    count = NQ[kind]
    rows = pl.ds(row0, count)
    low_q, low_k = low_half(count), low_half(KEYS)
    live = live_rows()
    ones = jnp.where(live, 1.0, 0.0).astype(BF)
    amount = shift_ref[kind, :count, :]
    onehot = keys_ref[kind]
    rel_mat = rel_ref[...]
    for first in range(0, D // 128, GROUP):
        pairs = range(first, first + GROUP)
        heads = [(pair, odd) for pair in pairs for odd in range(2)]
        q_tile = {p: qkv_ref[rows, pair_columns(p)[0]] for p in pairs}
        rel = {p: nn(q_tile[p], rel_mat) for p in pairs}
        rel = {p: barrel(rel[p], amount, True).astype(BF) for p in pairs}
        k_tile = {p: pad_rows(qkv_ref[rows, pair_columns(p)[1]] * BF(HD**-0.5)) for p in pairs}
        scores = {}
        for p, odd in heads:
            if odd:
                q_aug, k_aug = jnp.where(low_q, rel[p], q_tile[p]), jnp.where(low_k, onehot, k_tile[p])
            else:
                q_aug, k_aug = jnp.where(low_q, q_tile[p], rel[p]), jnp.where(low_k, k_tile[p], onehot)
            scores[p, odd] = nt(q_aug, k_aug)
        top = {h: jnp.max(scores[h], axis=1, keepdims=True) for h in heads}
        exponent = {h: jnp.exp(scores[h] - top[h]).astype(BF) for h in heads}
        both = {}
        for p, odd in heads:
            exp_ref[2 * p + odd, rows, :] = exponent[p, odd]
            v_tile = pad_rows(qkv_ref[rows, pair_columns(p)[2]])
            if kind == FULL:
                v_tile = jnp.where(live, v_tile, 0).astype(BF)
            v_aug = jnp.where(low_k, ones, v_tile) if odd else jnp.where(low_k, v_tile, ones)
            both[p, odd] = nn(exponent[p, odd], v_aug)
        for p in pairs:
            cols = pair_columns(p)[0]
            inverse = 1.0 / pltpu.roll(jnp.where(low_q, both[p, 1], both[p, 0]), HD, 1)
            inv_ref[rows, cols] = inverse
            att_ref[rows, cols] = (jnp.where(low_q, both[p, 0], both[p, 1]) * inverse).astype(BF)


PARTS = ((FULL, FULL), (FULL, FULL), (RIGHT, BOTTOM, CORNER))
PART_ROWS = tuple(sum(NQ[kind] for kind in part) for part in PARTS)
PART_OFFS = (0, PART_ROWS[0], PART_ROWS[0] + PART_ROWS[1])


TAIL = ((0, 576), (576, ROWS))


def qkv_kernel(
    x0, x1, x2, x3, gain_ref, w_hbm, x_hbm, hid_hbm, qkv_a, qkv_b, qkv_c,
    x_ref, hid_ref, rows_ref, w_ref, qkv_ref, sem, out_sem,
):
    loads = [
        pltpu.make_async_copy(w_hbm.at[:, D * t : D * (t + 1)], w_ref.at[t], sem.at[t]) for t in range(3)
    ]
    for load in loads:
        load.start()
    join_pieces((x0, x1, x2, x3), x_ref)
    kept = [
        pltpu.make_async_copy(src, dst, sem.at[3 + i])
        for i, (src, dst) in enumerate(((x_ref, x_hbm), (hid_ref, hid_hbm)))
    ]
    kept[0].start()
    gain = gain_ref[...]

    def norm_step(i, carry):
        rows = pl.ds(pl.multiple_of(i * 112, 16), 112)
        normed, _ = normalize(x_ref[rows, :].astype(F32))
        hidden = (normed * gain).astype(BF)
        rows_ref[rows, :] = hidden
        hid_ref[rows, :] = hidden
        return carry

    lax.fori_loop(0, ROWS // 112, norm_step, 0)
    for w in range(4):
        hid_ref[FULLR * w + SLOTS : FULLR * (w + 1), :] = jnp.zeros((FULLR - SLOTS, D), BF)
    kept[1].start()
    for load in loads:
        load.wait()

    def stores(t):
        cols = pl.ds(pl.multiple_of(D * t, 128), D)
        return [
            pltpu.make_async_copy(
                qkv_ref.at[t, pl.ds(offset, count), :], out.at[:, cols], out_sem.at[t, i]
            )
            for i, (out, offset, count) in enumerate(zip((qkv_a, qkv_b, qkv_c), PART_OFFS, PART_ROWS))
        ]

    def project_step(t, carry):
        qkv_ref[t] = nn(rows_ref[...], w_ref[t]).astype(BF)
        for store in stores(t):
            store.start()
        return carry

    lax.fori_loop(0, 3, project_step, 0)
    for t in range(3):
        for store in stores(t):
            store.wait()
    for store in kept:
        store.wait()


def qkv_rows(pieces, gain, wqkv):
    s = lambda *shape: jax.ShapeDtypeStruct(shape, BF)
    hbm = pl.BlockSpec(memory_space=pl.ANY)
    return pl.pallas_call(
        qkv_kernel,
        out_shape=(s(ROWS, D), s(ROWS, D)) + tuple(s(n, 3 * D) for n in PART_ROWS),
        in_specs=[vm()] * 5 + [hbm],
        out_specs=[hbm] * 5,
        scratch_shapes=[
            pltpu.VMEM((ROWS, D), BF), pltpu.VMEM((ROWS, D), BF), pltpu.VMEM((ROWS, D), BF),
            pltpu.VMEM((3, D, D), BF), pltpu.VMEM((3, ROWS, D), BF),
            pltpu.SemaphoreType.DMA((5,)), pltpu.SemaphoreType.DMA((3, 3)),
        ],
        compiler_params=params(32),
        cost_estimate=cost(10),
        name="norm_and_qkv",
    )(*pieces, gain, wqkv)


def attention_kernel(qkv_ref, rel_ref, shift_ref, keys_ref, att_ref, exp_ref, inv_ref, *, kinds):
    refs = (qkv_ref, att_ref, exp_ref, inv_ref, rel_ref, shift_ref, keys_ref)
    if kinds[0] == FULL:

        def step(w, carry):
            attend_window(FULL, pl.multiple_of(w * FULLR, 16), *refs)
            return carry

        lax.fori_loop(0, len(kinds), step, 0)
    else:
        row = 0
        for kind in kinds:
            attend_window(kind, row, *refs)
            row += NQ[kind]


def attention(part, qkv, rel, shift, keys):
    rows = PART_ROWS[part]
    s = lambda *shape, dtype=BF: jax.ShapeDtypeStruct(shape, dtype)
    return pl.pallas_call(
        functools.partial(attention_kernel, kinds=PARTS[part]),
        out_shape=(s(rows, D), s(D // HD, rows, KEYS), s(rows, D, dtype=F32)),
        in_specs=[vm()] * 4,
        out_specs=[vm()] * 3,
        compiler_params=params(24),
        cost_estimate=cost(10),
        name="attention_forward",
    )(qkv, rel, shift, keys)


def project_kernel(x_ref, att_a, att_b, att_c, wproj_ref, middle_ref):
    for ref, offset, count in zip((att_a, att_b, att_c), PART_OFFS, PART_ROWS):
        rows = slice(offset, offset + count)
        middle_ref[rows, :] = x_ref[rows, :].astype(F32) + nn(ref[...], wproj_ref[...])


def project(x, atts, wproj):
    return pl.pallas_call(
        project_kernel,
        out_shape=jax.ShapeDtypeStruct((ROWS, D), F32),
        in_specs=[vm()] * 5,
        out_specs=vm(),
        compiler_params=params(20),
        cost_estimate=cost(5),
        name="projection",
    )(x, *atts, wproj)


CHUNK = 512
LOCK = 1


def mlp_kernel(
    where_ref, middle_ref, g0, g1, g2, g3, gain_ref,
    p0, p1, p2, p3, q0, q1, q2, q3, q4, q5, d1, u1, d2, u2,
    o0, o1, o2, gmid_ref, down1, up1, down2, up2,
    gm_ref, out_rows, h2_ref, acc_mlp, acc_gh, gu1, ad2, w1_ref, w2_ref, downs, sem,
):
    half = where_ref[1]
    copies = []

    def fetch(src, dst):
        copies.append(pltpu.make_async_copy(src, dst, sem.at[len(copies)]))
        copies[-1].start()

    alpha, beta = (p0, p1, p2, p3), (q0, q1, q2, q3, q4, q5)
    for k in range(4):
        for j in range(4):
            for part, row, count, flag in alpha_block(k, j):
                rows = pl.ds(block_dst(QUART * k, flag, half), count)
                fetch(alpha[part].at[row : row + count, :], w1_ref.at[rows, D * j : D * (j + 1)])
            for part, row, count, flag in beta_block(k, j):
                rows = pl.ds(block_dst(QUART * k, flag, half), count)
                fetch(beta[part].at[row : row + count, :], w2_ref.at[rows, D * j : D * (j + 1)])
    join_pieces((g0, g1, g2, g3), gm_ref)
    for k in range(4):
        downs[k] = d1[:, QUART * k : QUART * (k + 1)]
        downs[4 + k] = u2[:, QUART * k : QUART * (k + 1)]
    for copy in copies:
        copy.wait()

    def merge(j, carry):
        cols = pl.ds(pl.multiple_of(D * j, 128), D)
        for k in range(4):
            rows = slice(QUART * k, QUART * (k + 1))
            w1_ref[rows, cols] = (w1_ref[rows, cols].astype(F32) + tn(downs[k], u1[:, cols])).astype(BF)
            w2_ref[rows, cols] = (w2_ref[rows, cols].astype(F32) + tn(downs[4 + k], d2[:, cols])).astype(BF)
        return carry

    lax.fori_loop(0, 4, merge, 0)
    gain = gain_ref[...]
    down1[...] = jnp.zeros_like(down1)
    up1[...] = jnp.zeros_like(up1)
    down2[...] = jnp.zeros_like(down2)
    up2[...] = jnp.zeros_like(up2)

    def tile_step(t, carry):
        rows = pl.ds(pl.multiple_of(t * HALF, 16), HALF)
        normed, _ = normalize(middle_ref[rows, :])
        h2 = (normed * gain).astype(BF)
        h2_ref[...] = h2
        gm = gm_ref[rows, :]
        ad1 = nt(d1[...], h2).astype(BF)
        gu2 = nt(u2[...], gm).astype(BF)
        acc_mlp[...] = jnp.zeros_like(acc_mlp)
        acc_gh[...] = jnp.zeros_like(acc_gh)
        gu1[...] = jnp.zeros_like(gu1)
        ad2[...] = jnp.zeros_like(ad2)

        def chunk_step(c, inner_carry):
            spans = [
                pl.ds(pl.multiple_of((c * LOCK + i) * CHUNK, CHUNK), CHUNK) for i in range(LOCK)
            ]
            h2 = h2_ref[...]
            gm = gm_ref[rows, :]
            inner = [nn(h2, w1_ref[:, span]) for span in spans]
            gact = [nn(gm, w2_ref[:, span]) for span in spans]
            act, ginner = [], []
            for i in range(LOCK):
                half = 0.5 * (1.0 + lax.erf(inner[i] * 2**-0.5))
                act.append((inner[i] * half).astype(BF))
                slope = half + inner[i] * (jnp.exp(-0.5 * inner[i] * inner[i]) * (2 * np.pi) ** -0.5)
                ginner.append((gact[i] * slope).astype(BF))
            for i, span in enumerate(spans):
                acc_mlp[...] += nt(act[i], w2_ref[:, span])
                acc_gh[...] += nt(ginner[i], w1_ref[:, span])
                up1[:, span] += nn(ad1, ginner[i])
                gu1[...] += nt(u1[:, span], ginner[i])
                ad2[...] += nt(d2[:, span], act[i])
                down2[:, span] += nn(gu2, act[i])
            return inner_carry

        lax.fori_loop(0, 4 * D // (CHUNK * LOCK), chunk_step, 0)
        down1[...] += nn(gu1[...].astype(BF), h2_ref[...])
        up2[...] += nn(ad2[...].astype(BF), gm_ref[rows, :])
        middle = middle_ref[rows, :]
        out_rows[rows, :] = (middle + acc_mlp[...]).astype(BF)
        normed, inv_std = normalize(middle)
        gmid_ref[rows, :] = gm_ref[rows, :].astype(F32) + norm_back(acc_gh[...] * gain, normed, inv_std)
        return carry

    lax.fori_loop(0, 2, tile_step, 0)
    split_pieces(out_rows, (o0, o1, o2))


def mlp(where, middle, pieces, gain, alpha, beta, d1, u1, d2, u2):
    s = lambda *shape, dtype=F32: jax.ShapeDtypeStruct(shape, dtype)
    return pl.pallas_call(
        mlp_kernel,
        out_shape=pieces_of(ROWS)
        + (s(ROWS, D), s(RANK, D), s(RANK, 4 * D), s(RANK, 4 * D), s(RANK, D)),
        in_specs=[sm()] + [vm()] * 6 + [pl.BlockSpec(memory_space=pl.ANY)] * 10 + [vm()] * 4,
        out_specs=[vm()] * 8,
        scratch_shapes=[
            pltpu.VMEM((ROWS, D), BF), pltpu.VMEM((ROWS, D), BF), pltpu.VMEM((HALF, D), BF),
            pltpu.VMEM((HALF, D), F32), pltpu.VMEM((HALF, D), F32),
            pltpu.VMEM((RANK, HALF), F32), pltpu.VMEM((RANK, HALF), F32),
            pltpu.VMEM((D, 4 * D), BF), pltpu.VMEM((D, 4 * D), BF), pltpu.VMEM((8, RANK, QUART), BF),
            pltpu.SemaphoreType.DMA((4 * 4 * 4,)),
        ],
        compiler_params=params(48),
        cost_estimate=cost(48),
        name="mlp_forward_backward",
    )(where, middle, *pieces, gain, *alpha, *beta, d1, u1, d2, u2)


def attend_back_window(
    kind, row0, qkv_ref, att_ref, exp_ref, inv_ref, gatt_ref, gqkv_ref, rel_ref, shift_ref, keys_ref
):
    count = NQ[kind]
    rows = pl.ds(row0, count)
    low_q, low_k = low_half(count), low_half(KEYS)
    live = live_rows()
    lane_k = lax.broadcasted_iota(jnp.int32, (KEYS, 128), 1) % HD
    lane_q = lax.broadcasted_iota(jnp.int32, (count, 128), 1) % HD
    ones = jnp.where(live & (lane_k < 2), 1.0, 0.0).astype(BF)
    across = jnp.where(
        low_half(128) != (lax.broadcasted_iota(jnp.int32, (128, 128), 0) < HD), -1.0, 0.0
    ).astype(BF)
    amount = shift_ref[kind, :count, :]
    onehot = keys_ref[kind]
    rel_mat = rel_ref[...]
    for first in range(0, D // 128, GROUP_BACK):
        pairs = range(first, first + GROUP_BACK)
        heads = [(pair, odd) for pair in pairs for odd in range(2)]
        go_tile = {
            p: (gatt_ref[rows, pair_columns(p)[0]].astype(F32) * inv_ref[rows, pair_columns(p)[0]]).astype(BF)
            for p in pairs
        }
        delta = {
            p: nn((go_tile[p].astype(F32) * att_ref[rows, pair_columns(p)[0]].astype(F32)).astype(BF), across)
            for p in pairs
        }
        go_t = {p: go_tile[p].T for p in pairs}
        gv = {}
        for p, odd in heads:
            gv[p, odd] = nn(go_t[p][HD * odd : HD * (odd + 1), :], exp_ref[2 * p + odd, rows, :])
        gscore = {}
        for p in pairs:
            high = delta[p].astype(BF)
            rest = (delta[p] - high.astype(F32)).astype(BF)
            low_delta = jnp.where(lane_q == 0, high, jnp.where(lane_q == 1, rest, 0)).astype(BF)
            v_tile = pad_rows(qkv_ref[rows, pair_columns(p)[2]])
            if kind == FULL:
                v_tile = jnp.where(live, v_tile, 0).astype(BF)
            gscore[p, 0] = nt(jnp.where(low_q, go_tile[p], low_delta), jnp.where(low_k, v_tile, ones))
            gscore[p, 1] = nt(jnp.where(low_q, low_delta, go_tile[p]), jnp.where(low_k, ones, v_tile))
        q_t = {p: qkv_ref[rows, pair_columns(p)[0]].T for p in pairs}
        gs = {(p, odd): (exp_ref[2 * p + odd, rows, :].astype(F32) * gscore[p, odd]).astype(BF) for p, odd in heads}
        gk = {(p, odd): nn(q_t[p][HD * odd : HD * (odd + 1), :], gs[p, odd]) for p, odd in heads}
        gq = {}
        for p in pairs:
            k_tile = pad_rows(qkv_ref[rows, pair_columns(p)[1]] * BF(HD**-0.5))
            gq[p, 0] = nn(gs[p, 0], jnp.where(low_k, k_tile, onehot))
            gq[p, 1] = nn(gs[p, 1], jnp.where(low_k, onehot, k_tile))
        sums = {p: barrel(jnp.where(low_q, gq[p, 1], gq[p, 0]), amount, False).astype(BF) for p in pairs}
        for p in pairs:
            cols, kcols, vcols = pair_columns(p)
            gv_tile = jnp.concatenate([gv[p, 0], gv[p, 1]], axis=0).astype(BF).T
            gqkv_ref[rows, vcols] = gv_tile[:count, :]
            gk_tile = (jnp.concatenate([gk[p, 0], gk[p, 1]], axis=0) * HD**-0.5).astype(BF).T
            gqkv_ref[rows, kcols] = gk_tile[:count, :]
            gqkv_ref[rows, cols] = (jnp.where(low_q, gq[p, 0], gq[p, 1]) + nt(sums[p], rel_mat)).astype(BF)


def attention_back_kernel(
    gmid_hbm, hid_hbm, qkv_a, qkv_b, qkv_c, att_a, att_b, att_c, exp_a, exp_b, exp_c, inv_a, inv_b, inv_c,
    wproj_ref, rel_ref, shift_ref, keys_ref, dqkv, uqkv, dproj, uproj,
    gqkv_hbm, down_q, up_q, down_p, up_p,
    gmid_ref, hid_ref, qkv_ref, att_ref, exp_ref, inv_ref, gqkv_ref, gb_ref, gatt_ref, sem, out_sem,
):
    spans = [pl.ds(offset, count) for offset, count in zip(PART_OFFS, PART_ROWS)]
    pairs = [(gmid_hbm, gmid_ref)]
    for part, srcs in enumerate(
        ((qkv_a, inv_a, att_a, exp_a), (qkv_b, inv_b, att_b, exp_b), (qkv_c, inv_c, att_c, exp_c))
    ):
        rows = spans[part]
        for src, dst in zip(srcs, (qkv_ref, inv_ref, att_ref)):
            pairs.append((src, dst.at[rows, :]))
        pairs.append((srcs[3], exp_ref.at[:, rows, :]))
    pairs.append((hid_hbm, hid_ref))
    loads = [pltpu.make_async_copy(src, dst, sem.at[i]) for i, (src, dst) in enumerate(pairs)]
    for load in loads:
        load.start()

    def wait_part(part):
        for load in loads[1 + 4 * part : 5 + 4 * part]:
            load.wait()

    stores = [
        pltpu.make_async_copy(gqkv_ref.at[rows, :], gqkv_hbm.at[rows, :], out_sem.at[i])
        for i, rows in enumerate(spans)
    ]
    loads[0].wait()
    gb_ref[...] = gmid_ref[...].astype(BF)
    gatt_ref[...] = nt(gb_ref[...], wproj_ref[...]).astype(BF)
    refs = (qkv_ref, att_ref, exp_ref, inv_ref, gatt_ref, gqkv_ref, rel_ref, shift_ref, keys_ref)

    def step(w, carry):
        for part in range(2):

            @pl.when(w == 2 * part)
            def _():
                wait_part(part)

        attend_back_window(FULL, pl.multiple_of(w * FULLR, 16), *refs)
        return carry

    lax.fori_loop(0, 4, step, 0)
    stores[0].start()
    stores[1].start()
    wait_part(2)
    for kind in (RIGHT, BOTTOM, CORNER):
        attend_back_window(kind, OFFS[kind], *refs)
    stores[2].start()
    up_p[...] = nn(nt(dproj[...], att_ref[...]).astype(BF), gb_ref[...])
    down_p[...] = nn(nt(uproj[...], gb_ref[...]).astype(BF), att_ref[...])
    loads[-1].wait()
    up_q[...] = nn(nt(dqkv[...], hid_ref[...]).astype(BF), gqkv_ref[...])
    down_q[...] = nn(nt(uqkv[...], gqkv_ref[...]).astype(BF), hid_ref[...])
    for store in stores:
        store.wait()


def attention_back(gmid, hid, qkvs, atts, exps, invs, wproj, rel, shift, keys, dqkv, uqkv, dproj, uproj):
    s = lambda *shape, dtype=F32: jax.ShapeDtypeStruct(shape, dtype)
    hbm = pl.BlockSpec(memory_space=pl.ANY)
    return pl.pallas_call(
        attention_back_kernel,
        out_shape=(s(ROWS, 3 * D, dtype=BF), s(RANK, D), s(RANK, 3 * D), s(RANK, D), s(RANK, D)),
        in_specs=[hbm] * 14 + [vm()] * 8,
        out_specs=[hbm] + [vm()] * 4,
        scratch_shapes=[
            pltpu.VMEM((ROWS, D), F32), pltpu.VMEM((ROWS, D), BF), pltpu.VMEM((ROWS, 3 * D), BF),
            pltpu.VMEM((ROWS, D), BF), pltpu.VMEM((D // HD, ROWS, KEYS), BF), pltpu.VMEM((ROWS, D), F32),
            pltpu.VMEM((ROWS, 3 * D), BF), pltpu.VMEM((ROWS, D), BF), pltpu.VMEM((ROWS, D), BF),
            pltpu.SemaphoreType.DMA((14,)), pltpu.SemaphoreType.DMA((3,)),
        ],
        compiler_params=params(52),
        cost_estimate=cost(28),
        name="attention_backward",
    )(gmid, hid, *qkvs, *atts, *exps, *invs, wproj, rel, shift, keys, dqkv, uqkv, dproj, uproj)


def token_grad_kernel(gmid_hbm, x_hbm, gqkv_hbm, gain_ref, wqkv_ref, o0, o1, o2,
                      gmid_ref, x_ref, gqkv_ref, gh_ref, out_rows, sem, *, low, high):
    span = pl.ds(low, high - low)
    copies = [
        pltpu.make_async_copy(src.at[span, :], dst, sem.at[i])
        for i, (src, dst) in enumerate(((gqkv_hbm, gqkv_ref), (x_hbm, x_ref), (gmid_hbm, gmid_ref)))
    ]
    for copy in copies:
        copy.start()
    copies[0].wait()
    gh_ref[...] = nt(gqkv_ref[...], wqkv_ref[...])
    copies[1].wait()
    copies[2].wait()
    gain = gain_ref[...]
    step = (high - low) // 2

    def norm_step(i, carry):
        rows = pl.ds(pl.multiple_of(i * step, 16), step)
        normed, inv_std = normalize(x_ref[rows, :].astype(F32))
        back = norm_back(gh_ref[rows, :] * gain, normed, inv_std)
        out_rows[rows, :] = (gmid_ref[rows, :] + back).astype(BF)
        return carry

    lax.fori_loop(0, 2, norm_step, 0)
    split_pieces(out_rows, (o0, o1, o2))


def token_grad(gmid, x, gqkv, gain, wqkv, low, high):
    count = high - low
    hbm = pl.BlockSpec(memory_space=pl.ANY)
    return pl.pallas_call(
        functools.partial(token_grad_kernel, low=low, high=high),
        out_shape=pieces_of(count),
        in_specs=[hbm, hbm, hbm, vm(), vm()],
        out_specs=[vm()] * 3,
        scratch_shapes=[
            pltpu.VMEM((count, D), F32), pltpu.VMEM((count, D), BF), pltpu.VMEM((count, 3 * D), BF),
            pltpu.VMEM((count, D), F32), pltpu.VMEM((count, D), BF), pltpu.SemaphoreType.DMA((3,)),
        ],
        compiler_params=params(28),
        cost_estimate=cost(8),
        name="token_gradient",
    )(gmid, x, gqkv, gain, wqkv)


def grad_pack_kernel(where_ref, down_q, up_q, down_p, up_p, down1, up1, down2, up2, o0, o1, o2, o3, buf_ref):
    mine = where_ref[0]
    for k in range(4):
        for i, ref in enumerate((down_q, down1, up_p, up2)):
            buf_ref[k, :RANK, QUART * i : QUART * (i + 1)] = ref[:, QUART * k : QUART * (k + 1)]
    for dest in range(4):
        k = jnp.bitwise_xor(mine, dest)
        ranks = slice(RANK // 4 * dest, RANK // 4 * (dest + 1))
        for j in range(4):
            base = RANK + 12 * j
            for t in range(3):
                buf_ref[k, base : base + 4, QUART * t : QUART * (t + 1)] = up_q[
                    ranks, D * t + QUART * j : D * t + QUART * (j + 1)
                ]
            buf_ref[k, base : base + 4, 3 * QUART :] = down_p[ranks, QUART * j : QUART * (j + 1)]
            buf_ref[k, base + 4 : base + 8, :] = up1[ranks, D * j : D * (j + 1)]
            buf_ref[k, base + 8 : base + 12, :] = down2[ranks, D * j : D * (j + 1)]
    for k, out in enumerate((o0, o1, o2, o3)):
        out[...] = buf_ref[k].astype(BF)


def grad_pack(where, *grads):
    return pl.pallas_call(
        grad_pack_kernel,
        out_shape=(jax.ShapeDtypeStruct((4 * RANK, D), BF),) * 4,
        in_specs=[sm()] + [vm()] * 8,
        out_specs=[vm()] * 4,
        scratch_shapes=[pltpu.VMEM((4, 4 * RANK, D), F32)],
        compiler_params=params(8),
        cost_estimate=cost(2),
        name="adapter_grad_pack",
    )(where, *grads)


def grad_sum_kernel(g0, g1, g2, g3, o0, o1, o2, o3, buf_ref):
    total = g0[...].astype(F32) + g1[...].astype(F32) + g2[...].astype(F32) + g3[...].astype(F32)
    buf_ref[...] = jnp.zeros_like(buf_ref)
    buf_ref[:RANK, :] = total[:RANK, :]
    for j, out in enumerate((o0, o1, o2, o3)):
        buf_ref[RANK : RANK + 12, :] = total[RANK + 12 * j : RANK + 12 * (j + 1), :]
        out[...] = buf_ref[...].astype(BF)


def grad_sum(pieces):
    return pl.pallas_call(
        grad_sum_kernel,
        out_shape=(jax.ShapeDtypeStruct((2 * RANK, D), BF),) * 4,
        in_specs=[vm()] * 4,
        out_specs=[vm()] * 4,
        scratch_shapes=[pltpu.VMEM((2 * RANK, D), F32)],
        compiler_params=params(4),
        cost_estimate=cost(2),
        name="adapter_grad_sum",
    )(*pieces)


def grad_adapters_kernel(index_ref, x_ref, qkv_dn, fc1_dn, proj_up, fc2_up, rest_ref, acc_ref):
    acc_ref[...] = jnp.zeros_like(acc_ref)

    def add(i, carry):
        acc_ref[index_ref[i]] += x_ref[i].astype(F32)
        return carry

    lax.fori_loop(0, x_ref.shape[0], add, 0)
    for i, ref in enumerate((qkv_dn, fc1_dn, proj_up, fc2_up)):
        ref[...] = acc_ref[:, :RANK, QUART * i : QUART * (i + 1)]
    rest_ref[...] = acc_ref[:, RANK:, :].astype(BF)


def grad_adapters(index, x):
    s = lambda n, dtype=F32: jax.ShapeDtypeStruct((ADAPT, RANK, n), dtype)
    return pl.pallas_call(
        grad_adapters_kernel,
        out_shape=(s(QUART), s(QUART), s(QUART), s(QUART), s(D, BF)),
        in_specs=[sm(), vm()],
        out_specs=[vm()] * 5,
        scratch_shapes=[pltpu.VMEM((ADAPT, 2 * RANK, D), F32)],
        compiler_params=params(8),
        cost_estimate=cost(2),
        name="adapter_grad_by_adapter",
    )(index, x)


def grad_join_kernel(where_ref, r0, r1, r2, r3, qkv_up, proj_dn, fc1_up, fc2_dn, buf_ref):
    mine = where_ref[0]
    heads = qkv_up.shape[2] // (3 * HD)
    for k, ref in enumerate((r0, r1, r2, r3)):
        buf_ref[jnp.bitwise_xor(mine, k)] = ref[...].astype(F32)
    for source in range(4):
        ranks = slice(RANK // 4 * source, RANK // 4 * (source + 1))
        for h in range(heads):
            for t in range(3):
                qkv_up[:, ranks, HD * (3 * h + t) : HD * (3 * h + t + 1)] = buf_ref[
                    source, :, 0:4, QUART * t + HD * h : QUART * t + HD * (h + 1)
                ]
        proj_dn[:, ranks, :] = buf_ref[source, :, 0:4, 3 * QUART :]
        fc1_up[:, ranks, :] = buf_ref[source, :, 4:8, :]
        fc2_dn[:, ranks, :] = buf_ref[source, :, 8:12, :]


def grad_join(where, pieces):
    s = lambda n: jax.ShapeDtypeStruct((ADAPT, RANK, n), F32)
    return pl.pallas_call(
        grad_join_kernel,
        out_shape=(s(3 * QUART), s(QUART), s(D), s(D)),
        in_specs=[sm()] + [vm()] * 4,
        out_specs=[vm()] * 4,
        scratch_shapes=[pltpu.VMEM((4, ADAPT, RANK, D), F32)],
        compiler_params=params(12),
        cost_estimate=cost(2),
        name="adapter_grad_join",
    )(where, *pieces)


def flip(values, axis, distance):
    size = lax.axis_size(axis)
    return lax.ppermute(values, axis, [(i, i ^ distance) for i in range(size)])


def send_rows(pieces):
    own, near, pair = pieces
    return [own, flip(near, "row", 1), flip(pair, "row", 2)]


def hand_on(pieces, *deps):
    own, near, crossed = pieces
    if deps:
        near, crossed = after((near, crossed), *deps)
    return [own, near, crossed, flip(crossed, "row", 1)]


def exchange(slots, axis):
    return [slots[0]] + [flip(slots[k], axis, k) for k in range(1, 4)]


def after(values, *deps):
    return lax.optimization_barrier((tuple(values), deps))[0]


def col_halves(half):
    return jnp.concatenate([flip(half, "col", j) for j in range(1, 4)], axis=0)


def col_pairs(half, other_row):
    two = jnp.concatenate([half, other_row], axis=0)
    return jnp.concatenate([other_row] + [flip(two, "col", j) for j in range(1, 4)], axis=0)


def rel_matrix(rel_h, rel_w):
    pad = jnp.zeros((32 - (2 * WIN - 1), HD), BF)
    block = jnp.concatenate([rel_h[::-1], pad, rel_w[::-1], pad], axis=0).T
    zero = jnp.zeros((HD, HD), BF)
    return jnp.concatenate(
        [jnp.concatenate([zero, block], axis=1), jnp.concatenate([block, zero], axis=1)], axis=0
    )


def body(
    tokens, grad_out, adapter_index, norm1_gain, norm2_gain, qkv_weight, proj_weight, fc1_weight, fc2_weight,
    rel_h, rel_w, qkv_down, qkv_up, proj_down, proj_up, fc1_down, fc1_up, fc2_down, fc2_up,
):
    members = lax.axis_size("col")
    batches = lax.axis_size("dp")
    row_index, col_index, dp_index = lax.axis_index("row"), lax.axis_index("col"), lax.axis_index("dp")
    half = dp_index % 2
    where = jnp.stack([row_index, half]).astype(jnp.int32)
    slot_images = (
        jnp.bitwise_xor(dp_index, jnp.arange(batches, dtype=jnp.int32))[:, None] * members
        + jnp.bitwise_xor(col_index, jnp.arange(members, dtype=jnp.int32))[None, :]
    ).reshape(-1)
    slot_adapters = jnp.sum(
        jnp.where(
            slot_images[:, None] == jnp.arange(adapter_index.shape[0], dtype=jnp.int32)[None, :],
            adapter_index[:, 0][None, :],
            0,
        ),
        axis=1,
    )
    pick = jnp.concatenate([slot_adapters[:4], half[None]]).astype(jnp.int32)
    swap = lambda m: jnp.swapaxes(m, 1, 2)

    rel = rel_matrix(rel_h, rel_w)
    shift, keys = jnp.asarray(SHIFT_NP), jnp.asarray(KEYS_NP)

    *token_slots, alpha_own, beta_own, alpha_half, beta_half = front(where, tokens, qkv_weight, proj_weight)
    cut = lambda m: lax.dynamic_slice_in_dim(m, half * HBLK, HBLK, 0)
    b0 = flip(beta_half, "row", 2)
    alpha_near = col_halves(alpha_half)
    x_pieces = send_rows(token_slots)
    *send, row_adapters = adapter_pack(
        pick, qkv_up, swap(proj_down), fc1_up, swap(fc2_down), swap(qkv_down), swap(fc1_down), proj_up, fc2_up,
        norm1_gain.reshape(1, -1), norm2_gain.reshape(1, -1),
    )
    beta_sent = [jnp.concatenate([beta_half, b0, send[j]], axis=0) for j in range(1, 4)]
    beta_got = [flip(m, "col", j) for j, m in enumerate(beta_sent, 1)]
    alpha_far = flip(alpha_near, "dp", 1)
    g = jnp.concatenate([alpha_own, alpha_near, alpha_far, row_adapters], axis=0)
    g, *x_pieces = after((g, *x_pieces))
    gy = flip(g, "row", 2)
    grad_slots = pack(where, grad_out)
    *beta_got, _ = after((*beta_got, grad_slots[0]))
    beta_near = jnp.concatenate([b0] + [m[:QUART] for m in beta_got], axis=0)
    col_adapters = [send[0]] + beta_got
    beta_far = flip(beta_near, "dp", 1)
    x_pieces = hand_on(x_pieces)

    fc1_half, = after((cut(fc1_weight),), *beta_got)
    fc2_half, = after((cut(fc2_weight),), gy)
    c0 = flip(fc2_half, "row", 2)
    fc1_near = [flip(fc1_half, "col", j) for j in range(1, 4)]

    *fc1_near, g, gy, beta_own, beta_near, beta_far = after((*fc1_near, g, gy, beta_own, beta_near, beta_far))
    alpha1 = [g, flip(g, "row", 1), gy, flip(gy, "row", 1)]
    beta1 = [beta_own, beta_near, beta_far] + [flip(m, "row", 1) for m in (beta_own, beta_near, beta_far)]
    grad_slots = after(tuple(grad_slots), gy)
    g_pieces = send_rows(grad_slots)
    two = jnp.concatenate([fc2_half, c0], axis=0)
    fc2_near = [flip(two, "col", j) for j in range(1, 4)]
    fc1_near = jnp.concatenate(fc1_near, axis=0)
    fc1_far = flip(fc1_near, "dp", 1)
    h = jnp.concatenate([fc1_weight, fc1_near, fc1_far], axis=0)
    alpha1[0], h, *g_pieces = after((alpha1[0], h, *g_pieces))
    hy = flip(h, "row", 2)
    wqkv, wproj, dqkv, uqkv, dproj, uproj, d1, u1, d2, u2, gain1, gain2 = prep1(
        where, alpha1, beta1, col_adapters
    )
    wqkv, *fc2_near = after((wqkv, *fc2_near))
    fc2_near = jnp.concatenate([c0] + fc2_near, axis=0)
    fc2_far = flip(fc2_near, "dp", 1)
    x, hid, *qkvs = qkv_rows(x_pieces, gain1, wqkv)
    g_pieces = hand_on(g_pieces, qkvs[0])
    part0 = attention(0, qkvs[0], rel, shift, keys)
    qkv1, = after((qkvs[1],), part0[0])
    part1 = attention(1, qkv1, rel, shift, keys)
    qkv2, _ = after((qkvs[2], part1[0]))
    part2 = attention(2, qkv2, rel, shift, keys)
    atts, exps, invs = zip(part0, part1, part2)
    atts = list(atts)
    atts[2], hy = after((atts[2], hy))
    alpha2 = [h, flip(h, "row", 1), hy, flip(hy, "row", 1)]
    middle = project(x, atts, wproj)
    middle, fc2_far = after((middle, fc2_far))
    beta2 = [fc2_weight, fc2_near, fc2_far] + [flip(m, "row", 1) for m in (fc2_weight, fc2_near, fc2_far)]

    *out_slots, gmid, down1, up1, down2, up2 = mlp(where, middle, g_pieces, gain2, alpha2, beta2, d1, u1, d2, u2)
    out_pieces = send_rows(out_slots)
    gqkv, down_q, up_q, down_p, up_p = attention_back(
        gmid, hid, qkvs, atts, exps, invs, wproj, rel, shift, keys, dqkv, uqkv, dproj, uproj
    )
    out_pieces = hand_on(out_pieces, gqkv)
    gqkv, down_q, up_q, down_p, up_p = after((gqkv, down_q, up_q, down_p, up_p), *out_pieces[:3])
    packed = grad_pack(where, down_q, up_q, down_p, up_p, down1, up1, down2, up2)
    *packed, gqkv = after((*packed, gqkv))
    row_sums = exchange(packed, "row")
    back0 = token_grad(gmid, x, gqkv, gain1, wqkv, *TAIL[0])
    *row_sums, gqkv, b0, b1, b2 = after((*row_sums, gqkv, *back0))
    back_pieces = send_rows((b0, b1, b2))
    summed = grad_sum(row_sums)
    *summed, gqkv = after((*summed, gqkv))
    images = exchange(summed, "col")
    back1 = token_grad(gmid, x, gqkv, gain1, wqkv, *TAIL[1])
    last_pieces = send_rows(back1)
    *images, near, crossed = after((*images, *back_pieces[1:]), back1[0])
    back_pieces = hand_on([back_pieces[0], near, crossed])
    images = jnp.stack(images)
    images, *out_pieces = after((images, *out_pieces))
    step = 1
    while step < batches:
        images = jnp.concatenate([images, flip(images, "dp", step)], axis=0)
        step *= 2
    result = unpack(where, out_pieces, BF)
    images, = after((images,), result)
    qkv_dn, fc1_dn, proj_upg, fc2_upg, rest = grad_adapters(slot_adapters.astype(jnp.int32), images)
    rests = [rest] + [flip(rest, "row", k) for k in range(1, 4)]
    grad_tokens = unpack(where, back_pieces + hand_on(last_pieces, rest), F32, TAIL)
    rests = after(tuple(rests), grad_tokens)
    qkv_upg, proj_dn, fc1_upg, fc2_dn = grad_join(where, rests)
    return (
        result, grad_tokens,
        swap(qkv_dn), qkv_upg, swap(proj_dn), proj_upg, swap(fc1_dn), fc1_upg, swap(fc2_dn), fc2_upg,
    )


def solution(mesh):
    return jax.shard_map(
        body,
        mesh=mesh,
        in_specs=(
            P("row", ("dp", "col")), P("row", ("dp", "col")), P(), P("row"), P("row"),
            P("row", "col"), P("col", "row"), P("row", "col"), P("row", "col"), P(), P(),
            P(None, "row", None), P(None, None, "col"), P(None, "col", None), P(None, None, "row"),
            P(None, "row", None), P(None, None, "col"), P(None, "col", None), P(None, None, "row"),
        ),
        out_specs=(
            P("row", ("dp", "col")), P("row", ("dp", "col")),
            P(None, "row", None), P(None, None, "col"), P(None, "col", None), P(None, None, "row"),
            P(None, "row", None), P(None, None, "col"), P(None, "col", None), P(None, None, "row"),
        ),
        check_vma=False,
    )
```

```python
import functools

import jax
import jax.numpy as jnp
import numpy as np
from jax import lax
from jax.experimental import pallas as pl
from jax.experimental.pallas import tpu as pltpu
from jax.sharding import PartitionSpec as P

D = 768
HD = 64
WIN = 14
SLOTS = WIN * WIN
SIDE = 64
ADAPT = 8
NWIN = 5
IMG_TOK = NWIN * NWIN * SLOTS
RANK = 16
EDGE = SIDE - (NWIN - 1) * WIN
QUART = D // 4
FULLR = 208
KEYS = 208
EDGER = EDGE * WIN
CORNR = EDGE * EDGE
ROWS = 4 * FULLR + 2 * EDGER + CORNR
HALF = ROWS // 2
HBLK = QUART // 2
EPSILON = 1e-06
BF = jnp.bfloat16
F32 = jnp.float32

FULL, RIGHT, BOTTOM, CORNER = 0, 1, 2, 3
NQ = (FULLR, EDGER, EDGER, CORNR)
OFFS = (0, 4 * FULLR, 4 * FULLR + EDGER, 4 * FULLR + 2 * EDGER)


def slot_order(kind):
    rows = EDGE if kind in (BOTTOM, CORNER) else WIN
    cols = EDGE if kind in (RIGHT, CORNER) else WIN
    kept = [a * WIN + b for a in range(rows) for b in range(cols)]
    rest = [s for s in range(SLOTS) if s not in set(kept)]
    return kept, kept + rest


def build_tables():
    shift = np.zeros((4, FULLR, 128), np.int32)
    keys = np.zeros((4, KEYS, 128), np.float32)
    for kind in range(4):
        kept, order = slot_order(kind)
        for i, s in enumerate(kept):
            for base in (0, 64):
                shift[kind, i, base : base + 32] = WIN - 1 - s // WIN
                shift[kind, i, base + 32 : base + 64] = WIN - 1 - s % WIN
        spare = order[0] if kind == FULL else order[-1]
        for i, s in enumerate(order + [spare] * (KEYS - SLOTS)):
            for base in (0, 64):
                keys[kind, i, base + s // WIN] = 1.0
                keys[kind, i, base + 32 + s % WIN] = 1.0
    return shift, keys.astype(jnp.bfloat16)


SHIFT_NP, KEYS_NP = build_tables()


def nn(a, b):
    return jnp.dot(a, b, preferred_element_type=F32)


def nt(a, b):
    return lax.dot_general(a, b, (((1,), (1,)), ((), ())), preferred_element_type=F32)


def tn(a, b):
    return lax.dot_general(a, b, (((0,), (0,)), ((), ())), preferred_element_type=F32)


def vm():
    return pl.BlockSpec(memory_space=pltpu.VMEM)


def hbm():
    return pl.BlockSpec(memory_space=pl.ANY)


def in_hbm(x):
    return pltpu.with_memory_space_constraint(x, pltpu.HBM)


def arg():
    return pl.BlockSpec(memory_space=pltpu.HBM)


def sm():
    return pl.BlockSpec(memory_space=pltpu.SMEM)


def params(mib=60):
    return pltpu.CompilerParams(vmem_limit_bytes=mib * 1024 * 1024)


def cost(us):
    return pl.CostEstimate(flops=int(us * 1e6), transcendentals=0, bytes_accessed=0)


def place_window(kind, count, moved, width, spare=-100000):
    row = lax.broadcasted_iota(jnp.int32, (count, width), 0)
    lane = lax.broadcasted_iota(jnp.int32, (count, width), 1)
    if kind in (RIGHT, CORNER):
        src = (row // EDGE) * WIN + row % EDGE
    else:
        src = jnp.where(row < SLOTS, row, spare)
    return (lane == src + moved).astype(F32).astype(BF)


def window_list(dest):
    items = [(FULL, FULLR * j, NWIN * dest + j) for j in range(4)]
    items.append((RIGHT, OFFS[1], NWIN * dest + 4))
    items.append((BOTTOM, OFFS[2], NWIN * 4 + dest))
    if dest == 3:
        items.append((CORNER, OFFS[3], NWIN * NWIN - 1))
    return items


def window_span(window):
    start = window * SLOTS
    low = start // 128 * 128
    high = min(-(-(start + SLOTS) // 128) * 128, IMG_TOK)
    return low, high, start - low


def pack_rows(mine, x_ref, rows_ref, spare):
    for dest in range(4):
        slot = jnp.bitwise_xor(mine, dest)
        if dest != 3:
            rows_ref[slot, OFFS[3] :, :] = jnp.zeros((CORNR, QUART), BF)
        for kind, offset, window in window_list(dest):
            low, high, moved = window_span(window)
            pick = place_window(kind, NQ[kind], moved, high - low, spare)
            rows_ref[slot, offset : offset + NQ[kind], :] = nt(pick, x_ref[:, low:high]).astype(BF)


def fold(rows_ref, outs):
    half = rows_ref.shape[1] // 2
    for slot, (out, base) in enumerate(((outs[0], 0), (outs[1], 0), (outs[2], 0), (outs[2], half))):
        out[base : base + half, :QUART] = rows_ref[slot, :half, :]
        out[base : base + half, QUART:] = rows_ref[slot, half:, :]


def pack_kernel(where_ref, x_hbm, o0, o1, o2, rows_ref, x_ref, sem):
    load = pltpu.make_async_copy(x_hbm, x_ref, sem)
    load.start()
    load.wait()
    pack_rows(where_ref[0], x_ref, rows_ref, -100000)
    fold(rows_ref, (o0, o1, o2))


def pieces_of(rows):
    piece = lambda n: jax.ShapeDtypeStruct((n, 2 * QUART), BF)
    return (piece(rows // 2), piece(rows // 2), piece(rows))


def pack(where, x):
    return pl.pallas_call(
        pack_kernel,
        out_shape=pieces_of(ROWS),
        in_specs=[sm(), arg()],
        out_specs=[vm()] * 3,
        scratch_shapes=[
            pltpu.VMEM((4, ROWS, QUART), BF), pltpu.VMEM((QUART, IMG_TOK), BF), pltpu.SemaphoreType.DMA,
        ],
        compiler_params=params(16),
        cost_estimate=cost(4),
        name="pack",
    )(where, in_hbm(x))


def front_kernel(
    where_ref, x_hbm, qkv_hbm, proj_hbm, o0, o1, o2, alpha_ref, beta_ref, alpha_half, beta_half,
    rows_ref, x_ref, qkv_w, proj_w, sem,
):
    loads = [
        pltpu.make_async_copy(src, dst, sem.at[i])
        for i, (src, dst) in enumerate(((qkv_hbm, qkv_w), (proj_hbm, proj_w), (x_hbm, x_ref)))
    ]
    for load in loads:
        load.start()
    loads[0].wait()
    loads[1].wait()
    heads = qkv_w.shape[1] // (3 * HD)
    for h in range(heads):
        for t in range(3):
            ref, base = (alpha_ref, QUART * t) if t < 2 else (beta_ref, 0)
            ref[:, base + HD * h : base + HD * (h + 1)] = qkv_w[:, HD * (3 * h + t) : HD * (3 * h + t + 1)]
    beta_ref[:, QUART:] = proj_w[...]
    rows = pl.ds(pl.multiple_of(where_ref[1] * HBLK, 32), HBLK)
    alpha_half[...] = alpha_ref[rows, :]
    beta_half[...] = beta_ref[rows, :]
    loads[2].wait()
    pack_rows(where_ref[0], x_ref, rows_ref, 0)
    fold(rows_ref, (o0, o1, o2))


def front(where, x, qkv_w, proj_w):
    s = lambda *shape: jax.ShapeDtypeStruct(shape, BF)
    return pl.pallas_call(
        front_kernel,
        out_shape=pieces_of(ROWS)
        + (s(QUART, 2 * QUART), s(QUART, 2 * QUART), s(HBLK, 2 * QUART), s(HBLK, 2 * QUART)),
        in_specs=[sm(), arg(), arg(), arg()],
        out_specs=[vm()] * 7,
        scratch_shapes=[
            pltpu.VMEM((4, ROWS, QUART), BF), pltpu.VMEM((QUART, IMG_TOK), BF),
            pltpu.VMEM(qkv_w.shape, BF), pltpu.VMEM(proj_w.shape, BF), pltpu.SemaphoreType.DMA((3,)),
        ],
        compiler_params=params(16),
        cost_estimate=cost(5),
        name="token_and_weight_pack",
    )(where, in_hbm(x), in_hbm(qkv_w), in_hbm(proj_w))


def unpack_kernel(where_ref, *refs, bounds):
    pieces, (out_ref, acc_ref, rows_ref) = refs[:-3], refs[-3:]
    mine = where_ref[0]
    acc_ref[...] = jnp.zeros_like(acc_ref)
    index = 0
    for low, high in bounds:
        half = (high - low) // 2
        for slot in range(4):
            piece = pieces[index]
            rows = slice(half, 2 * half) if slot == 3 else slice(0, half)
            rows_ref[slot, low : low + half, :] = piece[rows, :QUART]
            rows_ref[slot, low + half : high, :] = piece[rows, QUART:]
            index += 1

    for source in range(4):
        slot = jnp.bitwise_xor(mine, source)
        for kind, offset, window in window_list(source):
            low, high, moved = window_span(window)
            pick = place_window(kind, NQ[kind], moved, high - low)
            acc_ref[:, low:high] += tn(rows_ref[slot, offset : offset + NQ[kind], :], pick)
    out_ref[...] = acc_ref[:, :IMG_TOK].astype(out_ref.dtype)


def unpack(where, pieces, dtype, bounds=((0, ROWS),)):
    return pl.pallas_call(
        functools.partial(unpack_kernel, bounds=bounds),
        out_shape=jax.ShapeDtypeStruct((QUART, IMG_TOK), dtype),
        in_specs=[sm()] + [vm()] * len(pieces),
        out_specs=vm(),
        scratch_shapes=[
            pltpu.VMEM((QUART, -(-IMG_TOK // 128) * 128), F32),
            pltpu.VMEM((4, ROWS, QUART), BF),
        ],
        compiler_params=params(24),
        cost_estimate=cost(4),
        name="unpack",
    )(where, *pieces)


def join_pieces(pieces, dst_ref):
    for slot, piece in enumerate(pieces):
        rows = slice(HALF, ROWS) if slot == 3 else slice(0, HALF)
        dst_ref[:HALF, QUART * slot : QUART * (slot + 1)] = piece[rows, :QUART]
        dst_ref[HALF:, QUART * slot : QUART * (slot + 1)] = piece[rows, QUART:]


def split_pieces(src_ref, outs):
    half = src_ref.shape[0] // 2
    for slot, (out, base) in enumerate(((outs[0], 0), (outs[1], 0), (outs[2], 0), (outs[2], half))):
        out[base : base + half, :QUART] = src_ref[:half, QUART * slot : QUART * (slot + 1)]
        out[base : base + half, QUART:] = src_ref[half:, QUART * slot : QUART * (slot + 1)]


def adapter_pack_kernel(
    pick_ref, qkv_up_hbm, proj_dn_hbm, fc1_up_hbm, fc2_dn_hbm, qkv_dn_hbm, fc1_dn_hbm, proj_up_hbm, fc2_up_hbm,
    gain1, gain2, rel_h, rel_w, s0, s1, s2, s3, row_ref, rel_ref,
    qkv_up, proj_dn, fc1_up, fc2_dn, qkv_dn, fc1_dn, proj_up, fc2_up, sem,
):
    pairs = []
    for j in range(4):
        for src, dst in ((qkv_up_hbm, qkv_up), (proj_dn_hbm, proj_dn), (fc1_up_hbm, fc1_up), (fc2_dn_hbm, fc2_dn)):
            pairs.append((src.at[pick_ref[j]], dst.at[j]))
    for src, dst in ((qkv_dn_hbm, qkv_dn), (fc1_dn_hbm, fc1_dn), (proj_up_hbm, proj_up), (fc2_up_hbm, fc2_up)):
        pairs.append((src.at[pick_ref[0]], dst.at[0]))
    loads = [pltpu.make_async_copy(src, dst, sem.at[i]) for i, (src, dst) in enumerate(pairs)]
    for load in loads:
        load.start()
    offsets = rel_h.shape[0]
    reverse = (
        lax.broadcasted_iota(jnp.int32, (offsets, 32), 0) + lax.broadcasted_iota(jnp.int32, (offsets, 32), 1)
        == offsets - 1
    ).astype(F32).astype(BF)
    rel_ref[...] = jnp.zeros_like(rel_ref)
    for i, table in enumerate((rel_h, rel_w)):
        block = tn(table[...], reverse).astype(BF)
        rel_ref[:HD, HD + 32 * i : HD + 32 * (i + 1)] = block
        rel_ref[HD:, 32 * i : 32 * (i + 1)] = block
    for load in loads:
        load.wait()
    heads = qkv_up.shape[2] // (3 * HD)
    half = 2 * QUART
    for j, send_ref in enumerate((s0, s1, s2, s3)):
        for h in range(heads):
            for t in range(3):
                row, base = (0, QUART * t) if t < 2 else (RANK, 0)
                send_ref[row : row + RANK, base + HD * h : base + HD * (h + 1)] = qkv_up[
                    j, :, HD * (3 * h + t) : HD * (3 * h + t + 1)
                ]
        send_ref[RANK : 2 * RANK, QUART:] = proj_dn[j]
        for i, ref in enumerate((fc1_up, fc2_dn)):
            for part in range(2):
                row = RANK * (2 + 2 * i + part)
                send_ref[row : row + RANK, :] = ref[j, :, half * part : half * (part + 1)]
    for i, ref in enumerate((qkv_dn, fc1_dn, proj_up, fc2_up)):
        row, base = RANK * (i // 2), QUART * (i % 2)
        row_ref[row : row + RANK, base : base + QUART] = ref[0]
    for i, ref in enumerate((gain1, gain2)):
        row_ref[2 * RANK :, QUART * i : QUART * (i + 1)] = jnp.broadcast_to(ref[...], (RANK, QUART))


def adapter_pack(pick, *mats):
    s = lambda *shape: jax.ShapeDtypeStruct(shape, BF)
    return pl.pallas_call(
        adapter_pack_kernel,
        out_shape=(s(6 * RANK, 2 * QUART),) * 4 + (s(3 * RANK, 2 * QUART), s(128, 128)),
        in_specs=[sm()] + [arg()] * 8 + [vm()] * 4,
        out_specs=[vm()] * 6,
        scratch_shapes=[pltpu.VMEM((4,) + m.shape[1:], BF) for m in mats[:4]]
        + [pltpu.VMEM((1,) + m.shape[1:], BF) for m in mats[4:8]]
        + [pltpu.SemaphoreType.DMA((20,))],
        compiler_params=params(8),
        cost_estimate=cost(2),
        name="adapter_pack",
    )(pick, *(in_hbm(m) for m in mats[:8]), *mats[8:])


def alpha_block(k, j):
    part = k
    if j == 0:
        return [(part, 0, QUART, None)]
    return [
        (part, QUART + HBLK * (j - 1), HBLK, 0),
        (part, QUART + 3 * HBLK + HBLK * (j - 1), HBLK, 1),
    ]


def beta_block(k, j):
    core, cross = k % 2, k // 2
    base = 3 * core
    if j == 0 and not cross:
        return [(base, 0, QUART, None)]
    row = 0 if j == 0 else HBLK + QUART * (j - 1) + HBLK * cross
    return [(base + 1, row, HBLK, 0), (base + 2, row, HBLK, 1)]


def block_dst(start, flag, half):
    if flag is None:
        return start
    offset = half if flag == 0 else 1 - half
    return pl.multiple_of(start + offset * HBLK, 32)


def prep1_kernel(
    where_ref, p0, p1, p2, p3, q0, q1, q2, q3, q4, q5, a0, a1, a2, a3,
    wqkv_ref, wproj_ref, dqkv, uqkv, dproj, uproj, d1, u1, d2, u2, gain1, gain2, ups, downs,
):
    half = where_ref[1]
    for j, a in enumerate((a0, a1, a2, a3)):
        base = a.shape[0] - 6 * RANK
        part = lambda i: slice(base + RANK * i, base + RANK * (i + 1))
        for t in range(3):
            uqkv[:, D * t + QUART * j : D * t + QUART * (j + 1)] = a[
                part(t // 2), QUART * (t % 2) : QUART * (t % 2 + 1)
            ]
        dproj[:, QUART * j : QUART * (j + 1)] = a[part(1), QUART:]
        for i in range(2):
            u1[:, D * j + D // 2 * i : D * j + D // 2 * (i + 1)] = a[part(2 + i), :]
            d2[:, D * j + D // 2 * i : D * j + D // 2 * (i + 1)] = a[part(4 + i), :]
    for k, ref in enumerate((p0, p1, p2, p3)):
        for i, dst in enumerate((dqkv, d1, uproj, u2)):
            rows = slice(D + RANK * (i // 2), D + RANK * (i // 2 + 1))
            dst[:, QUART * k : QUART * (k + 1)] = ref[rows, QUART * (i % 2) : QUART * (i % 2 + 1)]
        for i, dst in enumerate((gain1, gain2)):
            row = D + 2 * RANK
            dst[:, QUART * k : QUART * (k + 1)] = ref[row : row + 1, QUART * i : QUART * (i + 1)].astype(F32)
    alpha, beta = (p0, p1, p2, p3), (q0, q1, q2, q3, q4, q5)
    for k in range(4):
        for j in range(4):
            for part, row, count, flag in alpha_block(k, j):
                rows = pl.ds(block_dst(QUART * k, flag, half), count)
                for t in range(2):
                    wqkv_ref[rows, D * t + QUART * j : D * t + QUART * (j + 1)] = alpha[part][
                        row : row + count, QUART * t : QUART * (t + 1)
                    ]
            for part, row, count, flag in beta_block(k, j):
                rows = pl.ds(block_dst(QUART * k, flag, half), count)
                wqkv_ref[rows, 2 * D + QUART * j : 2 * D + QUART * (j + 1)] = beta[part][
                    row : row + count, :QUART
                ]
                rows = pl.ds(block_dst(QUART * j, flag, half), count)
                wproj_ref[rows, QUART * k : QUART * (k + 1)] = beta[part][row : row + count, QUART:]
    for t in range(3):
        ups[t] = uqkv[:, D * t : D * (t + 1)]
    ups[3] = uproj[...]
    for k in range(4):
        downs[k] = dqkv[:, QUART * k : QUART * (k + 1)]
        downs[4 + k] = dproj[:, QUART * k : QUART * (k + 1)]

    def merge(t, carry):
        cols = pl.ds(pl.multiple_of(D * t, 128), D)
        for k in range(4):
            rows = slice(QUART * k, QUART * (k + 1))
            wqkv_ref[rows, cols] = (wqkv_ref[rows, cols].astype(F32) + tn(downs[k], ups[t])).astype(BF)
        return carry

    lax.fori_loop(0, 3, merge, 0)
    for k in range(4):
        rows = slice(QUART * k, QUART * (k + 1))
        wproj_ref[rows, :] = (wproj_ref[rows, :].astype(F32) + tn(downs[4 + k], ups[3])).astype(BF)


def prep1(where, alpha, beta, cols):
    s = lambda *shape: jax.ShapeDtypeStruct(shape, BF)
    return pl.pallas_call(
        prep1_kernel,
        out_shape=(
            s(D, 3 * D), s(D, D), s(RANK, D), s(RANK, 3 * D), s(RANK, D), s(RANK, D),
            s(RANK, D), s(RANK, 4 * D), s(RANK, 4 * D), s(RANK, D),
            jax.ShapeDtypeStruct((1, D), F32), jax.ShapeDtypeStruct((1, D), F32),
        ),
        in_specs=[sm()] + [vm()] * 14,
        out_specs=[vm()] * 12,
        scratch_shapes=[pltpu.VMEM((4, RANK, D), BF), pltpu.VMEM((8, RANK, QUART), BF)],
        compiler_params=params(24),
        cost_estimate=cost(7),
        name="attention_weights",
    )(where, *alpha, *beta, *cols)


def normalize(values):
    center = jnp.sum(values, axis=1, keepdims=True) / D
    shifted = values - center
    inv_std = lax.rsqrt(jnp.sum(shifted * shifted, axis=1, keepdims=True) / D + EPSILON)
    return shifted * inv_std, inv_std


def norm_back(grad, normed, inv_std):
    first = jnp.sum(grad, axis=1, keepdims=True) / D
    second = jnp.sum(grad * normed, axis=1, keepdims=True) / D
    return inv_std * (grad - first - normed * second)


def barrel(values, amount, left):
    for bit in (1, 2, 4, 8):
        moved = pltpu.roll(values, (128 - bit) if left else bit, 1)
        values = jnp.where((amount & bit) != 0, moved, values)
    return values


def low_half(count):
    return lax.broadcasted_iota(jnp.int32, (count, 128), 1) < HD


def pad_rows(tile):
    if tile.shape[0] == KEYS:
        return tile
    return jnp.concatenate([tile, jnp.zeros((KEYS - tile.shape[0], tile.shape[1]), tile.dtype)], axis=0)


def live_rows():
    return lax.broadcasted_iota(jnp.int32, (KEYS, 128), 0) < SLOTS


GROUP = 6
GROUP_BACK = 6


def pair_columns(pair):
    return tuple(slice(D * t + 128 * pair, D * t + 128 * (pair + 1)) for t in range(3))


def attend_window(kind, row0, qkv_ref, att_ref, exp_ref, inv_ref, rel_ref, shift_ref, keys_ref):
    count = NQ[kind]
    rows = pl.ds(row0, count)
    low_q, low_k = low_half(count), low_half(KEYS)
    live = live_rows()
    ones = jnp.where(live, 1.0, 0.0).astype(BF)
    amount = shift_ref[kind, :count, :]
    onehot = keys_ref[kind]
    rel_mat = rel_ref[...]
    for first in range(0, D // 128, GROUP):
        pairs = range(first, first + GROUP)
        heads = [(pair, odd) for pair in pairs for odd in range(2)]
        q_tile = {p: qkv_ref[rows, pair_columns(p)[0]] for p in pairs}
        rel = {p: nn(q_tile[p], rel_mat) for p in pairs}
        rel = {p: barrel(rel[p], amount, True).astype(BF) for p in pairs}
        k_tile = {p: pad_rows(qkv_ref[rows, pair_columns(p)[1]] * BF(HD**-0.5)) for p in pairs}
        scores = {}
        for p, odd in heads:
            if odd:
                q_aug, k_aug = jnp.where(low_q, rel[p], q_tile[p]), jnp.where(low_k, onehot, k_tile[p])
            else:
                q_aug, k_aug = jnp.where(low_q, q_tile[p], rel[p]), jnp.where(low_k, k_tile[p], onehot)
            scores[p, odd] = nt(q_aug, k_aug)
        top = {h: jnp.max(scores[h], axis=1, keepdims=True) for h in heads}
        exponent = {h: jnp.exp(scores[h] - top[h]).astype(BF) for h in heads}
        both = {}
        for p, odd in heads:
            exp_ref[2 * p + odd, rows, :] = exponent[p, odd]
            v_tile = pad_rows(qkv_ref[rows, pair_columns(p)[2]])
            if kind == FULL:
                v_tile = jnp.where(live, v_tile, 0).astype(BF)
            v_aug = jnp.where(low_k, ones, v_tile) if odd else jnp.where(low_k, v_tile, ones)
            both[p, odd] = nn(exponent[p, odd], v_aug)
        for p in pairs:
            cols = pair_columns(p)[0]
            inverse = 1.0 / pltpu.roll(jnp.where(low_q, both[p, 1], both[p, 0]), HD, 1)
            inv_ref[rows, cols] = inverse
            att_ref[rows, cols] = (jnp.where(low_q, both[p, 0], both[p, 1]) * inverse).astype(BF)


PARTS = ((FULL, FULL), (FULL, FULL), (RIGHT, BOTTOM, CORNER))
PART_ROWS = tuple(sum(NQ[kind] for kind in part) for part in PARTS)
PART_OFFS = (0, PART_ROWS[0], PART_ROWS[0] + PART_ROWS[1])


TAIL = ((0, 576), (576, ROWS))


def qkv_kernel(
    x0, x1, x2, x3, gain_ref, w_hbm, x_hbm, hid_hbm, qkv_a, qkv_b, qkv_c,
    x_ref, hid_ref, rows_ref, w_ref, qkv_ref, sem, out_sem,
):
    loads = [
        pltpu.make_async_copy(w_hbm.at[:, D * t : D * (t + 1)], w_ref.at[t], sem.at[t]) for t in range(3)
    ]
    for load in loads:
        load.start()
    join_pieces((x0, x1, x2, x3), x_ref)
    kept = [
        pltpu.make_async_copy(src, dst, sem.at[3 + i])
        for i, (src, dst) in enumerate(((x_ref, x_hbm), (hid_ref, hid_hbm)))
    ]
    kept[0].start()
    gain = gain_ref[...]

    def norm_step(i, carry):
        rows = pl.ds(pl.multiple_of(i * 112, 16), 112)
        normed, _ = normalize(x_ref[rows, :].astype(F32))
        hidden = (normed * gain).astype(BF)
        rows_ref[rows, :] = hidden
        hid_ref[rows, :] = hidden
        return carry

    lax.fori_loop(0, ROWS // 112, norm_step, 0)
    for w in range(4):
        hid_ref[FULLR * w + SLOTS : FULLR * (w + 1), :] = jnp.zeros((FULLR - SLOTS, D), BF)
    kept[1].start()
    for load in loads:
        load.wait()

    def stores(t):
        cols = pl.ds(pl.multiple_of(D * t, 128), D)
        return [
            pltpu.make_async_copy(
                qkv_ref.at[t, pl.ds(offset, count), :], out.at[:, cols], out_sem.at[t, i]
            )
            for i, (out, offset, count) in enumerate(zip((qkv_a, qkv_b, qkv_c), PART_OFFS, PART_ROWS))
        ]

    def project_step(t, carry):
        qkv_ref[t] = nn(rows_ref[...], w_ref[t]).astype(BF)
        for store in stores(t):
            store.start()
        return carry

    lax.fori_loop(0, 3, project_step, 0)
    for t in range(3):
        for store in stores(t):
            store.wait()
    for store in kept:
        store.wait()


def qkv_rows(pieces, gain, wqkv):
    s = lambda *shape: jax.ShapeDtypeStruct(shape, BF)
    return pl.pallas_call(
        qkv_kernel,
        out_shape=(s(ROWS, D), s(ROWS, D)) + tuple(s(n, 3 * D) for n in PART_ROWS),
        in_specs=[vm()] * 5 + [hbm()],
        out_specs=[hbm()] * 5,
        scratch_shapes=[
            pltpu.VMEM((ROWS, D), BF), pltpu.VMEM((ROWS, D), BF), pltpu.VMEM((ROWS, D), BF),
            pltpu.VMEM((3, D, D), BF), pltpu.VMEM((3, ROWS, D), BF),
            pltpu.SemaphoreType.DMA((5,)), pltpu.SemaphoreType.DMA((3, 3)),
        ],
        compiler_params=params(32),
        cost_estimate=cost(10),
        name="norm_and_qkv",
    )(*pieces, gain, wqkv)


def attention_kernel(qkv_ref, rel_ref, shift_ref, keys_ref, att_ref, exp_ref, inv_ref, *, kinds):
    refs = (qkv_ref, att_ref, exp_ref, inv_ref, rel_ref, shift_ref, keys_ref)
    if kinds[0] == FULL:

        def step(w, carry):
            attend_window(FULL, pl.multiple_of(w * FULLR, 16), *refs)
            return carry

        lax.fori_loop(0, len(kinds), step, 0)
    else:
        row = 0
        for kind in kinds:
            attend_window(kind, row, *refs)
            row += NQ[kind]


def attention(part, qkv, rel, shift, keys):
    rows = PART_ROWS[part]
    s = lambda *shape, dtype=BF: jax.ShapeDtypeStruct(shape, dtype)
    return pl.pallas_call(
        functools.partial(attention_kernel, kinds=PARTS[part]),
        out_shape=(s(rows, D), s(D // HD, rows, KEYS), s(rows, D, dtype=F32)),
        in_specs=[vm()] * 4,
        out_specs=[vm()] * 3,
        compiler_params=params(24),
        cost_estimate=cost(10),
        name="attention_forward",
    )(qkv, rel, shift, keys)


def project_kernel(x_ref, att_a, att_b, att_c, wproj_ref, middle_ref):
    for ref, offset, count in zip((att_a, att_b, att_c), PART_OFFS, PART_ROWS):
        rows = slice(offset, offset + count)
        middle_ref[rows, :] = x_ref[rows, :].astype(F32) + nn(ref[...], wproj_ref[...])


def project(x, atts, wproj):
    return pl.pallas_call(
        project_kernel,
        out_shape=jax.ShapeDtypeStruct((ROWS, D), F32),
        in_specs=[vm()] * 5,
        out_specs=vm(),
        compiler_params=params(20),
        cost_estimate=cost(5),
        name="projection",
    )(x, *atts, wproj)


CHUNK = 512
LOCK = 1


def mlp_kernel(
    where_ref, middle_ref, g0, g1, g2, g3, gain_ref,
    p0, p1, p2, p3, q0, q1, q2, q3, q4, q5, d1, u1, d2, u2,
    o0, o1, o2, gmid_ref, down1, up1, down2, up2,
    gm_ref, out_rows, h2_ref, acc_mlp, acc_gh, gu1, ad2, w1_ref, w2_ref, downs, sem,
):
    half = where_ref[1]
    copies = []

    def fetch(src, dst):
        copies.append(pltpu.make_async_copy(src, dst, sem.at[len(copies)]))
        copies[-1].start()

    alpha, beta = (p0, p1, p2, p3), (q0, q1, q2, q3, q4, q5)
    for k in range(4):
        for j in range(4):
            for part, row, count, flag in alpha_block(k, j):
                rows = pl.ds(block_dst(QUART * k, flag, half), count)
                fetch(alpha[part].at[row : row + count, :], w1_ref.at[rows, D * j : D * (j + 1)])
            for part, row, count, flag in beta_block(k, j):
                rows = pl.ds(block_dst(QUART * k, flag, half), count)
                fetch(beta[part].at[row : row + count, :], w2_ref.at[rows, D * j : D * (j + 1)])
    join_pieces((g0, g1, g2, g3), gm_ref)
    for k in range(4):
        downs[k] = d1[:, QUART * k : QUART * (k + 1)]
        downs[4 + k] = u2[:, QUART * k : QUART * (k + 1)]
    for copy in copies:
        copy.wait()

    def merge(j, carry):
        cols = pl.ds(pl.multiple_of(D * j, 128), D)
        for k in range(4):
            rows = slice(QUART * k, QUART * (k + 1))
            w1_ref[rows, cols] = (w1_ref[rows, cols].astype(F32) + tn(downs[k], u1[:, cols])).astype(BF)
            w2_ref[rows, cols] = (w2_ref[rows, cols].astype(F32) + tn(downs[4 + k], d2[:, cols])).astype(BF)
        return carry

    lax.fori_loop(0, 4, merge, 0)
    gain = gain_ref[...]
    down1[...] = jnp.zeros_like(down1)
    up1[...] = jnp.zeros_like(up1)
    down2[...] = jnp.zeros_like(down2)
    up2[...] = jnp.zeros_like(up2)

    def tile_step(t, carry):
        rows = pl.ds(pl.multiple_of(t * HALF, 16), HALF)
        normed, _ = normalize(middle_ref[rows, :])
        h2 = (normed * gain).astype(BF)
        h2_ref[...] = h2
        gm = gm_ref[rows, :]
        ad1 = nt(d1[...], h2).astype(BF)
        gu2 = nt(u2[...], gm).astype(BF)
        acc_mlp[...] = jnp.zeros_like(acc_mlp)
        acc_gh[...] = jnp.zeros_like(acc_gh)
        gu1[...] = jnp.zeros_like(gu1)
        ad2[...] = jnp.zeros_like(ad2)

        def chunk_step(c, inner_carry):
            spans = [
                pl.ds(pl.multiple_of((c * LOCK + i) * CHUNK, CHUNK), CHUNK) for i in range(LOCK)
            ]
            h2 = h2_ref[...]
            gm = gm_ref[rows, :]
            inner = [nn(h2, w1_ref[:, span]) for span in spans]
            gact = [nn(gm, w2_ref[:, span]) for span in spans]
            act, ginner = [], []
            for i in range(LOCK):
                half = 0.5 * (1.0 + lax.erf(inner[i] * 2**-0.5))
                act.append((inner[i] * half).astype(BF))
                slope = half + inner[i] * (jnp.exp(-0.5 * inner[i] * inner[i]) * (2 * np.pi) ** -0.5)
                ginner.append((gact[i] * slope).astype(BF))
            for i, span in enumerate(spans):
                acc_mlp[...] += nt(act[i], w2_ref[:, span])
                acc_gh[...] += nt(ginner[i], w1_ref[:, span])
                up1[:, span] += nn(ad1, ginner[i])
                gu1[...] += nt(u1[:, span], ginner[i])
                ad2[...] += nt(d2[:, span], act[i])
                down2[:, span] += nn(gu2, act[i])
            return inner_carry

        lax.fori_loop(0, 4 * D // (CHUNK * LOCK), chunk_step, 0)
        down1[...] += nn(gu1[...].astype(BF), h2_ref[...])
        up2[...] += nn(ad2[...].astype(BF), gm_ref[rows, :])
        middle = middle_ref[rows, :]
        out_rows[rows, :] = (middle + acc_mlp[...]).astype(BF)
        normed, inv_std = normalize(middle)
        gmid_ref[rows, :] = gm_ref[rows, :].astype(F32) + norm_back(acc_gh[...] * gain, normed, inv_std)
        return carry

    lax.fori_loop(0, 2, tile_step, 0)
    split_pieces(out_rows, (o0, o1, o2))


def mlp(where, middle, pieces, gain, alpha, beta, d1, u1, d2, u2):
    s = lambda *shape, dtype=F32: jax.ShapeDtypeStruct(shape, dtype)
    return pl.pallas_call(
        mlp_kernel,
        out_shape=pieces_of(ROWS)
        + (s(ROWS, D), s(RANK, D), s(RANK, 4 * D), s(RANK, 4 * D), s(RANK, D)),
        in_specs=[sm()] + [vm()] * 6 + [pl.BlockSpec(memory_space=pl.ANY)] * 10 + [vm()] * 4,
        out_specs=[vm()] * 8,
        scratch_shapes=[
            pltpu.VMEM((ROWS, D), BF), pltpu.VMEM((ROWS, D), BF), pltpu.VMEM((HALF, D), BF),
            pltpu.VMEM((HALF, D), F32), pltpu.VMEM((HALF, D), F32),
            pltpu.VMEM((RANK, HALF), F32), pltpu.VMEM((RANK, HALF), F32),
            pltpu.VMEM((D, 4 * D), BF), pltpu.VMEM((D, 4 * D), BF), pltpu.VMEM((8, RANK, QUART), BF),
            pltpu.SemaphoreType.DMA((4 * 4 * 4,)),
        ],
        compiler_params=params(48),
        cost_estimate=cost(48),
        name="mlp_forward_backward",
    )(where, middle, *pieces, gain, *alpha, *beta, d1, u1, d2, u2)


def attend_back_window(
    kind, row0, qkv_ref, att_ref, exp_ref, inv_ref, gatt_ref, gqkv_ref, rel_ref, shift_ref, keys_ref
):
    count = NQ[kind]
    rows = pl.ds(row0, count)
    low_q, low_k = low_half(count), low_half(KEYS)
    live = live_rows()
    lane_k = lax.broadcasted_iota(jnp.int32, (KEYS, 128), 1) % HD
    lane_q = lax.broadcasted_iota(jnp.int32, (count, 128), 1) % HD
    ones = jnp.where(live & (lane_k < 2), 1.0, 0.0).astype(BF)
    across = jnp.where(
        low_half(128) != (lax.broadcasted_iota(jnp.int32, (128, 128), 0) < HD), -1.0, 0.0
    ).astype(BF)
    amount = shift_ref[kind, :count, :]
    onehot = keys_ref[kind]
    rel_mat = rel_ref[...]
    for first in range(0, D // 128, GROUP_BACK):
        pairs = range(first, first + GROUP_BACK)
        heads = [(pair, odd) for pair in pairs for odd in range(2)]
        go_tile = {
            p: (gatt_ref[rows, pair_columns(p)[0]].astype(F32) * inv_ref[rows, pair_columns(p)[0]]).astype(BF)
            for p in pairs
        }
        delta = {
            p: nn((go_tile[p].astype(F32) * att_ref[rows, pair_columns(p)[0]].astype(F32)).astype(BF), across)
            for p in pairs
        }
        go_t = {p: go_tile[p].T for p in pairs}
        gv = {}
        for p, odd in heads:
            gv[p, odd] = nn(go_t[p][HD * odd : HD * (odd + 1), :], exp_ref[2 * p + odd, rows, :])
        gscore = {}
        for p in pairs:
            high = delta[p].astype(BF)
            rest = (delta[p] - high.astype(F32)).astype(BF)
            low_delta = jnp.where(lane_q == 0, high, jnp.where(lane_q == 1, rest, 0)).astype(BF)
            v_tile = pad_rows(qkv_ref[rows, pair_columns(p)[2]])
            if kind == FULL:
                v_tile = jnp.where(live, v_tile, 0).astype(BF)
            gscore[p, 0] = nt(jnp.where(low_q, go_tile[p], low_delta), jnp.where(low_k, v_tile, ones))
            gscore[p, 1] = nt(jnp.where(low_q, low_delta, go_tile[p]), jnp.where(low_k, ones, v_tile))
        q_t = {p: qkv_ref[rows, pair_columns(p)[0]].T for p in pairs}
        gs = {(p, odd): (exp_ref[2 * p + odd, rows, :].astype(F32) * gscore[p, odd]).astype(BF) for p, odd in heads}
        gk = {(p, odd): nn(q_t[p][HD * odd : HD * (odd + 1), :], gs[p, odd]) for p, odd in heads}
        gq = {}
        for p in pairs:
            k_tile = pad_rows(qkv_ref[rows, pair_columns(p)[1]] * BF(HD**-0.5))
            gq[p, 0] = nn(gs[p, 0], jnp.where(low_k, k_tile, onehot))
            gq[p, 1] = nn(gs[p, 1], jnp.where(low_k, onehot, k_tile))
        sums = {p: barrel(jnp.where(low_q, gq[p, 1], gq[p, 0]), amount, False).astype(BF) for p in pairs}
        for p in pairs:
            cols, kcols, vcols = pair_columns(p)
            gv_tile = jnp.concatenate([gv[p, 0], gv[p, 1]], axis=0).astype(BF).T
            gqkv_ref[rows, vcols] = gv_tile[:count, :]
            gk_tile = (jnp.concatenate([gk[p, 0], gk[p, 1]], axis=0) * HD**-0.5).astype(BF).T
            gqkv_ref[rows, kcols] = gk_tile[:count, :]
            gqkv_ref[rows, cols] = (jnp.where(low_q, gq[p, 0], gq[p, 1]) + nt(sums[p], rel_mat)).astype(BF)


def attention_back_kernel(
    gmid_hbm, hid_hbm, qkv_a, qkv_b, qkv_c, att_a, att_b, att_c, exp_a, exp_b, exp_c, inv_a, inv_b, inv_c,
    wproj_ref, rel_ref, shift_ref, keys_ref, dqkv, uqkv, dproj, uproj,
    gqkv_hbm, down_q, up_q, down_p, up_p,
    gmid_ref, hid_ref, qkv_ref, att_ref, exp_ref, inv_ref, gqkv_ref, gb_ref, gatt_ref, sem, out_sem,
):
    spans = [pl.ds(offset, count) for offset, count in zip(PART_OFFS, PART_ROWS)]
    pairs = [(gmid_hbm, gmid_ref)]
    for part, srcs in enumerate(
        ((qkv_a, inv_a, att_a, exp_a), (qkv_b, inv_b, att_b, exp_b), (qkv_c, inv_c, att_c, exp_c))
    ):
        rows = spans[part]
        for src, dst in zip(srcs, (qkv_ref, inv_ref, att_ref)):
            pairs.append((src, dst.at[rows, :]))
        pairs.append((srcs[3], exp_ref.at[:, rows, :]))
    pairs.append((hid_hbm, hid_ref))
    loads = [pltpu.make_async_copy(src, dst, sem.at[i]) for i, (src, dst) in enumerate(pairs)]
    for load in loads:
        load.start()

    def wait_part(part):
        for load in loads[1 + 4 * part : 5 + 4 * part]:
            load.wait()

    stores = [
        pltpu.make_async_copy(gqkv_ref.at[rows, :], gqkv_hbm.at[rows, :], out_sem.at[i])
        for i, rows in enumerate(spans)
    ]
    loads[0].wait()
    gb_ref[...] = gmid_ref[...].astype(BF)
    gatt_ref[...] = nt(gb_ref[...], wproj_ref[...]).astype(BF)
    refs = (qkv_ref, att_ref, exp_ref, inv_ref, gatt_ref, gqkv_ref, rel_ref, shift_ref, keys_ref)

    def step(w, carry):
        for part in range(2):

            @pl.when(w == 2 * part)
            def _():
                wait_part(part)

        attend_back_window(FULL, pl.multiple_of(w * FULLR, 16), *refs)
        return carry

    lax.fori_loop(0, 4, step, 0)
    stores[0].start()
    stores[1].start()
    wait_part(2)
    for kind in (RIGHT, BOTTOM, CORNER):
        attend_back_window(kind, OFFS[kind], *refs)
    stores[2].start()
    up_p[...] = nn(nt(dproj[...], att_ref[...]).astype(BF), gb_ref[...])
    down_p[...] = nn(nt(uproj[...], gb_ref[...]).astype(BF), att_ref[...])
    loads[-1].wait()
    up_q[...] = nn(nt(dqkv[...], hid_ref[...]).astype(BF), gqkv_ref[...])
    down_q[...] = nn(nt(uqkv[...], gqkv_ref[...]).astype(BF), hid_ref[...])
    for store in stores:
        store.wait()


def attention_back(gmid, hid, qkvs, atts, exps, invs, wproj, rel, shift, keys, dqkv, uqkv, dproj, uproj):
    s = lambda *shape, dtype=F32: jax.ShapeDtypeStruct(shape, dtype)
    return pl.pallas_call(
        attention_back_kernel,
        out_shape=(s(ROWS, 3 * D, dtype=BF), s(RANK, D), s(RANK, 3 * D), s(RANK, D), s(RANK, D)),
        in_specs=[hbm()] * 14 + [vm()] * 8,
        out_specs=[hbm()] + [vm()] * 4,
        scratch_shapes=[
            pltpu.VMEM((ROWS, D), F32), pltpu.VMEM((ROWS, D), BF), pltpu.VMEM((ROWS, 3 * D), BF),
            pltpu.VMEM((ROWS, D), BF), pltpu.VMEM((D // HD, ROWS, KEYS), BF), pltpu.VMEM((ROWS, D), F32),
            pltpu.VMEM((ROWS, 3 * D), BF), pltpu.VMEM((ROWS, D), BF), pltpu.VMEM((ROWS, D), BF),
            pltpu.SemaphoreType.DMA((14,)), pltpu.SemaphoreType.DMA((3,)),
        ],
        compiler_params=params(52),
        cost_estimate=cost(28),
        name="attention_backward",
    )(gmid, hid, *qkvs, *atts, *exps, *invs, wproj, rel, shift, keys, dqkv, uqkv, dproj, uproj)


def token_grad_kernel(gmid_hbm, x_hbm, gqkv_hbm, gain_ref, wqkv_ref, o0, o1, o2,
                      gmid_ref, x_ref, gqkv_ref, gh_ref, out_rows, sem, *, low, high):
    span = pl.ds(low, high - low)
    copies = [
        pltpu.make_async_copy(src.at[span, :], dst, sem.at[i])
        for i, (src, dst) in enumerate(((gqkv_hbm, gqkv_ref), (x_hbm, x_ref), (gmid_hbm, gmid_ref)))
    ]
    for copy in copies:
        copy.start()
    copies[0].wait()
    gh_ref[...] = nt(gqkv_ref[...], wqkv_ref[...])
    copies[1].wait()
    copies[2].wait()
    gain = gain_ref[...]
    step = (high - low) // 2

    def norm_step(i, carry):
        rows = pl.ds(pl.multiple_of(i * step, 16), step)
        normed, inv_std = normalize(x_ref[rows, :].astype(F32))
        back = norm_back(gh_ref[rows, :] * gain, normed, inv_std)
        out_rows[rows, :] = (gmid_ref[rows, :] + back).astype(BF)
        return carry

    lax.fori_loop(0, 2, norm_step, 0)
    split_pieces(out_rows, (o0, o1, o2))


def token_grad(gmid, x, gqkv, gain, wqkv, low, high):
    count = high - low
    return pl.pallas_call(
        functools.partial(token_grad_kernel, low=low, high=high),
        out_shape=pieces_of(count),
        in_specs=[hbm(), hbm(), hbm(), vm(), vm()],
        out_specs=[vm()] * 3,
        scratch_shapes=[
            pltpu.VMEM((count, D), F32), pltpu.VMEM((count, D), BF), pltpu.VMEM((count, 3 * D), BF),
            pltpu.VMEM((count, D), F32), pltpu.VMEM((count, D), BF), pltpu.SemaphoreType.DMA((3,)),
        ],
        compiler_params=params(28),
        cost_estimate=cost(8),
        name="token_gradient",
    )(gmid, x, gqkv, gain, wqkv)


def grad_pack_kernel(where_ref, down_q, up_q, down_p, up_p, down1, up1, down2, up2, o0, o1, o2, o3, buf_ref):
    mine = where_ref[0]
    for k in range(4):
        for i, ref in enumerate((down_q, down1, up_p, up2)):
            buf_ref[k, :RANK, QUART * i : QUART * (i + 1)] = ref[:, QUART * k : QUART * (k + 1)]
    for dest in range(4):
        k = jnp.bitwise_xor(mine, dest)
        ranks = slice(RANK // 4 * dest, RANK // 4 * (dest + 1))
        for j in range(4):
            base = RANK + 12 * j
            for t in range(3):
                buf_ref[k, base : base + 4, QUART * t : QUART * (t + 1)] = up_q[
                    ranks, D * t + QUART * j : D * t + QUART * (j + 1)
                ]
            buf_ref[k, base : base + 4, 3 * QUART :] = down_p[ranks, QUART * j : QUART * (j + 1)]
            buf_ref[k, base + 4 : base + 8, :] = up1[ranks, D * j : D * (j + 1)]
            buf_ref[k, base + 8 : base + 12, :] = down2[ranks, D * j : D * (j + 1)]
    for k, out in enumerate((o0, o1, o2, o3)):
        out[...] = buf_ref[k].astype(BF)


def grad_pack(where, *grads):
    return pl.pallas_call(
        grad_pack_kernel,
        out_shape=(jax.ShapeDtypeStruct((4 * RANK, D), BF),) * 4,
        in_specs=[sm()] + [vm()] * 8,
        out_specs=[vm()] * 4,
        scratch_shapes=[pltpu.VMEM((4, 4 * RANK, D), F32)],
        compiler_params=params(8),
        cost_estimate=cost(2),
        name="adapter_grad_pack",
    )(where, *grads)


def grad_sum_kernel(g0, g1, g2, g3, o0, o1, o2, o3, buf_ref):
    total = g0[...].astype(F32) + g1[...].astype(F32) + g2[...].astype(F32) + g3[...].astype(F32)
    buf_ref[...] = jnp.zeros_like(buf_ref)
    buf_ref[:RANK, :] = total[:RANK, :]
    for j, out in enumerate((o0, o1, o2, o3)):
        buf_ref[RANK : RANK + 12, :] = total[RANK + 12 * j : RANK + 12 * (j + 1), :]
        out[...] = buf_ref[...].astype(BF)


def grad_sum(pieces):
    return pl.pallas_call(
        grad_sum_kernel,
        out_shape=(jax.ShapeDtypeStruct((2 * RANK, D), BF),) * 4,
        in_specs=[vm()] * 4,
        out_specs=[vm()] * 4,
        scratch_shapes=[pltpu.VMEM((2 * RANK, D), F32)],
        compiler_params=params(4),
        cost_estimate=cost(2),
        name="adapter_grad_sum",
    )(*pieces)


def grad_adapters_kernel(index_ref, x_ref, qkv_dn, fc1_dn, proj_up, fc2_up, rest_ref, acc_ref):
    acc_ref[...] = jnp.zeros_like(acc_ref)

    def add(i, carry):
        acc_ref[index_ref[i]] += x_ref[i].astype(F32)
        return carry

    lax.fori_loop(0, x_ref.shape[0], add, 0)
    for i, ref in enumerate((qkv_dn, fc1_dn, proj_up, fc2_up)):
        ref[...] = acc_ref[:, :RANK, QUART * i : QUART * (i + 1)]
    rest_ref[...] = acc_ref[:, RANK:, :].astype(BF)


def grad_adapters(index, x):
    s = lambda n, dtype=F32: jax.ShapeDtypeStruct((ADAPT, RANK, n), dtype)
    return pl.pallas_call(
        grad_adapters_kernel,
        out_shape=(s(QUART), s(QUART), s(QUART), s(QUART), s(D, BF)),
        in_specs=[sm(), vm()],
        out_specs=[vm()] * 5,
        scratch_shapes=[pltpu.VMEM((ADAPT, 2 * RANK, D), F32)],
        compiler_params=params(8),
        cost_estimate=cost(2),
        name="adapter_grad_by_adapter",
    )(index, x)


def grad_join_kernel(where_ref, r0, r1, r2, r3, qkv_up, proj_dn, fc1_up, fc2_dn, buf_ref):
    mine = where_ref[0]
    heads = qkv_up.shape[2] // (3 * HD)
    for k, ref in enumerate((r0, r1, r2, r3)):
        buf_ref[jnp.bitwise_xor(mine, k)] = ref[...].astype(F32)
    for source in range(4):
        ranks = slice(RANK // 4 * source, RANK // 4 * (source + 1))
        for h in range(heads):
            for t in range(3):
                qkv_up[:, ranks, HD * (3 * h + t) : HD * (3 * h + t + 1)] = buf_ref[
                    source, :, 0:4, QUART * t + HD * h : QUART * t + HD * (h + 1)
                ]
        proj_dn[:, ranks, :] = buf_ref[source, :, 0:4, 3 * QUART :]
        fc1_up[:, ranks, :] = buf_ref[source, :, 4:8, :]
        fc2_dn[:, ranks, :] = buf_ref[source, :, 8:12, :]


def grad_join(where, pieces):
    s = lambda n: jax.ShapeDtypeStruct((ADAPT, RANK, n), F32)
    return pl.pallas_call(
        grad_join_kernel,
        out_shape=(s(3 * QUART), s(QUART), s(D), s(D)),
        in_specs=[sm()] + [vm()] * 4,
        out_specs=[vm()] * 4,
        scratch_shapes=[pltpu.VMEM((4, ADAPT, RANK, D), F32)],
        compiler_params=params(12),
        cost_estimate=cost(2),
        name="adapter_grad_join",
    )(where, *pieces)


def flip(values, axis, distance):
    size = lax.axis_size(axis)
    return lax.ppermute(values, axis, [(i, i ^ distance) for i in range(size)])


def send_rows(pieces):
    own, near, pair = pieces
    return [own, flip(near, "row", 1), flip(pair, "row", 2)]


def hand_on(pieces, *deps):
    own, near, crossed = pieces
    if deps:
        near, crossed = after((near, crossed), *deps)
    return [own, near, crossed, flip(crossed, "row", 1)]


def exchange(slots, axis):
    return [slots[0]] + [flip(slots[k], axis, k) for k in range(1, 4)]


def after(values, *deps):
    return lax.optimization_barrier((tuple(values), deps))[0]


def col_halves(half):
    return jnp.concatenate([flip(half, "col", j) for j in range(1, 4)], axis=0)


def col_pairs(half, other_row):
    two = jnp.concatenate([half, other_row], axis=0)
    return jnp.concatenate([other_row] + [flip(two, "col", j) for j in range(1, 4)], axis=0)


def body(
    tokens, grad_out, adapter_index, norm1_gain, norm2_gain, qkv_weight, proj_weight, fc1_weight, fc2_weight,
    rel_h, rel_w, qkv_down, qkv_up, proj_down, proj_up, fc1_down, fc1_up, fc2_down, fc2_up,
):
    members = lax.axis_size("col")
    batches = lax.axis_size("dp")
    row_index, col_index, dp_index = lax.axis_index("row"), lax.axis_index("col"), lax.axis_index("dp")
    half = dp_index % 2
    where = jnp.stack([row_index, half]).astype(jnp.int32)
    slot_images = (
        jnp.bitwise_xor(dp_index, jnp.arange(batches, dtype=jnp.int32))[:, None] * members
        + jnp.bitwise_xor(col_index, jnp.arange(members, dtype=jnp.int32))[None, :]
    ).reshape(-1)
    slot_adapters = jnp.sum(
        jnp.where(
            slot_images[:, None] == jnp.arange(adapter_index.shape[0], dtype=jnp.int32)[None, :],
            adapter_index[:, 0][None, :],
            0,
        ),
        axis=1,
    )
    pick = jnp.concatenate([slot_adapters[:4], half[None]]).astype(jnp.int32)
    swap = lambda m: jnp.swapaxes(m, 1, 2)

    shift, keys = jnp.asarray(SHIFT_NP), jnp.asarray(KEYS_NP)

    *token_slots, alpha_own, beta_own, alpha_half, beta_half = front(where, tokens, qkv_weight, proj_weight)
    cut = lambda m: lax.dynamic_slice_in_dim(m, half * HBLK, HBLK, 0)
    b0 = flip(beta_half, "row", 2)
    alpha_near = col_halves(alpha_half)
    x_pieces = send_rows(token_slots)
    *send, row_adapters, rel = adapter_pack(
        pick, qkv_up, swap(proj_down), fc1_up, swap(fc2_down), swap(qkv_down), swap(fc1_down), proj_up, fc2_up,
        norm1_gain.reshape(1, -1), norm2_gain.reshape(1, -1), rel_h, rel_w,
    )
    beta_sent = [jnp.concatenate([beta_half, b0, send[j]], axis=0) for j in range(1, 4)]
    beta_got = [flip(m, "col", j) for j, m in enumerate(beta_sent, 1)]
    alpha_near, x_pieces[1] = after((alpha_near, x_pieces[1]))
    alpha_far = flip(alpha_near, "dp", 1)
    g = jnp.concatenate([alpha_own, alpha_near, alpha_far, row_adapters], axis=0)
    fc2_half, = after((cut(fc2_weight),), x_pieces[2])
    c0 = flip(fc2_half, "row", 2)
    g, *x_pieces = after((g, *x_pieces), c0)
    gy = flip(g, "row", 2)
    grad_slots = pack(where, grad_out)
    *beta_got, _ = after((*beta_got, grad_slots[0]))
    beta_near = jnp.concatenate([b0] + [m[:QUART] for m in beta_got], axis=0)
    col_adapters = [send[0]] + beta_got
    beta_far = flip(beta_near, "dp", 1)
    x_pieces = hand_on(x_pieces)

    fc1_half, = after((cut(fc1_weight),), *beta_got)
    fc1_near = [flip(fc1_half, "col", j) for j in range(1, 4)]

    *fc1_near, g, gy, beta_own, beta_near, beta_far = after((*fc1_near, g, gy, beta_own, beta_near, beta_far))
    alpha1 = [g, flip(g, "row", 1), gy, flip(gy, "row", 1)]
    beta1 = [beta_own, beta_near, beta_far] + [flip(m, "row", 1) for m in (beta_own, beta_near, beta_far)]
    grad_slots = after(tuple(grad_slots), gy, c0)
    g_pieces = send_rows(grad_slots)
    two = jnp.concatenate([fc2_half, c0], axis=0)
    fc2_near = [flip(two, "col", j) for j in range(1, 4)]
    fc1_near = jnp.concatenate(fc1_near, axis=0)
    fc1_far = flip(fc1_near, "dp", 1)
    h = jnp.concatenate([fc1_weight, fc1_near, fc1_far], axis=0)
    wqkv, wproj, dqkv, uqkv, dproj, uproj, d1, u1, d2, u2, gain1, gain2 = prep1(
        where, alpha1, beta1, col_adapters
    )
    wqkv, h, *fc2_near = after((wqkv, h, *fc2_near))
    hy = flip(h, "row", 2)
    fc2_near = jnp.concatenate([c0] + fc2_near, axis=0)
    fc2_far = flip(fc2_near, "dp", 1)
    x, hid, *qkvs = qkv_rows(x_pieces, gain1, wqkv)
    *qkvs, _ = after((*qkvs, g_pieces[2]))
    g_pieces = hand_on(g_pieces, qkvs[0])
    part0 = attention(0, qkvs[0], rel, shift, keys)
    qkv1, = after((qkvs[1],), part0[0])
    part1 = attention(1, qkv1, rel, shift, keys)
    qkv2, _ = after((qkvs[2], part1[0]))
    part2 = attention(2, qkv2, rel, shift, keys)
    atts, exps, invs = zip(part0, part1, part2)
    atts = list(atts)
    atts[2], hy = after((atts[2], hy))
    alpha2 = [h, flip(h, "row", 1), hy, flip(hy, "row", 1)]
    middle = project(x, atts, wproj)
    middle, fc2_far = after((middle, fc2_far))
    beta2 = [fc2_weight, fc2_near, fc2_far] + [flip(m, "row", 1) for m in (fc2_weight, fc2_near, fc2_far)]

    *out_slots, gmid, down1, up1, down2, up2 = mlp(where, middle, g_pieces, gain2, alpha2, beta2, d1, u1, d2, u2)
    out_pieces = send_rows(out_slots)
    gqkv, down_q, up_q, down_p, up_p = attention_back(
        gmid, hid, qkvs, atts, exps, invs, wproj, rel, shift, keys, dqkv, uqkv, dproj, uproj
    )
    out_pieces = hand_on(out_pieces, gqkv)
    gqkv, down_q, up_q, down_p, up_p = after((gqkv, down_q, up_q, down_p, up_p), *out_pieces[:3])
    packed = grad_pack(where, down_q, up_q, down_p, up_p, down1, up1, down2, up2)
    *packed, gqkv = after((*packed, gqkv))
    row_sums = exchange(packed, "row")
    back0 = token_grad(gmid, x, gqkv, gain1, wqkv, *TAIL[0])
    *row_sums, gqkv, b0, b1, b2 = after((*row_sums, gqkv, *back0))
    back_pieces = send_rows((b0, b1, b2))
    summed = grad_sum(row_sums)
    *summed, gqkv = after((*summed, gqkv))
    images = exchange(summed, "col")
    back1 = token_grad(gmid, x, gqkv, gain1, wqkv, *TAIL[1])
    last_pieces = send_rows(back1)
    *images, near, crossed = after((*images, *back_pieces[1:]), back1[0])
    back_pieces = hand_on([back_pieces[0], near, crossed])
    images = jnp.stack(images)
    images, *out_pieces = after((images, *out_pieces))
    step = 1
    while step < batches:
        images = jnp.concatenate([images, flip(images, "dp", step)], axis=0)
        step *= 2
    result = unpack(where, out_pieces, BF)
    images, = after((images,), result)
    qkv_dn, fc1_dn, proj_upg, fc2_upg, rest = grad_adapters(slot_adapters.astype(jnp.int32), images)
    rests = [rest] + [flip(rest, "row", k) for k in range(1, 4)]
    grad_tokens = unpack(where, back_pieces + hand_on(last_pieces, rest), F32, TAIL)
    rests = after(tuple(rests), grad_tokens)
    qkv_upg, proj_dn, fc1_upg, fc2_dn = grad_join(where, rests)
    return (
        result, grad_tokens,
        swap(qkv_dn), qkv_upg, swap(proj_dn), proj_upg, swap(fc1_dn), fc1_upg, swap(fc2_dn), fc2_upg,
    )


def solution(mesh):
    return jax.shard_map(
        body,
        mesh=mesh,
        in_specs=(
            P("row", ("dp", "col")), P("row", ("dp", "col")), P(), P("row"), P("row"),
            P("row", "col"), P("col", "row"), P("row", "col"), P("row", "col"), P(), P(),
            P(None, "row", None), P(None, None, "col"), P(None, "col", None), P(None, None, "row"),
            P(None, "row", None), P(None, None, "col"), P(None, "col", None), P(None, None, "row"),
        ),
        out_specs=(
            P("row", ("dp", "col")), P("row", ("dp", "col")),
            P(None, "row", None), P(None, None, "col"), P(None, "col", None), P(None, None, "row"),
            P(None, "row", None), P(None, None, "col"), P(None, "col", None), P(None, None, "row"),
        ),
        check_vma=False,
    )
```

```python
import functools

import jax
import jax.numpy as jnp
import numpy as np
from jax import lax
from jax.experimental import pallas as pl
from jax.experimental.pallas import tpu as pltpu
from jax.sharding import PartitionSpec as P

D = 768
HD = 64
WIN = 14
SLOTS = WIN * WIN
SIDE = 64
ADAPT = 8
NWIN = 5
IMG_TOK = NWIN * NWIN * SLOTS
RANK = 16
EDGE = SIDE - (NWIN - 1) * WIN
QUART = D // 4
FULLR = 208
KEYS = 208
EDGER = EDGE * WIN
CORNR = EDGE * EDGE
ROWS = 4 * FULLR + 2 * EDGER + CORNR
HALF = ROWS // 2
HBLK = QUART // 2
EPSILON = 1e-06
BF = jnp.bfloat16
F32 = jnp.float32

FULL, RIGHT, BOTTOM, CORNER = 0, 1, 2, 3
NQ = (FULLR, EDGER, EDGER, CORNR)
OFFS = (0, 4 * FULLR, 4 * FULLR + EDGER, 4 * FULLR + 2 * EDGER)


def slot_order(kind):
    rows = EDGE if kind in (BOTTOM, CORNER) else WIN
    cols = EDGE if kind in (RIGHT, CORNER) else WIN
    kept = [a * WIN + b for a in range(rows) for b in range(cols)]
    rest = [s for s in range(SLOTS) if s not in set(kept)]
    return kept, kept + rest


def build_tables():
    shift = np.zeros((4, FULLR, 128), np.int32)
    keys = np.zeros((4, KEYS, 128), np.float32)
    for kind in range(4):
        kept, order = slot_order(kind)
        for i, s in enumerate(kept):
            for base in (0, 64):
                shift[kind, i, base : base + 32] = WIN - 1 - s // WIN
                shift[kind, i, base + 32 : base + 64] = WIN - 1 - s % WIN
        spare = order[0] if kind == FULL else order[-1]
        for i, s in enumerate(order + [spare] * (KEYS - SLOTS)):
            for base in (0, 64):
                keys[kind, i, base + s // WIN] = 1.0
                keys[kind, i, base + 32 + s % WIN] = 1.0
    return shift, keys.astype(jnp.bfloat16)


SHIFT_NP, KEYS_NP = build_tables()


def nn(a, b):
    return jnp.dot(a, b, preferred_element_type=F32)


def nt(a, b):
    return lax.dot_general(a, b, (((1,), (1,)), ((), ())), preferred_element_type=F32)


def tn(a, b):
    return lax.dot_general(a, b, (((0,), (0,)), ((), ())), preferred_element_type=F32)


def vm():
    return pl.BlockSpec(memory_space=pltpu.VMEM)


def hbm():
    return pl.BlockSpec(memory_space=pl.ANY)


def in_hbm(x):
    return pltpu.with_memory_space_constraint(x, pltpu.HBM)


def arg():
    return pl.BlockSpec(memory_space=pltpu.HBM)


def sm():
    return pl.BlockSpec(memory_space=pltpu.SMEM)


def params(mib=60):
    return pltpu.CompilerParams(vmem_limit_bytes=mib * 1024 * 1024)


def cost(us):
    return pl.CostEstimate(flops=int(us * 1e6), transcendentals=0, bytes_accessed=0)


def place_window(kind, count, moved, width, spare=-100000):
    row = lax.broadcasted_iota(jnp.int32, (count, width), 0)
    lane = lax.broadcasted_iota(jnp.int32, (count, width), 1)
    if kind in (RIGHT, CORNER):
        src = (row // EDGE) * WIN + row % EDGE
    else:
        src = jnp.where(row < SLOTS, row, spare)
    return (lane == src + moved).astype(F32).astype(BF)


def window_list(dest):
    items = [(FULL, FULLR * j, NWIN * dest + j) for j in range(4)]
    items.append((RIGHT, OFFS[1], NWIN * dest + 4))
    items.append((BOTTOM, OFFS[2], NWIN * 4 + dest))
    if dest == 3:
        items.append((CORNER, OFFS[3], NWIN * NWIN - 1))
    return items


def window_span(window):
    start = window * SLOTS
    low = start // 128 * 128
    high = min(-(-(start + SLOTS) // 128) * 128, IMG_TOK)
    return low, high, start - low


def pack_rows(mine, x_ref, rows_ref, spare):
    for dest in range(4):
        slot = jnp.bitwise_xor(mine, dest)
        if dest != 3:
            rows_ref[slot, OFFS[3] :, :] = jnp.zeros((CORNR, QUART), BF)
        for kind, offset, window in window_list(dest):
            low, high, moved = window_span(window)
            pick = place_window(kind, NQ[kind], moved, high - low, spare)
            rows_ref[slot, offset : offset + NQ[kind], :] = nt(pick, x_ref[:, low:high]).astype(BF)


def fold(rows_ref, outs):
    half = rows_ref.shape[1] // 2
    for slot, (out, base) in enumerate(((outs[0], 0), (outs[1], 0), (outs[2], 0), (outs[2], half))):
        out[base : base + half, :QUART] = rows_ref[slot, :half, :]
        out[base : base + half, QUART:] = rows_ref[slot, half:, :]


def pack_kernel(where_ref, x_hbm, o0, o1, o2, rows_ref, x_ref, sem):
    load = pltpu.make_async_copy(x_hbm, x_ref, sem)
    load.start()
    load.wait()
    pack_rows(where_ref[0], x_ref, rows_ref, -100000)
    fold(rows_ref, (o0, o1, o2))


def pieces_of(rows):
    piece = lambda n: jax.ShapeDtypeStruct((n, 2 * QUART), BF)
    return (piece(rows // 2), piece(rows // 2), piece(rows))


def pack(where, x):
    return pl.pallas_call(
        pack_kernel,
        out_shape=pieces_of(ROWS),
        in_specs=[sm(), arg()],
        out_specs=[vm()] * 3,
        scratch_shapes=[
            pltpu.VMEM((4, ROWS, QUART), BF), pltpu.VMEM((QUART, IMG_TOK), BF), pltpu.SemaphoreType.DMA,
        ],
        compiler_params=params(16),
        cost_estimate=cost(4),
        name="pack",
    )(where, in_hbm(x))


def front_kernel(
    where_ref, x_hbm, qkv_hbm, proj_hbm, o0, o1, o2, alpha_ref, beta_ref, alpha_half, beta_half,
    rows_ref, x_ref, qkv_w, proj_w, sem,
):
    loads = [
        pltpu.make_async_copy(src, dst, sem.at[i])
        for i, (src, dst) in enumerate(((qkv_hbm, qkv_w), (proj_hbm, proj_w), (x_hbm, x_ref)))
    ]
    for load in loads:
        load.start()
    loads[0].wait()
    loads[1].wait()
    heads = qkv_w.shape[1] // (3 * HD)
    for h in range(heads):
        for t in range(3):
            ref, base = (alpha_ref, QUART * t) if t < 2 else (beta_ref, 0)
            ref[:, base + HD * h : base + HD * (h + 1)] = qkv_w[:, HD * (3 * h + t) : HD * (3 * h + t + 1)]
    beta_ref[:, QUART:] = proj_w[...]
    rows = pl.ds(pl.multiple_of(where_ref[1] * HBLK, 32), HBLK)
    alpha_half[...] = alpha_ref[rows, :]
    beta_half[...] = beta_ref[rows, :]
    loads[2].wait()
    pack_rows(where_ref[0], x_ref, rows_ref, 0)
    fold(rows_ref, (o0, o1, o2))


def front(where, x, qkv_w, proj_w):
    s = lambda *shape: jax.ShapeDtypeStruct(shape, BF)
    return pl.pallas_call(
        front_kernel,
        out_shape=pieces_of(ROWS)
        + (s(QUART, 2 * QUART), s(QUART, 2 * QUART), s(HBLK, 2 * QUART), s(HBLK, 2 * QUART)),
        in_specs=[sm(), arg(), arg(), arg()],
        out_specs=[vm()] * 7,
        scratch_shapes=[
            pltpu.VMEM((4, ROWS, QUART), BF), pltpu.VMEM((QUART, IMG_TOK), BF),
            pltpu.VMEM(qkv_w.shape, BF), pltpu.VMEM(proj_w.shape, BF), pltpu.SemaphoreType.DMA((3,)),
        ],
        compiler_params=params(16),
        cost_estimate=cost(5),
        name="token_and_weight_pack",
    )(where, in_hbm(x), in_hbm(qkv_w), in_hbm(proj_w))


def unpack_kernel(where_ref, *refs, bounds):
    pieces, (out_ref, acc_ref, rows_ref) = refs[:-3], refs[-3:]
    mine = where_ref[0]
    acc_ref[...] = jnp.zeros_like(acc_ref)
    index = 0
    for low, high in bounds:
        half = (high - low) // 2
        for slot in range(4):
            piece = pieces[index]
            rows = slice(half, 2 * half) if slot == 3 else slice(0, half)
            rows_ref[slot, low : low + half, :] = piece[rows, :QUART]
            rows_ref[slot, low + half : high, :] = piece[rows, QUART:]
            index += 1

    for source in range(4):
        slot = jnp.bitwise_xor(mine, source)
        for kind, offset, window in window_list(source):
            low, high, moved = window_span(window)
            pick = place_window(kind, NQ[kind], moved, high - low)
            acc_ref[:, low:high] += tn(rows_ref[slot, offset : offset + NQ[kind], :], pick)
    out_ref[...] = acc_ref[:, :IMG_TOK].astype(out_ref.dtype)


def unpack(where, pieces, dtype, bounds=((0, ROWS),)):
    return pl.pallas_call(
        functools.partial(unpack_kernel, bounds=bounds),
        out_shape=jax.ShapeDtypeStruct((QUART, IMG_TOK), dtype),
        in_specs=[sm()] + [vm()] * len(pieces),
        out_specs=vm(),
        scratch_shapes=[
            pltpu.VMEM((QUART, -(-IMG_TOK // 128) * 128), F32),
            pltpu.VMEM((4, ROWS, QUART), BF),
        ],
        compiler_params=params(24),
        cost_estimate=cost(4),
        name="unpack",
    )(where, *pieces)


def join_pieces(pieces, dst_ref):
    for slot, piece in enumerate(pieces):
        rows = slice(HALF, ROWS) if slot == 3 else slice(0, HALF)
        dst_ref[:HALF, QUART * slot : QUART * (slot + 1)] = piece[rows, :QUART]
        dst_ref[HALF:, QUART * slot : QUART * (slot + 1)] = piece[rows, QUART:]


def split_pieces(src_ref, outs):
    half = src_ref.shape[0] // 2
    for slot, (out, base) in enumerate(((outs[0], 0), (outs[1], 0), (outs[2], 0), (outs[2], half))):
        out[base : base + half, :QUART] = src_ref[:half, QUART * slot : QUART * (slot + 1)]
        out[base : base + half, QUART:] = src_ref[half:, QUART * slot : QUART * (slot + 1)]


def adapter_pack_kernel(
    pick_ref, qkv_up_hbm, proj_dn_hbm, fc1_up_hbm, fc2_dn_hbm, qkv_dn_hbm, fc1_dn_hbm, proj_up_hbm, fc2_up_hbm,
    gain1, gain2, rel_h, rel_w, s0, s1, s2, s3, row_ref, rel_ref,
    qkv_up, proj_dn, fc1_up, fc2_dn, qkv_dn, fc1_dn, proj_up, fc2_up, sem,
):
    pairs = []
    for j in range(4):
        for src, dst in ((qkv_up_hbm, qkv_up), (proj_dn_hbm, proj_dn), (fc1_up_hbm, fc1_up), (fc2_dn_hbm, fc2_dn)):
            pairs.append((src.at[pick_ref[j]], dst.at[j]))
    for src, dst in ((qkv_dn_hbm, qkv_dn), (fc1_dn_hbm, fc1_dn), (proj_up_hbm, proj_up), (fc2_up_hbm, fc2_up)):
        pairs.append((src.at[pick_ref[0]], dst.at[0]))
    loads = [pltpu.make_async_copy(src, dst, sem.at[i]) for i, (src, dst) in enumerate(pairs)]
    for load in loads:
        load.start()
    offsets = rel_h.shape[0]
    reverse = (
        lax.broadcasted_iota(jnp.int32, (offsets, 32), 0) + lax.broadcasted_iota(jnp.int32, (offsets, 32), 1)
        == offsets - 1
    ).astype(F32).astype(BF)
    rel_ref[...] = jnp.zeros_like(rel_ref)
    for i, table in enumerate((rel_h, rel_w)):
        block = tn(table[...], reverse).astype(BF)
        rel_ref[:HD, HD + 32 * i : HD + 32 * (i + 1)] = block
        rel_ref[HD:, 32 * i : 32 * (i + 1)] = block
    for load in loads:
        load.wait()
    heads = qkv_up.shape[2] // (3 * HD)
    half = 2 * QUART
    for j, send_ref in enumerate((s0, s1, s2, s3)):
        for h in range(heads):
            for t in range(3):
                row, base = (0, QUART * t) if t < 2 else (RANK, 0)
                send_ref[row : row + RANK, base + HD * h : base + HD * (h + 1)] = qkv_up[
                    j, :, HD * (3 * h + t) : HD * (3 * h + t + 1)
                ]
        send_ref[RANK : 2 * RANK, QUART:] = proj_dn[j]
        for i, ref in enumerate((fc1_up, fc2_dn)):
            for part in range(2):
                row = RANK * (2 + 2 * i + part)
                send_ref[row : row + RANK, :] = ref[j, :, half * part : half * (part + 1)]
    for i, ref in enumerate((qkv_dn, fc1_dn, proj_up, fc2_up)):
        row, base = RANK * (i // 2), QUART * (i % 2)
        row_ref[row : row + RANK, base : base + QUART] = ref[0]
    for i, ref in enumerate((gain1, gain2)):
        row_ref[2 * RANK :, QUART * i : QUART * (i + 1)] = jnp.broadcast_to(ref[...], (RANK, QUART))


def adapter_pack(pick, *mats):
    s = lambda *shape: jax.ShapeDtypeStruct(shape, BF)
    return pl.pallas_call(
        adapter_pack_kernel,
        out_shape=(s(6 * RANK, 2 * QUART),) * 4 + (s(3 * RANK, 2 * QUART), s(128, 128)),
        in_specs=[sm()] + [arg()] * 8 + [vm()] * 4,
        out_specs=[vm()] * 6,
        scratch_shapes=[pltpu.VMEM((4,) + m.shape[1:], BF) for m in mats[:4]]
        + [pltpu.VMEM((1,) + m.shape[1:], BF) for m in mats[4:8]]
        + [pltpu.SemaphoreType.DMA((20,))],
        compiler_params=params(8),
        cost_estimate=cost(2),
        name="adapter_pack",
    )(pick, *(in_hbm(m) for m in mats[:8]), *mats[8:])


def alpha_block(k, j):
    part = k
    if j == 0:
        return [(part, 0, QUART, None)]
    return [
        (part, QUART + HBLK * (j - 1), HBLK, 0),
        (part, QUART + 3 * HBLK + HBLK * (j - 1), HBLK, 1),
    ]


def beta_block(k, j):
    core, cross = k % 2, k // 2
    base = 3 * core
    if j == 0 and not cross:
        return [(base, 0, QUART, None)]
    row = 0 if j == 0 else HBLK + QUART * (j - 1) + HBLK * cross
    return [(base + 1, row, HBLK, 0), (base + 2, row, HBLK, 1)]


def block_dst(start, flag, half):
    if flag is None:
        return start
    offset = half if flag == 0 else 1 - half
    return pl.multiple_of(start + offset * HBLK, 32)


def prep1_kernel(
    where_ref, p0, p1, p2, p3, q0, q1, q2, q3, q4, q5, a0, a1, a2, a3,
    wqkv_ref, wproj_ref, dqkv, uqkv, dproj, uproj, d1, u1, d2, u2, gain1, gain2, ups, downs,
):
    half = where_ref[1]
    for j, a in enumerate((a0, a1, a2, a3)):
        base = a.shape[0] - 6 * RANK
        part = lambda i: slice(base + RANK * i, base + RANK * (i + 1))
        for t in range(3):
            uqkv[:, D * t + QUART * j : D * t + QUART * (j + 1)] = a[
                part(t // 2), QUART * (t % 2) : QUART * (t % 2 + 1)
            ]
        dproj[:, QUART * j : QUART * (j + 1)] = a[part(1), QUART:]
        for i in range(2):
            u1[:, D * j + D // 2 * i : D * j + D // 2 * (i + 1)] = a[part(2 + i), :]
            d2[:, D * j + D // 2 * i : D * j + D // 2 * (i + 1)] = a[part(4 + i), :]
    for k, ref in enumerate((p0, p1, p2, p3)):
        for i, dst in enumerate((dqkv, d1, uproj, u2)):
            rows = slice(D + RANK * (i // 2), D + RANK * (i // 2 + 1))
            dst[:, QUART * k : QUART * (k + 1)] = ref[rows, QUART * (i % 2) : QUART * (i % 2 + 1)]
        for i, dst in enumerate((gain1, gain2)):
            row = D + 2 * RANK
            dst[:, QUART * k : QUART * (k + 1)] = ref[row : row + 1, QUART * i : QUART * (i + 1)].astype(F32)
    alpha, beta = (p0, p1, p2, p3), (q0, q1, q2, q3, q4, q5)
    for k in range(4):
        for j in range(4):
            for part, row, count, flag in alpha_block(k, j):
                rows = pl.ds(block_dst(QUART * k, flag, half), count)
                for t in range(2):
                    wqkv_ref[rows, D * t + QUART * j : D * t + QUART * (j + 1)] = alpha[part][
                        row : row + count, QUART * t : QUART * (t + 1)
                    ]
            for part, row, count, flag in beta_block(k, j):
                rows = pl.ds(block_dst(QUART * k, flag, half), count)
                wqkv_ref[rows, 2 * D + QUART * j : 2 * D + QUART * (j + 1)] = beta[part][
                    row : row + count, :QUART
                ]
                rows = pl.ds(block_dst(QUART * j, flag, half), count)
                wproj_ref[rows, QUART * k : QUART * (k + 1)] = beta[part][row : row + count, QUART:]
    for t in range(3):
        ups[t] = uqkv[:, D * t : D * (t + 1)]
    ups[3] = uproj[...]
    for k in range(4):
        downs[k] = dqkv[:, QUART * k : QUART * (k + 1)]
        downs[4 + k] = dproj[:, QUART * k : QUART * (k + 1)]

    def merge(t, carry):
        cols = pl.ds(pl.multiple_of(D * t, 128), D)
        for k in range(4):
            rows = slice(QUART * k, QUART * (k + 1))
            wqkv_ref[rows, cols] = (wqkv_ref[rows, cols].astype(F32) + tn(downs[k], ups[t])).astype(BF)
        return carry

    lax.fori_loop(0, 3, merge, 0)
    for k in range(4):
        rows = slice(QUART * k, QUART * (k + 1))
        wproj_ref[rows, :] = (wproj_ref[rows, :].astype(F32) + tn(downs[4 + k], ups[3])).astype(BF)


def prep1(where, alpha, beta, cols):
    s = lambda *shape: jax.ShapeDtypeStruct(shape, BF)
    return pl.pallas_call(
        prep1_kernel,
        out_shape=(
            s(D, 3 * D), s(D, D), s(RANK, D), s(RANK, 3 * D), s(RANK, D), s(RANK, D),
            s(RANK, D), s(RANK, 4 * D), s(RANK, 4 * D), s(RANK, D),
            jax.ShapeDtypeStruct((1, D), F32), jax.ShapeDtypeStruct((1, D), F32),
        ),
        in_specs=[sm()] + [vm()] * 14,
        out_specs=[vm()] * 12,
        scratch_shapes=[pltpu.VMEM((4, RANK, D), BF), pltpu.VMEM((8, RANK, QUART), BF)],
        compiler_params=params(24),
        cost_estimate=cost(7),
        name="attention_weights",
    )(where, *alpha, *beta, *cols)


def normalize(values):
    center = jnp.sum(values, axis=1, keepdims=True) / D
    shifted = values - center
    inv_std = lax.rsqrt(jnp.sum(shifted * shifted, axis=1, keepdims=True) / D + EPSILON)
    return shifted * inv_std, inv_std


def norm_back(grad, normed, inv_std):
    first = jnp.sum(grad, axis=1, keepdims=True) / D
    second = jnp.sum(grad * normed, axis=1, keepdims=True) / D
    return inv_std * (grad - first - normed * second)


def barrel(values, amount, left):
    for bit in (1, 2, 4, 8):
        moved = pltpu.roll(values, (128 - bit) if left else bit, 1)
        values = jnp.where((amount & bit) != 0, moved, values)
    return values


def low_half(count):
    return lax.broadcasted_iota(jnp.int32, (count, 128), 1) < HD


def pad_rows(tile):
    if tile.shape[0] == KEYS:
        return tile
    return jnp.concatenate([tile, jnp.zeros((KEYS - tile.shape[0], tile.shape[1]), tile.dtype)], axis=0)


def live_rows():
    return lax.broadcasted_iota(jnp.int32, (KEYS, 128), 0) < SLOTS


GROUP = 6
GROUP_BACK = 6


def pair_columns(pair):
    return tuple(slice(D * t + 128 * pair, D * t + 128 * (pair + 1)) for t in range(3))


def attend_window(kind, row0, qkv_ref, att_ref, exp_ref, inv_ref, rel_ref, shift_ref, keys_ref):
    count = NQ[kind]
    rows = pl.ds(row0, count)
    low_q, low_k = low_half(count), low_half(KEYS)
    live = live_rows()
    ones = jnp.where(live, 1.0, 0.0).astype(BF)
    amount = shift_ref[kind, :count, :]
    onehot = keys_ref[kind]
    rel_mat = rel_ref[...]
    for first in range(0, D // 128, GROUP):
        pairs = range(first, first + GROUP)
        heads = [(pair, odd) for pair in pairs for odd in range(2)]
        q_tile = {p: qkv_ref[rows, pair_columns(p)[0]] for p in pairs}
        rel = {p: nn(q_tile[p], rel_mat) for p in pairs}
        rel = {p: barrel(rel[p], amount, True).astype(BF) for p in pairs}
        k_tile = {p: pad_rows(qkv_ref[rows, pair_columns(p)[1]] * BF(HD**-0.5)) for p in pairs}
        scores = {}
        for p, odd in heads:
            if odd:
                q_aug, k_aug = jnp.where(low_q, rel[p], q_tile[p]), jnp.where(low_k, onehot, k_tile[p])
            else:
                q_aug, k_aug = jnp.where(low_q, q_tile[p], rel[p]), jnp.where(low_k, k_tile[p], onehot)
            scores[p, odd] = nt(q_aug, k_aug)
        top = {h: jnp.max(scores[h], axis=1, keepdims=True) for h in heads}
        exponent = {h: jnp.exp(scores[h] - top[h]).astype(BF) for h in heads}
        both = {}
        for p, odd in heads:
            exp_ref[2 * p + odd, rows, :] = exponent[p, odd]
            v_tile = pad_rows(qkv_ref[rows, pair_columns(p)[2]])
            if kind == FULL:
                v_tile = jnp.where(live, v_tile, 0).astype(BF)
            v_aug = jnp.where(low_k, ones, v_tile) if odd else jnp.where(low_k, v_tile, ones)
            both[p, odd] = nn(exponent[p, odd], v_aug)
        for p in pairs:
            cols = pair_columns(p)[0]
            inverse = 1.0 / pltpu.roll(jnp.where(low_q, both[p, 1], both[p, 0]), HD, 1)
            inv_ref[rows, cols] = inverse
            att_ref[rows, cols] = (jnp.where(low_q, both[p, 0], both[p, 1]) * inverse).astype(BF)


PARTS = ((FULL, FULL), (FULL, FULL), (RIGHT, BOTTOM, CORNER))
PART_ROWS = tuple(sum(NQ[kind] for kind in part) for part in PARTS)
PART_OFFS = (0, PART_ROWS[0], PART_ROWS[0] + PART_ROWS[1])


TAIL = ((0, 576), (576, ROWS))


def qkv_kernel(
    x0, x1, x2, x3, gain_ref, w_hbm, x_hbm, hid_hbm, qkv_a, qkv_b, qkv_c,
    x_ref, hid_ref, rows_ref, w_ref, qkv_ref, sem, out_sem,
):
    loads = [
        pltpu.make_async_copy(w_hbm.at[:, D * t : D * (t + 1)], w_ref.at[t], sem.at[t]) for t in range(3)
    ]
    for load in loads:
        load.start()
    join_pieces((x0, x1, x2, x3), x_ref)
    kept = [
        pltpu.make_async_copy(src, dst, sem.at[3 + i])
        for i, (src, dst) in enumerate(((x_ref, x_hbm), (hid_ref, hid_hbm)))
    ]
    kept[0].start()
    gain = gain_ref[...]

    def norm_step(i, carry):
        rows = pl.ds(pl.multiple_of(i * 112, 16), 112)
        normed, _ = normalize(x_ref[rows, :].astype(F32))
        hidden = (normed * gain).astype(BF)
        rows_ref[rows, :] = hidden
        hid_ref[rows, :] = hidden
        return carry

    lax.fori_loop(0, ROWS // 112, norm_step, 0)
    for w in range(4):
        hid_ref[FULLR * w + SLOTS : FULLR * (w + 1), :] = jnp.zeros((FULLR - SLOTS, D), BF)
    kept[1].start()
    for load in loads:
        load.wait()

    def stores(t):
        cols = pl.ds(pl.multiple_of(D * t, 128), D)
        return [
            pltpu.make_async_copy(
                qkv_ref.at[t, pl.ds(offset, count), :], out.at[:, cols], out_sem.at[t, i]
            )
            for i, (out, offset, count) in enumerate(zip((qkv_a, qkv_b, qkv_c), PART_OFFS, PART_ROWS))
        ]

    def project_step(t, carry):
        qkv_ref[t] = nn(rows_ref[...], w_ref[t]).astype(BF)
        for store in stores(t):
            store.start()
        return carry

    lax.fori_loop(0, 3, project_step, 0)
    for t in range(3):
        for store in stores(t):
            store.wait()
    for store in kept:
        store.wait()


def qkv_rows(pieces, gain, wqkv):
    s = lambda *shape: jax.ShapeDtypeStruct(shape, BF)
    return pl.pallas_call(
        qkv_kernel,
        out_shape=(s(ROWS, D), s(ROWS, D)) + tuple(s(n, 3 * D) for n in PART_ROWS),
        in_specs=[vm()] * 5 + [hbm()],
        out_specs=[hbm()] * 5,
        scratch_shapes=[
            pltpu.VMEM((ROWS, D), BF), pltpu.VMEM((ROWS, D), BF), pltpu.VMEM((ROWS, D), BF),
            pltpu.VMEM((3, D, D), BF), pltpu.VMEM((3, ROWS, D), BF),
            pltpu.SemaphoreType.DMA((5,)), pltpu.SemaphoreType.DMA((3, 3)),
        ],
        compiler_params=params(32),
        cost_estimate=cost(10),
        name="norm_and_qkv",
    )(*pieces, gain, wqkv)


def attention_kernel(qkv_ref, rel_ref, shift_ref, keys_ref, att_ref, exp_ref, inv_ref, *, kinds):
    refs = (qkv_ref, att_ref, exp_ref, inv_ref, rel_ref, shift_ref, keys_ref)
    if kinds[0] == FULL:

        def step(w, carry):
            attend_window(FULL, pl.multiple_of(w * FULLR, 16), *refs)
            return carry

        lax.fori_loop(0, len(kinds), step, 0)
    else:
        row = 0
        for kind in kinds:
            attend_window(kind, row, *refs)
            row += NQ[kind]


def attention(part, qkv, rel, shift, keys):
    rows = PART_ROWS[part]
    s = lambda *shape, dtype=BF: jax.ShapeDtypeStruct(shape, dtype)
    return pl.pallas_call(
        functools.partial(attention_kernel, kinds=PARTS[part]),
        out_shape=(s(rows, D), s(D // HD, rows, KEYS), s(rows, D, dtype=F32)),
        in_specs=[vm()] * 4,
        out_specs=[vm()] * 3,
        compiler_params=params(24),
        cost_estimate=cost(10),
        name="attention_forward",
    )(qkv, rel, shift, keys)


def project_kernel(x_ref, att_a, att_b, att_c, wproj_ref, middle_ref):
    for ref, offset, count in zip((att_a, att_b, att_c), PART_OFFS, PART_ROWS):
        rows = slice(offset, offset + count)
        middle_ref[rows, :] = x_ref[rows, :].astype(F32) + nn(ref[...], wproj_ref[...])


def project(x, atts, wproj):
    return pl.pallas_call(
        project_kernel,
        out_shape=jax.ShapeDtypeStruct((ROWS, D), F32),
        in_specs=[vm()] * 5,
        out_specs=vm(),
        compiler_params=params(20),
        cost_estimate=cost(5),
        name="projection",
    )(x, *atts, wproj)


CHUNK = 512
LOCK = 1


def mlp_kernel(
    where_ref, middle_ref, g0, g1, g2, g3, gain_ref,
    p0, p1, p2, p3, q0, q1, q2, q3, q4, q5, d1, u1, d2, u2,
    o0, o1, o2, gmid_ref, down1, up1, down2, up2,
    gm_ref, out_rows, h2_ref, acc_mlp, acc_gh, gu1, ad2, w1_ref, w2_ref, downs, sem,
):
    half = where_ref[1]
    copies = []

    def fetch(src, dst):
        copies.append(pltpu.make_async_copy(src, dst, sem.at[len(copies)]))
        copies[-1].start()

    alpha, beta = (p0, p1, p2, p3), (q0, q1, q2, q3, q4, q5)
    for k in range(4):
        for j in range(4):
            for part, row, count, flag in alpha_block(k, j):
                rows = pl.ds(block_dst(QUART * k, flag, half), count)
                fetch(alpha[part].at[row : row + count, :], w1_ref.at[rows, D * j : D * (j + 1)])
            for part, row, count, flag in beta_block(k, j):
                rows = pl.ds(block_dst(QUART * k, flag, half), count)
                fetch(beta[part].at[row : row + count, :], w2_ref.at[rows, D * j : D * (j + 1)])
    join_pieces((g0, g1, g2, g3), gm_ref)
    for k in range(4):
        downs[k] = d1[:, QUART * k : QUART * (k + 1)]
        downs[4 + k] = u2[:, QUART * k : QUART * (k + 1)]
    for copy in copies:
        copy.wait()

    def merge(j, carry):
        cols = pl.ds(pl.multiple_of(D * j, 128), D)
        for k in range(4):
            rows = slice(QUART * k, QUART * (k + 1))
            w1_ref[rows, cols] = (w1_ref[rows, cols].astype(F32) + tn(downs[k], u1[:, cols])).astype(BF)
            w2_ref[rows, cols] = (w2_ref[rows, cols].astype(F32) + tn(downs[4 + k], d2[:, cols])).astype(BF)
        return carry

    lax.fori_loop(0, 4, merge, 0)
    gain = gain_ref[...]
    down1[...] = jnp.zeros_like(down1)
    up1[...] = jnp.zeros_like(up1)
    down2[...] = jnp.zeros_like(down2)
    up2[...] = jnp.zeros_like(up2)

    def tile_step(t, carry):
        rows = pl.ds(pl.multiple_of(t * HALF, 16), HALF)
        normed, _ = normalize(middle_ref[rows, :])
        h2 = (normed * gain).astype(BF)
        h2_ref[...] = h2
        gm = gm_ref[rows, :]
        ad1 = nt(d1[...], h2).astype(BF)
        gu2 = nt(u2[...], gm).astype(BF)
        acc_mlp[...] = jnp.zeros_like(acc_mlp)
        acc_gh[...] = jnp.zeros_like(acc_gh)
        gu1[...] = jnp.zeros_like(gu1)
        ad2[...] = jnp.zeros_like(ad2)

        def chunk_step(c, inner_carry):
            spans = [
                pl.ds(pl.multiple_of((c * LOCK + i) * CHUNK, CHUNK), CHUNK) for i in range(LOCK)
            ]
            h2 = h2_ref[...]
            gm = gm_ref[rows, :]
            inner = [nn(h2, w1_ref[:, span]) for span in spans]
            gact = [nn(gm, w2_ref[:, span]) for span in spans]
            act, ginner = [], []
            for i in range(LOCK):
                half = 0.5 * (1.0 + lax.erf(inner[i] * 2**-0.5))
                act.append((inner[i] * half).astype(BF))
                slope = half + inner[i] * (jnp.exp(-0.5 * inner[i] * inner[i]) * (2 * np.pi) ** -0.5)
                ginner.append((gact[i] * slope).astype(BF))
            for i, span in enumerate(spans):
                acc_mlp[...] += nt(act[i], w2_ref[:, span])
                acc_gh[...] += nt(ginner[i], w1_ref[:, span])
                up1[:, span] += nn(ad1, ginner[i])
                gu1[...] += nt(u1[:, span], ginner[i])
                ad2[...] += nt(d2[:, span], act[i])
                down2[:, span] += nn(gu2, act[i])
            return inner_carry

        lax.fori_loop(0, 4 * D // (CHUNK * LOCK), chunk_step, 0)
        down1[...] += nn(gu1[...].astype(BF), h2_ref[...])
        up2[...] += nn(ad2[...].astype(BF), gm_ref[rows, :])
        middle = middle_ref[rows, :]
        out_rows[rows, :] = (middle + acc_mlp[...]).astype(BF)
        normed, inv_std = normalize(middle)
        gmid_ref[rows, :] = gm_ref[rows, :].astype(F32) + norm_back(acc_gh[...] * gain, normed, inv_std)
        return carry

    lax.fori_loop(0, 2, tile_step, 0)
    split_pieces(out_rows, (o0, o1, o2))


def mlp(where, middle, pieces, gain, alpha, beta, d1, u1, d2, u2):
    s = lambda *shape, dtype=F32: jax.ShapeDtypeStruct(shape, dtype)
    return pl.pallas_call(
        mlp_kernel,
        out_shape=pieces_of(ROWS)
        + (s(ROWS, D), s(RANK, D), s(RANK, 4 * D), s(RANK, 4 * D), s(RANK, D)),
        in_specs=[sm()] + [vm()] * 6 + [pl.BlockSpec(memory_space=pl.ANY)] * 10 + [vm()] * 4,
        out_specs=[vm()] * 8,
        scratch_shapes=[
            pltpu.VMEM((ROWS, D), BF), pltpu.VMEM((ROWS, D), BF), pltpu.VMEM((HALF, D), BF),
            pltpu.VMEM((HALF, D), F32), pltpu.VMEM((HALF, D), F32),
            pltpu.VMEM((RANK, HALF), F32), pltpu.VMEM((RANK, HALF), F32),
            pltpu.VMEM((D, 4 * D), BF), pltpu.VMEM((D, 4 * D), BF), pltpu.VMEM((8, RANK, QUART), BF),
            pltpu.SemaphoreType.DMA((4 * 4 * 4,)),
        ],
        compiler_params=params(48),
        cost_estimate=cost(48),
        name="mlp_forward_backward",
    )(where, middle, *pieces, gain, *alpha, *beta, d1, u1, d2, u2)


def attend_back_window(
    kind, row0, qkv_ref, att_ref, exp_ref, inv_ref, gatt_ref, gqkv_ref, rel_ref, shift_ref, keys_ref
):
    count = NQ[kind]
    rows = pl.ds(row0, count)
    low_q, low_k = low_half(count), low_half(KEYS)
    live = live_rows()
    lane_k = lax.broadcasted_iota(jnp.int32, (KEYS, 128), 1) % HD
    lane_q = lax.broadcasted_iota(jnp.int32, (count, 128), 1) % HD
    ones = jnp.where(live & (lane_k < 2), 1.0, 0.0).astype(BF)
    across = jnp.where(
        low_half(128) != (lax.broadcasted_iota(jnp.int32, (128, 128), 0) < HD), -1.0, 0.0
    ).astype(BF)
    amount = shift_ref[kind, :count, :]
    onehot = keys_ref[kind]
    rel_mat = rel_ref[...]
    for first in range(0, D // 128, GROUP_BACK):
        pairs = range(first, first + GROUP_BACK)
        heads = [(pair, odd) for pair in pairs for odd in range(2)]
        go_tile = {
            p: (gatt_ref[rows, pair_columns(p)[0]].astype(F32) * inv_ref[rows, pair_columns(p)[0]]).astype(BF)
            for p in pairs
        }
        delta = {
            p: nn((go_tile[p].astype(F32) * att_ref[rows, pair_columns(p)[0]].astype(F32)).astype(BF), across)
            for p in pairs
        }
        go_t = {p: go_tile[p].T for p in pairs}
        gv = {}
        for p, odd in heads:
            gv[p, odd] = nn(go_t[p][HD * odd : HD * (odd + 1), :], exp_ref[2 * p + odd, rows, :])
        gscore = {}
        for p in pairs:
            high = delta[p].astype(BF)
            rest = (delta[p] - high.astype(F32)).astype(BF)
            low_delta = jnp.where(lane_q == 0, high, jnp.where(lane_q == 1, rest, 0)).astype(BF)
            v_tile = pad_rows(qkv_ref[rows, pair_columns(p)[2]])
            if kind == FULL:
                v_tile = jnp.where(live, v_tile, 0).astype(BF)
            gscore[p, 0] = nt(jnp.where(low_q, go_tile[p], low_delta), jnp.where(low_k, v_tile, ones))
            gscore[p, 1] = nt(jnp.where(low_q, low_delta, go_tile[p]), jnp.where(low_k, ones, v_tile))
        q_t = {p: qkv_ref[rows, pair_columns(p)[0]].T for p in pairs}
        gs = {(p, odd): (exp_ref[2 * p + odd, rows, :].astype(F32) * gscore[p, odd]).astype(BF) for p, odd in heads}
        gk = {(p, odd): nn(q_t[p][HD * odd : HD * (odd + 1), :], gs[p, odd]) for p, odd in heads}
        gq = {}
        for p in pairs:
            k_tile = pad_rows(qkv_ref[rows, pair_columns(p)[1]] * BF(HD**-0.5))
            gq[p, 0] = nn(gs[p, 0], jnp.where(low_k, k_tile, onehot))
            gq[p, 1] = nn(gs[p, 1], jnp.where(low_k, onehot, k_tile))
        sums = {p: barrel(jnp.where(low_q, gq[p, 1], gq[p, 0]), amount, False).astype(BF) for p in pairs}
        for p in pairs:
            cols, kcols, vcols = pair_columns(p)
            gv_tile = jnp.concatenate([gv[p, 0], gv[p, 1]], axis=0).astype(BF).T
            gqkv_ref[rows, vcols] = gv_tile[:count, :]
            gk_tile = (jnp.concatenate([gk[p, 0], gk[p, 1]], axis=0) * HD**-0.5).astype(BF).T
            gqkv_ref[rows, kcols] = gk_tile[:count, :]
            gqkv_ref[rows, cols] = (jnp.where(low_q, gq[p, 0], gq[p, 1]) + nt(sums[p], rel_mat)).astype(BF)


def attention_back_kernel(
    gmid_hbm, hid_hbm, qkv_a, qkv_b, qkv_c, att_a, att_b, att_c, exp_a, exp_b, exp_c, inv_a, inv_b, inv_c,
    wproj_ref, rel_ref, shift_ref, keys_ref, dqkv, uqkv, dproj, uproj,
    gqkv_hbm, down_q, up_q, down_p, up_p,
    gmid_ref, hid_ref, qkv_ref, att_ref, exp_ref, inv_ref, gqkv_ref, gb_ref, gatt_ref, sem, out_sem,
):
    spans = [pl.ds(offset, count) for offset, count in zip(PART_OFFS, PART_ROWS)]
    pairs = [(gmid_hbm, gmid_ref)]
    for part, srcs in enumerate(
        ((qkv_a, inv_a, att_a, exp_a), (qkv_b, inv_b, att_b, exp_b), (qkv_c, inv_c, att_c, exp_c))
    ):
        rows = spans[part]
        for src, dst in zip(srcs, (qkv_ref, inv_ref, att_ref)):
            pairs.append((src, dst.at[rows, :]))
        pairs.append((srcs[3], exp_ref.at[:, rows, :]))
    pairs.append((hid_hbm, hid_ref))
    loads = [pltpu.make_async_copy(src, dst, sem.at[i]) for i, (src, dst) in enumerate(pairs)]
    for load in loads:
        load.start()

    def wait_part(part):
        for load in loads[1 + 4 * part : 5 + 4 * part]:
            load.wait()

    stores = [
        pltpu.make_async_copy(gqkv_ref.at[rows, :], gqkv_hbm.at[rows, :], out_sem.at[i])
        for i, rows in enumerate(spans)
    ]
    loads[0].wait()
    gb_ref[...] = gmid_ref[...].astype(BF)
    gatt_ref[...] = nt(gb_ref[...], wproj_ref[...]).astype(BF)
    refs = (qkv_ref, att_ref, exp_ref, inv_ref, gatt_ref, gqkv_ref, rel_ref, shift_ref, keys_ref)

    def step(w, carry):
        for part in range(2):

            @pl.when(w == 2 * part)
            def _():
                wait_part(part)

        attend_back_window(FULL, pl.multiple_of(w * FULLR, 16), *refs)
        return carry

    lax.fori_loop(0, 4, step, 0)
    stores[0].start()
    stores[1].start()
    wait_part(2)
    for kind in (RIGHT, BOTTOM, CORNER):
        attend_back_window(kind, OFFS[kind], *refs)
    stores[2].start()
    up_p[...] = nn(nt(dproj[...], att_ref[...]).astype(BF), gb_ref[...])
    down_p[...] = nn(nt(uproj[...], gb_ref[...]).astype(BF), att_ref[...])
    loads[-1].wait()
    up_q[...] = nn(nt(dqkv[...], hid_ref[...]).astype(BF), gqkv_ref[...])
    down_q[...] = nn(nt(uqkv[...], gqkv_ref[...]).astype(BF), hid_ref[...])
    for store in stores:
        store.wait()


def attention_back(gmid, hid, qkvs, atts, exps, invs, wproj, rel, shift, keys, dqkv, uqkv, dproj, uproj):
    s = lambda *shape, dtype=F32: jax.ShapeDtypeStruct(shape, dtype)
    return pl.pallas_call(
        attention_back_kernel,
        out_shape=(s(ROWS, 3 * D, dtype=BF), s(RANK, D), s(RANK, 3 * D), s(RANK, D), s(RANK, D)),
        in_specs=[hbm()] * 14 + [vm()] * 8,
        out_specs=[hbm()] + [vm()] * 4,
        scratch_shapes=[
            pltpu.VMEM((ROWS, D), F32), pltpu.VMEM((ROWS, D), BF), pltpu.VMEM((ROWS, 3 * D), BF),
            pltpu.VMEM((ROWS, D), BF), pltpu.VMEM((D // HD, ROWS, KEYS), BF), pltpu.VMEM((ROWS, D), F32),
            pltpu.VMEM((ROWS, 3 * D), BF), pltpu.VMEM((ROWS, D), BF), pltpu.VMEM((ROWS, D), BF),
            pltpu.SemaphoreType.DMA((14,)), pltpu.SemaphoreType.DMA((3,)),
        ],
        compiler_params=params(52),
        cost_estimate=cost(28),
        name="attention_backward",
    )(gmid, hid, *qkvs, *atts, *exps, *invs, wproj, rel, shift, keys, dqkv, uqkv, dproj, uproj)


def token_grad_kernel(gmid_hbm, x_hbm, gqkv_hbm, gain_ref, wqkv_ref, o0, o1, o2,
                      gmid_ref, x_ref, gqkv_ref, gh_ref, out_rows, sem, *, low, high):
    span = pl.ds(low, high - low)
    copies = [
        pltpu.make_async_copy(src.at[span, :], dst, sem.at[i])
        for i, (src, dst) in enumerate(((gqkv_hbm, gqkv_ref), (x_hbm, x_ref), (gmid_hbm, gmid_ref)))
    ]
    for copy in copies:
        copy.start()
    copies[0].wait()
    gh_ref[...] = nt(gqkv_ref[...], wqkv_ref[...])
    copies[1].wait()
    copies[2].wait()
    gain = gain_ref[...]
    step = (high - low) // 2

    def norm_step(i, carry):
        rows = pl.ds(pl.multiple_of(i * step, 16), step)
        normed, inv_std = normalize(x_ref[rows, :].astype(F32))
        back = norm_back(gh_ref[rows, :] * gain, normed, inv_std)
        out_rows[rows, :] = (gmid_ref[rows, :] + back).astype(BF)
        return carry

    lax.fori_loop(0, 2, norm_step, 0)
    split_pieces(out_rows, (o0, o1, o2))


def token_grad(gmid, x, gqkv, gain, wqkv, low, high):
    count = high - low
    return pl.pallas_call(
        functools.partial(token_grad_kernel, low=low, high=high),
        out_shape=pieces_of(count),
        in_specs=[hbm(), hbm(), hbm(), vm(), vm()],
        out_specs=[vm()] * 3,
        scratch_shapes=[
            pltpu.VMEM((count, D), F32), pltpu.VMEM((count, D), BF), pltpu.VMEM((count, 3 * D), BF),
            pltpu.VMEM((count, D), F32), pltpu.VMEM((count, D), BF), pltpu.SemaphoreType.DMA((3,)),
        ],
        compiler_params=params(28),
        cost_estimate=cost(8),
        name="token_gradient",
    )(gmid, x, gqkv, gain, wqkv)


def grad_pack_kernel(where_ref, down_q, up_q, down_p, up_p, down1, up1, down2, up2, o0, o1, o2, o3, buf_ref):
    mine = where_ref[0]
    for k in range(4):
        for i, ref in enumerate((down_q, down1, up_p, up2)):
            buf_ref[k, :RANK, QUART * i : QUART * (i + 1)] = ref[:, QUART * k : QUART * (k + 1)]
    for dest in range(4):
        k = jnp.bitwise_xor(mine, dest)
        ranks = slice(RANK // 4 * dest, RANK // 4 * (dest + 1))
        for j in range(4):
            base = RANK + 12 * j
            for t in range(3):
                buf_ref[k, base : base + 4, QUART * t : QUART * (t + 1)] = up_q[
                    ranks, D * t + QUART * j : D * t + QUART * (j + 1)
                ]
            buf_ref[k, base : base + 4, 3 * QUART :] = down_p[ranks, QUART * j : QUART * (j + 1)]
            buf_ref[k, base + 4 : base + 8, :] = up1[ranks, D * j : D * (j + 1)]
            buf_ref[k, base + 8 : base + 12, :] = down2[ranks, D * j : D * (j + 1)]
    for k, out in enumerate((o0, o1, o2, o3)):
        out[...] = buf_ref[k].astype(BF)


def grad_pack(where, *grads):
    return pl.pallas_call(
        grad_pack_kernel,
        out_shape=(jax.ShapeDtypeStruct((4 * RANK, D), BF),) * 4,
        in_specs=[sm()] + [vm()] * 8,
        out_specs=[vm()] * 4,
        scratch_shapes=[pltpu.VMEM((4, 4 * RANK, D), F32)],
        compiler_params=params(8),
        cost_estimate=cost(2),
        name="adapter_grad_pack",
    )(where, *grads)


def grad_sum_kernel(g0, g1, g2, g3, o0, o1, o2, o3, buf_ref):
    total = g0[...].astype(F32) + g1[...].astype(F32) + g2[...].astype(F32) + g3[...].astype(F32)
    buf_ref[...] = jnp.zeros_like(buf_ref)
    buf_ref[:RANK, :] = total[:RANK, :]
    for j, out in enumerate((o0, o1, o2, o3)):
        buf_ref[RANK : RANK + 12, :] = total[RANK + 12 * j : RANK + 12 * (j + 1), :]
        out[...] = buf_ref[...].astype(BF)


def grad_sum(pieces):
    return pl.pallas_call(
        grad_sum_kernel,
        out_shape=(jax.ShapeDtypeStruct((2 * RANK, D), BF),) * 4,
        in_specs=[vm()] * 4,
        out_specs=[vm()] * 4,
        scratch_shapes=[pltpu.VMEM((2 * RANK, D), F32)],
        compiler_params=params(4),
        cost_estimate=cost(2),
        name="adapter_grad_sum",
    )(*pieces)


def grad_adapters_kernel(index_ref, x_ref, qkv_dn, fc1_dn, proj_up, fc2_up, rest_ref, acc_ref):
    acc_ref[...] = jnp.zeros_like(acc_ref)

    def add(i, carry):
        acc_ref[index_ref[i]] += x_ref[i].astype(F32)
        return carry

    lax.fori_loop(0, x_ref.shape[0], add, 0)
    for i, ref in enumerate((qkv_dn, fc1_dn, proj_up, fc2_up)):
        ref[...] = acc_ref[:, :RANK, QUART * i : QUART * (i + 1)]
    rest_ref[...] = acc_ref[:, RANK:, :].astype(BF)


def grad_adapters(index, x):
    s = lambda n, dtype=F32: jax.ShapeDtypeStruct((ADAPT, RANK, n), dtype)
    return pl.pallas_call(
        grad_adapters_kernel,
        out_shape=(s(QUART), s(QUART), s(QUART), s(QUART), s(D, BF)),
        in_specs=[sm(), vm()],
        out_specs=[vm()] * 5,
        scratch_shapes=[pltpu.VMEM((ADAPT, 2 * RANK, D), F32)],
        compiler_params=params(8),
        cost_estimate=cost(2),
        name="adapter_grad_by_adapter",
    )(index, x)


def grad_join_kernel(where_ref, r0, r1, r2, r3, qkv_up, proj_dn, fc1_up, fc2_dn, buf_ref):
    mine = where_ref[0]
    heads = qkv_up.shape[2] // (3 * HD)
    for k, ref in enumerate((r0, r1, r2, r3)):
        buf_ref[jnp.bitwise_xor(mine, k)] = ref[...].astype(F32)
    for source in range(4):
        ranks = slice(RANK // 4 * source, RANK // 4 * (source + 1))
        for h in range(heads):
            for t in range(3):
                qkv_up[:, ranks, HD * (3 * h + t) : HD * (3 * h + t + 1)] = buf_ref[
                    source, :, 0:4, QUART * t + HD * h : QUART * t + HD * (h + 1)
                ]
        proj_dn[:, ranks, :] = buf_ref[source, :, 0:4, 3 * QUART :]
        fc1_up[:, ranks, :] = buf_ref[source, :, 4:8, :]
        fc2_dn[:, ranks, :] = buf_ref[source, :, 8:12, :]


def grad_join(where, pieces):
    s = lambda n: jax.ShapeDtypeStruct((ADAPT, RANK, n), F32)
    return pl.pallas_call(
        grad_join_kernel,
        out_shape=(s(3 * QUART), s(QUART), s(D), s(D)),
        in_specs=[sm()] + [vm()] * 4,
        out_specs=[vm()] * 4,
        scratch_shapes=[pltpu.VMEM((4, ADAPT, RANK, D), F32)],
        compiler_params=params(12),
        cost_estimate=cost(2),
        name="adapter_grad_join",
    )(where, *pieces)


def flip(values, axis, distance):
    size = lax.axis_size(axis)
    return lax.ppermute(values, axis, [(i, i ^ distance) for i in range(size)])


def send_rows(pieces, *deps):
    own, near, pair = pieces
    if deps:
        near, = after((near,), *deps)
    return [own, flip(near, "row", 1), flip(pair, "row", 2)]


def hand_on(pieces, *deps):
    own, near, crossed = pieces
    if deps:
        near, crossed = after((near, crossed), *deps)
    return [own, near, crossed, flip(crossed, "row", 1)]


def exchange(slots, axis):
    return [slots[0]] + [flip(slots[k], axis, k) for k in range(1, 4)]


def after(values, *deps):
    return lax.optimization_barrier((tuple(values), deps))[0]


def col_halves(half):
    return jnp.concatenate([flip(half, "col", j) for j in range(1, 4)], axis=0)


def col_pairs(half, other_row):
    two = jnp.concatenate([half, other_row], axis=0)
    return jnp.concatenate([other_row] + [flip(two, "col", j) for j in range(1, 4)], axis=0)


def body(
    tokens, grad_out, adapter_index, norm1_gain, norm2_gain, qkv_weight, proj_weight, fc1_weight, fc2_weight,
    rel_h, rel_w, qkv_down, qkv_up, proj_down, proj_up, fc1_down, fc1_up, fc2_down, fc2_up,
):
    members = lax.axis_size("col")
    batches = lax.axis_size("dp")
    row_index, col_index, dp_index = lax.axis_index("row"), lax.axis_index("col"), lax.axis_index("dp")
    half = dp_index % 2
    where = jnp.stack([row_index, half]).astype(jnp.int32)
    slot_images = (
        jnp.bitwise_xor(dp_index, jnp.arange(batches, dtype=jnp.int32))[:, None] * members
        + jnp.bitwise_xor(col_index, jnp.arange(members, dtype=jnp.int32))[None, :]
    ).reshape(-1)
    slot_adapters = jnp.sum(
        jnp.where(
            slot_images[:, None] == jnp.arange(adapter_index.shape[0], dtype=jnp.int32)[None, :],
            adapter_index[:, 0][None, :],
            0,
        ),
        axis=1,
    )
    pick = jnp.concatenate([slot_adapters[:4], half[None]]).astype(jnp.int32)
    swap = lambda m: jnp.swapaxes(m, 1, 2)

    shift, keys = jnp.asarray(SHIFT_NP), jnp.asarray(KEYS_NP)

    *token_slots, alpha_own, beta_own, alpha_half, beta_half = front(where, tokens, qkv_weight, proj_weight)
    cut = lambda m: lax.dynamic_slice_in_dim(m, half * HBLK, HBLK, 0)
    b0 = flip(beta_half, "row", 2)
    alpha_near = col_halves(alpha_half)
    x_pieces = send_rows(token_slots, b0)
    *send, row_adapters, rel = adapter_pack(
        pick, qkv_up, swap(proj_down), fc1_up, swap(fc2_down), swap(qkv_down), swap(fc1_down), proj_up, fc2_up,
        norm1_gain.reshape(1, -1), norm2_gain.reshape(1, -1), rel_h, rel_w,
    )
    beta_sent = [jnp.concatenate([beta_half, b0, send[j]], axis=0) for j in range(1, 4)]
    beta_got = [flip(m, "col", j) for j, m in enumerate(beta_sent, 1)]
    alpha_near, x_pieces[1] = after((alpha_near, x_pieces[1]))
    alpha_far = flip(alpha_near, "dp", 1)
    g = jnp.concatenate([alpha_own, alpha_near, alpha_far, row_adapters], axis=0)
    fc2_half, = after((cut(fc2_weight),), x_pieces[2], *beta_got)
    c0 = flip(fc2_half, "row", 2)
    g, *x_pieces = after((g, *x_pieces))
    gy = flip(g, "row", 2)
    grad_slots = pack(where, grad_out)
    *beta_got, _ = after((*beta_got, grad_slots[0]))
    beta_near = jnp.concatenate([b0] + [m[:QUART] for m in beta_got], axis=0)
    col_adapters = [send[0]] + beta_got
    beta_far = flip(beta_near, "dp", 1)
    x_pieces = hand_on(x_pieces)

    g1, own1, near1 = (flip(m, "row", 1) for m in (g, beta_own, beta_near))
    fc1_half, = after((cut(fc1_weight),), g1, own1, near1, x_pieces[3], c0)
    fc1_near = [flip(fc1_half, "col", j) for j in range(1, 4)]
    gy, beta_far, fc2_half, c0 = after((gy, beta_far, fc2_half, c0), *fc1_near)
    fc2_two = jnp.concatenate([fc2_half, c0], axis=0)
    fc2_near = [flip(fc2_two, "col", j) for j in range(1, 4)]
    gy1, far1 = flip(gy, "row", 1), flip(beta_far, "row", 1)
    *grad_slots, fc1_near = after((*grad_slots, jnp.concatenate(fc1_near, axis=0)), gy1, far1)
    fc1_far = flip(fc1_near, "dp", 1)
    g_pieces = send_rows(grad_slots, fc2_near[0], fc2_near[1], fc2_near[2])
    wqkv, wproj, dqkv, uqkv, dproj, uproj, d1, u1, d2, u2, gain1, gain2 = prep1(
        where, (g, g1, gy, gy1), (beta_own, beta_near, beta_far, own1, near1, far1), col_adapters
    )
    h = jnp.concatenate([fc1_weight, fc1_near, fc1_far], axis=0)
    wqkv, h, *fc2_near = after((wqkv, h, *fc2_near), g_pieces[2])
    hy = flip(h, "row", 2)
    fc2_near = jnp.concatenate([c0] + fc2_near, axis=0)
    fc2_far = flip(fc2_near, "dp", 1)
    x, hid, *qkvs = qkv_rows(x_pieces, gain1, wqkv)
    g_pieces = hand_on(g_pieces, qkvs[0])
    part0 = attention(0, qkvs[0], rel, shift, keys)
    qkv1, = after((qkvs[1],), part0[0])
    part1 = attention(1, qkv1, rel, shift, keys)
    qkv2, _ = after((qkvs[2], part1[0]))
    part2 = attention(2, qkv2, rel, shift, keys)
    atts, exps, invs = zip(part0, part1, part2)
    atts = list(atts)
    atts[2], hy = after((atts[2], hy))
    alpha2 = [h, flip(h, "row", 1), hy, flip(hy, "row", 1)]
    middle = project(x, atts, wproj)
    middle, fc2_far = after((middle, fc2_far))
    beta2 = [fc2_weight, fc2_near, fc2_far] + [flip(m, "row", 1) for m in (fc2_weight, fc2_near, fc2_far)]

    *out_slots, gmid, down1, up1, down2, up2 = mlp(where, middle, g_pieces, gain2, alpha2, beta2, d1, u1, d2, u2)
    out_pieces = send_rows(out_slots)
    gqkv, down_q, up_q, down_p, up_p = attention_back(
        gmid, hid, qkvs, atts, exps, invs, wproj, rel, shift, keys, dqkv, uqkv, dproj, uproj
    )
    out_pieces = hand_on(out_pieces, gqkv)
    gqkv, down_q, up_q, down_p, up_p = after((gqkv, down_q, up_q, down_p, up_p), *out_pieces[:3])
    packed = grad_pack(where, down_q, up_q, down_p, up_p, down1, up1, down2, up2)
    *packed, gqkv = after((*packed, gqkv))
    row_sums = exchange(packed, "row")
    back0 = token_grad(gmid, x, gqkv, gain1, wqkv, *TAIL[0])
    *row_sums, gqkv, b0, b1, b2 = after((*row_sums, gqkv, *back0))
    back_pieces = send_rows((b0, b1, b2))
    summed = grad_sum(row_sums)
    *summed, gqkv = after((*summed, gqkv))
    images = exchange(summed, "col")
    back1 = token_grad(gmid, x, gqkv, gain1, wqkv, *TAIL[1])
    last_pieces = send_rows(back1)
    *images, near, crossed = after((*images, *back_pieces[1:]), back1[0])
    back_pieces = hand_on([back_pieces[0], near, crossed])
    images = jnp.stack(images)
    images, *out_pieces = after((images, *out_pieces))
    step = 1
    while step < batches:
        images = jnp.concatenate([images, flip(images, "dp", step)], axis=0)
        step *= 2
    result = unpack(where, out_pieces, BF)
    images, = after((images,), result)
    qkv_dn, fc1_dn, proj_upg, fc2_upg, rest = grad_adapters(slot_adapters.astype(jnp.int32), images)
    rests = [rest] + [flip(rest, "row", k) for k in range(1, 4)]
    grad_tokens = unpack(where, back_pieces + hand_on(last_pieces, rest), F32, TAIL)
    rests = after(tuple(rests), grad_tokens)
    qkv_upg, proj_dn, fc1_upg, fc2_dn = grad_join(where, rests)
    return (
        result, grad_tokens,
        swap(qkv_dn), qkv_upg, swap(proj_dn), proj_upg, swap(fc1_dn), fc1_upg, swap(fc2_dn), fc2_upg,
    )


def solution(mesh):
    return jax.shard_map(
        body,
        mesh=mesh,
        in_specs=(
            P("row", ("dp", "col")), P("row", ("dp", "col")), P(), P("row"), P("row"),
            P("row", "col"), P("col", "row"), P("row", "col"), P("row", "col"), P(), P(),
            P(None, "row", None), P(None, None, "col"), P(None, "col", None), P(None, None, "row"),
            P(None, "row", None), P(None, None, "col"), P(None, "col", None), P(None, None, "row"),
        ),
        out_specs=(
            P("row", ("dp", "col")), P("row", ("dp", "col")),
            P(None, "row", None), P(None, None, "col"), P(None, "col", None), P(None, None, "row"),
            P(None, "row", None), P(None, None, "col"), P(None, "col", None), P(None, None, "row"),
        ),
        check_vma=False,
    )
```

```python
import functools

import jax
import jax.numpy as jnp
import numpy as np
from jax import lax
from jax.experimental import pallas as pl
from jax.experimental.pallas import tpu as pltpu
from jax.sharding import PartitionSpec as P

D = 768
HD = 64
WIN = 14
SLOTS = WIN * WIN
SIDE = 64
ADAPT = 8
NWIN = 5
IMG_TOK = NWIN * NWIN * SLOTS
RANK = 16
EDGE = SIDE - (NWIN - 1) * WIN
QUART = D // 4
FULLR = 208
KEYS = 208
EDGER = EDGE * WIN
CORNR = EDGE * EDGE
ROWS = 4 * FULLR + 2 * EDGER + CORNR
HALF = ROWS // 2
HBLK = QUART // 2
EPSILON = 1e-06
BF = jnp.bfloat16
F32 = jnp.float32

FULL, RIGHT, BOTTOM, CORNER = 0, 1, 2, 3
NQ = (FULLR, EDGER, EDGER, CORNR)
OFFS = (0, 4 * FULLR, 4 * FULLR + EDGER, 4 * FULLR + 2 * EDGER)


def slot_order(kind):
    rows = EDGE if kind in (BOTTOM, CORNER) else WIN
    cols = EDGE if kind in (RIGHT, CORNER) else WIN
    kept = [a * WIN + b for a in range(rows) for b in range(cols)]
    rest = [s for s in range(SLOTS) if s not in set(kept)]
    return kept, kept + rest


def build_tables():
    shift = np.zeros((4, FULLR, 128), np.int32)
    keys = np.zeros((4, KEYS, 128), np.float32)
    for kind in range(4):
        kept, order = slot_order(kind)
        for i, s in enumerate(kept):
            for base in (0, 64):
                shift[kind, i, base : base + 32] = WIN - 1 - s // WIN
                shift[kind, i, base + 32 : base + 64] = WIN - 1 - s % WIN
        spare = order[0] if kind == FULL else order[-1]
        for i, s in enumerate(order + [spare] * (KEYS - SLOTS)):
            for base in (0, 64):
                keys[kind, i, base + s // WIN] = 1.0
                keys[kind, i, base + 32 + s % WIN] = 1.0
    return shift, keys.astype(jnp.bfloat16)


SHIFT_NP, KEYS_NP = build_tables()


def nn(a, b):
    return jnp.dot(a, b, preferred_element_type=F32)


def nt(a, b):
    return lax.dot_general(a, b, (((1,), (1,)), ((), ())), preferred_element_type=F32)


def tn(a, b):
    return lax.dot_general(a, b, (((0,), (0,)), ((), ())), preferred_element_type=F32)


def vm():
    return pl.BlockSpec(memory_space=pltpu.VMEM)


def hbm():
    return pl.BlockSpec(memory_space=pl.ANY)


def in_hbm(x):
    return pltpu.with_memory_space_constraint(x, pltpu.HBM)


def arg():
    return pl.BlockSpec(memory_space=pltpu.HBM)


def sm():
    return pl.BlockSpec(memory_space=pltpu.SMEM)


def params(mib=60):
    return pltpu.CompilerParams(vmem_limit_bytes=mib * 1024 * 1024)


def cost(us):
    return pl.CostEstimate(flops=int(us * 1e6), transcendentals=0, bytes_accessed=0)


def place_window(kind, count, moved, width, spare=-100000):
    row = lax.broadcasted_iota(jnp.int32, (count, width), 0)
    lane = lax.broadcasted_iota(jnp.int32, (count, width), 1)
    if kind in (RIGHT, CORNER):
        src = (row // EDGE) * WIN + row % EDGE
    else:
        src = jnp.where(row < SLOTS, row, spare)
    return (lane == src + moved).astype(F32).astype(BF)


def window_list(dest):
    items = [(FULL, FULLR * j, NWIN * dest + j) for j in range(4)]
    items.append((RIGHT, OFFS[1], NWIN * dest + 4))
    items.append((BOTTOM, OFFS[2], NWIN * 4 + dest))
    if dest == 3:
        items.append((CORNER, OFFS[3], NWIN * NWIN - 1))
    return items


def window_span(window):
    start = window * SLOTS
    low = start // 128 * 128
    high = min(-(-(start + SLOTS) // 128) * 128, IMG_TOK)
    return low, high, start - low


def pack_rows(mine, x_ref, rows_ref, spare):
    for dest in range(4):
        slot = jnp.bitwise_xor(mine, dest)
        if dest != 3:
            rows_ref[slot, OFFS[3] :, :] = jnp.zeros((CORNR, QUART), BF)
        for kind, offset, window in window_list(dest):
            low, high, moved = window_span(window)
            pick = place_window(kind, NQ[kind], moved, high - low, spare)
            rows_ref[slot, offset : offset + NQ[kind], :] = nt(pick, x_ref[:, low:high]).astype(BF)


def fold(rows_ref, outs):
    half = rows_ref.shape[1] // 2
    for slot, (out, base) in enumerate(((outs[0], 0), (outs[1], 0), (outs[2], 0), (outs[2], half))):
        out[base : base + half, :QUART] = rows_ref[slot, :half, :]
        out[base : base + half, QUART:] = rows_ref[slot, half:, :]


def pack_kernel(where_ref, x_hbm, o0, o1, o2, rows_ref, x_ref, sem):
    load = pltpu.make_async_copy(x_hbm, x_ref, sem)
    load.start()
    load.wait()
    pack_rows(where_ref[0], x_ref, rows_ref, -100000)
    fold(rows_ref, (o0, o1, o2))


def pieces_of(rows):
    piece = lambda n: jax.ShapeDtypeStruct((n, 2 * QUART), BF)
    return (piece(rows // 2), piece(rows // 2), piece(rows))


def pack(where, x):
    return pl.pallas_call(
        pack_kernel,
        out_shape=pieces_of(ROWS),
        in_specs=[sm(), arg()],
        out_specs=[vm()] * 3,
        scratch_shapes=[
            pltpu.VMEM((4, ROWS, QUART), BF), pltpu.VMEM((QUART, IMG_TOK), BF), pltpu.SemaphoreType.DMA,
        ],
        compiler_params=params(16),
        cost_estimate=cost(4),
        name="pack",
    )(where, in_hbm(x))


def front_kernel(
    where_ref, x_hbm, qkv_hbm, proj_hbm, fc1_hbm, fc2_hbm,
    o0, o1, o2, alpha_ref, beta_ref, alpha_half, cross_ref, fc1_half, fc2_half,
    rows_ref, x_ref, qkv_w, proj_w, sem,
):
    rows = pl.ds(pl.multiple_of(where_ref[1] * HBLK, 32), HBLK)
    loads = [
        pltpu.make_async_copy(src, dst, sem.at[i])
        for i, (src, dst) in enumerate(
            (
                (qkv_hbm, qkv_w), (proj_hbm, proj_w), (fc2_hbm.at[rows, :], fc2_half),
                (fc1_hbm.at[rows, :], fc1_half), (x_hbm, x_ref),
            )
        )
    ]
    for load in loads:
        load.start()
    for load in loads[:4]:
        load.wait()
    heads = qkv_w.shape[1] // (3 * HD)
    for h in range(heads):
        for t in range(3):
            ref, base = (alpha_ref, QUART * t) if t < 2 else (beta_ref, 0)
            ref[:, base + HD * h : base + HD * (h + 1)] = qkv_w[:, HD * (3 * h + t) : HD * (3 * h + t + 1)]
    beta_ref[:, QUART:] = proj_w[...]
    alpha_half[...] = alpha_ref[rows, :]
    cross_ref[:HBLK, :] = beta_ref[rows, :]
    cross_ref[HBLK : 2 * HBLK, :] = fc2_half[:, : 2 * QUART]
    cross_ref[2 * HBLK :, :] = fc2_half[:, 2 * QUART :]
    loads[4].wait()
    pack_rows(where_ref[0], x_ref, rows_ref, 0)
    fold(rows_ref, (o0, o1, o2))


def front(where, x, qkv_w, proj_w, fc1_w, fc2_w):
    s = lambda *shape: jax.ShapeDtypeStruct(shape, BF)
    return pl.pallas_call(
        front_kernel,
        out_shape=pieces_of(ROWS)
        + (
            s(QUART, 2 * QUART), s(QUART, 2 * QUART), s(HBLK, 2 * QUART), s(3 * HBLK, 2 * QUART),
            s(HBLK, D), s(HBLK, D),
        ),
        in_specs=[sm()] + [arg()] * 5,
        out_specs=[vm()] * 9,
        scratch_shapes=[
            pltpu.VMEM((4, ROWS, QUART), BF), pltpu.VMEM((QUART, IMG_TOK), BF),
            pltpu.VMEM(qkv_w.shape, BF), pltpu.VMEM(proj_w.shape, BF), pltpu.SemaphoreType.DMA((5,)),
        ],
        compiler_params=params(16),
        cost_estimate=cost(5),
        name="token_and_weight_pack",
    )(where, *(in_hbm(m) for m in (x, qkv_w, proj_w, fc1_w, fc2_w)))


def unpack_kernel(where_ref, *refs, bounds):
    pieces, (out_ref, acc_ref, rows_ref) = refs[:-3], refs[-3:]
    mine = where_ref[0]
    acc_ref[...] = jnp.zeros_like(acc_ref)
    index = 0
    for low, high in bounds:
        half = (high - low) // 2
        for slot in range(4):
            piece = pieces[index]
            rows = slice(half, 2 * half) if slot == 3 else slice(0, half)
            rows_ref[slot, low : low + half, :] = piece[rows, :QUART]
            rows_ref[slot, low + half : high, :] = piece[rows, QUART:]
            index += 1

    for source in range(4):
        slot = jnp.bitwise_xor(mine, source)
        for kind, offset, window in window_list(source):
            low, high, moved = window_span(window)
            pick = place_window(kind, NQ[kind], moved, high - low)
            acc_ref[:, low:high] += tn(rows_ref[slot, offset : offset + NQ[kind], :], pick)
    out_ref[...] = acc_ref[:, :IMG_TOK].astype(out_ref.dtype)


def unpack(where, pieces, dtype, bounds=((0, ROWS),)):
    return pl.pallas_call(
        functools.partial(unpack_kernel, bounds=bounds),
        out_shape=jax.ShapeDtypeStruct((QUART, IMG_TOK), dtype),
        in_specs=[sm()] + [vm()] * len(pieces),
        out_specs=vm(),
        scratch_shapes=[
            pltpu.VMEM((QUART, -(-IMG_TOK // 128) * 128), F32),
            pltpu.VMEM((4, ROWS, QUART), BF),
        ],
        compiler_params=params(24),
        cost_estimate=cost(4),
        name="unpack",
    )(where, *pieces)


def join_pieces(pieces, dst_ref):
    for slot, piece in enumerate(pieces):
        rows = slice(HALF, ROWS) if slot == 3 else slice(0, HALF)
        dst_ref[:HALF, QUART * slot : QUART * (slot + 1)] = piece[rows, :QUART]
        dst_ref[HALF:, QUART * slot : QUART * (slot + 1)] = piece[rows, QUART:]


def split_pieces(src_ref, outs):
    half = src_ref.shape[0] // 2
    for slot, (out, base) in enumerate(((outs[0], 0), (outs[1], 0), (outs[2], 0), (outs[2], half))):
        out[base : base + half, :QUART] = src_ref[:half, QUART * slot : QUART * (slot + 1)]
        out[base : base + half, QUART:] = src_ref[half:, QUART * slot : QUART * (slot + 1)]


def adapter_pack_kernel(
    pick_ref, qkv_up_hbm, proj_dn_hbm, fc1_up_hbm, fc2_dn_hbm, qkv_dn_hbm, fc1_dn_hbm, proj_up_hbm, fc2_up_hbm,
    gain1, gain2, rel_h, rel_w, s0, s1, s2, s3, row_ref, rel_ref,
    qkv_up, proj_dn, fc1_up, fc2_dn, qkv_dn, fc1_dn, proj_up, fc2_up, sem,
):
    pairs = []
    for j in range(4):
        for src, dst in ((qkv_up_hbm, qkv_up), (proj_dn_hbm, proj_dn), (fc1_up_hbm, fc1_up), (fc2_dn_hbm, fc2_dn)):
            pairs.append((src.at[pick_ref[j]], dst.at[j]))
    for src, dst in ((qkv_dn_hbm, qkv_dn), (fc1_dn_hbm, fc1_dn), (proj_up_hbm, proj_up), (fc2_up_hbm, fc2_up)):
        pairs.append((src.at[pick_ref[0]], dst.at[0]))
    loads = [pltpu.make_async_copy(src, dst, sem.at[i]) for i, (src, dst) in enumerate(pairs)]
    for load in loads:
        load.start()
    offsets = rel_h.shape[0]
    reverse = (
        lax.broadcasted_iota(jnp.int32, (offsets, 32), 0) + lax.broadcasted_iota(jnp.int32, (offsets, 32), 1)
        == offsets - 1
    ).astype(F32).astype(BF)
    rel_ref[...] = jnp.zeros_like(rel_ref)
    for i, table in enumerate((rel_h, rel_w)):
        block = tn(table[...], reverse).astype(BF)
        rel_ref[:HD, HD + 32 * i : HD + 32 * (i + 1)] = block
        rel_ref[HD:, 32 * i : 32 * (i + 1)] = block
    for load in loads:
        load.wait()
    heads = qkv_up.shape[2] // (3 * HD)
    half = 2 * QUART
    for j, send_ref in enumerate((s0, s1, s2, s3)):
        for h in range(heads):
            for t in range(3):
                row, base = (0, QUART * t) if t < 2 else (RANK, 0)
                send_ref[row : row + RANK, base + HD * h : base + HD * (h + 1)] = qkv_up[
                    j, :, HD * (3 * h + t) : HD * (3 * h + t + 1)
                ]
        send_ref[RANK : 2 * RANK, QUART:] = proj_dn[j]
        for i, ref in enumerate((fc1_up, fc2_dn)):
            for part in range(2):
                row = RANK * (2 + 2 * i + part)
                send_ref[row : row + RANK, :] = ref[j, :, half * part : half * (part + 1)]
    for i, ref in enumerate((qkv_dn, fc1_dn, proj_up, fc2_up)):
        row, base = RANK * (i // 2), QUART * (i % 2)
        row_ref[row : row + RANK, base : base + QUART] = ref[0]
    for i, ref in enumerate((gain1, gain2)):
        row_ref[2 * RANK :, QUART * i : QUART * (i + 1)] = jnp.broadcast_to(ref[...], (RANK, QUART))


def adapter_pack(pick, *mats):
    s = lambda *shape: jax.ShapeDtypeStruct(shape, BF)
    return pl.pallas_call(
        adapter_pack_kernel,
        out_shape=(s(6 * RANK, 2 * QUART),) * 4 + (s(3 * RANK, 2 * QUART), s(128, 128)),
        in_specs=[sm()] + [arg()] * 8 + [vm()] * 4,
        out_specs=[vm()] * 6,
        scratch_shapes=[pltpu.VMEM((4,) + m.shape[1:], BF) for m in mats[:4]]
        + [pltpu.VMEM((1,) + m.shape[1:], BF) for m in mats[4:8]]
        + [pltpu.SemaphoreType.DMA((20,))],
        compiler_params=params(8),
        cost_estimate=cost(2),
        name="adapter_pack",
    )(pick, *(in_hbm(m) for m in mats[:8]), *mats[8:])


def alpha_block(k, j):
    part = k
    if j == 0:
        return [(part, 0, QUART, None)]
    return [
        (part, QUART + HBLK * (j - 1), HBLK, 0),
        (part, QUART + 3 * HBLK + HBLK * (j - 1), HBLK, 1),
    ]


def beta_block(k, j):
    core, cross = k % 2, k // 2
    base = 3 * core
    if j == 0 and not cross:
        return [(base, 0, QUART, None)]
    row = 0 if j == 0 else HBLK + QUART * (j - 1) + HBLK * cross
    return [(base + 1, row, HBLK, 0), (base + 2, row, HBLK, 1)]


def block_dst(start, flag, half):
    if flag is None:
        return start
    offset = half if flag == 0 else 1 - half
    return pl.multiple_of(start + offset * HBLK, 32)


def prep1_kernel(
    where_ref, p0, p1, p2, p3, q0, q1, q2, q3, q4, q5, a0, a1, a2, a3,
    wqkv_ref, wproj_ref, dqkv, uqkv, dproj, uproj, d1, u1, d2, u2, gain1, gain2, ups, downs,
):
    half = where_ref[1]
    for j, a in enumerate((a0, a1, a2, a3)):
        base = a.shape[0] - 6 * RANK
        part = lambda i: slice(base + RANK * i, base + RANK * (i + 1))
        for t in range(3):
            uqkv[:, D * t + QUART * j : D * t + QUART * (j + 1)] = a[
                part(t // 2), QUART * (t % 2) : QUART * (t % 2 + 1)
            ]
        dproj[:, QUART * j : QUART * (j + 1)] = a[part(1), QUART:]
        for i in range(2):
            u1[:, D * j + D // 2 * i : D * j + D // 2 * (i + 1)] = a[part(2 + i), :]
            d2[:, D * j + D // 2 * i : D * j + D // 2 * (i + 1)] = a[part(4 + i), :]
    for k, ref in enumerate((p0, p1, p2, p3)):
        for i, dst in enumerate((dqkv, d1, uproj, u2)):
            rows = slice(D + RANK * (i // 2), D + RANK * (i // 2 + 1))
            dst[:, QUART * k : QUART * (k + 1)] = ref[rows, QUART * (i % 2) : QUART * (i % 2 + 1)]
        for i, dst in enumerate((gain1, gain2)):
            row = D + 2 * RANK
            dst[:, QUART * k : QUART * (k + 1)] = ref[row : row + 1, QUART * i : QUART * (i + 1)].astype(F32)
    alpha, beta = (p0, p1, p2, p3), (q0, q1, q2, q3, q4, q5)
    for k in range(4):
        for j in range(4):
            for part, row, count, flag in alpha_block(k, j):
                rows = pl.ds(block_dst(QUART * k, flag, half), count)
                for t in range(2):
                    wqkv_ref[rows, D * t + QUART * j : D * t + QUART * (j + 1)] = alpha[part][
                        row : row + count, QUART * t : QUART * (t + 1)
                    ]
            for part, row, count, flag in beta_block(k, j):
                rows = pl.ds(block_dst(QUART * k, flag, half), count)
                wqkv_ref[rows, 2 * D + QUART * j : 2 * D + QUART * (j + 1)] = beta[part][
                    row : row + count, :QUART
                ]
                rows = pl.ds(block_dst(QUART * j, flag, half), count)
                wproj_ref[rows, QUART * k : QUART * (k + 1)] = beta[part][row : row + count, QUART:]
    for t in range(3):
        ups[t] = uqkv[:, D * t : D * (t + 1)]
    ups[3] = uproj[...]
    for k in range(4):
        downs[k] = dqkv[:, QUART * k : QUART * (k + 1)]
        downs[4 + k] = dproj[:, QUART * k : QUART * (k + 1)]

    def merge(t, carry):
        cols = pl.ds(pl.multiple_of(D * t, 128), D)
        for k in range(4):
            rows = slice(QUART * k, QUART * (k + 1))
            wqkv_ref[rows, cols] = (wqkv_ref[rows, cols].astype(F32) + tn(downs[k], ups[t])).astype(BF)
        return carry

    lax.fori_loop(0, 3, merge, 0)
    for k in range(4):
        rows = slice(QUART * k, QUART * (k + 1))
        wproj_ref[rows, :] = (wproj_ref[rows, :].astype(F32) + tn(downs[4 + k], ups[3])).astype(BF)


def prep1(where, alpha, beta, cols):
    s = lambda *shape: jax.ShapeDtypeStruct(shape, BF)
    return pl.pallas_call(
        prep1_kernel,
        out_shape=(
            s(D, 3 * D), s(D, D), s(RANK, D), s(RANK, 3 * D), s(RANK, D), s(RANK, D),
            s(RANK, D), s(RANK, 4 * D), s(RANK, 4 * D), s(RANK, D),
            jax.ShapeDtypeStruct((1, D), F32), jax.ShapeDtypeStruct((1, D), F32),
        ),
        in_specs=[sm()] + [vm()] * 14,
        out_specs=[vm()] * 12,
        scratch_shapes=[pltpu.VMEM((4, RANK, D), BF), pltpu.VMEM((8, RANK, QUART), BF)],
        compiler_params=params(24),
        cost_estimate=cost(7),
        name="attention_weights",
    )(where, *alpha, *beta, *cols)


def normalize(values):
    center = jnp.sum(values, axis=1, keepdims=True) / D
    shifted = values - center
    inv_std = lax.rsqrt(jnp.sum(shifted * shifted, axis=1, keepdims=True) / D + EPSILON)
    return shifted * inv_std, inv_std


def norm_back(grad, normed, inv_std):
    first = jnp.sum(grad, axis=1, keepdims=True) / D
    second = jnp.sum(grad * normed, axis=1, keepdims=True) / D
    return inv_std * (grad - first - normed * second)


def barrel(values, amount, left):
    for bit in (1, 2, 4, 8):
        moved = pltpu.roll(values, (128 - bit) if left else bit, 1)
        values = jnp.where((amount & bit) != 0, moved, values)
    return values


def low_half(count):
    return lax.broadcasted_iota(jnp.int32, (count, 128), 1) < HD


def pad_rows(tile):
    if tile.shape[0] == KEYS:
        return tile
    return jnp.concatenate([tile, jnp.zeros((KEYS - tile.shape[0], tile.shape[1]), tile.dtype)], axis=0)


def live_rows():
    return lax.broadcasted_iota(jnp.int32, (KEYS, 128), 0) < SLOTS


GROUP = 6
GROUP_BACK = 6


def pair_columns(pair):
    return tuple(slice(D * t + 128 * pair, D * t + 128 * (pair + 1)) for t in range(3))


def attend_window(kind, row0, qkv_ref, att_ref, exp_ref, inv_ref, rel_ref, shift_ref, keys_ref):
    count = NQ[kind]
    rows = pl.ds(row0, count)
    low_q, low_k = low_half(count), low_half(KEYS)
    live = live_rows()
    ones = jnp.where(live, 1.0, 0.0).astype(BF)
    amount = shift_ref[kind, :count, :]
    onehot = keys_ref[kind]
    rel_mat = rel_ref[...]
    for first in range(0, D // 128, GROUP):
        pairs = range(first, first + GROUP)
        heads = [(pair, odd) for pair in pairs for odd in range(2)]
        q_tile = {p: qkv_ref[rows, pair_columns(p)[0]] for p in pairs}
        rel = {p: nn(q_tile[p], rel_mat) for p in pairs}
        rel = {p: barrel(rel[p], amount, True).astype(BF) for p in pairs}
        k_tile = {p: pad_rows(qkv_ref[rows, pair_columns(p)[1]] * BF(HD**-0.5)) for p in pairs}
        scores = {}
        for p, odd in heads:
            if odd:
                q_aug, k_aug = jnp.where(low_q, rel[p], q_tile[p]), jnp.where(low_k, onehot, k_tile[p])
            else:
                q_aug, k_aug = jnp.where(low_q, q_tile[p], rel[p]), jnp.where(low_k, k_tile[p], onehot)
            scores[p, odd] = nt(q_aug, k_aug)
        top = {h: jnp.max(scores[h], axis=1, keepdims=True) for h in heads}
        exponent = {h: jnp.exp(scores[h] - top[h]).astype(BF) for h in heads}
        both = {}
        for p, odd in heads:
            exp_ref[2 * p + odd, rows, :] = exponent[p, odd]
            v_tile = pad_rows(qkv_ref[rows, pair_columns(p)[2]])
            if kind == FULL:
                v_tile = jnp.where(live, v_tile, 0).astype(BF)
            v_aug = jnp.where(low_k, ones, v_tile) if odd else jnp.where(low_k, v_tile, ones)
            both[p, odd] = nn(exponent[p, odd], v_aug)
        for p in pairs:
            cols = pair_columns(p)[0]
            inverse = 1.0 / pltpu.roll(jnp.where(low_q, both[p, 1], both[p, 0]), HD, 1)
            inv_ref[rows, cols] = inverse
            att_ref[rows, cols] = (jnp.where(low_q, both[p, 0], both[p, 1]) * inverse).astype(BF)


PARTS = ((FULL, FULL), (FULL, FULL), (RIGHT, BOTTOM, CORNER))
PART_ROWS = tuple(sum(NQ[kind] for kind in part) for part in PARTS)
PART_OFFS = (0, PART_ROWS[0], PART_ROWS[0] + PART_ROWS[1])


TAIL = ((0, 576), (576, ROWS))


def qkv_kernel(
    x0, x1, x2, x3, gain_ref, w_hbm, x_hbm, hid_hbm, qkv_a, qkv_b, qkv_c,
    x_ref, hid_ref, rows_ref, w_ref, qkv_ref, sem, out_sem,
):
    loads = [
        pltpu.make_async_copy(w_hbm.at[:, D * t : D * (t + 1)], w_ref.at[t], sem.at[t]) for t in range(3)
    ]
    for load in loads:
        load.start()
    join_pieces((x0, x1, x2, x3), x_ref)
    kept = [
        pltpu.make_async_copy(src, dst, sem.at[3 + i])
        for i, (src, dst) in enumerate(((x_ref, x_hbm), (hid_ref, hid_hbm)))
    ]
    kept[0].start()
    gain = gain_ref[...]

    def norm_step(i, carry):
        rows = pl.ds(pl.multiple_of(i * 112, 16), 112)
        normed, _ = normalize(x_ref[rows, :].astype(F32))
        hidden = (normed * gain).astype(BF)
        rows_ref[rows, :] = hidden
        hid_ref[rows, :] = hidden
        return carry

    lax.fori_loop(0, ROWS // 112, norm_step, 0)
    for w in range(4):
        hid_ref[FULLR * w + SLOTS : FULLR * (w + 1), :] = jnp.zeros((FULLR - SLOTS, D), BF)
    kept[1].start()
    for load in loads:
        load.wait()

    def stores(t):
        cols = pl.ds(pl.multiple_of(D * t, 128), D)
        return [
            pltpu.make_async_copy(
                qkv_ref.at[t, pl.ds(offset, count), :], out.at[:, cols], out_sem.at[t, i]
            )
            for i, (out, offset, count) in enumerate(zip((qkv_a, qkv_b, qkv_c), PART_OFFS, PART_ROWS))
        ]

    def project_step(t, carry):
        qkv_ref[t] = nn(rows_ref[...], w_ref[t]).astype(BF)
        for store in stores(t):
            store.start()
        return carry

    lax.fori_loop(0, 3, project_step, 0)
    for t in range(3):
        for store in stores(t):
            store.wait()
    for store in kept:
        store.wait()


def qkv_rows(pieces, gain, wqkv):
    s = lambda *shape: jax.ShapeDtypeStruct(shape, BF)
    return pl.pallas_call(
        qkv_kernel,
        out_shape=(s(ROWS, D), s(ROWS, D)) + tuple(s(n, 3 * D) for n in PART_ROWS),
        in_specs=[vm()] * 5 + [hbm()],
        out_specs=[hbm()] * 5,
        scratch_shapes=[
            pltpu.VMEM((ROWS, D), BF), pltpu.VMEM((ROWS, D), BF), pltpu.VMEM((ROWS, D), BF),
            pltpu.VMEM((3, D, D), BF), pltpu.VMEM((3, ROWS, D), BF),
            pltpu.SemaphoreType.DMA((5,)), pltpu.SemaphoreType.DMA((3, 3)),
        ],
        compiler_params=params(32),
        cost_estimate=cost(10),
        name="norm_and_qkv",
    )(*pieces, gain, wqkv)


def attention_kernel(qkv_ref, rel_ref, shift_ref, keys_ref, att_ref, exp_ref, inv_ref, *, kinds):
    refs = (qkv_ref, att_ref, exp_ref, inv_ref, rel_ref, shift_ref, keys_ref)
    if kinds[0] == FULL:

        def step(w, carry):
            attend_window(FULL, pl.multiple_of(w * FULLR, 16), *refs)
            return carry

        lax.fori_loop(0, len(kinds), step, 0)
    else:
        row = 0
        for kind in kinds:
            attend_window(kind, row, *refs)
            row += NQ[kind]


def attention(part, qkv, rel, shift, keys):
    rows = PART_ROWS[part]
    s = lambda *shape, dtype=BF: jax.ShapeDtypeStruct(shape, dtype)
    return pl.pallas_call(
        functools.partial(attention_kernel, kinds=PARTS[part]),
        out_shape=(s(rows, D), s(D // HD, rows, KEYS), s(rows, D, dtype=F32)),
        in_specs=[vm()] * 4,
        out_specs=[vm()] * 3,
        compiler_params=params(24),
        cost_estimate=cost(10),
        name="attention_forward",
    )(qkv, rel, shift, keys)


def project_kernel(x_ref, att_a, att_b, att_c, wproj_ref, middle_ref):
    for ref, offset, count in zip((att_a, att_b, att_c), PART_OFFS, PART_ROWS):
        rows = slice(offset, offset + count)
        middle_ref[rows, :] = x_ref[rows, :].astype(F32) + nn(ref[...], wproj_ref[...])


def project(x, atts, wproj):
    return pl.pallas_call(
        project_kernel,
        out_shape=jax.ShapeDtypeStruct((ROWS, D), F32),
        in_specs=[vm()] * 5,
        out_specs=vm(),
        compiler_params=params(20),
        cost_estimate=cost(5),
        name="projection",
    )(x, *atts, wproj)


CHUNK = 512
LOCK = 1


def mlp_kernel(
    where_ref, middle_ref, g0, g1, g2, g3, gain_ref,
    p0, p1, p2, p3, q0, q1, q2, q3, q4, q5, d1, u1, d2, u2,
    o0, o1, o2, gmid_ref, down1, up1, down2, up2,
    gm_ref, out_rows, h2_ref, acc_mlp, acc_gh, gu1, ad2, w1_ref, w2_ref, downs, sem,
):
    half = where_ref[1]
    copies = []

    def fetch(src, dst):
        copies.append(pltpu.make_async_copy(src, dst, sem.at[len(copies)]))
        copies[-1].start()

    alpha, beta = (p0, p1, p2, p3), (q0, q1, q2, q3, q4, q5)
    for k in range(4):
        for j in range(4):
            for part, row, count, flag in alpha_block(k, j):
                rows = pl.ds(block_dst(QUART * k, flag, half), count)
                fetch(alpha[part].at[row : row + count, :], w1_ref.at[rows, D * j : D * (j + 1)])
            for part, row, count, flag in beta_block(k, j):
                rows = pl.ds(block_dst(QUART * k, flag, half), count)
                fetch(beta[part].at[row : row + count, :], w2_ref.at[rows, D * j : D * (j + 1)])
    join_pieces((g0, g1, g2, g3), gm_ref)
    for k in range(4):
        downs[k] = d1[:, QUART * k : QUART * (k + 1)]
        downs[4 + k] = u2[:, QUART * k : QUART * (k + 1)]
    for copy in copies:
        copy.wait()

    def merge(j, carry):
        cols = pl.ds(pl.multiple_of(D * j, 128), D)
        for k in range(4):
            rows = slice(QUART * k, QUART * (k + 1))
            w1_ref[rows, cols] = (w1_ref[rows, cols].astype(F32) + tn(downs[k], u1[:, cols])).astype(BF)
            w2_ref[rows, cols] = (w2_ref[rows, cols].astype(F32) + tn(downs[4 + k], d2[:, cols])).astype(BF)
        return carry

    lax.fori_loop(0, 4, merge, 0)
    gain = gain_ref[...]
    down1[...] = jnp.zeros_like(down1)
    up1[...] = jnp.zeros_like(up1)
    down2[...] = jnp.zeros_like(down2)
    up2[...] = jnp.zeros_like(up2)

    def tile_step(t, carry):
        rows = pl.ds(pl.multiple_of(t * HALF, 16), HALF)
        normed, _ = normalize(middle_ref[rows, :])
        h2 = (normed * gain).astype(BF)
        h2_ref[...] = h2
        gm = gm_ref[rows, :]
        ad1 = nt(d1[...], h2).astype(BF)
        gu2 = nt(u2[...], gm).astype(BF)
        acc_mlp[...] = jnp.zeros_like(acc_mlp)
        acc_gh[...] = jnp.zeros_like(acc_gh)
        gu1[...] = jnp.zeros_like(gu1)
        ad2[...] = jnp.zeros_like(ad2)

        def chunk_step(c, inner_carry):
            spans = [
                pl.ds(pl.multiple_of((c * LOCK + i) * CHUNK, CHUNK), CHUNK) for i in range(LOCK)
            ]
            h2 = h2_ref[...]
            gm = gm_ref[rows, :]
            inner = [nn(h2, w1_ref[:, span]) for span in spans]
            gact = [nn(gm, w2_ref[:, span]) for span in spans]
            act, ginner = [], []
            for i in range(LOCK):
                half = 0.5 * (1.0 + lax.erf(inner[i] * 2**-0.5))
                act.append((inner[i] * half).astype(BF))
                slope = half + inner[i] * (jnp.exp(-0.5 * inner[i] * inner[i]) * (2 * np.pi) ** -0.5)
                ginner.append((gact[i] * slope).astype(BF))
            for i, span in enumerate(spans):
                acc_mlp[...] += nt(act[i], w2_ref[:, span])
                acc_gh[...] += nt(ginner[i], w1_ref[:, span])
                up1[:, span] += nn(ad1, ginner[i])
                gu1[...] += nt(u1[:, span], ginner[i])
                ad2[...] += nt(d2[:, span], act[i])
                down2[:, span] += nn(gu2, act[i])
            return inner_carry

        lax.fori_loop(0, 4 * D // (CHUNK * LOCK), chunk_step, 0)
        down1[...] += nn(gu1[...].astype(BF), h2_ref[...])
        up2[...] += nn(ad2[...].astype(BF), gm_ref[rows, :])
        middle = middle_ref[rows, :]
        out_rows[rows, :] = (middle + acc_mlp[...]).astype(BF)
        normed, inv_std = normalize(middle)
        gmid_ref[rows, :] = gm_ref[rows, :].astype(F32) + norm_back(acc_gh[...] * gain, normed, inv_std)
        return carry

    lax.fori_loop(0, 2, tile_step, 0)
    split_pieces(out_rows, (o0, o1, o2))


def mlp(where, middle, pieces, gain, alpha, beta, d1, u1, d2, u2):
    s = lambda *shape, dtype=F32: jax.ShapeDtypeStruct(shape, dtype)
    return pl.pallas_call(
        mlp_kernel,
        out_shape=pieces_of(ROWS)
        + (s(ROWS, D), s(RANK, D), s(RANK, 4 * D), s(RANK, 4 * D), s(RANK, D)),
        in_specs=[sm()] + [vm()] * 6 + [pl.BlockSpec(memory_space=pl.ANY)] * 10 + [vm()] * 4,
        out_specs=[vm()] * 8,
        scratch_shapes=[
            pltpu.VMEM((ROWS, D), BF), pltpu.VMEM((ROWS, D), BF), pltpu.VMEM((HALF, D), BF),
            pltpu.VMEM((HALF, D), F32), pltpu.VMEM((HALF, D), F32),
            pltpu.VMEM((RANK, HALF), F32), pltpu.VMEM((RANK, HALF), F32),
            pltpu.VMEM((D, 4 * D), BF), pltpu.VMEM((D, 4 * D), BF), pltpu.VMEM((8, RANK, QUART), BF),
            pltpu.SemaphoreType.DMA((4 * 4 * 4,)),
        ],
        compiler_params=params(48),
        cost_estimate=cost(48),
        name="mlp_forward_backward",
    )(where, middle, *pieces, gain, *alpha, *beta, d1, u1, d2, u2)


def attend_back_window(
    kind, row0, qkv_ref, att_ref, exp_ref, inv_ref, gatt_ref, gqkv_ref, rel_ref, shift_ref, keys_ref
):
    count = NQ[kind]
    rows = pl.ds(row0, count)
    low_q, low_k = low_half(count), low_half(KEYS)
    live = live_rows()
    lane_k = lax.broadcasted_iota(jnp.int32, (KEYS, 128), 1) % HD
    lane_q = lax.broadcasted_iota(jnp.int32, (count, 128), 1) % HD
    ones = jnp.where(live & (lane_k < 2), 1.0, 0.0).astype(BF)
    across = jnp.where(
        low_half(128) != (lax.broadcasted_iota(jnp.int32, (128, 128), 0) < HD), -1.0, 0.0
    ).astype(BF)
    amount = shift_ref[kind, :count, :]
    onehot = keys_ref[kind]
    rel_mat = rel_ref[...]
    for first in range(0, D // 128, GROUP_BACK):
        pairs = range(first, first + GROUP_BACK)
        heads = [(pair, odd) for pair in pairs for odd in range(2)]
        go_tile = {
            p: (gatt_ref[rows, pair_columns(p)[0]].astype(F32) * inv_ref[rows, pair_columns(p)[0]]).astype(BF)
            for p in pairs
        }
        delta = {
            p: nn((go_tile[p].astype(F32) * att_ref[rows, pair_columns(p)[0]].astype(F32)).astype(BF), across)
            for p in pairs
        }
        go_t = {p: go_tile[p].T for p in pairs}
        gv = {}
        for p, odd in heads:
            gv[p, odd] = nn(go_t[p][HD * odd : HD * (odd + 1), :], exp_ref[2 * p + odd, rows, :])
        gscore = {}
        for p in pairs:
            high = delta[p].astype(BF)
            rest = (delta[p] - high.astype(F32)).astype(BF)
            low_delta = jnp.where(lane_q == 0, high, jnp.where(lane_q == 1, rest, 0)).astype(BF)
            v_tile = pad_rows(qkv_ref[rows, pair_columns(p)[2]])
            if kind == FULL:
                v_tile = jnp.where(live, v_tile, 0).astype(BF)
            gscore[p, 0] = nt(jnp.where(low_q, go_tile[p], low_delta), jnp.where(low_k, v_tile, ones))
            gscore[p, 1] = nt(jnp.where(low_q, low_delta, go_tile[p]), jnp.where(low_k, ones, v_tile))
        q_t = {p: qkv_ref[rows, pair_columns(p)[0]].T for p in pairs}
        gs = {(p, odd): (exp_ref[2 * p + odd, rows, :].astype(F32) * gscore[p, odd]).astype(BF) for p, odd in heads}
        gk = {(p, odd): nn(q_t[p][HD * odd : HD * (odd + 1), :], gs[p, odd]) for p, odd in heads}
        gq = {}
        for p in pairs:
            k_tile = pad_rows(qkv_ref[rows, pair_columns(p)[1]] * BF(HD**-0.5))
            gq[p, 0] = nn(gs[p, 0], jnp.where(low_k, k_tile, onehot))
            gq[p, 1] = nn(gs[p, 1], jnp.where(low_k, onehot, k_tile))
        sums = {p: barrel(jnp.where(low_q, gq[p, 1], gq[p, 0]), amount, False).astype(BF) for p in pairs}
        for p in pairs:
            cols, kcols, vcols = pair_columns(p)
            gv_tile = jnp.concatenate([gv[p, 0], gv[p, 1]], axis=0).astype(BF).T
            gqkv_ref[rows, vcols] = gv_tile[:count, :]
            gk_tile = (jnp.concatenate([gk[p, 0], gk[p, 1]], axis=0) * HD**-0.5).astype(BF).T
            gqkv_ref[rows, kcols] = gk_tile[:count, :]
            gqkv_ref[rows, cols] = (jnp.where(low_q, gq[p, 0], gq[p, 1]) + nt(sums[p], rel_mat)).astype(BF)


def attention_back_kernel(
    gmid_hbm, hid_hbm, qkv_a, qkv_b, qkv_c, att_a, att_b, att_c, exp_a, exp_b, exp_c, inv_a, inv_b, inv_c,
    wproj_ref, rel_ref, shift_ref, keys_ref, dqkv, uqkv, dproj, uproj,
    gqkv_hbm, down_q, up_q, down_p, up_p,
    gmid_ref, hid_ref, qkv_ref, att_ref, exp_ref, inv_ref, gqkv_ref, gb_ref, gatt_ref, sem, out_sem,
):
    spans = [pl.ds(offset, count) for offset, count in zip(PART_OFFS, PART_ROWS)]
    pairs = [(gmid_hbm, gmid_ref)]
    for part, srcs in enumerate(
        ((qkv_a, inv_a, att_a, exp_a), (qkv_b, inv_b, att_b, exp_b), (qkv_c, inv_c, att_c, exp_c))
    ):
        rows = spans[part]
        for src, dst in zip(srcs, (qkv_ref, inv_ref, att_ref)):
            pairs.append((src, dst.at[rows, :]))
        pairs.append((srcs[3], exp_ref.at[:, rows, :]))
    pairs.append((hid_hbm, hid_ref))
    loads = [pltpu.make_async_copy(src, dst, sem.at[i]) for i, (src, dst) in enumerate(pairs)]
    for load in loads:
        load.start()

    def wait_part(part):
        for load in loads[1 + 4 * part : 5 + 4 * part]:
            load.wait()

    stores = [
        pltpu.make_async_copy(gqkv_ref.at[rows, :], gqkv_hbm.at[rows, :], out_sem.at[i])
        for i, rows in enumerate(spans)
    ]
    loads[0].wait()
    gb_ref[...] = gmid_ref[...].astype(BF)
    gatt_ref[...] = nt(gb_ref[...], wproj_ref[...]).astype(BF)
    refs = (qkv_ref, att_ref, exp_ref, inv_ref, gatt_ref, gqkv_ref, rel_ref, shift_ref, keys_ref)

    def step(w, carry):
        for part in range(2):

            @pl.when(w == 2 * part)
            def _():
                wait_part(part)

        attend_back_window(FULL, pl.multiple_of(w * FULLR, 16), *refs)
        return carry

    lax.fori_loop(0, 4, step, 0)
    stores[0].start()
    stores[1].start()
    wait_part(2)
    for kind in (RIGHT, BOTTOM, CORNER):
        attend_back_window(kind, OFFS[kind], *refs)
    stores[2].start()
    up_p[...] = nn(nt(dproj[...], att_ref[...]).astype(BF), gb_ref[...])
    down_p[...] = nn(nt(uproj[...], gb_ref[...]).astype(BF), att_ref[...])
    loads[-1].wait()
    up_q[...] = nn(nt(dqkv[...], hid_ref[...]).astype(BF), gqkv_ref[...])
    down_q[...] = nn(nt(uqkv[...], gqkv_ref[...]).astype(BF), hid_ref[...])
    for store in stores:
        store.wait()


def attention_back(gmid, hid, qkvs, atts, exps, invs, wproj, rel, shift, keys, dqkv, uqkv, dproj, uproj):
    s = lambda *shape, dtype=F32: jax.ShapeDtypeStruct(shape, dtype)
    return pl.pallas_call(
        attention_back_kernel,
        out_shape=(s(ROWS, 3 * D, dtype=BF), s(RANK, D), s(RANK, 3 * D), s(RANK, D), s(RANK, D)),
        in_specs=[hbm()] * 14 + [vm()] * 8,
        out_specs=[hbm()] + [vm()] * 4,
        scratch_shapes=[
            pltpu.VMEM((ROWS, D), F32), pltpu.VMEM((ROWS, D), BF), pltpu.VMEM((ROWS, 3 * D), BF),
            pltpu.VMEM((ROWS, D), BF), pltpu.VMEM((D // HD, ROWS, KEYS), BF), pltpu.VMEM((ROWS, D), F32),
            pltpu.VMEM((ROWS, 3 * D), BF), pltpu.VMEM((ROWS, D), BF), pltpu.VMEM((ROWS, D), BF),
            pltpu.SemaphoreType.DMA((14,)), pltpu.SemaphoreType.DMA((3,)),
        ],
        compiler_params=params(52),
        cost_estimate=cost(28),
        name="attention_backward",
    )(gmid, hid, *qkvs, *atts, *exps, *invs, wproj, rel, shift, keys, dqkv, uqkv, dproj, uproj)


def token_grad_kernel(gmid_hbm, x_hbm, gqkv_hbm, gain_ref, wqkv_ref, o0, o1, o2,
                      gmid_ref, x_ref, gqkv_ref, gh_ref, out_rows, sem, *, low, high):
    span = pl.ds(low, high - low)
    copies = [
        pltpu.make_async_copy(src.at[span, :], dst, sem.at[i])
        for i, (src, dst) in enumerate(((gqkv_hbm, gqkv_ref), (x_hbm, x_ref), (gmid_hbm, gmid_ref)))
    ]
    for copy in copies:
        copy.start()
    copies[0].wait()
    gh_ref[...] = nt(gqkv_ref[...], wqkv_ref[...])
    copies[1].wait()
    copies[2].wait()
    gain = gain_ref[...]
    step = (high - low) // 2

    def norm_step(i, carry):
        rows = pl.ds(pl.multiple_of(i * step, 16), step)
        normed, inv_std = normalize(x_ref[rows, :].astype(F32))
        back = norm_back(gh_ref[rows, :] * gain, normed, inv_std)
        out_rows[rows, :] = (gmid_ref[rows, :] + back).astype(BF)
        return carry

    lax.fori_loop(0, 2, norm_step, 0)
    split_pieces(out_rows, (o0, o1, o2))


def token_grad(gmid, x, gqkv, gain, wqkv, low, high):
    count = high - low
    return pl.pallas_call(
        functools.partial(token_grad_kernel, low=low, high=high),
        out_shape=pieces_of(count),
        in_specs=[hbm(), hbm(), hbm(), vm(), vm()],
        out_specs=[vm()] * 3,
        scratch_shapes=[
            pltpu.VMEM((count, D), F32), pltpu.VMEM((count, D), BF), pltpu.VMEM((count, 3 * D), BF),
            pltpu.VMEM((count, D), F32), pltpu.VMEM((count, D), BF), pltpu.SemaphoreType.DMA((3,)),
        ],
        compiler_params=params(28),
        cost_estimate=cost(8),
        name="token_gradient",
    )(gmid, x, gqkv, gain, wqkv)


def grad_pack_kernel(where_ref, down_q, up_q, down_p, up_p, down1, up1, down2, up2, o0, o1, o2, o3, buf_ref):
    mine = where_ref[0]
    for k in range(4):
        for i, ref in enumerate((down_q, down1, up_p, up2)):
            buf_ref[k, :RANK, QUART * i : QUART * (i + 1)] = ref[:, QUART * k : QUART * (k + 1)]
    for dest in range(4):
        k = jnp.bitwise_xor(mine, dest)
        ranks = slice(RANK // 4 * dest, RANK // 4 * (dest + 1))
        for j in range(4):
            base = RANK + 12 * j
            for t in range(3):
                buf_ref[k, base : base + 4, QUART * t : QUART * (t + 1)] = up_q[
                    ranks, D * t + QUART * j : D * t + QUART * (j + 1)
                ]
            buf_ref[k, base : base + 4, 3 * QUART :] = down_p[ranks, QUART * j : QUART * (j + 1)]
            buf_ref[k, base + 4 : base + 8, :] = up1[ranks, D * j : D * (j + 1)]
            buf_ref[k, base + 8 : base + 12, :] = down2[ranks, D * j : D * (j + 1)]
    for k, out in enumerate((o0, o1, o2, o3)):
        out[...] = buf_ref[k].astype(BF)


def grad_pack(where, *grads):
    return pl.pallas_call(
        grad_pack_kernel,
        out_shape=(jax.ShapeDtypeStruct((4 * RANK, D), BF),) * 4,
        in_specs=[sm()] + [vm()] * 8,
        out_specs=[vm()] * 4,
        scratch_shapes=[pltpu.VMEM((4, 4 * RANK, D), F32)],
        compiler_params=params(8),
        cost_estimate=cost(2),
        name="adapter_grad_pack",
    )(where, *grads)


def grad_sum_kernel(g0, g1, g2, g3, o0, o1, o2, o3, buf_ref):
    total = g0[...].astype(F32) + g1[...].astype(F32) + g2[...].astype(F32) + g3[...].astype(F32)
    buf_ref[...] = jnp.zeros_like(buf_ref)
    buf_ref[:RANK, :] = total[:RANK, :]
    for j, out in enumerate((o0, o1, o2, o3)):
        buf_ref[RANK : RANK + 12, :] = total[RANK + 12 * j : RANK + 12 * (j + 1), :]
        out[...] = buf_ref[...].astype(BF)


def grad_sum(pieces):
    return pl.pallas_call(
        grad_sum_kernel,
        out_shape=(jax.ShapeDtypeStruct((2 * RANK, D), BF),) * 4,
        in_specs=[vm()] * 4,
        out_specs=[vm()] * 4,
        scratch_shapes=[pltpu.VMEM((2 * RANK, D), F32)],
        compiler_params=params(4),
        cost_estimate=cost(2),
        name="adapter_grad_sum",
    )(*pieces)


def grad_adapters_kernel(index_ref, x_ref, qkv_dn, fc1_dn, proj_up, fc2_up, rest_ref, acc_ref):
    acc_ref[...] = jnp.zeros_like(acc_ref)

    def add(i, carry):
        acc_ref[index_ref[i]] += x_ref[i].astype(F32)
        return carry

    lax.fori_loop(0, x_ref.shape[0], add, 0)
    for i, ref in enumerate((qkv_dn, fc1_dn, proj_up, fc2_up)):
        ref[...] = acc_ref[:, :RANK, QUART * i : QUART * (i + 1)]
    rest_ref[...] = acc_ref[:, RANK:, :].astype(BF)


def grad_adapters(index, x):
    s = lambda n, dtype=F32: jax.ShapeDtypeStruct((ADAPT, RANK, n), dtype)
    return pl.pallas_call(
        grad_adapters_kernel,
        out_shape=(s(QUART), s(QUART), s(QUART), s(QUART), s(D, BF)),
        in_specs=[sm(), vm()],
        out_specs=[vm()] * 5,
        scratch_shapes=[pltpu.VMEM((ADAPT, 2 * RANK, D), F32)],
        compiler_params=params(8),
        cost_estimate=cost(2),
        name="adapter_grad_by_adapter",
    )(index, x)


def grad_join_kernel(where_ref, r0, r1, r2, r3, qkv_up, proj_dn, fc1_up, fc2_dn, buf_ref):
    mine = where_ref[0]
    heads = qkv_up.shape[2] // (3 * HD)
    for k, ref in enumerate((r0, r1, r2, r3)):
        buf_ref[jnp.bitwise_xor(mine, k)] = ref[...].astype(F32)
    for source in range(4):
        ranks = slice(RANK // 4 * source, RANK // 4 * (source + 1))
        for h in range(heads):
            for t in range(3):
                qkv_up[:, ranks, HD * (3 * h + t) : HD * (3 * h + t + 1)] = buf_ref[
                    source, :, 0:4, QUART * t + HD * h : QUART * t + HD * (h + 1)
                ]
        proj_dn[:, ranks, :] = buf_ref[source, :, 0:4, 3 * QUART :]
        fc1_up[:, ranks, :] = buf_ref[source, :, 4:8, :]
        fc2_dn[:, ranks, :] = buf_ref[source, :, 8:12, :]


def grad_join(where, pieces):
    s = lambda n: jax.ShapeDtypeStruct((ADAPT, RANK, n), F32)
    return pl.pallas_call(
        grad_join_kernel,
        out_shape=(s(3 * QUART), s(QUART), s(D), s(D)),
        in_specs=[sm()] + [vm()] * 4,
        out_specs=[vm()] * 4,
        scratch_shapes=[pltpu.VMEM((4, ADAPT, RANK, D), F32)],
        compiler_params=params(12),
        cost_estimate=cost(2),
        name="adapter_grad_join",
    )(where, *pieces)


def flip(values, axis, distance):
    size = lax.axis_size(axis)
    return lax.ppermute(values, axis, [(i, i ^ distance) for i in range(size)])


def send_rows(pieces, *deps):
    own, near, pair = pieces
    if deps:
        near, = after((near,), *deps)
    return [own, flip(near, "row", 1), flip(pair, "row", 2)]


def hand_on(pieces, *deps):
    own, near, crossed = pieces
    if deps:
        near, crossed = after((near, crossed), *deps)
    return [own, near, crossed, flip(crossed, "row", 1)]


def exchange(slots, axis):
    return [slots[0]] + [flip(slots[k], axis, k) for k in range(1, 4)]


def after(values, *deps):
    return lax.optimization_barrier((tuple(values), deps))[0]


def col_halves(half):
    return jnp.concatenate([flip(half, "col", j) for j in range(1, 4)], axis=0)


def col_pairs(half, other_row):
    two = jnp.concatenate([half, other_row], axis=0)
    return jnp.concatenate([other_row] + [flip(two, "col", j) for j in range(1, 4)], axis=0)


def body(
    tokens, grad_out, adapter_index, norm1_gain, norm2_gain, qkv_weight, proj_weight, fc1_weight, fc2_weight,
    rel_h, rel_w, qkv_down, qkv_up, proj_down, proj_up, fc1_down, fc1_up, fc2_down, fc2_up,
):
    members = lax.axis_size("col")
    batches = lax.axis_size("dp")
    row_index, col_index, dp_index = lax.axis_index("row"), lax.axis_index("col"), lax.axis_index("dp")
    half = dp_index % 2
    where = jnp.stack([row_index, half]).astype(jnp.int32)
    slot_images = (
        jnp.bitwise_xor(dp_index, jnp.arange(batches, dtype=jnp.int32))[:, None] * members
        + jnp.bitwise_xor(col_index, jnp.arange(members, dtype=jnp.int32))[None, :]
    ).reshape(-1)
    slot_adapters = jnp.sum(
        jnp.where(
            slot_images[:, None] == jnp.arange(adapter_index.shape[0], dtype=jnp.int32)[None, :],
            adapter_index[:, 0][None, :],
            0,
        ),
        axis=1,
    )
    pick = jnp.concatenate([slot_adapters[:4], half[None]]).astype(jnp.int32)
    swap = lambda m: jnp.swapaxes(m, 1, 2)

    shift, keys = jnp.asarray(SHIFT_NP), jnp.asarray(KEYS_NP)

    *token_slots, alpha_own, beta_own, alpha_half, cross, fc1_half, fc2_half = front(
        where, tokens, qkv_weight, proj_weight, fc1_weight, fc2_weight
    )
    crossed = flip(cross, "row", 2)
    beta_half, b0 = cross[:HBLK], crossed[:HBLK]
    c0 = jnp.concatenate([crossed[HBLK : 2 * HBLK], crossed[2 * HBLK :]], axis=1)
    alpha_near = col_halves(alpha_half)
    x_pieces = send_rows(token_slots, crossed)
    *send, row_adapters, rel = adapter_pack(
        pick, qkv_up, swap(proj_down), fc1_up, swap(fc2_down), swap(qkv_down), swap(fc1_down), proj_up, fc2_up,
        norm1_gain.reshape(1, -1), norm2_gain.reshape(1, -1), rel_h, rel_w,
    )
    beta_sent = [jnp.concatenate([beta_half, b0, send[j]], axis=0) for j in range(1, 4)]
    beta_got = [flip(m, "col", j) for j, m in enumerate(beta_sent, 1)]
    alpha_near, x_pieces[1] = after((alpha_near, x_pieces[1]))
    alpha_far = flip(alpha_near, "dp", 1)
    g = jnp.concatenate([alpha_own, alpha_near, alpha_far, row_adapters], axis=0)
    g, *x_pieces = after((g, *x_pieces))
    gy = flip(g, "row", 2)
    grad_slots = pack(where, grad_out)
    *beta_got, _ = after((*beta_got, grad_slots[0]))
    beta_near = jnp.concatenate([b0] + [m[:QUART] for m in beta_got], axis=0)
    col_adapters = [send[0]] + beta_got
    beta_far = flip(beta_near, "dp", 1)
    x_pieces = hand_on(x_pieces)

    g1, own1, near1 = (flip(m, "row", 1) for m in (g, beta_own, beta_near))
    fc1_half, = after((fc1_half,), g1, own1, near1, x_pieces[3])
    fc1_near = [flip(fc1_half, "col", j) for j in range(1, 4)]
    gy, beta_far, fc2_half, c0 = after((gy, beta_far, fc2_half, c0), *fc1_near)
    fc2_two = jnp.concatenate([fc2_half, c0], axis=0)
    fc2_near = [flip(fc2_two, "col", j) for j in range(1, 4)]
    gy1, far1 = flip(gy, "row", 1), flip(beta_far, "row", 1)
    *grad_slots, fc1_near = after((*grad_slots, jnp.concatenate(fc1_near, axis=0)), gy1, far1)
    fc1_far = flip(fc1_near, "dp", 1)
    g_pieces = send_rows(grad_slots, fc2_near[0], fc2_near[1], fc2_near[2])
    wqkv, wproj, dqkv, uqkv, dproj, uproj, d1, u1, d2, u2, gain1, gain2 = prep1(
        where, (g, g1, gy, gy1), (beta_own, beta_near, beta_far, own1, near1, far1), col_adapters
    )
    h = jnp.concatenate([fc1_weight, fc1_near, fc1_far], axis=0)
    wqkv, h, *fc2_near = after((wqkv, h, *fc2_near), g_pieces[2])
    hy = flip(h, "row", 2)
    fc2_near = jnp.concatenate([c0] + fc2_near, axis=0)
    fc2_far = flip(fc2_near, "dp", 1)
    x, hid, *qkvs = qkv_rows(x_pieces, gain1, wqkv)
    g_pieces = hand_on(g_pieces, qkvs[0])
    part0 = attention(0, qkvs[0], rel, shift, keys)
    qkv1, = after((qkvs[1],), part0[0])
    part1 = attention(1, qkv1, rel, shift, keys)
    qkv2, _ = after((qkvs[2], part1[0]))
    part2 = attention(2, qkv2, rel, shift, keys)
    atts, exps, invs = zip(part0, part1, part2)
    atts = list(atts)
    atts[2], hy = after((atts[2], hy))
    alpha2 = [h, flip(h, "row", 1), hy, flip(hy, "row", 1)]
    middle = project(x, atts, wproj)
    middle, fc2_far = after((middle, fc2_far))
    beta2 = [fc2_weight, fc2_near, fc2_far] + [flip(m, "row", 1) for m in (fc2_weight, fc2_near, fc2_far)]

    *out_slots, gmid, down1, up1, down2, up2 = mlp(where, middle, g_pieces, gain2, alpha2, beta2, d1, u1, d2, u2)
    out_pieces = send_rows(out_slots)
    gqkv, down_q, up_q, down_p, up_p = attention_back(
        gmid, hid, qkvs, atts, exps, invs, wproj, rel, shift, keys, dqkv, uqkv, dproj, uproj
    )
    out_pieces = hand_on(out_pieces, gqkv)
    gqkv, down_q, up_q, down_p, up_p = after((gqkv, down_q, up_q, down_p, up_p), *out_pieces[:3])
    packed = grad_pack(where, down_q, up_q, down_p, up_p, down1, up1, down2, up2)
    *packed, gqkv = after((*packed, gqkv))
    row_sums = exchange(packed, "row")
    back0 = token_grad(gmid, x, gqkv, gain1, wqkv, *TAIL[0])
    *row_sums, gqkv, b0, b1, b2 = after((*row_sums, gqkv, *back0))
    back_pieces = send_rows((b0, b1, b2))
    summed = grad_sum(row_sums)
    *summed, gqkv = after((*summed, gqkv))
    images = exchange(summed, "col")
    back1 = token_grad(gmid, x, gqkv, gain1, wqkv, *TAIL[1])
    last_pieces = send_rows(back1)
    *images, near, crossed = after((*images, *back_pieces[1:]), back1[0])
    back_pieces = hand_on([back_pieces[0], near, crossed])
    images = jnp.stack(images)
    images, *out_pieces = after((images, *out_pieces))
    step = 1
    while step < batches:
        images = jnp.concatenate([images, flip(images, "dp", step)], axis=0)
        step *= 2
    result = unpack(where, out_pieces, BF)
    images, = after((images,), result)
    qkv_dn, fc1_dn, proj_upg, fc2_upg, rest = grad_adapters(slot_adapters.astype(jnp.int32), images)
    rests = [rest] + [flip(rest, "row", k) for k in range(1, 4)]
    grad_tokens = unpack(where, back_pieces + hand_on(last_pieces, rest), F32, TAIL)
    rests = after(tuple(rests), grad_tokens)
    qkv_upg, proj_dn, fc1_upg, fc2_dn = grad_join(where, rests)
    return (
        result, grad_tokens,
        swap(qkv_dn), qkv_upg, swap(proj_dn), proj_upg, swap(fc1_dn), fc1_upg, swap(fc2_dn), fc2_upg,
    )


def solution(mesh):
    return jax.shard_map(
        body,
        mesh=mesh,
        in_specs=(
            P("row", ("dp", "col")), P("row", ("dp", "col")), P(), P("row"), P("row"),
            P("row", "col"), P("col", "row"), P("row", "col"), P("row", "col"), P(), P(),
            P(None, "row", None), P(None, None, "col"), P(None, "col", None), P(None, None, "row"),
            P(None, "row", None), P(None, None, "col"), P(None, "col", None), P(None, None, "row"),
        ),
        out_specs=(
            P("row", ("dp", "col")), P("row", ("dp", "col")),
            P(None, "row", None), P(None, None, "col"), P(None, "col", None), P(None, None, "row"),
            P(None, "row", None), P(None, None, "col"), P(None, "col", None), P(None, None, "row"),
        ),
        check_vma=False,
    )
```

```python
import functools

import jax
import jax.numpy as jnp
import numpy as np
from jax import lax
from jax.experimental import pallas as pl
from jax.experimental.pallas import tpu as pltpu
from jax.sharding import PartitionSpec as P

D = 768
HD = 64
WIN = 14
SLOTS = WIN * WIN
SIDE = 64
ADAPT = 8
NWIN = 5
IMG_TOK = NWIN * NWIN * SLOTS
RANK = 16
EDGE = SIDE - (NWIN - 1) * WIN
QUART = D // 4
FULLR = 208
KEYS = 208
EDGER = EDGE * WIN
CORNR = EDGE * EDGE
ROWS = 4 * FULLR + 2 * EDGER + CORNR
HALF = ROWS // 2
HBLK = QUART // 2
EPSILON = 1e-06
BF = jnp.bfloat16
F32 = jnp.float32

FULL, RIGHT, BOTTOM, CORNER = 0, 1, 2, 3
NQ = (FULLR, EDGER, EDGER, CORNR)
OFFS = (0, 4 * FULLR, 4 * FULLR + EDGER, 4 * FULLR + 2 * EDGER)


def slot_order(kind):
    rows = EDGE if kind in (BOTTOM, CORNER) else WIN
    cols = EDGE if kind in (RIGHT, CORNER) else WIN
    kept = [a * WIN + b for a in range(rows) for b in range(cols)]
    rest = [s for s in range(SLOTS) if s not in set(kept)]
    return kept, kept + rest


def build_tables():
    shift = np.zeros((4, FULLR, 128), np.int32)
    keys = np.zeros((4, KEYS, 128), np.float32)
    for kind in range(4):
        kept, order = slot_order(kind)
        for i, s in enumerate(kept):
            for base in (0, 64):
                shift[kind, i, base : base + 32] = WIN - 1 - s // WIN
                shift[kind, i, base + 32 : base + 64] = WIN - 1 - s % WIN
        spare = order[0] if kind == FULL else order[-1]
        for i, s in enumerate(order + [spare] * (KEYS - SLOTS)):
            for base in (0, 64):
                keys[kind, i, base + s // WIN] = 1.0
                keys[kind, i, base + 32 + s % WIN] = 1.0
    return shift, keys.astype(jnp.bfloat16)


SHIFT_NP, KEYS_NP = build_tables()


def nn(a, b):
    return jnp.dot(a, b, preferred_element_type=F32)


def nt(a, b):
    return lax.dot_general(a, b, (((1,), (1,)), ((), ())), preferred_element_type=F32)


def tn(a, b):
    return lax.dot_general(a, b, (((0,), (0,)), ((), ())), preferred_element_type=F32)


def vm():
    return pl.BlockSpec(memory_space=pltpu.VMEM)


def hbm():
    return pl.BlockSpec(memory_space=pl.ANY)


def in_hbm(x):
    return pltpu.with_memory_space_constraint(x, pltpu.HBM)


def arg():
    return pl.BlockSpec(memory_space=pltpu.HBM)


def sm():
    return pl.BlockSpec(memory_space=pltpu.SMEM)


def params(mib=60):
    return pltpu.CompilerParams(vmem_limit_bytes=mib * 1024 * 1024)


def cost(us):
    return pl.CostEstimate(flops=int(us * 1e6), transcendentals=0, bytes_accessed=0)


def place_window(kind, count, moved, width, spare=-100000):
    row = lax.broadcasted_iota(jnp.int32, (count, width), 0)
    lane = lax.broadcasted_iota(jnp.int32, (count, width), 1)
    if kind in (RIGHT, CORNER):
        src = (row // EDGE) * WIN + row % EDGE
    else:
        src = jnp.where(row < SLOTS, row, spare)
    return (lane == src + moved).astype(F32).astype(BF)


def window_list(dest):
    items = [(FULL, FULLR * j, NWIN * dest + j) for j in range(4)]
    items.append((RIGHT, OFFS[1], NWIN * dest + 4))
    items.append((BOTTOM, OFFS[2], NWIN * 4 + dest))
    if dest == 3:
        items.append((CORNER, OFFS[3], NWIN * NWIN - 1))
    return items


def window_span(window):
    start = window * SLOTS
    low = start // 128 * 128
    high = min(-(-(start + SLOTS) // 128) * 128, IMG_TOK)
    return low, high, start - low


def pack_rows(mine, x_ref, rows_ref, spare):
    for dest in range(4):
        slot = jnp.bitwise_xor(mine, dest)
        if dest != 3:
            rows_ref[slot, OFFS[3] :, :] = jnp.zeros((CORNR, QUART), BF)
        for kind, offset, window in window_list(dest):
            low, high, moved = window_span(window)
            pick = place_window(kind, NQ[kind], moved, high - low, spare)
            rows_ref[slot, offset : offset + NQ[kind], :] = nt(pick, x_ref[:, low:high]).astype(BF)


def fold(rows_ref, outs):
    half = rows_ref.shape[1] // 2
    for slot, (out, base) in enumerate(((outs[0], 0), (outs[1], 0), (outs[2], 0), (outs[2], half))):
        out[base : base + half, :QUART] = rows_ref[slot, :half, :]
        out[base : base + half, QUART:] = rows_ref[slot, half:, :]


def pack_kernel(where_ref, x_hbm, o0, o1, o2, rows_ref, x_ref, sem):
    load = pltpu.make_async_copy(x_hbm, x_ref, sem)
    load.start()
    load.wait()
    pack_rows(where_ref[0], x_ref, rows_ref, -100000)
    fold(rows_ref, (o0, o1, o2))


def pieces_of(rows):
    piece = lambda n: jax.ShapeDtypeStruct((n, 2 * QUART), BF)
    return (piece(rows // 2), piece(rows // 2), piece(rows))


def pack(where, x):
    return pl.pallas_call(
        pack_kernel,
        out_shape=pieces_of(ROWS),
        in_specs=[sm(), arg()],
        out_specs=[vm()] * 3,
        scratch_shapes=[
            pltpu.VMEM((4, ROWS, QUART), BF), pltpu.VMEM((QUART, IMG_TOK), BF), pltpu.SemaphoreType.DMA,
        ],
        compiler_params=params(16),
        cost_estimate=cost(4),
        name="pack",
    )(where, in_hbm(x))


def front_kernel(
    where_ref, x_hbm, qkv_hbm, proj_hbm, fc1_hbm, fc2_hbm,
    o0, o1, o2, alpha_ref, beta_ref, alpha_half, cross_ref, fc1_half, fc2_half,
    rows_ref, x_ref, qkv_w, proj_w, sem,
):
    rows = pl.ds(pl.multiple_of(where_ref[1] * HBLK, 32), HBLK)
    loads = [
        pltpu.make_async_copy(src, dst, sem.at[i])
        for i, (src, dst) in enumerate(
            (
                (qkv_hbm, qkv_w), (proj_hbm, proj_w), (fc2_hbm.at[rows, :], fc2_half),
                (fc1_hbm.at[rows, :], fc1_half), (x_hbm, x_ref),
            )
        )
    ]
    for load in loads:
        load.start()
    for load in loads[:4]:
        load.wait()
    heads = qkv_w.shape[1] // (3 * HD)
    for h in range(heads):
        for t in range(3):
            ref, base = (alpha_ref, QUART * t) if t < 2 else (beta_ref, 0)
            ref[:, base + HD * h : base + HD * (h + 1)] = qkv_w[:, HD * (3 * h + t) : HD * (3 * h + t + 1)]
    beta_ref[:, QUART:] = proj_w[...]
    alpha_half[...] = alpha_ref[rows, :]
    cross_ref[:HBLK, :] = beta_ref[rows, :]
    cross_ref[HBLK : 2 * HBLK, :] = fc2_half[:, : 2 * QUART]
    cross_ref[2 * HBLK :, :] = fc2_half[:, 2 * QUART :]
    loads[4].wait()
    pack_rows(where_ref[0], x_ref, rows_ref, 0)
    fold(rows_ref, (o0, o1, o2))


def front(where, x, qkv_w, proj_w, fc1_w, fc2_w):
    s = lambda *shape: jax.ShapeDtypeStruct(shape, BF)
    return pl.pallas_call(
        front_kernel,
        out_shape=pieces_of(ROWS)
        + (
            s(QUART, 2 * QUART), s(QUART, 2 * QUART), s(HBLK, 2 * QUART), s(3 * HBLK, 2 * QUART),
            s(HBLK, D), s(HBLK, D),
        ),
        in_specs=[sm()] + [arg()] * 5,
        out_specs=[vm()] * 9,
        scratch_shapes=[
            pltpu.VMEM((4, ROWS, QUART), BF), pltpu.VMEM((QUART, IMG_TOK), BF),
            pltpu.VMEM(qkv_w.shape, BF), pltpu.VMEM(proj_w.shape, BF), pltpu.SemaphoreType.DMA((5,)),
        ],
        compiler_params=params(16),
        cost_estimate=cost(5),
        name="token_and_weight_pack",
    )(where, *(in_hbm(m) for m in (x, qkv_w, proj_w, fc1_w, fc2_w)))


def unpack_kernel(where_ref, *refs, bounds):
    pieces, (out_ref, acc_ref, rows_ref) = refs[:-3], refs[-3:]
    mine = where_ref[0]
    acc_ref[...] = jnp.zeros_like(acc_ref)
    index = 0
    for low, high in bounds:
        half = (high - low) // 2
        for slot in range(4):
            piece = pieces[index]
            rows = slice(half, 2 * half) if slot == 3 else slice(0, half)
            rows_ref[slot, low : low + half, :] = piece[rows, :QUART]
            rows_ref[slot, low + half : high, :] = piece[rows, QUART:]
            index += 1

    for source in range(4):
        slot = jnp.bitwise_xor(mine, source)
        for kind, offset, window in window_list(source):
            low, high, moved = window_span(window)
            pick = place_window(kind, NQ[kind], moved, high - low)
            acc_ref[:, low:high] += tn(rows_ref[slot, offset : offset + NQ[kind], :], pick)
    out_ref[...] = acc_ref[:, :IMG_TOK].astype(out_ref.dtype)


def unpack(where, pieces, dtype, bounds=((0, ROWS),)):
    return pl.pallas_call(
        functools.partial(unpack_kernel, bounds=bounds),
        out_shape=jax.ShapeDtypeStruct((QUART, IMG_TOK), dtype),
        in_specs=[sm()] + [vm()] * len(pieces),
        out_specs=vm(),
        scratch_shapes=[
            pltpu.VMEM((QUART, -(-IMG_TOK // 128) * 128), F32),
            pltpu.VMEM((4, ROWS, QUART), BF),
        ],
        compiler_params=params(24),
        cost_estimate=cost(4),
        name="unpack",
    )(where, *pieces)


def join_pieces(pieces, dst_ref):
    for slot, piece in enumerate(pieces):
        rows = slice(HALF, ROWS) if slot == 3 else slice(0, HALF)
        dst_ref[:HALF, QUART * slot : QUART * (slot + 1)] = piece[rows, :QUART]
        dst_ref[HALF:, QUART * slot : QUART * (slot + 1)] = piece[rows, QUART:]


def split_pieces(src_ref, outs):
    half = src_ref.shape[0] // 2
    for slot, (out, base) in enumerate(((outs[0], 0), (outs[1], 0), (outs[2], 0), (outs[2], half))):
        out[base : base + half, :QUART] = src_ref[:half, QUART * slot : QUART * (slot + 1)]
        out[base : base + half, QUART:] = src_ref[half:, QUART * slot : QUART * (slot + 1)]


def adapter_pack_kernel(
    pick_ref, qkv_up_hbm, proj_dn_hbm, fc1_up_hbm, fc2_dn_hbm, qkv_dn_hbm, fc1_dn_hbm, proj_up_hbm, fc2_up_hbm,
    gain1, gain2, rel_h, rel_w, s0, s1, s2, s3, row_ref, rel_ref,
    qkv_up, proj_dn, fc1_up, fc2_dn, qkv_dn, fc1_dn, proj_up, fc2_up, sem,
):
    pairs = []
    for j in range(4):
        for src, dst in ((qkv_up_hbm, qkv_up), (proj_dn_hbm, proj_dn), (fc1_up_hbm, fc1_up), (fc2_dn_hbm, fc2_dn)):
            pairs.append((src.at[pick_ref[j]], dst.at[j]))
    for src, dst in ((qkv_dn_hbm, qkv_dn), (fc1_dn_hbm, fc1_dn), (proj_up_hbm, proj_up), (fc2_up_hbm, fc2_up)):
        pairs.append((src.at[pick_ref[0]], dst.at[0]))
    loads = [pltpu.make_async_copy(src, dst, sem.at[i]) for i, (src, dst) in enumerate(pairs)]
    for load in loads:
        load.start()
    offsets = rel_h.shape[0]
    reverse = (
        lax.broadcasted_iota(jnp.int32, (offsets, 32), 0) + lax.broadcasted_iota(jnp.int32, (offsets, 32), 1)
        == offsets - 1
    ).astype(F32).astype(BF)
    rel_ref[...] = jnp.zeros_like(rel_ref)
    for i, table in enumerate((rel_h, rel_w)):
        block = tn(table[...], reverse).astype(BF)
        rel_ref[:HD, HD + 32 * i : HD + 32 * (i + 1)] = block
        rel_ref[HD:, 32 * i : 32 * (i + 1)] = block
    for load in loads:
        load.wait()
    heads = qkv_up.shape[2] // (3 * HD)
    half = 2 * QUART
    for j, send_ref in enumerate((s0, s1, s2, s3)):
        for h in range(heads):
            for t in range(3):
                row, base = (0, QUART * t) if t < 2 else (RANK, 0)
                send_ref[row : row + RANK, base + HD * h : base + HD * (h + 1)] = qkv_up[
                    j, :, HD * (3 * h + t) : HD * (3 * h + t + 1)
                ]
        send_ref[RANK : 2 * RANK, QUART:] = proj_dn[j]
        for i, ref in enumerate((fc1_up, fc2_dn)):
            for part in range(2):
                row = RANK * (2 + 2 * i + part)
                send_ref[row : row + RANK, :] = ref[j, :, half * part : half * (part + 1)]
    for i, ref in enumerate((qkv_dn, fc1_dn, proj_up, fc2_up)):
        row, base = RANK * (i // 2), QUART * (i % 2)
        row_ref[row : row + RANK, base : base + QUART] = ref[0]
    for i, ref in enumerate((gain1, gain2)):
        row_ref[2 * RANK :, QUART * i : QUART * (i + 1)] = jnp.broadcast_to(ref[...], (RANK, QUART))


def adapter_pack(pick, *mats):
    s = lambda *shape: jax.ShapeDtypeStruct(shape, BF)
    return pl.pallas_call(
        adapter_pack_kernel,
        out_shape=(s(6 * RANK, 2 * QUART),) * 4 + (s(3 * RANK, 2 * QUART), s(128, 128)),
        in_specs=[sm()] + [arg()] * 8 + [vm()] * 4,
        out_specs=[vm()] * 6,
        scratch_shapes=[pltpu.VMEM((4,) + m.shape[1:], BF) for m in mats[:4]]
        + [pltpu.VMEM((1,) + m.shape[1:], BF) for m in mats[4:8]]
        + [pltpu.SemaphoreType.DMA((20,))],
        compiler_params=params(8),
        cost_estimate=cost(2),
        name="adapter_pack",
    )(pick, *(in_hbm(m) for m in mats[:8]), *mats[8:])


def alpha_block(k, j):
    part = k
    if j == 0:
        return [(part, 0, QUART, None)]
    return [
        (part, QUART + HBLK * (j - 1), HBLK, 0),
        (part, QUART + 3 * HBLK + HBLK * (j - 1), HBLK, 1),
    ]


def beta_block(k, j):
    core, cross = k % 2, k // 2
    base = 3 * core
    if j == 0 and not cross:
        return [(base, 0, QUART, None)]
    row = 0 if j == 0 else HBLK + QUART * (j - 1) + HBLK * cross
    return [(base + 1, row, HBLK, 0), (base + 2, row, HBLK, 1)]


def block_dst(start, flag, half):
    if flag is None:
        return start
    offset = half if flag == 0 else 1 - half
    return pl.multiple_of(start + offset * HBLK, 32)


def prep1_kernel(
    where_ref, p0, p1, p2, p3, q0, q1, q2, q3, q4, q5, a0, a1, a2, a3,
    wqkv_ref, wproj_ref, dqkv, uqkv, dproj, uproj, d1, u1, d2, u2, gain1, gain2, ups, downs,
):
    half = where_ref[1]
    for j, a in enumerate((a0, a1, a2, a3)):
        base = a.shape[0] - 6 * RANK
        part = lambda i: slice(base + RANK * i, base + RANK * (i + 1))
        for t in range(3):
            uqkv[:, D * t + QUART * j : D * t + QUART * (j + 1)] = a[
                part(t // 2), QUART * (t % 2) : QUART * (t % 2 + 1)
            ]
        dproj[:, QUART * j : QUART * (j + 1)] = a[part(1), QUART:]
        for i in range(2):
            u1[:, D * j + D // 2 * i : D * j + D // 2 * (i + 1)] = a[part(2 + i), :]
            d2[:, D * j + D // 2 * i : D * j + D // 2 * (i + 1)] = a[part(4 + i), :]
    for k, ref in enumerate((p0, p1, p2, p3)):
        for i, dst in enumerate((dqkv, d1, uproj, u2)):
            rows = slice(D + RANK * (i // 2), D + RANK * (i // 2 + 1))
            dst[:, QUART * k : QUART * (k + 1)] = ref[rows, QUART * (i % 2) : QUART * (i % 2 + 1)]
        for i, dst in enumerate((gain1, gain2)):
            row = D + 2 * RANK
            dst[:, QUART * k : QUART * (k + 1)] = ref[row : row + 1, QUART * i : QUART * (i + 1)].astype(F32)
    alpha, beta = (p0, p1, p2, p3), (q0, q1, q2, q3, q4, q5)
    for k in range(4):
        for j in range(4):
            for part, row, count, flag in alpha_block(k, j):
                rows = pl.ds(block_dst(QUART * k, flag, half), count)
                for t in range(2):
                    wqkv_ref[rows, D * t + QUART * j : D * t + QUART * (j + 1)] = alpha[part][
                        row : row + count, QUART * t : QUART * (t + 1)
                    ]
            for part, row, count, flag in beta_block(k, j):
                rows = pl.ds(block_dst(QUART * k, flag, half), count)
                wqkv_ref[rows, 2 * D + QUART * j : 2 * D + QUART * (j + 1)] = beta[part][
                    row : row + count, :QUART
                ]
                rows = pl.ds(block_dst(QUART * j, flag, half), count)
                wproj_ref[rows, QUART * k : QUART * (k + 1)] = beta[part][row : row + count, QUART:]
    for t in range(3):
        ups[t] = uqkv[:, D * t : D * (t + 1)]
    ups[3] = uproj[...]
    for k in range(4):
        downs[k] = dqkv[:, QUART * k : QUART * (k + 1)]
        downs[4 + k] = dproj[:, QUART * k : QUART * (k + 1)]

    def merge(t, carry):
        cols = pl.ds(pl.multiple_of(D * t, 128), D)
        for k in range(4):
            rows = slice(QUART * k, QUART * (k + 1))
            wqkv_ref[rows, cols] = (wqkv_ref[rows, cols].astype(F32) + tn(downs[k], ups[t])).astype(BF)
        return carry

    lax.fori_loop(0, 3, merge, 0)
    for k in range(4):
        rows = slice(QUART * k, QUART * (k + 1))
        wproj_ref[rows, :] = (wproj_ref[rows, :].astype(F32) + tn(downs[4 + k], ups[3])).astype(BF)


def prep1(where, alpha, beta, cols):
    s = lambda *shape: jax.ShapeDtypeStruct(shape, BF)
    return pl.pallas_call(
        prep1_kernel,
        out_shape=(
            s(D, 3 * D), s(D, D), s(RANK, D), s(RANK, 3 * D), s(RANK, D), s(RANK, D),
            s(RANK, D), s(RANK, 4 * D), s(RANK, 4 * D), s(RANK, D),
            jax.ShapeDtypeStruct((1, D), F32), jax.ShapeDtypeStruct((1, D), F32),
        ),
        in_specs=[sm()] + [vm()] * 14,
        out_specs=[vm()] * 12,
        scratch_shapes=[pltpu.VMEM((4, RANK, D), BF), pltpu.VMEM((8, RANK, QUART), BF)],
        compiler_params=params(24),
        cost_estimate=cost(7),
        name="attention_weights",
    )(where, *alpha, *beta, *cols)


def normalize(values):
    center = jnp.sum(values, axis=1, keepdims=True) / D
    shifted = values - center
    inv_std = lax.rsqrt(jnp.sum(shifted * shifted, axis=1, keepdims=True) / D + EPSILON)
    return shifted * inv_std, inv_std


def norm_back(grad, normed, inv_std):
    first = jnp.sum(grad, axis=1, keepdims=True) / D
    second = jnp.sum(grad * normed, axis=1, keepdims=True) / D
    return inv_std * (grad - first - normed * second)


def barrel(values, amount, left):
    for bit in (1, 2, 4, 8):
        moved = pltpu.roll(values, (128 - bit) if left else bit, 1)
        values = jnp.where((amount & bit) != 0, moved, values)
    return values


def low_half(count):
    return lax.broadcasted_iota(jnp.int32, (count, 128), 1) < HD


def pad_rows(tile):
    if tile.shape[0] == KEYS:
        return tile
    return jnp.concatenate([tile, jnp.zeros((KEYS - tile.shape[0], tile.shape[1]), tile.dtype)], axis=0)


def live_rows():
    return lax.broadcasted_iota(jnp.int32, (KEYS, 128), 0) < SLOTS


GROUP = 6
GROUP_BACK = 6


def pair_columns(pair):
    return tuple(slice(D * t + 128 * pair, D * t + 128 * (pair + 1)) for t in range(3))


def attend_window(kind, row0, qkv_ref, att_ref, exp_ref, inv_ref, rel_ref, shift_ref, keys_ref):
    count = NQ[kind]
    rows = pl.ds(row0, count)
    low_q, low_k = low_half(count), low_half(KEYS)
    live = live_rows()
    ones = jnp.where(live, 1.0, 0.0).astype(BF)
    amount = shift_ref[kind, :count, :]
    onehot = keys_ref[kind]
    rel_mat = rel_ref[...]
    for first in range(0, D // 128, GROUP):
        pairs = range(first, first + GROUP)
        heads = [(pair, odd) for pair in pairs for odd in range(2)]
        q_tile = {p: qkv_ref[rows, pair_columns(p)[0]] for p in pairs}
        rel = {p: nn(q_tile[p], rel_mat) for p in pairs}
        rel = {p: barrel(rel[p], amount, True).astype(BF) for p in pairs}
        k_tile = {p: pad_rows(qkv_ref[rows, pair_columns(p)[1]] * BF(HD**-0.5)) for p in pairs}
        scores = {}
        for p, odd in heads:
            if odd:
                q_aug, k_aug = jnp.where(low_q, rel[p], q_tile[p]), jnp.where(low_k, onehot, k_tile[p])
            else:
                q_aug, k_aug = jnp.where(low_q, q_tile[p], rel[p]), jnp.where(low_k, k_tile[p], onehot)
            scores[p, odd] = nt(q_aug, k_aug)
        top = {h: jnp.max(scores[h], axis=1, keepdims=True) for h in heads}
        exponent = {h: jnp.exp(scores[h] - top[h]).astype(BF) for h in heads}
        both = {}
        for p, odd in heads:
            exp_ref[2 * p + odd, rows, :] = exponent[p, odd]
            v_tile = pad_rows(qkv_ref[rows, pair_columns(p)[2]])
            if kind == FULL:
                v_tile = jnp.where(live, v_tile, 0).astype(BF)
            v_aug = jnp.where(low_k, ones, v_tile) if odd else jnp.where(low_k, v_tile, ones)
            both[p, odd] = nn(exponent[p, odd], v_aug)
        for p in pairs:
            cols = pair_columns(p)[0]
            inverse = 1.0 / pltpu.roll(jnp.where(low_q, both[p, 1], both[p, 0]), HD, 1)
            inv_ref[rows, cols] = inverse
            att_ref[rows, cols] = (jnp.where(low_q, both[p, 0], both[p, 1]) * inverse).astype(BF)


PARTS = ((FULL, FULL), (FULL, FULL), (RIGHT, BOTTOM, CORNER))
PART_ROWS = tuple(sum(NQ[kind] for kind in part) for part in PARTS)
PART_OFFS = (0, PART_ROWS[0], PART_ROWS[0] + PART_ROWS[1])


TAIL = ((0, 576), (576, ROWS))


def qkv_kernel(
    x0, x1, x2, x3, gain_ref, w_hbm, x_hbm, hid_hbm, qkv_a, qkv_b, qkv_c,
    x_ref, hid_ref, rows_ref, w_ref, qkv_ref, sem, out_sem,
):
    loads = [
        pltpu.make_async_copy(w_hbm.at[:, D * t : D * (t + 1)], w_ref.at[t], sem.at[t]) for t in range(3)
    ]
    for load in loads:
        load.start()
    join_pieces((x0, x1, x2, x3), x_ref)
    kept = [
        pltpu.make_async_copy(src, dst, sem.at[3 + i])
        for i, (src, dst) in enumerate(((x_ref, x_hbm), (hid_ref, hid_hbm)))
    ]
    kept[0].start()
    gain = gain_ref[...]

    def norm_step(i, carry):
        rows = pl.ds(pl.multiple_of(i * 112, 16), 112)
        normed, _ = normalize(x_ref[rows, :].astype(F32))
        hidden = (normed * gain).astype(BF)
        rows_ref[rows, :] = hidden
        hid_ref[rows, :] = hidden
        return carry

    lax.fori_loop(0, ROWS // 112, norm_step, 0)
    for w in range(4):
        hid_ref[FULLR * w + SLOTS : FULLR * (w + 1), :] = jnp.zeros((FULLR - SLOTS, D), BF)
    kept[1].start()
    for load in loads:
        load.wait()

    def stores(t):
        cols = pl.ds(pl.multiple_of(D * t, 128), D)
        return [
            pltpu.make_async_copy(
                qkv_ref.at[t, pl.ds(offset, count), :], out.at[:, cols], out_sem.at[t, i]
            )
            for i, (out, offset, count) in enumerate(zip((qkv_a, qkv_b, qkv_c), PART_OFFS, PART_ROWS))
        ]

    def project_step(t, carry):
        qkv_ref[t] = nn(rows_ref[...], w_ref[t]).astype(BF)
        for store in stores(t):
            store.start()
        return carry

    lax.fori_loop(0, 3, project_step, 0)
    for t in range(3):
        for store in stores(t):
            store.wait()
    for store in kept:
        store.wait()


def qkv_rows(pieces, gain, wqkv):
    s = lambda *shape: jax.ShapeDtypeStruct(shape, BF)
    return pl.pallas_call(
        qkv_kernel,
        out_shape=(s(ROWS, D), s(ROWS, D)) + tuple(s(n, 3 * D) for n in PART_ROWS),
        in_specs=[vm()] * 5 + [hbm()],
        out_specs=[hbm()] * 5,
        scratch_shapes=[
            pltpu.VMEM((ROWS, D), BF), pltpu.VMEM((ROWS, D), BF), pltpu.VMEM((ROWS, D), BF),
            pltpu.VMEM((3, D, D), BF), pltpu.VMEM((3, ROWS, D), BF),
            pltpu.SemaphoreType.DMA((5,)), pltpu.SemaphoreType.DMA((3, 3)),
        ],
        compiler_params=params(32),
        cost_estimate=cost(10),
        name="norm_and_qkv",
    )(*pieces, gain, wqkv)


def attention_kernel(qkv_ref, rel_ref, shift_ref, keys_ref, att_ref, exp_ref, inv_ref, *, kinds):
    refs = (qkv_ref, att_ref, exp_ref, inv_ref, rel_ref, shift_ref, keys_ref)
    if kinds[0] == FULL:

        def step(w, carry):
            attend_window(FULL, pl.multiple_of(w * FULLR, 16), *refs)
            return carry

        lax.fori_loop(0, len(kinds), step, 0)
    else:
        row = 0
        for kind in kinds:
            attend_window(kind, row, *refs)
            row += NQ[kind]


def attention(part, qkv, rel, shift, keys):
    rows = PART_ROWS[part]
    s = lambda *shape, dtype=BF: jax.ShapeDtypeStruct(shape, dtype)
    return pl.pallas_call(
        functools.partial(attention_kernel, kinds=PARTS[part]),
        out_shape=(s(rows, D), s(D // HD, rows, KEYS), s(rows, D, dtype=F32)),
        in_specs=[vm()] * 4,
        out_specs=[vm()] * 3,
        compiler_params=params(24),
        cost_estimate=cost(10),
        name="attention_forward",
    )(qkv, rel, shift, keys)


def project_kernel(x_ref, att_a, att_b, att_c, wproj_ref, middle_ref):
    for ref, offset, count in zip((att_a, att_b, att_c), PART_OFFS, PART_ROWS):
        rows = slice(offset, offset + count)
        middle_ref[rows, :] = x_ref[rows, :].astype(F32) + nn(ref[...], wproj_ref[...])


def project(x, atts, wproj):
    return pl.pallas_call(
        project_kernel,
        out_shape=jax.ShapeDtypeStruct((ROWS, D), F32),
        in_specs=[vm()] * 5,
        out_specs=vm(),
        compiler_params=params(20),
        cost_estimate=cost(5),
        name="projection",
    )(x, *atts, wproj)


CHUNK = 512
LOCK = 1


def mlp_kernel(
    where_ref, middle_ref, g0, g1, g2, g3, gain_ref,
    p0, p1, p2, p3, q0, q1, q2, q3, q4, q5, d1, u1, d2, u2,
    o0, o1, o2, gmid_ref, down1, up1, down2, up2,
    gm_ref, out_rows, h2_ref, acc_mlp, acc_gh, gu1, ad2, w1_ref, w2_ref, downs, sem,
):
    half = where_ref[1]
    copies = []

    def fetch(src, dst):
        copies.append(pltpu.make_async_copy(src, dst, sem.at[len(copies)]))
        copies[-1].start()

    alpha, beta = (p0, p1, p2, p3), (q0, q1, q2, q3, q4, q5)
    for k in range(4):
        for j in range(4):
            for part, row, count, flag in alpha_block(k, j):
                rows = pl.ds(block_dst(QUART * k, flag, half), count)
                fetch(alpha[part].at[row : row + count, :], w1_ref.at[rows, D * j : D * (j + 1)])
            for part, row, count, flag in beta_block(k, j):
                rows = pl.ds(block_dst(QUART * k, flag, half), count)
                fetch(beta[part].at[row : row + count, :], w2_ref.at[rows, D * j : D * (j + 1)])
    join_pieces((g0, g1, g2, g3), gm_ref)
    for k in range(4):
        downs[k] = d1[:, QUART * k : QUART * (k + 1)]
        downs[4 + k] = u2[:, QUART * k : QUART * (k + 1)]
    for copy in copies:
        copy.wait()

    def merge(j, carry):
        cols = pl.ds(pl.multiple_of(D * j, 128), D)
        for k in range(4):
            rows = slice(QUART * k, QUART * (k + 1))
            w1_ref[rows, cols] = (w1_ref[rows, cols].astype(F32) + tn(downs[k], u1[:, cols])).astype(BF)
            w2_ref[rows, cols] = (w2_ref[rows, cols].astype(F32) + tn(downs[4 + k], d2[:, cols])).astype(BF)
        return carry

    lax.fori_loop(0, 4, merge, 0)
    gain = gain_ref[...]
    down1[...] = jnp.zeros_like(down1)
    up1[...] = jnp.zeros_like(up1)
    down2[...] = jnp.zeros_like(down2)
    up2[...] = jnp.zeros_like(up2)

    def tile_step(t, carry):
        rows = pl.ds(pl.multiple_of(t * HALF, 16), HALF)
        normed, _ = normalize(middle_ref[rows, :])
        h2 = (normed * gain).astype(BF)
        h2_ref[...] = h2
        gm = gm_ref[rows, :]
        ad1 = nt(d1[...], h2).astype(BF)
        gu2 = nt(u2[...], gm).astype(BF)
        acc_mlp[...] = jnp.zeros_like(acc_mlp)
        acc_gh[...] = jnp.zeros_like(acc_gh)
        gu1[...] = jnp.zeros_like(gu1)
        ad2[...] = jnp.zeros_like(ad2)

        def chunk_step(c, inner_carry):
            spans = [
                pl.ds(pl.multiple_of((c * LOCK + i) * CHUNK, CHUNK), CHUNK) for i in range(LOCK)
            ]
            h2 = h2_ref[...]
            gm = gm_ref[rows, :]
            inner = [nn(h2, w1_ref[:, span]) for span in spans]
            gact = [nn(gm, w2_ref[:, span]) for span in spans]
            act, ginner = [], []
            for i in range(LOCK):
                half = 0.5 * (1.0 + lax.erf(inner[i] * 2**-0.5))
                act.append((inner[i] * half).astype(BF))
                slope = half + inner[i] * (jnp.exp(-0.5 * inner[i] * inner[i]) * (2 * np.pi) ** -0.5)
                ginner.append((gact[i] * slope).astype(BF))
            for i, span in enumerate(spans):
                acc_mlp[...] += nt(act[i], w2_ref[:, span])
                acc_gh[...] += nt(ginner[i], w1_ref[:, span])
                up1[:, span] += nn(ad1, ginner[i])
                gu1[...] += nt(u1[:, span], ginner[i])
                ad2[...] += nt(d2[:, span], act[i])
                down2[:, span] += nn(gu2, act[i])
            return inner_carry

        lax.fori_loop(0, 4 * D // (CHUNK * LOCK), chunk_step, 0)
        down1[...] += nn(gu1[...].astype(BF), h2_ref[...])
        up2[...] += nn(ad2[...].astype(BF), gm_ref[rows, :])
        middle = middle_ref[rows, :]
        out_rows[rows, :] = (middle + acc_mlp[...]).astype(BF)
        normed, inv_std = normalize(middle)
        gmid_ref[rows, :] = gm_ref[rows, :].astype(F32) + norm_back(acc_gh[...] * gain, normed, inv_std)
        return carry

    lax.fori_loop(0, 2, tile_step, 0)
    split_pieces(out_rows, (o0, o1, o2))


def mlp(where, middle, pieces, gain, alpha, beta, d1, u1, d2, u2):
    s = lambda *shape, dtype=F32: jax.ShapeDtypeStruct(shape, dtype)
    return pl.pallas_call(
        mlp_kernel,
        out_shape=pieces_of(ROWS)
        + (s(ROWS, D), s(RANK, D), s(RANK, 4 * D), s(RANK, 4 * D), s(RANK, D)),
        in_specs=[sm()] + [vm()] * 6 + [pl.BlockSpec(memory_space=pl.ANY)] * 10 + [vm()] * 4,
        out_specs=[vm()] * 8,
        scratch_shapes=[
            pltpu.VMEM((ROWS, D), BF), pltpu.VMEM((ROWS, D), BF), pltpu.VMEM((HALF, D), BF),
            pltpu.VMEM((HALF, D), F32), pltpu.VMEM((HALF, D), F32),
            pltpu.VMEM((RANK, HALF), F32), pltpu.VMEM((RANK, HALF), F32),
            pltpu.VMEM((D, 4 * D), BF), pltpu.VMEM((D, 4 * D), BF), pltpu.VMEM((8, RANK, QUART), BF),
            pltpu.SemaphoreType.DMA((4 * 4 * 4,)),
        ],
        compiler_params=params(48),
        cost_estimate=cost(48),
        name="mlp_forward_backward",
    )(where, middle, *pieces, gain, *alpha, *beta, d1, u1, d2, u2)


def attend_back_window(
    kind, row0, qkv_ref, att_ref, exp_ref, inv_ref, gatt_ref, gqkv_ref, rel_ref, shift_ref, keys_ref
):
    count = NQ[kind]
    rows = pl.ds(row0, count)
    low_q, low_k = low_half(count), low_half(KEYS)
    live = live_rows()
    lane_k = lax.broadcasted_iota(jnp.int32, (KEYS, 128), 1) % HD
    lane_q = lax.broadcasted_iota(jnp.int32, (count, 128), 1) % HD
    ones = jnp.where(live & (lane_k < 2), 1.0, 0.0).astype(BF)
    across = jnp.where(
        low_half(128) != (lax.broadcasted_iota(jnp.int32, (128, 128), 0) < HD), -1.0, 0.0
    ).astype(BF)
    amount = shift_ref[kind, :count, :]
    onehot = keys_ref[kind]
    rel_mat = rel_ref[...]
    for first in range(0, D // 128, GROUP_BACK):
        pairs = range(first, first + GROUP_BACK)
        heads = [(pair, odd) for pair in pairs for odd in range(2)]
        go_tile = {
            p: (gatt_ref[rows, pair_columns(p)[0]].astype(F32) * inv_ref[rows, pair_columns(p)[0]]).astype(BF)
            for p in pairs
        }
        delta = {
            p: nn((go_tile[p].astype(F32) * att_ref[rows, pair_columns(p)[0]].astype(F32)).astype(BF), across)
            for p in pairs
        }
        go_t = {p: go_tile[p].T for p in pairs}
        gv = {}
        for p, odd in heads:
            gv[p, odd] = nn(go_t[p][HD * odd : HD * (odd + 1), :], exp_ref[2 * p + odd, rows, :])
        gscore = {}
        for p in pairs:
            high = delta[p].astype(BF)
            rest = (delta[p] - high.astype(F32)).astype(BF)
            low_delta = jnp.where(lane_q == 0, high, jnp.where(lane_q == 1, rest, 0)).astype(BF)
            v_tile = pad_rows(qkv_ref[rows, pair_columns(p)[2]])
            if kind == FULL:
                v_tile = jnp.where(live, v_tile, 0).astype(BF)
            gscore[p, 0] = nt(jnp.where(low_q, go_tile[p], low_delta), jnp.where(low_k, v_tile, ones))
            gscore[p, 1] = nt(jnp.where(low_q, low_delta, go_tile[p]), jnp.where(low_k, ones, v_tile))
        q_t = {p: qkv_ref[rows, pair_columns(p)[0]].T for p in pairs}
        gs = {(p, odd): (exp_ref[2 * p + odd, rows, :].astype(F32) * gscore[p, odd]).astype(BF) for p, odd in heads}
        gk = {(p, odd): nn(q_t[p][HD * odd : HD * (odd + 1), :], gs[p, odd]) for p, odd in heads}
        gq = {}
        for p in pairs:
            k_tile = pad_rows(qkv_ref[rows, pair_columns(p)[1]] * BF(HD**-0.5))
            gq[p, 0] = nn(gs[p, 0], jnp.where(low_k, k_tile, onehot))
            gq[p, 1] = nn(gs[p, 1], jnp.where(low_k, onehot, k_tile))
        sums = {p: barrel(jnp.where(low_q, gq[p, 1], gq[p, 0]), amount, False).astype(BF) for p in pairs}
        for p in pairs:
            cols, kcols, vcols = pair_columns(p)
            gv_tile = jnp.concatenate([gv[p, 0], gv[p, 1]], axis=0).astype(BF).T
            gqkv_ref[rows, vcols] = gv_tile[:count, :]
            gk_tile = (jnp.concatenate([gk[p, 0], gk[p, 1]], axis=0) * HD**-0.5).astype(BF).T
            gqkv_ref[rows, kcols] = gk_tile[:count, :]
            gqkv_ref[rows, cols] = (jnp.where(low_q, gq[p, 0], gq[p, 1]) + nt(sums[p], rel_mat)).astype(BF)


def attention_back_kernel(
    gmid_hbm, hid_hbm, qkv_a, qkv_b, qkv_c, att_a, att_b, att_c, exp_a, exp_b, exp_c, inv_a, inv_b, inv_c,
    wproj_ref, rel_ref, shift_ref, keys_ref, dqkv, uqkv, dproj, uproj,
    gqkv_hbm, down_q, up_q, down_p, up_p,
    gmid_ref, hid_ref, qkv_ref, att_ref, exp_ref, inv_ref, gqkv_ref, gb_ref, gatt_ref, sem, out_sem,
):
    spans = [pl.ds(offset, count) for offset, count in zip(PART_OFFS, PART_ROWS)]
    pairs = [(gmid_hbm, gmid_ref)]
    for part, srcs in enumerate(
        ((qkv_a, inv_a, att_a, exp_a), (qkv_b, inv_b, att_b, exp_b), (qkv_c, inv_c, att_c, exp_c))
    ):
        rows = spans[part]
        for src, dst in zip(srcs, (qkv_ref, inv_ref, att_ref)):
            pairs.append((src, dst.at[rows, :]))
        pairs.append((srcs[3], exp_ref.at[:, rows, :]))
    pairs.append((hid_hbm, hid_ref))
    loads = [pltpu.make_async_copy(src, dst, sem.at[i]) for i, (src, dst) in enumerate(pairs)]
    for load in loads:
        load.start()

    def wait_part(part):
        for load in loads[1 + 4 * part : 5 + 4 * part]:
            load.wait()

    stores = [
        pltpu.make_async_copy(gqkv_ref.at[rows, :], gqkv_hbm.at[rows, :], out_sem.at[i])
        for i, rows in enumerate(spans)
    ]
    loads[0].wait()
    gb_ref[...] = gmid_ref[...].astype(BF)
    gatt_ref[...] = nt(gb_ref[...], wproj_ref[...]).astype(BF)
    refs = (qkv_ref, att_ref, exp_ref, inv_ref, gatt_ref, gqkv_ref, rel_ref, shift_ref, keys_ref)

    def step(w, carry):
        for part in range(2):

            @pl.when(w == 2 * part)
            def _():
                wait_part(part)

        attend_back_window(FULL, pl.multiple_of(w * FULLR, 16), *refs)
        return carry

    lax.fori_loop(0, 4, step, 0)
    stores[0].start()
    stores[1].start()
    wait_part(2)
    for kind in (RIGHT, BOTTOM, CORNER):
        attend_back_window(kind, OFFS[kind], *refs)
    stores[2].start()
    up_p[...] = nn(nt(dproj[...], att_ref[...]).astype(BF), gb_ref[...])
    down_p[...] = nn(nt(uproj[...], gb_ref[...]).astype(BF), att_ref[...])
    loads[-1].wait()
    up_q[...] = nn(nt(dqkv[...], hid_ref[...]).astype(BF), gqkv_ref[...])
    down_q[...] = nn(nt(uqkv[...], gqkv_ref[...]).astype(BF), hid_ref[...])
    for store in stores:
        store.wait()


def attention_back(gmid, hid, qkvs, atts, exps, invs, wproj, rel, shift, keys, dqkv, uqkv, dproj, uproj):
    s = lambda *shape, dtype=F32: jax.ShapeDtypeStruct(shape, dtype)
    return pl.pallas_call(
        attention_back_kernel,
        out_shape=(s(ROWS, 3 * D, dtype=BF), s(RANK, D), s(RANK, 3 * D), s(RANK, D), s(RANK, D)),
        in_specs=[hbm()] * 14 + [vm()] * 8,
        out_specs=[hbm()] + [vm()] * 4,
        scratch_shapes=[
            pltpu.VMEM((ROWS, D), F32), pltpu.VMEM((ROWS, D), BF), pltpu.VMEM((ROWS, 3 * D), BF),
            pltpu.VMEM((ROWS, D), BF), pltpu.VMEM((D // HD, ROWS, KEYS), BF), pltpu.VMEM((ROWS, D), F32),
            pltpu.VMEM((ROWS, 3 * D), BF), pltpu.VMEM((ROWS, D), BF), pltpu.VMEM((ROWS, D), BF),
            pltpu.SemaphoreType.DMA((14,)), pltpu.SemaphoreType.DMA((3,)),
        ],
        compiler_params=params(52),
        cost_estimate=cost(28),
        name="attention_backward",
    )(gmid, hid, *qkvs, *atts, *exps, *invs, wproj, rel, shift, keys, dqkv, uqkv, dproj, uproj)


def token_grad_kernel(gmid_hbm, x_hbm, gqkv_hbm, gain_ref, wqkv_ref, o0, o1, o2,
                      gmid_ref, x_ref, gqkv_ref, gh_ref, out_rows, sem, *, low, high):
    span = pl.ds(low, high - low)
    copies = [
        pltpu.make_async_copy(src.at[span, :], dst, sem.at[i])
        for i, (src, dst) in enumerate(((gqkv_hbm, gqkv_ref), (x_hbm, x_ref), (gmid_hbm, gmid_ref)))
    ]
    for copy in copies:
        copy.start()
    copies[0].wait()
    gh_ref[...] = nt(gqkv_ref[...], wqkv_ref[...])
    copies[1].wait()
    copies[2].wait()
    gain = gain_ref[...]
    step = (high - low) // 2

    def norm_step(i, carry):
        rows = pl.ds(pl.multiple_of(i * step, 16), step)
        normed, inv_std = normalize(x_ref[rows, :].astype(F32))
        back = norm_back(gh_ref[rows, :] * gain, normed, inv_std)
        out_rows[rows, :] = (gmid_ref[rows, :] + back).astype(BF)
        return carry

    lax.fori_loop(0, 2, norm_step, 0)
    split_pieces(out_rows, (o0, o1, o2))


def token_grad(gmid, x, gqkv, gain, wqkv, low, high):
    count = high - low
    return pl.pallas_call(
        functools.partial(token_grad_kernel, low=low, high=high),
        out_shape=pieces_of(count),
        in_specs=[hbm(), hbm(), arg(), vm(), vm()],
        out_specs=[vm()] * 3,
        scratch_shapes=[
            pltpu.VMEM((count, D), F32), pltpu.VMEM((count, D), BF), pltpu.VMEM((count, 3 * D), BF),
            pltpu.VMEM((count, D), F32), pltpu.VMEM((count, D), BF), pltpu.SemaphoreType.DMA((3,)),
        ],
        compiler_params=params(28),
        cost_estimate=cost(8),
        name="token_gradient",
    )(gmid, x, in_hbm(gqkv), gain, wqkv)


def grad_pack_kernel(where_ref, down_q, up_q, down_p, up_p, down1, up1, down2, up2, o0, o1, o2, o3, buf_ref):
    mine = where_ref[0]
    for k in range(4):
        for i, ref in enumerate((down_q, down1, up_p, up2)):
            buf_ref[k, :RANK, QUART * i : QUART * (i + 1)] = ref[:, QUART * k : QUART * (k + 1)]
    for dest in range(4):
        k = jnp.bitwise_xor(mine, dest)
        ranks = slice(RANK // 4 * dest, RANK // 4 * (dest + 1))
        for j in range(4):
            base = RANK + 12 * j
            for t in range(3):
                buf_ref[k, base : base + 4, QUART * t : QUART * (t + 1)] = up_q[
                    ranks, D * t + QUART * j : D * t + QUART * (j + 1)
                ]
            buf_ref[k, base : base + 4, 3 * QUART :] = down_p[ranks, QUART * j : QUART * (j + 1)]
            buf_ref[k, base + 4 : base + 8, :] = up1[ranks, D * j : D * (j + 1)]
            buf_ref[k, base + 8 : base + 12, :] = down2[ranks, D * j : D * (j + 1)]
    for k, out in enumerate((o0, o1, o2, o3)):
        out[...] = buf_ref[k].astype(BF)


def grad_pack(where, *grads):
    return pl.pallas_call(
        grad_pack_kernel,
        out_shape=(jax.ShapeDtypeStruct((4 * RANK, D), BF),) * 4,
        in_specs=[sm()] + [vm()] * 8,
        out_specs=[vm()] * 4,
        scratch_shapes=[pltpu.VMEM((4, 4 * RANK, D), F32)],
        compiler_params=params(8),
        cost_estimate=cost(2),
        name="adapter_grad_pack",
    )(where, *grads)


def grad_sum_kernel(g0, g1, g2, g3, o0, o1, o2, o3, buf_ref):
    total = g0[...].astype(F32) + g1[...].astype(F32) + g2[...].astype(F32) + g3[...].astype(F32)
    buf_ref[...] = jnp.zeros_like(buf_ref)
    buf_ref[:RANK, :] = total[:RANK, :]
    for j, out in enumerate((o0, o1, o2, o3)):
        buf_ref[RANK : RANK + 12, :] = total[RANK + 12 * j : RANK + 12 * (j + 1), :]
        out[...] = buf_ref[...].astype(BF)


def grad_sum(pieces):
    return pl.pallas_call(
        grad_sum_kernel,
        out_shape=(jax.ShapeDtypeStruct((2 * RANK, D), BF),) * 4,
        in_specs=[vm()] * 4,
        out_specs=[vm()] * 4,
        scratch_shapes=[pltpu.VMEM((2 * RANK, D), F32)],
        compiler_params=params(4),
        cost_estimate=cost(2),
        name="adapter_grad_sum",
    )(*pieces)


def grad_adapters_kernel(index_ref, x_ref, qkv_dn, fc1_dn, proj_up, fc2_up, rest_ref, acc_ref):
    acc_ref[...] = jnp.zeros_like(acc_ref)

    def add(i, carry):
        acc_ref[index_ref[i]] += x_ref[i].astype(F32)
        return carry

    lax.fori_loop(0, x_ref.shape[0], add, 0)
    for i, ref in enumerate((qkv_dn, fc1_dn, proj_up, fc2_up)):
        ref[...] = acc_ref[:, :RANK, QUART * i : QUART * (i + 1)]
    rest_ref[...] = acc_ref[:, RANK:, :].astype(BF)


def grad_adapters(index, x):
    s = lambda n, dtype=F32: jax.ShapeDtypeStruct((ADAPT, RANK, n), dtype)
    return pl.pallas_call(
        grad_adapters_kernel,
        out_shape=(s(QUART), s(QUART), s(QUART), s(QUART), s(D, BF)),
        in_specs=[sm(), vm()],
        out_specs=[vm()] * 5,
        scratch_shapes=[pltpu.VMEM((ADAPT, 2 * RANK, D), F32)],
        compiler_params=params(8),
        cost_estimate=cost(2),
        name="adapter_grad_by_adapter",
    )(index, x)


def grad_join_kernel(where_ref, r0, r1, r2, r3, qkv_up, proj_dn, fc1_up, fc2_dn, buf_ref):
    mine = where_ref[0]
    heads = qkv_up.shape[2] // (3 * HD)
    for k, ref in enumerate((r0, r1, r2, r3)):
        buf_ref[jnp.bitwise_xor(mine, k)] = ref[...].astype(F32)
    for source in range(4):
        ranks = slice(RANK // 4 * source, RANK // 4 * (source + 1))
        for h in range(heads):
            for t in range(3):
                qkv_up[:, ranks, HD * (3 * h + t) : HD * (3 * h + t + 1)] = buf_ref[
                    source, :, 0:4, QUART * t + HD * h : QUART * t + HD * (h + 1)
                ]
        proj_dn[:, ranks, :] = buf_ref[source, :, 0:4, 3 * QUART :]
        fc1_up[:, ranks, :] = buf_ref[source, :, 4:8, :]
        fc2_dn[:, ranks, :] = buf_ref[source, :, 8:12, :]


def grad_join(where, pieces):
    s = lambda n: jax.ShapeDtypeStruct((ADAPT, RANK, n), F32)
    return pl.pallas_call(
        grad_join_kernel,
        out_shape=(s(3 * QUART), s(QUART), s(D), s(D)),
        in_specs=[sm()] + [vm()] * 4,
        out_specs=[vm()] * 4,
        scratch_shapes=[pltpu.VMEM((4, ADAPT, RANK, D), F32)],
        compiler_params=params(12),
        cost_estimate=cost(2),
        name="adapter_grad_join",
    )(where, *pieces)


def flip(values, axis, distance):
    size = lax.axis_size(axis)
    return lax.ppermute(values, axis, [(i, i ^ distance) for i in range(size)])


def send_rows(pieces, *deps):
    own, near, pair = pieces
    if deps:
        near, = after((near,), *deps)
    return [own, flip(near, "row", 1), flip(pair, "row", 2)]


def hand_on(pieces, *deps):
    own, near, crossed = pieces
    if deps:
        near, crossed = after((near, crossed), *deps)
    return [own, near, crossed, flip(crossed, "row", 1)]


def exchange(slots, axis):
    return [slots[0]] + [flip(slots[k], axis, k) for k in range(1, 4)]


def after(values, *deps):
    return lax.optimization_barrier((tuple(values), deps))[0]


def col_halves(half):
    return jnp.concatenate([flip(half, "col", j) for j in range(1, 4)], axis=0)


def col_pairs(half, other_row):
    two = jnp.concatenate([half, other_row], axis=0)
    return jnp.concatenate([other_row] + [flip(two, "col", j) for j in range(1, 4)], axis=0)


def body(
    tokens, grad_out, adapter_index, norm1_gain, norm2_gain, qkv_weight, proj_weight, fc1_weight, fc2_weight,
    rel_h, rel_w, qkv_down, qkv_up, proj_down, proj_up, fc1_down, fc1_up, fc2_down, fc2_up,
):
    members = lax.axis_size("col")
    batches = lax.axis_size("dp")
    row_index, col_index, dp_index = lax.axis_index("row"), lax.axis_index("col"), lax.axis_index("dp")
    half = dp_index % 2
    where = jnp.stack([row_index, half]).astype(jnp.int32)
    slot_images = (
        jnp.bitwise_xor(dp_index, jnp.arange(batches, dtype=jnp.int32))[:, None] * members
        + jnp.bitwise_xor(col_index, jnp.arange(members, dtype=jnp.int32))[None, :]
    ).reshape(-1)
    slot_adapters = jnp.sum(
        jnp.where(
            slot_images[:, None] == jnp.arange(adapter_index.shape[0], dtype=jnp.int32)[None, :],
            adapter_index[:, 0][None, :],
            0,
        ),
        axis=1,
    )
    pick = jnp.concatenate([slot_adapters[:4], half[None]]).astype(jnp.int32)
    swap = lambda m: jnp.swapaxes(m, 1, 2)

    shift, keys = jnp.asarray(SHIFT_NP), jnp.asarray(KEYS_NP)

    *token_slots, alpha_own, beta_own, alpha_half, cross, fc1_half, fc2_half = front(
        where, tokens, qkv_weight, proj_weight, fc1_weight, fc2_weight
    )
    crossed = flip(cross, "row", 2)
    beta_half, b0 = cross[:HBLK], crossed[:HBLK]
    alpha_near = col_halves(alpha_half)
    x_pieces = send_rows(token_slots, crossed)
    *send, row_adapters, rel = adapter_pack(
        pick, qkv_up, swap(proj_down), fc1_up, swap(fc2_down), swap(qkv_down), swap(fc1_down), proj_up, fc2_up,
        norm1_gain.reshape(1, -1), norm2_gain.reshape(1, -1), rel_h, rel_w,
    )
    alpha_near, x_pieces[1] = after((alpha_near, x_pieces[1]))
    alpha_far = flip(alpha_near, "dp", 1)
    fc1_half, beta_own = after((fc1_half, beta_own), alpha_near)
    fc1_near = [flip(fc1_half, "col", j) for j in range(1, 4)]
    g = jnp.concatenate([alpha_own, alpha_near, alpha_far, row_adapters], axis=0)
    own1 = flip(beta_own, "row", 1)
    beta_sent = [jnp.concatenate([beta_half, b0, send[j]], axis=0) for j in range(1, 4)]
    *beta_sent, fc1_near = after((*beta_sent, jnp.concatenate(fc1_near, axis=0)), own1)
    beta_got = [flip(m, "col", j) for j, m in enumerate(beta_sent, 1)]
    fc1_far = flip(fc1_near, "dp", 1)
    g, *x_pieces = after((g, *x_pieces))
    gy = flip(g, "row", 2)
    grad_slots = pack(where, grad_out)
    *beta_got, fc1_far, _ = after((*beta_got, fc1_far, grad_slots[0]))
    beta_near = jnp.concatenate([b0] + [m[:QUART] for m in beta_got], axis=0)
    col_adapters = [send[0]] + beta_got
    beta_far = flip(beta_near, "dp", 1)
    g1, = after((g,), beta_near)
    g1, near1, gy1 = flip(g1, "row", 1), flip(beta_near, "row", 1), flip(gy, "row", 1)
    x_pieces = hand_on(x_pieces, beta_near)

    c0 = jnp.concatenate([crossed[HBLK : 2 * HBLK], crossed[2 * HBLK :]], axis=1)
    fc2_two = jnp.concatenate([fc2_half, c0], axis=0)
    h = jnp.concatenate([fc1_weight, fc1_near, fc1_far], axis=0)
    fc2_two, = after((fc2_two,), near1, g1, gy1)
    fc2_near = [flip(fc2_two, "col", j) for j in range(1, 4)]
    grad_own, grad_near, grad_pair = after(tuple(grad_slots), gy)
    grad_crossed = flip(grad_pair, "row", 2)
    beta_far, h, grad_crossed, *fc2_near = after((beta_far, h, grad_crossed, *fc2_near))
    far1 = flip(beta_far, "row", 1)
    hy = flip(h, "row", 2)
    fc2_near = jnp.concatenate([c0, *fc2_near], axis=0)
    fc2_far = flip(fc2_near, "dp", 1)
    wqkv, wproj, dqkv, uqkv, dproj, uproj, d1, u1, d2, u2, gain1, gain2 = prep1(
        where, (g, g1, gy, gy1), (beta_own, beta_near, beta_far, own1, near1, far1), col_adapters
    )
    grad_near, = after((grad_near,), wqkv)
    g_pieces = [grad_own, flip(grad_near, "row", 1), grad_crossed]
    x, hid, *qkvs = qkv_rows(x_pieces, gain1, wqkv)
    *qkvs, _ = after((*qkvs, g_pieces[1]))
    fc2_ahead = [flip(m, "row", 1) for m in (fc2_weight, fc2_near)]
    part0 = attention(0, qkvs[0], rel, shift, keys)
    qkv1, = after((qkvs[1],), part0[0], *fc2_ahead)
    part1 = attention(1, qkv1, rel, shift, keys)
    qkv2, _ = after((qkvs[2], part1[0]))
    part2 = attention(2, qkv2, rel, shift, keys)
    g_pieces = hand_on(g_pieces, part2[0])
    atts, exps, invs = zip(part0, part1, part2)
    atts = list(atts)
    atts[2], hy = after((atts[2], hy))
    alpha2 = [h, flip(h, "row", 1), hy, flip(hy, "row", 1)]
    middle = project(x, atts, wproj)
    middle, fc2_far = after((middle, fc2_far))
    beta2 = [fc2_weight, fc2_near, fc2_far, *fc2_ahead, flip(fc2_far, "row", 1)]

    *out_slots, gmid, down1, up1, down2, up2 = mlp(where, middle, g_pieces, gain2, alpha2, beta2, d1, u1, d2, u2)
    out_pieces = send_rows(out_slots)
    gqkv, down_q, up_q, down_p, up_p = attention_back(
        gmid, hid, qkvs, atts, exps, invs, wproj, rel, shift, keys, dqkv, uqkv, dproj, uproj
    )
    out_pieces = hand_on(out_pieces, gqkv)
    gqkv, down_q, up_q, down_p, up_p = after((gqkv, down_q, up_q, down_p, up_p), *out_pieces[:3])
    packed = grad_pack(where, down_q, up_q, down_p, up_p, down1, up1, down2, up2)
    *packed, gqkv = after((*packed, gqkv))
    row_sums = exchange(packed, "row")
    back0 = token_grad(gmid, x, gqkv, gain1, wqkv, *TAIL[0])
    *row_sums, gqkv, b0, b1, b2 = after((*row_sums, gqkv, *back0))
    back_pieces = send_rows((b0, b1, b2))
    summed = grad_sum(row_sums)
    *summed, gqkv = after((*summed, gqkv))
    images = exchange(summed, "col")
    back1 = token_grad(gmid, x, gqkv, gain1, wqkv, *TAIL[1])
    last_pieces = send_rows(back1)
    *images, near, crossed = after((*images, *back_pieces[1:]), back1[0])
    back_pieces = hand_on([back_pieces[0], near, crossed])
    images = jnp.stack(images)
    images, *out_pieces = after((images, *out_pieces))
    step = 1
    while step < batches:
        images = jnp.concatenate([images, flip(images, "dp", step)], axis=0)
        step *= 2
    result = unpack(where, out_pieces, BF)
    images, = after((images,), result)
    qkv_dn, fc1_dn, proj_upg, fc2_upg, rest = grad_adapters(slot_adapters.astype(jnp.int32), images)
    rests = [rest] + [flip(rest, "row", k) for k in range(1, 4)]
    grad_tokens = unpack(where, back_pieces + hand_on(last_pieces, rest), F32, TAIL)
    rests = after(tuple(rests), grad_tokens)
    qkv_upg, proj_dn, fc1_upg, fc2_dn = grad_join(where, rests)
    return (
        result, grad_tokens,
        swap(qkv_dn), qkv_upg, swap(proj_dn), proj_upg, swap(fc1_dn), fc1_upg, swap(fc2_dn), fc2_upg,
    )


def solution(mesh):
    return jax.shard_map(
        body,
        mesh=mesh,
        in_specs=(
            P("row", ("dp", "col")), P("row", ("dp", "col")), P(), P("row"), P("row"),
            P("row", "col"), P("col", "row"), P("row", "col"), P("row", "col"), P(), P(),
            P(None, "row", None), P(None, None, "col"), P(None, "col", None), P(None, None, "row"),
            P(None, "row", None), P(None, None, "col"), P(None, "col", None), P(None, None, "row"),
        ),
        out_specs=(
            P("row", ("dp", "col")), P("row", ("dp", "col")),
            P(None, "row", None), P(None, None, "col"), P(None, "col", None), P(None, None, "row"),
            P(None, "row", None), P(None, None, "col"), P(None, "col", None), P(None, None, "row"),
        ),
        check_vma=False,
    )
```

```python
import functools

import jax
import jax.numpy as jnp
import numpy as np
from jax import lax
from jax.experimental import pallas as pl
from jax.experimental.pallas import tpu as pltpu
from jax.sharding import PartitionSpec as P

D = 768
HD = 64
WIN = 14
SLOTS = WIN * WIN
SIDE = 64
ADAPT = 8
NWIN = 5
IMG_TOK = NWIN * NWIN * SLOTS
RANK = 16
EDGE = SIDE - (NWIN - 1) * WIN
QUART = D // 4
FULLR = 208
KEYS = 208
EDGER = EDGE * WIN
CORNR = EDGE * EDGE
ROWS = 4 * FULLR + 2 * EDGER + CORNR
HALF = ROWS // 2
HBLK = QUART // 2
EPSILON = 1e-06
BF = jnp.bfloat16
F32 = jnp.float32

FULL, RIGHT, BOTTOM, CORNER = 0, 1, 2, 3
NQ = (FULLR, EDGER, EDGER, CORNR)
OFFS = (0, 4 * FULLR, 4 * FULLR + EDGER, 4 * FULLR + 2 * EDGER)


def slot_order(kind):
    rows = EDGE if kind in (BOTTOM, CORNER) else WIN
    cols = EDGE if kind in (RIGHT, CORNER) else WIN
    kept = [a * WIN + b for a in range(rows) for b in range(cols)]
    rest = [s for s in range(SLOTS) if s not in set(kept)]
    return kept, kept + rest


def build_tables():
    shift = np.zeros((4, FULLR, 128), np.int32)
    keys = np.zeros((4, KEYS, 128), np.float32)
    for kind in range(4):
        kept, order = slot_order(kind)
        for i, s in enumerate(kept):
            for base in (0, 64):
                shift[kind, i, base : base + 32] = WIN - 1 - s // WIN
                shift[kind, i, base + 32 : base + 64] = WIN - 1 - s % WIN
        spare = order[0] if kind == FULL else order[-1]
        for i, s in enumerate(order + [spare] * (KEYS - SLOTS)):
            for base in (0, 64):
                keys[kind, i, base + s // WIN] = 1.0
                keys[kind, i, base + 32 + s % WIN] = 1.0
    return shift, keys.astype(jnp.bfloat16)


SHIFT_NP, KEYS_NP = build_tables()


def nn(a, b):
    return jnp.dot(a, b, preferred_element_type=F32)


def nt(a, b):
    return lax.dot_general(a, b, (((1,), (1,)), ((), ())), preferred_element_type=F32)


def tn(a, b):
    return lax.dot_general(a, b, (((0,), (0,)), ((), ())), preferred_element_type=F32)


def vm():
    return pl.BlockSpec(memory_space=pltpu.VMEM)


def hbm():
    return pl.BlockSpec(memory_space=pl.ANY)


def in_hbm(x):
    return pltpu.with_memory_space_constraint(x, pltpu.HBM)


def arg():
    return pl.BlockSpec(memory_space=pltpu.HBM)


def sm():
    return pl.BlockSpec(memory_space=pltpu.SMEM)


def params(mib=60):
    return pltpu.CompilerParams(vmem_limit_bytes=mib * 1024 * 1024)


def cost(us):
    return pl.CostEstimate(flops=int(us * 1e6), transcendentals=0, bytes_accessed=0)


def place_window(kind, count, moved, width, spare=-100000):
    row = lax.broadcasted_iota(jnp.int32, (count, width), 0)
    lane = lax.broadcasted_iota(jnp.int32, (count, width), 1)
    if kind in (RIGHT, CORNER):
        src = (row // EDGE) * WIN + row % EDGE
    else:
        src = jnp.where(row < SLOTS, row, spare)
    return (lane == src + moved).astype(F32).astype(BF)


def window_list(dest):
    items = [(FULL, FULLR * j, NWIN * dest + j) for j in range(4)]
    items.append((RIGHT, OFFS[1], NWIN * dest + 4))
    items.append((BOTTOM, OFFS[2], NWIN * 4 + dest))
    if dest == 3:
        items.append((CORNER, OFFS[3], NWIN * NWIN - 1))
    return items


def window_span(window):
    start = window * SLOTS
    low = start // 128 * 128
    high = min(-(-(start + SLOTS) // 128) * 128, IMG_TOK)
    return low, high, start - low


def pack_rows(mine, x_ref, rows_ref, spare):
    for dest in range(4):
        slot = jnp.bitwise_xor(mine, dest)
        if dest != 3:
            rows_ref[slot, OFFS[3] :, :] = jnp.zeros((CORNR, QUART), BF)
        for kind, offset, window in window_list(dest):
            low, high, moved = window_span(window)
            pick = place_window(kind, NQ[kind], moved, high - low, spare)
            rows_ref[slot, offset : offset + NQ[kind], :] = nt(pick, x_ref[:, low:high]).astype(BF)


def fold(rows_ref, outs):
    half = rows_ref.shape[1] // 2
    for slot, (out, base) in enumerate(((outs[0], 0), (outs[1], 0), (outs[2], 0), (outs[2], half))):
        out[base : base + half, :QUART] = rows_ref[slot, :half, :]
        out[base : base + half, QUART:] = rows_ref[slot, half:, :]


def pack_kernel(where_ref, x_hbm, o0, o1, o2, rows_ref, x_ref, sem):
    load = pltpu.make_async_copy(x_hbm, x_ref, sem)
    load.start()
    load.wait()
    pack_rows(where_ref[0], x_ref, rows_ref, -100000)
    fold(rows_ref, (o0, o1, o2))


def pieces_of(rows):
    piece = lambda n: jax.ShapeDtypeStruct((n, 2 * QUART), BF)
    return (piece(rows // 2), piece(rows // 2), piece(rows))


def pack(where, x):
    return pl.pallas_call(
        pack_kernel,
        out_shape=pieces_of(ROWS),
        in_specs=[sm(), arg()],
        out_specs=[vm()] * 3,
        scratch_shapes=[
            pltpu.VMEM((4, ROWS, QUART), BF), pltpu.VMEM((QUART, IMG_TOK), BF), pltpu.SemaphoreType.DMA,
        ],
        compiler_params=params(16),
        cost_estimate=cost(4),
        name="pack",
    )(where, in_hbm(x))


def front_kernel(
    where_ref, x_hbm, qkv_hbm, proj_hbm, fc1_hbm, fc2_hbm,
    o0, o1, o2, alpha_ref, beta_ref, alpha_half, cross_ref, fc1_half, fc2_half,
    rows_ref, x_ref, qkv_w, proj_w, sem,
):
    rows = pl.ds(pl.multiple_of(where_ref[1] * HBLK, 32), HBLK)
    loads = [
        pltpu.make_async_copy(src, dst, sem.at[i])
        for i, (src, dst) in enumerate(
            (
                (qkv_hbm, qkv_w), (proj_hbm, proj_w), (fc2_hbm.at[rows, :], fc2_half),
                (fc1_hbm.at[rows, :], fc1_half), (x_hbm, x_ref),
            )
        )
    ]
    for load in loads:
        load.start()
    for load in loads[:4]:
        load.wait()
    heads = qkv_w.shape[1] // (3 * HD)
    for h in range(heads):
        for t in range(3):
            ref, base = (alpha_ref, QUART * t) if t < 2 else (beta_ref, 0)
            ref[:, base + HD * h : base + HD * (h + 1)] = qkv_w[:, HD * (3 * h + t) : HD * (3 * h + t + 1)]
    beta_ref[:, QUART:] = proj_w[...]
    alpha_half[...] = alpha_ref[rows, :]
    cross_ref[:HBLK, :] = beta_ref[rows, :]
    cross_ref[HBLK : 2 * HBLK, :] = fc2_half[:, : 2 * QUART]
    cross_ref[2 * HBLK :, :] = fc2_half[:, 2 * QUART :]
    loads[4].wait()
    pack_rows(where_ref[0], x_ref, rows_ref, 0)
    fold(rows_ref, (o0, o1, o2))


def front(where, x, qkv_w, proj_w, fc1_w, fc2_w):
    s = lambda *shape: jax.ShapeDtypeStruct(shape, BF)
    return pl.pallas_call(
        front_kernel,
        out_shape=pieces_of(ROWS)
        + (
            s(QUART, 2 * QUART), s(QUART, 2 * QUART), s(HBLK, 2 * QUART), s(3 * HBLK, 2 * QUART),
            s(HBLK, D), s(HBLK, D),
        ),
        in_specs=[sm()] + [arg()] * 5,
        out_specs=[vm()] * 9,
        scratch_shapes=[
            pltpu.VMEM((4, ROWS, QUART), BF), pltpu.VMEM((QUART, IMG_TOK), BF),
            pltpu.VMEM(qkv_w.shape, BF), pltpu.VMEM(proj_w.shape, BF), pltpu.SemaphoreType.DMA((5,)),
        ],
        compiler_params=params(16),
        cost_estimate=cost(5),
        name="token_and_weight_pack",
    )(where, *(in_hbm(m) for m in (x, qkv_w, proj_w, fc1_w, fc2_w)))


def unpack_kernel(where_ref, *refs, bounds):
    pieces, (out_ref, acc_ref, rows_ref) = refs[:-3], refs[-3:]
    mine = where_ref[0]
    acc_ref[...] = jnp.zeros_like(acc_ref)
    index = 0
    for low, high in bounds:
        half = (high - low) // 2
        for slot in range(4):
            piece = pieces[index]
            rows = slice(half, 2 * half) if slot == 3 else slice(0, half)
            rows_ref[slot, low : low + half, :] = piece[rows, :QUART]
            rows_ref[slot, low + half : high, :] = piece[rows, QUART:]
            index += 1

    for source in range(4):
        slot = jnp.bitwise_xor(mine, source)
        for kind, offset, window in window_list(source):
            low, high, moved = window_span(window)
            pick = place_window(kind, NQ[kind], moved, high - low)
            acc_ref[:, low:high] += tn(rows_ref[slot, offset : offset + NQ[kind], :], pick)
    out_ref[...] = acc_ref[:, :IMG_TOK].astype(out_ref.dtype)


def unpack(where, pieces, dtype, bounds=((0, ROWS),)):
    return pl.pallas_call(
        functools.partial(unpack_kernel, bounds=bounds),
        out_shape=jax.ShapeDtypeStruct((QUART, IMG_TOK), dtype),
        in_specs=[sm()] + [vm()] * len(pieces),
        out_specs=vm(),
        scratch_shapes=[
            pltpu.VMEM((QUART, -(-IMG_TOK // 128) * 128), F32),
            pltpu.VMEM((4, ROWS, QUART), BF),
        ],
        compiler_params=params(24),
        cost_estimate=cost(4),
        name="unpack",
    )(where, *pieces)


def join_pieces(pieces, dst_ref):
    for slot, piece in enumerate(pieces):
        rows = slice(HALF, ROWS) if slot == 3 else slice(0, HALF)
        dst_ref[:HALF, QUART * slot : QUART * (slot + 1)] = piece[rows, :QUART]
        dst_ref[HALF:, QUART * slot : QUART * (slot + 1)] = piece[rows, QUART:]


def split_pieces(src_ref, outs):
    half = src_ref.shape[0] // 2
    for slot, (out, base) in enumerate(((outs[0], 0), (outs[1], 0), (outs[2], 0), (outs[2], half))):
        out[base : base + half, :QUART] = src_ref[:half, QUART * slot : QUART * (slot + 1)]
        out[base : base + half, QUART:] = src_ref[half:, QUART * slot : QUART * (slot + 1)]


def adapter_pack_kernel(
    pick_ref, qkv_up_hbm, proj_dn_hbm, fc1_up_hbm, fc2_dn_hbm, qkv_dn_hbm, fc1_dn_hbm, proj_up_hbm, fc2_up_hbm,
    gain1, gain2, rel_h, rel_w, s0, s1, s2, s3, row_ref, rel_ref,
    qkv_up, proj_dn, fc1_up, fc2_dn, qkv_dn, fc1_dn, proj_up, fc2_up, sem,
):
    pairs = []
    for j in range(4):
        for src, dst in ((qkv_up_hbm, qkv_up), (proj_dn_hbm, proj_dn), (fc1_up_hbm, fc1_up), (fc2_dn_hbm, fc2_dn)):
            pairs.append((src.at[pick_ref[j]], dst.at[j]))
    for src, dst in ((qkv_dn_hbm, qkv_dn), (fc1_dn_hbm, fc1_dn), (proj_up_hbm, proj_up), (fc2_up_hbm, fc2_up)):
        pairs.append((src.at[pick_ref[0]], dst.at[0]))
    loads = [pltpu.make_async_copy(src, dst, sem.at[i]) for i, (src, dst) in enumerate(pairs)]
    for load in loads:
        load.start()
    offsets = rel_h.shape[0]
    reverse = (
        lax.broadcasted_iota(jnp.int32, (offsets, 32), 0) + lax.broadcasted_iota(jnp.int32, (offsets, 32), 1)
        == offsets - 1
    ).astype(F32).astype(BF)
    rel_ref[...] = jnp.zeros_like(rel_ref)
    for i, table in enumerate((rel_h, rel_w)):
        block = tn(table[...], reverse).astype(BF)
        rel_ref[:HD, HD + 32 * i : HD + 32 * (i + 1)] = block
        rel_ref[HD:, 32 * i : 32 * (i + 1)] = block
    for load in loads:
        load.wait()
    heads = qkv_up.shape[2] // (3 * HD)
    half = 2 * QUART
    for j, send_ref in enumerate((s0, s1, s2, s3)):
        for h in range(heads):
            for t in range(3):
                row, base = (0, QUART * t) if t < 2 else (RANK, 0)
                send_ref[row : row + RANK, base + HD * h : base + HD * (h + 1)] = qkv_up[
                    j, :, HD * (3 * h + t) : HD * (3 * h + t + 1)
                ]
        send_ref[RANK : 2 * RANK, QUART:] = proj_dn[j]
        for i, ref in enumerate((fc1_up, fc2_dn)):
            for part in range(2):
                row = RANK * (2 + 2 * i + part)
                send_ref[row : row + RANK, :] = ref[j, :, half * part : half * (part + 1)]
    for i, ref in enumerate((qkv_dn, fc1_dn, proj_up, fc2_up)):
        row, base = RANK * (i // 2), QUART * (i % 2)
        row_ref[row : row + RANK, base : base + QUART] = ref[0]
    for i, ref in enumerate((gain1, gain2)):
        row_ref[2 * RANK :, QUART * i : QUART * (i + 1)] = jnp.broadcast_to(ref[...], (RANK, QUART))


def adapter_pack(pick, *mats):
    s = lambda *shape: jax.ShapeDtypeStruct(shape, BF)
    return pl.pallas_call(
        adapter_pack_kernel,
        out_shape=(s(6 * RANK, 2 * QUART),) * 4 + (s(3 * RANK, 2 * QUART), s(128, 128)),
        in_specs=[sm()] + [arg()] * 8 + [vm()] * 4,
        out_specs=[vm()] * 6,
        scratch_shapes=[pltpu.VMEM((4,) + m.shape[1:], BF) for m in mats[:4]]
        + [pltpu.VMEM((1,) + m.shape[1:], BF) for m in mats[4:8]]
        + [pltpu.SemaphoreType.DMA((20,))],
        compiler_params=params(8),
        cost_estimate=cost(2),
        name="adapter_pack",
    )(pick, *(in_hbm(m) for m in mats[:8]), *mats[8:])


def alpha_block(k, j):
    part = k
    if j == 0:
        return [(part, 0, QUART, None)]
    return [
        (part, QUART + HBLK * (j - 1), HBLK, 0),
        (part, QUART + 3 * HBLK + HBLK * (j - 1), HBLK, 1),
    ]


def beta_block(k, j):
    core, cross = k % 2, k // 2
    base = 3 * core
    if j == 0 and not cross:
        return [(base, 0, QUART, None)]
    row = 0 if j == 0 else HBLK + QUART * (j - 1) + HBLK * cross
    return [(base + 1, row, HBLK, 0), (base + 2, row, HBLK, 1)]


def block_dst(start, flag, half):
    if flag is None:
        return start
    offset = half if flag == 0 else 1 - half
    return pl.multiple_of(start + offset * HBLK, 32)


def prep1_kernel(
    where_ref, p0, p1, p2, p3, q0, q1, q2, q3, q4, q5, a0, a1, a2, a3,
    wqkv_ref, wproj_ref, dqkv, uqkv, dproj, uproj, d1, u1, d2, u2, gain1, gain2, ups, downs,
):
    half = where_ref[1]
    for j, a in enumerate((a0, a1, a2, a3)):
        base = a.shape[0] - 6 * RANK
        part = lambda i: slice(base + RANK * i, base + RANK * (i + 1))
        for t in range(3):
            uqkv[:, D * t + QUART * j : D * t + QUART * (j + 1)] = a[
                part(t // 2), QUART * (t % 2) : QUART * (t % 2 + 1)
            ]
        dproj[:, QUART * j : QUART * (j + 1)] = a[part(1), QUART:]
        for i in range(2):
            u1[:, D * j + D // 2 * i : D * j + D // 2 * (i + 1)] = a[part(2 + i), :]
            d2[:, D * j + D // 2 * i : D * j + D // 2 * (i + 1)] = a[part(4 + i), :]
    for k, ref in enumerate((p0, p1, p2, p3)):
        for i, dst in enumerate((dqkv, d1, uproj, u2)):
            rows = slice(D + RANK * (i // 2), D + RANK * (i // 2 + 1))
            dst[:, QUART * k : QUART * (k + 1)] = ref[rows, QUART * (i % 2) : QUART * (i % 2 + 1)]
        for i, dst in enumerate((gain1, gain2)):
            row = D + 2 * RANK
            dst[:, QUART * k : QUART * (k + 1)] = ref[row : row + 1, QUART * i : QUART * (i + 1)].astype(F32)
    alpha, beta = (p0, p1, p2, p3), (q0, q1, q2, q3, q4, q5)
    for k in range(4):
        for j in range(4):
            for part, row, count, flag in alpha_block(k, j):
                rows = pl.ds(block_dst(QUART * k, flag, half), count)
                for t in range(2):
                    wqkv_ref[rows, D * t + QUART * j : D * t + QUART * (j + 1)] = alpha[part][
                        row : row + count, QUART * t : QUART * (t + 1)
                    ]
            for part, row, count, flag in beta_block(k, j):
                rows = pl.ds(block_dst(QUART * k, flag, half), count)
                wqkv_ref[rows, 2 * D + QUART * j : 2 * D + QUART * (j + 1)] = beta[part][
                    row : row + count, :QUART
                ]
                rows = pl.ds(block_dst(QUART * j, flag, half), count)
                wproj_ref[rows, QUART * k : QUART * (k + 1)] = beta[part][row : row + count, QUART:]
    for t in range(3):
        ups[t] = uqkv[:, D * t : D * (t + 1)]
    ups[3] = uproj[...]
    for k in range(4):
        downs[k] = dqkv[:, QUART * k : QUART * (k + 1)]
        downs[4 + k] = dproj[:, QUART * k : QUART * (k + 1)]

    def merge(t, carry):
        cols = pl.ds(pl.multiple_of(D * t, 128), D)
        for k in range(4):
            rows = slice(QUART * k, QUART * (k + 1))
            wqkv_ref[rows, cols] = (wqkv_ref[rows, cols].astype(F32) + tn(downs[k], ups[t])).astype(BF)
        return carry

    lax.fori_loop(0, 3, merge, 0)
    for k in range(4):
        rows = slice(QUART * k, QUART * (k + 1))
        wproj_ref[rows, :] = (wproj_ref[rows, :].astype(F32) + tn(downs[4 + k], ups[3])).astype(BF)


def prep1(where, alpha, beta, cols):
    s = lambda *shape: jax.ShapeDtypeStruct(shape, BF)
    return pl.pallas_call(
        prep1_kernel,
        out_shape=(
            s(D, 3 * D), s(D, D), s(RANK, D), s(RANK, 3 * D), s(RANK, D), s(RANK, D),
            s(RANK, D), s(RANK, 4 * D), s(RANK, 4 * D), s(RANK, D),
            jax.ShapeDtypeStruct((1, D), F32), jax.ShapeDtypeStruct((1, D), F32),
        ),
        in_specs=[sm()] + [vm()] * 14,
        out_specs=[vm()] * 12,
        scratch_shapes=[pltpu.VMEM((4, RANK, D), BF), pltpu.VMEM((8, RANK, QUART), BF)],
        compiler_params=params(24),
        cost_estimate=cost(7),
        name="attention_weights",
    )(where, *alpha, *beta, *cols)


def normalize(values):
    center = jnp.sum(values, axis=1, keepdims=True) / D
    shifted = values - center
    inv_std = lax.rsqrt(jnp.sum(shifted * shifted, axis=1, keepdims=True) / D + EPSILON)
    return shifted * inv_std, inv_std


def norm_back(grad, normed, inv_std):
    first = jnp.sum(grad, axis=1, keepdims=True) / D
    second = jnp.sum(grad * normed, axis=1, keepdims=True) / D
    return inv_std * (grad - first - normed * second)


def barrel(values, amount, left):
    for bit in (1, 2, 4, 8):
        moved = pltpu.roll(values, (128 - bit) if left else bit, 1)
        values = jnp.where((amount & bit) != 0, moved, values)
    return values


def low_half(count):
    return lax.broadcasted_iota(jnp.int32, (count, 128), 1) < HD


def pad_rows(tile):
    if tile.shape[0] == KEYS:
        return tile
    return jnp.concatenate([tile, jnp.zeros((KEYS - tile.shape[0], tile.shape[1]), tile.dtype)], axis=0)


def live_rows():
    return lax.broadcasted_iota(jnp.int32, (KEYS, 128), 0) < SLOTS


GROUP = 6
GROUP_BACK = 6


def pair_columns(pair):
    return tuple(slice(D * t + 128 * pair, D * t + 128 * (pair + 1)) for t in range(3))


def attend_window(kind, row0, qkv_ref, att_ref, exp_ref, inv_ref, rel_ref, shift_ref, keys_ref):
    count = NQ[kind]
    rows = pl.ds(row0, count)
    low_q, low_k = low_half(count), low_half(KEYS)
    live = live_rows()
    ones = jnp.where(live, 1.0, 0.0).astype(BF)
    amount = shift_ref[kind, :count, :]
    onehot = keys_ref[kind]
    rel_mat = rel_ref[...]
    for first in range(0, D // 128, GROUP):
        pairs = range(first, first + GROUP)
        heads = [(pair, odd) for pair in pairs for odd in range(2)]
        q_tile = {p: qkv_ref[rows, pair_columns(p)[0]] for p in pairs}
        rel = {p: nn(q_tile[p], rel_mat) for p in pairs}
        rel = {p: barrel(rel[p], amount, True).astype(BF) for p in pairs}
        k_tile = {p: pad_rows(qkv_ref[rows, pair_columns(p)[1]] * BF(HD**-0.5)) for p in pairs}
        scores = {}
        for p, odd in heads:
            if odd:
                q_aug, k_aug = jnp.where(low_q, rel[p], q_tile[p]), jnp.where(low_k, onehot, k_tile[p])
            else:
                q_aug, k_aug = jnp.where(low_q, q_tile[p], rel[p]), jnp.where(low_k, k_tile[p], onehot)
            scores[p, odd] = nt(q_aug, k_aug)
        top = {h: jnp.max(scores[h], axis=1, keepdims=True) for h in heads}
        exponent = {h: jnp.exp(scores[h] - top[h]).astype(BF) for h in heads}
        both = {}
        for p, odd in heads:
            exp_ref[2 * p + odd, rows, :] = exponent[p, odd]
            v_tile = pad_rows(qkv_ref[rows, pair_columns(p)[2]])
            if kind == FULL:
                v_tile = jnp.where(live, v_tile, 0).astype(BF)
            v_aug = jnp.where(low_k, ones, v_tile) if odd else jnp.where(low_k, v_tile, ones)
            both[p, odd] = nn(exponent[p, odd], v_aug)
        for p in pairs:
            cols = pair_columns(p)[0]
            inverse = 1.0 / pltpu.roll(jnp.where(low_q, both[p, 1], both[p, 0]), HD, 1)
            inv_ref[rows, cols] = inverse
            att_ref[rows, cols] = (jnp.where(low_q, both[p, 0], both[p, 1]) * inverse).astype(BF)


PARTS = ((FULL, FULL), (FULL, FULL), (RIGHT, BOTTOM, CORNER))
PART_ROWS = tuple(sum(NQ[kind] for kind in part) for part in PARTS)
PART_OFFS = (0, PART_ROWS[0], PART_ROWS[0] + PART_ROWS[1])


TAIL = ((0, 576), (576, ROWS))


def qkv_kernel(
    x0, x1, x2, x3, gain_ref, w_hbm, x_hbm, hid_hbm, qkv_a, qkv_b, qkv_c,
    x_ref, hid_ref, rows_ref, w_ref, qkv_ref, sem, out_sem,
):
    loads = [
        pltpu.make_async_copy(w_hbm.at[:, D * t : D * (t + 1)], w_ref.at[t], sem.at[t]) for t in range(3)
    ]
    for load in loads:
        load.start()
    join_pieces((x0, x1, x2, x3), x_ref)
    kept = [
        pltpu.make_async_copy(src, dst, sem.at[3 + i])
        for i, (src, dst) in enumerate(((x_ref, x_hbm), (hid_ref, hid_hbm)))
    ]
    kept[0].start()
    gain = gain_ref[...]

    def norm_step(i, carry):
        rows = pl.ds(pl.multiple_of(i * 112, 16), 112)
        normed, _ = normalize(x_ref[rows, :].astype(F32))
        hidden = (normed * gain).astype(BF)
        rows_ref[rows, :] = hidden
        hid_ref[rows, :] = hidden
        return carry

    lax.fori_loop(0, ROWS // 112, norm_step, 0)
    for w in range(4):
        hid_ref[FULLR * w + SLOTS : FULLR * (w + 1), :] = jnp.zeros((FULLR - SLOTS, D), BF)
    kept[1].start()
    for load in loads:
        load.wait()

    def stores(t):
        cols = pl.ds(pl.multiple_of(D * t, 128), D)
        return [
            pltpu.make_async_copy(
                qkv_ref.at[t, pl.ds(offset, count), :], out.at[:, cols], out_sem.at[t, i]
            )
            for i, (out, offset, count) in enumerate(zip((qkv_a, qkv_b, qkv_c), PART_OFFS, PART_ROWS))
        ]

    def project_step(t, carry):
        qkv_ref[t] = nn(rows_ref[...], w_ref[t]).astype(BF)
        for store in stores(t):
            store.start()
        return carry

    lax.fori_loop(0, 3, project_step, 0)
    for t in range(3):
        for store in stores(t):
            store.wait()
    for store in kept:
        store.wait()


def qkv_rows(pieces, gain, wqkv):
    s = lambda *shape: jax.ShapeDtypeStruct(shape, BF)
    return pl.pallas_call(
        qkv_kernel,
        out_shape=(s(ROWS, D), s(ROWS, D)) + tuple(s(n, 3 * D) for n in PART_ROWS),
        in_specs=[vm()] * 5 + [hbm()],
        out_specs=[hbm()] * 5,
        scratch_shapes=[
            pltpu.VMEM((ROWS, D), BF), pltpu.VMEM((ROWS, D), BF), pltpu.VMEM((ROWS, D), BF),
            pltpu.VMEM((3, D, D), BF), pltpu.VMEM((3, ROWS, D), BF),
            pltpu.SemaphoreType.DMA((5,)), pltpu.SemaphoreType.DMA((3, 3)),
        ],
        compiler_params=params(32),
        cost_estimate=cost(10),
        name="norm_and_qkv",
    )(*pieces, gain, wqkv)


def attention_kernel(qkv_ref, rel_ref, shift_ref, keys_ref, att_ref, exp_ref, inv_ref, *, kinds):
    refs = (qkv_ref, att_ref, exp_ref, inv_ref, rel_ref, shift_ref, keys_ref)
    if kinds[0] == FULL:

        def step(w, carry):
            attend_window(FULL, pl.multiple_of(w * FULLR, 16), *refs)
            return carry

        lax.fori_loop(0, len(kinds), step, 0)
    else:
        row = 0
        for kind in kinds:
            attend_window(kind, row, *refs)
            row += NQ[kind]


def attention(part, qkv, rel, shift, keys):
    rows = PART_ROWS[part]
    s = lambda *shape, dtype=BF: jax.ShapeDtypeStruct(shape, dtype)
    return pl.pallas_call(
        functools.partial(attention_kernel, kinds=PARTS[part]),
        out_shape=(s(rows, D), s(D // HD, rows, KEYS), s(rows, D, dtype=F32)),
        in_specs=[vm()] * 4,
        out_specs=[vm()] * 3,
        compiler_params=params(24),
        cost_estimate=cost(10),
        name="attention_forward",
    )(qkv, rel, shift, keys)


def project_kernel(x_ref, att_a, att_b, att_c, wproj_ref, middle_ref):
    for ref, offset, count in zip((att_a, att_b, att_c), PART_OFFS, PART_ROWS):
        rows = slice(offset, offset + count)
        middle_ref[rows, :] = x_ref[rows, :].astype(F32) + nn(ref[...], wproj_ref[...])


def project(x, atts, wproj):
    return pl.pallas_call(
        project_kernel,
        out_shape=jax.ShapeDtypeStruct((ROWS, D), F32),
        in_specs=[vm()] * 5,
        out_specs=vm(),
        compiler_params=params(20),
        cost_estimate=cost(5),
        name="projection",
    )(x, *atts, wproj)


CHUNK = 512
LOCK = 1


def mlp_kernel(
    where_ref, middle_ref, g0, g1, g2, g3, gain_ref,
    p0, p1, p2, p3, q0, q1, q2, q3, q4, q5, d1, u1, d2, u2,
    o0, o1, o2, gmid_ref, down1, up1, down2, up2,
    gm_ref, out_rows, h2_ref, acc_mlp, acc_gh, gu1, ad2, w1_ref, w2_ref, downs, sem,
):
    half = where_ref[1]
    copies = []

    def fetch(src, dst):
        copies.append(pltpu.make_async_copy(src, dst, sem.at[len(copies)]))
        copies[-1].start()

    alpha, beta = (p0, p1, p2, p3), (q0, q1, q2, q3, q4, q5)
    for k in range(4):
        for j in range(4):
            for part, row, count, flag in alpha_block(k, j):
                rows = pl.ds(block_dst(QUART * k, flag, half), count)
                fetch(alpha[part].at[row : row + count, :], w1_ref.at[rows, D * j : D * (j + 1)])
            for part, row, count, flag in beta_block(k, j):
                rows = pl.ds(block_dst(QUART * k, flag, half), count)
                fetch(beta[part].at[row : row + count, :], w2_ref.at[rows, D * j : D * (j + 1)])
    join_pieces((g0, g1, g2, g3), gm_ref)
    for k in range(4):
        downs[k] = d1[:, QUART * k : QUART * (k + 1)]
        downs[4 + k] = u2[:, QUART * k : QUART * (k + 1)]
    for copy in copies:
        copy.wait()

    def merge(j, carry):
        cols = pl.ds(pl.multiple_of(D * j, 128), D)
        for k in range(4):
            rows = slice(QUART * k, QUART * (k + 1))
            w1_ref[rows, cols] = (w1_ref[rows, cols].astype(F32) + tn(downs[k], u1[:, cols])).astype(BF)
            w2_ref[rows, cols] = (w2_ref[rows, cols].astype(F32) + tn(downs[4 + k], d2[:, cols])).astype(BF)
        return carry

    lax.fori_loop(0, 4, merge, 0)
    gain = gain_ref[...]
    down1[...] = jnp.zeros_like(down1)
    up1[...] = jnp.zeros_like(up1)
    down2[...] = jnp.zeros_like(down2)
    up2[...] = jnp.zeros_like(up2)

    def tile_step(t, carry):
        rows = pl.ds(pl.multiple_of(t * HALF, 16), HALF)
        normed, _ = normalize(middle_ref[rows, :])
        h2 = (normed * gain).astype(BF)
        h2_ref[...] = h2
        gm = gm_ref[rows, :]
        ad1 = nt(d1[...], h2).astype(BF)
        gu2 = nt(u2[...], gm).astype(BF)
        acc_mlp[...] = jnp.zeros_like(acc_mlp)
        acc_gh[...] = jnp.zeros_like(acc_gh)
        gu1[...] = jnp.zeros_like(gu1)
        ad2[...] = jnp.zeros_like(ad2)

        def chunk_step(c, inner_carry):
            spans = [
                pl.ds(pl.multiple_of((c * LOCK + i) * CHUNK, CHUNK), CHUNK) for i in range(LOCK)
            ]
            h2 = h2_ref[...]
            gm = gm_ref[rows, :]
            inner = [nn(h2, w1_ref[:, span]) for span in spans]
            gact = [nn(gm, w2_ref[:, span]) for span in spans]
            act, ginner = [], []
            for i in range(LOCK):
                half = 0.5 * (1.0 + lax.erf(inner[i] * 2**-0.5))
                act.append((inner[i] * half).astype(BF))
                slope = half + inner[i] * (jnp.exp(-0.5 * inner[i] * inner[i]) * (2 * np.pi) ** -0.5)
                ginner.append((gact[i] * slope).astype(BF))
            for i, span in enumerate(spans):
                acc_mlp[...] += nt(act[i], w2_ref[:, span])
                acc_gh[...] += nt(ginner[i], w1_ref[:, span])
                up1[:, span] += nn(ad1, ginner[i])
                gu1[...] += nt(u1[:, span], ginner[i])
                ad2[...] += nt(d2[:, span], act[i])
                down2[:, span] += nn(gu2, act[i])
            return inner_carry

        lax.fori_loop(0, 4 * D // (CHUNK * LOCK), chunk_step, 0)
        down1[...] += nn(gu1[...].astype(BF), h2_ref[...])
        up2[...] += nn(ad2[...].astype(BF), gm_ref[rows, :])
        middle = middle_ref[rows, :]
        out_rows[rows, :] = (middle + acc_mlp[...]).astype(BF)
        normed, inv_std = normalize(middle)
        gmid_ref[rows, :] = gm_ref[rows, :].astype(F32) + norm_back(acc_gh[...] * gain, normed, inv_std)
        return carry

    lax.fori_loop(0, 2, tile_step, 0)
    split_pieces(out_rows, (o0, o1, o2))


def mlp(where, middle, pieces, gain, alpha, beta, d1, u1, d2, u2):
    s = lambda *shape, dtype=F32: jax.ShapeDtypeStruct(shape, dtype)
    return pl.pallas_call(
        mlp_kernel,
        out_shape=pieces_of(ROWS)
        + (s(ROWS, D), s(RANK, D), s(RANK, 4 * D), s(RANK, 4 * D), s(RANK, D)),
        in_specs=[sm()] + [vm()] * 6 + [pl.BlockSpec(memory_space=pl.ANY)] * 10 + [vm()] * 4,
        out_specs=[vm()] * 8,
        scratch_shapes=[
            pltpu.VMEM((ROWS, D), BF), pltpu.VMEM((ROWS, D), BF), pltpu.VMEM((HALF, D), BF),
            pltpu.VMEM((HALF, D), F32), pltpu.VMEM((HALF, D), F32),
            pltpu.VMEM((RANK, HALF), F32), pltpu.VMEM((RANK, HALF), F32),
            pltpu.VMEM((D, 4 * D), BF), pltpu.VMEM((D, 4 * D), BF), pltpu.VMEM((8, RANK, QUART), BF),
            pltpu.SemaphoreType.DMA((4 * 4 * 4,)),
        ],
        compiler_params=params(48),
        cost_estimate=cost(48),
        name="mlp_forward_backward",
    )(where, middle, *pieces, gain, *alpha, *beta, d1, u1, d2, u2)


def attend_back_window(
    kind, row0, qkv_ref, att_ref, exp_ref, inv_ref, gatt_ref, gqkv_ref, rel_ref, shift_ref, keys_ref
):
    count = NQ[kind]
    rows = pl.ds(row0, count)
    low_q, low_k = low_half(count), low_half(KEYS)
    live = live_rows()
    lane_k = lax.broadcasted_iota(jnp.int32, (KEYS, 128), 1) % HD
    lane_q = lax.broadcasted_iota(jnp.int32, (count, 128), 1) % HD
    ones = jnp.where(live & (lane_k < 2), 1.0, 0.0).astype(BF)
    across = jnp.where(
        low_half(128) != (lax.broadcasted_iota(jnp.int32, (128, 128), 0) < HD), -1.0, 0.0
    ).astype(BF)
    amount = shift_ref[kind, :count, :]
    onehot = keys_ref[kind]
    rel_mat = rel_ref[...]
    for first in range(0, D // 128, GROUP_BACK):
        pairs = range(first, first + GROUP_BACK)
        heads = [(pair, odd) for pair in pairs for odd in range(2)]
        go_tile = {
            p: (gatt_ref[rows, pair_columns(p)[0]].astype(F32) * inv_ref[rows, pair_columns(p)[0]]).astype(BF)
            for p in pairs
        }
        delta = {
            p: nn((go_tile[p].astype(F32) * att_ref[rows, pair_columns(p)[0]].astype(F32)).astype(BF), across)
            for p in pairs
        }
        go_t = {p: go_tile[p].T for p in pairs}
        gv = {}
        for p, odd in heads:
            gv[p, odd] = nn(go_t[p][HD * odd : HD * (odd + 1), :], exp_ref[2 * p + odd, rows, :])
        gscore = {}
        for p in pairs:
            high = delta[p].astype(BF)
            rest = (delta[p] - high.astype(F32)).astype(BF)
            low_delta = jnp.where(lane_q == 0, high, jnp.where(lane_q == 1, rest, 0)).astype(BF)
            v_tile = pad_rows(qkv_ref[rows, pair_columns(p)[2]])
            if kind == FULL:
                v_tile = jnp.where(live, v_tile, 0).astype(BF)
            gscore[p, 0] = nt(jnp.where(low_q, go_tile[p], low_delta), jnp.where(low_k, v_tile, ones))
            gscore[p, 1] = nt(jnp.where(low_q, low_delta, go_tile[p]), jnp.where(low_k, ones, v_tile))
        q_t = {p: qkv_ref[rows, pair_columns(p)[0]].T for p in pairs}
        gs = {(p, odd): (exp_ref[2 * p + odd, rows, :].astype(F32) * gscore[p, odd]).astype(BF) for p, odd in heads}
        gk = {(p, odd): nn(q_t[p][HD * odd : HD * (odd + 1), :], gs[p, odd]) for p, odd in heads}
        gq = {}
        for p in pairs:
            k_tile = pad_rows(qkv_ref[rows, pair_columns(p)[1]] * BF(HD**-0.5))
            gq[p, 0] = nn(gs[p, 0], jnp.where(low_k, k_tile, onehot))
            gq[p, 1] = nn(gs[p, 1], jnp.where(low_k, onehot, k_tile))
        sums = {p: barrel(jnp.where(low_q, gq[p, 1], gq[p, 0]), amount, False).astype(BF) for p in pairs}
        for p in pairs:
            cols, kcols, vcols = pair_columns(p)
            gv_tile = jnp.concatenate([gv[p, 0], gv[p, 1]], axis=0).astype(BF).T
            gqkv_ref[rows, vcols] = gv_tile[:count, :]
            gk_tile = (jnp.concatenate([gk[p, 0], gk[p, 1]], axis=0) * HD**-0.5).astype(BF).T
            gqkv_ref[rows, kcols] = gk_tile[:count, :]
            gqkv_ref[rows, cols] = (jnp.where(low_q, gq[p, 0], gq[p, 1]) + nt(sums[p], rel_mat)).astype(BF)


def attention_back_kernel(
    gmid_hbm, hid_hbm, qkv_a, qkv_b, qkv_c, att_a, att_b, att_c, exp_a, exp_b, exp_c, inv_a, inv_b, inv_c,
    wproj_ref, rel_ref, shift_ref, keys_ref, dqkv, uqkv, dproj, uproj,
    gqkv_hbm, down_q, up_q, down_p, up_p,
    gmid_ref, hid_ref, qkv_ref, att_ref, exp_ref, inv_ref, gqkv_ref, gb_ref, gatt_ref, sem, out_sem,
):
    spans = [pl.ds(offset, count) for offset, count in zip(PART_OFFS, PART_ROWS)]
    pairs = [(gmid_hbm, gmid_ref)]
    for part, srcs in enumerate(
        ((qkv_a, inv_a, att_a, exp_a), (qkv_b, inv_b, att_b, exp_b), (qkv_c, inv_c, att_c, exp_c))
    ):
        rows = spans[part]
        for src, dst in zip(srcs, (qkv_ref, inv_ref, att_ref)):
            pairs.append((src, dst.at[rows, :]))
        pairs.append((srcs[3], exp_ref.at[:, rows, :]))
    pairs.append((hid_hbm, hid_ref))
    loads = [pltpu.make_async_copy(src, dst, sem.at[i]) for i, (src, dst) in enumerate(pairs)]
    for load in loads:
        load.start()

    def wait_part(part):
        for load in loads[1 + 4 * part : 5 + 4 * part]:
            load.wait()

    stores = [
        pltpu.make_async_copy(gqkv_ref.at[rows, :], gqkv_hbm.at[rows, :], out_sem.at[i])
        for i, rows in enumerate(spans)
    ]
    loads[0].wait()
    gb_ref[...] = gmid_ref[...].astype(BF)
    gatt_ref[...] = nt(gb_ref[...], wproj_ref[...]).astype(BF)
    refs = (qkv_ref, att_ref, exp_ref, inv_ref, gatt_ref, gqkv_ref, rel_ref, shift_ref, keys_ref)

    def step(w, carry):
        for part in range(2):

            @pl.when(w == 2 * part)
            def _():
                wait_part(part)

        attend_back_window(FULL, pl.multiple_of(w * FULLR, 16), *refs)
        return carry

    lax.fori_loop(0, 4, step, 0)
    stores[0].start()
    stores[1].start()
    wait_part(2)
    for kind in (RIGHT, BOTTOM, CORNER):
        attend_back_window(kind, OFFS[kind], *refs)
    stores[2].start()
    up_p[...] = nn(nt(dproj[...], att_ref[...]).astype(BF), gb_ref[...])
    down_p[...] = nn(nt(uproj[...], gb_ref[...]).astype(BF), att_ref[...])
    loads[-1].wait()
    up_q[...] = nn(nt(dqkv[...], hid_ref[...]).astype(BF), gqkv_ref[...])
    down_q[...] = nn(nt(uqkv[...], gqkv_ref[...]).astype(BF), hid_ref[...])
    for store in stores:
        store.wait()


def attention_back(gmid, hid, qkvs, atts, exps, invs, wproj, rel, shift, keys, dqkv, uqkv, dproj, uproj):
    s = lambda *shape, dtype=F32: jax.ShapeDtypeStruct(shape, dtype)
    return pl.pallas_call(
        attention_back_kernel,
        out_shape=(s(ROWS, 3 * D, dtype=BF), s(RANK, D), s(RANK, 3 * D), s(RANK, D), s(RANK, D)),
        in_specs=[hbm()] * 14 + [vm()] * 8,
        out_specs=[hbm()] + [vm()] * 4,
        scratch_shapes=[
            pltpu.VMEM((ROWS, D), F32), pltpu.VMEM((ROWS, D), BF), pltpu.VMEM((ROWS, 3 * D), BF),
            pltpu.VMEM((ROWS, D), BF), pltpu.VMEM((D // HD, ROWS, KEYS), BF), pltpu.VMEM((ROWS, D), F32),
            pltpu.VMEM((ROWS, 3 * D), BF), pltpu.VMEM((ROWS, D), BF), pltpu.VMEM((ROWS, D), BF),
            pltpu.SemaphoreType.DMA((14,)), pltpu.SemaphoreType.DMA((3,)),
        ],
        compiler_params=params(52),
        cost_estimate=cost(28),
        name="attention_backward",
    )(gmid, hid, *qkvs, *atts, *exps, *invs, wproj, rel, shift, keys, dqkv, uqkv, dproj, uproj)


def token_grad_kernel(gmid_hbm, x_hbm, gqkv_hbm, gain_ref, wqkv_ref, o0, o1, o2,
                      gmid_ref, x_ref, gqkv_ref, gh_ref, out_rows, sem, *, low, high):
    span = pl.ds(low, high - low)
    copies = [
        pltpu.make_async_copy(src.at[span, :], dst, sem.at[i])
        for i, (src, dst) in enumerate(((gqkv_hbm, gqkv_ref), (x_hbm, x_ref), (gmid_hbm, gmid_ref)))
    ]
    for copy in copies:
        copy.start()
    copies[0].wait()
    gh_ref[...] = nt(gqkv_ref[...], wqkv_ref[...])
    copies[1].wait()
    copies[2].wait()
    gain = gain_ref[...]
    step = (high - low) // 2

    def norm_step(i, carry):
        rows = pl.ds(pl.multiple_of(i * step, 16), step)
        normed, inv_std = normalize(x_ref[rows, :].astype(F32))
        back = norm_back(gh_ref[rows, :] * gain, normed, inv_std)
        out_rows[rows, :] = (gmid_ref[rows, :] + back).astype(BF)
        return carry

    lax.fori_loop(0, 2, norm_step, 0)
    split_pieces(out_rows, (o0, o1, o2))


def token_grad(gmid, x, gqkv, gain, wqkv, low, high):
    count = high - low
    return pl.pallas_call(
        functools.partial(token_grad_kernel, low=low, high=high),
        out_shape=pieces_of(count),
        in_specs=[hbm(), hbm(), hbm(), vm(), vm()],
        out_specs=[vm()] * 3,
        scratch_shapes=[
            pltpu.VMEM((count, D), F32), pltpu.VMEM((count, D), BF), pltpu.VMEM((count, 3 * D), BF),
            pltpu.VMEM((count, D), F32), pltpu.VMEM((count, D), BF), pltpu.SemaphoreType.DMA((3,)),
        ],
        compiler_params=params(28),
        cost_estimate=cost(8),
        name="token_gradient",
    )(gmid, x, gqkv, gain, wqkv)


def grad_pack_kernel(where_ref, down_q, up_q, down_p, up_p, down1, up1, down2, up2, o0, o1, o2, o3, buf_ref):
    mine = where_ref[0]
    for k in range(4):
        for i, ref in enumerate((down_q, down1, up_p, up2)):
            buf_ref[k, :RANK, QUART * i : QUART * (i + 1)] = ref[:, QUART * k : QUART * (k + 1)]
    for dest in range(4):
        k = jnp.bitwise_xor(mine, dest)
        ranks = slice(RANK // 4 * dest, RANK // 4 * (dest + 1))
        for j in range(4):
            base = RANK + 12 * j
            for t in range(3):
                buf_ref[k, base : base + 4, QUART * t : QUART * (t + 1)] = up_q[
                    ranks, D * t + QUART * j : D * t + QUART * (j + 1)
                ]
            buf_ref[k, base : base + 4, 3 * QUART :] = down_p[ranks, QUART * j : QUART * (j + 1)]
            buf_ref[k, base + 4 : base + 8, :] = up1[ranks, D * j : D * (j + 1)]
            buf_ref[k, base + 8 : base + 12, :] = down2[ranks, D * j : D * (j + 1)]
    for k, out in enumerate((o0, o1, o2, o3)):
        out[...] = buf_ref[k].astype(BF)


def grad_pack(where, *grads):
    return pl.pallas_call(
        grad_pack_kernel,
        out_shape=(jax.ShapeDtypeStruct((4 * RANK, D), BF),) * 4,
        in_specs=[sm()] + [vm()] * 8,
        out_specs=[vm()] * 4,
        scratch_shapes=[pltpu.VMEM((4, 4 * RANK, D), F32)],
        compiler_params=params(8),
        cost_estimate=cost(2),
        name="adapter_grad_pack",
    )(where, *grads)


def grad_sum_kernel(g0, g1, g2, g3, o0, o1, o2, o3, buf_ref):
    total = g0[...].astype(F32) + g1[...].astype(F32) + g2[...].astype(F32) + g3[...].astype(F32)
    buf_ref[...] = jnp.zeros_like(buf_ref)
    buf_ref[:RANK, :] = total[:RANK, :]
    for j, out in enumerate((o0, o1, o2, o3)):
        buf_ref[RANK : RANK + 12, :] = total[RANK + 12 * j : RANK + 12 * (j + 1), :]
        out[...] = buf_ref[...].astype(BF)


def grad_sum(pieces):
    return pl.pallas_call(
        grad_sum_kernel,
        out_shape=(jax.ShapeDtypeStruct((2 * RANK, D), BF),) * 4,
        in_specs=[vm()] * 4,
        out_specs=[vm()] * 4,
        scratch_shapes=[pltpu.VMEM((2 * RANK, D), F32)],
        compiler_params=params(4),
        cost_estimate=cost(2),
        name="adapter_grad_sum",
    )(*pieces)


def grad_adapters_kernel(index_ref, x_ref, qkv_dn, fc1_dn, proj_up, fc2_up, rest_ref, acc_ref):
    acc_ref[...] = jnp.zeros_like(acc_ref)

    def add(i, carry):
        acc_ref[index_ref[i]] += x_ref[i].astype(F32)
        return carry

    lax.fori_loop(0, x_ref.shape[0], add, 0)
    for i, ref in enumerate((qkv_dn, fc1_dn, proj_up, fc2_up)):
        ref[...] = acc_ref[:, :RANK, QUART * i : QUART * (i + 1)]
    rest_ref[...] = acc_ref[:, RANK:, :].astype(BF)


def grad_adapters(index, x):
    s = lambda n, dtype=F32: jax.ShapeDtypeStruct((ADAPT, RANK, n), dtype)
    return pl.pallas_call(
        grad_adapters_kernel,
        out_shape=(s(QUART), s(QUART), s(QUART), s(QUART), s(D, BF)),
        in_specs=[sm(), vm()],
        out_specs=[vm()] * 5,
        scratch_shapes=[pltpu.VMEM((ADAPT, 2 * RANK, D), F32)],
        compiler_params=params(8),
        cost_estimate=cost(2),
        name="adapter_grad_by_adapter",
    )(index, x)


def grad_join_kernel(where_ref, r0, r1, r2, r3, qkv_up, proj_dn, fc1_up, fc2_dn, buf_ref):
    mine = where_ref[0]
    heads = qkv_up.shape[2] // (3 * HD)
    for k, ref in enumerate((r0, r1, r2, r3)):
        buf_ref[jnp.bitwise_xor(mine, k)] = ref[...].astype(F32)
    for source in range(4):
        ranks = slice(RANK // 4 * source, RANK // 4 * (source + 1))
        for h in range(heads):
            for t in range(3):
                qkv_up[:, ranks, HD * (3 * h + t) : HD * (3 * h + t + 1)] = buf_ref[
                    source, :, 0:4, QUART * t + HD * h : QUART * t + HD * (h + 1)
                ]
        proj_dn[:, ranks, :] = buf_ref[source, :, 0:4, 3 * QUART :]
        fc1_up[:, ranks, :] = buf_ref[source, :, 4:8, :]
        fc2_dn[:, ranks, :] = buf_ref[source, :, 8:12, :]


def grad_join(where, pieces):
    s = lambda n: jax.ShapeDtypeStruct((ADAPT, RANK, n), F32)
    return pl.pallas_call(
        grad_join_kernel,
        out_shape=(s(3 * QUART), s(QUART), s(D), s(D)),
        in_specs=[sm()] + [vm()] * 4,
        out_specs=[vm()] * 4,
        scratch_shapes=[pltpu.VMEM((4, ADAPT, RANK, D), F32)],
        compiler_params=params(12),
        cost_estimate=cost(2),
        name="adapter_grad_join",
    )(where, *pieces)


def flip(values, axis, distance):
    size = lax.axis_size(axis)
    return lax.ppermute(values, axis, [(i, i ^ distance) for i in range(size)])


def send_rows(pieces, *deps):
    own, near, pair = pieces
    if deps:
        near, = after((near,), *deps)
    return [own, flip(near, "row", 1), flip(pair, "row", 2)]


def hand_on(pieces, *deps):
    own, near, crossed = pieces
    if deps:
        near, crossed = after((near, crossed), *deps)
    return [own, near, crossed, flip(crossed, "row", 1)]


def exchange(slots, axis):
    return [slots[0]] + [flip(slots[k], axis, k) for k in range(1, 4)]


def after(values, *deps):
    return lax.optimization_barrier((tuple(values), deps))[0]


def col_halves(half):
    return jnp.concatenate([flip(half, "col", j) for j in range(1, 4)], axis=0)


def col_pairs(half, other_row):
    two = jnp.concatenate([half, other_row], axis=0)
    return jnp.concatenate([other_row] + [flip(two, "col", j) for j in range(1, 4)], axis=0)


def body(
    tokens, grad_out, adapter_index, norm1_gain, norm2_gain, qkv_weight, proj_weight, fc1_weight, fc2_weight,
    rel_h, rel_w, qkv_down, qkv_up, proj_down, proj_up, fc1_down, fc1_up, fc2_down, fc2_up,
):
    members = lax.axis_size("col")
    batches = lax.axis_size("dp")
    row_index, col_index, dp_index = lax.axis_index("row"), lax.axis_index("col"), lax.axis_index("dp")
    half = dp_index % 2
    where = jnp.stack([row_index, half]).astype(jnp.int32)
    slot_images = (
        jnp.bitwise_xor(dp_index, jnp.arange(batches, dtype=jnp.int32))[:, None] * members
        + jnp.bitwise_xor(col_index, jnp.arange(members, dtype=jnp.int32))[None, :]
    ).reshape(-1)
    slot_adapters = jnp.sum(
        jnp.where(
            slot_images[:, None] == jnp.arange(adapter_index.shape[0], dtype=jnp.int32)[None, :],
            adapter_index[:, 0][None, :],
            0,
        ),
        axis=1,
    )
    pick = jnp.concatenate([slot_adapters[:4], half[None]]).astype(jnp.int32)
    swap = lambda m: jnp.swapaxes(m, 1, 2)

    shift, keys = jnp.asarray(SHIFT_NP), jnp.asarray(KEYS_NP)

    *token_slots, alpha_own, beta_own, alpha_half, cross, fc1_half, fc2_half = front(
        where, tokens, qkv_weight, proj_weight, fc1_weight, fc2_weight
    )
    crossed = flip(cross, "row", 2)
    beta_half, b0 = cross[:HBLK], crossed[:HBLK]
    c0 = jnp.concatenate([crossed[HBLK : 2 * HBLK], crossed[2 * HBLK :]], axis=1)
    alpha_near = col_halves(alpha_half)
    x_pieces = send_rows(token_slots, crossed)
    *send, row_adapters, rel = adapter_pack(
        pick, qkv_up, swap(proj_down), fc1_up, swap(fc2_down), swap(qkv_down), swap(fc1_down), proj_up, fc2_up,
        norm1_gain.reshape(1, -1), norm2_gain.reshape(1, -1), rel_h, rel_w,
    )
    beta_sent = [jnp.concatenate([beta_half, b0, send[j]], axis=0) for j in range(1, 4)]
    beta_got = [flip(m, "col", j) for j, m in enumerate(beta_sent, 1)]
    alpha_near, x_pieces[1] = after((alpha_near, x_pieces[1]))
    alpha_far = flip(alpha_near, "dp", 1)
    g = jnp.concatenate([alpha_own, alpha_near, alpha_far, row_adapters], axis=0)
    g, *x_pieces = after((g, *x_pieces))
    gy = flip(g, "row", 2)
    grad_slots = pack(where, grad_out)
    *beta_got, _ = after((*beta_got, grad_slots[0]))
    beta_near = jnp.concatenate([b0] + [m[:QUART] for m in beta_got], axis=0)
    col_adapters = [send[0]] + beta_got
    beta_far = flip(beta_near, "dp", 1)
    x_pieces = hand_on(x_pieces)

    g1, own1, near1 = (flip(m, "row", 1) for m in (g, beta_own, beta_near))
    fc1_half, = after((fc1_half,), g1, own1, near1, x_pieces[3])
    fc1_near = [flip(fc1_half, "col", j) for j in range(1, 4)]
    gy, beta_far, fc2_half, c0 = after((gy, beta_far, fc2_half, c0), *fc1_near)
    fc2_two = jnp.concatenate([fc2_half, c0], axis=0)
    fc2_near = [flip(fc2_two, "col", j) for j in range(1, 4)]
    gy1, far1 = flip(gy, "row", 1), flip(beta_far, "row", 1)
    *grad_slots, fc1_near = after((*grad_slots, jnp.concatenate(fc1_near, axis=0)), gy1, far1)
    fc1_far = flip(fc1_near, "dp", 1)
    g_pieces = send_rows(grad_slots, fc2_near[0], fc2_near[1], fc2_near[2])
    wqkv, wproj, dqkv, uqkv, dproj, uproj, d1, u1, d2, u2, gain1, gain2 = prep1(
        where, (g, g1, gy, gy1), (beta_own, beta_near, beta_far, own1, near1, far1), col_adapters
    )
    h = jnp.concatenate([fc1_weight, fc1_near, fc1_far], axis=0)
    wqkv, h = after((wqkv, h), g_pieces[2])
    hy = flip(h, "row", 2)
    x, hid, *qkvs = qkv_rows(x_pieces, gain1, wqkv)
    *qkvs, n1, n2, n3 = after((*qkvs, *fc2_near))
    fc2_near = jnp.concatenate([c0, n1, n2, n3], axis=0)
    fc2_far = flip(fc2_near, "dp", 1)
    fc2_ahead = [flip(m, "row", 1) for m in (fc2_weight, fc2_near)]
    part0 = attention(0, qkvs[0], rel, shift, keys)
    qkv1, = after((qkvs[1],), part0[0], *fc2_ahead)
    part1 = attention(1, qkv1, rel, shift, keys)
    g_pieces = hand_on(g_pieces, part1[0])
    qkv2, _ = after((qkvs[2], part1[0]))
    part2 = attention(2, qkv2, rel, shift, keys)
    atts, exps, invs = zip(part0, part1, part2)
    atts = list(atts)
    atts[2], hy = after((atts[2], hy))
    alpha2 = [h, flip(h, "row", 1), hy, flip(hy, "row", 1)]
    middle = project(x, atts, wproj)
    middle, fc2_far = after((middle, fc2_far))
    beta2 = [fc2_weight, fc2_near, fc2_far, *fc2_ahead, flip(fc2_far, "row", 1)]

    *out_slots, gmid, down1, up1, down2, up2 = mlp(where, middle, g_pieces, gain2, alpha2, beta2, d1, u1, d2, u2)
    out_pieces = send_rows(out_slots)
    gqkv, down_q, up_q, down_p, up_p = attention_back(
        gmid, hid, qkvs, atts, exps, invs, wproj, rel, shift, keys, dqkv, uqkv, dproj, uproj
    )
    out_pieces = hand_on(out_pieces, gqkv)
    gqkv, down_q, up_q, down_p, up_p = after((gqkv, down_q, up_q, down_p, up_p), *out_pieces[:3])
    packed = grad_pack(where, down_q, up_q, down_p, up_p, down1, up1, down2, up2)
    *packed, gqkv = after((*packed, gqkv))
    row_sums = exchange(packed, "row")
    back0 = token_grad(gmid, x, gqkv, gain1, wqkv, *TAIL[0])
    *row_sums, gqkv, b0, b1, b2 = after((*row_sums, gqkv, *back0))
    back_pieces = send_rows((b0, b1, b2))
    summed = grad_sum(row_sums)
    *summed, gqkv = after((*summed, gqkv))
    images = exchange(summed, "col")
    back1 = token_grad(gmid, x, gqkv, gain1, wqkv, *TAIL[1])
    last_pieces = send_rows(back1)
    *images, near, crossed = after((*images, *back_pieces[1:]), back1[0])
    back_pieces = hand_on([back_pieces[0], near, crossed])
    images = jnp.stack(images)
    images, *out_pieces = after((images, *out_pieces))
    step = 1
    while step < batches:
        images = jnp.concatenate([images, flip(images, "dp", step)], axis=0)
        step *= 2
    result = unpack(where, out_pieces, BF)
    images, = after((images,), result)
    qkv_dn, fc1_dn, proj_upg, fc2_upg, rest = grad_adapters(slot_adapters.astype(jnp.int32), images)
    rests = [rest] + [flip(rest, "row", k) for k in range(1, 4)]
    grad_tokens = unpack(where, back_pieces + hand_on(last_pieces, rest), F32, TAIL)
    rests = after(tuple(rests), grad_tokens)
    qkv_upg, proj_dn, fc1_upg, fc2_dn = grad_join(where, rests)
    return (
        result, grad_tokens,
        swap(qkv_dn), qkv_upg, swap(proj_dn), proj_upg, swap(fc1_dn), fc1_upg, swap(fc2_dn), fc2_upg,
    )


def solution(mesh):
    return jax.shard_map(
        body,
        mesh=mesh,
        in_specs=(
            P("row", ("dp", "col")), P("row", ("dp", "col")), P(), P("row"), P("row"),
            P("row", "col"), P("col", "row"), P("row", "col"), P("row", "col"), P(), P(),
            P(None, "row", None), P(None, None, "col"), P(None, "col", None), P(None, None, "row"),
            P(None, "row", None), P(None, None, "col"), P(None, "col", None), P(None, None, "row"),
        ),
        out_specs=(
            P("row", ("dp", "col")), P("row", ("dp", "col")),
            P(None, "row", None), P(None, None, "col"), P(None, "col", None), P(None, None, "row"),
            P(None, "row", None), P(None, None, "col"), P(None, "col", None), P(None, None, "row"),
        ),
        check_vma=False,
    )
```

```python
import functools

import jax
import jax.numpy as jnp
import numpy as np
from jax import lax
from jax.experimental import pallas as pl
from jax.experimental.pallas import tpu as pltpu
from jax.sharding import PartitionSpec as P

D = 768
HD = 64
WIN = 14
SLOTS = WIN * WIN
SIDE = 64
ADAPT = 8
NWIN = 5
IMG_TOK = NWIN * NWIN * SLOTS
RANK = 16
EDGE = SIDE - (NWIN - 1) * WIN
QUART = D // 4
FULLR = 208
KEYS = 208
EDGER = EDGE * WIN
CORNR = EDGE * EDGE
ROWS = 4 * FULLR + 2 * EDGER + CORNR
HALF = ROWS // 2
HBLK = QUART // 2
EPSILON = 1e-06
BF = jnp.bfloat16
F32 = jnp.float32

FULL, RIGHT, BOTTOM, CORNER = 0, 1, 2, 3
NQ = (FULLR, EDGER, EDGER, CORNR)
OFFS = (0, 4 * FULLR, 4 * FULLR + EDGER, 4 * FULLR + 2 * EDGER)


def slot_order(kind):
    rows = EDGE if kind in (BOTTOM, CORNER) else WIN
    cols = EDGE if kind in (RIGHT, CORNER) else WIN
    kept = [a * WIN + b for a in range(rows) for b in range(cols)]
    rest = [s for s in range(SLOTS) if s not in set(kept)]
    return kept, kept + rest


def build_tables():
    shift = np.zeros((4, FULLR, 128), np.int32)
    keys = np.zeros((4, KEYS, 128), np.float32)
    for kind in range(4):
        kept, order = slot_order(kind)
        for i, s in enumerate(kept):
            for base in (0, 64):
                shift[kind, i, base : base + 32] = WIN - 1 - s // WIN
                shift[kind, i, base + 32 : base + 64] = WIN - 1 - s % WIN
        spare = order[0] if kind == FULL else order[-1]
        for i, s in enumerate(order + [spare] * (KEYS - SLOTS)):
            for base in (0, 64):
                keys[kind, i, base + s // WIN] = 1.0
                keys[kind, i, base + 32 + s % WIN] = 1.0
    return shift, keys.astype(jnp.bfloat16)


SHIFT_NP, KEYS_NP = build_tables()


def nn(a, b):
    return jnp.dot(a, b, preferred_element_type=F32)


def nt(a, b):
    return lax.dot_general(a, b, (((1,), (1,)), ((), ())), preferred_element_type=F32)


def tn(a, b):
    return lax.dot_general(a, b, (((0,), (0,)), ((), ())), preferred_element_type=F32)


def vm():
    return pl.BlockSpec(memory_space=pltpu.VMEM)


def hbm():
    return pl.BlockSpec(memory_space=pl.ANY)


def in_hbm(x):
    return pltpu.with_memory_space_constraint(x, pltpu.HBM)


def arg():
    return pl.BlockSpec(memory_space=pltpu.HBM)


def sm():
    return pl.BlockSpec(memory_space=pltpu.SMEM)


def params(mib=60):
    return pltpu.CompilerParams(vmem_limit_bytes=mib * 1024 * 1024)


def cost(us):
    return pl.CostEstimate(flops=int(us * 1e6), transcendentals=0, bytes_accessed=0)


def place_window(kind, count, moved, width, spare=-100000):
    row = lax.broadcasted_iota(jnp.int32, (count, width), 0)
    lane = lax.broadcasted_iota(jnp.int32, (count, width), 1)
    if kind in (RIGHT, CORNER):
        src = (row // EDGE) * WIN + row % EDGE
    else:
        src = jnp.where(row < SLOTS, row, spare)
    return (lane == src + moved).astype(F32).astype(BF)


def window_list(dest):
    items = [(FULL, FULLR * j, NWIN * dest + j) for j in range(4)]
    items.append((RIGHT, OFFS[1], NWIN * dest + 4))
    items.append((BOTTOM, OFFS[2], NWIN * 4 + dest))
    if dest == 3:
        items.append((CORNER, OFFS[3], NWIN * NWIN - 1))
    return items


def window_span(window):
    start = window * SLOTS
    low = start // 128 * 128
    high = min(-(-(start + SLOTS) // 128) * 128, IMG_TOK)
    return low, high, start - low


def pack_rows(mine, x_ref, rows_ref, spare):
    for dest in range(4):
        slot = jnp.bitwise_xor(mine, dest)
        if dest != 3:
            rows_ref[slot, OFFS[3] :, :] = jnp.zeros((CORNR, QUART), BF)
        for kind, offset, window in window_list(dest):
            low, high, moved = window_span(window)
            pick = place_window(kind, NQ[kind], moved, high - low, spare)
            rows_ref[slot, offset : offset + NQ[kind], :] = nt(pick, x_ref[:, low:high]).astype(BF)


def fold(rows_ref, outs):
    half = rows_ref.shape[1] // 2
    for slot, (out, base) in enumerate(((outs[0], 0), (outs[1], 0), (outs[2], 0), (outs[2], half))):
        out[base : base + half, :QUART] = rows_ref[slot, :half, :]
        out[base : base + half, QUART:] = rows_ref[slot, half:, :]


def pack_kernel(where_ref, x_hbm, o0, o1, o2, rows_ref, x_ref, sem):
    load = pltpu.make_async_copy(x_hbm, x_ref, sem)
    load.start()
    load.wait()
    pack_rows(where_ref[0], x_ref, rows_ref, -100000)
    fold(rows_ref, (o0, o1, o2))


def pieces_of(rows):
    piece = lambda n: jax.ShapeDtypeStruct((n, 2 * QUART), BF)
    return (piece(rows // 2), piece(rows // 2), piece(rows))


def pack(where, x):
    return pl.pallas_call(
        pack_kernel,
        out_shape=pieces_of(ROWS),
        in_specs=[sm(), arg()],
        out_specs=[vm()] * 3,
        scratch_shapes=[
            pltpu.VMEM((4, ROWS, QUART), BF), pltpu.VMEM((QUART, IMG_TOK), BF), pltpu.SemaphoreType.DMA,
        ],
        compiler_params=params(16),
        cost_estimate=cost(4),
        name="pack",
    )(where, in_hbm(x))


def front_kernel(
    where_ref, x_hbm, qkv_hbm, proj_hbm, fc1_hbm, fc2_hbm,
    o0, o1, o2, alpha_ref, beta_ref, alpha_half, cross_ref, fc1_half, fc2_half,
    rows_ref, x_ref, qkv_w, proj_w, sem,
):
    rows = pl.ds(pl.multiple_of(where_ref[1] * HBLK, 32), HBLK)
    loads = [
        pltpu.make_async_copy(src, dst, sem.at[i])
        for i, (src, dst) in enumerate(
            (
                (qkv_hbm, qkv_w), (proj_hbm, proj_w), (fc2_hbm.at[rows, :], fc2_half),
                (fc1_hbm.at[rows, :], fc1_half), (x_hbm, x_ref),
            )
        )
    ]
    for load in loads:
        load.start()
    for load in loads[:4]:
        load.wait()
    heads = qkv_w.shape[1] // (3 * HD)
    for h in range(heads):
        for t in range(3):
            ref, base = (alpha_ref, QUART * t) if t < 2 else (beta_ref, 0)
            ref[:, base + HD * h : base + HD * (h + 1)] = qkv_w[:, HD * (3 * h + t) : HD * (3 * h + t + 1)]
    beta_ref[:, QUART:] = proj_w[...]
    alpha_half[...] = alpha_ref[rows, :]
    cross_ref[:HBLK, :] = beta_ref[rows, :]
    cross_ref[HBLK : 2 * HBLK, :] = fc2_half[:, : 2 * QUART]
    cross_ref[2 * HBLK :, :] = fc2_half[:, 2 * QUART :]
    loads[4].wait()
    pack_rows(where_ref[0], x_ref, rows_ref, 0)
    fold(rows_ref, (o0, o1, o2))


def front(where, x, qkv_w, proj_w, fc1_w, fc2_w):
    s = lambda *shape: jax.ShapeDtypeStruct(shape, BF)
    return pl.pallas_call(
        front_kernel,
        out_shape=pieces_of(ROWS)
        + (
            s(QUART, 2 * QUART), s(QUART, 2 * QUART), s(HBLK, 2 * QUART), s(3 * HBLK, 2 * QUART),
            s(HBLK, D), s(HBLK, D),
        ),
        in_specs=[sm()] + [arg()] * 5,
        out_specs=[vm()] * 9,
        scratch_shapes=[
            pltpu.VMEM((4, ROWS, QUART), BF), pltpu.VMEM((QUART, IMG_TOK), BF),
            pltpu.VMEM(qkv_w.shape, BF), pltpu.VMEM(proj_w.shape, BF), pltpu.SemaphoreType.DMA((5,)),
        ],
        compiler_params=params(16),
        cost_estimate=cost(5),
        name="token_and_weight_pack",
    )(where, *(in_hbm(m) for m in (x, qkv_w, proj_w, fc1_w, fc2_w)))


def unpack_kernel(where_ref, *refs, bounds):
    pieces, (out_ref, acc_ref, rows_ref) = refs[:-3], refs[-3:]
    mine = where_ref[0]
    acc_ref[...] = jnp.zeros_like(acc_ref)
    index = 0
    for low, high in bounds:
        half = (high - low) // 2
        for slot in range(4):
            piece = pieces[index]
            rows = slice(half, 2 * half) if slot == 3 else slice(0, half)
            rows_ref[slot, low : low + half, :] = piece[rows, :QUART]
            rows_ref[slot, low + half : high, :] = piece[rows, QUART:]
            index += 1

    for source in range(4):
        slot = jnp.bitwise_xor(mine, source)
        for kind, offset, window in window_list(source):
            low, high, moved = window_span(window)
            pick = place_window(kind, NQ[kind], moved, high - low)
            acc_ref[:, low:high] += tn(rows_ref[slot, offset : offset + NQ[kind], :], pick)
    out_ref[...] = acc_ref[:, :IMG_TOK].astype(out_ref.dtype)


def unpack(where, pieces, dtype, bounds=((0, ROWS),)):
    return pl.pallas_call(
        functools.partial(unpack_kernel, bounds=bounds),
        out_shape=jax.ShapeDtypeStruct((QUART, IMG_TOK), dtype),
        in_specs=[sm()] + [vm()] * len(pieces),
        out_specs=vm(),
        scratch_shapes=[
            pltpu.VMEM((QUART, -(-IMG_TOK // 128) * 128), F32),
            pltpu.VMEM((4, ROWS, QUART), BF),
        ],
        compiler_params=params(24),
        cost_estimate=cost(4),
        name="unpack",
    )(where, *pieces)


def join_pieces(pieces, dst_ref):
    for slot, piece in enumerate(pieces):
        rows = slice(HALF, ROWS) if slot == 3 else slice(0, HALF)
        dst_ref[:HALF, QUART * slot : QUART * (slot + 1)] = piece[rows, :QUART]
        dst_ref[HALF:, QUART * slot : QUART * (slot + 1)] = piece[rows, QUART:]


def split_pieces(src_ref, outs):
    half = src_ref.shape[0] // 2
    for slot, (out, base) in enumerate(((outs[0], 0), (outs[1], 0), (outs[2], 0), (outs[2], half))):
        out[base : base + half, :QUART] = src_ref[:half, QUART * slot : QUART * (slot + 1)]
        out[base : base + half, QUART:] = src_ref[half:, QUART * slot : QUART * (slot + 1)]


def adapter_pack_kernel(
    pick_ref, qkv_up_hbm, proj_dn_hbm, fc1_up_hbm, fc2_dn_hbm, qkv_dn_hbm, fc1_dn_hbm, proj_up_hbm, fc2_up_hbm,
    gain1, gain2, rel_h, rel_w, s0, s1, s2, s3, row_ref, rel_ref,
    qkv_up, proj_dn, fc1_up, fc2_dn, qkv_dn, fc1_dn, proj_up, fc2_up, sem,
):
    pairs = []
    for j in range(4):
        for src, dst in ((qkv_up_hbm, qkv_up), (proj_dn_hbm, proj_dn), (fc1_up_hbm, fc1_up), (fc2_dn_hbm, fc2_dn)):
            pairs.append((src.at[pick_ref[j]], dst.at[j]))
    for src, dst in ((qkv_dn_hbm, qkv_dn), (fc1_dn_hbm, fc1_dn), (proj_up_hbm, proj_up), (fc2_up_hbm, fc2_up)):
        pairs.append((src.at[pick_ref[0]], dst.at[0]))
    loads = [pltpu.make_async_copy(src, dst, sem.at[i]) for i, (src, dst) in enumerate(pairs)]
    for load in loads:
        load.start()
    offsets = rel_h.shape[0]
    reverse = (
        lax.broadcasted_iota(jnp.int32, (offsets, 32), 0) + lax.broadcasted_iota(jnp.int32, (offsets, 32), 1)
        == offsets - 1
    ).astype(F32).astype(BF)
    rel_ref[...] = jnp.zeros_like(rel_ref)
    for i, table in enumerate((rel_h, rel_w)):
        block = tn(table[...], reverse).astype(BF)
        rel_ref[:HD, HD + 32 * i : HD + 32 * (i + 1)] = block
        rel_ref[HD:, 32 * i : 32 * (i + 1)] = block
    for load in loads:
        load.wait()
    heads = qkv_up.shape[2] // (3 * HD)
    half = 2 * QUART
    for j, send_ref in enumerate((s0, s1, s2, s3)):
        for h in range(heads):
            for t in range(3):
                row, base = (0, QUART * t) if t < 2 else (RANK, 0)
                send_ref[row : row + RANK, base + HD * h : base + HD * (h + 1)] = qkv_up[
                    j, :, HD * (3 * h + t) : HD * (3 * h + t + 1)
                ]
        send_ref[RANK : 2 * RANK, QUART:] = proj_dn[j]
        for i, ref in enumerate((fc1_up, fc2_dn)):
            for part in range(2):
                row = RANK * (2 + 2 * i + part)
                send_ref[row : row + RANK, :] = ref[j, :, half * part : half * (part + 1)]
    for i, ref in enumerate((qkv_dn, fc1_dn, proj_up, fc2_up)):
        row, base = RANK * (i // 2), QUART * (i % 2)
        row_ref[row : row + RANK, base : base + QUART] = ref[0]
    for i, ref in enumerate((gain1, gain2)):
        row_ref[2 * RANK :, QUART * i : QUART * (i + 1)] = jnp.broadcast_to(ref[...], (RANK, QUART))


def adapter_pack(pick, *mats):
    s = lambda *shape: jax.ShapeDtypeStruct(shape, BF)
    return pl.pallas_call(
        adapter_pack_kernel,
        out_shape=(s(6 * RANK, 2 * QUART),) * 4 + (s(3 * RANK, 2 * QUART), s(128, 128)),
        in_specs=[sm()] + [arg()] * 8 + [vm()] * 4,
        out_specs=[vm()] * 6,
        scratch_shapes=[pltpu.VMEM((4,) + m.shape[1:], BF) for m in mats[:4]]
        + [pltpu.VMEM((1,) + m.shape[1:], BF) for m in mats[4:8]]
        + [pltpu.SemaphoreType.DMA((20,))],
        compiler_params=params(8),
        cost_estimate=cost(2),
        name="adapter_pack",
    )(pick, *(in_hbm(m) for m in mats[:8]), *mats[8:])


def alpha_block(k, j):
    part = k
    if j == 0:
        return [(part, 0, QUART, None)]
    return [
        (part, QUART + HBLK * (j - 1), HBLK, 0),
        (part, QUART + 3 * HBLK + HBLK * (j - 1), HBLK, 1),
    ]


def beta_block(k, j):
    core, cross = k % 2, k // 2
    base = 3 * core
    if j == 0 and not cross:
        return [(base, 0, QUART, None)]
    row = 0 if j == 0 else HBLK + QUART * (j - 1) + HBLK * cross
    return [(base + 1, row, HBLK, 0), (base + 2, row, HBLK, 1)]


def block_dst(start, flag, half):
    if flag is None:
        return start
    offset = half if flag == 0 else 1 - half
    return pl.multiple_of(start + offset * HBLK, 32)


def prep1_kernel(
    where_ref, p0, p1, p2, p3, q0, q1, q2, q3, q4, q5, a0, a1, a2, a3,
    wqkv_ref, wproj_ref, dqkv, uqkv, dproj, uproj, d1, u1, d2, u2, gain1, gain2, ups, downs,
):
    half = where_ref[1]
    for j, a in enumerate((a0, a1, a2, a3)):
        base = a.shape[0] - 6 * RANK
        part = lambda i: slice(base + RANK * i, base + RANK * (i + 1))
        for t in range(3):
            uqkv[:, D * t + QUART * j : D * t + QUART * (j + 1)] = a[
                part(t // 2), QUART * (t % 2) : QUART * (t % 2 + 1)
            ]
        dproj[:, QUART * j : QUART * (j + 1)] = a[part(1), QUART:]
        for i in range(2):
            u1[:, D * j + D // 2 * i : D * j + D // 2 * (i + 1)] = a[part(2 + i), :]
            d2[:, D * j + D // 2 * i : D * j + D // 2 * (i + 1)] = a[part(4 + i), :]
    for k, ref in enumerate((p0, p1, p2, p3)):
        for i, dst in enumerate((dqkv, d1, uproj, u2)):
            rows = slice(D + RANK * (i // 2), D + RANK * (i // 2 + 1))
            dst[:, QUART * k : QUART * (k + 1)] = ref[rows, QUART * (i % 2) : QUART * (i % 2 + 1)]
        for i, dst in enumerate((gain1, gain2)):
            row = D + 2 * RANK
            dst[:, QUART * k : QUART * (k + 1)] = ref[row : row + 1, QUART * i : QUART * (i + 1)].astype(F32)
    alpha, beta = (p0, p1, p2, p3), (q0, q1, q2, q3, q4, q5)
    for k in range(4):
        for j in range(4):
            for part, row, count, flag in alpha_block(k, j):
                rows = pl.ds(block_dst(QUART * k, flag, half), count)
                for t in range(2):
                    wqkv_ref[rows, D * t + QUART * j : D * t + QUART * (j + 1)] = alpha[part][
                        row : row + count, QUART * t : QUART * (t + 1)
                    ]
            for part, row, count, flag in beta_block(k, j):
                rows = pl.ds(block_dst(QUART * k, flag, half), count)
                wqkv_ref[rows, 2 * D + QUART * j : 2 * D + QUART * (j + 1)] = beta[part][
                    row : row + count, :QUART
                ]
                rows = pl.ds(block_dst(QUART * j, flag, half), count)
                wproj_ref[rows, QUART * k : QUART * (k + 1)] = beta[part][row : row + count, QUART:]
    for t in range(3):
        ups[t] = uqkv[:, D * t : D * (t + 1)]
    ups[3] = uproj[...]
    for k in range(4):
        downs[k] = dqkv[:, QUART * k : QUART * (k + 1)]
        downs[4 + k] = dproj[:, QUART * k : QUART * (k + 1)]

    def merge(t, carry):
        cols = pl.ds(pl.multiple_of(D * t, 128), D)
        for k in range(4):
            rows = slice(QUART * k, QUART * (k + 1))
            wqkv_ref[rows, cols] = (wqkv_ref[rows, cols].astype(F32) + tn(downs[k], ups[t])).astype(BF)
        return carry

    lax.fori_loop(0, 3, merge, 0)
    for k in range(4):
        rows = slice(QUART * k, QUART * (k + 1))
        wproj_ref[rows, :] = (wproj_ref[rows, :].astype(F32) + tn(downs[4 + k], ups[3])).astype(BF)


def prep1(where, alpha, beta, cols):
    s = lambda *shape: jax.ShapeDtypeStruct(shape, BF)
    return pl.pallas_call(
        prep1_kernel,
        out_shape=(
            s(D, 3 * D), s(D, D), s(RANK, D), s(RANK, 3 * D), s(RANK, D), s(RANK, D),
            s(RANK, D), s(RANK, 4 * D), s(RANK, 4 * D), s(RANK, D),
            jax.ShapeDtypeStruct((1, D), F32), jax.ShapeDtypeStruct((1, D), F32),
        ),
        in_specs=[sm()] + [vm()] * 14,
        out_specs=[vm()] * 12,
        scratch_shapes=[pltpu.VMEM((4, RANK, D), BF), pltpu.VMEM((8, RANK, QUART), BF)],
        compiler_params=params(24),
        cost_estimate=cost(7),
        name="attention_weights",
    )(where, *alpha, *beta, *cols)


def normalize(values):
    center = jnp.sum(values, axis=1, keepdims=True) / D
    shifted = values - center
    inv_std = lax.rsqrt(jnp.sum(shifted * shifted, axis=1, keepdims=True) / D + EPSILON)
    return shifted * inv_std, inv_std


def norm_back(grad, normed, inv_std):
    first = jnp.sum(grad, axis=1, keepdims=True) / D
    second = jnp.sum(grad * normed, axis=1, keepdims=True) / D
    return inv_std * (grad - first - normed * second)


def barrel(values, amount, left):
    for bit in (1, 2, 4, 8):
        moved = pltpu.roll(values, (128 - bit) if left else bit, 1)
        values = jnp.where((amount & bit) != 0, moved, values)
    return values


def low_half(count):
    return lax.broadcasted_iota(jnp.int32, (count, 128), 1) < HD


def pad_rows(tile):
    if tile.shape[0] == KEYS:
        return tile
    return jnp.concatenate([tile, jnp.zeros((KEYS - tile.shape[0], tile.shape[1]), tile.dtype)], axis=0)


def live_rows():
    return lax.broadcasted_iota(jnp.int32, (KEYS, 128), 0) < SLOTS


GROUP = 6
GROUP_BACK = 6


def pair_columns(pair):
    return tuple(slice(D * t + 128 * pair, D * t + 128 * (pair + 1)) for t in range(3))


def attend_window(kind, row0, qkv_ref, att_ref, exp_ref, inv_ref, rel_ref, shift_ref, keys_ref):
    count = NQ[kind]
    rows = pl.ds(row0, count)
    low_q, low_k = low_half(count), low_half(KEYS)
    live = live_rows()
    ones = jnp.where(live, 1.0, 0.0).astype(BF)
    amount = shift_ref[kind, :count, :]
    onehot = keys_ref[kind]
    rel_mat = rel_ref[...]
    for first in range(0, D // 128, GROUP):
        pairs = range(first, first + GROUP)
        heads = [(pair, odd) for pair in pairs for odd in range(2)]
        q_tile = {p: qkv_ref[rows, pair_columns(p)[0]] for p in pairs}
        rel = {p: nn(q_tile[p], rel_mat) for p in pairs}
        rel = {p: barrel(rel[p], amount, True).astype(BF) for p in pairs}
        k_tile = {p: pad_rows(qkv_ref[rows, pair_columns(p)[1]] * BF(HD**-0.5)) for p in pairs}
        scores = {}
        for p, odd in heads:
            if odd:
                q_aug, k_aug = jnp.where(low_q, rel[p], q_tile[p]), jnp.where(low_k, onehot, k_tile[p])
            else:
                q_aug, k_aug = jnp.where(low_q, q_tile[p], rel[p]), jnp.where(low_k, k_tile[p], onehot)
            scores[p, odd] = nt(q_aug, k_aug)
        top = {h: jnp.max(scores[h], axis=1, keepdims=True) for h in heads}
        exponent = {h: jnp.exp(scores[h] - top[h]).astype(BF) for h in heads}
        both = {}
        for p, odd in heads:
            exp_ref[2 * p + odd, rows, :] = exponent[p, odd]
            v_tile = pad_rows(qkv_ref[rows, pair_columns(p)[2]])
            if kind == FULL:
                v_tile = jnp.where(live, v_tile, 0).astype(BF)
            v_aug = jnp.where(low_k, ones, v_tile) if odd else jnp.where(low_k, v_tile, ones)
            both[p, odd] = nn(exponent[p, odd], v_aug)
        for p in pairs:
            cols = pair_columns(p)[0]
            inverse = 1.0 / pltpu.roll(jnp.where(low_q, both[p, 1], both[p, 0]), HD, 1)
            inv_ref[rows, cols] = inverse
            att_ref[rows, cols] = (jnp.where(low_q, both[p, 0], both[p, 1]) * inverse).astype(BF)


PARTS = ((FULL, FULL), (FULL, FULL), (RIGHT, BOTTOM, CORNER))
PART_ROWS = tuple(sum(NQ[kind] for kind in part) for part in PARTS)
PART_OFFS = (0, PART_ROWS[0], PART_ROWS[0] + PART_ROWS[1])


TAIL = ((0, 576), (576, ROWS))


def qkv_kernel(
    x0, x1, x2, x3, gain_ref, w_hbm, x_hbm, hid_hbm, qkv_a, qkv_b, qkv_c,
    x_ref, hid_ref, rows_ref, w_ref, qkv_ref, sem, out_sem,
):
    loads = [
        pltpu.make_async_copy(w_hbm.at[:, D * t : D * (t + 1)], w_ref.at[t], sem.at[t]) for t in range(3)
    ]
    for load in loads:
        load.start()
    join_pieces((x0, x1, x2, x3), x_ref)
    kept = [
        pltpu.make_async_copy(src, dst, sem.at[3 + i])
        for i, (src, dst) in enumerate(((x_ref, x_hbm), (hid_ref, hid_hbm)))
    ]
    kept[0].start()
    gain = gain_ref[...]

    def norm_step(i, carry):
        rows = pl.ds(pl.multiple_of(i * 112, 16), 112)
        normed, _ = normalize(x_ref[rows, :].astype(F32))
        hidden = (normed * gain).astype(BF)
        rows_ref[rows, :] = hidden
        hid_ref[rows, :] = hidden
        return carry

    lax.fori_loop(0, ROWS // 112, norm_step, 0)
    for w in range(4):
        hid_ref[FULLR * w + SLOTS : FULLR * (w + 1), :] = jnp.zeros((FULLR - SLOTS, D), BF)
    kept[1].start()
    for load in loads:
        load.wait()

    def stores(t):
        cols = pl.ds(pl.multiple_of(D * t, 128), D)
        return [
            pltpu.make_async_copy(
                qkv_ref.at[t, pl.ds(offset, count), :], out.at[:, cols], out_sem.at[t, i]
            )
            for i, (out, offset, count) in enumerate(zip((qkv_a, qkv_b, qkv_c), PART_OFFS, PART_ROWS))
        ]

    def project_step(t, carry):
        qkv_ref[t] = nn(rows_ref[...], w_ref[t]).astype(BF)
        for store in stores(t):
            store.start()
        return carry

    lax.fori_loop(0, 3, project_step, 0)
    for t in range(3):
        for store in stores(t):
            store.wait()
    for store in kept:
        store.wait()


def qkv_rows(pieces, gain, wqkv):
    s = lambda *shape: jax.ShapeDtypeStruct(shape, BF)
    return pl.pallas_call(
        qkv_kernel,
        out_shape=(s(ROWS, D), s(ROWS, D)) + tuple(s(n, 3 * D) for n in PART_ROWS),
        in_specs=[vm()] * 5 + [hbm()],
        out_specs=[hbm()] * 5,
        scratch_shapes=[
            pltpu.VMEM((ROWS, D), BF), pltpu.VMEM((ROWS, D), BF), pltpu.VMEM((ROWS, D), BF),
            pltpu.VMEM((3, D, D), BF), pltpu.VMEM((3, ROWS, D), BF),
            pltpu.SemaphoreType.DMA((5,)), pltpu.SemaphoreType.DMA((3, 3)),
        ],
        compiler_params=params(32),
        cost_estimate=cost(10),
        name="norm_and_qkv",
    )(*pieces, gain, wqkv)


def attention_kernel(qkv_ref, rel_ref, shift_ref, keys_ref, att_ref, exp_ref, inv_ref, *, kinds):
    refs = (qkv_ref, att_ref, exp_ref, inv_ref, rel_ref, shift_ref, keys_ref)
    if kinds[0] == FULL:

        def step(w, carry):
            attend_window(FULL, pl.multiple_of(w * FULLR, 16), *refs)
            return carry

        lax.fori_loop(0, len(kinds), step, 0)
    else:
        row = 0
        for kind in kinds:
            attend_window(kind, row, *refs)
            row += NQ[kind]


def attention(part, qkv, rel, shift, keys):
    rows = PART_ROWS[part]
    s = lambda *shape, dtype=BF: jax.ShapeDtypeStruct(shape, dtype)
    return pl.pallas_call(
        functools.partial(attention_kernel, kinds=PARTS[part]),
        out_shape=(s(rows, D), s(D // HD, rows, KEYS), s(rows, D, dtype=F32)),
        in_specs=[vm()] * 4,
        out_specs=[vm()] * 3,
        compiler_params=params(24),
        cost_estimate=cost(10),
        name="attention_forward",
    )(qkv, rel, shift, keys)


def project_kernel(x_ref, att_a, att_b, att_c, wproj_ref, middle_ref):
    for ref, offset, count in zip((att_a, att_b, att_c), PART_OFFS, PART_ROWS):
        rows = slice(offset, offset + count)
        middle_ref[rows, :] = x_ref[rows, :].astype(F32) + nn(ref[...], wproj_ref[...])


def project(x, atts, wproj):
    return pl.pallas_call(
        project_kernel,
        out_shape=jax.ShapeDtypeStruct((ROWS, D), F32),
        in_specs=[vm()] * 5,
        out_specs=vm(),
        compiler_params=params(20),
        cost_estimate=cost(5),
        name="projection",
    )(x, *atts, wproj)


CHUNK = 512
LOCK = 1


def mlp_kernel(
    where_ref, middle_ref, g0, g1, g2, g3, gain_ref,
    p0, p1, p2, p3, q0, q1, q2, q3, q4, q5, d1, u1, d2, u2,
    o0, o1, o2, gmid_ref, down1, up1, down2, up2,
    gm_ref, out_rows, h2_ref, acc_mlp, acc_gh, gu1, ad2, w1_ref, w2_ref, downs, sem,
):
    half = where_ref[1]
    copies = []

    def fetch(src, dst):
        copies.append(pltpu.make_async_copy(src, dst, sem.at[len(copies)]))
        copies[-1].start()

    alpha, beta = (p0, p1, p2, p3), (q0, q1, q2, q3, q4, q5)
    for k in range(4):
        for j in range(4):
            for part, row, count, flag in alpha_block(k, j):
                rows = pl.ds(block_dst(QUART * k, flag, half), count)
                fetch(alpha[part].at[row : row + count, :], w1_ref.at[rows, D * j : D * (j + 1)])
            for part, row, count, flag in beta_block(k, j):
                rows = pl.ds(block_dst(QUART * k, flag, half), count)
                fetch(beta[part].at[row : row + count, :], w2_ref.at[rows, D * j : D * (j + 1)])
    join_pieces((g0, g1, g2, g3), gm_ref)
    for k in range(4):
        downs[k] = d1[:, QUART * k : QUART * (k + 1)]
        downs[4 + k] = u2[:, QUART * k : QUART * (k + 1)]
    for copy in copies:
        copy.wait()

    def merge(j, carry):
        cols = pl.ds(pl.multiple_of(D * j, 128), D)
        for k in range(4):
            rows = slice(QUART * k, QUART * (k + 1))
            w1_ref[rows, cols] = (w1_ref[rows, cols].astype(F32) + tn(downs[k], u1[:, cols])).astype(BF)
            w2_ref[rows, cols] = (w2_ref[rows, cols].astype(F32) + tn(downs[4 + k], d2[:, cols])).astype(BF)
        return carry

    lax.fori_loop(0, 4, merge, 0)
    gain = gain_ref[...]
    down1[...] = jnp.zeros_like(down1)
    up1[...] = jnp.zeros_like(up1)
    down2[...] = jnp.zeros_like(down2)
    up2[...] = jnp.zeros_like(up2)

    def tile_step(t, carry):
        rows = pl.ds(pl.multiple_of(t * HALF, 16), HALF)
        normed, _ = normalize(middle_ref[rows, :])
        h2 = (normed * gain).astype(BF)
        h2_ref[...] = h2
        gm = gm_ref[rows, :]
        ad1 = nt(d1[...], h2).astype(BF)
        gu2 = nt(u2[...], gm).astype(BF)
        acc_mlp[...] = jnp.zeros_like(acc_mlp)
        acc_gh[...] = jnp.zeros_like(acc_gh)
        gu1[...] = jnp.zeros_like(gu1)
        ad2[...] = jnp.zeros_like(ad2)

        def chunk_step(c, inner_carry):
            spans = [
                pl.ds(pl.multiple_of((c * LOCK + i) * CHUNK, CHUNK), CHUNK) for i in range(LOCK)
            ]
            h2 = h2_ref[...]
            gm = gm_ref[rows, :]
            inner = [nn(h2, w1_ref[:, span]) for span in spans]
            gact = [nn(gm, w2_ref[:, span]) for span in spans]
            act, ginner = [], []
            for i in range(LOCK):
                half = 0.5 * (1.0 + lax.erf(inner[i] * 2**-0.5))
                act.append((inner[i] * half).astype(BF))
                slope = half + inner[i] * (jnp.exp(-0.5 * inner[i] * inner[i]) * (2 * np.pi) ** -0.5)
                ginner.append((gact[i] * slope).astype(BF))
            for i, span in enumerate(spans):
                acc_mlp[...] += nt(act[i], w2_ref[:, span])
                acc_gh[...] += nt(ginner[i], w1_ref[:, span])
                up1[:, span] += nn(ad1, ginner[i])
                gu1[...] += nt(u1[:, span], ginner[i])
                ad2[...] += nt(d2[:, span], act[i])
                down2[:, span] += nn(gu2, act[i])
            return inner_carry

        lax.fori_loop(0, 4 * D // (CHUNK * LOCK), chunk_step, 0)
        down1[...] += nn(gu1[...].astype(BF), h2_ref[...])
        up2[...] += nn(ad2[...].astype(BF), gm_ref[rows, :])
        middle = middle_ref[rows, :]
        out_rows[rows, :] = (middle + acc_mlp[...]).astype(BF)
        normed, inv_std = normalize(middle)
        gmid_ref[rows, :] = gm_ref[rows, :].astype(F32) + norm_back(acc_gh[...] * gain, normed, inv_std)
        return carry

    lax.fori_loop(0, 2, tile_step, 0)
    split_pieces(out_rows, (o0, o1, o2))


def mlp(where, middle, pieces, gain, alpha, beta, d1, u1, d2, u2):
    s = lambda *shape, dtype=F32: jax.ShapeDtypeStruct(shape, dtype)
    return pl.pallas_call(
        mlp_kernel,
        out_shape=pieces_of(ROWS)
        + (s(ROWS, D), s(RANK, D), s(RANK, 4 * D), s(RANK, 4 * D), s(RANK, D)),
        in_specs=[sm()] + [vm()] * 6 + [pl.BlockSpec(memory_space=pl.ANY)] * 10 + [vm()] * 4,
        out_specs=[vm()] * 8,
        scratch_shapes=[
            pltpu.VMEM((ROWS, D), BF), pltpu.VMEM((ROWS, D), BF), pltpu.VMEM((HALF, D), BF),
            pltpu.VMEM((HALF, D), F32), pltpu.VMEM((HALF, D), F32),
            pltpu.VMEM((RANK, HALF), F32), pltpu.VMEM((RANK, HALF), F32),
            pltpu.VMEM((D, 4 * D), BF), pltpu.VMEM((D, 4 * D), BF), pltpu.VMEM((8, RANK, QUART), BF),
            pltpu.SemaphoreType.DMA((4 * 4 * 4,)),
        ],
        compiler_params=params(48),
        cost_estimate=cost(48),
        name="mlp_forward_backward",
    )(where, middle, *pieces, gain, *alpha, *beta, d1, u1, d2, u2)


def attend_back_window(
    kind, row0, qkv_ref, att_ref, exp_ref, inv_ref, gatt_ref, gqkv_ref, rel_ref, shift_ref, keys_ref
):
    count = NQ[kind]
    rows = pl.ds(row0, count)
    low_q, low_k = low_half(count), low_half(KEYS)
    live = live_rows()
    lane_k = lax.broadcasted_iota(jnp.int32, (KEYS, 128), 1) % HD
    lane_q = lax.broadcasted_iota(jnp.int32, (count, 128), 1) % HD
    ones = jnp.where(live & (lane_k < 2), 1.0, 0.0).astype(BF)
    across = jnp.where(
        low_half(128) != (lax.broadcasted_iota(jnp.int32, (128, 128), 0) < HD), -1.0, 0.0
    ).astype(BF)
    amount = shift_ref[kind, :count, :]
    onehot = keys_ref[kind]
    rel_mat = rel_ref[...]
    for first in range(0, D // 128, GROUP_BACK):
        pairs = range(first, first + GROUP_BACK)
        heads = [(pair, odd) for pair in pairs for odd in range(2)]
        go_tile = {
            p: (gatt_ref[rows, pair_columns(p)[0]].astype(F32) * inv_ref[rows, pair_columns(p)[0]]).astype(BF)
            for p in pairs
        }
        delta = {
            p: nn((go_tile[p].astype(F32) * att_ref[rows, pair_columns(p)[0]].astype(F32)).astype(BF), across)
            for p in pairs
        }
        go_t = {p: go_tile[p].T for p in pairs}
        gv = {}
        for p, odd in heads:
            gv[p, odd] = nn(go_t[p][HD * odd : HD * (odd + 1), :], exp_ref[2 * p + odd, rows, :])
        gscore = {}
        for p in pairs:
            high = delta[p].astype(BF)
            rest = (delta[p] - high.astype(F32)).astype(BF)
            low_delta = jnp.where(lane_q == 0, high, jnp.where(lane_q == 1, rest, 0)).astype(BF)
            v_tile = pad_rows(qkv_ref[rows, pair_columns(p)[2]])
            if kind == FULL:
                v_tile = jnp.where(live, v_tile, 0).astype(BF)
            gscore[p, 0] = nt(jnp.where(low_q, go_tile[p], low_delta), jnp.where(low_k, v_tile, ones))
            gscore[p, 1] = nt(jnp.where(low_q, low_delta, go_tile[p]), jnp.where(low_k, ones, v_tile))
        q_t = {p: qkv_ref[rows, pair_columns(p)[0]].T for p in pairs}
        gs = {(p, odd): (exp_ref[2 * p + odd, rows, :].astype(F32) * gscore[p, odd]).astype(BF) for p, odd in heads}
        gk = {(p, odd): nn(q_t[p][HD * odd : HD * (odd + 1), :], gs[p, odd]) for p, odd in heads}
        gq = {}
        for p in pairs:
            k_tile = pad_rows(qkv_ref[rows, pair_columns(p)[1]] * BF(HD**-0.5))
            gq[p, 0] = nn(gs[p, 0], jnp.where(low_k, k_tile, onehot))
            gq[p, 1] = nn(gs[p, 1], jnp.where(low_k, onehot, k_tile))
        sums = {p: barrel(jnp.where(low_q, gq[p, 1], gq[p, 0]), amount, False).astype(BF) for p in pairs}
        for p in pairs:
            cols, kcols, vcols = pair_columns(p)
            gv_tile = jnp.concatenate([gv[p, 0], gv[p, 1]], axis=0).astype(BF).T
            gqkv_ref[rows, vcols] = gv_tile[:count, :]
            gk_tile = (jnp.concatenate([gk[p, 0], gk[p, 1]], axis=0) * HD**-0.5).astype(BF).T
            gqkv_ref[rows, kcols] = gk_tile[:count, :]
            gqkv_ref[rows, cols] = (jnp.where(low_q, gq[p, 0], gq[p, 1]) + nt(sums[p], rel_mat)).astype(BF)


def attention_back_kernel(
    gmid_hbm, hid_hbm, qkv_a, qkv_b, qkv_c, att_a, att_b, att_c, exp_a, exp_b, exp_c, inv_a, inv_b, inv_c,
    wproj_ref, rel_ref, shift_ref, keys_ref, dqkv, uqkv, dproj, uproj,
    gqkv_hbm, down_q, up_q, down_p, up_p,
    gmid_ref, hid_ref, qkv_ref, att_ref, exp_ref, inv_ref, gqkv_ref, gb_ref, gatt_ref, sem, out_sem,
):
    spans = [pl.ds(offset, count) for offset, count in zip(PART_OFFS, PART_ROWS)]
    pairs = [(gmid_hbm, gmid_ref)]
    for part, srcs in enumerate(
        ((qkv_a, inv_a, att_a, exp_a), (qkv_b, inv_b, att_b, exp_b), (qkv_c, inv_c, att_c, exp_c))
    ):
        rows = spans[part]
        for src, dst in zip(srcs, (qkv_ref, inv_ref, att_ref)):
            pairs.append((src, dst.at[rows, :]))
        pairs.append((srcs[3], exp_ref.at[:, rows, :]))
    pairs.append((hid_hbm, hid_ref))
    loads = [pltpu.make_async_copy(src, dst, sem.at[i]) for i, (src, dst) in enumerate(pairs)]
    for load in loads:
        load.start()

    def wait_part(part):
        for load in loads[1 + 4 * part : 5 + 4 * part]:
            load.wait()

    stores = [
        pltpu.make_async_copy(gqkv_ref.at[rows, :], gqkv_hbm.at[rows, :], out_sem.at[i])
        for i, rows in enumerate(spans)
    ]
    loads[0].wait()
    gb_ref[...] = gmid_ref[...].astype(BF)
    gatt_ref[...] = nt(gb_ref[...], wproj_ref[...]).astype(BF)
    refs = (qkv_ref, att_ref, exp_ref, inv_ref, gatt_ref, gqkv_ref, rel_ref, shift_ref, keys_ref)

    def step(w, carry):
        for part in range(2):

            @pl.when(w == 2 * part)
            def _():
                wait_part(part)

        attend_back_window(FULL, pl.multiple_of(w * FULLR, 16), *refs)
        return carry

    lax.fori_loop(0, 4, step, 0)
    stores[0].start()
    stores[1].start()
    wait_part(2)
    for kind in (RIGHT, BOTTOM, CORNER):
        attend_back_window(kind, OFFS[kind], *refs)
    stores[2].start()
    up_p[...] = nn(nt(dproj[...], att_ref[...]).astype(BF), gb_ref[...])
    down_p[...] = nn(nt(uproj[...], gb_ref[...]).astype(BF), att_ref[...])
    loads[-1].wait()
    up_q[...] = nn(nt(dqkv[...], hid_ref[...]).astype(BF), gqkv_ref[...])
    down_q[...] = nn(nt(uqkv[...], gqkv_ref[...]).astype(BF), hid_ref[...])
    for store in stores:
        store.wait()


def attention_back(gmid, hid, qkvs, atts, exps, invs, wproj, rel, shift, keys, dqkv, uqkv, dproj, uproj):
    s = lambda *shape, dtype=F32: jax.ShapeDtypeStruct(shape, dtype)
    return pl.pallas_call(
        attention_back_kernel,
        out_shape=(s(ROWS, 3 * D, dtype=BF), s(RANK, D), s(RANK, 3 * D), s(RANK, D), s(RANK, D)),
        in_specs=[hbm()] * 14 + [vm()] * 8,
        out_specs=[hbm()] + [vm()] * 4,
        scratch_shapes=[
            pltpu.VMEM((ROWS, D), F32), pltpu.VMEM((ROWS, D), BF), pltpu.VMEM((ROWS, 3 * D), BF),
            pltpu.VMEM((ROWS, D), BF), pltpu.VMEM((D // HD, ROWS, KEYS), BF), pltpu.VMEM((ROWS, D), F32),
            pltpu.VMEM((ROWS, 3 * D), BF), pltpu.VMEM((ROWS, D), BF), pltpu.VMEM((ROWS, D), BF),
            pltpu.SemaphoreType.DMA((14,)), pltpu.SemaphoreType.DMA((3,)),
        ],
        compiler_params=params(52),
        cost_estimate=cost(28),
        name="attention_backward",
    )(gmid, hid, *qkvs, *atts, *exps, *invs, wproj, rel, shift, keys, dqkv, uqkv, dproj, uproj)


def token_grad_kernel(gmid_hbm, x_hbm, gqkv_hbm, gain_ref, wqkv_ref, o0, o1, o2,
                      gmid_ref, x_ref, gqkv_ref, gh_ref, out_rows, sem, *, low, high):
    span = pl.ds(low, high - low)
    copies = [
        pltpu.make_async_copy(src.at[span, :], dst, sem.at[i])
        for i, (src, dst) in enumerate(((gqkv_hbm, gqkv_ref), (x_hbm, x_ref), (gmid_hbm, gmid_ref)))
    ]
    for copy in copies:
        copy.start()
    copies[0].wait()
    gh_ref[...] = nt(gqkv_ref[...], wqkv_ref[...])
    copies[1].wait()
    copies[2].wait()
    gain = gain_ref[...]
    step = (high - low) // 2

    def norm_step(i, carry):
        rows = pl.ds(pl.multiple_of(i * step, 16), step)
        normed, inv_std = normalize(x_ref[rows, :].astype(F32))
        back = norm_back(gh_ref[rows, :] * gain, normed, inv_std)
        out_rows[rows, :] = (gmid_ref[rows, :] + back).astype(BF)
        return carry

    lax.fori_loop(0, 2, norm_step, 0)
    split_pieces(out_rows, (o0, o1, o2))


def token_grad(gmid, x, gqkv, gain, wqkv, low, high):
    count = high - low
    return pl.pallas_call(
        functools.partial(token_grad_kernel, low=low, high=high),
        out_shape=pieces_of(count),
        in_specs=[hbm(), hbm(), hbm(), vm(), vm()],
        out_specs=[vm()] * 3,
        scratch_shapes=[
            pltpu.VMEM((count, D), F32), pltpu.VMEM((count, D), BF), pltpu.VMEM((count, 3 * D), BF),
            pltpu.VMEM((count, D), F32), pltpu.VMEM((count, D), BF), pltpu.SemaphoreType.DMA((3,)),
        ],
        compiler_params=params(28),
        cost_estimate=cost(8),
        name="token_gradient",
    )(gmid, x, gqkv, gain, wqkv)


def grad_pack_kernel(where_ref, down_q, up_q, down_p, up_p, down1, up1, down2, up2, o0, o1, o2, o3, buf_ref):
    mine = where_ref[0]
    for k in range(4):
        for i, ref in enumerate((down_q, down1, up_p, up2)):
            buf_ref[k, :RANK, QUART * i : QUART * (i + 1)] = ref[:, QUART * k : QUART * (k + 1)]
    for dest in range(4):
        k = jnp.bitwise_xor(mine, dest)
        ranks = slice(RANK // 4 * dest, RANK // 4 * (dest + 1))
        for j in range(4):
            base = RANK + 12 * j
            for t in range(3):
                buf_ref[k, base : base + 4, QUART * t : QUART * (t + 1)] = up_q[
                    ranks, D * t + QUART * j : D * t + QUART * (j + 1)
                ]
            buf_ref[k, base : base + 4, 3 * QUART :] = down_p[ranks, QUART * j : QUART * (j + 1)]
            buf_ref[k, base + 4 : base + 8, :] = up1[ranks, D * j : D * (j + 1)]
            buf_ref[k, base + 8 : base + 12, :] = down2[ranks, D * j : D * (j + 1)]
    for k, out in enumerate((o0, o1, o2, o3)):
        out[...] = buf_ref[k].astype(BF)


def grad_pack(where, *grads):
    return pl.pallas_call(
        grad_pack_kernel,
        out_shape=(jax.ShapeDtypeStruct((4 * RANK, D), BF),) * 4,
        in_specs=[sm()] + [vm()] * 8,
        out_specs=[vm()] * 4,
        scratch_shapes=[pltpu.VMEM((4, 4 * RANK, D), F32)],
        compiler_params=params(8),
        cost_estimate=cost(2),
        name="adapter_grad_pack",
    )(where, *grads)


def grad_sum_kernel(g0, g1, g2, g3, o0, o1, o2, o3, buf_ref):
    total = g0[...].astype(F32) + g1[...].astype(F32) + g2[...].astype(F32) + g3[...].astype(F32)
    buf_ref[...] = jnp.zeros_like(buf_ref)
    buf_ref[:RANK, :] = total[:RANK, :]
    for j, out in enumerate((o0, o1, o2, o3)):
        buf_ref[RANK : RANK + 12, :] = total[RANK + 12 * j : RANK + 12 * (j + 1), :]
        out[...] = buf_ref[...].astype(BF)


def grad_sum(pieces):
    return pl.pallas_call(
        grad_sum_kernel,
        out_shape=(jax.ShapeDtypeStruct((2 * RANK, D), BF),) * 4,
        in_specs=[vm()] * 4,
        out_specs=[vm()] * 4,
        scratch_shapes=[pltpu.VMEM((2 * RANK, D), F32)],
        compiler_params=params(4),
        cost_estimate=cost(2),
        name="adapter_grad_sum",
    )(*pieces)


def grad_adapters_kernel(index_ref, x_ref, qkv_dn, fc1_dn, proj_up, fc2_up, rest_ref, acc_ref):
    acc_ref[...] = jnp.zeros_like(acc_ref)

    def add(i, carry):
        acc_ref[index_ref[i]] += x_ref[i].astype(F32)
        return carry

    lax.fori_loop(0, x_ref.shape[0], add, 0)
    for i, ref in enumerate((qkv_dn, fc1_dn, proj_up, fc2_up)):
        ref[...] = acc_ref[:, :RANK, QUART * i : QUART * (i + 1)]
    rest_ref[...] = acc_ref[:, RANK:, :].astype(BF)


def grad_adapters(index, x):
    s = lambda n, dtype=F32: jax.ShapeDtypeStruct((ADAPT, RANK, n), dtype)
    return pl.pallas_call(
        grad_adapters_kernel,
        out_shape=(s(QUART), s(QUART), s(QUART), s(QUART), s(D, BF)),
        in_specs=[sm(), vm()],
        out_specs=[vm()] * 5,
        scratch_shapes=[pltpu.VMEM((ADAPT, 2 * RANK, D), F32)],
        compiler_params=params(8),
        cost_estimate=cost(2),
        name="adapter_grad_by_adapter",
    )(index, x)


def grad_join_kernel(where_ref, r0, r1, r2, r3, qkv_up, proj_dn, fc1_up, fc2_dn, buf_ref):
    mine = where_ref[0]
    heads = qkv_up.shape[2] // (3 * HD)
    for k, ref in enumerate((r0, r1, r2, r3)):
        buf_ref[jnp.bitwise_xor(mine, k)] = ref[...].astype(F32)
    for source in range(4):
        ranks = slice(RANK // 4 * source, RANK // 4 * (source + 1))
        for h in range(heads):
            for t in range(3):
                qkv_up[:, ranks, HD * (3 * h + t) : HD * (3 * h + t + 1)] = buf_ref[
                    source, :, 0:4, QUART * t + HD * h : QUART * t + HD * (h + 1)
                ]
        proj_dn[:, ranks, :] = buf_ref[source, :, 0:4, 3 * QUART :]
        fc1_up[:, ranks, :] = buf_ref[source, :, 4:8, :]
        fc2_dn[:, ranks, :] = buf_ref[source, :, 8:12, :]


def grad_join(where, pieces):
    s = lambda n: jax.ShapeDtypeStruct((ADAPT, RANK, n), F32)
    return pl.pallas_call(
        grad_join_kernel,
        out_shape=(s(3 * QUART), s(QUART), s(D), s(D)),
        in_specs=[sm()] + [vm()] * 4,
        out_specs=[vm()] * 4,
        scratch_shapes=[pltpu.VMEM((4, ADAPT, RANK, D), F32)],
        compiler_params=params(12),
        cost_estimate=cost(2),
        name="adapter_grad_join",
    )(where, *pieces)


def flip(values, axis, distance):
    size = lax.axis_size(axis)
    return lax.ppermute(values, axis, [(i, i ^ distance) for i in range(size)])


def send_rows(pieces, *deps):
    own, near, pair = pieces
    if deps:
        near, = after((near,), *deps)
    return [own, flip(near, "row", 1), flip(pair, "row", 2)]


def hand_on(pieces, *deps):
    own, near, crossed = pieces
    if deps:
        near, crossed = after((near, crossed), *deps)
    return [own, near, crossed, flip(crossed, "row", 1)]


def exchange(slots, axis):
    return [slots[0]] + [flip(slots[k], axis, k) for k in range(1, 4)]


def after(values, *deps):
    return lax.optimization_barrier((tuple(values), deps))[0]


def col_halves(half):
    return jnp.concatenate([flip(half, "col", j) for j in range(1, 4)], axis=0)


def col_pairs(half, other_row):
    two = jnp.concatenate([half, other_row], axis=0)
    return jnp.concatenate([other_row] + [flip(two, "col", j) for j in range(1, 4)], axis=0)


def body(
    tokens, grad_out, adapter_index, norm1_gain, norm2_gain, qkv_weight, proj_weight, fc1_weight, fc2_weight,
    rel_h, rel_w, qkv_down, qkv_up, proj_down, proj_up, fc1_down, fc1_up, fc2_down, fc2_up,
):
    members = lax.axis_size("col")
    batches = lax.axis_size("dp")
    row_index, col_index, dp_index = lax.axis_index("row"), lax.axis_index("col"), lax.axis_index("dp")
    half = dp_index % 2
    where = jnp.stack([row_index, half]).astype(jnp.int32)
    slot_images = (
        jnp.bitwise_xor(dp_index, jnp.arange(batches, dtype=jnp.int32))[:, None] * members
        + jnp.bitwise_xor(col_index, jnp.arange(members, dtype=jnp.int32))[None, :]
    ).reshape(-1)
    slot_adapters = jnp.sum(
        jnp.where(
            slot_images[:, None] == jnp.arange(adapter_index.shape[0], dtype=jnp.int32)[None, :],
            adapter_index[:, 0][None, :],
            0,
        ),
        axis=1,
    )
    pick = jnp.concatenate([slot_adapters[:4], half[None]]).astype(jnp.int32)
    swap = lambda m: jnp.swapaxes(m, 1, 2)

    shift, keys = jnp.asarray(SHIFT_NP), jnp.asarray(KEYS_NP)

    *token_slots, alpha_own, beta_own, alpha_half, cross, fc1_half, fc2_half = front(
        where, tokens, qkv_weight, proj_weight, fc1_weight, fc2_weight
    )
    crossed = flip(cross, "row", 2)
    beta_half, b0 = cross[:HBLK], crossed[:HBLK]
    c0 = jnp.concatenate([crossed[HBLK : 2 * HBLK], crossed[2 * HBLK :]], axis=1)
    alpha_near = col_halves(alpha_half)
    x_pieces = send_rows(token_slots, crossed)
    *send, row_adapters, rel = adapter_pack(
        pick, qkv_up, swap(proj_down), fc1_up, swap(fc2_down), swap(qkv_down), swap(fc1_down), proj_up, fc2_up,
        norm1_gain.reshape(1, -1), norm2_gain.reshape(1, -1), rel_h, rel_w,
    )
    beta_sent = [jnp.concatenate([beta_half, b0, send[j]], axis=0) for j in range(1, 4)]
    beta_got = [flip(m, "col", j) for j, m in enumerate(beta_sent, 1)]
    alpha_near, x_pieces[1] = after((alpha_near, x_pieces[1]))
    alpha_far = flip(alpha_near, "dp", 1)
    g = jnp.concatenate([alpha_own, alpha_near, alpha_far, row_adapters], axis=0)
    g, *x_pieces = after((g, *x_pieces))
    gy = flip(g, "row", 2)
    grad_slots = pack(where, grad_out)
    *beta_got, _ = after((*beta_got, grad_slots[0]))
    beta_near = jnp.concatenate([b0] + [m[:QUART] for m in beta_got], axis=0)
    col_adapters = [send[0]] + beta_got
    beta_far = flip(beta_near, "dp", 1)
    x_pieces = hand_on(x_pieces)

    g1, own1, near1 = (flip(m, "row", 1) for m in (g, beta_own, beta_near))
    fc1_half, = after((fc1_half,), g1, own1, near1, x_pieces[3])
    fc1_near = [flip(fc1_half, "col", j) for j in range(1, 4)]
    gy, beta_far, fc2_half, c0 = after((gy, beta_far, fc2_half, c0), *fc1_near)
    fc2_two = jnp.concatenate([fc2_half, c0], axis=0)
    fc2_near = [flip(fc2_two, "col", j) for j in range(1, 4)]
    gy1, far1 = flip(gy, "row", 1), flip(beta_far, "row", 1)
    *grad_slots, fc1_near = after((*grad_slots, jnp.concatenate(fc1_near, axis=0)), gy1, far1)
    fc1_far = flip(fc1_near, "dp", 1)
    g_pieces = [grad_slots[0], grad_slots[1], flip(grad_slots[2], "row", 2)]
    wqkv, wproj, dqkv, uqkv, dproj, uproj, d1, u1, d2, u2, gain1, gain2 = prep1(
        where, (g, g1, gy, gy1), (beta_own, beta_near, beta_far, own1, near1, far1), col_adapters
    )
    h = jnp.concatenate([fc1_weight, fc1_near, fc1_far], axis=0)
    wqkv, h = after((wqkv, h), g_pieces[2])
    hy = flip(h, "row", 2)
    x, hid, *qkvs = qkv_rows(x_pieces, gain1, wqkv)
    *qkvs, n1, n2, n3 = after((*qkvs, *fc2_near))
    fc2_near = jnp.concatenate([c0, n1, n2, n3], axis=0)
    fc2_far = flip(fc2_near, "dp", 1)
    fc2_ahead = [flip(m, "row", 1) for m in (fc2_weight, fc2_near)]
    g_pieces[1], = after((g_pieces[1],), qkvs[0])
    g_pieces[1] = flip(g_pieces[1], "row", 1)
    g_pieces = hand_on(g_pieces, qkvs[0])
    part0 = attention(0, qkvs[0], rel, shift, keys)
    qkv1, = after((qkvs[1],), part0[0], g_pieces[3], *fc2_ahead)
    part1 = attention(1, qkv1, rel, shift, keys)
    qkv2, _ = after((qkvs[2], part1[0]))
    part2 = attention(2, qkv2, rel, shift, keys)
    atts, exps, invs = zip(part0, part1, part2)
    atts = list(atts)
    atts[2], hy = after((atts[2], hy))
    alpha2 = [h, flip(h, "row", 1), hy, flip(hy, "row", 1)]
    middle = project(x, atts, wproj)
    middle, fc2_far = after((middle, fc2_far))
    beta2 = [fc2_weight, fc2_near, fc2_far, *fc2_ahead, flip(fc2_far, "row", 1)]

    *out_slots, gmid, down1, up1, down2, up2 = mlp(where, middle, g_pieces, gain2, alpha2, beta2, d1, u1, d2, u2)
    out_pieces = send_rows(out_slots)
    gqkv, down_q, up_q, down_p, up_p = attention_back(
        gmid, hid, qkvs, atts, exps, invs, wproj, rel, shift, keys, dqkv, uqkv, dproj, uproj
    )
    out_pieces = hand_on(out_pieces, gqkv)
    gqkv, down_q, up_q, down_p, up_p = after((gqkv, down_q, up_q, down_p, up_p), *out_pieces[:3])
    packed = grad_pack(where, down_q, up_q, down_p, up_p, down1, up1, down2, up2)
    *packed, gqkv = after((*packed, gqkv))
    row_sums = exchange(packed, "row")
    back0 = token_grad(gmid, x, gqkv, gain1, wqkv, *TAIL[0])
    *row_sums, gqkv, b0, b1, b2 = after((*row_sums, gqkv, *back0))
    back_pieces = send_rows((b0, b1, b2))
    summed = grad_sum(row_sums)
    *summed, gqkv = after((*summed, gqkv))
    images = exchange(summed, "col")
    back1 = token_grad(gmid, x, gqkv, gain1, wqkv, *TAIL[1])
    last_pieces = send_rows(back1)
    *images, near, crossed = after((*images, *back_pieces[1:]), back1[0])
    back_pieces = hand_on([back_pieces[0], near, crossed])
    images = jnp.stack(images)
    images, *out_pieces = after((images, *out_pieces))
    step = 1
    while step < batches:
        images = jnp.concatenate([images, flip(images, "dp", step)], axis=0)
        step *= 2
    result = unpack(where, out_pieces, BF)
    images, = after((images,), result)
    qkv_dn, fc1_dn, proj_upg, fc2_upg, rest = grad_adapters(slot_adapters.astype(jnp.int32), images)
    rests = [rest] + [flip(rest, "row", k) for k in range(1, 4)]
    grad_tokens = unpack(where, back_pieces + hand_on(last_pieces, rest), F32, TAIL)
    rests = after(tuple(rests), grad_tokens)
    qkv_upg, proj_dn, fc1_upg, fc2_dn = grad_join(where, rests)
    return (
        result, grad_tokens,
        swap(qkv_dn), qkv_upg, swap(proj_dn), proj_upg, swap(fc1_dn), fc1_upg, swap(fc2_dn), fc2_upg,
    )


def solution(mesh):
    return jax.shard_map(
        body,
        mesh=mesh,
        in_specs=(
            P("row", ("dp", "col")), P("row", ("dp", "col")), P(), P("row"), P("row"),
            P("row", "col"), P("col", "row"), P("row", "col"), P("row", "col"), P(), P(),
            P(None, "row", None), P(None, None, "col"), P(None, "col", None), P(None, None, "row"),
            P(None, "row", None), P(None, None, "col"), P(None, "col", None), P(None, None, "row"),
        ),
        out_specs=(
            P("row", ("dp", "col")), P("row", ("dp", "col")),
            P(None, "row", None), P(None, None, "col"), P(None, "col", None), P(None, None, "row"),
            P(None, "row", None), P(None, None, "col"), P(None, "col", None), P(None, None, "row"),
        ),
        check_vma=False,
    )
```

```python
import functools

import jax
import jax.numpy as jnp
import numpy as np
from jax import lax
from jax.experimental import pallas as pl
from jax.experimental.pallas import tpu as pltpu
from jax.sharding import PartitionSpec as P

D = 768
HD = 64
WIN = 14
SLOTS = WIN * WIN
SIDE = 64
ADAPT = 8
NWIN = 5
IMG_TOK = NWIN * NWIN * SLOTS
RANK = 16
EDGE = SIDE - (NWIN - 1) * WIN
QUART = D // 4
FULLR = 208
KEYS = 208
EDGER = EDGE * WIN
CORNR = EDGE * EDGE
ROWS = 4 * FULLR + 2 * EDGER + CORNR
HALF = ROWS // 2
HBLK = QUART // 2
EPSILON = 1e-06
BF = jnp.bfloat16
F32 = jnp.float32

FULL, RIGHT, BOTTOM, CORNER = 0, 1, 2, 3
NQ = (FULLR, EDGER, EDGER, CORNR)
OFFS = (0, 4 * FULLR, 4 * FULLR + EDGER, 4 * FULLR + 2 * EDGER)


def slot_order(kind):
    rows = EDGE if kind in (BOTTOM, CORNER) else WIN
    cols = EDGE if kind in (RIGHT, CORNER) else WIN
    kept = [a * WIN + b for a in range(rows) for b in range(cols)]
    rest = [s for s in range(SLOTS) if s not in set(kept)]
    return kept, kept + rest


def build_tables():
    shift = np.zeros((4, FULLR, 128), np.int32)
    keys = np.zeros((4, KEYS, 128), np.float32)
    for kind in range(4):
        kept, order = slot_order(kind)
        for i, s in enumerate(kept):
            for base in (0, 64):
                shift[kind, i, base : base + 32] = WIN - 1 - s // WIN
                shift[kind, i, base + 32 : base + 64] = WIN - 1 - s % WIN
        spare = order[0] if kind == FULL else order[-1]
        for i, s in enumerate(order + [spare] * (KEYS - SLOTS)):
            for base in (0, 64):
                keys[kind, i, base + s // WIN] = 1.0
                keys[kind, i, base + 32 + s % WIN] = 1.0
    return shift, keys.astype(jnp.bfloat16)


SHIFT_NP, KEYS_NP = build_tables()


def nn(a, b):
    return jnp.dot(a, b, preferred_element_type=F32)


def nt(a, b):
    return lax.dot_general(a, b, (((1,), (1,)), ((), ())), preferred_element_type=F32)


def tn(a, b):
    return lax.dot_general(a, b, (((0,), (0,)), ((), ())), preferred_element_type=F32)


def vm():
    return pl.BlockSpec(memory_space=pltpu.VMEM)


def hbm():
    return pl.BlockSpec(memory_space=pl.ANY)


def in_hbm(x):
    return pltpu.with_memory_space_constraint(x, pltpu.HBM)


def arg():
    return pl.BlockSpec(memory_space=pltpu.HBM)


def sm():
    return pl.BlockSpec(memory_space=pltpu.SMEM)


def params(mib=60):
    return pltpu.CompilerParams(vmem_limit_bytes=mib * 1024 * 1024)


def cost(us):
    return pl.CostEstimate(flops=int(us * 1e6), transcendentals=0, bytes_accessed=0)


def place_window(kind, count, moved, width, spare=-100000):
    row = lax.broadcasted_iota(jnp.int32, (count, width), 0)
    lane = lax.broadcasted_iota(jnp.int32, (count, width), 1)
    if kind in (RIGHT, CORNER):
        src = (row // EDGE) * WIN + row % EDGE
    else:
        src = jnp.where(row < SLOTS, row, spare)
    return (lane == src + moved).astype(F32).astype(BF)


def window_list(dest):
    items = [(FULL, FULLR * j, NWIN * dest + j) for j in range(4)]
    items.append((RIGHT, OFFS[1], NWIN * dest + 4))
    items.append((BOTTOM, OFFS[2], NWIN * 4 + dest))
    if dest == 3:
        items.append((CORNER, OFFS[3], NWIN * NWIN - 1))
    return items


def window_span(window):
    start = window * SLOTS
    low = start // 128 * 128
    high = min(-(-(start + SLOTS) // 128) * 128, IMG_TOK)
    return low, high, start - low


def pack_rows(mine, x_ref, rows_ref, spare):
    for dest in range(4):
        slot = jnp.bitwise_xor(mine, dest)
        if dest != 3:
            rows_ref[slot, OFFS[3] :, :] = jnp.zeros((CORNR, QUART), BF)
        for kind, offset, window in window_list(dest):
            low, high, moved = window_span(window)
            pick = place_window(kind, NQ[kind], moved, high - low, spare)
            rows_ref[slot, offset : offset + NQ[kind], :] = nt(pick, x_ref[:, low:high]).astype(BF)


def fold(rows_ref, outs):
    half = rows_ref.shape[1] // 2
    for slot, (out, base) in enumerate(((outs[0], 0), (outs[1], 0), (outs[2], 0), (outs[2], half))):
        out[base : base + half, :QUART] = rows_ref[slot, :half, :]
        out[base : base + half, QUART:] = rows_ref[slot, half:, :]


def pack_kernel(where_ref, x_hbm, o0, o1, o2, rows_ref, x_ref, sem):
    load = pltpu.make_async_copy(x_hbm, x_ref, sem)
    load.start()
    load.wait()
    pack_rows(where_ref[0], x_ref, rows_ref, -100000)
    fold(rows_ref, (o0, o1, o2))


def pieces_of(rows):
    piece = lambda n: jax.ShapeDtypeStruct((n, 2 * QUART), BF)
    return (piece(rows // 2), piece(rows // 2), piece(rows))


def pack(where, x):
    return pl.pallas_call(
        pack_kernel,
        out_shape=pieces_of(ROWS),
        in_specs=[sm(), arg()],
        out_specs=[vm()] * 3,
        scratch_shapes=[
            pltpu.VMEM((4, ROWS, QUART), BF), pltpu.VMEM((QUART, IMG_TOK), BF), pltpu.SemaphoreType.DMA,
        ],
        compiler_params=params(16),
        cost_estimate=cost(4),
        name="pack",
    )(where, in_hbm(x))


def front_kernel(
    where_ref, x_hbm, qkv_hbm, proj_hbm, fc1_hbm, fc2_hbm,
    o0, o1, o2, alpha_ref, beta_ref, alpha_half, cross_ref, fc1_half, fc2_half,
    rows_ref, x_ref, qkv_w, proj_w, sem,
):
    rows = pl.ds(pl.multiple_of(where_ref[1] * HBLK, 32), HBLK)
    loads = [
        pltpu.make_async_copy(src, dst, sem.at[i])
        for i, (src, dst) in enumerate(
            (
                (qkv_hbm, qkv_w), (proj_hbm, proj_w), (fc2_hbm.at[rows, :], fc2_half),
                (fc1_hbm.at[rows, :], fc1_half), (x_hbm, x_ref),
            )
        )
    ]
    for load in loads:
        load.start()
    for load in loads[:4]:
        load.wait()
    heads = qkv_w.shape[1] // (3 * HD)
    for h in range(heads):
        for t in range(3):
            ref, base = (alpha_ref, QUART * t) if t < 2 else (beta_ref, 0)
            ref[:, base + HD * h : base + HD * (h + 1)] = qkv_w[:, HD * (3 * h + t) : HD * (3 * h + t + 1)]
    beta_ref[:, QUART:] = proj_w[...]
    alpha_half[...] = alpha_ref[rows, :]
    cross_ref[:HBLK, :] = beta_ref[rows, :]
    cross_ref[HBLK : 2 * HBLK, :] = fc2_half[:, : 2 * QUART]
    cross_ref[2 * HBLK :, :] = fc2_half[:, 2 * QUART :]
    loads[4].wait()
    pack_rows(where_ref[0], x_ref, rows_ref, 0)
    fold(rows_ref, (o0, o1, o2))


def front(where, x, qkv_w, proj_w, fc1_w, fc2_w):
    s = lambda *shape: jax.ShapeDtypeStruct(shape, BF)
    return pl.pallas_call(
        front_kernel,
        out_shape=pieces_of(ROWS)
        + (
            s(QUART, 2 * QUART), s(QUART, 2 * QUART), s(HBLK, 2 * QUART), s(3 * HBLK, 2 * QUART),
            s(HBLK, D), s(HBLK, D),
        ),
        in_specs=[sm()] + [arg()] * 5,
        out_specs=[vm()] * 9,
        scratch_shapes=[
            pltpu.VMEM((4, ROWS, QUART), BF), pltpu.VMEM((QUART, IMG_TOK), BF),
            pltpu.VMEM(qkv_w.shape, BF), pltpu.VMEM(proj_w.shape, BF), pltpu.SemaphoreType.DMA((5,)),
        ],
        compiler_params=params(16),
        cost_estimate=cost(5),
        name="token_and_weight_pack",
    )(where, *(in_hbm(m) for m in (x, qkv_w, proj_w, fc1_w, fc2_w)))


def unpack_kernel(where_ref, *refs, bounds):
    pieces, (out_ref, acc_ref, rows_ref) = refs[:-3], refs[-3:]
    mine = where_ref[0]
    acc_ref[...] = jnp.zeros_like(acc_ref)
    index = 0
    for low, high in bounds:
        half = (high - low) // 2
        for slot in range(4):
            piece = pieces[index]
            rows = slice(half, 2 * half) if slot == 3 else slice(0, half)
            rows_ref[slot, low : low + half, :] = piece[rows, :QUART]
            rows_ref[slot, low + half : high, :] = piece[rows, QUART:]
            index += 1

    for source in range(4):
        slot = jnp.bitwise_xor(mine, source)
        for kind, offset, window in window_list(source):
            low, high, moved = window_span(window)
            pick = place_window(kind, NQ[kind], moved, high - low)
            acc_ref[:, low:high] += tn(rows_ref[slot, offset : offset + NQ[kind], :], pick)
    out_ref[...] = acc_ref[:, :IMG_TOK].astype(out_ref.dtype)


def unpack(where, pieces, dtype, bounds=((0, ROWS),)):
    return pl.pallas_call(
        functools.partial(unpack_kernel, bounds=bounds),
        out_shape=jax.ShapeDtypeStruct((QUART, IMG_TOK), dtype),
        in_specs=[sm()] + [vm()] * len(pieces),
        out_specs=vm(),
        scratch_shapes=[
            pltpu.VMEM((QUART, -(-IMG_TOK // 128) * 128), F32),
            pltpu.VMEM((4, ROWS, QUART), BF),
        ],
        compiler_params=params(24),
        cost_estimate=cost(4),
        name="unpack",
    )(where, *pieces)


def join_pieces(pieces, dst_ref):
    for slot, piece in enumerate(pieces):
        rows = slice(HALF, ROWS) if slot == 3 else slice(0, HALF)
        dst_ref[:HALF, QUART * slot : QUART * (slot + 1)] = piece[rows, :QUART]
        dst_ref[HALF:, QUART * slot : QUART * (slot + 1)] = piece[rows, QUART:]


def split_pieces(src_ref, outs):
    half = src_ref.shape[0] // 2
    for slot, (out, base) in enumerate(((outs[0], 0), (outs[1], 0), (outs[2], 0), (outs[2], half))):
        out[base : base + half, :QUART] = src_ref[:half, QUART * slot : QUART * (slot + 1)]
        out[base : base + half, QUART:] = src_ref[half:, QUART * slot : QUART * (slot + 1)]


def adapter_pack_kernel(
    pick_ref, qkv_up_hbm, proj_dn_hbm, fc1_up_hbm, fc2_dn_hbm, qkv_dn_hbm, fc1_dn_hbm, proj_up_hbm, fc2_up_hbm,
    gain1, gain2, rel_h, rel_w, s0, s1, s2, s3, row_ref, rel_ref,
    qkv_up, proj_dn, fc1_up, fc2_dn, qkv_dn, fc1_dn, proj_up, fc2_up, sem,
):
    pairs = []
    for j in range(4):
        for src, dst in ((qkv_up_hbm, qkv_up), (proj_dn_hbm, proj_dn), (fc1_up_hbm, fc1_up), (fc2_dn_hbm, fc2_dn)):
            pairs.append((src.at[pick_ref[j]], dst.at[j]))
    for src, dst in ((qkv_dn_hbm, qkv_dn), (fc1_dn_hbm, fc1_dn), (proj_up_hbm, proj_up), (fc2_up_hbm, fc2_up)):
        pairs.append((src.at[pick_ref[0]], dst.at[0]))
    loads = [pltpu.make_async_copy(src, dst, sem.at[i]) for i, (src, dst) in enumerate(pairs)]
    for load in loads:
        load.start()
    offsets = rel_h.shape[0]
    reverse = (
        lax.broadcasted_iota(jnp.int32, (offsets, 32), 0) + lax.broadcasted_iota(jnp.int32, (offsets, 32), 1)
        == offsets - 1
    ).astype(F32).astype(BF)
    rel_ref[...] = jnp.zeros_like(rel_ref)
    for i, table in enumerate((rel_h, rel_w)):
        block = tn(table[...], reverse).astype(BF)
        rel_ref[:HD, HD + 32 * i : HD + 32 * (i + 1)] = block
        rel_ref[HD:, 32 * i : 32 * (i + 1)] = block
    for load in loads:
        load.wait()
    heads = qkv_up.shape[2] // (3 * HD)
    half = 2 * QUART
    for j, send_ref in enumerate((s0, s1, s2, s3)):
        for h in range(heads):
            for t in range(3):
                row, base = (0, QUART * t) if t < 2 else (RANK, 0)
                send_ref[row : row + RANK, base + HD * h : base + HD * (h + 1)] = qkv_up[
                    j, :, HD * (3 * h + t) : HD * (3 * h + t + 1)
                ]
        send_ref[RANK : 2 * RANK, QUART:] = proj_dn[j]
        for i, ref in enumerate((fc1_up, fc2_dn)):
            for part in range(2):
                row = RANK * (2 + 2 * i + part)
                send_ref[row : row + RANK, :] = ref[j, :, half * part : half * (part + 1)]
    for i, ref in enumerate((qkv_dn, fc1_dn, proj_up, fc2_up)):
        row, base = RANK * (i // 2), QUART * (i % 2)
        row_ref[row : row + RANK, base : base + QUART] = ref[0]
    for i, ref in enumerate((gain1, gain2)):
        row_ref[2 * RANK :, QUART * i : QUART * (i + 1)] = jnp.broadcast_to(ref[...], (RANK, QUART))


def adapter_pack(pick, *mats):
    s = lambda *shape: jax.ShapeDtypeStruct(shape, BF)
    return pl.pallas_call(
        adapter_pack_kernel,
        out_shape=(s(6 * RANK, 2 * QUART),) * 4 + (s(3 * RANK, 2 * QUART), s(128, 128)),
        in_specs=[sm()] + [arg()] * 8 + [vm()] * 4,
        out_specs=[vm()] * 6,
        scratch_shapes=[pltpu.VMEM((4,) + m.shape[1:], BF) for m in mats[:4]]
        + [pltpu.VMEM((1,) + m.shape[1:], BF) for m in mats[4:8]]
        + [pltpu.SemaphoreType.DMA((20,))],
        compiler_params=params(8),
        cost_estimate=cost(2),
        name="adapter_pack",
    )(pick, *(in_hbm(m) for m in mats[:8]), *mats[8:])


def alpha_block(k, j):
    part = k
    if j == 0:
        return [(part, 0, QUART, None)]
    return [
        (part, QUART + HBLK * (j - 1), HBLK, 0),
        (part, QUART + 3 * HBLK + HBLK * (j - 1), HBLK, 1),
    ]


def beta_block(k, j):
    core, cross = k % 2, k // 2
    base = 3 * core
    if j == 0 and not cross:
        return [(base, 0, QUART, None)]
    row = 0 if j == 0 else HBLK + QUART * (j - 1) + HBLK * cross
    return [(base + 1, row, HBLK, 0), (base + 2, row, HBLK, 1)]


def block_dst(start, flag, half):
    if flag is None:
        return start
    offset = half if flag == 0 else 1 - half
    return pl.multiple_of(start + offset * HBLK, 32)


def prep1_kernel(
    where_ref, p0, p1, p2, p3, q0, q1, q2, q3, q4, q5, a0, a1, a2, a3,
    wqkv_ref, wproj_ref, dqkv, uqkv, dproj, uproj, d1, u1, d2, u2, gain1, gain2, ups, downs,
):
    half = where_ref[1]
    for j, a in enumerate((a0, a1, a2, a3)):
        base = a.shape[0] - 6 * RANK
        part = lambda i: slice(base + RANK * i, base + RANK * (i + 1))
        for t in range(3):
            uqkv[:, D * t + QUART * j : D * t + QUART * (j + 1)] = a[
                part(t // 2), QUART * (t % 2) : QUART * (t % 2 + 1)
            ]
        dproj[:, QUART * j : QUART * (j + 1)] = a[part(1), QUART:]
        for i in range(2):
            u1[:, D * j + D // 2 * i : D * j + D // 2 * (i + 1)] = a[part(2 + i), :]
            d2[:, D * j + D // 2 * i : D * j + D // 2 * (i + 1)] = a[part(4 + i), :]
    for k, ref in enumerate((p0, p1, p2, p3)):
        for i, dst in enumerate((dqkv, d1, uproj, u2)):
            rows = slice(D + RANK * (i // 2), D + RANK * (i // 2 + 1))
            dst[:, QUART * k : QUART * (k + 1)] = ref[rows, QUART * (i % 2) : QUART * (i % 2 + 1)]
        for i, dst in enumerate((gain1, gain2)):
            row = D + 2 * RANK
            dst[:, QUART * k : QUART * (k + 1)] = ref[row : row + 1, QUART * i : QUART * (i + 1)].astype(F32)
    alpha, beta = (p0, p1, p2, p3), (q0, q1, q2, q3, q4, q5)
    for k in range(4):
        for j in range(4):
            for part, row, count, flag in alpha_block(k, j):
                rows = pl.ds(block_dst(QUART * k, flag, half), count)
                for t in range(2):
                    wqkv_ref[rows, D * t + QUART * j : D * t + QUART * (j + 1)] = alpha[part][
                        row : row + count, QUART * t : QUART * (t + 1)
                    ]
            for part, row, count, flag in beta_block(k, j):
                rows = pl.ds(block_dst(QUART * k, flag, half), count)
                wqkv_ref[rows, 2 * D + QUART * j : 2 * D + QUART * (j + 1)] = beta[part][
                    row : row + count, :QUART
                ]
                rows = pl.ds(block_dst(QUART * j, flag, half), count)
                wproj_ref[rows, QUART * k : QUART * (k + 1)] = beta[part][row : row + count, QUART:]
    for t in range(3):
        ups[t] = uqkv[:, D * t : D * (t + 1)]
    ups[3] = uproj[...]
    for k in range(4):
        downs[k] = dqkv[:, QUART * k : QUART * (k + 1)]
        downs[4 + k] = dproj[:, QUART * k : QUART * (k + 1)]

    def merge(t, carry):
        cols = pl.ds(pl.multiple_of(D * t, 128), D)
        for k in range(4):
            rows = slice(QUART * k, QUART * (k + 1))
            wqkv_ref[rows, cols] = (wqkv_ref[rows, cols].astype(F32) + tn(downs[k], ups[t])).astype(BF)
        return carry

    lax.fori_loop(0, 3, merge, 0)
    for k in range(4):
        rows = slice(QUART * k, QUART * (k + 1))
        wproj_ref[rows, :] = (wproj_ref[rows, :].astype(F32) + tn(downs[4 + k], ups[3])).astype(BF)


def prep1(where, alpha, beta, cols):
    s = lambda *shape: jax.ShapeDtypeStruct(shape, BF)
    return pl.pallas_call(
        prep1_kernel,
        out_shape=(
            s(D, 3 * D), s(D, D), s(RANK, D), s(RANK, 3 * D), s(RANK, D), s(RANK, D),
            s(RANK, D), s(RANK, 4 * D), s(RANK, 4 * D), s(RANK, D),
            jax.ShapeDtypeStruct((1, D), F32), jax.ShapeDtypeStruct((1, D), F32),
        ),
        in_specs=[sm()] + [vm()] * 14,
        out_specs=[vm()] * 12,
        scratch_shapes=[pltpu.VMEM((4, RANK, D), BF), pltpu.VMEM((8, RANK, QUART), BF)],
        compiler_params=params(24),
        cost_estimate=cost(7),
        name="attention_weights",
    )(where, *alpha, *beta, *cols)


def normalize(values):
    center = jnp.sum(values, axis=1, keepdims=True) / D
    shifted = values - center
    inv_std = lax.rsqrt(jnp.sum(shifted * shifted, axis=1, keepdims=True) / D + EPSILON)
    return shifted * inv_std, inv_std


def norm_back(grad, normed, inv_std):
    first = jnp.sum(grad, axis=1, keepdims=True) / D
    second = jnp.sum(grad * normed, axis=1, keepdims=True) / D
    return inv_std * (grad - first - normed * second)


def barrel(values, amount, left):
    for bit in (1, 2, 4, 8):
        moved = pltpu.roll(values, (128 - bit) if left else bit, 1)
        values = jnp.where((amount & bit) != 0, moved, values)
    return values


def low_half(count):
    return lax.broadcasted_iota(jnp.int32, (count, 128), 1) < HD


def pad_rows(tile):
    if tile.shape[0] == KEYS:
        return tile
    return jnp.concatenate([tile, jnp.zeros((KEYS - tile.shape[0], tile.shape[1]), tile.dtype)], axis=0)


def live_rows():
    return lax.broadcasted_iota(jnp.int32, (KEYS, 128), 0) < SLOTS


GROUP = 6
GROUP_BACK = 6


def pair_columns(pair):
    return tuple(slice(D * t + 128 * pair, D * t + 128 * (pair + 1)) for t in range(3))


def attend_window(kind, row0, qkv_ref, att_ref, exp_ref, inv_ref, rel_ref, shift_ref, keys_ref):
    count = NQ[kind]
    rows = pl.ds(row0, count)
    low_q, low_k = low_half(count), low_half(KEYS)
    live = live_rows()
    ones = jnp.where(live, 1.0, 0.0).astype(BF)
    amount = shift_ref[kind, :count, :]
    onehot = keys_ref[kind]
    rel_mat = rel_ref[...]
    for first in range(0, D // 128, GROUP):
        pairs = range(first, first + GROUP)
        heads = [(pair, odd) for pair in pairs for odd in range(2)]
        q_tile = {p: qkv_ref[rows, pair_columns(p)[0]] for p in pairs}
        rel = {p: nn(q_tile[p], rel_mat) for p in pairs}
        rel = {p: barrel(rel[p], amount, True).astype(BF) for p in pairs}
        k_tile = {p: pad_rows(qkv_ref[rows, pair_columns(p)[1]] * BF(HD**-0.5)) for p in pairs}
        scores = {}
        for p, odd in heads:
            if odd:
                q_aug, k_aug = jnp.where(low_q, rel[p], q_tile[p]), jnp.where(low_k, onehot, k_tile[p])
            else:
                q_aug, k_aug = jnp.where(low_q, q_tile[p], rel[p]), jnp.where(low_k, k_tile[p], onehot)
            scores[p, odd] = nt(q_aug, k_aug)
        top = {h: jnp.max(scores[h], axis=1, keepdims=True) for h in heads}
        exponent = {h: jnp.exp(scores[h] - top[h]).astype(BF) for h in heads}
        both = {}
        for p, odd in heads:
            exp_ref[2 * p + odd, rows, :] = exponent[p, odd]
            v_tile = pad_rows(qkv_ref[rows, pair_columns(p)[2]])
            if kind == FULL:
                v_tile = jnp.where(live, v_tile, 0).astype(BF)
            v_aug = jnp.where(low_k, ones, v_tile) if odd else jnp.where(low_k, v_tile, ones)
            both[p, odd] = nn(exponent[p, odd], v_aug)
        for p in pairs:
            cols = pair_columns(p)[0]
            inverse = 1.0 / pltpu.roll(jnp.where(low_q, both[p, 1], both[p, 0]), HD, 1)
            inv_ref[rows, cols] = inverse
            att_ref[rows, cols] = (jnp.where(low_q, both[p, 0], both[p, 1]) * inverse).astype(BF)


PARTS = ((FULL, FULL), (FULL, FULL), (RIGHT, BOTTOM, CORNER))
PART_ROWS = tuple(sum(NQ[kind] for kind in part) for part in PARTS)
PART_OFFS = (0, PART_ROWS[0], PART_ROWS[0] + PART_ROWS[1])


TAIL = ((0, 576), (576, ROWS))


def qkv_kernel(
    x0, x1, x2, x3, gain_ref, w_hbm, x_hbm, hid_hbm, qkv_a, qkv_b, qkv_c,
    x_ref, hid_ref, rows_ref, w_ref, qkv_ref, sem, out_sem,
):
    loads = [
        pltpu.make_async_copy(w_hbm.at[:, D * t : D * (t + 1)], w_ref.at[t], sem.at[t]) for t in range(3)
    ]
    for load in loads:
        load.start()
    join_pieces((x0, x1, x2, x3), x_ref)
    kept = [
        pltpu.make_async_copy(src, dst, sem.at[3 + i])
        for i, (src, dst) in enumerate(((x_ref, x_hbm), (hid_ref, hid_hbm)))
    ]
    kept[0].start()
    gain = gain_ref[...]

    def norm_step(i, carry):
        rows = pl.ds(pl.multiple_of(i * 112, 16), 112)
        normed, _ = normalize(x_ref[rows, :].astype(F32))
        hidden = (normed * gain).astype(BF)
        rows_ref[rows, :] = hidden
        hid_ref[rows, :] = hidden
        return carry

    lax.fori_loop(0, ROWS // 112, norm_step, 0)
    for w in range(4):
        hid_ref[FULLR * w + SLOTS : FULLR * (w + 1), :] = jnp.zeros((FULLR - SLOTS, D), BF)
    kept[1].start()
    for load in loads:
        load.wait()

    def stores(t):
        cols = pl.ds(pl.multiple_of(D * t, 128), D)
        return [
            pltpu.make_async_copy(
                qkv_ref.at[t, pl.ds(offset, count), :], out.at[:, cols], out_sem.at[t, i]
            )
            for i, (out, offset, count) in enumerate(zip((qkv_a, qkv_b, qkv_c), PART_OFFS, PART_ROWS))
        ]

    def project_step(t, carry):
        qkv_ref[t] = nn(rows_ref[...], w_ref[t]).astype(BF)
        for store in stores(t):
            store.start()
        return carry

    lax.fori_loop(0, 3, project_step, 0)
    for t in range(3):
        for store in stores(t):
            store.wait()
    for store in kept:
        store.wait()


def qkv_rows(pieces, gain, wqkv):
    s = lambda *shape: jax.ShapeDtypeStruct(shape, BF)
    return pl.pallas_call(
        qkv_kernel,
        out_shape=(s(ROWS, D), s(ROWS, D)) + tuple(s(n, 3 * D) for n in PART_ROWS),
        in_specs=[vm()] * 5 + [hbm()],
        out_specs=[hbm()] * 5,
        scratch_shapes=[
            pltpu.VMEM((ROWS, D), BF), pltpu.VMEM((ROWS, D), BF), pltpu.VMEM((ROWS, D), BF),
            pltpu.VMEM((3, D, D), BF), pltpu.VMEM((3, ROWS, D), BF),
            pltpu.SemaphoreType.DMA((5,)), pltpu.SemaphoreType.DMA((3, 3)),
        ],
        compiler_params=params(32),
        cost_estimate=cost(10),
        name="norm_and_qkv",
    )(*pieces, gain, wqkv)


def attention_kernel(qkv_ref, rel_ref, shift_ref, keys_ref, att_ref, exp_ref, inv_ref, *, kinds):
    refs = (qkv_ref, att_ref, exp_ref, inv_ref, rel_ref, shift_ref, keys_ref)
    if kinds[0] == FULL:

        def step(w, carry):
            attend_window(FULL, pl.multiple_of(w * FULLR, 16), *refs)
            return carry

        lax.fori_loop(0, len(kinds), step, 0)
    else:
        row = 0
        for kind in kinds:
            attend_window(kind, row, *refs)
            row += NQ[kind]


def attention(part, qkv, rel, shift, keys):
    rows = PART_ROWS[part]
    s = lambda *shape, dtype=BF: jax.ShapeDtypeStruct(shape, dtype)
    return pl.pallas_call(
        functools.partial(attention_kernel, kinds=PARTS[part]),
        out_shape=(s(rows, D), s(D // HD, rows, KEYS), s(rows, D, dtype=F32)),
        in_specs=[vm()] * 4,
        out_specs=[vm()] * 3,
        compiler_params=params(24),
        cost_estimate=cost(10),
        name="attention_forward",
    )(qkv, rel, shift, keys)


def project_kernel(x_ref, att_a, att_b, att_c, wproj_ref, middle_ref):
    for ref, offset, count in zip((att_a, att_b, att_c), PART_OFFS, PART_ROWS):
        rows = slice(offset, offset + count)
        middle_ref[rows, :] = x_ref[rows, :].astype(F32) + nn(ref[...], wproj_ref[...])


def project(x, atts, wproj):
    return pl.pallas_call(
        project_kernel,
        out_shape=jax.ShapeDtypeStruct((ROWS, D), F32),
        in_specs=[vm()] * 5,
        out_specs=vm(),
        compiler_params=params(20),
        cost_estimate=cost(5),
        name="projection",
    )(x, *atts, wproj)


CHUNK = 512
LOCK = 1


def mlp_kernel(
    where_ref, middle_ref, g0, g1, g2, g3, gain_ref,
    p0, p1, p2, p3, q0, q1, q2, q3, q4, q5, d1, u1, d2, u2,
    o0, o1, o2, gmid_ref, down1, up1, down2, up2,
    gm_ref, out_rows, h2_ref, acc_mlp, acc_gh, gu1, ad2, w1_ref, w2_ref, downs, sem,
):
    half = where_ref[1]
    copies = []

    def fetch(src, dst):
        copies.append(pltpu.make_async_copy(src, dst, sem.at[len(copies)]))
        copies[-1].start()

    alpha, beta = (p0, p1, p2, p3), (q0, q1, q2, q3, q4, q5)
    for k in range(4):
        for j in range(4):
            for part, row, count, flag in alpha_block(k, j):
                rows = pl.ds(block_dst(QUART * k, flag, half), count)
                fetch(alpha[part].at[row : row + count, :], w1_ref.at[rows, D * j : D * (j + 1)])
            for part, row, count, flag in beta_block(k, j):
                rows = pl.ds(block_dst(QUART * k, flag, half), count)
                fetch(beta[part].at[row : row + count, :], w2_ref.at[rows, D * j : D * (j + 1)])
    join_pieces((g0, g1, g2, g3), gm_ref)
    for k in range(4):
        downs[k] = d1[:, QUART * k : QUART * (k + 1)]
        downs[4 + k] = u2[:, QUART * k : QUART * (k + 1)]
    for copy in copies:
        copy.wait()

    def merge(j, carry):
        cols = pl.ds(pl.multiple_of(D * j, 128), D)
        for k in range(4):
            rows = slice(QUART * k, QUART * (k + 1))
            w1_ref[rows, cols] = (w1_ref[rows, cols].astype(F32) + tn(downs[k], u1[:, cols])).astype(BF)
            w2_ref[rows, cols] = (w2_ref[rows, cols].astype(F32) + tn(downs[4 + k], d2[:, cols])).astype(BF)
        return carry

    lax.fori_loop(0, 4, merge, 0)
    gain = gain_ref[...]
    down1[...] = jnp.zeros_like(down1)
    up1[...] = jnp.zeros_like(up1)
    down2[...] = jnp.zeros_like(down2)
    up2[...] = jnp.zeros_like(up2)

    def tile_step(t, carry):
        rows = pl.ds(pl.multiple_of(t * HALF, 16), HALF)
        normed, _ = normalize(middle_ref[rows, :])
        h2 = (normed * gain).astype(BF)
        h2_ref[...] = h2
        gm = gm_ref[rows, :]
        ad1 = nt(d1[...], h2).astype(BF)
        gu2 = nt(u2[...], gm).astype(BF)
        acc_mlp[...] = jnp.zeros_like(acc_mlp)
        acc_gh[...] = jnp.zeros_like(acc_gh)
        gu1[...] = jnp.zeros_like(gu1)
        ad2[...] = jnp.zeros_like(ad2)

        def chunk_step(c, inner_carry):
            spans = [
                pl.ds(pl.multiple_of((c * LOCK + i) * CHUNK, CHUNK), CHUNK) for i in range(LOCK)
            ]
            h2 = h2_ref[...]
            gm = gm_ref[rows, :]
            inner = [nn(h2, w1_ref[:, span]) for span in spans]
            gact = [nn(gm, w2_ref[:, span]) for span in spans]
            act, ginner = [], []
            for i in range(LOCK):
                half = 0.5 * (1.0 + lax.erf(inner[i] * 2**-0.5))
                act.append((inner[i] * half).astype(BF))
                slope = half + inner[i] * (jnp.exp(-0.5 * inner[i] * inner[i]) * (2 * np.pi) ** -0.5)
                ginner.append((gact[i] * slope).astype(BF))
            for i, span in enumerate(spans):
                acc_mlp[...] += nt(act[i], w2_ref[:, span])
                acc_gh[...] += nt(ginner[i], w1_ref[:, span])
                up1[:, span] += nn(ad1, ginner[i])
                gu1[...] += nt(u1[:, span], ginner[i])
                ad2[...] += nt(d2[:, span], act[i])
                down2[:, span] += nn(gu2, act[i])
            return inner_carry

        lax.fori_loop(0, 4 * D // (CHUNK * LOCK), chunk_step, 0)
        down1[...] += nn(gu1[...].astype(BF), h2_ref[...])
        up2[...] += nn(ad2[...].astype(BF), gm_ref[rows, :])
        middle = middle_ref[rows, :]
        out_rows[rows, :] = (middle + acc_mlp[...]).astype(BF)
        normed, inv_std = normalize(middle)
        gmid_ref[rows, :] = gm_ref[rows, :].astype(F32) + norm_back(acc_gh[...] * gain, normed, inv_std)
        return carry

    lax.fori_loop(0, 2, tile_step, 0)
    split_pieces(out_rows, (o0, o1, o2))


def mlp(where, middle, pieces, gain, alpha, beta, d1, u1, d2, u2):
    s = lambda *shape, dtype=F32: jax.ShapeDtypeStruct(shape, dtype)
    return pl.pallas_call(
        mlp_kernel,
        out_shape=pieces_of(ROWS)
        + (s(ROWS, D), s(RANK, D), s(RANK, 4 * D), s(RANK, 4 * D), s(RANK, D)),
        in_specs=[sm()] + [vm()] * 6 + [pl.BlockSpec(memory_space=pl.ANY)] * 10 + [vm()] * 4,
        out_specs=[vm()] * 8,
        scratch_shapes=[
            pltpu.VMEM((ROWS, D), BF), pltpu.VMEM((ROWS, D), BF), pltpu.VMEM((HALF, D), BF),
            pltpu.VMEM((HALF, D), F32), pltpu.VMEM((HALF, D), F32),
            pltpu.VMEM((RANK, HALF), F32), pltpu.VMEM((RANK, HALF), F32),
            pltpu.VMEM((D, 4 * D), BF), pltpu.VMEM((D, 4 * D), BF), pltpu.VMEM((8, RANK, QUART), BF),
            pltpu.SemaphoreType.DMA((4 * 4 * 4,)),
        ],
        compiler_params=params(48),
        cost_estimate=cost(48),
        name="mlp_forward_backward",
    )(where, middle, *pieces, gain, *alpha, *beta, d1, u1, d2, u2)


def attend_back_window(
    kind, row0, qkv_ref, att_ref, exp_ref, inv_ref, gatt_ref, gqkv_ref, rel_ref, shift_ref, keys_ref
):
    count = NQ[kind]
    rows = pl.ds(row0, count)
    low_q, low_k = low_half(count), low_half(KEYS)
    live = live_rows()
    lane_k = lax.broadcasted_iota(jnp.int32, (KEYS, 128), 1) % HD
    lane_q = lax.broadcasted_iota(jnp.int32, (count, 128), 1) % HD
    ones = jnp.where(live & (lane_k < 2), 1.0, 0.0).astype(BF)
    across = jnp.where(
        low_half(128) != (lax.broadcasted_iota(jnp.int32, (128, 128), 0) < HD), -1.0, 0.0
    ).astype(BF)
    amount = shift_ref[kind, :count, :]
    onehot = keys_ref[kind]
    rel_mat = rel_ref[...]
    for first in range(0, D // 128, GROUP_BACK):
        pairs = range(first, first + GROUP_BACK)
        heads = [(pair, odd) for pair in pairs for odd in range(2)]
        go_tile = {
            p: (gatt_ref[rows, pair_columns(p)[0]].astype(F32) * inv_ref[rows, pair_columns(p)[0]]).astype(BF)
            for p in pairs
        }
        delta = {
            p: nn((go_tile[p].astype(F32) * att_ref[rows, pair_columns(p)[0]].astype(F32)).astype(BF), across)
            for p in pairs
        }
        go_t = {p: go_tile[p].T for p in pairs}
        gv = {}
        for p, odd in heads:
            gv[p, odd] = nn(go_t[p][HD * odd : HD * (odd + 1), :], exp_ref[2 * p + odd, rows, :])
        gscore = {}
        for p in pairs:
            high = delta[p].astype(BF)
            rest = (delta[p] - high.astype(F32)).astype(BF)
            low_delta = jnp.where(lane_q == 0, high, jnp.where(lane_q == 1, rest, 0)).astype(BF)
            v_tile = pad_rows(qkv_ref[rows, pair_columns(p)[2]])
            if kind == FULL:
                v_tile = jnp.where(live, v_tile, 0).astype(BF)
            gscore[p, 0] = nt(jnp.where(low_q, go_tile[p], low_delta), jnp.where(low_k, v_tile, ones))
            gscore[p, 1] = nt(jnp.where(low_q, low_delta, go_tile[p]), jnp.where(low_k, ones, v_tile))
        q_t = {p: qkv_ref[rows, pair_columns(p)[0]].T for p in pairs}
        gs = {(p, odd): (exp_ref[2 * p + odd, rows, :].astype(F32) * gscore[p, odd]).astype(BF) for p, odd in heads}
        gk = {(p, odd): nn(q_t[p][HD * odd : HD * (odd + 1), :], gs[p, odd]) for p, odd in heads}
        gq = {}
        for p in pairs:
            k_tile = pad_rows(qkv_ref[rows, pair_columns(p)[1]] * BF(HD**-0.5))
            gq[p, 0] = nn(gs[p, 0], jnp.where(low_k, k_tile, onehot))
            gq[p, 1] = nn(gs[p, 1], jnp.where(low_k, onehot, k_tile))
        sums = {p: barrel(jnp.where(low_q, gq[p, 1], gq[p, 0]), amount, False).astype(BF) for p in pairs}
        for p in pairs:
            cols, kcols, vcols = pair_columns(p)
            gv_tile = jnp.concatenate([gv[p, 0], gv[p, 1]], axis=0).astype(BF).T
            gqkv_ref[rows, vcols] = gv_tile[:count, :]
            gk_tile = (jnp.concatenate([gk[p, 0], gk[p, 1]], axis=0) * HD**-0.5).astype(BF).T
            gqkv_ref[rows, kcols] = gk_tile[:count, :]
            gqkv_ref[rows, cols] = (jnp.where(low_q, gq[p, 0], gq[p, 1]) + nt(sums[p], rel_mat)).astype(BF)


def attention_back_kernel(
    gmid_hbm, hid_hbm, qkv_a, qkv_b, qkv_c, att_a, att_b, att_c, exp_a, exp_b, exp_c, inv_a, inv_b, inv_c,
    wproj_ref, rel_ref, shift_ref, keys_ref, dqkv, uqkv, dproj, uproj,
    gqkv_hbm, down_q, up_q, down_p, up_p,
    gmid_ref, hid_ref, qkv_ref, att_ref, exp_ref, inv_ref, gqkv_ref, gb_ref, gatt_ref, sem, out_sem,
):
    spans = [pl.ds(offset, count) for offset, count in zip(PART_OFFS, PART_ROWS)]
    pairs = [(gmid_hbm, gmid_ref)]
    for part, srcs in enumerate(
        ((qkv_a, inv_a, att_a, exp_a), (qkv_b, inv_b, att_b, exp_b), (qkv_c, inv_c, att_c, exp_c))
    ):
        rows = spans[part]
        for src, dst in zip(srcs, (qkv_ref, inv_ref, att_ref)):
            pairs.append((src, dst.at[rows, :]))
        pairs.append((srcs[3], exp_ref.at[:, rows, :]))
    pairs.append((hid_hbm, hid_ref))
    loads = [pltpu.make_async_copy(src, dst, sem.at[i]) for i, (src, dst) in enumerate(pairs)]
    for load in loads:
        load.start()

    def wait_part(part):
        for load in loads[1 + 4 * part : 5 + 4 * part]:
            load.wait()

    stores = [
        pltpu.make_async_copy(gqkv_ref.at[rows, :], gqkv_hbm.at[rows, :], out_sem.at[i])
        for i, rows in enumerate(spans)
    ]
    loads[0].wait()
    gb_ref[...] = gmid_ref[...].astype(BF)
    gatt_ref[...] = nt(gb_ref[...], wproj_ref[...]).astype(BF)
    refs = (qkv_ref, att_ref, exp_ref, inv_ref, gatt_ref, gqkv_ref, rel_ref, shift_ref, keys_ref)

    def step(w, carry):
        for part in range(2):

            @pl.when(w == 2 * part)
            def _():
                wait_part(part)

        attend_back_window(FULL, pl.multiple_of(w * FULLR, 16), *refs)
        return carry

    lax.fori_loop(0, 4, step, 0)
    stores[0].start()
    stores[1].start()
    wait_part(2)
    for kind in (RIGHT, BOTTOM, CORNER):
        attend_back_window(kind, OFFS[kind], *refs)
    stores[2].start()
    up_p[...] = nn(nt(dproj[...], att_ref[...]).astype(BF), gb_ref[...])
    down_p[...] = nn(nt(uproj[...], gb_ref[...]).astype(BF), att_ref[...])
    loads[-1].wait()
    up_q[...] = nn(nt(dqkv[...], hid_ref[...]).astype(BF), gqkv_ref[...])
    down_q[...] = nn(nt(uqkv[...], gqkv_ref[...]).astype(BF), hid_ref[...])
    for store in stores:
        store.wait()


def attention_back(gmid, hid, qkvs, atts, exps, invs, wproj, rel, shift, keys, dqkv, uqkv, dproj, uproj):
    s = lambda *shape, dtype=F32: jax.ShapeDtypeStruct(shape, dtype)
    return pl.pallas_call(
        attention_back_kernel,
        out_shape=(s(ROWS, 3 * D, dtype=BF), s(RANK, D), s(RANK, 3 * D), s(RANK, D), s(RANK, D)),
        in_specs=[hbm()] * 14 + [vm()] * 8,
        out_specs=[hbm()] + [vm()] * 4,
        scratch_shapes=[
            pltpu.VMEM((ROWS, D), F32), pltpu.VMEM((ROWS, D), BF), pltpu.VMEM((ROWS, 3 * D), BF),
            pltpu.VMEM((ROWS, D), BF), pltpu.VMEM((D // HD, ROWS, KEYS), BF), pltpu.VMEM((ROWS, D), F32),
            pltpu.VMEM((ROWS, 3 * D), BF), pltpu.VMEM((ROWS, D), BF), pltpu.VMEM((ROWS, D), BF),
            pltpu.SemaphoreType.DMA((14,)), pltpu.SemaphoreType.DMA((3,)),
        ],
        compiler_params=params(52),
        cost_estimate=cost(28),
        name="attention_backward",
    )(gmid, hid, *qkvs, *atts, *exps, *invs, wproj, rel, shift, keys, dqkv, uqkv, dproj, uproj)


def token_grad_kernel(gmid_hbm, x_hbm, gqkv_hbm, gain_ref, wqkv_ref, o0, o1, o2,
                      gmid_ref, x_ref, gqkv_ref, gh_ref, out_rows, sem, *, low, high):
    span = pl.ds(low, high - low)
    copies = [
        pltpu.make_async_copy(src.at[span, :], dst, sem.at[i])
        for i, (src, dst) in enumerate(((gqkv_hbm, gqkv_ref), (x_hbm, x_ref), (gmid_hbm, gmid_ref)))
    ]
    for copy in copies:
        copy.start()
    copies[0].wait()
    gh_ref[...] = nt(gqkv_ref[...], wqkv_ref[...])
    copies[1].wait()
    copies[2].wait()
    gain = gain_ref[...]
    step = (high - low) // 2

    def norm_step(i, carry):
        rows = pl.ds(pl.multiple_of(i * step, 16), step)
        normed, inv_std = normalize(x_ref[rows, :].astype(F32))
        back = norm_back(gh_ref[rows, :] * gain, normed, inv_std)
        out_rows[rows, :] = (gmid_ref[rows, :] + back).astype(BF)
        return carry

    lax.fori_loop(0, 2, norm_step, 0)
    split_pieces(out_rows, (o0, o1, o2))


def token_grad(gmid, x, gqkv, gain, wqkv, low, high):
    count = high - low
    return pl.pallas_call(
        functools.partial(token_grad_kernel, low=low, high=high),
        out_shape=pieces_of(count),
        in_specs=[hbm(), hbm(), hbm(), vm(), vm()],
        out_specs=[vm()] * 3,
        scratch_shapes=[
            pltpu.VMEM((count, D), F32), pltpu.VMEM((count, D), BF), pltpu.VMEM((count, 3 * D), BF),
            pltpu.VMEM((count, D), F32), pltpu.VMEM((count, D), BF), pltpu.SemaphoreType.DMA((3,)),
        ],
        compiler_params=params(28),
        cost_estimate=cost(8),
        name="token_gradient",
    )(gmid, x, gqkv, gain, wqkv)


def grad_pack_kernel(where_ref, down_q, up_q, down_p, up_p, down1, up1, down2, up2, o0, o1, o2, o3, buf_ref):
    mine = where_ref[0]
    for k in range(4):
        for i, ref in enumerate((down_q, down1, up_p, up2)):
            buf_ref[k, :RANK, QUART * i : QUART * (i + 1)] = ref[:, QUART * k : QUART * (k + 1)]
    for dest in range(4):
        k = jnp.bitwise_xor(mine, dest)
        ranks = slice(RANK // 4 * dest, RANK // 4 * (dest + 1))
        for j in range(4):
            base = RANK + 12 * j
            for t in range(3):
                buf_ref[k, base : base + 4, QUART * t : QUART * (t + 1)] = up_q[
                    ranks, D * t + QUART * j : D * t + QUART * (j + 1)
                ]
            buf_ref[k, base : base + 4, 3 * QUART :] = down_p[ranks, QUART * j : QUART * (j + 1)]
            buf_ref[k, base + 4 : base + 8, :] = up1[ranks, D * j : D * (j + 1)]
            buf_ref[k, base + 8 : base + 12, :] = down2[ranks, D * j : D * (j + 1)]
    for k, out in enumerate((o0, o1, o2, o3)):
        out[...] = buf_ref[k].astype(BF)


def grad_pack(where, *grads):
    return pl.pallas_call(
        grad_pack_kernel,
        out_shape=(jax.ShapeDtypeStruct((4 * RANK, D), BF),) * 4,
        in_specs=[sm()] + [vm()] * 8,
        out_specs=[vm()] * 4,
        scratch_shapes=[pltpu.VMEM((4, 4 * RANK, D), F32)],
        compiler_params=params(8),
        cost_estimate=cost(2),
        name="adapter_grad_pack",
    )(where, *grads)


def grad_sum_kernel(g0, g1, g2, g3, o0, o1, o2, o3, buf_ref):
    total = g0[...].astype(F32) + g1[...].astype(F32) + g2[...].astype(F32) + g3[...].astype(F32)
    buf_ref[...] = jnp.zeros_like(buf_ref)
    buf_ref[:RANK, :] = total[:RANK, :]
    for j, out in enumerate((o0, o1, o2, o3)):
        buf_ref[RANK : RANK + 12, :] = total[RANK + 12 * j : RANK + 12 * (j + 1), :]
        out[...] = buf_ref[...].astype(BF)


def grad_sum(pieces):
    return pl.pallas_call(
        grad_sum_kernel,
        out_shape=(jax.ShapeDtypeStruct((2 * RANK, D), BF),) * 4,
        in_specs=[vm()] * 4,
        out_specs=[vm()] * 4,
        scratch_shapes=[pltpu.VMEM((2 * RANK, D), F32)],
        compiler_params=params(4),
        cost_estimate=cost(2),
        name="adapter_grad_sum",
    )(*pieces)


def grad_adapters_kernel(index_ref, x_ref, qkv_dn, fc1_dn, proj_up, fc2_up, rest_ref, acc_ref):
    acc_ref[...] = jnp.zeros_like(acc_ref)

    def add(i, carry):
        acc_ref[index_ref[i]] += x_ref[i].astype(F32)
        return carry

    lax.fori_loop(0, x_ref.shape[0], add, 0)
    for i, ref in enumerate((qkv_dn, fc1_dn, proj_up, fc2_up)):
        ref[...] = acc_ref[:, :RANK, QUART * i : QUART * (i + 1)]
    rest_ref[...] = acc_ref[:, RANK:, :].astype(BF)


def grad_adapters(index, x):
    s = lambda n, dtype=F32: jax.ShapeDtypeStruct((ADAPT, RANK, n), dtype)
    return pl.pallas_call(
        grad_adapters_kernel,
        out_shape=(s(QUART), s(QUART), s(QUART), s(QUART), s(D, BF)),
        in_specs=[sm(), vm()],
        out_specs=[vm()] * 5,
        scratch_shapes=[pltpu.VMEM((ADAPT, 2 * RANK, D), F32)],
        compiler_params=params(8),
        cost_estimate=cost(2),
        name="adapter_grad_by_adapter",
    )(index, x)


def grad_join_kernel(where_ref, r0, r1, r2, r3, qkv_up, proj_dn, fc1_up, fc2_dn, buf_ref):
    mine = where_ref[0]
    heads = qkv_up.shape[2] // (3 * HD)
    for k, ref in enumerate((r0, r1, r2, r3)):
        buf_ref[jnp.bitwise_xor(mine, k)] = ref[...].astype(F32)
    for source in range(4):
        ranks = slice(RANK // 4 * source, RANK // 4 * (source + 1))
        for h in range(heads):
            for t in range(3):
                qkv_up[:, ranks, HD * (3 * h + t) : HD * (3 * h + t + 1)] = buf_ref[
                    source, :, 0:4, QUART * t + HD * h : QUART * t + HD * (h + 1)
                ]
        proj_dn[:, ranks, :] = buf_ref[source, :, 0:4, 3 * QUART :]
        fc1_up[:, ranks, :] = buf_ref[source, :, 4:8, :]
        fc2_dn[:, ranks, :] = buf_ref[source, :, 8:12, :]


def grad_join(where, pieces):
    s = lambda n: jax.ShapeDtypeStruct((ADAPT, RANK, n), F32)
    return pl.pallas_call(
        grad_join_kernel,
        out_shape=(s(3 * QUART), s(QUART), s(D), s(D)),
        in_specs=[sm()] + [vm()] * 4,
        out_specs=[vm()] * 4,
        scratch_shapes=[pltpu.VMEM((4, ADAPT, RANK, D), F32)],
        compiler_params=params(12),
        cost_estimate=cost(2),
        name="adapter_grad_join",
    )(where, *pieces)


def flip(values, axis, distance):
    size = lax.axis_size(axis)
    return lax.ppermute(values, axis, [(i, i ^ distance) for i in range(size)])


def send_rows(pieces, *deps):
    own, near, pair = pieces
    if deps:
        near, = after((near,), *deps)
    return [own, flip(near, "row", 1), flip(pair, "row", 2)]


def hand_on(pieces, *deps):
    own, near, crossed = pieces
    if deps:
        near, crossed = after((near, crossed), *deps)
    return [own, near, crossed, flip(crossed, "row", 1)]


def exchange(slots, axis):
    return [slots[0]] + [flip(slots[k], axis, k) for k in range(1, 4)]


def after(values, *deps):
    return lax.optimization_barrier((tuple(values), deps))[0]


def col_halves(half):
    return jnp.concatenate([flip(half, "col", j) for j in range(1, 4)], axis=0)


def col_pairs(half, other_row):
    two = jnp.concatenate([half, other_row], axis=0)
    return jnp.concatenate([other_row] + [flip(two, "col", j) for j in range(1, 4)], axis=0)


def body(
    tokens, grad_out, adapter_index, norm1_gain, norm2_gain, qkv_weight, proj_weight, fc1_weight, fc2_weight,
    rel_h, rel_w, qkv_down, qkv_up, proj_down, proj_up, fc1_down, fc1_up, fc2_down, fc2_up,
):
    members = lax.axis_size("col")
    batches = lax.axis_size("dp")
    row_index, col_index, dp_index = lax.axis_index("row"), lax.axis_index("col"), lax.axis_index("dp")
    half = dp_index % 2
    where = jnp.stack([row_index, half]).astype(jnp.int32)
    slot_images = (
        jnp.bitwise_xor(dp_index, jnp.arange(batches, dtype=jnp.int32))[:, None] * members
        + jnp.bitwise_xor(col_index, jnp.arange(members, dtype=jnp.int32))[None, :]
    ).reshape(-1)
    slot_adapters = jnp.sum(
        jnp.where(
            slot_images[:, None] == jnp.arange(adapter_index.shape[0], dtype=jnp.int32)[None, :],
            adapter_index[:, 0][None, :],
            0,
        ),
        axis=1,
    )
    pick = jnp.concatenate([slot_adapters[:4], half[None]]).astype(jnp.int32)
    swap = lambda m: jnp.swapaxes(m, 1, 2)

    shift, keys = jnp.asarray(SHIFT_NP), jnp.asarray(KEYS_NP)

    *token_slots, alpha_own, beta_own, alpha_half, cross, fc1_half, fc2_half = front(
        where, tokens, qkv_weight, proj_weight, fc1_weight, fc2_weight
    )
    crossed = flip(cross, "row", 2)
    beta_half, b0 = cross[:HBLK], crossed[:HBLK]
    c0 = jnp.concatenate([crossed[HBLK : 2 * HBLK], crossed[2 * HBLK :]], axis=1)
    alpha_near = col_halves(alpha_half)
    x_pieces = send_rows(token_slots, crossed)
    *send, row_adapters, rel = adapter_pack(
        pick, qkv_up, swap(proj_down), fc1_up, swap(fc2_down), swap(qkv_down), swap(fc1_down), proj_up, fc2_up,
        norm1_gain.reshape(1, -1), norm2_gain.reshape(1, -1), rel_h, rel_w,
    )
    beta_sent = [jnp.concatenate([beta_half, b0, send[j]], axis=0) for j in range(1, 4)]
    beta_got = [flip(m, "col", j) for j, m in enumerate(beta_sent, 1)]
    alpha_near, x_pieces[1] = after((alpha_near, x_pieces[1]))
    alpha_far = flip(alpha_near, "dp", 1)
    g = jnp.concatenate([alpha_own, alpha_near, alpha_far, row_adapters], axis=0)
    g, *x_pieces = after((g, *x_pieces))
    gy = flip(g, "row", 2)
    grad_slots = pack(where, grad_out)
    *beta_got, _ = after((*beta_got, grad_slots[0]))
    beta_near = jnp.concatenate([b0] + [m[:QUART] for m in beta_got], axis=0)
    col_adapters = [send[0]] + beta_got
    beta_far = flip(beta_near, "dp", 1)
    x_pieces = hand_on(x_pieces)

    g1, own1, near1 = (flip(m, "row", 1) for m in (g, beta_own, beta_near))
    fc1_half, = after((fc1_half,), g1, own1, near1, x_pieces[3])
    fc1_near = [flip(fc1_half, "col", j) for j in range(1, 4)]
    gy, beta_far, fc2_half, c0 = after((gy, beta_far, fc2_half, c0), *fc1_near)
    fc2_two = jnp.concatenate([fc2_half, c0], axis=0)
    fc2_near = [flip(fc2_two, "col", j) for j in range(1, 4)]
    gy1, far1 = flip(gy, "row", 1), flip(beta_far, "row", 1)
    *grad_slots, fc1_near = after((*grad_slots, jnp.concatenate(fc1_near, axis=0)), gy1, far1)
    fc1_far = flip(fc1_near, "dp", 1)
    g_pieces = [grad_slots[0], grad_slots[1], flip(grad_slots[2], "row", 2)]
    wqkv, wproj, dqkv, uqkv, dproj, uproj, d1, u1, d2, u2, gain1, gain2 = prep1(
        where, (g, g1, gy, gy1), (beta_own, beta_near, beta_far, own1, near1, far1), col_adapters
    )
    h = jnp.concatenate([fc1_weight, fc1_near, fc1_far], axis=0)
    wqkv, h = after((wqkv, h), g_pieces[2])
    hy = flip(h, "row", 2)
    x, hid, *qkvs = qkv_rows(x_pieces, gain1, wqkv)
    *qkvs, n1, n2, n3 = after((*qkvs, *fc2_near))
    fc2_near = jnp.concatenate([c0, n1, n2, n3], axis=0)
    fc2_far = flip(fc2_near, "dp", 1)
    fc2_ahead = [flip(m, "row", 1) for m in (fc2_weight, fc2_near)]
    g_pieces[1], = after((g_pieces[1],), qkvs[0])
    g_pieces[1] = flip(g_pieces[1], "row", 1)
    g_pieces = hand_on(g_pieces, qkvs[0])
    part0 = attention(0, qkvs[0], rel, shift, keys)
    qkv1, = after((qkvs[1],), part0[0], g_pieces[3], *fc2_ahead)
    part1 = attention(1, qkv1, rel, shift, keys)
    qkv2, _ = after((qkvs[2], part1[0]))
    part2 = attention(2, qkv2, rel, shift, keys)
    atts, exps, invs = zip(part0, part1, part2)
    atts = list(atts)
    atts[2], hy = after((atts[2], hy))
    alpha2 = [h, flip(h, "row", 1), hy, flip(hy, "row", 1)]
    middle = project(x, atts, wproj)
    middle, fc2_far = after((middle, fc2_far))
    beta2 = [fc2_weight, fc2_near, fc2_far, *fc2_ahead, flip(fc2_far, "row", 1)]

    *out_slots, gmid, down1, up1, down2, up2 = mlp(where, middle, g_pieces, gain2, alpha2, beta2, d1, u1, d2, u2)
    out_pieces = send_rows(out_slots)
    gqkv, down_q, up_q, down_p, up_p = attention_back(
        gmid, hid, qkvs, atts, exps, invs, wproj, rel, shift, keys, dqkv, uqkv, dproj, uproj
    )
    out_pieces = hand_on(out_pieces, gqkv)
    gqkv, down_q, up_q, down_p, up_p = after((gqkv, down_q, up_q, down_p, up_p), *out_pieces[:3])
    packed = grad_pack(where, down_q, up_q, down_p, up_p, down1, up1, down2, up2)
    *packed, gqkv = after((*packed, gqkv))
    row_sums = exchange(packed, "row")
    back0 = token_grad(gmid, x, gqkv, gain1, wqkv, *TAIL[0])
    *row_sums, gqkv, b0, b1, b2 = after((*row_sums, gqkv, *back0))
    back_pieces = send_rows((b0, b1, b2))
    summed = grad_sum(row_sums)
    *summed, gqkv = after((*summed, gqkv))
    images = exchange(summed, "col")
    back1 = token_grad(gmid, x, gqkv, gain1, wqkv, *TAIL[1])
    last_pieces = send_rows(back1)
    *images, near, crossed = after((*images, *back_pieces[1:]), back1[0])
    back_pieces = hand_on([back_pieces[0], near, crossed])
    images = jnp.stack(images)
    images, *out_pieces = after((images, *out_pieces))
    step = 1
    while step < batches:
        images = jnp.concatenate([images, flip(images, "dp", step)], axis=0)
        step *= 2
    result = unpack(where, out_pieces, BF)
    images, = after((images,), result)
    qkv_dn, fc1_dn, proj_upg, fc2_upg, rest = grad_adapters(slot_adapters.astype(jnp.int32), images)
    near_rest, far_rest = flip(rest, "row", 1), flip(rest, "row", 2)
    grad_tokens = unpack(where, back_pieces + hand_on(last_pieces, near_rest), F32, TAIL)
    rests = [rest, near_rest, far_rest, flip(far_rest, "row", 1)]
    rests = after(tuple(rests), grad_tokens)
    qkv_upg, proj_dn, fc1_upg, fc2_dn = grad_join(where, rests)
    return (
        result, grad_tokens,
        swap(qkv_dn), qkv_upg, swap(proj_dn), proj_upg, swap(fc1_dn), fc1_upg, swap(fc2_dn), fc2_upg,
    )


def solution(mesh):
    return jax.shard_map(
        body,
        mesh=mesh,
        in_specs=(
            P("row", ("dp", "col")), P("row", ("dp", "col")), P(), P("row"), P("row"),
            P("row", "col"), P("col", "row"), P("row", "col"), P("row", "col"), P(), P(),
            P(None, "row", None), P(None, None, "col"), P(None, "col", None), P(None, None, "row"),
            P(None, "row", None), P(None, None, "col"), P(None, "col", None), P(None, None, "row"),
        ),
        out_specs=(
            P("row", ("dp", "col")), P("row", ("dp", "col")),
            P(None, "row", None), P(None, None, "col"), P(None, "col", None), P(None, None, "row"),
            P(None, "row", None), P(None, None, "col"), P(None, "col", None), P(None, None, "row"),
        ),
        check_vma=False,
    )
```

```python
import functools

import jax
import jax.numpy as jnp
import numpy as np
from jax import lax
from jax.experimental import pallas as pl
from jax.experimental.pallas import tpu as pltpu
from jax.sharding import PartitionSpec as P

D = 768
HD = 64
WIN = 14
SLOTS = WIN * WIN
SIDE = 64
ADAPT = 8
NWIN = 5
IMG_TOK = NWIN * NWIN * SLOTS
RANK = 16
EDGE = SIDE - (NWIN - 1) * WIN
QUART = D // 4
FULLR = 208
KEYS = 208
EDGER = EDGE * WIN
CORNR = EDGE * EDGE
ROWS = 4 * FULLR + 2 * EDGER + CORNR
HALF = ROWS // 2
HBLK = QUART // 2
EPSILON = 1e-06
BF = jnp.bfloat16
F32 = jnp.float32

FULL, RIGHT, BOTTOM, CORNER = 0, 1, 2, 3
NQ = (FULLR, EDGER, EDGER, CORNR)
OFFS = (0, 4 * FULLR, 4 * FULLR + EDGER, 4 * FULLR + 2 * EDGER)


def slot_order(kind):
    rows = EDGE if kind in (BOTTOM, CORNER) else WIN
    cols = EDGE if kind in (RIGHT, CORNER) else WIN
    kept = [a * WIN + b for a in range(rows) for b in range(cols)]
    rest = [s for s in range(SLOTS) if s not in set(kept)]
    return kept, kept + rest


def build_tables():
    shift = np.zeros((4, FULLR, 128), np.int32)
    keys = np.zeros((4, KEYS, 128), np.float32)
    for kind in range(4):
        kept, order = slot_order(kind)
        for i, s in enumerate(kept):
            for base in (0, 64):
                shift[kind, i, base : base + 32] = WIN - 1 - s // WIN
                shift[kind, i, base + 32 : base + 64] = WIN - 1 - s % WIN
        spare = order[0] if kind == FULL else order[-1]
        for i, s in enumerate(order + [spare] * (KEYS - SLOTS)):
            for base in (0, 64):
                keys[kind, i, base + s // WIN] = 1.0
                keys[kind, i, base + 32 + s % WIN] = 1.0
    return shift, keys.astype(jnp.bfloat16)


SHIFT_NP, KEYS_NP = build_tables()


def nn(a, b):
    return jnp.dot(a, b, preferred_element_type=F32)


def nt(a, b):
    return lax.dot_general(a, b, (((1,), (1,)), ((), ())), preferred_element_type=F32)


def tn(a, b):
    return lax.dot_general(a, b, (((0,), (0,)), ((), ())), preferred_element_type=F32)


def vm():
    return pl.BlockSpec(memory_space=pltpu.VMEM)


def hbm():
    return pl.BlockSpec(memory_space=pl.ANY)


def in_hbm(x):
    return pltpu.with_memory_space_constraint(x, pltpu.HBM)


def arg():
    return pl.BlockSpec(memory_space=pltpu.HBM)


def sm():
    return pl.BlockSpec(memory_space=pltpu.SMEM)


def params(mib=60):
    return pltpu.CompilerParams(vmem_limit_bytes=mib * 1024 * 1024)


def cost(us):
    return pl.CostEstimate(flops=int(us * 1e6), transcendentals=0, bytes_accessed=0)


def place_window(kind, count, moved, width, spare=-100000):
    row = lax.broadcasted_iota(jnp.int32, (count, width), 0)
    lane = lax.broadcasted_iota(jnp.int32, (count, width), 1)
    if kind in (RIGHT, CORNER):
        src = (row // EDGE) * WIN + row % EDGE
    else:
        src = jnp.where(row < SLOTS, row, spare)
    return (lane == src + moved).astype(F32).astype(BF)


def window_list(dest):
    items = [(FULL, FULLR * j, NWIN * dest + j) for j in range(4)]
    items.append((RIGHT, OFFS[1], NWIN * dest + 4))
    items.append((BOTTOM, OFFS[2], NWIN * 4 + dest))
    if dest == 3:
        items.append((CORNER, OFFS[3], NWIN * NWIN - 1))
    return items


def window_span(window):
    start = window * SLOTS
    low = start // 128 * 128
    high = min(-(-(start + SLOTS) // 128) * 128, IMG_TOK)
    return low, high, start - low


def pack_rows(mine, x_ref, rows_ref, spare):
    for dest in range(4):
        slot = jnp.bitwise_xor(mine, dest)
        if dest != 3:
            rows_ref[slot, OFFS[3] :, :] = jnp.zeros((CORNR, QUART), BF)
        for kind, offset, window in window_list(dest):
            low, high, moved = window_span(window)
            pick = place_window(kind, NQ[kind], moved, high - low, spare)
            rows_ref[slot, offset : offset + NQ[kind], :] = nt(pick, x_ref[:, low:high]).astype(BF)


def fold(rows_ref, outs):
    half = rows_ref.shape[1] // 2
    for slot, (out, base) in enumerate(((outs[0], 0), (outs[1], 0), (outs[2], 0), (outs[2], half))):
        out[base : base + half, :QUART] = rows_ref[slot, :half, :]
        out[base : base + half, QUART:] = rows_ref[slot, half:, :]


def pack_kernel(where_ref, x_hbm, o0, o1, o2, rows_ref, x_ref, sem):
    load = pltpu.make_async_copy(x_hbm, x_ref, sem)
    load.start()
    load.wait()
    pack_rows(where_ref[0], x_ref, rows_ref, -100000)
    fold(rows_ref, (o0, o1, o2))


def pieces_of(rows):
    piece = lambda n: jax.ShapeDtypeStruct((n, 2 * QUART), BF)
    return (piece(rows // 2), piece(rows // 2), piece(rows))


def pack(where, x):
    return pl.pallas_call(
        pack_kernel,
        out_shape=pieces_of(ROWS),
        in_specs=[sm(), arg()],
        out_specs=[vm()] * 3,
        scratch_shapes=[
            pltpu.VMEM((4, ROWS, QUART), BF), pltpu.VMEM((QUART, IMG_TOK), BF), pltpu.SemaphoreType.DMA,
        ],
        compiler_params=params(16),
        cost_estimate=cost(4),
        name="pack",
    )(where, in_hbm(x))


def front_kernel(
    where_ref, x_hbm, qkv_hbm, proj_hbm, fc1_hbm, fc2_hbm,
    o0, o1, o2, alpha_ref, beta_ref, alpha_half, cross_ref, fc1_half, fc2_half,
    rows_ref, x_ref, qkv_w, proj_w, sem,
):
    rows = pl.ds(pl.multiple_of(where_ref[1] * HBLK, 32), HBLK)
    loads = [
        pltpu.make_async_copy(src, dst, sem.at[i])
        for i, (src, dst) in enumerate(
            (
                (qkv_hbm, qkv_w), (proj_hbm, proj_w), (fc2_hbm.at[rows, :], fc2_half),
                (fc1_hbm.at[rows, :], fc1_half), (x_hbm, x_ref),
            )
        )
    ]
    for load in loads:
        load.start()
    for load in loads[:4]:
        load.wait()
    heads = qkv_w.shape[1] // (3 * HD)
    for h in range(heads):
        for t in range(3):
            ref, base = (alpha_ref, QUART * t) if t < 2 else (beta_ref, 0)
            ref[:, base + HD * h : base + HD * (h + 1)] = qkv_w[:, HD * (3 * h + t) : HD * (3 * h + t + 1)]
    beta_ref[:, QUART:] = proj_w[...]
    alpha_half[...] = alpha_ref[rows, :]
    cross_ref[:HBLK, :] = beta_ref[rows, :]
    cross_ref[HBLK : 2 * HBLK, :] = fc2_half[:, : 2 * QUART]
    cross_ref[2 * HBLK :, :] = fc2_half[:, 2 * QUART :]
    loads[4].wait()
    pack_rows(where_ref[0], x_ref, rows_ref, 0)
    fold(rows_ref, (o0, o1, o2))


def front(where, x, qkv_w, proj_w, fc1_w, fc2_w):
    s = lambda *shape: jax.ShapeDtypeStruct(shape, BF)
    return pl.pallas_call(
        front_kernel,
        out_shape=pieces_of(ROWS)
        + (
            s(QUART, 2 * QUART), s(QUART, 2 * QUART), s(HBLK, 2 * QUART), s(3 * HBLK, 2 * QUART),
            s(HBLK, D), s(HBLK, D),
        ),
        in_specs=[sm()] + [arg()] * 5,
        out_specs=[vm()] * 9,
        scratch_shapes=[
            pltpu.VMEM((4, ROWS, QUART), BF), pltpu.VMEM((QUART, IMG_TOK), BF),
            pltpu.VMEM(qkv_w.shape, BF), pltpu.VMEM(proj_w.shape, BF), pltpu.SemaphoreType.DMA((5,)),
        ],
        compiler_params=params(16),
        cost_estimate=cost(5),
        name="token_and_weight_pack",
    )(where, *(in_hbm(m) for m in (x, qkv_w, proj_w, fc1_w, fc2_w)))


def unpack_kernel(where_ref, *refs, bounds):
    pieces, (out_ref, acc_ref, rows_ref) = refs[:-3], refs[-3:]
    mine = where_ref[0]
    acc_ref[...] = jnp.zeros_like(acc_ref)
    index = 0
    for low, high in bounds:
        half = (high - low) // 2
        for slot in range(4):
            piece = pieces[index]
            rows = slice(half, 2 * half) if slot == 3 else slice(0, half)
            rows_ref[slot, low : low + half, :] = piece[rows, :QUART]
            rows_ref[slot, low + half : high, :] = piece[rows, QUART:]
            index += 1

    for source in range(4):
        slot = jnp.bitwise_xor(mine, source)
        for kind, offset, window in window_list(source):
            low, high, moved = window_span(window)
            pick = place_window(kind, NQ[kind], moved, high - low)
            acc_ref[:, low:high] += tn(rows_ref[slot, offset : offset + NQ[kind], :], pick)
    out_ref[...] = acc_ref[:, :IMG_TOK].astype(out_ref.dtype)


def unpack(where, pieces, dtype, bounds=((0, ROWS),)):
    return pl.pallas_call(
        functools.partial(unpack_kernel, bounds=bounds),
        out_shape=jax.ShapeDtypeStruct((QUART, IMG_TOK), dtype),
        in_specs=[sm()] + [vm()] * len(pieces),
        out_specs=vm(),
        scratch_shapes=[
            pltpu.VMEM((QUART, -(-IMG_TOK // 128) * 128), F32),
            pltpu.VMEM((4, ROWS, QUART), BF),
        ],
        compiler_params=params(24),
        cost_estimate=cost(4),
        name="unpack",
    )(where, *pieces)


def join_pieces(pieces, dst_ref):
    for slot, piece in enumerate(pieces):
        rows = slice(HALF, ROWS) if slot == 3 else slice(0, HALF)
        dst_ref[:HALF, QUART * slot : QUART * (slot + 1)] = piece[rows, :QUART]
        dst_ref[HALF:, QUART * slot : QUART * (slot + 1)] = piece[rows, QUART:]


def split_pieces(src_ref, outs):
    half = src_ref.shape[0] // 2
    for slot, (out, base) in enumerate(((outs[0], 0), (outs[1], 0), (outs[2], 0), (outs[2], half))):
        out[base : base + half, :QUART] = src_ref[:half, QUART * slot : QUART * (slot + 1)]
        out[base : base + half, QUART:] = src_ref[half:, QUART * slot : QUART * (slot + 1)]


def adapter_pack_kernel(
    pick_ref, qkv_up_hbm, proj_dn_hbm, fc1_up_hbm, fc2_dn_hbm, qkv_dn_hbm, fc1_dn_hbm, proj_up_hbm, fc2_up_hbm,
    gain1, gain2, rel_h, rel_w, s0, s1, s2, s3, row_ref, rel_ref,
    qkv_up, proj_dn, fc1_up, fc2_dn, qkv_dn, fc1_dn, proj_up, fc2_up, sem,
):
    pairs = []
    for j in range(4):
        for src, dst in ((qkv_up_hbm, qkv_up), (proj_dn_hbm, proj_dn), (fc1_up_hbm, fc1_up), (fc2_dn_hbm, fc2_dn)):
            pairs.append((src.at[pick_ref[j]], dst.at[j]))
    for src, dst in ((qkv_dn_hbm, qkv_dn), (fc1_dn_hbm, fc1_dn), (proj_up_hbm, proj_up), (fc2_up_hbm, fc2_up)):
        pairs.append((src.at[pick_ref[0]], dst.at[0]))
    loads = [pltpu.make_async_copy(src, dst, sem.at[i]) for i, (src, dst) in enumerate(pairs)]
    for load in loads:
        load.start()
    offsets = rel_h.shape[0]
    reverse = (
        lax.broadcasted_iota(jnp.int32, (offsets, 32), 0) + lax.broadcasted_iota(jnp.int32, (offsets, 32), 1)
        == offsets - 1
    ).astype(F32).astype(BF)
    rel_ref[...] = jnp.zeros_like(rel_ref)
    for i, table in enumerate((rel_h, rel_w)):
        block = tn(table[...], reverse).astype(BF)
        rel_ref[:HD, HD + 32 * i : HD + 32 * (i + 1)] = block
        rel_ref[HD:, 32 * i : 32 * (i + 1)] = block
    for load in loads:
        load.wait()
    heads = qkv_up.shape[2] // (3 * HD)
    half = 2 * QUART
    for j, send_ref in enumerate((s0, s1, s2, s3)):
        for h in range(heads):
            for t in range(3):
                row, base = (0, QUART * t) if t < 2 else (RANK, 0)
                send_ref[row : row + RANK, base + HD * h : base + HD * (h + 1)] = qkv_up[
                    j, :, HD * (3 * h + t) : HD * (3 * h + t + 1)
                ]
        send_ref[RANK : 2 * RANK, QUART:] = proj_dn[j]
        for i, ref in enumerate((fc1_up, fc2_dn)):
            for part in range(2):
                row = RANK * (2 + 2 * i + part)
                send_ref[row : row + RANK, :] = ref[j, :, half * part : half * (part + 1)]
    for i, ref in enumerate((qkv_dn, fc1_dn, proj_up, fc2_up)):
        row, base = RANK * (i // 2), QUART * (i % 2)
        row_ref[row : row + RANK, base : base + QUART] = ref[0]
    for i, ref in enumerate((gain1, gain2)):
        row_ref[2 * RANK :, QUART * i : QUART * (i + 1)] = jnp.broadcast_to(ref[...], (RANK, QUART))


def adapter_pack(pick, *mats):
    s = lambda *shape: jax.ShapeDtypeStruct(shape, BF)
    return pl.pallas_call(
        adapter_pack_kernel,
        out_shape=(s(6 * RANK, 2 * QUART),) * 4 + (s(3 * RANK, 2 * QUART), s(128, 128)),
        in_specs=[sm()] + [arg()] * 8 + [vm()] * 4,
        out_specs=[vm()] * 6,
        scratch_shapes=[pltpu.VMEM((4,) + m.shape[1:], BF) for m in mats[:4]]
        + [pltpu.VMEM((1,) + m.shape[1:], BF) for m in mats[4:8]]
        + [pltpu.SemaphoreType.DMA((20,))],
        compiler_params=params(8),
        cost_estimate=cost(2),
        name="adapter_pack",
    )(pick, *(in_hbm(m) for m in mats[:8]), *mats[8:])


def alpha_block(k, j):
    part = k
    if j == 0:
        return [(part, 0, QUART, None)]
    return [
        (part, QUART + HBLK * (j - 1), HBLK, 0),
        (part, QUART + 3 * HBLK + HBLK * (j - 1), HBLK, 1),
    ]


def beta_block(k, j):
    core, cross = k % 2, k // 2
    base = 3 * core
    if j == 0 and not cross:
        return [(base, 0, QUART, None)]
    row = 0 if j == 0 else HBLK + QUART * (j - 1) + HBLK * cross
    return [(base + 1, row, HBLK, 0), (base + 2, row, HBLK, 1)]


def block_dst(start, flag, half):
    if flag is None:
        return start
    offset = half if flag == 0 else 1 - half
    return pl.multiple_of(start + offset * HBLK, 32)


def prep1_kernel(
    where_ref, p0, p1, p2, p3, q0, q1, q2, q3, q4, q5, a0, a1, a2, a3,
    wqkv_ref, wproj_ref, dqkv, uqkv, dproj, uproj, d1, u1, d2, u2, gain1, gain2, ups, downs,
):
    half = where_ref[1]
    for j, a in enumerate((a0, a1, a2, a3)):
        base = a.shape[0] - 6 * RANK
        part = lambda i: slice(base + RANK * i, base + RANK * (i + 1))
        for t in range(3):
            uqkv[:, D * t + QUART * j : D * t + QUART * (j + 1)] = a[
                part(t // 2), QUART * (t % 2) : QUART * (t % 2 + 1)
            ]
        dproj[:, QUART * j : QUART * (j + 1)] = a[part(1), QUART:]
        for i in range(2):
            u1[:, D * j + D // 2 * i : D * j + D // 2 * (i + 1)] = a[part(2 + i), :]
            d2[:, D * j + D // 2 * i : D * j + D // 2 * (i + 1)] = a[part(4 + i), :]
    for k, ref in enumerate((p0, p1, p2, p3)):
        for i, dst in enumerate((dqkv, d1, uproj, u2)):
            rows = slice(D + RANK * (i // 2), D + RANK * (i // 2 + 1))
            dst[:, QUART * k : QUART * (k + 1)] = ref[rows, QUART * (i % 2) : QUART * (i % 2 + 1)]
        for i, dst in enumerate((gain1, gain2)):
            row = D + 2 * RANK
            dst[:, QUART * k : QUART * (k + 1)] = ref[row : row + 1, QUART * i : QUART * (i + 1)].astype(F32)
    alpha, beta = (p0, p1, p2, p3), (q0, q1, q2, q3, q4, q5)
    for k in range(4):
        for j in range(4):
            for part, row, count, flag in alpha_block(k, j):
                rows = pl.ds(block_dst(QUART * k, flag, half), count)
                for t in range(2):
                    wqkv_ref[rows, D * t + QUART * j : D * t + QUART * (j + 1)] = alpha[part][
                        row : row + count, QUART * t : QUART * (t + 1)
                    ]
            for part, row, count, flag in beta_block(k, j):
                rows = pl.ds(block_dst(QUART * k, flag, half), count)
                wqkv_ref[rows, 2 * D + QUART * j : 2 * D + QUART * (j + 1)] = beta[part][
                    row : row + count, :QUART
                ]
                rows = pl.ds(block_dst(QUART * j, flag, half), count)
                wproj_ref[rows, QUART * k : QUART * (k + 1)] = beta[part][row : row + count, QUART:]
    for t in range(3):
        ups[t] = uqkv[:, D * t : D * (t + 1)]
    ups[3] = uproj[...]
    for k in range(4):
        downs[k] = dqkv[:, QUART * k : QUART * (k + 1)]
        downs[4 + k] = dproj[:, QUART * k : QUART * (k + 1)]

    def merge(t, carry):
        cols = pl.ds(pl.multiple_of(D * t, 128), D)
        for k in range(4):
            rows = slice(QUART * k, QUART * (k + 1))
            wqkv_ref[rows, cols] = (wqkv_ref[rows, cols].astype(F32) + tn(downs[k], ups[t])).astype(BF)
        return carry

    lax.fori_loop(0, 3, merge, 0)
    for k in range(4):
        rows = slice(QUART * k, QUART * (k + 1))
        wproj_ref[rows, :] = (wproj_ref[rows, :].astype(F32) + tn(downs[4 + k], ups[3])).astype(BF)


def prep1(where, alpha, beta, cols):
    s = lambda *shape: jax.ShapeDtypeStruct(shape, BF)
    return pl.pallas_call(
        prep1_kernel,
        out_shape=(
            s(D, 3 * D), s(D, D), s(RANK, D), s(RANK, 3 * D), s(RANK, D), s(RANK, D),
            s(RANK, D), s(RANK, 4 * D), s(RANK, 4 * D), s(RANK, D),
            jax.ShapeDtypeStruct((1, D), F32), jax.ShapeDtypeStruct((1, D), F32),
        ),
        in_specs=[sm()] + [vm()] * 14,
        out_specs=[vm()] * 12,
        scratch_shapes=[pltpu.VMEM((4, RANK, D), BF), pltpu.VMEM((8, RANK, QUART), BF)],
        compiler_params=params(24),
        cost_estimate=cost(7),
        name="attention_weights",
    )(where, *alpha, *beta, *cols)


def normalize(values):
    center = jnp.sum(values, axis=1, keepdims=True) / D
    shifted = values - center
    inv_std = lax.rsqrt(jnp.sum(shifted * shifted, axis=1, keepdims=True) / D + EPSILON)
    return shifted * inv_std, inv_std


def norm_back(grad, normed, inv_std):
    first = jnp.sum(grad, axis=1, keepdims=True) / D
    second = jnp.sum(grad * normed, axis=1, keepdims=True) / D
    return inv_std * (grad - first - normed * second)


def barrel(values, amount, left):
    for bit in (1, 2, 4, 8):
        moved = pltpu.roll(values, (128 - bit) if left else bit, 1)
        values = jnp.where((amount & bit) != 0, moved, values)
    return values


def low_half(count):
    return lax.broadcasted_iota(jnp.int32, (count, 128), 1) < HD


def pad_rows(tile):
    if tile.shape[0] == KEYS:
        return tile
    return jnp.concatenate([tile, jnp.zeros((KEYS - tile.shape[0], tile.shape[1]), tile.dtype)], axis=0)


def live_rows():
    return lax.broadcasted_iota(jnp.int32, (KEYS, 128), 0) < SLOTS


GROUP = 6
GROUP_BACK = 6


def pair_columns(pair):
    return tuple(slice(D * t + 128 * pair, D * t + 128 * (pair + 1)) for t in range(3))


def attend_window(kind, row0, qkv_ref, att_ref, exp_ref, inv_ref, rel_ref, shift_ref, keys_ref):
    count = NQ[kind]
    rows = pl.ds(row0, count)
    low_q, low_k = low_half(count), low_half(KEYS)
    live = live_rows()
    ones = jnp.where(live, 1.0, 0.0).astype(BF)
    amount = shift_ref[kind, :count, :]
    onehot = keys_ref[kind]
    rel_mat = rel_ref[...]
    for first in range(0, D // 128, GROUP):
        pairs = range(first, first + GROUP)
        heads = [(pair, odd) for pair in pairs for odd in range(2)]
        q_tile = {p: qkv_ref[rows, pair_columns(p)[0]] for p in pairs}
        rel = {p: nn(q_tile[p], rel_mat) for p in pairs}
        rel = {p: barrel(rel[p], amount, True).astype(BF) for p in pairs}
        k_tile = {p: pad_rows(qkv_ref[rows, pair_columns(p)[1]] * BF(HD**-0.5)) for p in pairs}
        scores = {}
        for p, odd in heads:
            if odd:
                q_aug, k_aug = jnp.where(low_q, rel[p], q_tile[p]), jnp.where(low_k, onehot, k_tile[p])
            else:
                q_aug, k_aug = jnp.where(low_q, q_tile[p], rel[p]), jnp.where(low_k, k_tile[p], onehot)
            scores[p, odd] = nt(q_aug, k_aug)
        top = {h: jnp.max(scores[h], axis=1, keepdims=True) for h in heads}
        exponent = {h: jnp.exp(scores[h] - top[h]).astype(BF) for h in heads}
        both = {}
        for p, odd in heads:
            exp_ref[2 * p + odd, rows, :] = exponent[p, odd]
            v_tile = pad_rows(qkv_ref[rows, pair_columns(p)[2]])
            if kind == FULL:
                v_tile = jnp.where(live, v_tile, 0).astype(BF)
            v_aug = jnp.where(low_k, ones, v_tile) if odd else jnp.where(low_k, v_tile, ones)
            both[p, odd] = nn(exponent[p, odd], v_aug)
        for p in pairs:
            cols = pair_columns(p)[0]
            inverse = 1.0 / pltpu.roll(jnp.where(low_q, both[p, 1], both[p, 0]), HD, 1)
            inv_ref[rows, cols] = inverse
            att_ref[rows, cols] = (jnp.where(low_q, both[p, 0], both[p, 1]) * inverse).astype(BF)


PARTS = ((FULL, FULL), (FULL, FULL), (RIGHT, BOTTOM, CORNER))
PART_ROWS = tuple(sum(NQ[kind] for kind in part) for part in PARTS)
PART_OFFS = (0, PART_ROWS[0], PART_ROWS[0] + PART_ROWS[1])


TAIL = ((0, 640), (640, ROWS))


def qkv_kernel(
    x0, x1, x2, x3, gain_ref, w_hbm, x_hbm, hid_hbm, qkv_a, qkv_b, qkv_c,
    x_ref, hid_ref, rows_ref, w_ref, qkv_ref, sem, out_sem,
):
    loads = [
        pltpu.make_async_copy(w_hbm.at[:, D * t : D * (t + 1)], w_ref.at[t], sem.at[t]) for t in range(3)
    ]
    for load in loads:
        load.start()
    join_pieces((x0, x1, x2, x3), x_ref)
    kept = [
        pltpu.make_async_copy(src, dst, sem.at[3 + i])
        for i, (src, dst) in enumerate(((x_ref, x_hbm), (hid_ref, hid_hbm)))
    ]
    kept[0].start()
    gain = gain_ref[...]

    def norm_step(i, carry):
        rows = pl.ds(pl.multiple_of(i * 112, 16), 112)
        normed, _ = normalize(x_ref[rows, :].astype(F32))
        hidden = (normed * gain).astype(BF)
        rows_ref[rows, :] = hidden
        hid_ref[rows, :] = hidden
        return carry

    lax.fori_loop(0, ROWS // 112, norm_step, 0)
    for w in range(4):
        hid_ref[FULLR * w + SLOTS : FULLR * (w + 1), :] = jnp.zeros((FULLR - SLOTS, D), BF)
    kept[1].start()
    for load in loads:
        load.wait()

    def stores(t):
        cols = pl.ds(pl.multiple_of(D * t, 128), D)
        return [
            pltpu.make_async_copy(
                qkv_ref.at[t, pl.ds(offset, count), :], out.at[:, cols], out_sem.at[t, i]
            )
            for i, (out, offset, count) in enumerate(zip((qkv_a, qkv_b, qkv_c), PART_OFFS, PART_ROWS))
        ]

    def project_step(t, carry):
        qkv_ref[t] = nn(rows_ref[...], w_ref[t]).astype(BF)
        for store in stores(t):
            store.start()
        return carry

    lax.fori_loop(0, 3, project_step, 0)
    for t in range(3):
        for store in stores(t):
            store.wait()
    for store in kept:
        store.wait()


def qkv_rows(pieces, gain, wqkv):
    s = lambda *shape: jax.ShapeDtypeStruct(shape, BF)
    return pl.pallas_call(
        qkv_kernel,
        out_shape=(s(ROWS, D), s(ROWS, D)) + tuple(s(n, 3 * D) for n in PART_ROWS),
        in_specs=[vm()] * 5 + [hbm()],
        out_specs=[hbm()] * 5,
        scratch_shapes=[
            pltpu.VMEM((ROWS, D), BF), pltpu.VMEM((ROWS, D), BF), pltpu.VMEM((ROWS, D), BF),
            pltpu.VMEM((3, D, D), BF), pltpu.VMEM((3, ROWS, D), BF),
            pltpu.SemaphoreType.DMA((5,)), pltpu.SemaphoreType.DMA((3, 3)),
        ],
        compiler_params=params(32),
        cost_estimate=cost(10),
        name="norm_and_qkv",
    )(*pieces, gain, wqkv)


def attention_kernel(qkv_ref, rel_ref, shift_ref, keys_ref, att_ref, exp_ref, inv_ref, *, kinds):
    refs = (qkv_ref, att_ref, exp_ref, inv_ref, rel_ref, shift_ref, keys_ref)
    if kinds[0] == FULL:

        def step(w, carry):
            attend_window(FULL, pl.multiple_of(w * FULLR, 16), *refs)
            return carry

        lax.fori_loop(0, len(kinds), step, 0)
    else:
        row = 0
        for kind in kinds:
            attend_window(kind, row, *refs)
            row += NQ[kind]


def attention(part, qkv, rel, shift, keys):
    rows = PART_ROWS[part]
    s = lambda *shape, dtype=BF: jax.ShapeDtypeStruct(shape, dtype)
    return pl.pallas_call(
        functools.partial(attention_kernel, kinds=PARTS[part]),
        out_shape=(s(rows, D), s(D // HD, rows, KEYS), s(rows, D, dtype=F32)),
        in_specs=[vm()] * 4,
        out_specs=[vm()] * 3,
        compiler_params=params(24),
        cost_estimate=cost(10),
        name="attention_forward",
    )(qkv, rel, shift, keys)


def project_kernel(x_ref, att_a, att_b, att_c, wproj_ref, middle_ref):
    for ref, offset, count in zip((att_a, att_b, att_c), PART_OFFS, PART_ROWS):
        rows = slice(offset, offset + count)
        middle_ref[rows, :] = x_ref[rows, :].astype(F32) + nn(ref[...], wproj_ref[...])


def project(x, atts, wproj):
    return pl.pallas_call(
        project_kernel,
        out_shape=jax.ShapeDtypeStruct((ROWS, D), F32),
        in_specs=[vm()] * 5,
        out_specs=vm(),
        compiler_params=params(20),
        cost_estimate=cost(5),
        name="projection",
    )(x, *atts, wproj)


CHUNK = 512
LOCK = 1


def mlp_kernel(
    where_ref, middle_ref, g0, g1, g2, g3, gain_ref,
    p0, p1, p2, p3, q0, q1, q2, q3, q4, q5, d1, u1, d2, u2,
    o0, o1, o2, gmid_ref, down1, up1, down2, up2,
    gm_ref, out_rows, h2_ref, acc_mlp, acc_gh, gu1, ad2, w1_ref, w2_ref, downs, sem,
):
    half = where_ref[1]
    copies = []

    def fetch(src, dst):
        copies.append(pltpu.make_async_copy(src, dst, sem.at[len(copies)]))
        copies[-1].start()

    alpha, beta = (p0, p1, p2, p3), (q0, q1, q2, q3, q4, q5)
    for k in range(4):
        for j in range(4):
            for part, row, count, flag in alpha_block(k, j):
                rows = pl.ds(block_dst(QUART * k, flag, half), count)
                fetch(alpha[part].at[row : row + count, :], w1_ref.at[rows, D * j : D * (j + 1)])
            for part, row, count, flag in beta_block(k, j):
                rows = pl.ds(block_dst(QUART * k, flag, half), count)
                fetch(beta[part].at[row : row + count, :], w2_ref.at[rows, D * j : D * (j + 1)])
    join_pieces((g0, g1, g2, g3), gm_ref)
    for k in range(4):
        downs[k] = d1[:, QUART * k : QUART * (k + 1)]
        downs[4 + k] = u2[:, QUART * k : QUART * (k + 1)]
    for copy in copies:
        copy.wait()

    def merge(j, carry):
        cols = pl.ds(pl.multiple_of(D * j, 128), D)
        for k in range(4):
            rows = slice(QUART * k, QUART * (k + 1))
            w1_ref[rows, cols] = (w1_ref[rows, cols].astype(F32) + tn(downs[k], u1[:, cols])).astype(BF)
            w2_ref[rows, cols] = (w2_ref[rows, cols].astype(F32) + tn(downs[4 + k], d2[:, cols])).astype(BF)
        return carry

    lax.fori_loop(0, 4, merge, 0)
    gain = gain_ref[...]
    down1[...] = jnp.zeros_like(down1)
    up1[...] = jnp.zeros_like(up1)
    down2[...] = jnp.zeros_like(down2)
    up2[...] = jnp.zeros_like(up2)

    def tile_step(t, carry):
        rows = pl.ds(pl.multiple_of(t * HALF, 16), HALF)
        normed, _ = normalize(middle_ref[rows, :])
        h2 = (normed * gain).astype(BF)
        h2_ref[...] = h2
        gm = gm_ref[rows, :]
        ad1 = nt(d1[...], h2).astype(BF)
        gu2 = nt(u2[...], gm).astype(BF)
        acc_mlp[...] = jnp.zeros_like(acc_mlp)
        acc_gh[...] = jnp.zeros_like(acc_gh)
        gu1[...] = jnp.zeros_like(gu1)
        ad2[...] = jnp.zeros_like(ad2)

        def chunk_step(c, inner_carry):
            spans = [
                pl.ds(pl.multiple_of((c * LOCK + i) * CHUNK, CHUNK), CHUNK) for i in range(LOCK)
            ]
            h2 = h2_ref[...]
            gm = gm_ref[rows, :]
            inner = [nn(h2, w1_ref[:, span]) for span in spans]
            gact = [nn(gm, w2_ref[:, span]) for span in spans]
            act, ginner = [], []
            for i in range(LOCK):
                half = 0.5 * (1.0 + lax.erf(inner[i] * 2**-0.5))
                act.append((inner[i] * half).astype(BF))
                slope = half + inner[i] * (jnp.exp(-0.5 * inner[i] * inner[i]) * (2 * np.pi) ** -0.5)
                ginner.append((gact[i] * slope).astype(BF))
            for i, span in enumerate(spans):
                acc_mlp[...] += nt(act[i], w2_ref[:, span])
                acc_gh[...] += nt(ginner[i], w1_ref[:, span])
                up1[:, span] += nn(ad1, ginner[i])
                gu1[...] += nt(u1[:, span], ginner[i])
                ad2[...] += nt(d2[:, span], act[i])
                down2[:, span] += nn(gu2, act[i])
            return inner_carry

        lax.fori_loop(0, 4 * D // (CHUNK * LOCK), chunk_step, 0)
        down1[...] += nn(gu1[...].astype(BF), h2_ref[...])
        up2[...] += nn(ad2[...].astype(BF), gm_ref[rows, :])
        middle = middle_ref[rows, :]
        out_rows[rows, :] = (middle + acc_mlp[...]).astype(BF)
        normed, inv_std = normalize(middle)
        gmid_ref[rows, :] = gm_ref[rows, :].astype(F32) + norm_back(acc_gh[...] * gain, normed, inv_std)
        return carry

    lax.fori_loop(0, 2, tile_step, 0)
    split_pieces(out_rows, (o0, o1, o2))


def mlp(where, middle, pieces, gain, alpha, beta, d1, u1, d2, u2):
    s = lambda *shape, dtype=F32: jax.ShapeDtypeStruct(shape, dtype)
    return pl.pallas_call(
        mlp_kernel,
        out_shape=pieces_of(ROWS)
        + (s(ROWS, D), s(RANK, D), s(RANK, 4 * D), s(RANK, 4 * D), s(RANK, D)),
        in_specs=[sm()] + [vm()] * 6 + [pl.BlockSpec(memory_space=pl.ANY)] * 10 + [vm()] * 4,
        out_specs=[vm()] * 8,
        scratch_shapes=[
            pltpu.VMEM((ROWS, D), BF), pltpu.VMEM((ROWS, D), BF), pltpu.VMEM((HALF, D), BF),
            pltpu.VMEM((HALF, D), F32), pltpu.VMEM((HALF, D), F32),
            pltpu.VMEM((RANK, HALF), F32), pltpu.VMEM((RANK, HALF), F32),
            pltpu.VMEM((D, 4 * D), BF), pltpu.VMEM((D, 4 * D), BF), pltpu.VMEM((8, RANK, QUART), BF),
            pltpu.SemaphoreType.DMA((4 * 4 * 4,)),
        ],
        compiler_params=params(48),
        cost_estimate=cost(48),
        name="mlp_forward_backward",
    )(where, middle, *pieces, gain, *alpha, *beta, d1, u1, d2, u2)


def attend_back_window(
    kind, row0, qkv_ref, att_ref, exp_ref, inv_ref, gatt_ref, gqkv_ref, rel_ref, shift_ref, keys_ref
):
    count = NQ[kind]
    rows = pl.ds(row0, count)
    low_q, low_k = low_half(count), low_half(KEYS)
    live = live_rows()
    lane_k = lax.broadcasted_iota(jnp.int32, (KEYS, 128), 1) % HD
    lane_q = lax.broadcasted_iota(jnp.int32, (count, 128), 1) % HD
    ones = jnp.where(live & (lane_k < 2), 1.0, 0.0).astype(BF)
    across = jnp.where(
        low_half(128) != (lax.broadcasted_iota(jnp.int32, (128, 128), 0) < HD), -1.0, 0.0
    ).astype(BF)
    amount = shift_ref[kind, :count, :]
    onehot = keys_ref[kind]
    rel_mat = rel_ref[...]
    for first in range(0, D // 128, GROUP_BACK):
        pairs = range(first, first + GROUP_BACK)
        heads = [(pair, odd) for pair in pairs for odd in range(2)]
        go_tile = {
            p: (gatt_ref[rows, pair_columns(p)[0]].astype(F32) * inv_ref[rows, pair_columns(p)[0]]).astype(BF)
            for p in pairs
        }
        delta = {
            p: nn((go_tile[p].astype(F32) * att_ref[rows, pair_columns(p)[0]].astype(F32)).astype(BF), across)
            for p in pairs
        }
        go_t = {p: go_tile[p].T for p in pairs}
        gv = {}
        for p, odd in heads:
            gv[p, odd] = nn(go_t[p][HD * odd : HD * (odd + 1), :], exp_ref[2 * p + odd, rows, :])
        gscore = {}
        for p in pairs:
            high = delta[p].astype(BF)
            rest = (delta[p] - high.astype(F32)).astype(BF)
            low_delta = jnp.where(lane_q == 0, high, jnp.where(lane_q == 1, rest, 0)).astype(BF)
            v_tile = pad_rows(qkv_ref[rows, pair_columns(p)[2]])
            if kind == FULL:
                v_tile = jnp.where(live, v_tile, 0).astype(BF)
            gscore[p, 0] = nt(jnp.where(low_q, go_tile[p], low_delta), jnp.where(low_k, v_tile, ones))
            gscore[p, 1] = nt(jnp.where(low_q, low_delta, go_tile[p]), jnp.where(low_k, ones, v_tile))
        q_t = {p: qkv_ref[rows, pair_columns(p)[0]].T for p in pairs}
        gs = {(p, odd): (exp_ref[2 * p + odd, rows, :].astype(F32) * gscore[p, odd]).astype(BF) for p, odd in heads}
        gk = {(p, odd): nn(q_t[p][HD * odd : HD * (odd + 1), :], gs[p, odd]) for p, odd in heads}
        gq = {}
        for p in pairs:
            k_tile = pad_rows(qkv_ref[rows, pair_columns(p)[1]] * BF(HD**-0.5))
            gq[p, 0] = nn(gs[p, 0], jnp.where(low_k, k_tile, onehot))
            gq[p, 1] = nn(gs[p, 1], jnp.where(low_k, onehot, k_tile))
        sums = {p: barrel(jnp.where(low_q, gq[p, 1], gq[p, 0]), amount, False).astype(BF) for p in pairs}
        for p in pairs:
            cols, kcols, vcols = pair_columns(p)
            gv_tile = jnp.concatenate([gv[p, 0], gv[p, 1]], axis=0).astype(BF).T
            gqkv_ref[rows, vcols] = gv_tile[:count, :]
            gk_tile = (jnp.concatenate([gk[p, 0], gk[p, 1]], axis=0) * HD**-0.5).astype(BF).T
            gqkv_ref[rows, kcols] = gk_tile[:count, :]
            gqkv_ref[rows, cols] = (jnp.where(low_q, gq[p, 0], gq[p, 1]) + nt(sums[p], rel_mat)).astype(BF)


def attention_back_kernel(
    gmid_hbm, hid_hbm, qkv_a, qkv_b, qkv_c, att_a, att_b, att_c, exp_a, exp_b, exp_c, inv_a, inv_b, inv_c,
    wproj_ref, rel_ref, shift_ref, keys_ref, dqkv, uqkv, dproj, uproj,
    gqkv_hbm, down_q, up_q, down_p, up_p,
    gmid_ref, hid_ref, qkv_ref, att_ref, exp_ref, inv_ref, gqkv_ref, gb_ref, gatt_ref, sem, out_sem,
):
    spans = [pl.ds(offset, count) for offset, count in zip(PART_OFFS, PART_ROWS)]
    pairs = [(gmid_hbm, gmid_ref)]
    for part, srcs in enumerate(
        ((qkv_a, inv_a, att_a, exp_a), (qkv_b, inv_b, att_b, exp_b), (qkv_c, inv_c, att_c, exp_c))
    ):
        rows = spans[part]
        for src, dst in zip(srcs, (qkv_ref, inv_ref, att_ref)):
            pairs.append((src, dst.at[rows, :]))
        pairs.append((srcs[3], exp_ref.at[:, rows, :]))
    pairs.append((hid_hbm, hid_ref))
    loads = [pltpu.make_async_copy(src, dst, sem.at[i]) for i, (src, dst) in enumerate(pairs)]
    for load in loads:
        load.start()

    def wait_part(part):
        for load in loads[1 + 4 * part : 5 + 4 * part]:
            load.wait()

    stores = [
        pltpu.make_async_copy(gqkv_ref.at[rows, :], gqkv_hbm.at[rows, :], out_sem.at[i])
        for i, rows in enumerate(spans)
    ]
    loads[0].wait()
    gb_ref[...] = gmid_ref[...].astype(BF)
    gatt_ref[...] = nt(gb_ref[...], wproj_ref[...]).astype(BF)
    refs = (qkv_ref, att_ref, exp_ref, inv_ref, gatt_ref, gqkv_ref, rel_ref, shift_ref, keys_ref)

    def step(w, carry):
        for part in range(2):

            @pl.when(w == 2 * part)
            def _():
                wait_part(part)

        attend_back_window(FULL, pl.multiple_of(w * FULLR, 16), *refs)
        return carry

    lax.fori_loop(0, 4, step, 0)
    stores[0].start()
    stores[1].start()
    wait_part(2)
    for kind in (RIGHT, BOTTOM, CORNER):
        attend_back_window(kind, OFFS[kind], *refs)
    stores[2].start()
    up_p[...] = nn(nt(dproj[...], att_ref[...]).astype(BF), gb_ref[...])
    down_p[...] = nn(nt(uproj[...], gb_ref[...]).astype(BF), att_ref[...])
    loads[-1].wait()
    up_q[...] = nn(nt(dqkv[...], hid_ref[...]).astype(BF), gqkv_ref[...])
    down_q[...] = nn(nt(uqkv[...], gqkv_ref[...]).astype(BF), hid_ref[...])
    for store in stores:
        store.wait()


def attention_back(gmid, hid, qkvs, atts, exps, invs, wproj, rel, shift, keys, dqkv, uqkv, dproj, uproj):
    s = lambda *shape, dtype=F32: jax.ShapeDtypeStruct(shape, dtype)
    return pl.pallas_call(
        attention_back_kernel,
        out_shape=(s(ROWS, 3 * D, dtype=BF), s(RANK, D), s(RANK, 3 * D), s(RANK, D), s(RANK, D)),
        in_specs=[hbm()] * 14 + [vm()] * 8,
        out_specs=[hbm()] + [vm()] * 4,
        scratch_shapes=[
            pltpu.VMEM((ROWS, D), F32), pltpu.VMEM((ROWS, D), BF), pltpu.VMEM((ROWS, 3 * D), BF),
            pltpu.VMEM((ROWS, D), BF), pltpu.VMEM((D // HD, ROWS, KEYS), BF), pltpu.VMEM((ROWS, D), F32),
            pltpu.VMEM((ROWS, 3 * D), BF), pltpu.VMEM((ROWS, D), BF), pltpu.VMEM((ROWS, D), BF),
            pltpu.SemaphoreType.DMA((14,)), pltpu.SemaphoreType.DMA((3,)),
        ],
        compiler_params=params(52),
        cost_estimate=cost(28),
        name="attention_backward",
    )(gmid, hid, *qkvs, *atts, *exps, *invs, wproj, rel, shift, keys, dqkv, uqkv, dproj, uproj)


def token_grad_kernel(gmid_hbm, x_hbm, gqkv_hbm, gain_ref, wqkv_ref, o0, o1, o2,
                      gmid_ref, x_ref, gqkv_ref, gh_ref, out_rows, sem, *, low, high):
    span = pl.ds(low, high - low)
    copies = [
        pltpu.make_async_copy(src.at[span, :], dst, sem.at[i])
        for i, (src, dst) in enumerate(((gqkv_hbm, gqkv_ref), (x_hbm, x_ref), (gmid_hbm, gmid_ref)))
    ]
    for copy in copies:
        copy.start()
    copies[0].wait()
    gh_ref[...] = nt(gqkv_ref[...], wqkv_ref[...])
    copies[1].wait()
    copies[2].wait()
    gain = gain_ref[...]
    step = (high - low) // 2

    def norm_step(i, carry):
        rows = pl.ds(pl.multiple_of(i * step, 16), step)
        normed, inv_std = normalize(x_ref[rows, :].astype(F32))
        back = norm_back(gh_ref[rows, :] * gain, normed, inv_std)
        out_rows[rows, :] = (gmid_ref[rows, :] + back).astype(BF)
        return carry

    lax.fori_loop(0, 2, norm_step, 0)
    split_pieces(out_rows, (o0, o1, o2))


def token_grad(gmid, x, gqkv, gain, wqkv, low, high):
    count = high - low
    return pl.pallas_call(
        functools.partial(token_grad_kernel, low=low, high=high),
        out_shape=pieces_of(count),
        in_specs=[hbm(), hbm(), hbm(), vm(), vm()],
        out_specs=[vm()] * 3,
        scratch_shapes=[
            pltpu.VMEM((count, D), F32), pltpu.VMEM((count, D), BF), pltpu.VMEM((count, 3 * D), BF),
            pltpu.VMEM((count, D), F32), pltpu.VMEM((count, D), BF), pltpu.SemaphoreType.DMA((3,)),
        ],
        compiler_params=params(28),
        cost_estimate=cost(8),
        name="token_gradient",
    )(gmid, x, gqkv, gain, wqkv)


def grad_pack_kernel(where_ref, down_q, up_q, down_p, up_p, down1, up1, down2, up2, o0, o1, o2, o3, buf_ref):
    mine = where_ref[0]
    for k in range(4):
        for i, ref in enumerate((down_q, down1, up_p, up2)):
            buf_ref[k, :RANK, QUART * i : QUART * (i + 1)] = ref[:, QUART * k : QUART * (k + 1)]
    for dest in range(4):
        k = jnp.bitwise_xor(mine, dest)
        ranks = slice(RANK // 4 * dest, RANK // 4 * (dest + 1))
        for j in range(4):
            base = RANK + 12 * j
            for t in range(3):
                buf_ref[k, base : base + 4, QUART * t : QUART * (t + 1)] = up_q[
                    ranks, D * t + QUART * j : D * t + QUART * (j + 1)
                ]
            buf_ref[k, base : base + 4, 3 * QUART :] = down_p[ranks, QUART * j : QUART * (j + 1)]
            buf_ref[k, base + 4 : base + 8, :] = up1[ranks, D * j : D * (j + 1)]
            buf_ref[k, base + 8 : base + 12, :] = down2[ranks, D * j : D * (j + 1)]
    for k, out in enumerate((o0, o1, o2, o3)):
        out[...] = buf_ref[k].astype(BF)


def grad_pack(where, *grads):
    return pl.pallas_call(
        grad_pack_kernel,
        out_shape=(jax.ShapeDtypeStruct((4 * RANK, D), BF),) * 4,
        in_specs=[sm()] + [vm()] * 8,
        out_specs=[vm()] * 4,
        scratch_shapes=[pltpu.VMEM((4, 4 * RANK, D), F32)],
        compiler_params=params(8),
        cost_estimate=cost(2),
        name="adapter_grad_pack",
    )(where, *grads)


def grad_sum_kernel(g0, g1, g2, g3, o0, o1, o2, o3, buf_ref):
    total = g0[...].astype(F32) + g1[...].astype(F32) + g2[...].astype(F32) + g3[...].astype(F32)
    buf_ref[...] = jnp.zeros_like(buf_ref)
    buf_ref[:RANK, :] = total[:RANK, :]
    for j, out in enumerate((o0, o1, o2, o3)):
        buf_ref[RANK : RANK + 12, :] = total[RANK + 12 * j : RANK + 12 * (j + 1), :]
        out[...] = buf_ref[...].astype(BF)


def grad_sum(pieces):
    return pl.pallas_call(
        grad_sum_kernel,
        out_shape=(jax.ShapeDtypeStruct((2 * RANK, D), BF),) * 4,
        in_specs=[vm()] * 4,
        out_specs=[vm()] * 4,
        scratch_shapes=[pltpu.VMEM((2 * RANK, D), F32)],
        compiler_params=params(4),
        cost_estimate=cost(2),
        name="adapter_grad_sum",
    )(*pieces)


def grad_adapters_kernel(index_ref, x_ref, qkv_dn, fc1_dn, proj_up, fc2_up, rest_ref, acc_ref):
    acc_ref[...] = jnp.zeros_like(acc_ref)

    def add(i, carry):
        acc_ref[index_ref[i]] += x_ref[i].astype(F32)
        return carry

    lax.fori_loop(0, x_ref.shape[0], add, 0)
    for i, ref in enumerate((qkv_dn, fc1_dn, proj_up, fc2_up)):
        ref[...] = acc_ref[:, :RANK, QUART * i : QUART * (i + 1)]
    rest_ref[...] = acc_ref[:, RANK:, :].astype(BF)


def grad_adapters(index, x):
    s = lambda n, dtype=F32: jax.ShapeDtypeStruct((ADAPT, RANK, n), dtype)
    return pl.pallas_call(
        grad_adapters_kernel,
        out_shape=(s(QUART), s(QUART), s(QUART), s(QUART), s(D, BF)),
        in_specs=[sm(), vm()],
        out_specs=[vm()] * 5,
        scratch_shapes=[pltpu.VMEM((ADAPT, 2 * RANK, D), F32)],
        compiler_params=params(8),
        cost_estimate=cost(2),
        name="adapter_grad_by_adapter",
    )(index, x)


def grad_join_kernel(where_ref, r0, r1, r2, r3, qkv_up, proj_dn, fc1_up, fc2_dn, buf_ref):
    mine = where_ref[0]
    heads = qkv_up.shape[2] // (3 * HD)
    for k, ref in enumerate((r0, r1, r2, r3)):
        buf_ref[jnp.bitwise_xor(mine, k)] = ref[...].astype(F32)
    for source in range(4):
        ranks = slice(RANK // 4 * source, RANK // 4 * (source + 1))
        for h in range(heads):
            for t in range(3):
                qkv_up[:, ranks, HD * (3 * h + t) : HD * (3 * h + t + 1)] = buf_ref[
                    source, :, 0:4, QUART * t + HD * h : QUART * t + HD * (h + 1)
                ]
        proj_dn[:, ranks, :] = buf_ref[source, :, 0:4, 3 * QUART :]
        fc1_up[:, ranks, :] = buf_ref[source, :, 4:8, :]
        fc2_dn[:, ranks, :] = buf_ref[source, :, 8:12, :]


def grad_join(where, pieces):
    s = lambda n: jax.ShapeDtypeStruct((ADAPT, RANK, n), F32)
    return pl.pallas_call(
        grad_join_kernel,
        out_shape=(s(3 * QUART), s(QUART), s(D), s(D)),
        in_specs=[sm()] + [vm()] * 4,
        out_specs=[vm()] * 4,
        scratch_shapes=[pltpu.VMEM((4, ADAPT, RANK, D), F32)],
        compiler_params=params(12),
        cost_estimate=cost(2),
        name="adapter_grad_join",
    )(where, *pieces)


def flip(values, axis, distance):
    size = lax.axis_size(axis)
    return lax.ppermute(values, axis, [(i, i ^ distance) for i in range(size)])


def send_rows(pieces, *deps):
    own, near, pair = pieces
    if deps:
        near, = after((near,), *deps)
    return [own, flip(near, "row", 1), flip(pair, "row", 2)]


def hand_on(pieces, *deps):
    own, near, crossed = pieces
    if deps:
        near, crossed = after((near, crossed), *deps)
    return [own, near, crossed, flip(crossed, "row", 1)]


def exchange(slots, axis):
    return [slots[0]] + [flip(slots[k], axis, k) for k in range(1, 4)]


def after(values, *deps):
    return lax.optimization_barrier((tuple(values), deps))[0]


def col_halves(half):
    return jnp.concatenate([flip(half, "col", j) for j in range(1, 4)], axis=0)


def col_pairs(half, other_row):
    two = jnp.concatenate([half, other_row], axis=0)
    return jnp.concatenate([other_row] + [flip(two, "col", j) for j in range(1, 4)], axis=0)


def body(
    tokens, grad_out, adapter_index, norm1_gain, norm2_gain, qkv_weight, proj_weight, fc1_weight, fc2_weight,
    rel_h, rel_w, qkv_down, qkv_up, proj_down, proj_up, fc1_down, fc1_up, fc2_down, fc2_up,
):
    members = lax.axis_size("col")
    batches = lax.axis_size("dp")
    row_index, col_index, dp_index = lax.axis_index("row"), lax.axis_index("col"), lax.axis_index("dp")
    half = dp_index % 2
    where = jnp.stack([row_index, half]).astype(jnp.int32)
    slot_images = (
        jnp.bitwise_xor(dp_index, jnp.arange(batches, dtype=jnp.int32))[:, None] * members
        + jnp.bitwise_xor(col_index, jnp.arange(members, dtype=jnp.int32))[None, :]
    ).reshape(-1)
    slot_adapters = jnp.sum(
        jnp.where(
            slot_images[:, None] == jnp.arange(adapter_index.shape[0], dtype=jnp.int32)[None, :],
            adapter_index[:, 0][None, :],
            0,
        ),
        axis=1,
    )
    pick = jnp.concatenate([slot_adapters[:4], half[None]]).astype(jnp.int32)
    swap = lambda m: jnp.swapaxes(m, 1, 2)

    shift, keys = jnp.asarray(SHIFT_NP), jnp.asarray(KEYS_NP)

    *token_slots, alpha_own, beta_own, alpha_half, cross, fc1_half, fc2_half = front(
        where, tokens, qkv_weight, proj_weight, fc1_weight, fc2_weight
    )
    crossed = flip(cross, "row", 2)
    beta_half, b0 = cross[:HBLK], crossed[:HBLK]
    c0 = jnp.concatenate([crossed[HBLK : 2 * HBLK], crossed[2 * HBLK :]], axis=1)
    alpha_near = col_halves(alpha_half)
    x_pieces = send_rows(token_slots, crossed)
    *send, row_adapters, rel = adapter_pack(
        pick, qkv_up, swap(proj_down), fc1_up, swap(fc2_down), swap(qkv_down), swap(fc1_down), proj_up, fc2_up,
        norm1_gain.reshape(1, -1), norm2_gain.reshape(1, -1), rel_h, rel_w,
    )
    beta_sent = [jnp.concatenate([beta_half, b0, send[j]], axis=0) for j in range(1, 4)]
    beta_got = [flip(m, "col", j) for j, m in enumerate(beta_sent, 1)]
    alpha_near, x_pieces[1] = after((alpha_near, x_pieces[1]))
    alpha_far = flip(alpha_near, "dp", 1)
    g = jnp.concatenate([alpha_own, alpha_near, alpha_far, row_adapters], axis=0)
    g, *x_pieces = after((g, *x_pieces))
    gy = flip(g, "row", 2)
    grad_slots = pack(where, grad_out)
    *beta_got, _ = after((*beta_got, grad_slots[0]))
    beta_near = jnp.concatenate([b0] + [m[:QUART] for m in beta_got], axis=0)
    col_adapters = [send[0]] + beta_got
    beta_far = flip(beta_near, "dp", 1)
    x_pieces = hand_on(x_pieces)

    g1, own1, near1 = (flip(m, "row", 1) for m in (g, beta_own, beta_near))
    fc1_half, = after((fc1_half,), g1, own1, near1, x_pieces[3])
    fc1_near = [flip(fc1_half, "col", j) for j in range(1, 4)]
    gy, beta_far, fc2_half, c0 = after((gy, beta_far, fc2_half, c0), *fc1_near)
    fc2_two = jnp.concatenate([fc2_half, c0], axis=0)
    fc2_near = [flip(fc2_two, "col", j) for j in range(1, 4)]
    gy1, far1 = flip(gy, "row", 1), flip(beta_far, "row", 1)
    *grad_slots, fc1_near = after((*grad_slots, jnp.concatenate(fc1_near, axis=0)), gy1, far1)
    fc1_far = flip(fc1_near, "dp", 1)
    g_pieces = [grad_slots[0], grad_slots[1], flip(grad_slots[2], "row", 2)]
    wqkv, wproj, dqkv, uqkv, dproj, uproj, d1, u1, d2, u2, gain1, gain2 = prep1(
        where, (g, g1, gy, gy1), (beta_own, beta_near, beta_far, own1, near1, far1), col_adapters
    )
    h = jnp.concatenate([fc1_weight, fc1_near, fc1_far], axis=0)
    wqkv, h = after((wqkv, h), g_pieces[2])
    hy = flip(h, "row", 2)
    x, hid, *qkvs = qkv_rows(x_pieces, gain1, wqkv)
    *qkvs, n1, n2, n3 = after((*qkvs, *fc2_near))
    fc2_near = jnp.concatenate([c0, n1, n2, n3], axis=0)
    fc2_far = flip(fc2_near, "dp", 1)
    fc2_ahead = [flip(m, "row", 1) for m in (fc2_weight, fc2_near)]
    g_pieces[1], = after((g_pieces[1],), qkvs[0])
    g_pieces[1] = flip(g_pieces[1], "row", 1)
    g_pieces = hand_on(g_pieces, qkvs[0])
    part0 = attention(0, qkvs[0], rel, shift, keys)
    qkv1, = after((qkvs[1],), part0[0], g_pieces[3], *fc2_ahead)
    part1 = attention(1, qkv1, rel, shift, keys)
    qkv2, _ = after((qkvs[2], part1[0]))
    part2 = attention(2, qkv2, rel, shift, keys)
    atts, exps, invs = zip(part0, part1, part2)
    atts = list(atts)
    atts[2], hy = after((atts[2], hy))
    alpha2 = [h, flip(h, "row", 1), hy, flip(hy, "row", 1)]
    middle = project(x, atts, wproj)
    middle, fc2_far = after((middle, fc2_far))
    beta2 = [fc2_weight, fc2_near, fc2_far, *fc2_ahead, flip(fc2_far, "row", 1)]

    *out_slots, gmid, down1, up1, down2, up2 = mlp(where, middle, g_pieces, gain2, alpha2, beta2, d1, u1, d2, u2)
    out_pieces = send_rows(out_slots)
    gqkv, down_q, up_q, down_p, up_p = attention_back(
        gmid, hid, qkvs, atts, exps, invs, wproj, rel, shift, keys, dqkv, uqkv, dproj, uproj
    )
    out_pieces = hand_on(out_pieces, gqkv)
    gqkv, down_q, up_q, down_p, up_p = after((gqkv, down_q, up_q, down_p, up_p), *out_pieces[:3])
    packed = grad_pack(where, down_q, up_q, down_p, up_p, down1, up1, down2, up2)
    *packed, gqkv = after((*packed, gqkv))
    row_sums = exchange(packed, "row")
    back0 = token_grad(gmid, x, gqkv, gain1, wqkv, *TAIL[0])
    *row_sums, gqkv, b0, b1, b2 = after((*row_sums, gqkv, *back0))
    back_pieces = send_rows((b0, b1, b2))
    summed = grad_sum(row_sums)
    *summed, gqkv = after((*summed, gqkv))
    images = exchange(summed, "col")
    back1 = token_grad(gmid, x, gqkv, gain1, wqkv, *TAIL[1])
    last_pieces = send_rows(back1)
    *images, near, crossed = after((*images, *back_pieces[1:]), back1[0])
    back_pieces = hand_on([back_pieces[0], near, crossed])
    images = jnp.stack(images)
    images, *out_pieces = after((images, *out_pieces))
    step = 1
    while step < batches:
        images = jnp.concatenate([images, flip(images, "dp", step)], axis=0)
        step *= 2
    result = unpack(where, out_pieces, BF)
    images, = after((images,), result)
    qkv_dn, fc1_dn, proj_upg, fc2_upg, rest = grad_adapters(slot_adapters.astype(jnp.int32), images)
    rests = [rest] + [flip(rest, "row", k) for k in range(1, 4)]
    grad_tokens = unpack(where, back_pieces + hand_on(last_pieces, rest), F32, TAIL)
    rests = after(tuple(rests), grad_tokens)
    qkv_upg, proj_dn, fc1_upg, fc2_dn = grad_join(where, rests)
    return (
        result, grad_tokens,
        swap(qkv_dn), qkv_upg, swap(proj_dn), proj_upg, swap(fc1_dn), fc1_upg, swap(fc2_dn), fc2_upg,
    )


def solution(mesh):
    return jax.shard_map(
        body,
        mesh=mesh,
        in_specs=(
            P("row", ("dp", "col")), P("row", ("dp", "col")), P(), P("row"), P("row"),
            P("row", "col"), P("col", "row"), P("row", "col"), P("row", "col"), P(), P(),
            P(None, "row", None), P(None, None, "col"), P(None, "col", None), P(None, None, "row"),
            P(None, "row", None), P(None, None, "col"), P(None, "col", None), P(None, None, "row"),
        ),
        out_specs=(
            P("row", ("dp", "col")), P("row", ("dp", "col")),
            P(None, "row", None), P(None, None, "col"), P(None, "col", None), P(None, None, "row"),
            P(None, "row", None), P(None, None, "col"), P(None, "col", None), P(None, None, "row"),
        ),
        check_vma=False,
    )
```
